32 devices in a mesh: space: 8 (over z, core), chan: 4 (over y, x).
Axes of the slice: x: 2, y: 2, z: 4, core: 2. Of those that a mesh axis runs over, the one named last changes fastest.
Arguments:
- current_atmosphere: float32 [1, 96, 122880], P(None, 'space', 'chan'), may hold values from -6 to 6
- truth_one: float32 [1, 96, 122880], P(None, 'space', 'chan'), may hold values from -6 to 6
- truth_two: float32 [1, 96, 122880], P(None, 'space', 'chan'), may hold values from -6 to 6
- storm_codes: int32 [1], replicated, may hold values from 16 to 192
- pre_gain: float32 [768], P('chan'), may hold values from 0.5 to 1.5
- pre_shift: float32 [768], P('chan'), may hold values from -0.6 to 0.6
- mix_weight_in: float32 [2, 8, 96, 96], P(None, 'chan'), may hold values from -0.625 to 0.625
- mix_bias_in: float32 [2, 8, 96], P(None, 'chan'), may hold values from -0.6 to 0.6
- mix_weight_out: float32 [2, 8, 96, 96], P(None, 'chan'), may hold values from -0.625 to 0.625
- mix_bias_out: float32 [2, 8, 96], P(None, 'chan'), may hold values from -0.6 to 0.6
- post_gain: float32 [768], P('chan'), may hold values from 0.5 to 1.5
- post_shift: float32 [768], P('chan'), may hold values from -0.6 to 0.6
- up_weight: bfloat16 [768, 3072], P(None, 'chan'), may hold values from -0.21875 to 0.21875
- up_bias: bfloat16 [3072], P('chan'), may hold values from -0.59765625 to 0.59765625
- down_weight: bfloat16 [3072, 768], P('chan'), may hold values from -0.109375 to 0.109375
- down_bias: bfloat16 [768], P('chan'), may hold values from -0.59765625 to 0.59765625
Outputs:
- forecast_one: float32 [1, 96, 122880], P(None, 'space', 'chan')
- forecast_two: float32 [1, 96, 122880], P(None, 'space', 'chan')
- state_grad: float32 [1, 96, 122880], P(None, 'space', 'chan')
- grad_pre_gain: float32 [768], P('chan')
- grad_pre_shift: float32 [768], P('chan')
- grad_mix_weight_in: float32 [2, 8, 96, 96], P(None, 'chan')
- grad_mix_bias_in: float32 [2, 8, 96], P(None, 'chan')
- grad_mix_weight_out: float32 [2, 8, 96, 96], P(None, 'chan')
- grad_mix_bias_out: float32 [2, 8, 96], P(None, 'chan')
- grad_post_gain: float32 [768], P('chan')
- grad_post_shift: float32 [768], P('chan')
- grad_up_weight: float32 [768, 3072], P(None, 'chan')
- grad_up_bias: float32 [3072], P('chan')
- grad_down_weight: float32 [3072, 768], P('chan')
- grad_down_bias: float32 [768], P('chan')
The draws below stay inside these ranges and needn't reach their ends.
Inputs may be any that keep to these rules, and one draw needn't show every extreme that they name: `storm_codes`: a sample's weight in the loss is its code divided by 64.
All inputs are finite; a program needn't handle non-finite values.
Results may differ from the reference program's by a relative error of at most 0.033.
Values may be sent and summed in bfloat16 or wider, within the bound.
A program may use at most 256 MiB of HBM per device.

```python
import jax
import jax.numpy as jnp
from jax import lax

D = 768
NB = 8
FF = 3072
BS = 96
W = 160
KW = 81
H = 96
B = 1


def block_levels(key, shape, shards, smallest, largest):
    def one(position, blocks):
        steps = jax.random.uniform(jax.random.fold_in(jax.random.fold_in(key, 6), position), (blocks,), jnp.float32, smallest / len(shards), largest / len(shards))
        return jnp.repeat(jnp.exp(steps), shape[position] // blocks).reshape((-1,) + (1,) * (len(shape) - position - 1))

    level = one(*shards[0])
    for cut in shards[1:]:
        level = level * one(*cut)
    return level


def normal_values(key, dims, width, bound, pieces=(), dtype=jnp.bfloat16):
    factor_of = block_levels(key, dims, pieces, -0.22, 0.18) if pieces else 1.0
    drawn = jax.random.normal(key, dims, jnp.float32) * width * factor_of
    return jnp.minimum(jnp.maximum(drawn, -bound), bound).astype(dtype)


def setup_inputs(seed: int = 0) -> dict:
    key_of = jax.random.split(jax.random.key(seed), 17)
    current_atmosphere = normal_values(key_of[0], (B, H, D * W), 1.0, 6.0, ((1, 8), (2, 4)), jnp.float32)
    truth_one = normal_values(key_of[1], (B, H, D * W), 1.0, 6.0, ((1, 8), (2, 4)), jnp.float32)
    truth_two = normal_values(key_of[2], (B, H, D * W), 1.0, 6.0, ((1, 8), (2, 4)), jnp.float32)
    storm_codes = jax.random.randint(key_of[3], (B,), 16, 193).astype(jnp.int32)
    pre_gain = jnp.clip(1.0 + 0.1 * jax.random.normal(key_of[4], (D,), jnp.float32), 0.5, 1.5)
    pre_shift = normal_values(key_of[5], (D,), 0.1, 0.6, ((0, 4),), jnp.float32)
    mix_weight_in = normal_values(key_of[6], (2, NB, BS, BS), BS ** -0.5, 0.625, ((1, 4),), jnp.float32)
    mix_bias_in = normal_values(key_of[7], (2, NB, BS), 0.1, 0.6, ((1, 4),), jnp.float32)
    mix_weight_out = normal_values(key_of[8], (2, NB, BS, BS), BS ** -0.5, 0.625, ((1, 4),), jnp.float32)
    mix_bias_out = normal_values(key_of[9], (2, NB, BS), 0.1, 0.6, ((1, 4),), jnp.float32)
    post_gain = jnp.clip(1.0 + 0.1 * jax.random.normal(key_of[10], (D,), jnp.float32), 0.5, 1.5)
    post_shift = normal_values(key_of[11], (D,), 0.1, 0.6, ((0, 4),), jnp.float32)
    up_weight = normal_values(key_of[12], (D, FF), D ** -0.5, 0.21875, ((1, 4),))
    up_bias = normal_values(key_of[13], (FF,), 0.1, 0.59765625, ((0, 4),))
    down_weight = normal_values(key_of[14], (FF, D), FF ** -0.5, 0.109375, ((0, 4),))
    down_bias = normal_values(key_of[15], (D,), 0.1, 0.59765625, ((0, 4),))
    return {"current_atmosphere": current_atmosphere, "truth_one": truth_one, "truth_two": truth_two, "storm_codes": storm_codes, "pre_gain": pre_gain, "pre_shift": pre_shift, "mix_weight_in": mix_weight_in, "mix_bias_in": mix_bias_in, "mix_weight_out": mix_weight_out, "mix_bias_out": mix_bias_out, "post_gain": post_gain, "post_shift": post_shift, "up_weight": up_weight, "up_bias": up_bias, "down_weight": down_weight, "down_bias": down_bias}


NORM_EPS = 1e-06
SHRINK_LEVEL = 0.01
FULL_PRECISION = lax.Precision.HIGHEST

@jax.custom_vjp
def low(v):
    return lax.optimization_barrier(v.astype(jnp.bfloat16)).astype(jnp.float32)

@jax.custom_vjp
def low_back(v):
    return v

def low_keep(v):
    return (low(v), None)

def low_pass(kept, grad):
    return (grad,)

def back_keep(v):
    return (v, None)

def back_low(kept, grad):
    return (low(grad),)
low.defvjp(low_keep, low_pass)
low_back.defvjp(back_keep, back_low)

def to_cells(flat_field):
    samples, height = (flat_field.shape[0], flat_field.shape[1])
    return jnp.transpose(flat_field.reshape(samples, height, D, W), (0, 1, 3, 2))

def to_flat(cell_field):
    samples, height = (cell_field.shape[0], cell_field.shape[1])
    return jnp.transpose(cell_field, (0, 1, 3, 2)).reshape(samples, height, D * W)

def layer_norm(values, gain, offset):
    average = lax.optimization_barrier(jnp.mean(values, axis=-1, keepdims=True))
    centred = values - average
    variance = lax.optimization_barrier(jnp.mean(centred * centred, axis=-1, keepdims=True))
    return centred * lax.rsqrt(variance + NORM_EPS) * gain + offset

def shrink(values):
    return values - jnp.clip(values, -SHRINK_LEVEL, SHRINK_LEVEL)

def block_mix(values, matrix):
    return jnp.einsum('bhkni,nio->bhkno', values, matrix, precision=FULL_PRECISION)

def spectral(normed, w_first, b_first, w_second, b_second):
    samples, height, columns, features = normed.shape
    spectrum = jnp.fft.rfft2(normed, axes=(1, 2), norm='ortho')[:, :, :KW, :]
    spectrum = spectrum.reshape(samples, height, KW, NB, BS)
    real_part = jnp.real(spectrum)
    imag_part = jnp.imag(spectrum)
    first_real = jax.nn.relu(block_mix(real_part, w_first[0]) - block_mix(imag_part, w_first[1]) + b_first[0])
    first_imag = jax.nn.relu(block_mix(imag_part, w_first[0]) + block_mix(real_part, w_first[1]) + b_first[1])
    second_real = shrink(block_mix(first_real, w_second[0]) - block_mix(first_imag, w_second[1]) + b_second[0])
    second_imag = shrink(block_mix(first_imag, w_second[0]) + block_mix(first_real, w_second[1]) + b_second[1])
    filtered = (second_real + 1j * second_imag).reshape(samples, height, KW, features)
    filtered = jnp.pad(filtered, ((0, 0), (0, 0), (0, columns // 2 + 1 - KW), (0, 0)))
    return jnp.fft.irfft2(filtered, s=(height, columns), axes=(1, 2), norm='ortho')

def feed_forward(entry, up_weight, up_bias, down_weight, down_bias):
    layout = entry.shape
    flat_rows = low(entry.reshape(-1, layout[-1]))
    hidden = low_back(jnp.dot(flat_rows, up_weight, precision=FULL_PRECISION) + up_bias)
    active = low(jax.nn.gelu(hidden, approximate=False))
    output = low_back(jnp.dot(active, down_weight, precision=FULL_PRECISION) + down_bias)
    return output.reshape(layout)

def filter_block(values, cyclone_importance_grid):
    pre_gain, pre_shift, mix_weight_in, mix_bias_in, mix_weight_out, mix_bias_out, post_gain, post_shift, up_weight, up_bias, down_weight, down_bias = cyclone_importance_grid
    normed = layer_norm(values, pre_gain, pre_shift)
    middle = spectral(normed, mix_weight_in, mix_bias_in, mix_weight_out, mix_bias_out) + normed + values
    entry = layer_norm(middle, post_gain, post_shift)
    return feed_forward(entry, up_weight, up_bias, down_weight, down_bias) + middle

def reference(current_atmosphere, truth_one, truth_two, storm_codes, pre_gain, pre_shift, mix_weight_in, mix_bias_in, mix_weight_out, mix_bias_out, post_gain, post_shift, up_weight, up_bias, down_weight, down_bias):
    cyclone_importance_grid = tuple((item.astype(jnp.float32) for item in (pre_gain, pre_shift, mix_weight_in, mix_bias_in, mix_weight_out, mix_bias_out, post_gain, post_shift, up_weight, up_bias, down_weight, down_bias)))
    sample_weight = (storm_codes.astype(jnp.float32) / 64.0).reshape(-1, 1, 1, 1)
    target_one = to_cells(truth_one)
    target_two = to_cells(truth_two)

    def objective_number(start_flat, *params):
        start = to_cells(start_flat)
        first_step = filter_block(start, params)
        second_step = filter_block(first_step, params)
        error_one = first_step - target_one
        error_two = second_step - target_two
        total_objective = 0.5 * jnp.sum(sample_weight * (error_one * error_one + error_two * error_two))
        return (total_objective, (to_flat(first_step), to_flat(second_step)))
    total_objective, adjoint_mapping, twofold_prediction = jax.vjp(objective_number, current_atmosphere, *cyclone_importance_grid, has_aux=True)
    model_derivatives = adjoint_mapping(jnp.ones_like(total_objective))
    return (twofold_prediction[0], twofold_prediction[1]) + tuple(model_derivatives)
```

```python
import functools
import math

import jax
import jax.numpy as jnp
import ml_dtypes
import numpy as np
from jax import lax
from jax.experimental import pallas as pl
from jax.experimental.pallas import tpu as pltpu
from jax.sharding import PartitionSpec as P

W = 160
KW = 81


NORM_EPS = 1e-06
SHRINK_LEVEL = 0.01
FULL_PRECISION = lax.Precision.HIGHEST


def exact_gelu(values):
    return jax.nn.gelu(values, approximate=False)


def shrink(values):
    return values - jnp.clip(values, -SHRINK_LEVEL, SHRINK_LEVEL)


def block_mix(values, matrix):
    return jnp.einsum("bhkni,nio->bhkno", values, matrix, precision=FULL_PRECISION)


def row_tables(columns, kept_modes, padded_modes):
    places = jnp.arange(columns, dtype=jnp.int32)[:, None]
    orders = jnp.arange(padded_modes, dtype=jnp.int32)[None, :]
    angles = 2.0 * math.pi / columns * (places * orders % columns).astype(jnp.float32)
    factor = 1.0 / math.sqrt(columns)
    single = jnp.logical_or(orders == 0, 2 * orders == columns)
    doubled = jnp.where(single, 1.0, 2.0).astype(jnp.float32)
    used = jnp.where(orders < kept_modes, 1.0, 0.0).astype(jnp.float32)
    return (
        jnp.cos(angles) * factor * used,
        -jnp.sin(angles) * factor * used,
        jnp.transpose(jnp.cos(angles) * doubled * factor * used),
        jnp.transpose(jnp.sin(angles) * doubled * factor * used),
    )


def along_rows(values, tables):
    return jnp.stack(
        [
            jnp.einsum("bhwc,wk->bhkc", values, tables[0], precision=FULL_PRECISION),
            jnp.einsum("bhwc,wk->bhkc", values, tables[1], precision=FULL_PRECISION),
        ]
    )


def along_rows_back(paired, tables):
    return jnp.einsum("bhkc,wk->bhwc", paired[0], tables[0], precision=FULL_PRECISION) + jnp.einsum(
        "bhkc,wk->bhwc", paired[1], tables[1], precision=FULL_PRECISION
    )


def rows_inverse(paired, tables):
    return jnp.einsum("bhkc,kw->bhwc", paired[0], tables[2], precision=FULL_PRECISION) - jnp.einsum(
        "bhkc,kw->bhwc", paired[1], tables[3], precision=FULL_PRECISION
    )


def rows_inverse_back(values, tables):
    return jnp.stack(
        [
            jnp.einsum("bhwc,kw->bhkc", values, tables[2], precision=FULL_PRECISION),
            -jnp.einsum("bhwc,kw->bhkc", values, tables[3], precision=FULL_PRECISION),
        ]
    )


def column_tables(height):
    orders = jnp.arange(height, dtype=jnp.int32)[:, None]
    places = jnp.arange(height, dtype=jnp.int32)[None, :]
    angles = 2.0 * math.pi / height * (orders * places % height).astype(jnp.float32)
    factor = 1.0 / math.sqrt(height)
    return (jnp.cos(angles) * factor, jnp.sin(angles) * factor)


def to_freq(matrix, values):
    return jnp.einsum("kh,bhmc->bkmc", matrix, values, precision=FULL_PRECISION)


def from_freq(matrix, values):
    return jnp.einsum("kh,bkmc->bhmc", matrix, values, precision=FULL_PRECISION)


def spectral_core(paired, w_first, b_first, w_second, b_second):
    samples, height, kept_modes, channels = paired.shape[1:]
    blocks, block_size = (w_first.shape[1], w_first.shape[2])
    cosine, sine_table = column_tables(height)
    real_in, imag_in = (paired[0], paired[1])
    split_form = (samples, height, kept_modes, blocks, block_size)
    real_part = (to_freq(cosine, real_in) + to_freq(sine_table, imag_in)).reshape(split_form)
    imag_part = (to_freq(cosine, imag_in) - to_freq(sine_table, real_in)).reshape(split_form)
    first_real = jax.nn.relu(
        block_mix(real_part, w_first[0]) - block_mix(imag_part, w_first[1]) + b_first[0]
    )
    first_imag = jax.nn.relu(
        block_mix(imag_part, w_first[0]) + block_mix(real_part, w_first[1]) + b_first[1]
    )
    joined_form = (samples, height, kept_modes, channels)
    second_real = shrink(
        block_mix(first_real, w_second[0]) - block_mix(first_imag, w_second[1]) + b_second[0]
    ).reshape(joined_form)
    second_imag = shrink(
        block_mix(first_imag, w_second[0]) + block_mix(first_real, w_second[1]) + b_second[1]
    ).reshape(joined_form)
    out_real = from_freq(cosine, second_real) - from_freq(sine_table, second_imag)
    out_imag = from_freq(cosine, second_imag) + from_freq(sine_table, second_real)
    return jnp.stack([out_real, out_imag])


def column_layout(paired):
    return lax.all_to_all(paired, "space", split_axis=3, concat_axis=2, tiled=True)


def row_layout(paired):
    return lax.all_to_all(
        paired.astype(jnp.bfloat16), "space", split_axis=2, concat_axis=3, tiled=True
    ).astype(paired.dtype)


def norm_forward(values, gain, offset):
    width_all = values.shape[-1] * lax.axis_size("chan")
    totals = lax.psum((jnp.sum(values, axis=-1), jnp.sum(values * values, axis=-1)), "chan")
    average = totals[0] / width_all
    variance = totals[1] / width_all - average * average
    inverse_dev = lax.rsqrt(variance + NORM_EPS)[..., None]
    scaled = (values - average[..., None]) * inverse_dev
    return (scaled * gain + offset, (scaled, inverse_dev))


def norm_backward(gradient, gain, saved):
    scaled, inverse_dev = saved
    width_all = scaled.shape[-1] * lax.axis_size("chan")
    scaled_grad = gradient * gain
    totals = lax.psum(
        (jnp.sum(scaled_grad, axis=-1), jnp.sum(scaled_grad * scaled, axis=-1)), "chan"
    )
    values_grad = inverse_dev * (
        scaled_grad - totals[0][..., None] / width_all - scaled * (totals[1][..., None] / width_all)
    )
    return (
        values_grad,
        jnp.sum(gradient * scaled, axis=(0, 1, 2)),
        jnp.sum(gradient, axis=(0, 1, 2)),
    )


def shards(
    current_atmosphere,
    truth_one,
    truth_two,
    storm_codes,
    pre_gain,
    pre_shift,
    mix_weight_in,
    mix_bias_in,
    mix_weight_out,
    mix_bias_out,
    post_gain,
    post_shift,
    up_weight,
    up_bias,
    down_weight,
    down_bias,
):
    samples, rows_here, merged = current_atmosphere.shape
    columns = W
    channels = merged // columns
    total_rows = samples * rows_here * columns
    space_count = lax.axis_size("space")
    padded_modes = (KW + space_count - 1) // space_count * space_count
    tables = row_tables(columns, KW, padded_modes)

    def to_cells(flat_field):
        return jnp.transpose(
            flat_field.reshape(samples, rows_here, channels, columns), (0, 1, 3, 2)
        )

    def to_flat(cell_field):
        return jnp.transpose(cell_field, (0, 1, 3, 2)).reshape(samples, rows_here, merged)

    start_cells = to_cells(current_atmosphere)
    target_one = to_cells(truth_one)
    target_two = to_cells(truth_two)
    weight_of = (storm_codes.astype(jnp.float32) / 64.0).reshape(-1, 1, 1, 1)
    full_up, full_down, full_up_bias, full_down_bias = (up_weight, down_weight, up_bias, down_bias)

    def mlp_forward(inputs):
        gathered = lax.all_gather(inputs, "chan", axis=1, tiled=True)
        hidden = jnp.dot(
            gathered, full_up, preferred_element_type=jnp.float32
        ) + full_up_bias.astype(jnp.float32)
        active_full, gelu_pull = jax.vjp(exact_gelu, hidden)
        active = active_full.astype(jnp.bfloat16)
        product = jnp.dot(active, full_down, preferred_element_type=jnp.float32)
        output = lax.psum_scatter(
            product.astype(jnp.bfloat16), "chan", scatter_dimension=1, tiled=True
        ).astype(jnp.float32) + full_down_bias.astype(jnp.float32)
        return (output, (gathered, gelu_pull, active))

    def mlp_backward(gradient, saved):
        gathered, gelu_pull, active = saved
        grad_low = gradient.astype(jnp.bfloat16)
        grad_rows = lax.all_gather(grad_low, "chan", axis=1, tiled=True)
        down_bias_grad = jnp.sum(grad_low.astype(jnp.float32), axis=0)
        down_grad = jnp.dot(active.T, grad_rows, preferred_element_type=jnp.float32)
        active_grad = jnp.dot(grad_rows, full_down.T, preferred_element_type=jnp.float32)
        hidden_grad = gelu_pull(active_grad)[0].astype(jnp.bfloat16)
        up_grad = jnp.dot(gathered.T, hidden_grad, preferred_element_type=jnp.float32)
        up_bias_grad = jnp.sum(hidden_grad.astype(jnp.float32), axis=0)
        input_part = jnp.dot(hidden_grad, full_up.T, preferred_element_type=jnp.float32)
        input_grad = lax.psum_scatter(
            input_part.astype(jnp.bfloat16), "chan", scatter_dimension=1, tiled=True
        ).astype(jnp.float32)
        return (input_grad, (up_grad, up_bias_grad, down_grad, down_bias_grad))

    def forward_block(values):
        normed, first_saved = norm_forward(values, pre_gain, pre_shift)
        modal_in = column_layout(along_rows(normed, tables))
        filtered, core_pull = jax.vjp(
            spectral_core, modal_in, mix_weight_in, mix_bias_in, mix_weight_out, mix_bias_out
        )
        middle = rows_inverse(row_layout(filtered), tables) + normed + values
        entry, second_residuals = norm_forward(middle, post_gain, post_shift)
        output, mlp_saved = mlp_forward(entry.astype(jnp.bfloat16).reshape(total_rows, channels))
        return (
            output.reshape(values.shape) + middle,
            (first_saved, core_pull, second_residuals, mlp_saved),
        )

    def backward_block(gradient, saved):
        first_saved, core_pull, second_residuals, mlp_saved = saved
        mlp_grad, dense_grads = mlp_backward(gradient.reshape(total_rows, channels), mlp_saved)
        middle_part, post_gain_grad, post_shift_grad = norm_backward(
            mlp_grad.reshape(gradient.shape), post_gain, second_residuals
        )
        middle_grad = middle_part + gradient
        filter_grads = core_pull(column_layout(rows_inverse_back(middle_grad, tables)))
        normed_grad = along_rows_back(row_layout(filter_grads[0]), tables) + middle_grad
        input_part, pre_gain_grad, pre_shift_grad = norm_backward(
            normed_grad, pre_gain, first_saved
        )
        return (
            input_part + middle_grad,
            (pre_gain_grad, pre_shift_grad)
            + tuple(filter_grads[1:])
            + (post_gain_grad, post_shift_grad)
            + dense_grads,
        )

    first_out, first_saved_all = forward_block(start_cells)
    second_out, second_saved_all = forward_block(first_out)
    carried, grads_late = backward_block(weight_of * (second_out - target_two), second_saved_all)
    input_grad, grads_early = backward_block(
        weight_of * (first_out - target_one) + carried, first_saved_all
    )
    summed = jax.tree.map(jnp.add, grads_early, grads_late)
    (
        sum_pre_gain,
        sum_pre_shift,
        sum_mix_w_in,
        summed_mixing_bias_input,
        sum_mix_w_out,
        sum_mix_b_out,
        sum_post_gain,
        sum_post_shift,
        sum_up,
        sum_up_bias,
        sum_down,
        sum_down_bias,
    ) = summed
    totals = (
        lax.psum(sum_pre_gain.astype(jnp.bfloat16), "space").astype(jnp.float32),
        lax.psum(sum_pre_shift.astype(jnp.bfloat16), "space").astype(jnp.float32),
        lax.psum(sum_mix_w_in.astype(jnp.bfloat16), "space").astype(jnp.float32),
        lax.psum(summed_mixing_bias_input.astype(jnp.bfloat16), "space").astype(jnp.float32),
        lax.psum(sum_mix_w_out.astype(jnp.bfloat16), "space").astype(jnp.float32),
        lax.psum(sum_mix_b_out.astype(jnp.bfloat16), "space").astype(jnp.float32),
        lax.psum(sum_post_gain.astype(jnp.bfloat16), "space").astype(jnp.float32),
        lax.psum(sum_post_shift.astype(jnp.bfloat16), "space").astype(jnp.float32),
        lax.psum(sum_up.astype(jnp.bfloat16), "space").astype(jnp.float32),
        lax.psum(sum_up_bias.astype(jnp.bfloat16), "space").astype(jnp.float32),
        lax.psum(sum_down.astype(jnp.bfloat16), "space").astype(jnp.float32),
        lax.psum(sum_down_bias.astype(jnp.bfloat16), "space").astype(jnp.float32),
    )
    return (to_flat(first_out), to_flat(second_out), to_flat(input_grad)) + tuple(totals)


BF = jnp.bfloat16
F32 = jnp.float32
MESH_ID = pl.DeviceIdType.MESH
VMEM_BYTES = 66 * 1024 * 1024 - 1024 * 1024


def mm(a, b):
    return jnp.dot(a, b, preferred_element_type=F32)


def mm_nt(a, b):
    return lax.dot_general(a, b, (((1,), (1,)), ((), ())), preferred_element_type=F32)


def mm_tn(a, b):
    return lax.dot_general(a, b, (((0,), (0,)), ((), ())), preferred_element_type=F32)


def halves(v):
    high = v.astype(BF)
    return high, (v - high.astype(F32)).astype(BF)


def mm3(a, b):
    return mm(a[0], b[0]) + (mm(a[0], b[1]) + mm(a[1], b[0]))


def const_halves(table):
    table = np.asarray(table, np.float32)
    high = table.astype(ml_dtypes.bfloat16)
    low = (table - high.astype(np.float32)).astype(ml_dtypes.bfloat16)
    return jnp.asarray(high), jnp.asarray(low)


def row_constants(columns):
    half = columns // 2
    place = np.arange(columns)
    mode = np.arange(half)
    angle = 2.0 * np.pi * np.outer(mode, place) / columns
    real = np.cos(angle)
    imag = -np.sin(angle)
    imag[0] = np.cos(np.pi * place)
    forward = np.concatenate([real, imag]) / np.sqrt(columns)
    weight = np.where(mode == 0, 1.0, 2.0)
    inverse = (forward * np.concatenate([weight, weight])[:, None]).T
    return forward, inverse


def column_constants(height, rows, group):
    owners = height // rows
    angle = 2.0 * np.pi * np.outer(np.arange(height), np.arange(height)) / height
    cosine = np.cos(angle) / np.sqrt(height)
    sine = np.sin(angle) / np.sqrt(height)

    def spread(matrix):
        wide = np.zeros((group, height, owners, group, rows))
        for column in range(group):
            wide[column, :, :, column, :] = matrix.reshape(height, owners, rows)
        return wide.reshape(group * height, owners * group * rows)

    cosine, sine = spread(cosine), spread(sine)
    return np.block([[cosine, sine], [-sine, cosine]])


def signal_peers(axis, count, barrier):
    me = lax.axis_index(axis)
    for step in range(1, count):
        pl.semaphore_signal(
            barrier, inc=1, device_id={axis: lax.rem(me + step, count)}, device_id_type=MESH_ID
        )


def push(axis, count, step, source, target, send_sem, recv_sem):
    peer = lax.rem(lax.axis_index(axis) + step, count)
    return pltpu.make_async_remote_copy(
        src_ref=source,
        dst_ref=target,
        send_sem=send_sem.at[step],
        recv_sem=recv_sem.at[step],
        device_id={axis: peer},
        device_id_type=MESH_ID,
    )


def params(collective_id=None):
    return pltpu.CompilerParams(
        collective_id=collective_id,
        has_side_effects=collective_id is not None,
        vmem_limit_bytes=VMEM_BYTES,
    )


def vmem(count):
    return [pl.BlockSpec(memory_space=pltpu.VMEM)] * count


def cells_from_lines(lines_ref, h, scratch_ref):
    features = scratch_ref.shape[1]
    per = 640 // W
    groups = features // per
    wide = jnp.concatenate(
        [lines_ref[h, pl.ds(part, groups, stride=5), :] for part in range(5)], axis=1
    )
    for part in range(per):
        piece = wide[:, part * W : (part + 1) * W]
        scratch_ref[0, pl.ds(part, groups, stride=per), :] = piece[:, :128]
        scratch_ref[1, pl.ds(part, groups, stride=per), :] = jnp.concatenate(
            [piece[:, 128:], jnp.zeros((groups, 256 - W), F32)], axis=1
        )
    return jnp.concatenate([scratch_ref[0], scratch_ref[1][:, : W - 128]], axis=1)


def enter_kernel(lines_ref, cells_ref, scratch_ref):
    cells_ref[0] = cells_from_lines(lines_ref, 0, scratch_ref).T


def enter(lines, features, columns):
    rows = lines.shape[0]
    return pl.pallas_call(
        enter_kernel,
        grid=(rows,),
        in_specs=[pl.BlockSpec((1,) + lines.shape[1:], lambda h: (h, 0, 0))],
        out_specs=pl.BlockSpec((1, columns, features), lambda h: (h, 0, 0)),
        out_shape=jax.ShapeDtypeStruct((rows, columns, features), F32),
        scratch_shapes=[pltpu.VMEM((2, features, 128), F32)],
        compiler_params=params(),
        name="enter",
    )(lines)


def leave_kernel(cells_ref, lines_ref, scratch_ref):
    features = scratch_ref.shape[1]
    per = 640 // W
    groups = features // per
    block = cells_ref[0].T
    scratch_ref[0] = block[:, :128]
    scratch_ref[1] = jnp.concatenate([block[:, 128:], jnp.zeros((features, 256 - W), F32)], axis=1)
    wide = jnp.concatenate(
        [
            piece
            for part in range(per)
            for piece in (
                scratch_ref[0, pl.ds(part, groups, stride=per), :],
                scratch_ref[1, pl.ds(part, groups, stride=per), :][:, : W - 128],
            )
        ],
        axis=1,
    )
    for part in range(5):
        lines_ref[0, pl.ds(part, groups, stride=5), :] = wide[:, part * 128 : (part + 1) * 128]


def leave(cells):
    rows, columns, features = cells.shape
    lines = features * columns // 128
    return pl.pallas_call(
        leave_kernel,
        grid=(rows,),
        in_specs=[pl.BlockSpec((1, columns, features), lambda h: (h, 0, 0))],
        out_specs=pl.BlockSpec((1, lines, 128), lambda h: (h, 0, 0)),
        out_shape=jax.ShapeDtypeStruct((rows, lines, 128), F32),
        scratch_shapes=[pltpu.VMEM((2, features, 128), F32)],
        compiler_params=params(),
        name="leave",
    )(cells)


def entry_norm_kernel(
    chans, lines_ref, cells_ref, unit_ref, dev_ref, flat_ref, scratch_ref, mine_ref, all_ref, send_sem, recv_sem
):
    rows = lines_ref.shape[0]
    features, columns = flat_ref.shape[1:]
    me = lax.axis_index("chan")
    barrier = pltpu.get_barrier_semaphore()
    signal_peers("chan", chans, barrier)

    def first(h, carry):
        block = cells_from_lines(lines_ref, h, scratch_ref)
        flat_ref[h] = block
        total = jnp.sum(block, axis=0, keepdims=True)
        centred = block - total * (1.0 / features)
        mine_ref[pl.ds(h, 1), :] = total
        mine_ref[pl.ds(rows + h, 1), :] = jnp.sum(centred * centred, axis=0, keepdims=True)
        return carry

    lax.fori_loop(0, rows, first, 0)
    all_ref[me] = mine_ref[...]
    pl.semaphore_wait(barrier, chans - 1)
    copies = [
        push("chan", chans, step, mine_ref, all_ref.at[me], send_sem, recv_sem)
        for step in range(1, chans)
    ]
    for copy in copies:
        copy.start()
    for copy in copies:
        copy.wait()
    totals = [all_ref[j] for j in range(chans)]
    mean = sum(t[:rows] for t in totals) * (1.0 / (features * chans))
    spread = sum(
        t[rows:] + features * jnp.square(t[:rows] * (1.0 / features) - mean) for t in totals
    ) * (1.0 / (features * chans))
    inverse = lax.rsqrt(spread + NORM_EPS)
    mine_ref[pl.ds(0, rows), :] = mean
    mine_ref[pl.ds(rows, rows), :] = inverse

    def second(h, carry):
        block = flat_ref[h]
        inv = mine_ref[pl.ds(rows + h, 1), :]
        cells_ref[h] = block.T
        unit_ref[h] = ((block - mine_ref[pl.ds(h, 1), :]) * inv).T
        dev_ref[h] = jnp.broadcast_to(inv, (8, columns)).T
        return carry

    lax.fori_loop(0, rows, second, 0)


def entry_norm(lines, features, columns, chans):
    rows = lines.shape[0]
    return pl.pallas_call(
        functools.partial(entry_norm_kernel, chans),
        in_specs=vmem(1),
        out_specs=vmem(3),
        out_shape=(
            jax.ShapeDtypeStruct((rows, columns, features), F32),
            jax.ShapeDtypeStruct((rows, columns, features), F32),
            jax.ShapeDtypeStruct((rows, columns, 8), F32),
        ),
        scratch_shapes=[
            pltpu.VMEM((rows, features, columns), F32),
            pltpu.VMEM((2, features, 128), F32),
            pltpu.VMEM((2 * rows, columns), F32),
            pltpu.VMEM((chans, 2 * rows, columns), F32),
            pltpu.SemaphoreType.DMA((chans,)),
            pltpu.SemaphoreType.DMA((chans,)),
        ],
        compiler_params=params(0),
        name="entry_norm",
    )(lines)


def pack_lanes(flat_ref, place, real, imag):
    flat_ref[0, place, :] = real[:, :128]
    flat_ref[1, place, :] = imag[:, :128]
    flat_ref[2, place, :] = jnp.concatenate([real[:, 128:], imag[:, 128:]], axis=1)


def unpack_lanes(flat_ref, place):
    rest = flat_ref[2, place, :]
    real = jnp.concatenate([flat_ref[0, place, :], rest[:, :64]], axis=1)
    imag = jnp.concatenate([flat_ref[1, place, :], rest[:, 64:]], axis=1)
    return real, imag


def block_of(index, size):
    return pl.ds(pl.multiple_of(index * size, 8), size)


def send_plain(spaces, chunk, flat_ref, send_ref, recv_ref, sems):
    me = lax.axis_index("space")
    copies = []
    for step in list(range(1, spaces)) + [0]:
        peer = lax.rem(me + step, spaces)
        rows = flat_ref[:, block_of(peer, chunk), :].astype(BF)
        if step == 0:
            recv_ref[me] = rows
        else:
            send_ref[peer] = rows
            copy = push("space", spaces, step, send_ref.at[peer], recv_ref.at[me], *sems)
            copy.start()
            copies.append(copy)
    return copies


def take_plain(spaces, chunk, flat_ref, recv_ref, copies):
    me = lax.axis_index("space")
    for step in range(spaces):
        if step:
            copies[step - 1].wait()
        source = lax.rem(me - step + spaces, spaces)
        flat_ref[:, block_of(source, chunk), :] = recv_ref[source].astype(F32)


LEVEL = 32000.0


def send_fixed(spaces, chunk, flat_ref, send_ref, recv_ref, sems):
    me = lax.axis_index("space")
    largest = jnp.max(jnp.abs(flat_ref[...]), axis=1, keepdims=True)
    grade = jnp.ceil(jnp.log2(jnp.maximum(largest, 1e-30)) * 256.0 + 0.01)
    scale = LEVEL * jnp.exp2(grade * (-1.0 / 256.0))
    mark = jnp.broadcast_to(grade, (3, 8, 128))
    copies = []
    for step in list(range(1, spaces)) + [0]:
        peer = lax.rem(me + step, spaces)
        rows = flat_ref[:, block_of(peer, chunk), :]
        coded = jnp.concatenate([jnp.round(rows * scale), mark], axis=1).astype(jnp.int32).astype(jnp.int16)
        if step == 0:
            recv_ref[me] = coded
        else:
            send_ref[peer] = coded
            copy = push("space", spaces, step, send_ref.at[peer], recv_ref.at[me], *sems)
            copy.start()
            copies.append(copy)
    return copies


def take_fixed(spaces, chunk, flat_ref, recv_ref, copies):
    me = lax.axis_index("space")
    for step in range(spaces):
        if step:
            copies[step - 1].wait()
        source = lax.rem(me - step + spaces, spaces)
        values = recv_ref[source].astype(jnp.int32).astype(F32)
        scale = jnp.exp2(values[:, chunk : chunk + 1] * (1.0 / 256.0)) * (1.0 / LEVEL)
        flat_ref[:, block_of(source, chunk), :] = values[:, :chunk] * scale


def exchange_shape(fixed, spaces, chunk):
    if fixed:
        return (spaces, 3, chunk + 8, 128), jnp.int16
    return (spaces, 3, chunk, 128), BF


def pair_inputs(q, spaces, chunk, thick, flat_ref, even_ref):
    p = jnp.maximum(q - 1, 0)
    extra = (q == 0).astype(F32)
    zeroth = jnp.logical_and(lax.axis_index("space") == 0, p == 0).astype(F32)
    parts = [
        unpack_lanes(flat_ref, pl.ds(pl.multiple_of(s * chunk + p * thick, 8), thick)) for s in range(spaces)
    ]
    real = jnp.concatenate([part[0] for part in parts], axis=0)
    imag = jnp.concatenate([part[1] for part in parts], axis=0)
    chosen = imag * (even_ref[...] * zeroth)
    real = real * (1.0 - extra) + chosen * extra
    imag = (imag - chosen) * (1.0 - extra)
    return p, zeroth, jnp.concatenate([real, imag], axis=0)


def pair_outputs(q, p, zeroth, result, spaces, chunk, thick, flat_ref, even_ref, kept_ref):
    half = result.shape[0] // 2
    real, imag = result[:half], result[half:]
    chosen = even_ref[...] * zeroth
    imag = imag * (1.0 - chosen) + kept_ref[...] * chosen

    @pl.when(q == 0)
    def _():
        kept_ref[...] = real

    for s in range(spaces):
        place = pl.ds(pl.multiple_of(s * chunk + p * thick, 8), thick)
        own = slice(s * thick, (s + 1) * thick)
        pack_lanes(flat_ref, place, real[own], imag[own])


def spectral_forward_kernel(
    spaces,
    chans,
    fine,
    x_ref,
    unit_ref,
    gain_ref,
    shift_ref,
    row_ref,
    rowinv_ref,
    col_ref,
    colinv_ref,
    mix_ref,
    bias_ref,
    even_ref,
    middle_ref,
    mid_ref,
    spec_ref,
    first_ref,
    second_ref,
    flat_ref,
    back_ref,
    kept_ref,
    send1_ref,
    recv1_ref,
    send2_ref,
    recv2_ref,
    own_ref,
    s1,
    r1,
    s2,
    r2,
    s3,
    r3,
):
    rows, columns, features = x_ref.shape
    modes = columns // 2
    chunk = flat_ref.shape[1] // spaces
    half = even_ref.shape[0]
    thick = half // spaces
    pairs = chunk // thick
    barrier = pltpu.get_barrier_semaphore()
    signal_peers("space", spaces, barrier)
    signal_peers("chan", chans, barrier)
    gain = gain_ref[...]
    shift = shift_ref[...]

    def to_modes(h, carry):
        normed = halves(unit_ref[h] * gain + shift)
        out = mm3((row_ref[0], row_ref[1]), normed)
        pack_lanes(flat_ref, pl.ds(h, modes, stride=rows), out[:modes], out[modes:])
        return carry

    lax.fori_loop(0, rows, to_modes, 0)
    pl.semaphore_wait(barrier, spaces + chans - 2)
    copies = send_fixed(spaces, chunk, flat_ref, send1_ref, recv1_ref, (s1, r1))
    take_fixed(spaces, chunk, flat_ref, recv1_ref, copies)

    def filter_pair(q, carry):
        p, zeroth, block = pair_inputs(q, spaces, chunk, thick, flat_ref, even_ref)
        spec = mm3((col_ref[0], col_ref[1]), halves(block))
        spec_ref[q] = spec.astype(BF)
        parts = halves(spec)
        straight = mm3(parts, (mix_ref[0, 0, 0], mix_ref[0, 0, 1]))
        crossed = mm3(parts, (mix_ref[0, 1, 0], mix_ref[0, 1, 1]))
        first = jnp.concatenate(
            [
                jnp.maximum(straight[:half] - crossed[half:] + bias_ref[0:1], 0.0),
                jnp.maximum(straight[half:] + crossed[:half] + bias_ref[1:2], 0.0),
            ],
            axis=0,
        )
        first_ref[q] = first.astype(BF)
        parts = halves(first)
        straight = mm3(parts, (mix_ref[1, 0, 0], mix_ref[1, 0, 1]))
        crossed = mm3(parts, (mix_ref[1, 1, 0], mix_ref[1, 1, 1]))
        second = jnp.concatenate(
            [
                straight[:half] - crossed[half:] + bias_ref[2:3],
                straight[half:] + crossed[:half] + bias_ref[3:4],
            ],
            axis=0,
        )
        second = second - jnp.clip(second, -SHRINK_LEVEL, SHRINK_LEVEL)
        second_ref[q] = second.astype(BF)
        if fine:
            result = mm3((colinv_ref[0], colinv_ref[1]), halves(second))
        else:
            result = mm(colinv_ref[0], second.astype(BF))
        pair_outputs(q, p, zeroth, result, spaces, chunk, thick, back_ref, even_ref, kept_ref)
        return carry

    kept_ref[...] = jnp.zeros_like(kept_ref)
    lax.fori_loop(0, pairs + 1, filter_pair, 0)
    if fine:
        copies = send_fixed(spaces, chunk, back_ref, send2_ref, recv2_ref, (s2, r2))
        take_fixed(spaces, chunk, back_ref, recv2_ref, copies)
    else:
        copies = send_plain(spaces, chunk, back_ref, send2_ref, recv2_ref, (s2, r2))
        take_plain(spaces, chunk, back_ref, recv2_ref, copies)

    me = lax.axis_index("chan")
    share = rows // chans
    copies = []
    for step in list(range(1, chans)) + [0]:
        peer = lax.rem(me + step, chans)

        def to_places(i, carry):
            h = peer * share + i
            real, imag = unpack_lanes(back_ref, pl.ds(h, modes, stride=rows))
            block = jnp.concatenate([real, imag], axis=0)
            if fine:
                out = mm3((rowinv_ref[0], rowinv_ref[1]), halves(block))
            else:
                out = mm(rowinv_ref[0], block.astype(BF))
            middle = out + (unit_ref[h] * gain + shift) + x_ref[h]
            middle_ref[h] = middle
            own_ref[peer, pl.ds(pl.multiple_of(i * columns, 16), columns), :] = middle.astype(BF)
            return carry

        lax.fori_loop(0, share, to_places, 0)
        if step:
            copy = push("chan", chans, step, own_ref.at[peer], mid_ref.at[me], s3, r3)
            copy.start()
            copies.append(copy)
        else:
            mid_ref[me] = own_ref[me]
    for copy in copies:
        copy.wait()


def spectral_forward(x, unit, gain, shift, tables, mix, bias, fine, spaces, chans, collective_id):
    rows, columns, features = x.shape
    modes = columns // 2
    total = modes * rows
    chunk = total // spaces
    half = tables["even"].shape[0]
    pairs = chunk // (half // spaces)
    cells = rows * columns // chans
    shape1, kind1 = exchange_shape(True, spaces, chunk)
    shape2, kind2 = exchange_shape(fine, spaces, chunk)
    kept = jax.ShapeDtypeStruct((pairs + 1, 2 * half, features), BF)
    return pl.pallas_call(
        functools.partial(spectral_forward_kernel, spaces, chans, fine),
        in_specs=vmem(11),
        out_specs=vmem(5),
        out_shape=(
            jax.ShapeDtypeStruct((rows, columns, features), F32),
            jax.ShapeDtypeStruct((chans, cells, features), BF),
            kept,
            kept,
            kept,
        ),
        scratch_shapes=[
            pltpu.VMEM((3, total, 128), F32),
            pltpu.VMEM((3, total, 128), F32),
            pltpu.VMEM((half, features), F32),
            pltpu.VMEM(shape1, kind1),
            pltpu.VMEM(shape1, kind1),
            pltpu.VMEM(shape2, kind2),
            pltpu.VMEM(shape2, kind2),
            pltpu.VMEM((chans, cells, features), BF),
        ]
        + [pltpu.SemaphoreType.DMA((spaces,))] * 4
        + [pltpu.SemaphoreType.DMA((chans,))] * 2,
        compiler_params=params(collective_id),
        name="spectral_forward",
    )(
        x,
        unit,
        gain,
        shift,
        tables["row"],
        tables["rowinv"],
        tables["col"],
        tables["colinv"],
        mix,
        bias,
        tables["even"],
    )


def spectral_backward_kernel(
    spaces,
    chans,
    g_ref,
    dv_ref,
    unit_ref,
    dev_ref,
    gain_ref,
    rowinv_t_ref,
    row_t_ref,
    col_ref,
    colinv_ref,
    mix_ref,
    even_ref,
    spec_ref,
    first_ref,
    second_ref,
    out_ref,
    mixgrad_ref,
    biasgrad_ref,
    normgrad_ref,
    flat_ref,
    back_ref,
    kept_ref,
    scaled_ref,
    sums_ref,
    all_ref,
    send1_ref,
    recv1_ref,
    send2_ref,
    recv2_ref,
    s1,
    r1,
    s2,
    r2,
    s3,
    r3,
):
    rows, columns, features = g_ref.shape
    modes = columns // 2
    chunk = flat_ref.shape[1] // spaces
    half = even_ref.shape[0]
    thick = half // spaces
    pairs = chunk // thick
    barrier = pltpu.get_barrier_semaphore()
    signal_peers("space", spaces, barrier)
    signal_peers("chan", chans, barrier)
    gain = gain_ref[...]

    def to_modes(h, carry):
        middle_grad = g_ref[h] + dv_ref[h].astype(F32)
        out_ref[h] = middle_grad
        out = mm(rowinv_t_ref[...], middle_grad.astype(BF))
        pack_lanes(flat_ref, pl.ds(h, modes, stride=rows), out[:modes], out[modes:])
        return carry

    lax.fori_loop(0, rows, to_modes, 0)
    pl.semaphore_wait(barrier, spaces + chans - 2)
    copies = send_plain(spaces, chunk, flat_ref, send1_ref, recv1_ref, (s1, r1))
    take_plain(spaces, chunk, flat_ref, recv1_ref, copies)
    mixgrad_ref[...] = jnp.zeros_like(mixgrad_ref)
    biasgrad_ref[...] = jnp.zeros_like(biasgrad_ref)
    kept_ref[...] = jnp.zeros_like(kept_ref)

    def turned(v):
        return jnp.concatenate([v[half:], -v[:half]], axis=0)

    def note_bias(index, value):
        biasgrad_ref[index : index + 1, :] += jnp.sum(value, axis=0, keepdims=True)

    def filter_pair(q, carry):
        p, zeroth, block = pair_inputs(q, spaces, chunk, thick, flat_ref, even_ref)
        grad = mm(col_ref[0], block.astype(BF))
        grad = jnp.where(second_ref[q].astype(F32) == 0.0, 0.0, grad)
        note_bias(2, grad[:half])
        note_bias(3, grad[half:])
        low = grad.astype(BF)
        first = first_ref[q]
        mixgrad_ref[1, 0] += mm_tn(first, low)
        mixgrad_ref[1, 1] += mm_tn(first, turned(grad).astype(BF))
        straight = mm_nt(low, mix_ref[1, 0, 0])
        crossed = mm_nt(low, mix_ref[1, 1, 0])
        grad = jnp.concatenate(
            [straight[:half] + crossed[half:], straight[half:] - crossed[:half]], axis=0
        )
        grad = jnp.where(first.astype(F32) > 0.0, grad, 0.0)
        note_bias(0, grad[:half])
        note_bias(1, grad[half:])
        low = grad.astype(BF)
        spec = spec_ref[q]
        mixgrad_ref[0, 0] += mm_tn(spec, low)
        mixgrad_ref[0, 1] += mm_tn(spec, turned(grad).astype(BF))
        straight = mm_nt(low, mix_ref[0, 0, 0])
        crossed = mm_nt(low, mix_ref[0, 1, 0])
        grad = jnp.concatenate(
            [straight[:half] + crossed[half:], straight[half:] - crossed[:half]], axis=0
        )
        result = mm(colinv_ref[0], grad.astype(BF))
        pair_outputs(q, p, zeroth, result, spaces, chunk, thick, back_ref, even_ref, kept_ref)
        return carry

    lax.fori_loop(0, pairs + 1, filter_pair, 0)
    copies = send_plain(spaces, chunk, back_ref, send2_ref, recv2_ref, (s2, r2))
    take_plain(spaces, chunk, back_ref, recv2_ref, copies)
    lane = lax.broadcasted_iota(jnp.int32, (columns, 128), 1)
    normgrad_ref[...] = jnp.zeros_like(normgrad_ref)

    def to_places(h, table):
        real, imag = unpack_lanes(back_ref, pl.ds(h, modes, stride=rows))
        block = jnp.concatenate([real, imag], axis=0)
        grad = mm(row_t_ref[...], block.astype(BF)) + out_ref[h]
        unit = unit_ref[h]
        normgrad_ref[0:1, :] += jnp.sum(grad * unit, axis=0, keepdims=True)
        normgrad_ref[1:2, :] += jnp.sum(grad, axis=0, keepdims=True)
        scaled = grad * gain
        scaled_ref[h] = scaled
        one = jnp.sum(scaled, axis=1, keepdims=True)
        two = jnp.sum(scaled * unit, axis=1, keepdims=True)
        table = jnp.where(lane == h, one, table)
        return jnp.where(lane == rows + h, two, table)

    table = lax.fori_loop(0, rows, to_places, jnp.zeros((columns, 128), F32))
    me = lax.axis_index("chan")
    turned_table = table.T[: 2 * rows]
    sums_ref[...] = turned_table
    all_ref[me] = turned_table
    copies = [push("chan", chans, step, sums_ref, all_ref.at[me], s3, r3) for step in range(1, chans)]
    for copy in copies:
        copy.start()
    for copy in copies:
        copy.wait()
    means = sum(all_ref[j] for j in range(chans)) * (1.0 / (features * chans))
    means = jnp.concatenate([means, jnp.zeros((128 - 2 * rows, columns), F32)], axis=0).T

    def finish(h, carry):
        one = jnp.sum(jnp.where(lane == h, means, 0.0), axis=1, keepdims=True)
        two = jnp.sum(jnp.where(lane == rows + h, means, 0.0), axis=1, keepdims=True)
        inverse = dev_ref[h][:, :1]
        out_ref[h] += inverse * (scaled_ref[h] - one - unit_ref[h] * two)
        return carry

    lax.fori_loop(0, rows, finish, 0)


def spectral_backward(g, dv, unit, dev, gain, tables, mix, saved, spaces, chans, collective_id):
    rows, columns, features = g.shape
    modes = columns // 2
    total = modes * rows
    chunk = total // spaces
    half = tables["even"].shape[0]
    shape, kind = exchange_shape(False, spaces, chunk)
    return pl.pallas_call(
        functools.partial(spectral_backward_kernel, spaces, chans),
        in_specs=vmem(14),
        out_specs=vmem(4),
        out_shape=(
            jax.ShapeDtypeStruct((rows, columns, features), F32),
            jax.ShapeDtypeStruct((2, 2, features, features), F32),
            jax.ShapeDtypeStruct((8, features), F32),
            jax.ShapeDtypeStruct((8, features), F32),
        ),
        scratch_shapes=[
            pltpu.VMEM((3, total, 128), F32),
            pltpu.VMEM((3, total, 128), F32),
            pltpu.VMEM((half, features), F32),
            pltpu.VMEM((rows, columns, features), F32),
            pltpu.VMEM((2 * rows, columns), F32),
            pltpu.VMEM((chans, 2 * rows, columns), F32),
        ]
        + [pltpu.VMEM(shape, kind)] * 4
        + [pltpu.SemaphoreType.DMA((spaces,))] * 4
        + [pltpu.SemaphoreType.DMA((chans,))] * 2,
        compiler_params=params(collective_id),
        name="spectral_backward",
    )(
        g,
        dv,
        unit,
        dev,
        gain,
        tables["rowinv_t"],
        tables["row_t"],
        tables["col"],
        tables["colinv"],
        mix,
        tables["even"],
        *saved,
    )


ERF = (0.254829592, -0.284496736, 1.421413741, -1.453152027, 1.061405429)


def gelu_and_slope(v):
    a = jnp.abs(v) * math.sqrt(0.5)
    t = 1.0 / (1.0 + 0.3275911 * a)
    e = jnp.exp(-a * a)
    tail = 0.5 * e * t * (ERF[0] + t * (ERF[1] + t * (ERF[2] + t * (ERF[3] + t * ERF[4]))))
    below = jnp.where(v >= 0.0, 1.0 - tail, tail)
    return v * below, below + v * e * (1.0 / math.sqrt(2.0 * math.pi))


def three_parts(v):
    a = v.astype(BF)
    rest = v - a.astype(F32)
    b = rest.astype(BF)
    return [a, b, (rest - b.astype(F32)).astype(BF)]


def ffn_forward_kernel(
    chans,
    steps,
    mid_ref,
    gain_ref,
    shift_ref,
    up_ref,
    upb_ref,
    down_ref,
    downb_ref,
    home_ref,
    entry_ref,
    unit_ref,
    dev_ref,
    active_ref,
    slope_ref,
    total_ref,
    send_ref,
    land_ref,
    ss,
    rs,
):
    t = pl.program_id(0)
    barrier = pltpu.get_barrier_semaphore()
    features = mid_ref.shape[2]
    cells = mid_ref.shape[1]

    def middle():
        return jnp.concatenate([mid_ref[j].astype(F32) for j in range(chans)], axis=1)

    @pl.when(t == 0)
    def _():
        signal_peers("chan", chans, barrier)
        value = middle()
        mean = jnp.mean(value, axis=1, keepdims=True)
        centred = value - mean
        inverse = lax.rsqrt(jnp.mean(centred * centred, axis=1, keepdims=True) + NORM_EPS)
        unit = centred * inverse
        unit_ref[...] = unit.astype(BF)
        dev_ref[...] = jnp.broadcast_to(inverse, dev_ref.shape)
        entry_ref[...] = (unit * gain_ref[...] + shift_ref[...]).astype(BF)
        total_ref[...] = value + downb_ref[...]

    hidden = mm(entry_ref[...], up_ref[0]) + upb_ref[...]
    active, slope = gelu_and_slope(hidden)
    active = active.astype(BF)
    active_ref[...] = active
    slope_ref[...] = slope.astype(BF)
    total_ref[...] += mm(active, down_ref[0])

    @pl.when(t == steps - 1)
    def _():
        me = lax.axis_index("chan")
        value = total_ref[...]
        mean = jnp.mean(value, axis=1, keepdims=True)
        centred = value - mean
        inverse = lax.rsqrt(jnp.mean(centred * centred, axis=1, keepdims=True) + NORM_EPS)
        outer = value - middle()
        stats = jnp.concatenate(
            three_parts(mean) + three_parts(inverse) + [jnp.zeros((cells, 256 - features - 6), BF)], axis=1
        )
        pl.semaphore_wait(barrier, chans - 1)
        for j in range(chans):
            send_ref[j] = jnp.concatenate(
                [outer[:, j * features : (j + 1) * features].astype(BF), stats], axis=1
            )
        copies = []
        for step in range(1, chans):
            peer = lax.rem(me + step, chans)
            copy = push("chan", chans, step, send_ref.at[peer], land_ref.at[me], ss, rs)
            copy.start()
            copies.append(copy)
        home_ref[me] = send_ref[me]
        for step in range(1, chans):
            copies[step - 1].wait()
            source = lax.rem(me - step + chans, chans)
            home_ref[source] = land_ref[source]


def fixed_block(shape):
    return pl.BlockSpec(shape, lambda t: (0,) * len(shape))


def ffn_forward(mid, gain, shift, up, upb, down, downb, chans, collective_id):
    cells, features = mid.shape[1:]
    width = features * chans
    local = up.shape[2]
    tile = 256
    per = local // tile
    steps = chans * per
    hidden = chans * local
    return pl.pallas_call(
        functools.partial(ffn_forward_kernel, chans, steps),
        grid=(steps,),
        in_specs=[
            fixed_block((chans, cells, features)),
            fixed_block((1, width)),
            fixed_block((1, width)),
            pl.BlockSpec((1, width, tile), lambda t: (t // per, 0, t % per)),
            pl.BlockSpec((1, tile), lambda t: (0, t)),
            pl.BlockSpec((1, tile, width), lambda t: (t // per, t % per, 0)),
            fixed_block((1, width)),
        ],
        out_specs=[
            fixed_block((chans, cells, 256)),
            fixed_block((cells, width)),
            fixed_block((cells, width)),
            fixed_block((cells, 128)),
            pl.BlockSpec((cells, tile), lambda t: (0, t)),
            pl.BlockSpec((cells, tile), lambda t: (0, t)),
        ],
        out_shape=(
            jax.ShapeDtypeStruct((chans, cells, 256), BF),
            jax.ShapeDtypeStruct((cells, width), BF),
            jax.ShapeDtypeStruct((cells, width), BF),
            jax.ShapeDtypeStruct((cells, 128), F32),
            jax.ShapeDtypeStruct((cells, hidden), BF),
            jax.ShapeDtypeStruct((cells, hidden), BF),
        ),
        scratch_shapes=[
            pltpu.VMEM((cells, width), F32),
            pltpu.VMEM((chans, cells, 256), BF),
            pltpu.VMEM((chans, cells, 256), BF),
            pltpu.SemaphoreType.DMA((chans,)),
            pltpu.SemaphoreType.DMA((chans,)),
        ],
        compiler_params=params(collective_id),
        name="ffn_forward",
    )(mid, gain, shift, up, upb, down, downb)


def ffn_backward_kernel(
    chans,
    steps,
    more,
    *refs,
):
    if more:
        prev_down_ref, prev_up_ref = refs[:2]
        refs = refs[2:]
    (
        g_ref,
        entry_ref,
        unit_ref,
        dev_ref,
        gain_ref,
        active_ref,
        slope_ref,
        up_ref,
        down_ref,
        home_ref,
        gdown_ref,
        gup_ref,
        gupb_ref,
        small_ref,
        upper_ref,
        total_ref,
        land_ref,
        send_ref,
        last_ref,
        s1,
        r1,
        s2,
        r2,
    ) = refs
    t = pl.program_id(0)
    barrier = pltpu.get_barrier_semaphore()
    features = g_ref.shape[2]
    width = features * chans
    me = lax.axis_index("chan")

    @pl.when(t == 0)
    def _():
        signal_peers("chan", chans, barrier)
        pl.semaphore_wait(barrier, chans - 1)
        copies = []
        for step in range(1, chans):
            peer = lax.rem(me + step, chans)
            copy = push("chan", chans, step, g_ref.at[peer], land_ref.at[me], s1, r1)
            copy.start()
            copies.append(copy)
        land_ref[me] = g_ref[me]
        total_ref[...] = jnp.zeros_like(total_ref)
        for copy in copies:
            copy.wait()
        upper = jnp.concatenate([land_ref[j].astype(F32) for j in range(chans)], axis=1)
        upper_ref[...] = upper.astype(BF)
        small_ref[...] = jnp.zeros_like(small_ref)
        small_ref[2:3, :] = jnp.sum(upper, axis=0, keepdims=True)

    upper = upper_ref[...]
    gdown = mm_tn(active_ref[...], upper)
    lower = mm_nt(upper, down_ref[0]) * slope_ref[...].astype(F32)
    gupb_ref[...] = jnp.sum(lower, axis=0, keepdims=True)
    lower = lower.astype(BF)
    gup = mm_tn(entry_ref[...], lower)
    if more:
        gdown += prev_down_ref[0].astype(F32)
        gup += prev_up_ref[0].astype(F32)
    gdown_ref[0] = gdown.astype(BF)
    gup_ref[0] = gup.astype(BF)
    total_ref[...] += mm_nt(lower, up_ref[0])

    @pl.when(t == steps - 1)
    def _():
        grad = total_ref[...]
        unit = unit_ref[...].astype(F32)
        small_ref[0:1, :] = jnp.sum(grad * unit, axis=0, keepdims=True)
        small_ref[1:2, :] = jnp.sum(grad, axis=0, keepdims=True)
        scaled = grad * gain_ref[...]
        one = jnp.mean(scaled, axis=1, keepdims=True)
        two = jnp.mean(scaled * unit, axis=1, keepdims=True)
        result = dev_ref[:, :1] * (scaled - one - unit * two)
        for j in range(chans):
            send_ref[j] = result[:, j * features : (j + 1) * features].astype(BF)
        copies = []
        for step in range(1, chans):
            peer = lax.rem(me + step, chans)
            copy = push("chan", chans, step, send_ref.at[peer], last_ref.at[me], s2, r2)
            copy.start()
            copies.append(copy)
        home_ref[me] = send_ref[me]
        for step in range(1, chans):
            copies[step - 1].wait()
            source = lax.rem(me - step + chans, chans)
            home_ref[source] = last_ref[source]


def ffn_backward(g, saved, gain, up, down, before, chans, collective_id):
    entry, unit, dev, active, slope = saved
    cells, features = g.shape[1:]
    width = features * chans
    local = up.shape[2]
    tile = 256
    per = local // tile
    steps = chans * per
    hidden = chans * local
    down_spec = pl.BlockSpec((1, tile, width), lambda t: (t // per, t % per, 0))
    up_spec = pl.BlockSpec((1, width, tile), lambda t: (t // per, 0, t % per))
    more = before is not None
    return pl.pallas_call(
        functools.partial(ffn_backward_kernel, chans, steps, more),
        grid=(steps,),
        in_specs=([down_spec, up_spec] if more else [])
        + [
            fixed_block((chans, cells, features)),
            fixed_block((cells, width)),
            fixed_block((cells, width)),
            fixed_block((cells, 128)),
            fixed_block((1, width)),
            pl.BlockSpec((cells, tile), lambda t: (0, t)),
            pl.BlockSpec((cells, tile), lambda t: (0, t)),
            up_spec,
            down_spec,
        ],
        out_specs=[
            fixed_block((chans, cells, features)),
            down_spec,
            up_spec,
            pl.BlockSpec((1, tile), lambda t: (0, t)),
            fixed_block((8, width)),
        ],
        out_shape=(
            jax.ShapeDtypeStruct((chans, cells, features), BF),
            jax.ShapeDtypeStruct((chans, local, width), BF),
            jax.ShapeDtypeStruct((chans, width, local), BF),
            jax.ShapeDtypeStruct((1, hidden), F32),
            jax.ShapeDtypeStruct((8, width), F32),
        ),
        scratch_shapes=[
            pltpu.VMEM((cells, width), BF),
            pltpu.VMEM((cells, width), F32),
            pltpu.VMEM((chans, cells, features), BF),
            pltpu.VMEM((chans, cells, features), BF),
            pltpu.VMEM((chans, cells, features), BF),
        ]
        + [pltpu.SemaphoreType.DMA((chans,))] * 4,
        compiler_params=params(collective_id),
        name="ffn_backward",
    )(*(before if more else ()), g, entry, unit, dev, gain, active, slope, up, down)


def block_diagonal(weights):
    blocks = weights.shape[1]
    rows = [
        jnp.concatenate(
            [weights[:, b] if b == other else jnp.zeros_like(weights[:, b]) for other in range(blocks)], axis=2
        )
        for b in range(blocks)
    ]
    return jnp.concatenate(rows, axis=1)


def diagonal_blocks(matrices, blocks):
    size = matrices.shape[-1] // blocks
    return jnp.stack(
        [matrices[:, b * size : (b + 1) * size, b * size : (b + 1) * size] for b in range(blocks)], axis=1
    )


def shards_fast(
    current_atmosphere,
    truth_one,
    truth_two,
    storm_codes,
    pre_gain,
    pre_shift,
    mix_weight_in,
    mix_bias_in,
    mix_weight_out,
    mix_bias_out,
    post_gain,
    post_shift,
    up_weight,
    up_bias,
    down_weight,
    down_bias,
):
    rows, merged = current_atmosphere.shape[1:]
    columns = W
    features = merged // columns
    spaces = lax.axis_size("space")
    chans = lax.axis_size("chan")
    height = rows * spaces
    width = features * chans
    blocks = mix_weight_in.shape[1]
    thick = 2 * rows
    cells = rows * columns // chans

    forward, inverse = row_constants(columns)
    column = column_constants(height, rows, 2)
    even = (np.arange(spaces * thick) // rows % 2 == 0).astype(np.float32)
    tables = {
        "row": jnp.stack(const_halves(forward)),
        "rowinv": jnp.stack(const_halves(inverse)),
        "rowinv_t": const_halves(inverse.T)[0],
        "row_t": const_halves(forward.T)[0],
        "col": jnp.stack(const_halves(column)),
        "colinv": jnp.stack(const_halves(column.T)),
        "even": jnp.asarray(np.repeat(even[:, None], features, axis=1)),
    }

    def lines(flat):
        return flat.reshape(rows, merged // 128, 128)

    def flat(line_field):
        return line_field.reshape(1, rows, merged)

    weight = (storm_codes.astype(F32) / 64.0).reshape(1, 1, 1)
    mix = jnp.stack([block_diagonal(mix_weight_in), block_diagonal(mix_weight_out)])
    high = lax.reduce_precision(mix, 8, 7)
    mix = jnp.stack([high.astype(BF), (mix - high).astype(BF)], axis=2)
    bias = jnp.concatenate([mix_bias_in.reshape(2, features), mix_bias_out.reshape(2, features)])
    bias = jnp.concatenate([bias, jnp.zeros((4, features), F32)])
    gain_row = pre_gain.reshape(1, features)
    shift_row = pre_shift.reshape(1, features)

    up_all = lax.all_gather(up_weight, "chan", axis=0)
    down_all = lax.all_gather(down_weight, "chan", axis=0)
    small = lax.all_gather(
        jnp.concatenate([post_gain, post_shift, down_bias.astype(F32), up_bias.astype(F32)]), "chan", axis=0
    )
    gain_all = small[:, :features].reshape(1, width)
    shift_all = small[:, features : 2 * features].reshape(1, width)
    downb_all = small[:, 2 * features : 3 * features].reshape(1, width)
    upb_all = small[:, 3 * features :].reshape(1, -1)

    x_one, unit_one, dev_one = entry_norm(lines(current_atmosphere), features, columns, chans)

    def forward_block(x, unit, fine, number):
        middle, mid, *spectral_saved = spectral_forward(
            x, unit, gain_row, shift_row, tables, mix, bias, fine, spaces, chans, 1 + number
        )
        home, *ffn_saved = ffn_forward(
            mid, gain_all, shift_all, up_all, upb_all, down_all, downb_all, chans, 3
        )
        home = home.reshape(rows, columns, 256).astype(F32)
        result = home[:, :, :features] + middle
        mean = home[:, :, features : features + 1] + (
            home[:, :, features + 1 : features + 2] + home[:, :, features + 2 : features + 3]
        )
        dev = home[:, :, features + 3 : features + 4] + (
            home[:, :, features + 4 : features + 5] + home[:, :, features + 5 : features + 6]
        )
        return result, mean, dev, spectral_saved, ffn_saved

    first, mean, dev_two, spectral_one, ffn_one = forward_block(x_one, unit_one, True, 0)
    unit_two = (first - mean) * dev_two
    dev_two = jnp.broadcast_to(dev_two, (rows, columns, 8))
    second, _, _, spectral_two, ffn_two = forward_block(first, unit_two, False, 1)

    target_two = enter(lines(truth_two), features, columns)
    target_one = enter(lines(truth_one), features, columns)

    def backward_block(g, unit, dev, spectral_saved, ffn_saved, before):
        low = g.astype(BF).reshape(chans, cells, features)
        dv, gdown, gup, gupb, dense = ffn_backward(low, ffn_saved, gain_all, up_all, down_all, before, chans, 4 + (before is not None))
        out, mixgrad, biasgrad, normgrad = spectral_backward(
            g,
            dv.reshape(rows, columns, features),
            unit,
            dev,
            gain_row,
            tables,
            mix,
            spectral_saved,
            spaces,
            chans,
            6,
        )
        return out, (gdown, gup), (gupb, dense), (mixgrad, biasgrad, normgrad)

    carried, dense_late, small_late, mix_late = backward_block(
        weight * (second - target_two), unit_two, dev_two, spectral_two, ffn_two, None
    )
    state_grad, dense_all, small_early, mix_early = backward_block(
        weight * (first - target_one) + carried, unit_one, dev_one, spectral_one, ffn_one, dense_late
    )

    gdown = lax.psum_scatter(dense_all[0], "chan", scatter_dimension=0)
    gup = lax.psum_scatter(dense_all[1], "chan", scatter_dimension=0)
    gdown, gup = lax.psum((gdown, gup), "space")
    gupb, dense = jax.tree.map(jnp.add, small_early, small_late)
    packed = jnp.concatenate(
        [gupb.reshape(chans, -1)] + [dense[i].reshape(chans, features) for i in range(3)], axis=1
    )
    packed = lax.psum_scatter(packed, "chan", scatter_dimension=0)
    mixgrad, biasgrad, normgrad = jax.tree.map(jnp.add, mix_early, mix_late)
    packed, mixgrad, biasgrad, normgrad = lax.psum((packed, mixgrad, biasgrad, normgrad), "space")
    local = up_weight.shape[1]

    return (
        flat(leave(first)),
        flat(leave(second)),
        flat(leave(state_grad)),
        normgrad[0],
        normgrad[1],
        diagonal_blocks(mixgrad[0], blocks),
        biasgrad[0:2].reshape(2, blocks, -1),
        diagonal_blocks(mixgrad[1], blocks),
        biasgrad[2:4].reshape(2, blocks, -1),
        packed[local : local + features],
        packed[local + features : local + 2 * features],
        gup.astype(F32),
        packed[:local],
        gdown.astype(F32),
        packed[local + 2 * features :],
    )


def suits(mesh):
    spaces, chans = mesh.shape["space"], mesh.shape["chan"]
    return (spaces, chans) == (8, 4)


def solution(mesh):
    in_specs = (
        P(None, "space", "chan"),
        P(None, "space", "chan"),
        P(None, "space", "chan"),
        P(),
        P("chan"),
        P("chan"),
        P(None, "chan", None, None),
        P(None, "chan", None),
        P(None, "chan", None, None),
        P(None, "chan", None),
        P("chan"),
        P("chan"),
        P(None, "chan"),
        P("chan"),
        P("chan", None),
        P("chan"),
    )
    out_specs = (
        P(None, "space", "chan"),
        P(None, "space", "chan"),
        P(None, "space", "chan"),
        P("chan"),
        P("chan"),
        P(None, "chan", None, None),
        P(None, "chan", None),
        P(None, "chan", None, None),
        P(None, "chan", None),
        P("chan"),
        P("chan"),
        P(None, "chan"),
        P("chan"),
        P("chan", None),
        P("chan"),
    )
    return jax.shard_map(shards_fast if suits(mesh) else shards, mesh=mesh, in_specs=in_specs, out_specs=out_specs, check_vma=False)
```

```python
import functools
import math
import types

import jax
import jax.numpy as jnp
import ml_dtypes
import numpy as np
from jax import lax
from jax.experimental import pallas as pl
from jax.experimental.pallas import tpu as pltpu
from jax.sharding import PartitionSpec as P

W = 160
KW = 81


NORM_EPS = 1e-06
SHRINK_LEVEL = 0.01
FULL_PRECISION = lax.Precision.HIGHEST


def exact_gelu(values):
    return jax.nn.gelu(values, approximate=False)


def shrink(values):
    return values - jnp.clip(values, -SHRINK_LEVEL, SHRINK_LEVEL)


def block_mix(values, matrix):
    return jnp.einsum("bhkni,nio->bhkno", values, matrix, precision=FULL_PRECISION)


def row_tables(columns, kept_modes, padded_modes):
    places = jnp.arange(columns, dtype=jnp.int32)[:, None]
    orders = jnp.arange(padded_modes, dtype=jnp.int32)[None, :]
    angles = 2.0 * math.pi / columns * (places * orders % columns).astype(jnp.float32)
    factor = 1.0 / math.sqrt(columns)
    single = jnp.logical_or(orders == 0, 2 * orders == columns)
    doubled = jnp.where(single, 1.0, 2.0).astype(jnp.float32)
    used = jnp.where(orders < kept_modes, 1.0, 0.0).astype(jnp.float32)
    return (
        jnp.cos(angles) * factor * used,
        -jnp.sin(angles) * factor * used,
        jnp.transpose(jnp.cos(angles) * doubled * factor * used),
        jnp.transpose(jnp.sin(angles) * doubled * factor * used),
    )


def along_rows(values, tables):
    return jnp.stack(
        [
            jnp.einsum("bhwc,wk->bhkc", values, tables[0], precision=FULL_PRECISION),
            jnp.einsum("bhwc,wk->bhkc", values, tables[1], precision=FULL_PRECISION),
        ]
    )


def along_rows_back(paired, tables):
    return jnp.einsum("bhkc,wk->bhwc", paired[0], tables[0], precision=FULL_PRECISION) + jnp.einsum(
        "bhkc,wk->bhwc", paired[1], tables[1], precision=FULL_PRECISION
    )


def rows_inverse(paired, tables):
    return jnp.einsum("bhkc,kw->bhwc", paired[0], tables[2], precision=FULL_PRECISION) - jnp.einsum(
        "bhkc,kw->bhwc", paired[1], tables[3], precision=FULL_PRECISION
    )


def rows_inverse_back(values, tables):
    return jnp.stack(
        [
            jnp.einsum("bhwc,kw->bhkc", values, tables[2], precision=FULL_PRECISION),
            -jnp.einsum("bhwc,kw->bhkc", values, tables[3], precision=FULL_PRECISION),
        ]
    )


def column_tables(height):
    orders = jnp.arange(height, dtype=jnp.int32)[:, None]
    places = jnp.arange(height, dtype=jnp.int32)[None, :]
    angles = 2.0 * math.pi / height * (orders * places % height).astype(jnp.float32)
    factor = 1.0 / math.sqrt(height)
    return (jnp.cos(angles) * factor, jnp.sin(angles) * factor)


def to_freq(matrix, values):
    return jnp.einsum("kh,bhmc->bkmc", matrix, values, precision=FULL_PRECISION)


def from_freq(matrix, values):
    return jnp.einsum("kh,bkmc->bhmc", matrix, values, precision=FULL_PRECISION)


def spectral_core(paired, w_first, b_first, w_second, b_second):
    samples, height, kept_modes, channels = paired.shape[1:]
    blocks, block_size = (w_first.shape[1], w_first.shape[2])
    cosine, sine_table = column_tables(height)
    real_in, imag_in = (paired[0], paired[1])
    split_form = (samples, height, kept_modes, blocks, block_size)
    real_part = (to_freq(cosine, real_in) + to_freq(sine_table, imag_in)).reshape(split_form)
    imag_part = (to_freq(cosine, imag_in) - to_freq(sine_table, real_in)).reshape(split_form)
    first_real = jax.nn.relu(
        block_mix(real_part, w_first[0]) - block_mix(imag_part, w_first[1]) + b_first[0]
    )
    first_imag = jax.nn.relu(
        block_mix(imag_part, w_first[0]) + block_mix(real_part, w_first[1]) + b_first[1]
    )
    joined_form = (samples, height, kept_modes, channels)
    second_real = shrink(
        block_mix(first_real, w_second[0]) - block_mix(first_imag, w_second[1]) + b_second[0]
    ).reshape(joined_form)
    second_imag = shrink(
        block_mix(first_imag, w_second[0]) + block_mix(first_real, w_second[1]) + b_second[1]
    ).reshape(joined_form)
    out_real = from_freq(cosine, second_real) - from_freq(sine_table, second_imag)
    out_imag = from_freq(cosine, second_imag) + from_freq(sine_table, second_real)
    return jnp.stack([out_real, out_imag])


def column_layout(paired):
    return lax.all_to_all(paired, "space", split_axis=3, concat_axis=2, tiled=True)


def row_layout(paired):
    return lax.all_to_all(
        paired.astype(jnp.bfloat16), "space", split_axis=2, concat_axis=3, tiled=True
    ).astype(paired.dtype)


def norm_forward(values, gain, offset):
    width_all = values.shape[-1] * lax.axis_size("chan")
    totals = lax.psum((jnp.sum(values, axis=-1), jnp.sum(values * values, axis=-1)), "chan")
    average = totals[0] / width_all
    variance = totals[1] / width_all - average * average
    inverse_dev = lax.rsqrt(variance + NORM_EPS)[..., None]
    scaled = (values - average[..., None]) * inverse_dev
    return (scaled * gain + offset, (scaled, inverse_dev))


def norm_backward(gradient, gain, saved):
    scaled, inverse_dev = saved
    width_all = scaled.shape[-1] * lax.axis_size("chan")
    scaled_grad = gradient * gain
    totals = lax.psum(
        (jnp.sum(scaled_grad, axis=-1), jnp.sum(scaled_grad * scaled, axis=-1)), "chan"
    )
    values_grad = inverse_dev * (
        scaled_grad - totals[0][..., None] / width_all - scaled * (totals[1][..., None] / width_all)
    )
    return (
        values_grad,
        jnp.sum(gradient * scaled, axis=(0, 1, 2)),
        jnp.sum(gradient, axis=(0, 1, 2)),
    )


def shards(
    current_atmosphere,
    truth_one,
    truth_two,
    storm_codes,
    pre_gain,
    pre_shift,
    mix_weight_in,
    mix_bias_in,
    mix_weight_out,
    mix_bias_out,
    post_gain,
    post_shift,
    up_weight,
    up_bias,
    down_weight,
    down_bias,
):
    samples, rows_here, merged = current_atmosphere.shape
    columns = W
    channels = merged // columns
    total_rows = samples * rows_here * columns
    space_count = lax.axis_size("space")
    padded_modes = (KW + space_count - 1) // space_count * space_count
    tables = row_tables(columns, KW, padded_modes)

    def to_cells(flat_field):
        return jnp.transpose(
            flat_field.reshape(samples, rows_here, channels, columns), (0, 1, 3, 2)
        )

    def to_flat(cell_field):
        return jnp.transpose(cell_field, (0, 1, 3, 2)).reshape(samples, rows_here, merged)

    start_cells = to_cells(current_atmosphere)
    target_one = to_cells(truth_one)
    target_two = to_cells(truth_two)
    weight_of = (storm_codes.astype(jnp.float32) / 64.0).reshape(-1, 1, 1, 1)
    full_up, full_down, full_up_bias, full_down_bias = (up_weight, down_weight, up_bias, down_bias)

    def mlp_forward(inputs):
        gathered = lax.all_gather(inputs, "chan", axis=1, tiled=True)
        hidden = jnp.dot(
            gathered, full_up, preferred_element_type=jnp.float32
        ) + full_up_bias.astype(jnp.float32)
        active_full, gelu_pull = jax.vjp(exact_gelu, hidden)
        active = active_full.astype(jnp.bfloat16)
        product = jnp.dot(active, full_down, preferred_element_type=jnp.float32)
        output = lax.psum_scatter(
            product.astype(jnp.bfloat16), "chan", scatter_dimension=1, tiled=True
        ).astype(jnp.float32) + full_down_bias.astype(jnp.float32)
        return (output, (gathered, gelu_pull, active))

    def mlp_backward(gradient, saved):
        gathered, gelu_pull, active = saved
        grad_low = gradient.astype(jnp.bfloat16)
        grad_rows = lax.all_gather(grad_low, "chan", axis=1, tiled=True)
        down_bias_grad = jnp.sum(grad_low.astype(jnp.float32), axis=0)
        down_grad = jnp.dot(active.T, grad_rows, preferred_element_type=jnp.float32)
        active_grad = jnp.dot(grad_rows, full_down.T, preferred_element_type=jnp.float32)
        hidden_grad = gelu_pull(active_grad)[0].astype(jnp.bfloat16)
        up_grad = jnp.dot(gathered.T, hidden_grad, preferred_element_type=jnp.float32)
        up_bias_grad = jnp.sum(hidden_grad.astype(jnp.float32), axis=0)
        input_part = jnp.dot(hidden_grad, full_up.T, preferred_element_type=jnp.float32)
        input_grad = lax.psum_scatter(
            input_part.astype(jnp.bfloat16), "chan", scatter_dimension=1, tiled=True
        ).astype(jnp.float32)
        return (input_grad, (up_grad, up_bias_grad, down_grad, down_bias_grad))

    def forward_block(values):
        normed, first_saved = norm_forward(values, pre_gain, pre_shift)
        modal_in = column_layout(along_rows(normed, tables))
        filtered, core_pull = jax.vjp(
            spectral_core, modal_in, mix_weight_in, mix_bias_in, mix_weight_out, mix_bias_out
        )
        middle = rows_inverse(row_layout(filtered), tables) + normed + values
        entry, second_residuals = norm_forward(middle, post_gain, post_shift)
        output, mlp_saved = mlp_forward(entry.astype(jnp.bfloat16).reshape(total_rows, channels))
        return (
            output.reshape(values.shape) + middle,
            (first_saved, core_pull, second_residuals, mlp_saved),
        )

    def backward_block(gradient, saved):
        first_saved, core_pull, second_residuals, mlp_saved = saved
        mlp_grad, dense_grads = mlp_backward(gradient.reshape(total_rows, channels), mlp_saved)
        middle_part, post_gain_grad, post_shift_grad = norm_backward(
            mlp_grad.reshape(gradient.shape), post_gain, second_residuals
        )
        middle_grad = middle_part + gradient
        filter_grads = core_pull(column_layout(rows_inverse_back(middle_grad, tables)))
        normed_grad = along_rows_back(row_layout(filter_grads[0]), tables) + middle_grad
        input_part, pre_gain_grad, pre_shift_grad = norm_backward(
            normed_grad, pre_gain, first_saved
        )
        return (
            input_part + middle_grad,
            (pre_gain_grad, pre_shift_grad)
            + tuple(filter_grads[1:])
            + (post_gain_grad, post_shift_grad)
            + dense_grads,
        )

    first_out, first_saved_all = forward_block(start_cells)
    second_out, second_saved_all = forward_block(first_out)
    carried, grads_late = backward_block(weight_of * (second_out - target_two), second_saved_all)
    input_grad, grads_early = backward_block(
        weight_of * (first_out - target_one) + carried, first_saved_all
    )
    summed = jax.tree.map(jnp.add, grads_early, grads_late)
    (
        sum_pre_gain,
        sum_pre_shift,
        sum_mix_w_in,
        summed_mixing_bias_input,
        sum_mix_w_out,
        sum_mix_b_out,
        sum_post_gain,
        sum_post_shift,
        sum_up,
        sum_up_bias,
        sum_down,
        sum_down_bias,
    ) = summed
    totals = (
        lax.psum(sum_pre_gain.astype(jnp.bfloat16), "space").astype(jnp.float32),
        lax.psum(sum_pre_shift.astype(jnp.bfloat16), "space").astype(jnp.float32),
        lax.psum(sum_mix_w_in.astype(jnp.bfloat16), "space").astype(jnp.float32),
        lax.psum(summed_mixing_bias_input.astype(jnp.bfloat16), "space").astype(jnp.float32),
        lax.psum(sum_mix_w_out.astype(jnp.bfloat16), "space").astype(jnp.float32),
        lax.psum(sum_mix_b_out.astype(jnp.bfloat16), "space").astype(jnp.float32),
        lax.psum(sum_post_gain.astype(jnp.bfloat16), "space").astype(jnp.float32),
        lax.psum(sum_post_shift.astype(jnp.bfloat16), "space").astype(jnp.float32),
        lax.psum(sum_up.astype(jnp.bfloat16), "space").astype(jnp.float32),
        lax.psum(sum_up_bias.astype(jnp.bfloat16), "space").astype(jnp.float32),
        lax.psum(sum_down.astype(jnp.bfloat16), "space").astype(jnp.float32),
        lax.psum(sum_down_bias.astype(jnp.bfloat16), "space").astype(jnp.float32),
    )
    return (to_flat(first_out), to_flat(second_out), to_flat(input_grad)) + tuple(totals)


BF = jnp.bfloat16
F32 = jnp.float32
MESH_ID = pl.DeviceIdType.MESH
VMEM_BYTES = 66 * 1024 * 1024 - 1024 * 1024


def mm(a, b):
    return jnp.dot(a, b, preferred_element_type=F32)


def mm_nt(a, b):
    return lax.dot_general(a, b, (((1,), (1,)), ((), ())), preferred_element_type=F32)


def mm_tn(a, b):
    return lax.dot_general(a, b, (((0,), (0,)), ((), ())), preferred_element_type=F32)


def halves(v):
    high = v.astype(BF)
    return high, (v - high.astype(F32)).astype(BF)


def mm3(a, b):
    return mm(a[0], b[0]) + (mm(a[0], b[1]) + mm(a[1], b[0]))


def const_halves(table):
    table = np.asarray(table, np.float32)
    high = table.astype(ml_dtypes.bfloat16)
    low = (table - high.astype(np.float32)).astype(ml_dtypes.bfloat16)
    return jnp.asarray(high), jnp.asarray(low)


def row_constants(columns):
    half = columns // 2
    place = np.arange(columns)
    mode = np.arange(half)
    angle = 2.0 * np.pi * np.outer(mode, place) / columns
    real = np.cos(angle)
    imag = -np.sin(angle)
    imag[0] = np.cos(np.pi * place)
    forward = np.concatenate([real, imag]) / np.sqrt(columns)
    weight = np.where(mode == 0, 1.0, 2.0)
    inverse = (forward * np.concatenate([weight, weight])[:, None]).T
    return forward, inverse


def column_constants(height, rows, group):
    owners = height // rows
    angle = 2.0 * np.pi * np.outer(np.arange(height), np.arange(height)) / height
    cosine = np.cos(angle) / np.sqrt(height)
    sine = np.sin(angle) / np.sqrt(height)

    def spread(matrix):
        wide = np.zeros((group, height, owners, group, rows))
        for column in range(group):
            wide[column, :, :, column, :] = matrix.reshape(height, owners, rows)
        return wide.reshape(group * height, owners * group * rows)

    cosine, sine = spread(cosine), spread(sine)
    return np.block([[cosine, sine], [-sine, cosine]])


def signal_peers(axis, count, barrier):
    me = lax.axis_index(axis)
    for step in range(1, count):
        pl.semaphore_signal(
            barrier, inc=1, device_id={axis: lax.rem(me + step, count)}, device_id_type=MESH_ID
        )


def push(axis, count, step, source, target, send_sem, recv_sem):
    peer = lax.rem(lax.axis_index(axis) + step, count)
    return pltpu.make_async_remote_copy(
        src_ref=source,
        dst_ref=target,
        send_sem=send_sem.at[step],
        recv_sem=recv_sem.at[step],
        device_id={axis: peer},
        device_id_type=MESH_ID,
    )


def params(collective_id=None):
    return pltpu.CompilerParams(
        collective_id=collective_id,
        has_side_effects=collective_id is not None,
        vmem_limit_bytes=VMEM_BYTES,
    )


def launch(body, ins, outs, scratch, name, collective_id=None, in_specs=None, out_specs=None, grid=()):
    in_specs, out_specs = in_specs or {}, out_specs or {}
    names = list(ins) + list(outs) + list(scratch)
    whole = pl.BlockSpec(memory_space=pltpu.VMEM)
    results = pl.pallas_call(
        lambda *refs: body(types.SimpleNamespace(**dict(zip(names, refs)))),
        grid=grid,
        in_specs=[in_specs.get(key, whole) for key in ins],
        out_specs=[out_specs.get(key, whole) for key in outs],
        out_shape=[jax.ShapeDtypeStruct(*outs[key]) for key in outs],
        scratch_shapes=list(scratch.values()),
        compiler_params=params(collective_id),
        name=name,
    )(*ins.values())
    return dict(zip(outs, results))


IN_PLACE = pl.BlockSpec(memory_space=pl.ANY)


def sems(count):
    return pltpu.SemaphoreType.DMA((count,))


def run_copies(copies):
    for copy in copies:
        copy.start()
    for copy in copies:
        copy.wait()


def cells_from_lines(lines_ref, h, scratch_ref):
    features = scratch_ref.shape[1]
    per = 640 // W
    groups = features // per
    wide = jnp.concatenate(
        [lines_ref[h, pl.ds(part, groups, stride=5), :] for part in range(5)], axis=1
    )
    for part in range(per):
        piece = wide[:, part * W : (part + 1) * W]
        scratch_ref[0, pl.ds(part, groups, stride=per), :] = piece[:, :128]
        scratch_ref[1, pl.ds(part, groups, stride=per), :] = jnp.concatenate(
            [piece[:, 128:], jnp.zeros((groups, 256 - W), F32)], axis=1
        )
    return jnp.concatenate([scratch_ref[0], scratch_ref[1][:, : W - 128]], axis=1)


def enter(lines_ref, cells_ref, scratch_ref):
    def row(h, carry):
        cells_ref[h] = cells_from_lines(lines_ref, h, scratch_ref).T
        return carry

    lax.fori_loop(0, lines_ref.shape[0], row, 0)


def leave(cells_ref, lines_ref, scratch_ref):
    features = scratch_ref.shape[1]
    per = 640 // W
    groups = features // per

    def row(h, carry):
        block = cells_ref[h].T
        scratch_ref[0] = block[:, :128]
        scratch_ref[1] = jnp.concatenate([block[:, 128:], jnp.zeros((features, 256 - W), F32)], axis=1)
        wide = jnp.concatenate(
            [
                piece
                for part in range(per)
                for piece in (
                    scratch_ref[0, pl.ds(part, groups, stride=per), :],
                    scratch_ref[1, pl.ds(part, groups, stride=per), :][:, : W - 128],
                )
            ],
            axis=1,
        )
        for part in range(5):
            lines_ref[h, pl.ds(part, groups, stride=5), :] = wide[:, part * 128 : (part + 1) * 128]
        return carry

    lax.fori_loop(0, lines_ref.shape[0], row, 0)


def entry_norm(lines, vectors, sizes):
    rows, features, columns, spaces, chans = sizes

    def body(r):
        me = lax.axis_index("chan")
        barrier = pltpu.get_barrier_semaphore()
        signal_peers("chan", chans, barrier)

        def first(h, carry):
            block = cells_from_lines(r.lines, h, r.turn)
            r.flat[h] = block
            total = jnp.sum(block, axis=0, keepdims=True)
            centred = block - total * (1.0 / features)
            r.mine[pl.ds(h, 1), :] = total
            r.mine[pl.ds(rows + h, 1), :] = jnp.sum(centred * centred, axis=0, keepdims=True)
            return carry

        lax.fori_loop(0, rows, first, 0)
        r.all[me] = r.mine[...]
        r.gathered[me] = r.vectors[...]
        pl.semaphore_wait(barrier, chans - 1)
        run_copies(
            [push("chan", chans, step, r.mine, r.all.at[me], r.s1, r.r1) for step in range(1, chans)]
            + [push("chan", chans, step, r.vectors, r.gathered.at[me], r.s2, r.r2) for step in range(1, chans)]
        )
        totals = [r.all[j] for j in range(chans)]
        mean = sum(t[:rows] for t in totals) * (1.0 / (features * chans))
        spread = sum(
            t[rows:] + features * jnp.square(t[:rows] * (1.0 / features) - mean) for t in totals
        ) * (1.0 / (features * chans))
        inverse = lax.rsqrt(spread + NORM_EPS)
        r.mine[pl.ds(0, rows), :] = mean
        r.mine[pl.ds(rows, rows), :] = inverse

        def second(h, carry):
            block = r.flat[h]
            inv = r.mine[pl.ds(rows + h, 1), :]
            r.x[h] = block.T
            r.unit[h] = ((block - r.mine[pl.ds(h, 1), :]) * inv).T
            r.dev[h] = jnp.broadcast_to(inv, (8, columns)).T
            return carry

        lax.fori_loop(0, rows, second, 0)

    field = ((rows, columns, features), F32)
    return launch(
        body,
        {"lines": lines, "vectors": vectors},
        {
            "x": field,
            "unit": field,
            "dev": ((rows, columns, 8), F32),
            "gathered": ((chans,) + vectors.shape, F32),
        },
        {
            "flat": pltpu.VMEM((rows, features, columns), F32),
            "turn": pltpu.VMEM((2, features, 128), F32),
            "mine": pltpu.VMEM((2 * rows, columns), F32),
            "all": pltpu.VMEM((chans, 2 * rows, columns), F32),
            "s1": sems(chans),
            "r1": sems(chans),
            "s2": sems(chans),
            "r2": sems(chans),
        },
        "entry_norm",
        0,
    )


def pack_lanes(flat_ref, place, real, imag):
    flat_ref[0, place, :] = real[:, :128]
    flat_ref[1, place, :] = imag[:, :128]
    flat_ref[2, place, :] = jnp.concatenate([real[:, 128:], imag[:, 128:]], axis=1)


def unpack_lanes(flat_ref, place):
    rest = flat_ref[2, place, :]
    real = jnp.concatenate([flat_ref[0, place, :], rest[:, :64]], axis=1)
    imag = jnp.concatenate([flat_ref[1, place, :], rest[:, 64:]], axis=1)
    return real, imag


def block_of(index, size):
    return pl.ds(pl.multiple_of(index * size, 8), size)


def send_plain(spaces, chunk, flat_ref, send_ref, recv_ref, sems):
    me = lax.axis_index("space")
    copies = []
    for step in list(range(1, spaces)) + [0]:
        peer = lax.rem(me + step, spaces)
        rows = flat_ref[:, block_of(peer, chunk), :].astype(BF)
        if step == 0:
            recv_ref[me] = rows
        else:
            send_ref[peer] = rows
            copy = push("space", spaces, step, send_ref.at[peer], recv_ref.at[me], *sems)
            copy.start()
            copies.append(copy)
    return copies


def take_plain(spaces, chunk, flat_ref, recv_ref, copies):
    me = lax.axis_index("space")
    for step in range(spaces):
        if step:
            copies[step - 1].wait()
        source = lax.rem(me - step + spaces, spaces)
        flat_ref[:, block_of(source, chunk), :] = recv_ref[source].astype(F32)


LEVEL = 32000.0


def send_fixed(spaces, chunk, flat_ref, send_ref, recv_ref, sems):
    me = lax.axis_index("space")
    largest = jnp.max(jnp.abs(flat_ref[...]), axis=1, keepdims=True)
    grade = jnp.ceil(jnp.log2(jnp.maximum(largest, 1e-30)) * 256.0 + 0.01)
    scale = LEVEL * jnp.exp2(grade * (-1.0 / 256.0))
    mark = jnp.broadcast_to(grade, (3, 8, 128))
    copies = []
    for step in list(range(1, spaces)) + [0]:
        peer = lax.rem(me + step, spaces)
        rows = flat_ref[:, block_of(peer, chunk), :]
        coded = jnp.concatenate([jnp.round(rows * scale), mark], axis=1).astype(jnp.int32).astype(jnp.int16)
        if step == 0:
            recv_ref[me] = coded
        else:
            send_ref[peer] = coded
            copy = push("space", spaces, step, send_ref.at[peer], recv_ref.at[me], *sems)
            copy.start()
            copies.append(copy)
    return copies


def take_fixed(spaces, chunk, flat_ref, recv_ref, copies):
    me = lax.axis_index("space")
    for step in range(spaces):
        if step:
            copies[step - 1].wait()
        source = lax.rem(me - step + spaces, spaces)
        values = recv_ref[source].astype(jnp.int32).astype(F32)
        scale = jnp.exp2(values[:, chunk : chunk + 1] * (1.0 / 256.0)) * (1.0 / LEVEL)
        flat_ref[:, block_of(source, chunk), :] = values[:, :chunk] * scale


def exchange_shape(fixed, spaces, chunk):
    if fixed:
        return (spaces, 3, chunk + 8, 128), jnp.int16
    return (spaces, 3, chunk, 128), BF


def pair_inputs(q, spaces, chunk, thick, flat_ref, even_ref):
    p = jnp.maximum(q - 1, 0)
    extra = (q == 0).astype(F32)
    zeroth = jnp.logical_and(lax.axis_index("space") == 0, p == 0).astype(F32)
    parts = [
        unpack_lanes(flat_ref, pl.ds(pl.multiple_of(s * chunk + p * thick, 8), thick)) for s in range(spaces)
    ]
    real = jnp.concatenate([part[0] for part in parts], axis=0)
    imag = jnp.concatenate([part[1] for part in parts], axis=0)
    chosen = imag * (even_ref[...] * zeroth)
    real = real * (1.0 - extra) + chosen * extra
    imag = (imag - chosen) * (1.0 - extra)
    return p, zeroth, jnp.concatenate([real, imag], axis=0)


def pair_outputs(q, p, zeroth, result, spaces, chunk, thick, flat_ref, even_ref, kept_ref):
    half = result.shape[0] // 2
    real, imag = result[:half], result[half:]
    chosen = even_ref[...] * zeroth
    imag = imag * (1.0 - chosen) + kept_ref[...] * chosen

    @pl.when(q == 0)
    def _():
        kept_ref[...] = real

    for s in range(spaces):
        place = pl.ds(pl.multiple_of(s * chunk + p * thick, 8), thick)
        own = slice(s * thick, (s + 1) * thick)
        pack_lanes(flat_ref, place, real[own], imag[own])


def spectral_forward(source, gain, shift, tables, mix, bias, relayout, fine, sizes, collective_id):
    rows, features, columns, spaces, chans = sizes
    opening = "x" in source
    modes = columns // 2
    total = modes * rows
    chunk = total // spaces
    half = tables["even"].shape[0]
    thick = half // spaces
    pairs = chunk // thick
    cells = rows * columns // chans
    share = rows // chans

    def body(r):
        barrier = pltpu.get_barrier_semaphore()
        signal_peers("space", spaces, barrier)
        signal_peers("chan", chans, barrier)
        gain = r.gain[...]
        shift = r.shift[...]

        def to_modes(h, carry):
            if opening:
                unit = r.unit[h]
            else:
                home = r.home[h].astype(F32)
                x = home[:, :features] + r.before[h]
                mean = home[:, features : features + 1] + (
                    home[:, features + 1 : features + 2] + home[:, features + 2 : features + 3]
                )
                dev = home[:, features + 3 : features + 4] + (
                    home[:, features + 4 : features + 5] + home[:, features + 5 : features + 6]
                )
                unit = (x - mean) * dev
                r.x[h] = x
                r.unit[h] = unit
                r.dev[h] = jnp.broadcast_to(dev, (columns, 8))
            out = mm3((r.row[0], r.row[1]), halves(unit * gain + shift))
            pack_lanes(r.flat, pl.ds(h, modes, stride=rows), out[:modes], out[modes:])
            return carry

        lax.fori_loop(0, rows, to_modes, 0)
        pl.semaphore_wait(barrier, spaces + chans - 2)
        copies = send_fixed(spaces, chunk, r.flat, r.send1, r.recv1, (r.s1, r.r1))
        if opening:
            enter(r.lines_a, r.cells_a, r.turn)
        else:
            leave(r.x, r.lines_x, r.turn)
        take_fixed(spaces, chunk, r.flat, r.recv1, copies)

        def filter_pair(q, carry):
            p, zeroth, block = pair_inputs(q, spaces, chunk, thick, r.flat, r.even)
            spec = mm3((r.col[0], r.col[1]), halves(block))
            r.spec[q] = spec.astype(BF)
            parts = halves(spec)
            straight = mm3(parts, (r.mix[0, 0, 0], r.mix[0, 0, 1]))
            crossed = mm3(parts, (r.mix[0, 1, 0], r.mix[0, 1, 1]))
            first = jnp.concatenate(
                [
                    jnp.maximum(straight[:half] - crossed[half:] + r.bias[0:1], 0.0),
                    jnp.maximum(straight[half:] + crossed[:half] + r.bias[1:2], 0.0),
                ],
                axis=0,
            )
            r.first[q] = first.astype(BF)
            parts = halves(first)
            straight = mm3(parts, (r.mix[1, 0, 0], r.mix[1, 0, 1]))
            crossed = mm3(parts, (r.mix[1, 1, 0], r.mix[1, 1, 1]))
            second = jnp.concatenate(
                [
                    straight[:half] - crossed[half:] + r.bias[2:3],
                    straight[half:] + crossed[:half] + r.bias[3:4],
                ],
                axis=0,
            )
            second = second - jnp.clip(second, -SHRINK_LEVEL, SHRINK_LEVEL)
            r.second[q] = second.astype(BF)
            if fine:
                result = mm3((r.colinv[0], r.colinv[1]), halves(second))
            else:
                result = mm(r.colinv[0], second.astype(BF))
            pair_outputs(q, p, zeroth, result, spaces, chunk, thick, r.back, r.even, r.kept)
            return carry

        r.kept[...] = jnp.zeros_like(r.kept)
        lax.fori_loop(0, pairs + 1, filter_pair, 0)
        send, take = (send_fixed, take_fixed) if fine else (send_plain, take_plain)
        copies = send(spaces, chunk, r.back, r.send2, r.recv2, (r.s2, r.r2))
        if opening:
            enter(r.lines_b, r.cells_b, r.turn)
        take(spaces, chunk, r.back, r.recv2, copies)

        me = lax.axis_index("chan")
        copies = []
        for step in list(range(1, chans)) + [0]:
            peer = lax.rem(me + step, chans)

            def to_places(i, carry):
                h = peer * share + i
                real, imag = unpack_lanes(r.back, pl.ds(h, modes, stride=rows))
                block = jnp.concatenate([real, imag], axis=0)
                if fine:
                    out = mm3((r.rowinv[0], r.rowinv[1]), halves(block))
                else:
                    out = mm(r.rowinv[0], block.astype(BF))
                middle = out + (r.unit[h] * gain + shift) + r.x[h]
                r.middle[h] = middle
                r.own[peer, pl.ds(pl.multiple_of(i * columns, 16), columns), :] = middle.astype(BF)
                return carry

            lax.fori_loop(0, share, to_places, 0)
            if step:
                copy = push("chan", chans, step, r.own.at[peer], r.mid.at[me], r.s3, r.r3)
                copy.start()
                copies.append(copy)
            else:
                r.mid[me] = r.own[me]
        for copy in copies:
            copy.wait()

    field = ((rows, columns, features), F32)
    kept = ((pairs + 1, 2 * half, features), BF)
    line_field = ((rows, features * columns // 128, 128), F32)
    ins = dict(source)
    ins.update(gain=gain, shift=shift, mix=mix, bias=bias)
    ins.update({key: tables[key] for key in ("row", "rowinv", "col", "colinv", "even")})
    outs = {
        "middle": field,
        "mid": ((chans, cells, features), BF),
        "spec": kept,
        "first": kept,
        "second": kept,
    }
    if opening:
        ins.update(lines_a=relayout[0], lines_b=relayout[1])
        outs.update(cells_a=field, cells_b=field)
    else:
        outs.update(x=field, unit=field, dev=((rows, columns, 8), F32), lines_x=line_field)
    shape1, kind1 = exchange_shape(True, spaces, chunk)
    shape2, kind2 = exchange_shape(fine, spaces, chunk)
    return launch(
        body,
        ins,
        outs,
        {
            "flat": pltpu.VMEM((3, total, 128), F32),
            "back": pltpu.VMEM((3, total, 128), F32),
            "kept": pltpu.VMEM((half, features), F32),
            "turn": pltpu.VMEM((2, features, 128), F32),
            "send1": pltpu.VMEM(shape1, kind1),
            "recv1": pltpu.VMEM(shape1, kind1),
            "send2": pltpu.VMEM(shape2, kind2),
            "recv2": pltpu.VMEM(shape2, kind2),
            "own": pltpu.VMEM((chans, cells, features), BF),
            "s1": sems(spaces),
            "r1": sems(spaces),
            "s2": sems(spaces),
            "r2": sems(spaces),
            "s3": sems(chans),
            "r3": sems(chans),
        },
        "spectral_forward",
        collective_id,
    )


def spectral_backward(g, dv, unit, dev, gain, tables, mix, saved, leaving, before, dense, sizes, collective_id):
    rows, features, columns, spaces, chans = sizes
    modes = columns // 2
    total = modes * rows
    chunk = total // spaces
    half = tables["even"].shape[0]
    thick = half // spaces
    pairs = chunk // thick
    size = features // 2

    def body(r):
        barrier = pltpu.get_barrier_semaphore()
        signal_peers("space", spaces, barrier)
        signal_peers("chan", chans, barrier)
        gain = r.gain[...]
        me = lax.axis_index("chan")

        def to_modes(h, carry):
            middle_grad = r.g[h] + r.dv[h].astype(F32)
            r.out[h] = middle_grad
            out = mm(r.rowinv_t[...], middle_grad.astype(BF))
            pack_lanes(r.flat, pl.ds(h, modes, stride=rows), out[:modes], out[modes:])
            return carry

        lax.fori_loop(0, rows, to_modes, 0)
        pl.semaphore_wait(barrier, spaces + chans - 2)
        copies = send_plain(spaces, chunk, r.flat, r.send1, r.recv1, (r.s1, r.r1))
        slow = []
        if dense is not None:
            for step in range(1, chans):
                peer = lax.rem(me + step, chans)
                slow.append(push("chan", chans, step, r.weights.at[peer], r.landed.at[me], r.s4, r.r4))
                slow.append(push("chan", chans, step, r.rest.at[peer], r.rest_landed.at[me], r.s5, r.r5))
            for copy in slow:
                copy.start()
        if leaving is not None:
            leave(r.leaving, r.lines, r.turn)
        r.mixgrad[...] = jnp.zeros_like(r.mixgrad)
        r.biasgrad[...] = jnp.zeros_like(r.biasgrad)
        r.kept[...] = jnp.zeros_like(r.kept)
        take_plain(spaces, chunk, r.flat, r.recv1, copies)

        def turned(v):
            return jnp.concatenate([v[half:], -v[:half]], axis=0)

        def note_bias(index, value):
            r.biasgrad[index : index + 1, :] += jnp.sum(value, axis=0, keepdims=True)

        def filter_pair(q, carry):
            p, zeroth, block = pair_inputs(q, spaces, chunk, thick, r.flat, r.even)
            grad = mm(r.col[0], block.astype(BF))
            grad = jnp.where(r.second[q].astype(F32) == 0.0, 0.0, grad)
            note_bias(2, grad[:half])
            note_bias(3, grad[half:])
            low = grad.astype(BF)
            first = r.first[q]
            r.mixgrad[1, 0] += mm_tn(first, low)
            r.mixgrad[1, 1] += mm_tn(first, turned(grad).astype(BF))
            straight = mm_nt(low, r.mix[1, 0, 0])
            crossed = mm_nt(low, r.mix[1, 1, 0])
            grad = jnp.concatenate(
                [straight[:half] + crossed[half:], straight[half:] - crossed[:half]], axis=0
            )
            grad = jnp.where(first.astype(F32) > 0.0, grad, 0.0)
            note_bias(0, grad[:half])
            note_bias(1, grad[half:])
            low = grad.astype(BF)
            spec = r.spec[q]
            r.mixgrad[0, 0] += mm_tn(spec, low)
            r.mixgrad[0, 1] += mm_tn(spec, turned(grad).astype(BF))
            straight = mm_nt(low, r.mix[0, 0, 0])
            crossed = mm_nt(low, r.mix[0, 1, 0])
            grad = jnp.concatenate(
                [straight[:half] + crossed[half:], straight[half:] - crossed[:half]], axis=0
            )
            result = mm(r.colinv[0], grad.astype(BF))
            pair_outputs(q, p, zeroth, result, spaces, chunk, thick, r.back, r.even, r.kept)
            return carry

        lax.fori_loop(0, pairs + 1, filter_pair, 0)
        copies = send_plain(spaces, chunk, r.back, r.send2, r.recv2, (r.s2, r.r2))
        normgrad = jnp.zeros((2, features), F32)
        for layer in range(2):
            for part in range(2):
                for block in range(2):
                    own = slice(block * size, (block + 1) * size)
                    piece = r.mixgrad[layer, part][own, own]
                    piece = jnp.concatenate([piece, jnp.zeros((size, 128 - size), F32)], axis=1)
                    start = ((layer * 2 + part) * 2 + block) * size
                    place = slice(start, start + size)
                    r.sums[place, :] = piece + r.before[place, :] if before is not None else piece
        take_plain(spaces, chunk, r.back, r.recv2, copies)
        lane = lax.broadcasted_iota(jnp.int32, (columns, 128), 1)

        def to_places(h, carry):
            table, one_sum, two_sum = carry
            real, imag = unpack_lanes(r.back, pl.ds(h, modes, stride=rows))
            block = jnp.concatenate([real, imag], axis=0)
            grad = mm(r.row_t[...], block.astype(BF)) + r.out[h]
            unit = r.unit[h]
            one_sum += jnp.sum(grad * unit, axis=0, keepdims=True)
            two_sum += jnp.sum(grad, axis=0, keepdims=True)
            scaled = grad * gain
            r.scaled[h] = scaled
            one = jnp.sum(scaled, axis=1, keepdims=True)
            two = jnp.sum(scaled * unit, axis=1, keepdims=True)
            table = jnp.where(lane == h, one, table)
            return jnp.where(lane == rows + h, two, table), one_sum, two_sum

        none = jnp.zeros((1, features), F32)
        table, one_sum, two_sum = lax.fori_loop(
            0, rows, to_places, (jnp.zeros((columns, 128), F32), none, none)
        )
        table = table.T[: 2 * rows]
        r.mine[...] = table
        r.all[me] = table
        copies = [push("chan", chans, step, r.mine, r.all.at[me], r.s3, r.r3) for step in range(1, chans)]
        for copy in copies:
            copy.start()
        vectors = jnp.concatenate([r.biasgrad[0:4], one_sum, two_sum, none, none], axis=0)
        wide = jnp.concatenate([vectors, jnp.zeros((8, 256 - features), F32)], axis=1)
        wide = jnp.concatenate([wide[:, :128], wide[:, 128:]], axis=0)
        place = slice(8 * size, 8 * size + 16)
        r.sums[place, :] = wide + r.before[place, :] if before is not None else wide
        for copy in copies:
            copy.wait()
        means = sum(r.all[j] for j in range(chans)) * (1.0 / (features * chans))
        means = jnp.concatenate([means, jnp.zeros((128 - 2 * rows, columns), F32)], axis=0).T

        def finish(h, carry):
            one = jnp.sum(jnp.where(lane == h, means, 0.0), axis=1, keepdims=True)
            two = jnp.sum(jnp.where(lane == rows + h, means, 0.0), axis=1, keepdims=True)
            inverse = r.dev[h][:, :1]
            r.out[h] += inverse * (r.scaled[h] - one - r.unit[h] * two)
            return carry

        lax.fori_loop(0, rows, finish, 0)
        for copy in slow:
            copy.wait()

    field = ((rows, columns, features), F32)
    shape, kind = exchange_shape(False, spaces, chunk)
    ins = {"g": g, "dv": dv, "unit": unit, "dev": dev, "gain": gain, "mix": mix}
    ins.update({key: tables[key] for key in ("rowinv_t", "row_t", "col", "colinv", "even")})
    ins.update({key: saved[key] for key in ("spec", "first", "second")})
    outs = {"out": field, "sums": ((8 * size + 16, 128), F32)}
    scratch = {
        "flat": pltpu.VMEM((3, total, 128), F32),
        "back": pltpu.VMEM((3, total, 128), F32),
        "kept": pltpu.VMEM((half, features), F32),
        "turn": pltpu.VMEM((2, features, 128), F32),
        "scaled": pltpu.VMEM((rows, columns, features), F32),
        "mixgrad": pltpu.VMEM((2, 2, features, features), F32),
        "biasgrad": pltpu.VMEM((8, features), F32),
        "mine": pltpu.VMEM((2 * rows, columns), F32),
        "all": pltpu.VMEM((chans, 2 * rows, columns), F32),
        "send1": pltpu.VMEM(shape, kind),
        "recv1": pltpu.VMEM(shape, kind),
        "send2": pltpu.VMEM(shape, kind),
        "recv2": pltpu.VMEM(shape, kind),
        "s1": sems(spaces),
        "r1": sems(spaces),
        "s2": sems(spaces),
        "r2": sems(spaces),
        "s3": sems(chans),
        "r3": sems(chans),
    }
    in_specs, out_specs = {}, {}
    if leaving is not None:
        ins.update(leaving=leaving)
        outs.update(lines=((rows, features * columns // 128, 128), F32))
    if before is not None:
        ins.update(before=before)
    if dense is not None:
        weights, rest = dense
        ins.update(weights=weights, rest=rest)
        outs.update(landed=(weights.shape, BF), rest_landed=(rest.shape, F32))
        in_specs.update(weights=IN_PLACE, rest=IN_PLACE)
        out_specs.update(landed=IN_PLACE, rest_landed=IN_PLACE)
        scratch.update(s4=sems(chans), r4=sems(chans), s5=sems(chans), r5=sems(chans))
    return launch(body, ins, outs, scratch, "spectral_backward", collective_id, in_specs, out_specs)


ERF = (0.254829592, -0.284496736, 1.421413741, -1.453152027, 1.061405429)


def gelu_and_slope(v):
    a = jnp.abs(v) * math.sqrt(0.5)
    t = 1.0 / (1.0 + 0.3275911 * a)
    e = jnp.exp(-a * a)
    tail = 0.5 * e * t * (ERF[0] + t * (ERF[1] + t * (ERF[2] + t * (ERF[3] + t * ERF[4]))))
    below = jnp.where(v >= 0.0, 1.0 - tail, tail)
    return v * below, below + v * e * (1.0 / math.sqrt(2.0 * math.pi))


def three_parts(v):
    a = v.astype(BF)
    rest = v - a.astype(F32)
    b = rest.astype(BF)
    return [a, b, (rest - b.astype(F32)).astype(BF)]


def fixed_block(shape):
    return pl.BlockSpec(shape, lambda t: (0,) * len(shape))


def full_vector(gathered_ref, start, size):
    chans = gathered_ref.shape[0]
    return jnp.concatenate([gathered_ref[j, 1:2, start : start + size] for j in range(chans)], axis=1)


def ffn_forward(mid, gathered, up, down, sizes, collective_id):
    rows, features, columns, spaces, chans = sizes
    cells = mid.shape[1]
    width = features * chans
    local = up.shape[2]
    tile = 256
    per = local // tile
    steps = chans * per
    hidden = chans * local

    def body(r):
        t = pl.program_id(0)
        barrier = pltpu.get_barrier_semaphore()

        def middle():
            return jnp.concatenate([r.mid[j].astype(F32) for j in range(chans)], axis=1)

        @pl.when(t == 0)
        def _():
            signal_peers("chan", chans, barrier)
            value = middle()
            mean = jnp.mean(value, axis=1, keepdims=True)
            centred = value - mean
            inverse = lax.rsqrt(jnp.mean(centred * centred, axis=1, keepdims=True) + NORM_EPS)
            unit = centred * inverse
            r.unit[...] = unit.astype(BF)
            r.dev[...] = jnp.broadcast_to(inverse, r.dev.shape)
            gain = full_vector(r.gathered, 0, features)
            shift = full_vector(r.gathered, features, features)
            r.entry[...] = (unit * gain + shift).astype(BF)
            r.total[...] = value + full_vector(r.gathered, 2 * features, features)

        bias = r.gathered[t // per, 0:1, pl.ds(pl.multiple_of((t % per) * tile, tile), tile)]
        value = mm(r.entry[...], r.up[0]) + bias
        active, slope = gelu_and_slope(value)
        active = active.astype(BF)
        r.active[...] = active
        r.slope[...] = slope.astype(BF)
        r.total[...] += mm(active, r.down[0])

        @pl.when(t == steps - 1)
        def _():
            me = lax.axis_index("chan")
            value = r.total[...]
            mean = jnp.mean(value, axis=1, keepdims=True)
            centred = value - mean
            inverse = lax.rsqrt(jnp.mean(centred * centred, axis=1, keepdims=True) + NORM_EPS)
            outer = value - middle()
            stats = jnp.concatenate(
                three_parts(mean) + three_parts(inverse) + [jnp.zeros((cells, 256 - features - 6), BF)],
                axis=1,
            )
            pl.semaphore_wait(barrier, chans - 1)
            for j in range(chans):
                r.send[j] = jnp.concatenate(
                    [outer[:, j * features : (j + 1) * features].astype(BF), stats], axis=1
                )
            copies = []
            for step in range(1, chans):
                peer = lax.rem(me + step, chans)
                copy = push("chan", chans, step, r.send.at[peer], r.land.at[me], r.s1, r.r1)
                copy.start()
                copies.append(copy)
            r.home[me] = r.send[me]
            for step in range(1, chans):
                copies[step - 1].wait()
                sender = lax.rem(me - step + chans, chans)
                r.home[sender] = r.land[sender]

    return launch(
        body,
        {"mid": mid, "gathered": gathered, "up": up, "down": down},
        {
            "home": ((chans, cells, 256), BF),
            "entry": ((cells, width), BF),
            "unit": ((cells, width), BF),
            "dev": ((cells, 128), F32),
            "active": ((cells, hidden), BF),
            "slope": ((cells, hidden), BF),
        },
        {
            "total": pltpu.VMEM((cells, width), F32),
            "send": pltpu.VMEM((chans, cells, 256), BF),
            "land": pltpu.VMEM((chans, cells, 256), BF),
            "s1": sems(chans),
            "r1": sems(chans),
        },
        "ffn_forward",
        collective_id,
        {
            "mid": fixed_block(mid.shape),
            "gathered": fixed_block(gathered.shape),
            "up": pl.BlockSpec((1, width, tile), lambda t: (t // per, 0, t % per)),
            "down": pl.BlockSpec((1, tile, width), lambda t: (t // per, t % per, 0)),
        },
        {
            "home": fixed_block((chans, cells, 256)),
            "entry": fixed_block((cells, width)),
            "unit": fixed_block((cells, width)),
            "dev": fixed_block((cells, 128)),
            "active": pl.BlockSpec((cells, tile), lambda t: (0, t)),
            "slope": pl.BlockSpec((cells, tile), lambda t: (0, t)),
        },
        (steps,),
    )


def ffn_backward(source, target, weight, saved, gathered, up, down, before, sizes, collective_id):
    rows, features, columns, spaces, chans = sizes
    final = "home" in source
    cells = rows * columns // chans
    width = features * chans
    local = up.shape[2]
    tile = 256
    per = local // tile
    steps = chans * per

    def body(r):
        t = pl.program_id(0)
        barrier = pltpu.get_barrier_semaphore()
        me = lax.axis_index("chan")
        place = lax.axis_index("space")
        core = lax.rem(place, 2)
        sibling = place + 1 - 2 * core

        def swap(step):
            return pltpu.make_async_remote_copy(
                src_ref=r.give.at[step],
                dst_ref=r.take.at[step],
                send_sem=r.s3.at[step],
                recv_sem=r.r3.at[step],
                device_id={"space": sibling},
                device_id_type=MESH_ID,
            )

        @pl.when(t == 0)
        def _():
            signal_peers("chan", chans, barrier)
            if not final:
                pl.semaphore_signal(barrier, inc=1, device_id={"space": sibling}, device_id_type=MESH_ID)
            for j in range(chans):
                if final:
                    value = r.home[j].astype(F32)[:, :features] + r.middle[j]
                    r.x[j] = value
                    grad = r.weight[0:1, 0:1] * (value - r.target[j])
                else:
                    grad = r.weight[0:1, 0:1] * (r.x[j] - r.target[j]) + r.carried[j]
                r.g[j] = grad
                r.low[j] = grad.astype(BF)
            pl.semaphore_wait(barrier, chans - 1 if final else chans)
            copies = []
            for step in range(1, chans):
                peer = lax.rem(me + step, chans)
                copy = push("chan", chans, step, r.low.at[peer], r.land.at[me], r.s1, r.r1)
                copy.start()
                copies.append(copy)
            r.land[me] = r.low[me]
            r.total[...] = jnp.zeros_like(r.total)
            r.small[...] = jnp.zeros_like(r.small)
            for copy in copies:
                copy.wait()
            upper = jnp.concatenate([r.land[j].astype(F32) for j in range(chans)], axis=1)
            r.upper[...] = upper.astype(BF)
            r.small[2:3, :] = jnp.sum(upper, axis=0, keepdims=True)

        upper = r.upper[...]
        gdown = mm_tn(r.active[...], upper)
        lower = mm_nt(upper, r.down[0]) * r.slope[...].astype(F32)
        r.upb[pl.ds(t, 1), :] = jnp.sum(lower, axis=0, keepdims=True)
        lower = lower.astype(BF)
        gup = mm_tn(lower, r.entry[...])
        r.total[...] += mm_nt(lower, r.up[0])
        if final:
            r.gdown[0] = gdown.astype(BF)
            r.gup[0] = gup.astype(BF)
        else:
            gdown += r.prev_down[0].astype(F32)
            gup += r.prev_up[0].astype(F32)
            second = core == 1
            r.keep[t] = jnp.where(second, gup, gdown)
            r.give[t] = jnp.where(second, gdown, gup).astype(BF)
            swap(t).start()

        @pl.when(t == steps - 1)
        def _():
            grad = r.total[...]
            unit = r.unit[...].astype(F32)
            r.small[0:1, :] = jnp.sum(grad * unit, axis=0, keepdims=True)
            r.small[1:2, :] = jnp.sum(grad, axis=0, keepdims=True)
            scaled = grad * full_vector(r.gathered, 0, features)
            one = jnp.mean(scaled, axis=1, keepdims=True)
            two = jnp.mean(scaled * unit, axis=1, keepdims=True)
            result = r.dev[:, :1] * (scaled - one - unit * two)
            for j in range(chans):
                r.send[j] = result[:, j * features : (j + 1) * features].astype(BF)
            copies = []
            for step in range(1, chans):
                peer = lax.rem(me + step, chans)
                copy = push("chan", chans, step, r.send.at[peer], r.last.at[me], r.s2, r.r2)
                copy.start()
                copies.append(copy)
            r.dv[me] = r.send[me]
            r.rest[...] = jnp.zeros_like(r.rest)
            for j in range(chans):
                for k in range(per):
                    r.rest[j, 0:1, k * tile : (k + 1) * tile] = r.upb[j * per + k : j * per + k + 1, :]
                for k in range(3):
                    r.rest[j, 1 + k : 2 + k, 0:features] = r.small[k : k + 1, j * features : (j + 1) * features]
            if not final:
                r.rest[...] += r.prev_rest[...]
                for step in range(steps):
                    swap(step).wait()
                    r.sum[step // per, (step % per) * tile : (step % per + 1) * tile, :] = (
                        r.keep[step] + r.take[step].astype(F32)
                    ).astype(BF)
            for step in range(1, chans):
                copies[step - 1].wait()
                sender = lax.rem(me - step + chans, chans)
                r.dv[sender] = r.last[sender]

    by_cells = (chans, cells, features)
    weights = (chans, local, width)
    up_spec = pl.BlockSpec((1, width, tile), lambda t: (t // per, 0, t % per))
    hidden_spec = pl.BlockSpec((1, tile, width), lambda t: (t // per, t % per, 0))
    cell_spec = pl.BlockSpec((cells, tile), lambda t: (0, t))
    ins = {key: value.reshape(chans, cells, -1) for key, value in source.items()}
    ins["target"] = target.reshape(by_cells)
    ins["weight"] = weight
    ins.update({key: saved[key] for key in ("entry", "unit", "dev", "active", "slope")})
    ins.update(gathered=gathered, up=up, down=down)
    in_specs = {key: fixed_block(value.shape) for key, value in ins.items()}
    in_specs.update(active=cell_spec, slope=cell_spec, up=up_spec, down=hidden_spec)
    outs = {
        "g": (by_cells, F32),
        "dv": (by_cells, BF),
        "rest": ((chans, 8, local), F32),
    }
    scratch = {
        "low": pltpu.VMEM(by_cells, BF),
        "land": pltpu.VMEM(by_cells, BF),
        "send": pltpu.VMEM(by_cells, BF),
        "last": pltpu.VMEM(by_cells, BF),
        "upper": pltpu.VMEM((cells, width), BF),
        "total": pltpu.VMEM((cells, width), F32),
        "small": pltpu.VMEM((8, width), F32),
        "upb": pltpu.VMEM((-(-steps // 8) * 8, tile), F32),
        "s1": sems(chans),
        "r1": sems(chans),
        "s2": sems(chans),
        "r2": sems(chans),
    }
    if final:
        outs.update(x=(by_cells, F32), gdown=(weights, BF), gup=(weights, BF))
        out_specs = {key: fixed_block(outs[key][0]) for key in outs}
        out_specs.update(gdown=hidden_spec, gup=hidden_spec)
    else:
        ins.update(prev_down=before[0], prev_up=before[1], prev_rest=before[2])
        in_specs.update(prev_down=hidden_spec, prev_up=hidden_spec, prev_rest=fixed_block(before[2].shape))
        outs.update(sum=(weights, BF))
        out_specs = {key: fixed_block(outs[key][0]) for key in outs}
        scratch.update(
            keep=pltpu.VMEM((steps, tile, width), F32),
            give=pltpu.VMEM((steps, tile, width), BF),
            take=pltpu.VMEM((steps, tile, width), BF),
            s3=sems(steps),
            r3=sems(steps),
        )
    return launch(body, ins, outs, scratch, "ffn_backward", collective_id, in_specs, out_specs, (steps,))


def gather_gradients(weights, landed, rest, rest_landed, sums, field, sizes, collective_id):
    rows, features, columns, spaces, chans = sizes
    local, width = weights.shape[1:]
    levels = spaces // 2
    piece = local // levels
    small = sums.shape[0]
    extra = small + 32
    part = -(-extra // (16 * levels)) * 16

    def body(r):
        barrier = pltpu.get_barrier_semaphore()
        me = lax.axis_index("chan")
        place = lax.axis_index("space")
        core = lax.rem(place, 2)
        level = place // 2
        sibling = place + 1 - 2 * core
        others = [lax.rem(level + step, levels) for step in range(1, levels)]
        for other in others:
            pl.semaphore_signal(barrier, inc=1, device_id={"space": 2 * other + core}, device_id_type=MESH_ID)
        pl.semaphore_signal(barrier, inc=1, device_id={"space": sibling}, device_id_type=MESH_ID)

        def send(source, target, step, send_sem, recv_sem):
            return pltpu.make_async_remote_copy(
                src_ref=source,
                dst_ref=target,
                send_sem=send_sem.at[step],
                recv_sem=recv_sem.at[step],
                device_id={"space": 2 * others[step - 1] + core},
                device_id_type=MESH_ID,
            )

        def to_sibling(source, target, step, send_sem, recv_sem):
            return pltpu.make_async_remote_copy(
                src_ref=source,
                dst_ref=target,
                send_sem=send_sem.at[step],
                recv_sem=recv_sem.at[step],
                device_id={"space": sibling},
                device_id_type=MESH_ID,
            )

        loads = [pltpu.make_async_copy(r.weights.at[me], r.terms.at[0], r.load.at[0])]
        loads += [pltpu.make_async_copy(r.rest.at[me], r.rest_terms.at[0], r.load.at[1])]
        for step in range(1, chans):
            source = lax.rem(me + step, chans)
            loads.append(pltpu.make_async_copy(r.landed.at[source], r.terms.at[step], r.load.at[2 * step]))
            loads.append(
                pltpu.make_async_copy(r.rest_landed.at[source], r.rest_terms.at[step], r.load.at[2 * step + 1])
            )
        run_copies(loads)
        for q in range(levels):
            own = slice(q * piece, (q + 1) * piece)
            r.a_send[q] = sum(r.terms[j, own, :].astype(F32) for j in range(chans)).astype(BF)
        r.table[...] = jnp.zeros_like(r.table)
        r.table[0:small, :] = r.sums[...]
        tail = sum(r.rest_terms[j] for j in range(chans))
        for k in range(local // 128):
            lanes = slice(k * 128, (k + 1) * 128)
            r.table[small + k : small + k + 1, :] = tail[0:1, lanes]
        for k in range(3):
            line = jnp.concatenate([tail[1 + k : 2 + k, :features], jnp.zeros((1, 256 - features), F32)], axis=1)
            r.table[small + 8 + 2 * k : small + 9 + 2 * k, :] = line[:, :128]
            r.table[small + 9 + 2 * k : small + 10 + 2 * k, :] = line[:, 128:]
        for q in range(levels):
            r.b_send[q] = r.table[q * part : (q + 1) * part, :].astype(BF)
        pl.semaphore_wait(barrier, levels)
        first = []
        for step in range(1, levels):
            first.append(send(r.a_send.at[others[step - 1]], r.a_land.at[level], step, r.s1, r.r1))
            first.append(send(r.b_send.at[others[step - 1]], r.b_land.at[level], step, r.s2, r.r2))
        for copy in first:
            copy.start()
        leave(r.field, r.lines, r.turn)
        a = r.a_send[level].astype(F32)
        b = r.b_send[level].astype(F32)
        for step in range(1, levels):
            first[2 * step - 2].wait()
            first[2 * step - 1].wait()
            source = lax.rem(level - step + levels, levels)
            a += r.a_land[source].astype(F32)
            b += r.b_land[source].astype(F32)
        r.a_own[...] = a.astype(BF)
        r.b_own[...] = b.astype(BF)
        last = [to_sibling(r.a_own, r.a_other.at[level], 0, r.s5, r.r5)]
        last += [to_sibling(r.b_own, r.b_other.at[level], 0, r.s6, r.r6)]
        second = []
        for step in range(1, levels):
            second.append(send(r.a_own, r.a_full.at[level], step, r.s3, r.r3))
            second.append(send(r.b_own, r.b_full.at[level], step, r.s4, r.r4))
        for copy in second + last:
            copy.start()
        r.a_full[level] = r.a_own[...]
        r.b_full[level] = r.b_own[...]
        for step in range(1, levels):
            second[2 * step - 2].wait()
            second[2 * step - 1].wait()
            source = lax.rem(level - step + levels, levels)
            more = [to_sibling(r.a_full.at[source], r.a_other.at[source], step, r.s5, r.r5)]
            more += [to_sibling(r.b_full.at[source], r.b_other.at[source], step, r.s6, r.r6)]
            for copy in more:
                copy.start()
            last += more
        for copy in last:
            copy.wait()
        swap = core == 1
        for q in range(levels):
            own = slice(q * piece, (q + 1) * piece)
            mine, theirs = r.a_full[q].astype(F32), r.a_other[q].astype(F32)
            r.down[own, :] = jnp.where(swap, theirs, mine)
            r.up[:, own] = jnp.where(swap, mine, theirs).T
            r.table[q * part : (q + 1) * part, :] = r.b_full[q].astype(F32) + r.b_other[q].astype(F32)
        size = features // 2
        for layer, target in enumerate((r.mix_in, r.mix_out)):
            for half in range(2):
                for block in range(2):
                    start = ((layer * 2 + half) * 2 + block) * size
                    target[half, block] = r.table[start : start + size, :size]
        base = 8 * size

        def vector(k):
            return jnp.concatenate(
                [r.table[base + k : base + k + 1, :], r.table[base + 8 + k : base + 9 + k, : features - 128]], axis=1
            )

        for k, target in enumerate((r.bias_in, r.bias_in, r.bias_out, r.bias_out)):
            value = vector(k)
            target[k % 2, 0:1, :] = value[:, :size]
            target[k % 2, 1:2, :] = value[:, size:]
        r.pre[0:1, :] = vector(4)
        r.pre[1:2, :] = vector(5)
        for k in range(local // 128):
            r.upb[0:1, k * 128 : (k + 1) * 128] = r.table[small + k : small + k + 1, :]
        for k in range(3):
            r.post[k : k + 1, :] = jnp.concatenate(
                [
                    r.table[small + 8 + 2 * k : small + 9 + 2 * k, :],
                    r.table[small + 9 + 2 * k : small + 10 + 2 * k, : features - 128],
                ],
                axis=1,
            )

    size = features // 2
    return launch(
        body,
        {
            "weights": weights,
            "landed": landed,
            "rest": rest,
            "rest_landed": rest_landed,
            "sums": sums,
            "field": field,
        },
        {
            "down": ((local, width), F32),
            "up": ((width, local), F32),
            "lines": ((rows, features * columns // 128, 128), F32),
            "mix_in": ((2, 2, size, size), F32),
            "mix_out": ((2, 2, size, size), F32),
            "bias_in": ((2, 2, size), F32),
            "bias_out": ((2, 2, size), F32),
            "pre": ((2, features), F32),
            "post": ((3, features), F32),
            "upb": ((1, local), F32),
        },
        {
            "terms": pltpu.VMEM((chans, local, width), BF),
            "rest_terms": pltpu.VMEM((chans,) + rest.shape[1:], F32),
            "table": pltpu.VMEM((part * levels, 128), F32),
            "turn": pltpu.VMEM((2, features, 128), F32),
            "a_send": pltpu.VMEM((levels, piece, width), BF),
            "a_land": pltpu.VMEM((levels, piece, width), BF),
            "a_own": pltpu.VMEM((piece, width), BF),
            "a_full": pltpu.VMEM((levels, piece, width), BF),
            "a_other": pltpu.VMEM((levels, piece, width), BF),
            "b_send": pltpu.VMEM((levels, part, 128), BF),
            "b_land": pltpu.VMEM((levels, part, 128), BF),
            "b_own": pltpu.VMEM((part, 128), BF),
            "b_full": pltpu.VMEM((levels, part, 128), BF),
            "b_other": pltpu.VMEM((levels, part, 128), BF),
            "load": sems(2 * chans),
            **{key + str(k): sems(levels) for k in range(1, 7) for key in ("s", "r")},
        },
        "gather_gradients",
        collective_id,
        {key: IN_PLACE for key in ("weights", "landed", "rest", "rest_landed")},
    )


def block_diagonal(weights):
    blocks = weights.shape[1]
    rows = [
        jnp.concatenate(
            [weights[:, b] if b == other else jnp.zeros_like(weights[:, b]) for other in range(blocks)], axis=2
        )
        for b in range(blocks)
    ]
    return jnp.concatenate(rows, axis=1)


def shards_fast(
    current_atmosphere,
    truth_one,
    truth_two,
    storm_codes,
    pre_gain,
    pre_shift,
    mix_weight_in,
    mix_bias_in,
    mix_weight_out,
    mix_bias_out,
    post_gain,
    post_shift,
    up_weight,
    up_bias,
    down_weight,
    down_bias,
):
    rows, merged = current_atmosphere.shape[1:]
    columns = W
    features = merged // columns
    spaces = lax.axis_size("space")
    chans = lax.axis_size("chan")
    sizes = (rows, features, columns, spaces, chans)
    height = rows * spaces
    thick = 2 * rows
    local = up_weight.shape[1]

    forward, inverse = row_constants(columns)
    column = column_constants(height, rows, 2)
    even = (np.arange(spaces * thick) // rows % 2 == 0).astype(np.float32)
    tables = {
        "row": jnp.stack(const_halves(forward)),
        "rowinv": jnp.stack(const_halves(inverse)),
        "rowinv_t": const_halves(inverse.T)[0],
        "row_t": const_halves(forward.T)[0],
        "col": jnp.stack(const_halves(column)),
        "colinv": jnp.stack(const_halves(column.T)),
        "even": jnp.asarray(np.repeat(even[:, None], features, axis=1)),
    }

    def lines(flat):
        return flat.reshape(rows, merged // 128, 128)

    def flat(line_field):
        return line_field.reshape(1, rows, merged)

    weight = jnp.broadcast_to((storm_codes.astype(F32) / 64.0).reshape(1, 1), (8, 128))
    mix = jnp.stack([block_diagonal(mix_weight_in), block_diagonal(mix_weight_out)])
    high = lax.reduce_precision(mix, 8, 7)
    mix = jnp.stack([high.astype(BF), (mix - high).astype(BF)], axis=2)
    bias = jnp.concatenate([mix_bias_in.reshape(2, features), mix_bias_out.reshape(2, features)])
    gain_row = pre_gain.reshape(1, features)
    shift_row = pre_shift.reshape(1, features)

    up_all = lax.all_gather(up_weight, "chan", axis=0)
    down_all = lax.all_gather(down_weight, "chan", axis=0)
    norms = jnp.concatenate(
        [post_gain, post_shift, down_bias.astype(F32), jnp.zeros((local - 3 * features,), F32)]
    )
    vectors = jnp.concatenate(
        [up_bias.astype(F32).reshape(1, local), norms.reshape(1, local), jnp.zeros((6, local), F32)]
    )

    start = entry_norm(lines(current_atmosphere), vectors, sizes)
    gathered = start["gathered"]
    one = spectral_forward(
        {"x": start["x"], "unit": start["unit"]},
        gain_row,
        shift_row,
        tables,
        mix,
        bias,
        (lines(truth_one), lines(truth_two)),
        True,
        sizes,
        1,
    )
    ffn_one = ffn_forward(one["mid"], gathered, up_all, down_all, sizes, 3)
    two = spectral_forward(
        {"before": one["middle"], "home": ffn_one["home"].reshape(rows, columns, 256)},
        gain_row,
        shift_row,
        tables,
        mix,
        bias,
        None,
        False,
        sizes,
        2,
    )
    ffn_two = ffn_forward(two["mid"], gathered, up_all, down_all, sizes, 3)

    late = ffn_backward(
        {"home": ffn_two["home"], "middle": two["middle"]},
        one["cells_b"],
        weight,
        ffn_two,
        gathered,
        up_all,
        down_all,
        None,
        sizes,
        4,
    )

    def fields(value):
        return value.reshape(rows, columns, features)

    back_two = spectral_backward(
        fields(late["g"]),
        fields(late["dv"]),
        two["unit"],
        two["dev"],
        gain_row,
        tables,
        mix,
        two,
        fields(late["x"]),
        None,
        None,
        sizes,
        6,
    )
    early = ffn_backward(
        {"x": two["x"], "carried": back_two["out"]},
        one["cells_a"],
        weight,
        ffn_one,
        gathered,
        up_all,
        down_all,
        (late["gdown"], late["gup"], late["rest"]),
        sizes,
        5,
    )
    back_one = spectral_backward(
        fields(early["g"]),
        fields(early["dv"]),
        start["unit"],
        start["dev"],
        gain_row,
        tables,
        mix,
        one,
        None,
        back_two["sums"],
        (early["sum"], early["rest"]),
        sizes,
        7,
    )
    end = gather_gradients(
        early["sum"],
        back_one["landed"],
        early["rest"],
        back_one["rest_landed"],
        back_one["sums"],
        back_one["out"],
        sizes,
        8,
    )
    return (
        flat(two["lines_x"]),
        flat(back_two["lines"]),
        flat(end["lines"]),
        end["pre"][0],
        end["pre"][1],
        end["mix_in"],
        end["bias_in"],
        end["mix_out"],
        end["bias_out"],
        end["post"][0],
        end["post"][1],
        end["up"],
        end["upb"].reshape(local),
        end["down"],
        end["post"][2],
    )


def suits(mesh):
    spaces, chans = mesh.shape["space"], mesh.shape["chan"]
    return (spaces, chans) == (8, 4)


def solution(mesh):
    in_specs = (
        P(None, "space", "chan"),
        P(None, "space", "chan"),
        P(None, "space", "chan"),
        P(),
        P("chan"),
        P("chan"),
        P(None, "chan", None, None),
        P(None, "chan", None),
        P(None, "chan", None, None),
        P(None, "chan", None),
        P("chan"),
        P("chan"),
        P(None, "chan"),
        P("chan"),
        P("chan", None),
        P("chan"),
    )
    out_specs = (
        P(None, "space", "chan"),
        P(None, "space", "chan"),
        P(None, "space", "chan"),
        P("chan"),
        P("chan"),
        P(None, "chan", None, None),
        P(None, "chan", None),
        P(None, "chan", None, None),
        P(None, "chan", None),
        P("chan"),
        P("chan"),
        P(None, "chan"),
        P("chan"),
        P("chan", None),
        P("chan"),
    )
    return jax.shard_map(shards_fast if suits(mesh) else shards, mesh=mesh, in_specs=in_specs, out_specs=out_specs, check_vma=False)
```

```python
import functools
import math
import types

import jax
import jax.numpy as jnp
import ml_dtypes
import numpy as np
from jax import lax
from jax.experimental import pallas as pl
from jax.experimental.pallas import tpu as pltpu
from jax.sharding import PartitionSpec as P

W = 160
KW = 81


NORM_EPS = 1e-06
SHRINK_LEVEL = 0.01
FULL_PRECISION = lax.Precision.HIGHEST


def exact_gelu(values):
    return jax.nn.gelu(values, approximate=False)


def shrink(values):
    return values - jnp.clip(values, -SHRINK_LEVEL, SHRINK_LEVEL)


def block_mix(values, matrix):
    return jnp.einsum("bhkni,nio->bhkno", values, matrix, precision=FULL_PRECISION)


def row_tables(columns, kept_modes, padded_modes):
    places = jnp.arange(columns, dtype=jnp.int32)[:, None]
    orders = jnp.arange(padded_modes, dtype=jnp.int32)[None, :]
    angles = 2.0 * math.pi / columns * (places * orders % columns).astype(jnp.float32)
    factor = 1.0 / math.sqrt(columns)
    single = jnp.logical_or(orders == 0, 2 * orders == columns)
    doubled = jnp.where(single, 1.0, 2.0).astype(jnp.float32)
    used = jnp.where(orders < kept_modes, 1.0, 0.0).astype(jnp.float32)
    return (
        jnp.cos(angles) * factor * used,
        -jnp.sin(angles) * factor * used,
        jnp.transpose(jnp.cos(angles) * doubled * factor * used),
        jnp.transpose(jnp.sin(angles) * doubled * factor * used),
    )


def along_rows(values, tables):
    return jnp.stack(
        [
            jnp.einsum("bhwc,wk->bhkc", values, tables[0], precision=FULL_PRECISION),
            jnp.einsum("bhwc,wk->bhkc", values, tables[1], precision=FULL_PRECISION),
        ]
    )


def along_rows_back(paired, tables):
    return jnp.einsum("bhkc,wk->bhwc", paired[0], tables[0], precision=FULL_PRECISION) + jnp.einsum(
        "bhkc,wk->bhwc", paired[1], tables[1], precision=FULL_PRECISION
    )


def rows_inverse(paired, tables):
    return jnp.einsum("bhkc,kw->bhwc", paired[0], tables[2], precision=FULL_PRECISION) - jnp.einsum(
        "bhkc,kw->bhwc", paired[1], tables[3], precision=FULL_PRECISION
    )


def rows_inverse_back(values, tables):
    return jnp.stack(
        [
            jnp.einsum("bhwc,kw->bhkc", values, tables[2], precision=FULL_PRECISION),
            -jnp.einsum("bhwc,kw->bhkc", values, tables[3], precision=FULL_PRECISION),
        ]
    )


def column_tables(height):
    orders = jnp.arange(height, dtype=jnp.int32)[:, None]
    places = jnp.arange(height, dtype=jnp.int32)[None, :]
    angles = 2.0 * math.pi / height * (orders * places % height).astype(jnp.float32)
    factor = 1.0 / math.sqrt(height)
    return (jnp.cos(angles) * factor, jnp.sin(angles) * factor)


def to_freq(matrix, values):
    return jnp.einsum("kh,bhmc->bkmc", matrix, values, precision=FULL_PRECISION)


def from_freq(matrix, values):
    return jnp.einsum("kh,bkmc->bhmc", matrix, values, precision=FULL_PRECISION)


def spectral_core(paired, w_first, b_first, w_second, b_second):
    samples, height, kept_modes, channels = paired.shape[1:]
    blocks, block_size = (w_first.shape[1], w_first.shape[2])
    cosine, sine_table = column_tables(height)
    real_in, imag_in = (paired[0], paired[1])
    split_form = (samples, height, kept_modes, blocks, block_size)
    real_part = (to_freq(cosine, real_in) + to_freq(sine_table, imag_in)).reshape(split_form)
    imag_part = (to_freq(cosine, imag_in) - to_freq(sine_table, real_in)).reshape(split_form)
    first_real = jax.nn.relu(
        block_mix(real_part, w_first[0]) - block_mix(imag_part, w_first[1]) + b_first[0]
    )
    first_imag = jax.nn.relu(
        block_mix(imag_part, w_first[0]) + block_mix(real_part, w_first[1]) + b_first[1]
    )
    joined_form = (samples, height, kept_modes, channels)
    second_real = shrink(
        block_mix(first_real, w_second[0]) - block_mix(first_imag, w_second[1]) + b_second[0]
    ).reshape(joined_form)
    second_imag = shrink(
        block_mix(first_imag, w_second[0]) + block_mix(first_real, w_second[1]) + b_second[1]
    ).reshape(joined_form)
    out_real = from_freq(cosine, second_real) - from_freq(sine_table, second_imag)
    out_imag = from_freq(cosine, second_imag) + from_freq(sine_table, second_real)
    return jnp.stack([out_real, out_imag])


def column_layout(paired):
    return lax.all_to_all(paired, "space", split_axis=3, concat_axis=2, tiled=True)


def row_layout(paired):
    return lax.all_to_all(
        paired.astype(jnp.bfloat16), "space", split_axis=2, concat_axis=3, tiled=True
    ).astype(paired.dtype)


def norm_forward(values, gain, offset):
    width_all = values.shape[-1] * lax.axis_size("chan")
    totals = lax.psum((jnp.sum(values, axis=-1), jnp.sum(values * values, axis=-1)), "chan")
    average = totals[0] / width_all
    variance = totals[1] / width_all - average * average
    inverse_dev = lax.rsqrt(variance + NORM_EPS)[..., None]
    scaled = (values - average[..., None]) * inverse_dev
    return (scaled * gain + offset, (scaled, inverse_dev))


def norm_backward(gradient, gain, saved):
    scaled, inverse_dev = saved
    width_all = scaled.shape[-1] * lax.axis_size("chan")
    scaled_grad = gradient * gain
    totals = lax.psum(
        (jnp.sum(scaled_grad, axis=-1), jnp.sum(scaled_grad * scaled, axis=-1)), "chan"
    )
    values_grad = inverse_dev * (
        scaled_grad - totals[0][..., None] / width_all - scaled * (totals[1][..., None] / width_all)
    )
    return (
        values_grad,
        jnp.sum(gradient * scaled, axis=(0, 1, 2)),
        jnp.sum(gradient, axis=(0, 1, 2)),
    )


def shards(
    current_atmosphere,
    truth_one,
    truth_two,
    storm_codes,
    pre_gain,
    pre_shift,
    mix_weight_in,
    mix_bias_in,
    mix_weight_out,
    mix_bias_out,
    post_gain,
    post_shift,
    up_weight,
    up_bias,
    down_weight,
    down_bias,
):
    samples, rows_here, merged = current_atmosphere.shape
    columns = W
    channels = merged // columns
    total_rows = samples * rows_here * columns
    space_count = lax.axis_size("space")
    padded_modes = (KW + space_count - 1) // space_count * space_count
    tables = row_tables(columns, KW, padded_modes)

    def to_cells(flat_field):
        return jnp.transpose(
            flat_field.reshape(samples, rows_here, channels, columns), (0, 1, 3, 2)
        )

    def to_flat(cell_field):
        return jnp.transpose(cell_field, (0, 1, 3, 2)).reshape(samples, rows_here, merged)

    start_cells = to_cells(current_atmosphere)
    target_one = to_cells(truth_one)
    target_two = to_cells(truth_two)
    weight_of = (storm_codes.astype(jnp.float32) / 64.0).reshape(-1, 1, 1, 1)
    full_up, full_down, full_up_bias, full_down_bias = (up_weight, down_weight, up_bias, down_bias)

    def mlp_forward(inputs):
        gathered = lax.all_gather(inputs, "chan", axis=1, tiled=True)
        hidden = jnp.dot(
            gathered, full_up, preferred_element_type=jnp.float32
        ) + full_up_bias.astype(jnp.float32)
        active_full, gelu_pull = jax.vjp(exact_gelu, hidden)
        active = active_full.astype(jnp.bfloat16)
        product = jnp.dot(active, full_down, preferred_element_type=jnp.float32)
        output = lax.psum_scatter(
            product.astype(jnp.bfloat16), "chan", scatter_dimension=1, tiled=True
        ).astype(jnp.float32) + full_down_bias.astype(jnp.float32)
        return (output, (gathered, gelu_pull, active))

    def mlp_backward(gradient, saved):
        gathered, gelu_pull, active = saved
        grad_low = gradient.astype(jnp.bfloat16)
        grad_rows = lax.all_gather(grad_low, "chan", axis=1, tiled=True)
        down_bias_grad = jnp.sum(grad_low.astype(jnp.float32), axis=0)
        down_grad = jnp.dot(active.T, grad_rows, preferred_element_type=jnp.float32)
        active_grad = jnp.dot(grad_rows, full_down.T, preferred_element_type=jnp.float32)
        hidden_grad = gelu_pull(active_grad)[0].astype(jnp.bfloat16)
        up_grad = jnp.dot(gathered.T, hidden_grad, preferred_element_type=jnp.float32)
        up_bias_grad = jnp.sum(hidden_grad.astype(jnp.float32), axis=0)
        input_part = jnp.dot(hidden_grad, full_up.T, preferred_element_type=jnp.float32)
        input_grad = lax.psum_scatter(
            input_part.astype(jnp.bfloat16), "chan", scatter_dimension=1, tiled=True
        ).astype(jnp.float32)
        return (input_grad, (up_grad, up_bias_grad, down_grad, down_bias_grad))

    def forward_block(values):
        normed, first_saved = norm_forward(values, pre_gain, pre_shift)
        modal_in = column_layout(along_rows(normed, tables))
        filtered, core_pull = jax.vjp(
            spectral_core, modal_in, mix_weight_in, mix_bias_in, mix_weight_out, mix_bias_out
        )
        middle = rows_inverse(row_layout(filtered), tables) + normed + values
        entry, second_residuals = norm_forward(middle, post_gain, post_shift)
        output, mlp_saved = mlp_forward(entry.astype(jnp.bfloat16).reshape(total_rows, channels))
        return (
            output.reshape(values.shape) + middle,
            (first_saved, core_pull, second_residuals, mlp_saved),
        )

    def backward_block(gradient, saved):
        first_saved, core_pull, second_residuals, mlp_saved = saved
        mlp_grad, dense_grads = mlp_backward(gradient.reshape(total_rows, channels), mlp_saved)
        middle_part, post_gain_grad, post_shift_grad = norm_backward(
            mlp_grad.reshape(gradient.shape), post_gain, second_residuals
        )
        middle_grad = middle_part + gradient
        filter_grads = core_pull(column_layout(rows_inverse_back(middle_grad, tables)))
        normed_grad = along_rows_back(row_layout(filter_grads[0]), tables) + middle_grad
        input_part, pre_gain_grad, pre_shift_grad = norm_backward(
            normed_grad, pre_gain, first_saved
        )
        return (
            input_part + middle_grad,
            (pre_gain_grad, pre_shift_grad)
            + tuple(filter_grads[1:])
            + (post_gain_grad, post_shift_grad)
            + dense_grads,
        )

    first_out, first_saved_all = forward_block(start_cells)
    second_out, second_saved_all = forward_block(first_out)
    carried, grads_late = backward_block(weight_of * (second_out - target_two), second_saved_all)
    input_grad, grads_early = backward_block(
        weight_of * (first_out - target_one) + carried, first_saved_all
    )
    summed = jax.tree.map(jnp.add, grads_early, grads_late)
    (
        sum_pre_gain,
        sum_pre_shift,
        sum_mix_w_in,
        summed_mixing_bias_input,
        sum_mix_w_out,
        sum_mix_b_out,
        sum_post_gain,
        sum_post_shift,
        sum_up,
        sum_up_bias,
        sum_down,
        sum_down_bias,
    ) = summed
    totals = (
        lax.psum(sum_pre_gain.astype(jnp.bfloat16), "space").astype(jnp.float32),
        lax.psum(sum_pre_shift.astype(jnp.bfloat16), "space").astype(jnp.float32),
        lax.psum(sum_mix_w_in.astype(jnp.bfloat16), "space").astype(jnp.float32),
        lax.psum(summed_mixing_bias_input.astype(jnp.bfloat16), "space").astype(jnp.float32),
        lax.psum(sum_mix_w_out.astype(jnp.bfloat16), "space").astype(jnp.float32),
        lax.psum(sum_mix_b_out.astype(jnp.bfloat16), "space").astype(jnp.float32),
        lax.psum(sum_post_gain.astype(jnp.bfloat16), "space").astype(jnp.float32),
        lax.psum(sum_post_shift.astype(jnp.bfloat16), "space").astype(jnp.float32),
        lax.psum(sum_up.astype(jnp.bfloat16), "space").astype(jnp.float32),
        lax.psum(sum_up_bias.astype(jnp.bfloat16), "space").astype(jnp.float32),
        lax.psum(sum_down.astype(jnp.bfloat16), "space").astype(jnp.float32),
        lax.psum(sum_down_bias.astype(jnp.bfloat16), "space").astype(jnp.float32),
    )
    return (to_flat(first_out), to_flat(second_out), to_flat(input_grad)) + tuple(totals)


BF = jnp.bfloat16
F32 = jnp.float32
MESH_ID = pl.DeviceIdType.MESH
VMEM_BYTES = 66 * 1024 * 1024 - 1024 * 1024


def mm(a, b):
    return jnp.dot(a, b, preferred_element_type=F32)


def mm_nt(a, b):
    return lax.dot_general(a, b, (((1,), (1,)), ((), ())), preferred_element_type=F32)


def mm_tn(a, b):
    return lax.dot_general(a, b, (((0,), (0,)), ((), ())), preferred_element_type=F32)


def halves(v):
    high = v.astype(BF)
    return high, (v - high.astype(F32)).astype(BF)


def mm3(a, b):
    return mm(a[0], b[0]) + (mm(a[0], b[1]) + mm(a[1], b[0]))


def const_halves(table):
    table = np.asarray(table, np.float32)
    high = table.astype(ml_dtypes.bfloat16)
    low = (table - high.astype(np.float32)).astype(ml_dtypes.bfloat16)
    return jnp.asarray(high), jnp.asarray(low)


def row_constants(columns):
    half = columns // 2
    place = np.arange(columns)
    mode = np.arange(half)
    angle = 2.0 * np.pi * np.outer(mode, place) / columns
    real = np.cos(angle)
    imag = -np.sin(angle)
    imag[0] = np.cos(np.pi * place)
    forward = np.concatenate([real, imag]) / np.sqrt(columns)
    weight = np.where(mode == 0, 1.0, 2.0)
    inverse = (forward * np.concatenate([weight, weight])[:, None]).T
    return forward, inverse


def column_constants(height, rows, group):
    owners = height // rows
    angle = 2.0 * np.pi * np.outer(np.arange(height), np.arange(height)) / height
    cosine = np.cos(angle) / np.sqrt(height)
    sine = np.sin(angle) / np.sqrt(height)

    def spread(matrix):
        wide = np.zeros((group, height, owners, group, rows))
        for column in range(group):
            wide[column, :, :, column, :] = matrix.reshape(height, owners, rows)
        return wide.reshape(group * height, owners * group * rows)

    cosine, sine = spread(cosine), spread(sine)
    return np.block([[cosine, sine], [-sine, cosine]])


def signal_peers(axis, count, barrier):
    me = lax.axis_index(axis)
    for step in range(1, count):
        pl.semaphore_signal(
            barrier, inc=1, device_id={axis: lax.rem(me + step, count)}, device_id_type=MESH_ID
        )


def push(axis, count, step, source, target, send_sem, recv_sem):
    peer = lax.rem(lax.axis_index(axis) + step, count)
    return pltpu.make_async_remote_copy(
        src_ref=source,
        dst_ref=target,
        send_sem=send_sem.at[step],
        recv_sem=recv_sem.at[step],
        device_id={axis: peer},
        device_id_type=MESH_ID,
    )


def params(collective_id=None):
    return pltpu.CompilerParams(
        collective_id=collective_id,
        has_side_effects=collective_id is not None,
        vmem_limit_bytes=VMEM_BYTES,
    )


def launch(body, ins, outs, scratch, name, collective_id=None, in_specs=None, out_specs=None, grid=()):
    in_specs, out_specs = in_specs or {}, out_specs or {}
    names = list(ins) + list(outs) + list(scratch)
    whole = pl.BlockSpec(memory_space=pltpu.VMEM)
    results = pl.pallas_call(
        lambda *refs: body(types.SimpleNamespace(**dict(zip(names, refs)))),
        grid=grid,
        in_specs=[in_specs.get(key, whole) for key in ins],
        out_specs=[out_specs.get(key, whole) for key in outs],
        out_shape=[jax.ShapeDtypeStruct(*outs[key]) for key in outs],
        scratch_shapes=list(scratch.values()),
        compiler_params=params(collective_id),
        name=name,
    )(*ins.values())
    return dict(zip(outs, results))


IN_PLACE = pl.BlockSpec(memory_space=pl.ANY)


def sems(*counts):
    return pltpu.SemaphoreType.DMA(counts)


def run_copies(copies):
    for copy in copies:
        copy.start()
    for copy in copies:
        copy.wait()


def cells_from_lines(lines_ref, h, scratch_ref):
    features = scratch_ref.shape[1]
    per = 640 // W
    groups = features // per
    wide = jnp.concatenate(
        [lines_ref[h, pl.ds(part, groups, stride=5), :] for part in range(5)], axis=1
    )
    for part in range(per):
        piece = wide[:, part * W : (part + 1) * W]
        scratch_ref[0, pl.ds(part, groups, stride=per), :] = piece[:, :128]
        scratch_ref[1, pl.ds(part, groups, stride=per), :] = jnp.concatenate(
            [piece[:, 128:], jnp.zeros((groups, 256 - W), F32)], axis=1
        )
    return jnp.concatenate([scratch_ref[0], scratch_ref[1][:, : W - 128]], axis=1)


def enter(lines_ref, cells_ref, scratch_ref):
    def row(h, carry):
        cells_ref[h] = cells_from_lines(lines_ref, h, scratch_ref).T
        return carry

    lax.fori_loop(0, lines_ref.shape[0], row, 0)


def leave(cells_ref, lines_ref, scratch_ref):
    features = scratch_ref.shape[1]
    per = 640 // W
    groups = features // per

    def row(h, carry):
        block = cells_ref[h].T
        scratch_ref[0] = block[:, :128]
        scratch_ref[1] = jnp.concatenate([block[:, 128:], jnp.zeros((features, 256 - W), F32)], axis=1)
        wide = jnp.concatenate(
            [
                piece
                for part in range(per)
                for piece in (
                    scratch_ref[0, pl.ds(part, groups, stride=per), :],
                    scratch_ref[1, pl.ds(part, groups, stride=per), :][:, : W - 128],
                )
            ],
            axis=1,
        )
        for part in range(5):
            lines_ref[h, pl.ds(part, groups, stride=5), :] = wide[:, part * 128 : (part + 1) * 128]
        return carry

    lax.fori_loop(0, lines_ref.shape[0], row, 0)


def entry_norm(lines, vectors, sizes):
    rows, features, columns, spaces, chans = sizes

    def body(r):
        me = lax.axis_index("chan")
        barrier = pltpu.get_barrier_semaphore()
        signal_peers("chan", chans, barrier)

        def first(h, carry):
            block = cells_from_lines(r.lines, h, r.turn)
            r.flat[h] = block
            total = jnp.sum(block, axis=0, keepdims=True)
            centred = block - total * (1.0 / features)
            r.mine[pl.ds(h, 1), :] = total
            r.mine[pl.ds(rows + h, 1), :] = jnp.sum(centred * centred, axis=0, keepdims=True)
            return carry

        lax.fori_loop(0, rows, first, 0)
        r.all[me] = r.mine[...]
        r.gathered[me] = r.vectors[...]
        pl.semaphore_wait(barrier, chans - 1)
        run_copies(
            [push("chan", chans, step, r.mine, r.all.at[me], r.s1, r.r1) for step in range(1, chans)]
            + [push("chan", chans, step, r.vectors, r.gathered.at[me], r.s2, r.r2) for step in range(1, chans)]
        )
        totals = [r.all[j] for j in range(chans)]
        mean = sum(t[:rows] for t in totals) * (1.0 / (features * chans))
        spread = sum(
            t[rows:] + features * jnp.square(t[:rows] * (1.0 / features) - mean) for t in totals
        ) * (1.0 / (features * chans))
        inverse = lax.rsqrt(spread + NORM_EPS)
        r.mine[pl.ds(0, rows), :] = mean
        r.mine[pl.ds(rows, rows), :] = inverse

        def second(h, carry):
            block = r.flat[h]
            inv = r.mine[pl.ds(rows + h, 1), :]
            r.x[h] = block.T
            r.unit[h] = ((block - r.mine[pl.ds(h, 1), :]) * inv).T
            r.dev[h] = jnp.broadcast_to(inv, (8, columns)).T
            return carry

        lax.fori_loop(0, rows, second, 0)

    field = ((rows, columns, features), F32)
    return launch(
        body,
        {"lines": lines, "vectors": vectors},
        {
            "x": field,
            "unit": field,
            "dev": ((rows, columns, 8), F32),
            "gathered": ((chans,) + vectors.shape, F32),
        },
        {
            "flat": pltpu.VMEM((rows, features, columns), F32),
            "turn": pltpu.VMEM((2, features, 128), F32),
            "mine": pltpu.VMEM((2 * rows, columns), F32),
            "all": pltpu.VMEM((chans, 2 * rows, columns), F32),
            "s1": sems(chans),
            "r1": sems(chans),
            "s2": sems(chans),
            "r2": sems(chans),
        },
        "entry_norm",
        0,
    )


def pack_lanes(flat_ref, place, real, imag):
    flat_ref[0, place, :] = real[:, :128]
    flat_ref[1, place, :] = imag[:, :128]
    flat_ref[2, place, :] = jnp.concatenate([real[:, 128:], imag[:, 128:]], axis=1)


def join_lanes(first, second, rest):
    real = jnp.concatenate([first, rest[:, :64]], axis=1)
    imag = jnp.concatenate([second, rest[:, 64:]], axis=1)
    return real, imag


def unpack_lanes(flat_ref, place):
    return join_lanes(flat_ref[0, place, :], flat_ref[1, place, :], flat_ref[2, place, :])


LEVEL = 32000.0


def encode_fixed(values):
    largest = jnp.max(jnp.abs(values), axis=1, keepdims=True)
    grade = jnp.ceil(jnp.log2(jnp.maximum(largest, 1e-30)) * 256.0 + 0.01)
    coded = jnp.round(values * (LEVEL * jnp.exp2(grade * (-1.0 / 256.0))))
    lines = [coded[k] for k in range(3)] + [grade[k] for k in range(3)] + [jnp.zeros((5, 128), F32)]
    return jnp.concatenate(lines, axis=0).astype(jnp.int32).astype(jnp.int16)


def decode_fixed(coded, thick):
    values = coded.astype(jnp.int32).astype(F32)
    scale = jnp.exp2(values[3 * thick : 3 * thick + 3] * (1.0 / 256.0)) * (1.0 / LEVEL)
    return [values[k * thick : (k + 1) * thick] * scale[k : k + 1] for k in range(3)]


def encode_plain(values):
    return jnp.concatenate([values[k] for k in range(3)], axis=0).astype(BF)


def decode_plain(coded, thick):
    values = coded.astype(F32)
    return [values[k * thick : (k + 1) * thick] for k in range(3)]


class Exchange:
    def __init__(self, fixed, spaces, thick, send_ref, recv_ref, send_sem, recv_sem):
        self.encode, self.decode = (encode_fixed, decode_fixed) if fixed else (encode_plain, decode_plain)
        self.spaces, self.thick = spaces, thick
        self.send_ref, self.recv_ref = send_ref, recv_ref
        self.send_sem, self.recv_sem = send_sem, recv_sem
        self.me = lax.axis_index("space")

    @staticmethod
    def shape(fixed, spaces, thick, pairs):
        return pltpu.VMEM((pairs, spaces, 3 * thick + (8 if fixed else 0), 128), jnp.int16 if fixed else BF)

    def copy(self, p, step):
        peer = lax.rem(self.me + step, self.spaces)
        return pltpu.make_async_remote_copy(
            src_ref=self.send_ref.at[p, peer],
            dst_ref=self.recv_ref.at[p, self.me],
            send_sem=self.send_sem.at[p, step],
            recv_sem=self.recv_sem.at[p, step],
            device_id={"space": peer},
            device_id_type=MESH_ID,
        )

    def send(self, p, flat_ref, start_of):
        for step in list(range(1, self.spaces)) + [0]:
            peer = lax.rem(self.me + step, self.spaces)
            rows = pl.ds(pl.multiple_of(start_of(peer), 8), self.thick)
            coded = self.encode(flat_ref[:, rows, :])
            if step:
                self.send_ref[p, peer] = coded
                self.copy(p, step).start()
            else:
                self.recv_ref[p, peer] = coded

    def arrive(self, p):
        for step in range(1, self.spaces):
            self.copy(p, step).wait_recv()

    def take(self, p, source):
        return self.decode(self.recv_ref[p, source], self.thick)

    def close(self, pairs):
        def pair(p, carry):
            for step in range(1, self.spaces):
                self.copy(p, step).wait_send()
            return carry

        lax.fori_loop(0, pairs, pair, 0)


def pair_inputs(q, exchange, even_ref):
    p = jnp.maximum(q - 1, 0)

    @pl.when(q != 1)
    def _():
        exchange.arrive(p)

    extra = (q == 0).astype(F32)
    zeroth = jnp.logical_and(exchange.me == 0, p == 0).astype(F32)
    parts = [join_lanes(*exchange.take(p, s)) for s in range(exchange.spaces)]
    real = jnp.concatenate([part[0] for part in parts], axis=0)
    imag = jnp.concatenate([part[1] for part in parts], axis=0)
    chosen = imag * (even_ref[...] * zeroth)
    real = real * (1.0 - extra) + chosen * extra
    imag = (imag - chosen) * (1.0 - extra)
    return p, zeroth, jnp.concatenate([real, imag], axis=0)


def pair_outputs(q, p, zeroth, result, exchange, even_ref, kept_ref, stage_ref):
    half = result.shape[0] // 2
    real, imag = result[:half], result[half:]

    @pl.when(q == 0)
    def _():
        kept_ref[...] = real

    @pl.when(q > 0)
    def _():
        chosen = even_ref[...] * zeroth
        pack_lanes(stage_ref, slice(None), real, imag * (1.0 - chosen) + kept_ref[...] * chosen)
        exchange.send(p, stage_ref, lambda peer: peer * exchange.thick)


def collect(exchange, pairs, chunk, flat_ref):
    def pair(p, carry):
        exchange.arrive(p)
        for s in range(exchange.spaces):
            rows = pl.ds(pl.multiple_of(s * chunk + p * exchange.thick, 8), exchange.thick)
            for k, part in enumerate(exchange.take(p, s)):
                flat_ref[k, rows, :] = part
        return carry

    lax.fori_loop(0, pairs, pair, 0)


def send_modes(exchange, pairs, chunk, flat_ref):
    def pair(p, carry):
        exchange.send(p, flat_ref, lambda peer: peer * chunk + p * exchange.thick)
        return carry

    lax.fori_loop(0, pairs, pair, 0)


def spectral_forward(source, weights, gain, shift, tables, mix, bias, relayout, fine, sizes, collective_id):
    rows, features, columns, spaces, chans = sizes
    opening = "x" in source
    modes = columns // 2
    total = modes * rows
    chunk = total // spaces
    half = tables["even"].shape[0]
    thick = half // spaces
    pairs = chunk // thick
    cells = rows * columns // chans
    share = rows // chans

    def body(r):
        barrier = pltpu.get_barrier_semaphore()
        signal_peers("space", spaces, barrier)
        signal_peers("chan", chans, barrier)
        gain = r.gain[...]
        shift = r.shift[...]

        def to_modes(h, carry):
            if opening:
                unit = r.unit[h]
            else:
                home = r.home[h].astype(F32)
                x = home[:, :features] + r.before[h]
                mean = home[:, features : features + 1] + (
                    home[:, features + 1 : features + 2] + home[:, features + 2 : features + 3]
                )
                dev = home[:, features + 3 : features + 4] + (
                    home[:, features + 4 : features + 5] + home[:, features + 5 : features + 6]
                )
                unit = (x - mean) * dev
                r.x[h] = x
                r.unit[h] = unit
                r.dev[h] = jnp.broadcast_to(dev, (columns, 8))
            out = mm3((r.row[0], r.row[1]), halves(unit * gain + shift))
            pack_lanes(r.flat, pl.ds(h, modes, stride=rows), out[:modes], out[modes:])
            return carry

        lax.fori_loop(0, rows, to_modes, 0)
        pl.semaphore_wait(barrier, spaces + chans - 2)
        there = Exchange(True, spaces, thick, r.send1, r.recv1, r.s1, r.r1)
        back = Exchange(fine, spaces, thick, r.send2, r.recv2, r.s2, r.r2)
        send_modes(there, pairs, chunk, r.flat)
        me = lax.axis_index("chan")
        slow = []
        if opening:
            core = lax.rem(there.me, 2)

            def pass_on(kind, slot, number):
                sibling = there.me + 1 - 2 * core
                return pltpu.make_async_remote_copy(
                    src_ref=r.weights.at[kind] if number < 2 else r.all_weights.at[kind, slot],
                    dst_ref=r.all_weights.at[kind, slot],
                    send_sem=r.s5.at[number],
                    recv_sem=r.r5.at[number],
                    device_id={"space": sibling},
                    device_id_type=MESH_ID,
                )

            slow = [
                push("chan", chans, step, r.weights.at[core], r.all_weights.at[core, me], r.s4, r.r4)
                for step in range(1, chans)
            ]
            passed = [pass_on(0, me, 0), pass_on(1, me, 1)]
            for copy in slow + passed:
                copy.start()
        enter(r.lines_a, r.cells_a, r.turn)

        def filter_pair(q, carry):
            p, zeroth, block = pair_inputs(q, there, r.even)
            spec = mm3((r.col[0], r.col[1]), halves(block))
            r.spec[q] = spec.astype(BF)
            parts = halves(spec)
            straight = mm3(parts, (r.mix[0, 0, 0], r.mix[0, 0, 1]))
            crossed = mm3(parts, (r.mix[0, 1, 0], r.mix[0, 1, 1]))
            first = jnp.concatenate(
                [
                    jnp.maximum(straight[:half] - crossed[half:] + r.bias[0:1], 0.0),
                    jnp.maximum(straight[half:] + crossed[:half] + r.bias[1:2], 0.0),
                ],
                axis=0,
            )
            r.first[q] = first.astype(BF)
            parts = halves(first)
            straight = mm3(parts, (r.mix[1, 0, 0], r.mix[1, 0, 1]))
            crossed = mm3(parts, (r.mix[1, 1, 0], r.mix[1, 1, 1]))
            second = jnp.concatenate(
                [
                    straight[:half] - crossed[half:] + r.bias[2:3],
                    straight[half:] + crossed[:half] + r.bias[3:4],
                ],
                axis=0,
            )
            second = second - jnp.clip(second, -SHRINK_LEVEL, SHRINK_LEVEL)
            r.second[q] = second.astype(BF)
            if fine:
                result = mm3((r.colinv[0], r.colinv[1]), halves(second))
            else:
                result = mm(r.colinv[0], second.astype(BF))
            pair_outputs(q, p, zeroth, result, back, r.even, r.kept, r.stage)
            return carry

        lax.fori_loop(0, pairs + 1, filter_pair, 0)
        if opening:
            for step in range(1, chans):
                slow[step - 1].wait()
                sender = lax.rem(me - step + chans, chans)
                copy = pass_on(core, sender, 1 + step)
                copy.start()
                passed.append(copy)
        collect(back, pairs, chunk, r.flat)
        copies = []
        for step in list(range(1, chans)) + [0]:
            peer = lax.rem(me + step, chans)

            def to_places(i, carry):
                h = peer * share + i
                real, imag = unpack_lanes(r.flat, pl.ds(h, modes, stride=rows))
                block = jnp.concatenate([real, imag], axis=0)
                if fine:
                    out = mm3((r.rowinv[0], r.rowinv[1]), halves(block))
                else:
                    out = mm(r.rowinv[0], block.astype(BF))
                middle = out + (r.unit[h] * gain + shift) + r.x[h]
                r.middle[h] = middle
                r.own[peer, pl.ds(pl.multiple_of(i * columns, 16), columns), :] = middle.astype(BF)
                return carry

            lax.fori_loop(0, share, to_places, 0)
            if step:
                copy = push("chan", chans, step, r.own.at[peer], r.mid.at[me], r.s3, r.r3)
                copy.start()
                copies.append(copy)
            else:
                r.mid[me] = r.own[me]
        there.close(pairs)
        back.close(pairs)
        for copy in copies:
            copy.wait()
        if opening:
            for copy in passed:
                copy.wait()

    field = ((rows, columns, features), F32)
    kept = ((pairs + 1, 2 * half, features), BF)
    ins = dict(source)
    ins.update(gain=gain, shift=shift, mix=mix, bias=bias)
    ins.update({key: tables[key] for key in ("row", "rowinv", "col", "colinv", "even")})
    outs = {
        "middle": field,
        "mid": ((chans, cells, features), BF),
        "spec": kept,
        "first": kept,
        "second": kept,
    }
    in_specs, out_specs = {}, {}
    scratch = {
        "flat": pltpu.VMEM((3, total, 128), F32),
        "stage": pltpu.VMEM((3, half, 128), F32),
        "kept": pltpu.VMEM((half, features), F32),
        "turn": pltpu.VMEM((2, features, 128), F32),
        "send1": Exchange.shape(True, spaces, thick, pairs),
        "recv1": Exchange.shape(True, spaces, thick, pairs),
        "send2": Exchange.shape(fine, spaces, thick, pairs),
        "recv2": Exchange.shape(fine, spaces, thick, pairs),
        "own": pltpu.VMEM((chans, cells, features), BF),
        "s1": sems(pairs, spaces),
        "r1": sems(pairs, spaces),
        "s2": sems(pairs, spaces),
        "r2": sems(pairs, spaces),
        "s3": sems(chans),
        "r3": sems(chans),
    }
    ins.update(lines_a=relayout)
    outs.update(cells_a=field)
    if opening:
        ins.update(weights=weights)
        outs.update(all_weights=((2, chans) + weights.shape[1:], BF))
        in_specs.update(weights=IN_PLACE)
        out_specs.update(all_weights=IN_PLACE)
        scratch.update(s4=sems(chans), r4=sems(chans), s5=sems(chans + 1), r5=sems(chans + 1))
    else:
        outs.update(x=field, unit=field, dev=((rows, columns, 8), F32))
    return launch(body, ins, outs, scratch, "spectral_forward", collective_id, in_specs, out_specs)


def spectral_backward(
    g, dv, unit, dev, gain, tables, mix, saved, leaving, following, before, dense, sizes, collective_id
):
    rows, features, columns, spaces, chans = sizes
    modes = columns // 2
    total = modes * rows
    chunk = total // spaces
    half = tables["even"].shape[0]
    thick = half // spaces
    pairs = chunk // thick
    size = features // 2

    def body(r):
        barrier = pltpu.get_barrier_semaphore()
        signal_peers("space", spaces, barrier)
        signal_peers("chan", chans, barrier)
        gain = r.gain[...]
        me = lax.axis_index("chan")

        def to_modes(h, carry):
            middle_grad = r.g[h] + r.dv[h].astype(F32)
            r.out[h] = middle_grad
            out = mm(r.rowinv_t[...], middle_grad.astype(BF))
            pack_lanes(r.flat, pl.ds(h, modes, stride=rows), out[:modes], out[modes:])
            return carry

        lax.fori_loop(0, rows, to_modes, 0)
        pl.semaphore_wait(barrier, spaces + chans - 2)
        there = Exchange(False, spaces, thick, r.send1, r.recv1, r.s1, r.r1)
        back = Exchange(False, spaces, thick, r.send2, r.recv2, r.s2, r.r2)
        send_modes(there, pairs, chunk, r.flat)
        slow = []
        if dense is not None:
            for step in range(1, chans):
                peer = lax.rem(me + step, chans)
                slow.append(push("chan", chans, step, r.weights.at[peer], r.landed.at[me], r.s4, r.r4))
                slow.append(push("chan", chans, step, r.rest.at[peer], r.rest_landed.at[me], r.s5, r.r5))
            for copy in slow:
                copy.start()
        leave(r.leaving, r.lines, r.turn)
        r.mixgrad[...] = jnp.zeros_like(r.mixgrad)
        r.biasgrad[...] = jnp.zeros_like(r.biasgrad)

        def turned(v):
            return jnp.concatenate([v[half:], -v[:half]], axis=0)

        def note_bias(index, value):
            r.biasgrad[index : index + 1, :] += jnp.sum(value, axis=0, keepdims=True)

        def filter_pair(q, carry):
            p, zeroth, block = pair_inputs(q, there, r.even)
            grad = mm(r.col[0], block.astype(BF))
            grad = jnp.where(r.second[q].astype(F32) == 0.0, 0.0, grad)
            note_bias(2, grad[:half])
            note_bias(3, grad[half:])
            low = grad.astype(BF)
            first = r.first[q]
            r.mixgrad[1, 0] += mm_tn(first, low)
            r.mixgrad[1, 1] += mm_tn(first, turned(grad).astype(BF))
            straight = mm_nt(low, r.mix[1, 0, 0])
            crossed = mm_nt(low, r.mix[1, 1, 0])
            grad = jnp.concatenate(
                [straight[:half] + crossed[half:], straight[half:] - crossed[:half]], axis=0
            )
            grad = jnp.where(first.astype(F32) > 0.0, grad, 0.0)
            note_bias(0, grad[:half])
            note_bias(1, grad[half:])
            low = grad.astype(BF)
            spec = r.spec[q]
            r.mixgrad[0, 0] += mm_tn(spec, low)
            r.mixgrad[0, 1] += mm_tn(spec, turned(grad).astype(BF))
            straight = mm_nt(low, r.mix[0, 0, 0])
            crossed = mm_nt(low, r.mix[0, 1, 0])
            grad = jnp.concatenate(
                [straight[:half] + crossed[half:], straight[half:] - crossed[:half]], axis=0
            )
            result = mm(r.colinv[0], grad.astype(BF))
            pair_outputs(q, p, zeroth, result, back, r.even, r.kept, r.stage)
            return carry

        lax.fori_loop(0, pairs + 1, filter_pair, 0)
        for layer in range(2):
            for part in range(2):
                for block in range(2):
                    own = slice(block * size, (block + 1) * size)
                    piece = r.mixgrad[layer, part][own, own]
                    piece = jnp.concatenate([piece, jnp.zeros((size, 128 - size), F32)], axis=1)
                    start = ((layer * 2 + part) * 2 + block) * size
                    place = slice(start, start + size)
                    r.sums[place, :] = piece + r.before[place, :] if before is not None else piece
        collect(back, pairs, chunk, r.flat)
        lane = lax.broadcasted_iota(jnp.int32, (columns, 128), 1)

        def to_places(h, carry):
            table, one_sum, two_sum = carry
            real, imag = unpack_lanes(r.flat, pl.ds(h, modes, stride=rows))
            block = jnp.concatenate([real, imag], axis=0)
            grad = mm(r.row_t[...], block.astype(BF)) + r.out[h]
            unit = r.unit[h]
            one_sum += jnp.sum(grad * unit, axis=0, keepdims=True)
            two_sum += jnp.sum(grad, axis=0, keepdims=True)
            scaled = grad * gain
            r.scaled[h] = scaled
            one = jnp.sum(scaled, axis=1, keepdims=True)
            two = jnp.sum(scaled * unit, axis=1, keepdims=True)
            table = jnp.where(lane == h, one, table)
            return jnp.where(lane == rows + h, two, table), one_sum, two_sum

        none = jnp.zeros((1, features), F32)
        table, one_sum, two_sum = lax.fori_loop(
            0, rows, to_places, (jnp.zeros((columns, 128), F32), none, none)
        )
        table = table.T[: 2 * rows]
        r.mine[...] = table
        r.all[me] = table
        copies = [push("chan", chans, step, r.mine, r.all.at[me], r.s3, r.r3) for step in range(1, chans)]
        for copy in copies:
            copy.start()
        vectors = jnp.concatenate([r.biasgrad[0:4], one_sum, two_sum, none, none], axis=0)
        wide = jnp.concatenate([vectors, jnp.zeros((8, 256 - features), F32)], axis=1)
        wide = jnp.concatenate([wide[:, :128], wide[:, 128:]], axis=0)
        place = slice(8 * size, 8 * size + 16)
        r.sums[place, :] = wide + r.before[place, :] if before is not None else wide
        for copy in copies:
            copy.wait()
        means = sum(r.all[j] for j in range(chans)) * (1.0 / (features * chans))
        means = jnp.concatenate([means, jnp.zeros((128 - 2 * rows, columns), F32)], axis=0).T

        def result(h):
            one = jnp.sum(jnp.where(lane == h, means, 0.0), axis=1, keepdims=True)
            two = jnp.sum(jnp.where(lane == rows + h, means, 0.0), axis=1, keepdims=True)
            inverse = r.dev[h][:, :1]
            return r.out[h] + inverse * (r.scaled[h] - one - r.unit[h] * two)

        if following is None:

            def finish(h, carry):
                r.out[h] = result(h)
                return carry

            lax.fori_loop(0, rows, finish, 0)
        else:
            share = rows // chans
            copies = []
            for step in list(range(1, chans)) + [0]:
                peer = lax.rem(me + step, chans)

                def finish(i, carry):
                    h = peer * share + i
                    grad = r.weight[0:1, 0:1] * (r.x[h] - r.target[h]) + result(h)
                    r.out[h] = grad
                    r.own[peer, pl.ds(pl.multiple_of(i * columns, 16), columns), :] = grad.astype(BF)
                    return carry

                lax.fori_loop(0, share, finish, 0)
                if step:
                    copy = push("chan", chans, step, r.own.at[peer], r.upper.at[me], r.s6, r.r6)
                    copy.start()
                    copies.append(copy)
                else:
                    r.upper[me] = r.own[me]
            for copy in copies:
                copy.wait()
        there.close(pairs)
        back.close(pairs)
        for copy in slow:
            copy.wait()

    field = ((rows, columns, features), F32)
    ins = {"g": g, "dv": dv, "unit": unit, "dev": dev, "gain": gain, "mix": mix}
    ins.update({key: tables[key] for key in ("rowinv_t", "row_t", "col", "colinv", "even")})
    ins.update({key: saved[key] for key in ("spec", "first", "second")})
    outs = {"out": field, "sums": ((8 * size + 16, 128), F32)}
    scratch = {
        "flat": pltpu.VMEM((3, total, 128), F32),
        "stage": pltpu.VMEM((3, half, 128), F32),
        "kept": pltpu.VMEM((half, features), F32),
        "turn": pltpu.VMEM((2, features, 128), F32),
        "scaled": pltpu.VMEM((rows, columns, features), F32),
        "mixgrad": pltpu.VMEM((2, 2, features, features), F32),
        "biasgrad": pltpu.VMEM((8, features), F32),
        "mine": pltpu.VMEM((2 * rows, columns), F32),
        "all": pltpu.VMEM((chans, 2 * rows, columns), F32),
        "send1": Exchange.shape(False, spaces, thick, pairs),
        "recv1": Exchange.shape(False, spaces, thick, pairs),
        "send2": Exchange.shape(False, spaces, thick, pairs),
        "recv2": Exchange.shape(False, spaces, thick, pairs),
        "s1": sems(pairs, spaces),
        "r1": sems(pairs, spaces),
        "s2": sems(pairs, spaces),
        "r2": sems(pairs, spaces),
        "s3": sems(chans),
        "r3": sems(chans),
    }
    in_specs, out_specs = {}, {}
    ins.update(leaving=leaving)
    outs.update(lines=((rows, features * columns // 128, 128), F32))
    if following is not None:
        ins.update(x=following[0], target=following[1], weight=following[2])
        outs.update(upper=((chans, rows * columns // chans, features), BF))
        scratch.update(
            own=pltpu.VMEM((chans, rows * columns // chans, features), BF), s6=sems(chans), r6=sems(chans)
        )
    if before is not None:
        ins.update(before=before)
    if dense is not None:
        weights, rest = dense
        ins.update(weights=weights, rest=rest)
        outs.update(landed=(weights.shape, BF), rest_landed=(rest.shape, F32))
        in_specs.update(weights=IN_PLACE, rest=IN_PLACE)
        out_specs.update(landed=IN_PLACE, rest_landed=IN_PLACE)
        scratch.update(s4=sems(chans), r4=sems(chans), s5=sems(chans), r5=sems(chans))
    return launch(body, ins, outs, scratch, "spectral_backward", collective_id, in_specs, out_specs)


ERF = (0.254829592, -0.284496736, 1.421413741, -1.453152027, 1.061405429)


def gelu_and_slope(v):
    a = jnp.abs(v) * math.sqrt(0.5)
    t = 1.0 / (1.0 + 0.3275911 * a)
    e = jnp.exp(-a * a)
    tail = 0.5 * e * t * (ERF[0] + t * (ERF[1] + t * (ERF[2] + t * (ERF[3] + t * ERF[4]))))
    below = jnp.where(v >= 0.0, 1.0 - tail, tail)
    return v * below, below + v * e * (1.0 / math.sqrt(2.0 * math.pi))


def three_parts(v):
    a = v.astype(BF)
    rest = v - a.astype(F32)
    b = rest.astype(BF)
    return [a, b, (rest - b.astype(F32)).astype(BF)]


def fixed_block(shape):
    return pl.BlockSpec(shape, lambda t: (0,) * len(shape))


def full_vector(gathered_ref, start, size):
    chans = gathered_ref.shape[0]
    return jnp.concatenate([gathered_ref[j, 1:2, start : start + size] for j in range(chans)], axis=1)


def ffn_forward(mid, gathered, weights, sizes, collective_id):
    rows, features, columns, spaces, chans = sizes
    cells = mid.shape[1]
    width = features * chans
    local = weights.shape[3]
    tile = 256
    per = local // tile
    steps = chans * per
    hidden = chans * local

    def body(r):
        t = pl.program_id(0)
        barrier = pltpu.get_barrier_semaphore()

        def middle():
            return jnp.concatenate([r.mid[j].astype(F32) for j in range(chans)], axis=1)

        @pl.when(t == 0)
        def _():
            signal_peers("chan", chans, barrier)
            value = middle()
            mean = jnp.mean(value, axis=1, keepdims=True)
            centred = value - mean
            inverse = lax.rsqrt(jnp.mean(centred * centred, axis=1, keepdims=True) + NORM_EPS)
            unit = centred * inverse
            r.unit[...] = unit.astype(BF)
            r.dev[...] = jnp.broadcast_to(inverse, r.dev.shape)
            gain = full_vector(r.gathered, 0, features)
            shift = full_vector(r.gathered, features, features)
            r.entry[...] = (unit * gain + shift).astype(BF)
            r.total[...] = value + full_vector(r.gathered, 2 * features, features)

        bias = r.gathered[t // per, 0:1, pl.ds(pl.multiple_of((t % per) * tile, tile), tile)]
        value = mm(r.entry[...], r.up[0, 0]) + bias
        active, slope = gelu_and_slope(value)
        active = active.astype(BF)
        r.active[...] = active
        r.slope[...] = slope.astype(BF)
        r.total[...] += mm(active, r.down[0, 0])

        @pl.when(t == steps - 1)
        def _():
            me = lax.axis_index("chan")
            value = r.total[...]
            mean = jnp.mean(value, axis=1, keepdims=True)
            centred = value - mean
            inverse = lax.rsqrt(jnp.mean(centred * centred, axis=1, keepdims=True) + NORM_EPS)
            outer = value - middle()
            stats = jnp.concatenate(
                three_parts(mean) + three_parts(inverse) + [jnp.zeros((cells, 256 - features - 6), BF)],
                axis=1,
            )
            pl.semaphore_wait(barrier, chans - 1)
            for j in range(chans):
                r.send[j] = jnp.concatenate(
                    [outer[:, j * features : (j + 1) * features].astype(BF), stats], axis=1
                )
            copies = []
            for step in range(1, chans):
                peer = lax.rem(me + step, chans)
                copy = push("chan", chans, step, r.send.at[peer], r.land.at[me], r.s1, r.r1)
                copy.start()
                copies.append(copy)
            r.home[me] = r.send[me]
            for step in range(1, chans):
                copies[step - 1].wait()
                sender = lax.rem(me - step + chans, chans)
                r.home[sender] = r.land[sender]

    return launch(
        body,
        {"mid": mid, "gathered": gathered, "up": weights, "down": weights},
        {
            "home": ((chans, cells, 256), BF),
            "entry": ((cells, width), BF),
            "unit": ((cells, width), BF),
            "dev": ((cells, 128), F32),
            "active": ((cells, hidden), BF),
            "slope": ((cells, hidden), BF),
        },
        {
            "total": pltpu.VMEM((cells, width), F32),
            "send": pltpu.VMEM((chans, cells, 256), BF),
            "land": pltpu.VMEM((chans, cells, 256), BF),
            "s1": sems(chans),
            "r1": sems(chans),
        },
        "ffn_forward",
        collective_id,
        {
            "mid": fixed_block(mid.shape),
            "gathered": fixed_block(gathered.shape),
            "up": pl.BlockSpec((1, 1, width, tile), lambda t: (0, t // per, 0, t % per)),
            "down": pl.BlockSpec((1, 1, tile, width), lambda t: (1, t // per, t % per, 0)),
        },
        {
            "home": fixed_block((chans, cells, 256)),
            "entry": fixed_block((cells, width)),
            "unit": fixed_block((cells, width)),
            "dev": fixed_block((cells, 128)),
            "active": pl.BlockSpec((cells, tile), lambda t: (0, t)),
            "slope": pl.BlockSpec((cells, tile), lambda t: (0, t)),
        },
        (steps,),
    )


def ffn_backward(source, saved, gathered, weights, before, sizes, collective_id):
    rows, features, columns, spaces, chans = sizes
    final = "home" in source
    cells = rows * columns // chans
    width = features * chans
    local = weights.shape[3]
    tile = 256
    per = local // tile
    steps = chans * per

    def body(r):
        t = pl.program_id(0)
        barrier = pltpu.get_barrier_semaphore()
        me = lax.axis_index("chan")
        place = lax.axis_index("space")
        core = lax.rem(place, 2)
        sibling = place + 1 - 2 * core

        def swap(step):
            return pltpu.make_async_remote_copy(
                src_ref=r.give.at[step],
                dst_ref=r.take.at[step],
                send_sem=r.s3.at[step],
                recv_sem=r.r3.at[step],
                device_id={"space": sibling},
                device_id_type=MESH_ID,
            )

        @pl.when(t == 0)
        def _():
            signal_peers("chan", chans, barrier)
            r.total[...] = jnp.zeros_like(r.total)
            r.small[...] = jnp.zeros_like(r.small)
            if final:
                for j in range(chans):
                    value = r.home[j].astype(F32)[:, :features] + r.middle[j]
                    r.x[j] = value
                    grad = r.weight[0:1, 0:1] * (value - r.target[j])
                    r.g[j] = grad
                    r.low[j] = grad.astype(BF)
                pl.semaphore_wait(barrier, chans - 1)
                copies = []
                for step in range(1, chans):
                    peer = lax.rem(me + step, chans)
                    copy = push("chan", chans, step, r.low.at[peer], r.land.at[me], r.s1, r.r1)
                    copy.start()
                    copies.append(copy)
                r.land[me] = r.low[me]
                for copy in copies:
                    copy.wait()
                landed = r.land
            else:
                pl.semaphore_signal(barrier, inc=1, device_id={"space": sibling}, device_id_type=MESH_ID)
                pl.semaphore_wait(barrier, chans)
                landed = r.came
            upper = jnp.concatenate([landed[j].astype(F32) for j in range(chans)], axis=1)
            r.upper[...] = upper.astype(BF)
            r.small[2:3, :] = jnp.sum(upper, axis=0, keepdims=True)

        upper = r.upper[...]
        gdown = mm_tn(r.active[...], upper)
        lower = mm_nt(upper, r.down[0, 0]) * r.slope[...].astype(F32)
        r.upb[pl.ds(t, 1), :] = jnp.sum(lower, axis=0, keepdims=True)
        lower = lower.astype(BF)
        gup = mm_tn(lower, r.entry[...])
        r.total[...] += mm_nt(lower, r.up[0, 0])
        if final:
            r.gdown[0] = gdown.astype(BF)
            r.gup[0] = gup.astype(BF)
        else:
            gdown += r.prev_down[0].astype(F32)
            gup += r.prev_up[0].astype(F32)
            second = core == 1
            r.keep[t] = jnp.where(second, gup, gdown)
            r.give[t] = jnp.where(second, gdown, gup).astype(BF)
            swap(t).start()

        @pl.when(t == steps - 1)
        def _():
            grad = r.total[...]
            unit = r.unit[...].astype(F32)
            r.small[0:1, :] = jnp.sum(grad * unit, axis=0, keepdims=True)
            r.small[1:2, :] = jnp.sum(grad, axis=0, keepdims=True)
            scaled = grad * full_vector(r.gathered, 0, features)
            one = jnp.mean(scaled, axis=1, keepdims=True)
            two = jnp.mean(scaled * unit, axis=1, keepdims=True)
            result = r.dev[:, :1] * (scaled - one - unit * two)
            for j in range(chans):
                r.send[j] = result[:, j * features : (j + 1) * features].astype(BF)
            copies = []
            for step in range(1, chans):
                peer = lax.rem(me + step, chans)
                copy = push("chan", chans, step, r.send.at[peer], r.last.at[me], r.s2, r.r2)
                copy.start()
                copies.append(copy)
            r.dv[me] = r.send[me]
            r.rest[...] = jnp.zeros_like(r.rest)
            for j in range(chans):
                for k in range(per):
                    r.rest[j, 0:1, k * tile : (k + 1) * tile] = r.upb[j * per + k : j * per + k + 1, :]
                for k in range(3):
                    r.rest[j, 1 + k : 2 + k, 0:features] = r.small[k : k + 1, j * features : (j + 1) * features]
            if not final:
                r.rest[...] += r.prev_rest[...]
                for step in range(steps):
                    swap(step).wait()
                    r.sum[step // per, (step % per) * tile : (step % per + 1) * tile, :] = (
                        r.keep[step] + r.take[step].astype(F32)
                    ).astype(BF)
            for step in range(1, chans):
                copies[step - 1].wait()
                sender = lax.rem(me - step + chans, chans)
                r.dv[sender] = r.last[sender]

    by_cells = (chans, cells, features)
    grads = (chans, local, width)
    up_spec = pl.BlockSpec((1, 1, width, tile), lambda t: (0, t // per, 0, t % per))
    down_spec = pl.BlockSpec((1, 1, tile, width), lambda t: (1, t // per, t % per, 0))
    hidden_spec = pl.BlockSpec((1, tile, width), lambda t: (t // per, t % per, 0))
    cell_spec = pl.BlockSpec((cells, tile), lambda t: (0, t))
    ins = {key: value if key == "weight" else value.reshape(chans, cells, -1) for key, value in source.items()}
    ins.update({key: saved[key] for key in ("entry", "unit", "dev", "active", "slope")})
    ins.update(gathered=gathered, up=weights, down=weights)
    in_specs = {key: fixed_block(value.shape) for key, value in ins.items()}
    in_specs.update(active=cell_spec, slope=cell_spec, up=up_spec, down=down_spec)
    outs = {
        "dv": (by_cells, BF),
        "rest": ((chans, 8, local), F32),
    }
    scratch = {
        "send": pltpu.VMEM(by_cells, BF),
        "last": pltpu.VMEM(by_cells, BF),
        "upper": pltpu.VMEM((cells, width), BF),
        "total": pltpu.VMEM((cells, width), F32),
        "small": pltpu.VMEM((8, width), F32),
        "upb": pltpu.VMEM((-(-steps // 8) * 8, tile), F32),
        "s2": sems(chans),
        "r2": sems(chans),
    }
    if final:
        scratch.update(
            low=pltpu.VMEM(by_cells, BF), land=pltpu.VMEM(by_cells, BF), s1=sems(chans), r1=sems(chans)
        )
        outs.update(g=(by_cells, F32), x=(by_cells, F32), gdown=(grads, BF), gup=(grads, BF))
        out_specs = {key: fixed_block(outs[key][0]) for key in outs}
        out_specs.update(gdown=hidden_spec, gup=hidden_spec)
    else:
        ins.update(prev_down=before[0], prev_up=before[1], prev_rest=before[2])
        in_specs.update(prev_down=hidden_spec, prev_up=hidden_spec, prev_rest=fixed_block(before[2].shape))
        outs.update(sum=(grads, BF))
        out_specs = {key: fixed_block(outs[key][0]) for key in outs}
        scratch.update(
            keep=pltpu.VMEM((steps, tile, width), F32),
            give=pltpu.VMEM((steps, tile, width), BF),
            take=pltpu.VMEM((steps, tile, width), BF),
            s3=sems(steps),
            r3=sems(steps),
        )
    return launch(body, ins, outs, scratch, "ffn_backward", collective_id, in_specs, out_specs, (steps,))


def gather_gradients(weights, landed, rest, rest_landed, sums, field, sizes, collective_id):
    rows, features, columns, spaces, chans = sizes
    local, width = weights.shape[1:]
    levels = spaces // 2
    piece = local // levels
    small = sums.shape[0]
    extra = small + 32
    part = -(-extra // (16 * levels)) * 16

    def body(r):
        barrier = pltpu.get_barrier_semaphore()
        me = lax.axis_index("chan")
        place = lax.axis_index("space")
        core = lax.rem(place, 2)
        level = place // 2
        sibling = place + 1 - 2 * core
        others = [lax.rem(level + step, levels) for step in range(1, levels)]
        for other in others:
            pl.semaphore_signal(barrier, inc=1, device_id={"space": 2 * other + core}, device_id_type=MESH_ID)
        pl.semaphore_signal(barrier, inc=1, device_id={"space": sibling}, device_id_type=MESH_ID)

        def send(source, target, step, send_sem, recv_sem):
            return pltpu.make_async_remote_copy(
                src_ref=source,
                dst_ref=target,
                send_sem=send_sem.at[step],
                recv_sem=recv_sem.at[step],
                device_id={"space": 2 * others[step - 1] + core},
                device_id_type=MESH_ID,
            )

        def to_sibling(source, target, step, send_sem, recv_sem):
            return pltpu.make_async_remote_copy(
                src_ref=source,
                dst_ref=target,
                send_sem=send_sem.at[step],
                recv_sem=recv_sem.at[step],
                device_id={"space": sibling},
                device_id_type=MESH_ID,
            )

        loads = [pltpu.make_async_copy(r.weights.at[me], r.terms.at[0], r.load.at[0])]
        loads += [pltpu.make_async_copy(r.rest.at[me], r.rest_terms.at[0], r.load.at[1])]
        for step in range(1, chans):
            source = lax.rem(me + step, chans)
            loads.append(pltpu.make_async_copy(r.landed.at[source], r.terms.at[step], r.load.at[2 * step]))
            loads.append(
                pltpu.make_async_copy(r.rest_landed.at[source], r.rest_terms.at[step], r.load.at[2 * step + 1])
            )
        run_copies(loads)
        for q in range(levels):
            own = slice(q * piece, (q + 1) * piece)
            r.a_send[q] = sum(r.terms[j, own, :].astype(F32) for j in range(chans)).astype(BF)
        r.table[...] = jnp.zeros_like(r.table)
        r.table[0:small, :] = r.sums[...]
        tail = sum(r.rest_terms[j] for j in range(chans))
        for k in range(local // 128):
            lanes = slice(k * 128, (k + 1) * 128)
            r.table[small + k : small + k + 1, :] = tail[0:1, lanes]
        for k in range(3):
            line = jnp.concatenate([tail[1 + k : 2 + k, :features], jnp.zeros((1, 256 - features), F32)], axis=1)
            r.table[small + 8 + 2 * k : small + 9 + 2 * k, :] = line[:, :128]
            r.table[small + 9 + 2 * k : small + 10 + 2 * k, :] = line[:, 128:]
        for q in range(levels):
            r.b_send[q] = r.table[q * part : (q + 1) * part, :].astype(BF)
        pl.semaphore_wait(barrier, levels)
        first = []
        for step in range(1, levels):
            first.append(send(r.a_send.at[others[step - 1]], r.a_land.at[level], step, r.s1, r.r1))
            first.append(send(r.b_send.at[others[step - 1]], r.b_land.at[level], step, r.s2, r.r2))
        for copy in first:
            copy.start()
        leave(r.field, r.lines, r.turn)
        a = r.a_send[level].astype(F32)
        b = r.b_send[level].astype(F32)
        for step in range(1, levels):
            first[2 * step - 2].wait()
            first[2 * step - 1].wait()
            source = lax.rem(level - step + levels, levels)
            a += r.a_land[source].astype(F32)
            b += r.b_land[source].astype(F32)
        r.a_own[...] = a.astype(BF)
        r.b_own[...] = b.astype(BF)
        last = [to_sibling(r.a_own, r.a_other.at[level], 0, r.s5, r.r5)]
        last += [to_sibling(r.b_own, r.b_other.at[level], 0, r.s6, r.r6)]
        second = []
        for step in range(1, levels):
            second.append(send(r.a_own, r.a_full.at[level], step, r.s3, r.r3))
            second.append(send(r.b_own, r.b_full.at[level], step, r.s4, r.r4))
        for copy in second + last:
            copy.start()
        r.a_full[level] = r.a_own[...]
        r.b_full[level] = r.b_own[...]
        for step in range(1, levels):
            second[2 * step - 2].wait()
            second[2 * step - 1].wait()
            source = lax.rem(level - step + levels, levels)
            more = [to_sibling(r.a_full.at[source], r.a_other.at[source], step, r.s5, r.r5)]
            more += [to_sibling(r.b_full.at[source], r.b_other.at[source], step, r.s6, r.r6)]
            for copy in more:
                copy.start()
            last += more
        for copy in last:
            copy.wait()

    return launch(
        body,
        {
            "weights": weights,
            "landed": landed,
            "rest": rest,
            "rest_landed": rest_landed,
            "sums": sums,
            "field": field,
        },
        {
            "lines": ((rows, features * columns // 128, 128), F32),
            "a_full": ((levels, piece, width), BF),
            "a_other": ((levels, piece, width), BF),
            "b_full": ((levels, part, 128), BF),
            "b_other": ((levels, part, 128), BF),
        },
        {
            "terms": pltpu.VMEM((chans, local, width), BF),
            "rest_terms": pltpu.VMEM((chans,) + rest.shape[1:], F32),
            "table": pltpu.VMEM((part * levels, 128), F32),
            "turn": pltpu.VMEM((2, features, 128), F32),
            "a_send": pltpu.VMEM((levels, piece, width), BF),
            "a_land": pltpu.VMEM((levels, piece, width), BF),
            "a_own": pltpu.VMEM((piece, width), BF),
            "b_send": pltpu.VMEM((levels, part, 128), BF),
            "b_land": pltpu.VMEM((levels, part, 128), BF),
            "b_own": pltpu.VMEM((part, 128), BF),
            "load": sems(2 * chans),
            **{key + str(k): sems(levels) for k in range(1, 7) for key in ("s", "r")},
        },
        "gather_gradients",
        collective_id,
        {key: IN_PLACE for key in ("weights", "landed", "rest", "rest_landed")},
    )


def unpack_gradients(parts, small, sizes):
    rows, features, columns, spaces, chans = sizes
    levels, piece, width = parts["a_full"].shape
    part = parts["b_full"].shape[1]
    local = levels * piece
    size = features // 2

    def body(r):
        swap = lax.rem(lax.axis_index("space"), 2) == 1
        for q in range(levels):
            own = slice(q * piece, (q + 1) * piece)
            mine, theirs = r.a_full[q].astype(F32), r.a_other[q].astype(F32)
            r.down[own, :] = jnp.where(swap, theirs, mine)
            r.up[:, own] = jnp.where(swap, mine, theirs).T
            r.table[q * part : (q + 1) * part, :] = r.b_full[q].astype(F32) + r.b_other[q].astype(F32)
        for layer, target in enumerate((r.mix_in, r.mix_out)):
            for half in range(2):
                for block in range(2):
                    start = ((layer * 2 + half) * 2 + block) * size
                    target[half, block] = r.table[start : start + size, :size]
        base = 8 * size

        def vector(k):
            return jnp.concatenate(
                [r.table[base + k : base + k + 1, :], r.table[base + 8 + k : base + 9 + k, : features - 128]], axis=1
            )

        for k, target in enumerate((r.bias_in, r.bias_in, r.bias_out, r.bias_out)):
            value = vector(k)
            target[k % 2, 0:1, :] = value[:, :size]
            target[k % 2, 1:2, :] = value[:, size:]
        r.pre_gain[...] = vector(4)
        r.pre_shift[...] = vector(5)
        for k in range(local // 128):
            r.upb[0:1, k * 128 : (k + 1) * 128] = r.table[small + k : small + k + 1, :]
        for k, target in enumerate((r.post_gain, r.post_shift, r.downb)):
            target[...] = jnp.concatenate(
                [
                    r.table[small + 8 + 2 * k : small + 9 + 2 * k, :],
                    r.table[small + 9 + 2 * k : small + 10 + 2 * k, : features - 128],
                ],
                axis=1,
            )


    return launch(
        body,
        {key: parts[key] for key in ("a_full", "a_other", "b_full", "b_other")},
        {
            "down": ((local, width), F32),
            "up": ((width, local), F32),
            "mix_in": ((2, 2, size, size), F32),
            "mix_out": ((2, 2, size, size), F32),
            "bias_in": ((2, 2, size), F32),
            "bias_out": ((2, 2, size), F32),
            "pre_gain": ((1, features), F32),
            "pre_shift": ((1, features), F32),
            "post_gain": ((1, features), F32),
            "post_shift": ((1, features), F32),
            "downb": ((1, features), F32),
            "upb": ((1, local), F32),
        },
        {"table": pltpu.VMEM((part * levels, 128), F32)},
        "unpack_gradients",
    )


def block_diagonal(weights):
    blocks = weights.shape[1]
    rows = [
        jnp.concatenate(
            [weights[:, b] if b == other else jnp.zeros_like(weights[:, b]) for other in range(blocks)], axis=2
        )
        for b in range(blocks)
    ]
    return jnp.concatenate(rows, axis=1)


def shards_fast(
    current_atmosphere,
    truth_one,
    truth_two,
    storm_codes,
    pre_gain,
    pre_shift,
    mix_weight_in,
    mix_bias_in,
    mix_weight_out,
    mix_bias_out,
    post_gain,
    post_shift,
    up_weight,
    up_bias,
    down_weight,
    down_bias,
):
    rows, merged = current_atmosphere.shape[1:]
    columns = W
    features = merged // columns
    spaces = lax.axis_size("space")
    chans = lax.axis_size("chan")
    sizes = (rows, features, columns, spaces, chans)
    height = rows * spaces
    thick = 2 * rows
    local = up_weight.shape[1]

    forward, inverse = row_constants(columns)
    column = column_constants(height, rows, 2)
    even = (np.arange(spaces * thick) // rows % 2 == 0).astype(np.float32)
    tables = {
        "row": jnp.stack(const_halves(forward)),
        "rowinv": jnp.stack(const_halves(inverse)),
        "rowinv_t": const_halves(inverse.T)[0],
        "row_t": const_halves(forward.T)[0],
        "col": jnp.stack(const_halves(column)),
        "colinv": jnp.stack(const_halves(column.T)),
        "even": jnp.asarray(np.repeat(even[:, None], features, axis=1)),
    }

    def lines(flat):
        return flat.reshape(rows, merged // 128, 128)

    def flat(line_field):
        return line_field.reshape(1, rows, merged)

    weight = jnp.broadcast_to((storm_codes.astype(F32) / 64.0).reshape(1, 1), (8, 128))
    mix = jnp.stack([block_diagonal(mix_weight_in), block_diagonal(mix_weight_out)])
    high = lax.reduce_precision(mix, 8, 7)
    mix = jnp.stack([high.astype(BF), (mix - high).astype(BF)], axis=2)
    bias = jnp.concatenate([mix_bias_in.reshape(2, features), mix_bias_out.reshape(2, features)])
    gain_row = pre_gain.reshape(1, features)
    shift_row = pre_shift.reshape(1, features)

    weights = jnp.stack([up_weight, down_weight])
    norms = jnp.concatenate(
        [post_gain, post_shift, down_bias.astype(F32), jnp.zeros((local - 3 * features,), F32)]
    )
    vectors = jnp.concatenate(
        [up_bias.astype(F32).reshape(1, local), norms.reshape(1, local), jnp.zeros((6, local), F32)]
    )

    def fields(value):
        return value.reshape(rows, columns, features)

    start = entry_norm(lines(current_atmosphere), vectors, sizes)
    gathered = start["gathered"]
    shared = (gain_row, shift_row, tables, mix, bias)
    one = spectral_forward(
        {"x": start["x"], "unit": start["unit"]}, weights, *shared, lines(truth_one), True, sizes, 1
    )
    weights = one["all_weights"]
    ffn_one = ffn_forward(one["mid"], gathered, weights, sizes, 3)
    two = spectral_forward(
        {"before": one["middle"], "home": ffn_one["home"].reshape(rows, columns, 256)},
        None,
        *shared,
        lines(truth_two),
        False,
        sizes,
        2,
    )
    ffn_two = ffn_forward(two["mid"], gathered, weights, sizes, 3)
    late = ffn_backward(
        {"home": ffn_two["home"], "middle": two["middle"], "target": two["cells_a"], "weight": weight},
        ffn_two,
        gathered,
        weights,
        None,
        sizes,
        4,
    )
    back_two = spectral_backward(
        fields(late["g"]),
        fields(late["dv"]),
        two["unit"],
        two["dev"],
        gain_row,
        tables,
        mix,
        two,
        two["x"],
        (two["x"], one["cells_a"], weight),
        None,
        None,
        sizes,
        6,
    )
    early = ffn_backward(
        {"came": back_two["upper"]},
        ffn_one,
        gathered,
        weights,
        (late["gdown"], late["gup"], late["rest"]),
        sizes,
        5,
    )
    back_one = spectral_backward(
        back_two["out"],
        fields(early["dv"]),
        start["unit"],
        start["dev"],
        gain_row,
        tables,
        mix,
        one,
        fields(late["x"]),
        None,
        back_two["sums"],
        (early["sum"], early["rest"]),
        sizes,
        7,
    )
    end = gather_gradients(
        early["sum"],
        back_one["landed"],
        early["rest"],
        back_one["rest_landed"],
        back_one["sums"],
        back_one["out"],
        sizes,
        8,
    )
    grads = unpack_gradients(end, back_one["sums"].shape[0], sizes)
    return (
        flat(back_two["lines"]),
        flat(back_one["lines"]),
        flat(end["lines"]),
        grads["pre_gain"].reshape(features),
        grads["pre_shift"].reshape(features),
        grads["mix_in"],
        grads["bias_in"],
        grads["mix_out"],
        grads["bias_out"],
        grads["post_gain"].reshape(features),
        grads["post_shift"].reshape(features),
        grads["up"],
        grads["upb"].reshape(local),
        grads["down"],
        grads["downb"].reshape(features),
    )


def suits(mesh):
    spaces, chans = mesh.shape["space"], mesh.shape["chan"]
    return (spaces, chans) == (8, 4)


def solution(mesh):
    in_specs = (
        P(None, "space", "chan"),
        P(None, "space", "chan"),
        P(None, "space", "chan"),
        P(),
        P("chan"),
        P("chan"),
        P(None, "chan", None, None),
        P(None, "chan", None),
        P(None, "chan", None, None),
        P(None, "chan", None),
        P("chan"),
        P("chan"),
        P(None, "chan"),
        P("chan"),
        P("chan", None),
        P("chan"),
    )
    out_specs = (
        P(None, "space", "chan"),
        P(None, "space", "chan"),
        P(None, "space", "chan"),
        P("chan"),
        P("chan"),
        P(None, "chan", None, None),
        P(None, "chan", None),
        P(None, "chan", None, None),
        P(None, "chan", None),
        P("chan"),
        P("chan"),
        P(None, "chan"),
        P("chan"),
        P("chan", None),
        P("chan"),
    )
    return jax.shard_map(shards_fast if suits(mesh) else shards, mesh=mesh, in_specs=in_specs, out_specs=out_specs, check_vma=False)
```

```python
import functools
import math
import types

import jax
import jax.numpy as jnp
import ml_dtypes
import numpy as np
from jax import lax
from jax.experimental import pallas as pl
from jax.experimental.pallas import tpu as pltpu
from jax.sharding import PartitionSpec as P

W = 160
KW = 81


NORM_EPS = 1e-06
SHRINK_LEVEL = 0.01
FULL_PRECISION = lax.Precision.HIGHEST


def exact_gelu(values):
    return jax.nn.gelu(values, approximate=False)


def shrink(values):
    return values - jnp.clip(values, -SHRINK_LEVEL, SHRINK_LEVEL)


def block_mix(values, matrix):
    return jnp.einsum("bhkni,nio->bhkno", values, matrix, precision=FULL_PRECISION)


def row_tables(columns, kept_modes, padded_modes):
    places = jnp.arange(columns, dtype=jnp.int32)[:, None]
    orders = jnp.arange(padded_modes, dtype=jnp.int32)[None, :]
    angles = 2.0 * math.pi / columns * (places * orders % columns).astype(jnp.float32)
    factor = 1.0 / math.sqrt(columns)
    single = jnp.logical_or(orders == 0, 2 * orders == columns)
    doubled = jnp.where(single, 1.0, 2.0).astype(jnp.float32)
    used = jnp.where(orders < kept_modes, 1.0, 0.0).astype(jnp.float32)
    return (
        jnp.cos(angles) * factor * used,
        -jnp.sin(angles) * factor * used,
        jnp.transpose(jnp.cos(angles) * doubled * factor * used),
        jnp.transpose(jnp.sin(angles) * doubled * factor * used),
    )


def along_rows(values, tables):
    return jnp.stack(
        [
            jnp.einsum("bhwc,wk->bhkc", values, tables[0], precision=FULL_PRECISION),
            jnp.einsum("bhwc,wk->bhkc", values, tables[1], precision=FULL_PRECISION),
        ]
    )


def along_rows_back(paired, tables):
    return jnp.einsum("bhkc,wk->bhwc", paired[0], tables[0], precision=FULL_PRECISION) + jnp.einsum(
        "bhkc,wk->bhwc", paired[1], tables[1], precision=FULL_PRECISION
    )


def rows_inverse(paired, tables):
    return jnp.einsum("bhkc,kw->bhwc", paired[0], tables[2], precision=FULL_PRECISION) - jnp.einsum(
        "bhkc,kw->bhwc", paired[1], tables[3], precision=FULL_PRECISION
    )


def rows_inverse_back(values, tables):
    return jnp.stack(
        [
            jnp.einsum("bhwc,kw->bhkc", values, tables[2], precision=FULL_PRECISION),
            -jnp.einsum("bhwc,kw->bhkc", values, tables[3], precision=FULL_PRECISION),
        ]
    )


def column_tables(height):
    orders = jnp.arange(height, dtype=jnp.int32)[:, None]
    places = jnp.arange(height, dtype=jnp.int32)[None, :]
    angles = 2.0 * math.pi / height * (orders * places % height).astype(jnp.float32)
    factor = 1.0 / math.sqrt(height)
    return (jnp.cos(angles) * factor, jnp.sin(angles) * factor)


def to_freq(matrix, values):
    return jnp.einsum("kh,bhmc->bkmc", matrix, values, precision=FULL_PRECISION)


def from_freq(matrix, values):
    return jnp.einsum("kh,bkmc->bhmc", matrix, values, precision=FULL_PRECISION)


def spectral_core(paired, w_first, b_first, w_second, b_second):
    samples, height, kept_modes, channels = paired.shape[1:]
    blocks, block_size = (w_first.shape[1], w_first.shape[2])
    cosine, sine_table = column_tables(height)
    real_in, imag_in = (paired[0], paired[1])
    split_form = (samples, height, kept_modes, blocks, block_size)
    real_part = (to_freq(cosine, real_in) + to_freq(sine_table, imag_in)).reshape(split_form)
    imag_part = (to_freq(cosine, imag_in) - to_freq(sine_table, real_in)).reshape(split_form)
    first_real = jax.nn.relu(
        block_mix(real_part, w_first[0]) - block_mix(imag_part, w_first[1]) + b_first[0]
    )
    first_imag = jax.nn.relu(
        block_mix(imag_part, w_first[0]) + block_mix(real_part, w_first[1]) + b_first[1]
    )
    joined_form = (samples, height, kept_modes, channels)
    second_real = shrink(
        block_mix(first_real, w_second[0]) - block_mix(first_imag, w_second[1]) + b_second[0]
    ).reshape(joined_form)
    second_imag = shrink(
        block_mix(first_imag, w_second[0]) + block_mix(first_real, w_second[1]) + b_second[1]
    ).reshape(joined_form)
    out_real = from_freq(cosine, second_real) - from_freq(sine_table, second_imag)
    out_imag = from_freq(cosine, second_imag) + from_freq(sine_table, second_real)
    return jnp.stack([out_real, out_imag])


def column_layout(paired):
    return lax.all_to_all(paired, "space", split_axis=3, concat_axis=2, tiled=True)


def row_layout(paired):
    return lax.all_to_all(
        paired.astype(jnp.bfloat16), "space", split_axis=2, concat_axis=3, tiled=True
    ).astype(paired.dtype)


def norm_forward(values, gain, offset):
    width_all = values.shape[-1] * lax.axis_size("chan")
    totals = lax.psum((jnp.sum(values, axis=-1), jnp.sum(values * values, axis=-1)), "chan")
    average = totals[0] / width_all
    variance = totals[1] / width_all - average * average
    inverse_dev = lax.rsqrt(variance + NORM_EPS)[..., None]
    scaled = (values - average[..., None]) * inverse_dev
    return (scaled * gain + offset, (scaled, inverse_dev))


def norm_backward(gradient, gain, saved):
    scaled, inverse_dev = saved
    width_all = scaled.shape[-1] * lax.axis_size("chan")
    scaled_grad = gradient * gain
    totals = lax.psum(
        (jnp.sum(scaled_grad, axis=-1), jnp.sum(scaled_grad * scaled, axis=-1)), "chan"
    )
    values_grad = inverse_dev * (
        scaled_grad - totals[0][..., None] / width_all - scaled * (totals[1][..., None] / width_all)
    )
    return (
        values_grad,
        jnp.sum(gradient * scaled, axis=(0, 1, 2)),
        jnp.sum(gradient, axis=(0, 1, 2)),
    )


def shards(
    current_atmosphere,
    truth_one,
    truth_two,
    storm_codes,
    pre_gain,
    pre_shift,
    mix_weight_in,
    mix_bias_in,
    mix_weight_out,
    mix_bias_out,
    post_gain,
    post_shift,
    up_weight,
    up_bias,
    down_weight,
    down_bias,
):
    samples, rows_here, merged = current_atmosphere.shape
    columns = W
    channels = merged // columns
    total_rows = samples * rows_here * columns
    space_count = lax.axis_size("space")
    padded_modes = (KW + space_count - 1) // space_count * space_count
    tables = row_tables(columns, KW, padded_modes)

    def to_cells(flat_field):
        return jnp.transpose(
            flat_field.reshape(samples, rows_here, channels, columns), (0, 1, 3, 2)
        )

    def to_flat(cell_field):
        return jnp.transpose(cell_field, (0, 1, 3, 2)).reshape(samples, rows_here, merged)

    start_cells = to_cells(current_atmosphere)
    target_one = to_cells(truth_one)
    target_two = to_cells(truth_two)
    weight_of = (storm_codes.astype(jnp.float32) / 64.0).reshape(-1, 1, 1, 1)
    full_up, full_down, full_up_bias, full_down_bias = (up_weight, down_weight, up_bias, down_bias)

    def mlp_forward(inputs):
        gathered = lax.all_gather(inputs, "chan", axis=1, tiled=True)
        hidden = jnp.dot(
            gathered, full_up, preferred_element_type=jnp.float32
        ) + full_up_bias.astype(jnp.float32)
        active_full, gelu_pull = jax.vjp(exact_gelu, hidden)
        active = active_full.astype(jnp.bfloat16)
        product = jnp.dot(active, full_down, preferred_element_type=jnp.float32)
        output = lax.psum_scatter(
            product.astype(jnp.bfloat16), "chan", scatter_dimension=1, tiled=True
        ).astype(jnp.float32) + full_down_bias.astype(jnp.float32)
        return (output, (gathered, gelu_pull, active))

    def mlp_backward(gradient, saved):
        gathered, gelu_pull, active = saved
        grad_low = gradient.astype(jnp.bfloat16)
        grad_rows = lax.all_gather(grad_low, "chan", axis=1, tiled=True)
        down_bias_grad = jnp.sum(grad_low.astype(jnp.float32), axis=0)
        down_grad = jnp.dot(active.T, grad_rows, preferred_element_type=jnp.float32)
        active_grad = jnp.dot(grad_rows, full_down.T, preferred_element_type=jnp.float32)
        hidden_grad = gelu_pull(active_grad)[0].astype(jnp.bfloat16)
        up_grad = jnp.dot(gathered.T, hidden_grad, preferred_element_type=jnp.float32)
        up_bias_grad = jnp.sum(hidden_grad.astype(jnp.float32), axis=0)
        input_part = jnp.dot(hidden_grad, full_up.T, preferred_element_type=jnp.float32)
        input_grad = lax.psum_scatter(
            input_part.astype(jnp.bfloat16), "chan", scatter_dimension=1, tiled=True
        ).astype(jnp.float32)
        return (input_grad, (up_grad, up_bias_grad, down_grad, down_bias_grad))

    def forward_block(values):
        normed, first_saved = norm_forward(values, pre_gain, pre_shift)
        modal_in = column_layout(along_rows(normed, tables))
        filtered, core_pull = jax.vjp(
            spectral_core, modal_in, mix_weight_in, mix_bias_in, mix_weight_out, mix_bias_out
        )
        middle = rows_inverse(row_layout(filtered), tables) + normed + values
        entry, second_residuals = norm_forward(middle, post_gain, post_shift)
        output, mlp_saved = mlp_forward(entry.astype(jnp.bfloat16).reshape(total_rows, channels))
        return (
            output.reshape(values.shape) + middle,
            (first_saved, core_pull, second_residuals, mlp_saved),
        )

    def backward_block(gradient, saved):
        first_saved, core_pull, second_residuals, mlp_saved = saved
        mlp_grad, dense_grads = mlp_backward(gradient.reshape(total_rows, channels), mlp_saved)
        middle_part, post_gain_grad, post_shift_grad = norm_backward(
            mlp_grad.reshape(gradient.shape), post_gain, second_residuals
        )
        middle_grad = middle_part + gradient
        filter_grads = core_pull(column_layout(rows_inverse_back(middle_grad, tables)))
        normed_grad = along_rows_back(row_layout(filter_grads[0]), tables) + middle_grad
        input_part, pre_gain_grad, pre_shift_grad = norm_backward(
            normed_grad, pre_gain, first_saved
        )
        return (
            input_part + middle_grad,
            (pre_gain_grad, pre_shift_grad)
            + tuple(filter_grads[1:])
            + (post_gain_grad, post_shift_grad)
            + dense_grads,
        )

    first_out, first_saved_all = forward_block(start_cells)
    second_out, second_saved_all = forward_block(first_out)
    carried, grads_late = backward_block(weight_of * (second_out - target_two), second_saved_all)
    input_grad, grads_early = backward_block(
        weight_of * (first_out - target_one) + carried, first_saved_all
    )
    summed = jax.tree.map(jnp.add, grads_early, grads_late)
    (
        sum_pre_gain,
        sum_pre_shift,
        sum_mix_w_in,
        summed_mixing_bias_input,
        sum_mix_w_out,
        sum_mix_b_out,
        sum_post_gain,
        sum_post_shift,
        sum_up,
        sum_up_bias,
        sum_down,
        sum_down_bias,
    ) = summed
    totals = (
        lax.psum(sum_pre_gain.astype(jnp.bfloat16), "space").astype(jnp.float32),
        lax.psum(sum_pre_shift.astype(jnp.bfloat16), "space").astype(jnp.float32),
        lax.psum(sum_mix_w_in.astype(jnp.bfloat16), "space").astype(jnp.float32),
        lax.psum(summed_mixing_bias_input.astype(jnp.bfloat16), "space").astype(jnp.float32),
        lax.psum(sum_mix_w_out.astype(jnp.bfloat16), "space").astype(jnp.float32),
        lax.psum(sum_mix_b_out.astype(jnp.bfloat16), "space").astype(jnp.float32),
        lax.psum(sum_post_gain.astype(jnp.bfloat16), "space").astype(jnp.float32),
        lax.psum(sum_post_shift.astype(jnp.bfloat16), "space").astype(jnp.float32),
        lax.psum(sum_up.astype(jnp.bfloat16), "space").astype(jnp.float32),
        lax.psum(sum_up_bias.astype(jnp.bfloat16), "space").astype(jnp.float32),
        lax.psum(sum_down.astype(jnp.bfloat16), "space").astype(jnp.float32),
        lax.psum(sum_down_bias.astype(jnp.bfloat16), "space").astype(jnp.float32),
    )
    return (to_flat(first_out), to_flat(second_out), to_flat(input_grad)) + tuple(totals)


BF = jnp.bfloat16
F32 = jnp.float32
MESH_ID = pl.DeviceIdType.MESH
VMEM_BYTES = 66 * 1024 * 1024 - 1024 * 1024


def mm(a, b):
    return jnp.dot(a, b, preferred_element_type=F32)


def mm_nt(a, b):
    return lax.dot_general(a, b, (((1,), (1,)), ((), ())), preferred_element_type=F32)


def mm_tn(a, b):
    return lax.dot_general(a, b, (((0,), (0,)), ((), ())), preferred_element_type=F32)


def halves(v):
    high = v.astype(BF)
    return high, (v - high.astype(F32)).astype(BF)


def mm3(a, b):
    return mm(a[0], b[0]) + (mm(a[0], b[1]) + mm(a[1], b[0]))


def const_halves(table):
    table = np.asarray(table, np.float32)
    high = table.astype(ml_dtypes.bfloat16)
    low = (table - high.astype(np.float32)).astype(ml_dtypes.bfloat16)
    return jnp.asarray(high), jnp.asarray(low)


def row_constants(columns):
    half = columns // 2
    place = np.arange(columns)
    mode = np.arange(half)
    angle = 2.0 * np.pi * np.outer(mode, place) / columns
    real = np.cos(angle)
    imag = -np.sin(angle)
    imag[0] = np.cos(np.pi * place)
    forward = np.concatenate([real, imag]) / np.sqrt(columns)
    weight = np.where(mode == 0, 1.0, 2.0)
    inverse = (forward * np.concatenate([weight, weight])[:, None]).T
    return forward, inverse


def column_constants(height, rows, group):
    owners = height // rows
    angle = 2.0 * np.pi * np.outer(np.arange(height), np.arange(height)) / height
    cosine = np.cos(angle) / np.sqrt(height)
    sine = np.sin(angle) / np.sqrt(height)

    def spread(matrix):
        wide = np.zeros((group, height, owners, group, rows))
        for column in range(group):
            wide[column, :, :, column, :] = matrix.reshape(height, owners, rows)
        return wide.reshape(group * height, owners * group * rows)

    cosine, sine = spread(cosine), spread(sine)
    return np.block([[cosine, sine], [-sine, cosine]])


def signal_peers(axis, count, barrier):
    me = lax.axis_index(axis)
    for step in range(1, count):
        pl.semaphore_signal(
            barrier, inc=1, device_id={axis: lax.rem(me + step, count)}, device_id_type=MESH_ID
        )


def push(axis, count, step, source, target, send_sem, recv_sem):
    peer = lax.rem(lax.axis_index(axis) + step, count)
    return pltpu.make_async_remote_copy(
        src_ref=source,
        dst_ref=target,
        send_sem=send_sem.at[step],
        recv_sem=recv_sem.at[step],
        device_id={axis: peer},
        device_id_type=MESH_ID,
    )


def params(collective_id=None):
    return pltpu.CompilerParams(
        collective_id=collective_id,
        has_side_effects=collective_id is not None,
        vmem_limit_bytes=VMEM_BYTES,
    )


def launch(body, ins, outs, scratch, name, collective_id=None, in_specs=None, out_specs=None, grid=()):
    in_specs, out_specs = in_specs or {}, out_specs or {}
    names = list(ins) + list(outs) + list(scratch)
    whole = pl.BlockSpec(memory_space=pltpu.VMEM)
    results = pl.pallas_call(
        lambda *refs: body(types.SimpleNamespace(**dict(zip(names, refs)))),
        grid=grid,
        in_specs=[in_specs.get(key, whole) for key in ins],
        out_specs=[out_specs.get(key, whole) for key in outs],
        out_shape=[jax.ShapeDtypeStruct(*outs[key]) for key in outs],
        scratch_shapes=list(scratch.values()),
        compiler_params=params(collective_id),
        name=name,
    )(*ins.values())
    return dict(zip(outs, results))


IN_PLACE = pl.BlockSpec(memory_space=pl.ANY)


def sems(*counts):
    return pltpu.SemaphoreType.DMA(counts)


def run_copies(copies):
    for copy in copies:
        copy.start()
    for copy in copies:
        copy.wait()


def cells_from_lines(lines_ref, h, scratch_ref):
    features = scratch_ref.shape[1]
    per = 640 // W
    groups = features // per
    wide = jnp.concatenate(
        [lines_ref[h, pl.ds(part, groups, stride=5), :] for part in range(5)], axis=1
    )
    for part in range(per):
        piece = wide[:, part * W : (part + 1) * W]
        scratch_ref[0, pl.ds(part, groups, stride=per), :] = piece[:, :128]
        scratch_ref[1, pl.ds(part, groups, stride=per), :] = jnp.concatenate(
            [piece[:, 128:], jnp.zeros((groups, 256 - W), F32)], axis=1
        )
    return jnp.concatenate([scratch_ref[0], scratch_ref[1][:, : W - 128]], axis=1)


def enter(lines_ref, cells_ref, scratch_ref):
    def row(h, carry):
        cells_ref[h] = cells_from_lines(lines_ref, h, scratch_ref).T
        return carry

    lax.fori_loop(0, lines_ref.shape[0], row, 0)


def leave(cells_ref, lines_ref, scratch_ref):
    features = scratch_ref.shape[1]
    per = 640 // W
    groups = features // per

    def row(h, carry):
        block = cells_ref[h].T
        scratch_ref[0] = block[:, :128]
        scratch_ref[1] = jnp.concatenate([block[:, 128:], jnp.zeros((features, 256 - W), F32)], axis=1)
        wide = jnp.concatenate(
            [
                piece
                for part in range(per)
                for piece in (
                    scratch_ref[0, pl.ds(part, groups, stride=per), :],
                    scratch_ref[1, pl.ds(part, groups, stride=per), :][:, : W - 128],
                )
            ],
            axis=1,
        )
        for part in range(5):
            lines_ref[h, pl.ds(part, groups, stride=5), :] = wide[:, part * 128 : (part + 1) * 128]
        return carry

    lax.fori_loop(0, lines_ref.shape[0], row, 0)


def pack_lanes(flat_ref, place, real, imag):
    flat_ref[0, place, :] = real[:, :128]
    flat_ref[1, place, :] = imag[:, :128]
    flat_ref[2, place, :] = jnp.concatenate([real[:, 128:], imag[:, 128:]], axis=1)


def join_lanes(first, second, rest):
    real = jnp.concatenate([first, rest[:, :64]], axis=1)
    imag = jnp.concatenate([second, rest[:, 64:]], axis=1)
    return real, imag


def unpack_lanes(flat_ref, place):
    return join_lanes(flat_ref[0, place, :], flat_ref[1, place, :], flat_ref[2, place, :])


LEVEL = 32000.0


def encode_fixed(values):
    largest = jnp.max(jnp.abs(values), axis=1, keepdims=True)
    grade = jnp.ceil(jnp.log2(jnp.maximum(largest, 1e-30)) * 256.0 + 0.01)
    coded = jnp.round(values * (LEVEL * jnp.exp2(grade * (-1.0 / 256.0))))
    lines = [coded[k] for k in range(3)] + [grade[k] for k in range(3)] + [jnp.zeros((5, 128), F32)]
    return jnp.concatenate(lines, axis=0).astype(jnp.int32).astype(jnp.int16)


def decode_fixed(coded, thick):
    values = coded.astype(jnp.int32).astype(F32)
    scale = jnp.exp2(values[3 * thick : 3 * thick + 3] * (1.0 / 256.0)) * (1.0 / LEVEL)
    return [values[k * thick : (k + 1) * thick] * scale[k : k + 1] for k in range(3)]


def encode_plain(values):
    return jnp.concatenate([values[k] for k in range(3)], axis=0).astype(BF)


def decode_plain(coded, thick):
    values = coded.astype(F32)
    return [values[k * thick : (k + 1) * thick] for k in range(3)]


class Exchange:
    def __init__(self, fixed, spaces, thick, send_ref, recv_ref, send_sem, recv_sem):
        self.encode, self.decode = (encode_fixed, decode_fixed) if fixed else (encode_plain, decode_plain)
        self.spaces, self.thick = spaces, thick
        self.send_ref, self.recv_ref = send_ref, recv_ref
        self.send_sem, self.recv_sem = send_sem, recv_sem
        self.me = lax.axis_index("space")

    @staticmethod
    def shape(fixed, spaces, thick, pairs):
        return pltpu.VMEM((pairs, spaces, 3 * thick + (8 if fixed else 0), 128), jnp.int16 if fixed else BF)

    def copy(self, p, step):
        peer = lax.rem(self.me + step, self.spaces)
        return pltpu.make_async_remote_copy(
            src_ref=self.send_ref.at[p, peer],
            dst_ref=self.recv_ref.at[p, self.me],
            send_sem=self.send_sem.at[p, step],
            recv_sem=self.recv_sem.at[p, step],
            device_id={"space": peer},
            device_id_type=MESH_ID,
        )

    def send(self, p, flat_ref, start_of):
        for step in list(range(1, self.spaces)) + [0]:
            peer = lax.rem(self.me + step, self.spaces)
            rows = pl.ds(pl.multiple_of(start_of(peer), 8), self.thick)
            coded = self.encode(flat_ref[:, rows, :])
            if step:
                self.send_ref[p, peer] = coded
                self.copy(p, step).start()
            else:
                self.recv_ref[p, peer] = coded

    def arrive(self, p):
        for step in range(1, self.spaces):
            self.copy(p, step).wait_recv()

    def take(self, p, source):
        return self.decode(self.recv_ref[p, source], self.thick)

    def close(self, pairs):
        def pair(p, carry):
            for step in range(1, self.spaces):
                self.copy(p, step).wait_send()
            return carry

        lax.fori_loop(0, pairs, pair, 0)


def pair_inputs(q, exchange, even_ref):
    p = jnp.maximum(q - 1, 0)

    @pl.when(q != 1)
    def _():
        exchange.arrive(p)

    extra = (q == 0).astype(F32)
    zeroth = jnp.logical_and(exchange.me == 0, p == 0).astype(F32)
    parts = [join_lanes(*exchange.take(p, s)) for s in range(exchange.spaces)]
    real = jnp.concatenate([part[0] for part in parts], axis=0)
    imag = jnp.concatenate([part[1] for part in parts], axis=0)
    chosen = imag * (even_ref[...] * zeroth)
    real = real * (1.0 - extra) + chosen * extra
    imag = (imag - chosen) * (1.0 - extra)
    return p, zeroth, jnp.concatenate([real, imag], axis=0)


def pair_outputs(q, p, zeroth, result, exchange, even_ref, kept_ref, stage_ref):
    half = result.shape[0] // 2
    real, imag = result[:half], result[half:]

    @pl.when(q == 0)
    def _():
        kept_ref[...] = real

    @pl.when(q > 0)
    def _():
        chosen = even_ref[...] * zeroth
        pack_lanes(stage_ref, slice(None), real, imag * (1.0 - chosen) + kept_ref[...] * chosen)
        exchange.send(p, stage_ref, lambda peer: peer * exchange.thick)


def collect(exchange, pairs, chunk, flat_ref):
    def pair(p, carry):
        exchange.arrive(p)
        for s in range(exchange.spaces):
            rows = pl.ds(pl.multiple_of(s * chunk + p * exchange.thick, 8), exchange.thick)
            for k, part in enumerate(exchange.take(p, s)):
                flat_ref[k, rows, :] = part
        return carry

    lax.fori_loop(0, pairs, pair, 0)


def send_modes(exchange, pairs, chunk, flat_ref):
    def pair(p, carry):
        exchange.send(p, flat_ref, lambda peer: peer * chunk + p * exchange.thick)
        return carry

    lax.fori_loop(0, pairs, pair, 0)


class Plan:
    def __init__(self, rows, features, columns, spaces, chans, local):
        self.rows, self.features, self.columns = rows, features, columns
        self.spaces, self.chans, self.local = spaces, chans, local
        self.modes = columns // 2
        self.total = self.modes * rows
        self.chunk = self.total // spaces
        self.thick = 2 * rows
        self.half = self.thick * spaces
        self.pairs = self.chunk // self.thick
        self.cells = rows * columns // chans
        self.share = rows // chans
        self.width = features * chans
        self.tile = 256
        self.per = local // self.tile
        self.steps = chans * self.per
        self.size = features // 2
        self.small = 8 * self.size + 16
        self.field = ((rows, columns, features), F32)
        self.by_cells = ((chans, self.cells, features), BF)
        self.wide = ((self.cells, self.width), BF)
        self.tiles = ((self.steps, self.cells, self.tile), BF)
        self.lines = ((rows, features * columns // 128, 128), F32)
        self.dev = ((rows, columns, 8), F32)
        self.dev_wide = ((self.cells, 128), F32)
        self.kept = ((self.pairs + 1, 2 * self.half, features), BF)
        self.mix = ((2, 2, 2, features, features), BF)
        self.weights = ((2, chans, local, self.width), BF)
        self.rest = ((chans, 8, local), F32)
        self.sums = ((self.small, 128), F32)
        self.grads = ((2, self.steps, self.tile, self.width), BF)
        self.vectors = ((chans, 8, local), F32)

    def exchange_scratch(self, fixed_there, fixed_back):
        made = {}
        for name, fixed in (("1", fixed_there), ("2", fixed_back)):
            shape = Exchange.shape(fixed, self.spaces, self.thick, self.pairs)
            made["send" + name] = made["recv" + name] = shape
            made["s" + name] = made["r" + name] = sems(self.pairs, self.spaces)
        return made

    def spectral_scratch(self):
        return {
            "flat": pltpu.VMEM((3, self.total, 128), F32),
            "stage": pltpu.VMEM((3, self.half, 128), F32),
            "last": pltpu.VMEM((self.half, self.features), F32),
            "turn": pltpu.VMEM((2, self.features, 128), F32),
        }


def scratch_of(shaped):
    return pltpu.VMEM(*shaped)


def greet(plan):
    barrier = pltpu.get_barrier_semaphore()
    signal_peers("space", plan.spaces, barrier)
    signal_peers("chan", plan.chans, barrier)
    return lambda: pl.semaphore_wait(barrier, plan.spaces + plan.chans - 2)


def spread_chan(plan, source_ref, target_ref, send_sem, recv_sem):
    me = lax.axis_index("chan")
    copies = []
    for step in range(1, plan.chans):
        peer = lax.rem(me + step, plan.chans)
        copy = push("chan", plan.chans, step, source_ref.at[peer], target_ref.at[me], send_sem, recv_sem)
        copy.start()
        copies.append(copy)
    target_ref[me] = source_ref[me]
    return copies


def wait_all(copies):
    for copy in copies:
        copy.wait()


def rows_to_modes(plan, table, flat_ref, value_of, exact):
    def row(h, carry):
        value = value_of(h)
        out = mm3(table, halves(value)) if exact else mm(table, value.astype(BF))
        pack_lanes(flat_ref, pl.ds(h, plan.modes, stride=plan.rows), out[: plan.modes], out[plan.modes :])
        return carry

    lax.fori_loop(0, plan.rows, row, 0)


def filter_forward(plan, r, there, back, fine):
    half = plan.half

    def filter_pair(q, carry):
        p, zeroth, block = pair_inputs(q, there, r.even)
        spec = mm3((r.col[0], r.col[1]), halves(block))
        r.spec[q] = spec.astype(BF)
        parts = halves(spec)
        straight = mm3(parts, (r.mix[0, 0, 0], r.mix[0, 0, 1]))
        crossed = mm3(parts, (r.mix[0, 1, 0], r.mix[0, 1, 1]))
        first = jnp.concatenate(
            [
                jnp.maximum(straight[:half] - crossed[half:] + r.bias[0:1], 0.0),
                jnp.maximum(straight[half:] + crossed[:half] + r.bias[1:2], 0.0),
            ],
            axis=0,
        )
        r.first[q] = first.astype(BF)
        parts = halves(first)
        straight = mm3(parts, (r.mix[1, 0, 0], r.mix[1, 0, 1]))
        crossed = mm3(parts, (r.mix[1, 1, 0], r.mix[1, 1, 1]))
        second = jnp.concatenate(
            [
                straight[:half] - crossed[half:] + r.bias[2:3],
                straight[half:] + crossed[:half] + r.bias[3:4],
            ],
            axis=0,
        )
        second = second - jnp.clip(second, -SHRINK_LEVEL, SHRINK_LEVEL)
        r.second[q] = second.astype(BF)
        if fine:
            result = mm3((r.colinv[0], r.colinv[1]), halves(second))
        else:
            result = mm(r.colinv[0], second.astype(BF))
        pair_outputs(q, p, zeroth, result, back, r.even, r.last, r.stage)
        return carry

    lax.fori_loop(0, plan.pairs + 1, filter_pair, 0)


def modes_to_rows(plan, flat_ref, h):
    real, imag = unpack_lanes(flat_ref, pl.ds(h, plan.modes, stride=plan.rows))
    return jnp.concatenate([real, imag], axis=0)


def rows_of_chunks(plan, row, send_chunk):
    me = lax.axis_index("chan")
    for step in list(range(1, plan.chans)) + [0]:
        peer = lax.rem(me + step, plan.chans)

        def one(i, carry):
            row(peer * plan.share + i, peer, pl.ds(pl.multiple_of(i * plan.columns, 16), plan.columns))
            return carry

        lax.fori_loop(0, plan.share, one, 0)
        send_chunk(step, peer)


def rows_forward(plan, r, fine, unit_ref, x_ref, middle_ref):
    me = lax.axis_index("chan")
    gain, shift = r.gain[...].reshape(1, -1), r.shift[...].reshape(1, -1)
    copies = []

    def row(h, peer, place):
        block = modes_to_rows(plan, r.flat, h)
        if fine:
            out = mm3((r.rowinv[0], r.rowinv[1]), halves(block))
        else:
            out = mm(r.rowinv[0], block.astype(BF))
        middle = out + (unit_ref[h] * gain + shift) + x_ref[h]
        middle_ref[h] = middle
        r.own[peer, place, :] = middle.astype(BF)

    def send_chunk(step, peer):
        if step:
            copy = push("chan", plan.chans, step, r.own.at[peer], r.mid.at[me], r.s3, r.r3)
            copy.start()
            copies.append(copy)
        else:
            r.mid[me] = r.own[me]

    rows_of_chunks(plan, row, send_chunk)
    return copies


BLOCK = 80


def by_blocks(plan, step):
    def one(i, carry):
        step(pl.ds(pl.multiple_of(i * BLOCK, 16), BLOCK))
        return carry

    lax.fori_loop(0, plan.cells // BLOCK, one, 0)


def joined(chunks_ref, place):
    return jnp.concatenate([chunks_ref[j, place, :].astype(F32) for j in range(chunks_ref.shape[0])], axis=1)


def full_vector(gathered_ref, start, size):
    chans = gathered_ref.shape[0]
    return jnp.concatenate([gathered_ref[j, 1:2, start : start + size] for j in range(chans)], axis=1)


def moments(value):
    mean = jnp.mean(value, axis=1, keepdims=True)
    centred = value - mean
    return mean, centred, lax.rsqrt(jnp.mean(centred * centred, axis=1, keepdims=True) + NORM_EPS)


ERF = (0.254829592, -0.284496736, 1.421413741, -1.453152027, 1.061405429)


def gelu_and_slope(v):
    e = jnp.exp2(v * v * (-0.5 / math.log(2.0)))
    below = 1.0 + (0.3275911 * math.sqrt(0.5)) * jnp.abs(v)
    t = pl.reciprocal(below, approx=True)
    t = t * (2.0 - below * t)
    c = [0.5 * k for k in ERF]
    tail = (e * t) * (c[0] + t * (c[1] + t * (c[2] + t * (c[3] + t * c[4]))))
    below = jnp.where(v >= 0.0, 1.0 - tail, tail)
    active = v * below
    return active, below + (v * (1.0 / math.sqrt(2.0 * math.pi))) * e


def three_parts(v):
    a = v.astype(BF)
    rest = v - a.astype(F32)
    b = rest.astype(BF)
    return [a, b, (rest - b.astype(F32)).astype(BF)]


def tile_of(plan, t):
    return t // plan.per, pl.ds(pl.multiple_of((t % plan.per) * plan.tile, plan.tile), plan.tile)


def up_tile(plan, r, t):
    j, place = tile_of(plan, t)
    return r.w[0, j, :, place]


def down_tile(plan, r, t):
    j, place = tile_of(plan, t)
    return r.w[1, j, place, :]


def ffn_scratch(plan):
    shape = (plan.cells, plan.tile)
    made = {key: pltpu.VMEM(shape, F32) for key in ("wide_a", "wide_b")}
    made.update({key: pltpu.VMEM(shape, BF) for key in ("thin_a", "thin_b")})
    made.update(
        total=pltpu.VMEM((plan.cells, plan.width), F32),
        entry=scratch_of(plan.wide),
        unit_wide=scratch_of(plan.wide),
        dev_wide=scratch_of(plan.dev_wide),
        active=scratch_of(plan.tiles),
        slope=scratch_of(plan.tiles),
        gathered=scratch_of(plan.vectors),
    )
    return made


def staggered(plan, r, lead, turn, trail):
    last = plan.steps - 1
    r.thin_b[...] = jnp.zeros_like(r.thin_b)
    r.wide_a[...] = lead(0)

    def pair(u, carry):
        t = 2 * u
        r.wide_b[...] = lead(t + 1)
        trail(r.thin_b[...], jnp.maximum(t - 1, 0))
        r.thin_a[...] = turn(r.wide_a[...], t)
        r.wide_a[...] = lead(jnp.minimum(t + 2, last))
        trail(r.thin_a[...], t)
        r.thin_b[...] = turn(r.wide_b[...], t + 1)
        return carry

    lax.fori_loop(0, plan.steps // 2, pair, 0)
    trail(r.thin_b[...], last)


def ffn_forward(plan, r):
    gain = full_vector(r.gathered, 0, plan.features)
    shift = full_vector(r.gathered, plan.features, plan.features)
    bias = full_vector(r.gathered, 2 * plan.features, plan.features)

    def prepare(place):
        mean, centred, inverse = moments(joined(r.mid, place))
        unit = centred * inverse
        r.unit_wide[place, :] = unit.astype(BF)
        r.dev_wide[place, :] = jnp.broadcast_to(inverse, (BLOCK, 128))
        r.entry[place, :] = (unit * gain + shift).astype(BF)
        r.total[place, :] = jnp.broadcast_to(bias, (BLOCK, plan.width))

    by_blocks(plan, prepare)

    def lead(t):
        j, place = tile_of(plan, t)
        return mm(r.entry[...], up_tile(plan, r, t)) + r.gathered[j, 0:1, place]

    def turn(value, t):
        active, slope = gelu_and_slope(value)
        active = active.astype(BF)
        r.active[t] = active
        r.slope[t] = slope.astype(BF)
        return active

    def trail(active, t):
        r.total[...] += mm(active, down_tile(plan, r, t))

    staggered(plan, r, lead, turn, trail)


def ffn_backward(plan, r):
    r.small[...] = jnp.zeros_like(r.small)
    r.total[...] = jnp.zeros_like(r.total)

    def lead(t):
        return mm_nt(r.upper[...], down_tile(plan, r, t))

    def turn(value, t):
        lower = value * r.slope[t].astype(F32)
        r.upb[pl.ds(t, 1), :] = jnp.sum(lower, axis=0, keepdims=True)
        lower = lower.astype(BF)
        r.slope[t] = lower
        return lower

    def trail(lower, t):
        r.total[...] += mm_nt(lower, up_tile(plan, r, t))

    staggered(plan, r, lead, turn, trail)
    gain = full_vector(r.gathered, 0, plan.features)

    def finish(place):
        grad = r.total[place, :]
        unit = r.unit_wide[place, :].astype(F32)
        r.small[0:1, :] += jnp.sum(grad * unit, axis=0, keepdims=True)
        r.small[1:2, :] += jnp.sum(grad, axis=0, keepdims=True)
        r.small[2:3, :] += jnp.sum(r.upper[place, :].astype(F32), axis=0, keepdims=True)
        scaled = grad * gain
        one = jnp.mean(scaled, axis=1, keepdims=True)
        two = jnp.mean(scaled * unit, axis=1, keepdims=True)
        result = r.dev_wide[place, :][:, :1] * (scaled - one - unit * two)
        for j in range(plan.chans):
            r.leaving[j, place, :] = result[:, j * plan.features : (j + 1) * plan.features].astype(BF)

    by_blocks(plan, finish)


def vector_gradients(plan, r, rest_ref):
    rest_ref[...] = jnp.zeros_like(rest_ref)
    for j in range(plan.chans):
        for k in range(plan.per):
            line = j * plan.per + k
            rest_ref[j, 0:1, k * plan.tile : (k + 1) * plan.tile] = r.upb[line : line + 1, :]
        for k in range(3):
            rest_ref[j, 1 + k : 2 + k, 0 : plan.features] = r.small[
                k : k + 1, j * plan.features : (j + 1) * plan.features
            ]


def weight_gradients(r, t):
    return mm_tn(r.active[t], r.upper[...]), mm_tn(r.slope[t], r.entry[...])


def filter_backward(plan, r, there, back):
    half = plan.half
    r.mixgrad[...] = jnp.zeros_like(r.mixgrad)
    r.biasgrad[...] = jnp.zeros_like(r.biasgrad)

    def turned(v):
        return jnp.concatenate([v[half:], -v[:half]], axis=0)

    def note_bias(index, value):
        r.biasgrad[index : index + 1, :] += jnp.sum(value, axis=0, keepdims=True)

    def through(low, layer):
        straight = mm_nt(low, r.mix[layer, 0, 0])
        crossed = mm_nt(low, r.mix[layer, 1, 0])
        return jnp.concatenate([straight[:half] + crossed[half:], straight[half:] - crossed[:half]], axis=0)

    def filter_pair(q, carry):
        p, zeroth, block = pair_inputs(q, there, r.even)
        grad = mm(r.col[0], block.astype(BF))
        grad = jnp.where(r.second[q].astype(F32) == 0.0, 0.0, grad)
        note_bias(2, grad[:half])
        note_bias(3, grad[half:])
        low = grad.astype(BF)
        first = r.first[q]
        r.mixgrad[1, 0] += mm_tn(first, low)
        r.mixgrad[1, 1] += mm_tn(first, turned(grad).astype(BF))
        grad = jnp.where(first.astype(F32) > 0.0, through(low, 1), 0.0)
        note_bias(0, grad[:half])
        note_bias(1, grad[half:])
        low = grad.astype(BF)
        spec = r.spec[q]
        r.mixgrad[0, 0] += mm_tn(spec, low)
        r.mixgrad[0, 1] += mm_tn(spec, turned(grad).astype(BF))
        result = mm(r.colinv[0], through(low, 0).astype(BF))
        pair_outputs(q, p, zeroth, result, back, r.even, r.last, r.stage)
        return carry

    lax.fori_loop(0, plan.pairs + 1, filter_pair, 0)


def mix_gradients(plan, r, before_ref):
    size = plan.size
    for layer in range(2):
        for part in range(2):
            for block in range(2):
                own = slice(block * size, (block + 1) * size)
                piece = r.mixgrad[layer, part][own, own]
                piece = jnp.concatenate([piece, jnp.zeros((size, 128 - size), F32)], axis=1)
                start = ((layer * 2 + part) * 2 + block) * size
                place = slice(start, start + size)
                r.sums[place, :] = piece if before_ref is None else piece + before_ref[place, :]


def rows_backward(plan, r, unit_ref, before_ref):
    gain = r.gain[...].reshape(1, -1)
    me = lax.axis_index("chan")
    lane = lax.broadcasted_iota(jnp.int32, (plan.columns, 128), 1)

    def row(h, carry):
        table, one_sum, two_sum = carry
        block = modes_to_rows(plan, r.flat, h)
        grad = mm(r.row_t[...], block.astype(BF)) + r.out[h]
        unit = unit_ref[h]
        one_sum += jnp.sum(grad * unit, axis=0, keepdims=True)
        two_sum += jnp.sum(grad, axis=0, keepdims=True)
        scaled = grad * gain
        r.scaled[h] = scaled
        one = jnp.sum(scaled, axis=1, keepdims=True)
        two = jnp.sum(scaled * unit, axis=1, keepdims=True)
        table = jnp.where(lane == h, one, table)
        return jnp.where(lane == plan.rows + h, two, table), one_sum, two_sum

    none = jnp.zeros((1, plan.features), F32)
    table, one_sum, two_sum = lax.fori_loop(
        0, plan.rows, row, (jnp.zeros((plan.columns, 128), F32), none, none)
    )
    table = table.T[: 2 * plan.rows]
    r.mine[...] = table
    r.all[me] = table
    copies = [
        push("chan", plan.chans, step, r.mine, r.all.at[me], r.s4, r.r4) for step in range(1, plan.chans)
    ]
    for copy in copies:
        copy.start()
    vectors = jnp.concatenate([r.biasgrad[0:4], one_sum, two_sum, none, none], axis=0)
    wide = jnp.concatenate([vectors, jnp.zeros((8, 256 - plan.features), F32)], axis=1)
    wide = jnp.concatenate([wide[:, :128], wide[:, 128:]], axis=0)
    place = slice(8 * plan.size, plan.small)
    r.sums[place, :] = wide if before_ref is None else wide + before_ref[place, :]
    return copies


def input_gradient(plan, r, unit_ref, dev_ref):
    lane = lax.broadcasted_iota(jnp.int32, (plan.columns, 128), 1)
    means = sum(r.all[j] for j in range(plan.chans)) * (1.0 / plan.width)
    padding = jnp.zeros((128 - 2 * plan.rows, plan.columns), F32)
    means = jnp.concatenate([means, padding], axis=0).T

    def result(h):
        one = jnp.sum(jnp.where(lane == h, means, 0.0), axis=1, keepdims=True)
        two = jnp.sum(jnp.where(lane == plan.rows + h, means, 0.0), axis=1, keepdims=True)
        return r.out[h] + dev_ref[h][:, :1] * (r.scaled[h] - one - unit_ref[h] * two)

    return result


def norm_sums_scratch(plan):
    return {
        "scaled": scratch_of(plan.field),
        "mixgrad": pltpu.VMEM((2, 2, plan.features, plan.features), F32),
        "biasgrad": pltpu.VMEM((8, plan.features), F32),
        "mine": pltpu.VMEM((2 * plan.rows, plan.columns), F32),
        "all": pltpu.VMEM((plan.chans, 2 * plan.rows, plan.columns), F32),
        "s4": sems(plan.chans),
        "r4": sems(plan.chans),
    }


class Moves:
    def __init__(self, sem):
        self.sem, self.count, self.open = sem, 0, []

    def start(self, source, target):
        copy = pltpu.make_async_copy(source, target, self.sem.at[self.count])
        self.count += 1
        copy.start()
        self.open.append(copy)
        return copy

    def close(self):
        wait_all(self.open)


def launch_first(plan, args, tables):
    rows, features, chans = plan.rows, plan.features, plan.chans

    def body(r):
        me = lax.axis_index("chan")
        place = lax.axis_index("space")
        core = lax.rem(place, 2)
        sibling = place + 1 - 2 * core
        met = greet(plan)
        moves = Moves(r.dma)
        moves.start(r.up, r.w.at[0, me])
        moves.start(r.down, r.w.at[1, me])
        loaded = moves.start(r.lines_t, r.lines_in)
        own_weights = moves.open[:2]
        moves.open = []

        def spread(kind, source):
            return [
                push("chan", chans, step, source, r.w.at[kind, me], r.s5, r.r5) for step in range(1, chans)
            ]

        def row_of(ref):
            return ref[...].reshape(1, -1).astype(F32)

        r.vectors[...] = jnp.zeros_like(r.vectors)
        r.vectors[0:1, :] = row_of(r.upb)
        r.vectors[1:2, 0:features] = row_of(r.post_gain)
        r.vectors[1:2, features : 2 * features] = row_of(r.post_shift)
        r.vectors[1:2, 2 * features : 3 * features] = row_of(r.downb)
        r.gathered[me] = r.vectors[...]
        met()
        for kind, source in enumerate((r.up, r.down)):

            @pl.when(core == kind)
            def _():
                for copy in spread(kind, source):
                    copy.start()

        given = [push("chan", chans, step, r.vectors, r.gathered.at[me], r.s6, r.r6) for step in range(1, chans)]
        for copy in given:
            copy.start()
        for layer, (source, bias) in enumerate(((r.mix_in, r.bias_in), (r.mix_out, r.bias_out))):
            for part in range(2):
                zero = jnp.zeros((plan.size, plan.size), F32)
                value = jnp.concatenate(
                    [
                        jnp.concatenate([source[part, 0], zero], axis=1),
                        jnp.concatenate([zero, source[part, 1]], axis=1),
                    ],
                    axis=0,
                )
                high, low = halves(value)
                r.mix[layer, part, 0] = high
                r.mix[layer, part, 1] = low
                line = 2 * layer + part
                r.bias[line : line + 1, :] = jnp.concatenate([bias[part, 0:1, :], bias[part, 1:2, :]], axis=1)
        moves.start(r.mix, r.mix_kept)

        def first(h, carry):
            block = cells_from_lines(r.lines_x, h, r.turn)
            r.turned[h] = block
            total = jnp.sum(block, axis=0, keepdims=True)
            centred = block - total * (1.0 / features)
            r.mine[pl.ds(h, 1), :] = total
            r.mine[pl.ds(rows + h, 1), :] = jnp.sum(centred * centred, axis=0, keepdims=True)
            return carry

        lax.fori_loop(0, rows, first, 0)
        r.all[me] = r.mine[...]
        run_copies([push("chan", chans, step, r.mine, r.all.at[me], r.s4, r.r4) for step in range(1, chans)])
        totals = [r.all[j] for j in range(chans)]
        mean = sum(t[:rows] for t in totals) * (1.0 / plan.width)
        spread_sum = sum(
            t[rows:] + features * jnp.square(t[:rows] * (1.0 / features) - mean) for t in totals
        ) * (1.0 / plan.width)
        r.mine[pl.ds(0, rows), :] = mean
        r.mine[pl.ds(rows, rows), :] = lax.rsqrt(spread_sum + NORM_EPS)
        gain, shift = r.gain[...].reshape(1, -1), r.shift[...].reshape(1, -1)

        def normed(h):
            block = r.turned[h]
            inverse = r.mine[pl.ds(rows + h, 1), :]
            r.x[h] = block.T
            unit = ((block - r.mine[pl.ds(h, 1), :]) * inverse).T
            r.unit[h] = unit
            r.dev[h] = jnp.broadcast_to(inverse, (8, plan.columns)).T
            return unit * gain + shift

        there = Exchange(True, plan.spaces, plan.thick, r.send1, r.recv1, r.s1, r.r1)
        back = Exchange(True, plan.spaces, plan.thick, r.send2, r.recv2, r.s2, r.r2)
        rows_to_modes(plan, (r.row[0], r.row[1]), r.flat, normed, True)
        send_modes(there, plan.pairs, plan.chunk, r.flat)
        moves.start(r.unit, r.unit_kept)
        moves.start(r.dev, r.dev_kept)
        loaded.wait()
        enter(r.lines_in, r.cells_t, r.turn)
        moves.start(r.cells_t, r.cells_kept)
        filter_forward(plan, r, there, back, True)
        for source, target in ((r.spec, r.spec_kept), (r.first, r.first_kept), (r.second, r.second_kept)):
            moves.start(source, target)
        collect(back, plan.pairs, plan.chunk, r.flat)
        copies = rows_forward(plan, r, True, r.unit, r.x, r.middle)
        moves.start(r.middle, r.middle_kept)
        passed = []
        for step in range(1, chans):
            push("chan", chans, step, r.up, r.w.at[core, me], r.s5, r.r5).wait()
            sender = lax.rem(me - step + chans, chans)
            copy = pltpu.make_async_remote_copy(
                src_ref=r.w.at[core, sender],
                dst_ref=r.w.at[core, sender],
                send_sem=r.s7.at[step],
                recv_sem=r.r7.at[step],
                device_id={"space": sibling},
                device_id_type=MESH_ID,
            )
            copy.start()
            passed.append(copy)
        wait_all(copies + given + passed)
        wait_all(own_weights)
        moves.start(r.w, r.w_kept)
        ffn_forward(plan, r)
        saved = ("active", "slope", "entry", "unit_wide", "dev_wide", "gathered")
        for key in saved:
            moves.start(getattr(r, key), getattr(r, key + "_kept"))

        def last(block):
            outer = r.total[block, :]
            mean, _, inverse = moments(outer + joined(r.mid, block))
            stats = three_parts(mean) + three_parts(inverse)
            stats = jnp.concatenate(stats + [jnp.zeros((BLOCK, 256 - features - 6), BF)], axis=1)
            for j in range(chans):
                r.leaving[j, block, :] = jnp.concatenate(
                    [outer[:, j * features : (j + 1) * features].astype(BF), stats], axis=1
                )

        by_blocks(plan, last)
        wait_all(spread_chan(plan, r.leaving, r.home, r.s8, r.r8))
        there.close(plan.pairs)
        back.close(plan.pairs)
        moves.close()

    home = ((chans, plan.cells, 256), BF)
    outs = {
        "home": home,
        "middle_kept": plan.field,
        "unit_kept": plan.field,
        "dev_kept": plan.dev,
        "cells_kept": plan.field,
        "spec_kept": plan.kept,
        "first_kept": plan.kept,
        "second_kept": plan.kept,
        "mix_kept": plan.mix,
        "w_kept": plan.weights,
        "active_kept": plan.tiles,
        "slope_kept": plan.tiles,
        "entry_kept": plan.wide,
        "unit_wide_kept": plan.wide,
        "dev_wide_kept": plan.dev_wide,
        "gathered_kept": plan.vectors,
        "bias": ((8, features), F32),
    }
    ins = dict(args)
    ins.update({key: tables[key] for key in ("row", "rowinv", "col", "colinv", "even")})
    scratch = {
        "dma": sems(20),
        "x": scratch_of(plan.field),
        "unit": scratch_of(plan.field),
        "dev": scratch_of(plan.dev),
        "middle": scratch_of(plan.field),
        "cells_t": scratch_of(plan.field),
        "lines_in": scratch_of(plan.lines),
        "turned": pltpu.VMEM((rows, features, plan.columns), F32),
        "mine": pltpu.VMEM((2 * rows, plan.columns), F32),
        "all": pltpu.VMEM((chans, 2 * rows, plan.columns), F32),
        "spec": scratch_of(plan.kept),
        "first": scratch_of(plan.kept),
        "second": scratch_of(plan.kept),
        "mix": scratch_of(plan.mix),
        "w": scratch_of(plan.weights),
        "vectors": pltpu.VMEM((8, plan.local), F32),
        "own": scratch_of(plan.by_cells),
        "mid": scratch_of(plan.by_cells),
        "leaving": scratch_of(home),
        **plan.exchange_scratch(True, True),
        **plan.spectral_scratch(),
        **ffn_scratch(plan),
        **{key + str(k): sems(chans) for k in range(3, 9) for key in ("s", "r")},
    }
    in_place = ("up", "down", "lines_t")
    return launch(
        body,
        ins,
        outs,
        scratch,
        "first_forward",
        0,
        {key: IN_PLACE for key in in_place},
        {key: IN_PLACE for key in outs if key.endswith("_kept")},
    )


def launch_second(plan, args, one, tables):
    rows, features, chans = plan.rows, plan.features, plan.chans

    def body(r):
        me = lax.axis_index("chan")
        met = greet(plan)
        moves = Moves(r.dma)
        loaded = moves.start(r.lines_t, r.lines_in)
        weights = moves.start(r.w_kept, r.w)
        vectors = moves.start(r.gathered_kept, r.gathered)
        earlier = moves.start(r.cells_kept, r.cells_one)
        moves.open = []
        gain, shift = r.gain[...].reshape(1, -1), r.shift[...].reshape(1, -1)
        weight = r.codes[0].astype(F32) * (1.0 / 64.0)

        def normed(h):
            home = r.home[h].astype(F32)
            x = home[:, :features] + r.before[h]
            parts = [home[:, features + k : features + k + 1] for k in range(6)]
            mean = parts[0] + (parts[1] + parts[2])
            dev = parts[3] + (parts[4] + parts[5])
            unit = (x - mean) * dev
            r.x[h] = x
            r.unit[h] = unit
            r.dev[h] = jnp.broadcast_to(dev, (plan.columns, 8))
            return unit * gain + shift

        rows_to_modes(plan, (r.row[0], r.row[1]), r.flat, normed, True)
        met()
        there = Exchange(True, plan.spaces, plan.thick, r.send1, r.recv1, r.s1, r.r1)
        back = Exchange(False, plan.spaces, plan.thick, r.send2, r.recv2, r.s2, r.r2)
        send_modes(there, plan.pairs, plan.chunk, r.flat)
        loaded.wait()
        enter(r.lines_in, r.cells_t, r.turn)

        def low_target(h, peer, place):
            r.own[peer, place, :] = r.cells_t[h].astype(BF)

        targets = []

        def send_target(step, peer):
            if step:
                copy = push("chan", chans, step, r.own.at[peer], r.target.at[me], r.s5, r.r5)
                copy.start()
                targets.append(copy)
            else:
                r.target[me] = r.own[me]

        rows_of_chunks(plan, low_target, send_target)
        filter_forward(plan, r, there, back, False)
        collect(back, plan.pairs, plan.chunk, r.flat)
        there.close(plan.pairs)
        back.close(plan.pairs)
        wait_all(targets)
        copies = rows_forward(plan, r, False, r.unit, r.x, r.before)
        weights.wait()
        vectors.wait()
        wait_all(copies)
        ffn_forward(plan, r)

        def errors(block):
            outer = r.total[block, :]
            error = outer + joined(r.mid, block) - joined(r.target, block)
            r.upper[block, :] = (weight * error).astype(BF)
            for j in range(chans):
                r.leaving[j, block, :] = outer[:, j * features : (j + 1) * features].astype(BF)

        by_blocks(plan, errors)
        copies = spread_chan(plan, r.leaving, r.landed, r.s6, r.r6)
        for copy in copies:
            copy.wait_send()
        ffn_backward(plan, r)
        for copy in copies:
            copy.wait_recv()
        copies = spread_chan(plan, r.leaving, r.own, r.s7, r.r7)

        def grads(u, carry):
            for slot in range(2):
                t = 2 * u + slot
                stores = [
                    pltpu.make_async_copy(r.grad.at[slot, k], r.grads_kept.at[k, t], r.dma2.at[slot, k])
                    for k in range(2)
                ]

                @pl.when(u > 0)
                def _():
                    wait_all(stores)

                for k, value in enumerate(weight_gradients(r, t)):
                    r.grad[slot, k] = value.astype(BF)
                    stores[k].start()
            return carry

        lax.fori_loop(0, plan.steps // 2, grads, 0)
        vector_gradients(plan, r, r.rest)
        wait_all(copies)

        def middle_grad(h):
            quarter = h // plan.share
            place = pl.ds(pl.multiple_of((h % plan.share) * plan.columns, 16), plan.columns)
            x = r.landed[quarter, place, :].astype(F32) + r.before[h]
            r.before[h] = x
            grad = weight * (x - r.cells_t[h]) + r.own[quarter, place, :].astype(F32)
            r.out[h] = grad
            return grad

        rows_to_modes(plan, r.rowinv_t[...], r.flat, middle_grad, False)
        there = Exchange(False, plan.spaces, plan.thick, r.send3, r.recv3, r.s3_, r.r3_)
        back = Exchange(False, plan.spaces, plan.thick, r.send2, r.recv2, r.s2, r.r2)
        send_modes(there, plan.pairs, plan.chunk, r.flat)
        moves.start(r.before, r.second_x)
        leave(r.x, r.lines, r.turn)
        filter_backward(plan, r, there, back)
        mix_gradients(plan, r, None)
        collect(back, plan.pairs, plan.chunk, r.flat)
        copies = rows_backward(plan, r, r.unit, None)
        earlier.wait()
        wait_all(copies)
        result = input_gradient(plan, r, r.unit, r.dev)
        copies = []

        def row(h, peer, place):
            grad = weight * (r.x[h] - r.cells_one[h]) + result(h)
            r.out[h] = grad
            r.own[peer, place, :] = grad.astype(BF)

        def send_chunk(step, peer):
            if step:
                copy = push("chan", chans, step, r.own.at[peer], r.came.at[me], r.s8, r.r8)
                copy.start()
                copies.append(copy)
            else:
                r.came[me] = r.own[me]

        rows_of_chunks(plan, row, send_chunk)
        for slot in range(2):
            for k in range(2):
                pltpu.make_async_copy(
                    r.grad.at[slot, k], r.grads_kept.at[k, plan.steps - 2 + slot], r.dma2.at[slot, k]
                ).wait()
        wait_all(copies)
        there.close(plan.pairs)
        back.close(plan.pairs)
        moves.close()

    ins = {
        "home": one["home"].reshape(rows, plan.columns, 256),
        "before": one["middle_kept"],
        "w_kept": one["w_kept"],
        "gathered_kept": one["gathered_kept"],
        "cells_kept": one["cells_kept"],
        "mix": one["mix_kept"],
        "bias": one["bias"],
        **args,
    }
    ins.update({key: tables[key] for key in ("row", "rowinv", "rowinv_t", "row_t", "col", "colinv", "even")})
    outs = {
        "out": plan.field,
        "came": plan.by_cells,
        "lines": plan.lines,
        "second_x": plan.field,
        "sums": plan.sums,
        "rest": plan.rest,
        "grads_kept": plan.grads,
    }
    exchange = Exchange.shape(False, plan.spaces, plan.thick, plan.pairs)
    scratch = {
        "dma": sems(8),
        "dma2": sems(2, 2),
        "x": scratch_of(plan.field),
        "unit": scratch_of(plan.field),
        "dev": scratch_of(plan.dev),
        "cells_t": scratch_of(plan.field),
        "cells_one": scratch_of(plan.field),
        "lines_in": scratch_of(plan.lines),
        "spec": scratch_of(plan.kept),
        "first": scratch_of(plan.kept),
        "second": scratch_of(plan.kept),
        "w": scratch_of(plan.weights),
        "own": scratch_of(plan.by_cells),
        "mid": scratch_of(plan.by_cells),
        "target": scratch_of(plan.by_cells),
        "leaving": scratch_of(plan.by_cells),
        "landed": scratch_of(plan.by_cells),
        "upper": scratch_of(plan.wide),
        "small": pltpu.VMEM((8, plan.width), F32),
        "upb": pltpu.VMEM((16, plan.tile), F32),
        "grad": pltpu.VMEM((2, 2, plan.tile, plan.width), BF),
        "send3": exchange,
        "recv3": exchange,
        "s3_": sems(plan.pairs, plan.spaces),
        "r3_": sems(plan.pairs, plan.spaces),
        **plan.exchange_scratch(True, False),
        **plan.spectral_scratch(),
        **ffn_scratch(plan),
        **norm_sums_scratch(plan),
        **{key + str(k): sems(chans) for k in (3, 5, 6, 7, 8) for key in ("s", "r")},
    }
    in_specs = {key: IN_PLACE for key in ("w_kept", "gathered_kept", "cells_kept", "lines_t")}
    in_specs["codes"] = pl.BlockSpec(memory_space=pltpu.SMEM)
    return launch(
        body,
        ins,
        outs,
        scratch,
        "second_step",
        1,
        in_specs,
        {key: IN_PLACE for key in ("second_x", "grads_kept")},
    )


def launch_third(plan, args, one, two, tables):
    rows, features, chans, spaces = plan.rows, plan.features, plan.chans, plan.spaces
    local, width = plan.local, plan.width
    levels = spaces // 2
    piece = local // levels
    small = plan.small
    part = -(-(small + 32) // (16 * levels)) * 16

    def body(r):
        me = lax.axis_index("chan")
        place = lax.axis_index("space")
        core = lax.rem(place, 2)
        level = place // 2
        sibling = place + 1 - 2 * core
        others = [lax.rem(level + step, levels) for step in range(1, levels)]
        met = greet(plan)
        moves = Moves(r.dma)
        gradient = moves.start(r.g, r.out)
        early = [
            moves.start(source, target)
            for source, target in (
                (r.w_kept, r.w),
                (r.slope_kept, r.slope),
                (r.unit_wide_kept, r.unit_wide),
                (r.dev_wide_kept, r.dev_wide),
                (r.gathered_kept, r.gathered),
            )
        ]
        middle = [moves.start(r.active_kept, r.active), moves.start(r.entry_kept, r.entry)]
        late = [
            moves.start(source, target)
            for source, target in (
                (r.spec_kept, r.spec),
                (r.first_kept, r.first),
                (r.second_kept, r.second),
                (r.unit_kept, r.unit),
                (r.dev_kept, r.dev),
                (r.second_x, r.scaled),
            )
        ]
        moves.open = []

        def upper(block):
            r.upper[block, :] = joined(r.came, block).astype(BF)

        by_blocks(plan, upper)
        wait_all(early)
        ffn_backward(plan, r)
        met()
        copies = spread_chan(plan, r.leaving, r.own, r.s7, r.r7)
        vector_gradients(plan, r, r.rest)
        r.rest[...] += r.rest_before[...]
        vectors = [
            push("chan", chans, step, r.rest.at[lax.rem(me + step, chans)], r.rest_land.at[me], r.s6, r.r6)
            for step in range(1, chans)
        ]
        for copy in vectors:
            copy.start()
        r.rest_land[me] = r.rest[me]
        wait_all(middle)

        def order(i):
            return lax.rem((me + 1) * plan.per + i, plan.steps)

        def fetch(i, k):
            return pltpu.make_async_copy(r.grads_kept.at[k, order(i)], r.prev.at[i % 2, k], r.dma2.at[i % 2, k])

        def swap(i):
            return pltpu.make_async_remote_copy(
                src_ref=r.give.at[i % 2],
                dst_ref=r.take.at[i % 3],
                send_sem=r.s9.at[i],
                recv_sem=r.r9.at[i],
                device_id={"space": sibling},
                device_id_type=MESH_ID,
            )

        def ship(i):
            step = 1 + i // plan.per
            return pltpu.make_async_remote_copy(
                src_ref=r.keep.at[i],
                dst_ref=r.land.at[step - 1, i % plan.per],
                send_sem=r.s10.at[i],
                recv_sem=r.r10.at[i],
                device_id={"chan": lax.rem(me + step, chans)},
                device_id_type=MESH_ID,
            )

        for k in range(2):
            fetch(0, k).start()

        def settle(i):
            swap(i).wait()
            r.keep[i] = (r.keep[i].astype(F32) + r.take[i % 3].astype(F32)).astype(BF)

        def block(i, carry):
            for k in range(2):
                fetch(i, k).wait()

            @pl.when(i + 1 < plan.steps)
            def _():
                for k in range(2):
                    fetch(i + 1, k).start()

            values = [
                (value + r.prev[i % 2, k].astype(F32)).astype(BF)
                for k, value in enumerate(weight_gradients(r, order(i)))
            ]

            @pl.when(i > 0)
            def _():
                settle(i - 1)

                @pl.when(i - 1 < plan.steps - plan.per)
                def _():
                    ship(i - 1).start()

            for kind in range(2):

                @pl.when(core == kind)
                def _():
                    r.keep[i] = values[kind]
                    r.give[i % 2] = values[1 - kind]

            swap(i).start()
            return carry

        lax.fori_loop(0, plan.steps, block, 0)
        settle(plan.steps - 1)
        wait_all(copies)
        wait_all(late)
        gradient.wait()

        def middle_grad(h):
            quarter = h // plan.share
            rows_here = pl.ds(pl.multiple_of((h % plan.share) * plan.columns, 16), plan.columns)
            grad = r.out[h] + r.own[quarter, rows_here, :].astype(F32)
            r.out[h] = grad
            return grad

        rows_to_modes(plan, r.rowinv_t[...], r.flat, middle_grad, False)
        there = Exchange(False, spaces, plan.thick, r.send1, r.recv1, r.s1, r.r1)
        back = Exchange(False, spaces, plan.thick, r.send2, r.recv2, r.s2, r.r2)
        send_modes(there, plan.pairs, plan.chunk, r.flat)
        leave(r.scaled, r.lines, r.turn)
        moves.start(r.lines, r.lines_x)
        filter_backward(plan, r, there, back)
        mix_gradients(plan, r, r.sums_before)

        def arrived(i, carry):
            ship(i).wait()
            return carry

        lax.fori_loop(0, plan.steps - plan.per, arrived, 0)
        wait_all(vectors)
        def send(source, target, step, send_sem, recv_sem):
            return pltpu.make_async_remote_copy(
                src_ref=source,
                dst_ref=target,
                send_sem=send_sem.at[step],
                recv_sem=recv_sem.at[step],
                device_id={"space": 2 * others[step - 1] + core},
                device_id_type=MESH_ID,
            )

        def to_sibling(source, target, step, send_sem, recv_sem):
            return pltpu.make_async_remote_copy(
                src_ref=source,
                dst_ref=target,
                send_sem=send_sem.at[step],
                recv_sem=recv_sem.at[step],
                device_id={"space": sibling},
                device_id_type=MESH_ID,
            )

        def total(line, carry):
            tile, inside = line // (plan.tile // 64), line % (plan.tile // 64)
            own = pl.ds(pl.multiple_of(inside * 64, 64), 64)
            value = r.keep[plan.steps - plan.per + tile, own, :].astype(F32)
            value += sum(r.land[j, tile, own, :].astype(F32) for j in range(chans - 1))
            target = pl.ds(pl.multiple_of((line % (piece // 64)) * 64, 64), 64)
            r.a_send[line // (piece // 64), target, :] = value.astype(BF)
            return carry

        lax.fori_loop(0, local // 64, total, 0)
        collect(back, plan.pairs, plan.chunk, r.flat)
        wide = [
            send(r.a_send.at[others[step - 1]], r.a_land.at[level], step, r.s11, r.r11)
            for step in range(1, levels)
        ]
        for copy in wide:
            copy.start()
        copies = rows_backward(plan, r, r.unit, r.sums_before)
        r.table[...] = jnp.zeros_like(r.table)
        r.table[0:small, :] = r.sums[...]
        tail = sum(r.rest_land[j] for j in range(chans))
        for k in range(local // 128):
            lanes = slice(k * 128, (k + 1) * 128)
            r.table[small + k : small + k + 1, :] = tail[0:1, lanes]
        for k in range(3):
            line = jnp.concatenate([tail[1 + k : 2 + k, :features], jnp.zeros((1, 256 - features), F32)], axis=1)
            r.table[small + 8 + 2 * k : small + 9 + 2 * k, :] = line[:, :128]
            r.table[small + 9 + 2 * k : small + 10 + 2 * k, :] = line[:, 128:]
        for q in range(levels):
            r.b_send[q] = r.table[q * part : (q + 1) * part, :].astype(BF)
        thin = [
            send(r.b_send.at[others[step - 1]], r.b_land.at[level], step, r.s12, r.r12)
            for step in range(1, levels)
        ]
        for copy in thin:
            copy.start()
        wait_all(copies)
        result = input_gradient(plan, r, r.unit, r.dev)

        def finish(h, carry):
            r.out[h] = result(h)
            return carry

        lax.fori_loop(0, rows, finish, 0)
        a = r.a_send[level].astype(F32)
        b = r.b_send[level].astype(F32)
        for step in range(1, levels):
            wide[step - 1].wait()
            thin[step - 1].wait()
            source = lax.rem(level - step + levels, levels)
            a += r.a_land[source].astype(F32)
            b += r.b_land[source].astype(F32)
        r.a_own[...] = a.astype(BF)
        r.b_own[...] = b.astype(BF)
        last = [to_sibling(r.a_own, r.a_other.at[level], 0, r.s13, r.r13)]
        last += [to_sibling(r.b_own, r.b_other.at[level], 0, r.s14, r.r14)]
        again = []
        for step in range(1, levels):
            again.append(send(r.a_own, r.a_full.at[level], step, r.s15, r.r15))
            again.append(send(r.b_own, r.b_full.at[level], step, r.s16, r.r16))
        for copy in again + last:
            copy.start()
        r.a_full[level] = r.a_own[...]
        r.b_full[level] = r.b_own[...]
        moves.close()
        moves.open = []
        leave(r.out, r.lines, r.turn)
        moves.start(r.lines, r.lines_out)
        for step in range(1, levels):
            again[2 * step - 2].wait()
            again[2 * step - 1].wait()
            source = lax.rem(level - step + levels, levels)
            more = [to_sibling(r.a_full.at[source], r.a_other.at[source], step, r.s13, r.r13)]
            more += [to_sibling(r.b_full.at[source], r.b_other.at[source], step, r.s14, r.r14)]
            for copy in more:
                copy.start()
            last += more
        wait_all(last)
        moves.close()
        there.close(plan.pairs)
        back.close(plan.pairs)

    ins = {
        "g": two["out"],
        "came": two["came"],
        "second_x": two["second_x"],
        "sums_before": two["sums"],
        "rest_before": two["rest"],
        "grads_kept": two["grads_kept"],
        "mix": one["mix_kept"],
        **{
            key: one[key]
            for key in (
                "w_kept",
                "slope_kept",
                "active_kept",
                "entry_kept",
                "unit_wide_kept",
                "dev_wide_kept",
                "gathered_kept",
                "spec_kept",
                "first_kept",
                "second_kept",
                "unit_kept",
                "dev_kept",
            )
        },
        **args,
    }
    ins.update({key: tables[key] for key in ("rowinv_t", "row_t", "col", "colinv", "even")})
    outs = {
        "lines_x": plan.lines,
        "lines_out": plan.lines,
        "a_full": ((levels, piece, width), BF),
        "a_other": ((levels, piece, width), BF),
        "b_full": ((levels, part, 128), BF),
        "b_other": ((levels, part, 128), BF),
    }
    blocks = pltpu.VMEM((plan.steps, plan.tile, width), BF)
    scratch = {
        "dma": sems(16),
        "dma2": sems(2, 2),
        "lines": scratch_of(plan.lines),
        "unit": scratch_of(plan.field),
        "dev": scratch_of(plan.dev),
        "out": scratch_of(plan.field),
        "spec": scratch_of(plan.kept),
        "first": scratch_of(plan.kept),
        "second": scratch_of(plan.kept),
        "w": scratch_of(plan.weights),
        "own": scratch_of(plan.by_cells),
        "leaving": scratch_of(plan.by_cells),
        "upper": scratch_of(plan.wide),
        "small": pltpu.VMEM((8, width), F32),
        "upb": pltpu.VMEM((16, plan.tile), F32),
        "sums": scratch_of(plan.sums),
        "rest": scratch_of(plan.rest),
        "rest_land": scratch_of(plan.rest),
        "prev": pltpu.VMEM((2, 2, plan.tile, width), BF),
        "keep": blocks,
        "give": pltpu.VMEM((2, plan.tile, width), BF),
        "take": pltpu.VMEM((3, plan.tile, width), BF),
        "land": pltpu.VMEM((chans - 1, plan.per, plan.tile, width), BF),
        "table": pltpu.VMEM((part * levels, 128), F32),
        "a_send": pltpu.VMEM((levels, piece, width), BF),
        "a_land": pltpu.VMEM((levels, piece, width), BF),
        "a_own": pltpu.VMEM((piece, width), BF),
        "b_send": pltpu.VMEM((levels, part, 128), BF),
        "b_land": pltpu.VMEM((levels, part, 128), BF),
        "b_own": pltpu.VMEM((part, 128), BF),
        **plan.exchange_scratch(False, False),
        **plan.spectral_scratch(),
        **ffn_scratch(plan),
        **norm_sums_scratch(plan),
        **{key + str(k): sems(chans) for k in (6, 7) for key in ("s", "r")},
        **{key + str(k): sems(plan.steps) for k in (9, 10) for key in ("s", "r")},
        **{key + str(k): sems(levels) for k in range(11, 17) for key in ("s", "r")},
    }
    in_place = [key for key in ins if key.endswith("_kept") and key != "mix_kept"] + ["second_x", "g"]
    return launch(
        body,
        ins,
        outs,
        scratch,
        "first_backward",
        2,
        {key: IN_PLACE for key in in_place},
        {key: IN_PLACE for key in ("lines_x", "lines_out")},
    )


def unpack_gradients(plan, parts):
    features, small = plan.features, plan.small
    levels, piece, width = parts["a_full"].shape
    part = parts["b_full"].shape[1]
    local = levels * piece
    size = features // 2

    def body(r):
        swap = lax.rem(lax.axis_index("space"), 2) == 1
        for q in range(levels):
            own = slice(q * piece, (q + 1) * piece)
            mine, theirs = r.a_full[q].astype(F32), r.a_other[q].astype(F32)
            r.down[own, :] = jnp.where(swap, theirs, mine)
            r.up[:, own] = jnp.where(swap, mine, theirs).T
            r.table[q * part : (q + 1) * part, :] = r.b_full[q].astype(F32) + r.b_other[q].astype(F32)
        for layer, target in enumerate((r.mix_in, r.mix_out)):
            for half in range(2):
                for block in range(2):
                    start = ((layer * 2 + half) * 2 + block) * size
                    target[half, block] = r.table[start : start + size, :size]
        base = 8 * size

        def vector(k):
            return jnp.concatenate(
                [r.table[base + k : base + k + 1, :], r.table[base + 8 + k : base + 9 + k, : features - 128]], axis=1
            )

        for k, target in enumerate((r.bias_in, r.bias_in, r.bias_out, r.bias_out)):
            value = vector(k)
            target[k % 2, 0:1, :] = value[:, :size]
            target[k % 2, 1:2, :] = value[:, size:]
        r.pre_gain[...] = vector(4)
        r.pre_shift[...] = vector(5)
        for k in range(local // 128):
            r.upb[0:1, k * 128 : (k + 1) * 128] = r.table[small + k : small + k + 1, :]
        for k, target in enumerate((r.post_gain, r.post_shift, r.downb)):
            target[...] = jnp.concatenate(
                [
                    r.table[small + 8 + 2 * k : small + 9 + 2 * k, :],
                    r.table[small + 9 + 2 * k : small + 10 + 2 * k, : features - 128],
                ],
                axis=1,
            )


    return launch(
        body,
        {key: parts[key] for key in ("a_full", "a_other", "b_full", "b_other")},
        {
            "down": ((local, width), F32),
            "up": ((width, local), F32),
            "mix_in": ((2, 2, size, size), F32),
            "mix_out": ((2, 2, size, size), F32),
            "bias_in": ((2, 2, size), F32),
            "bias_out": ((2, 2, size), F32),
            "pre_gain": ((1, features), F32),
            "pre_shift": ((1, features), F32),
            "post_gain": ((1, features), F32),
            "post_shift": ((1, features), F32),
            "downb": ((1, features), F32),
            "upb": ((1, local), F32),
        },
        {"table": pltpu.VMEM((part * levels, 128), F32)},
        "unpack_gradients",
    )


def shards_fast(
    current_atmosphere,
    truth_one,
    truth_two,
    storm_codes,
    pre_gain,
    pre_shift,
    mix_weight_in,
    mix_bias_in,
    mix_weight_out,
    mix_bias_out,
    post_gain,
    post_shift,
    up_weight,
    up_bias,
    down_weight,
    down_bias,
):
    rows, merged = current_atmosphere.shape[1:]
    columns = W
    features = merged // columns
    plan = Plan(
        rows, features, columns, lax.axis_size("space"), lax.axis_size("chan"), up_weight.shape[1]
    )
    forward, inverse = row_constants(columns)
    column = column_constants(rows * plan.spaces, rows, 2)
    even = (np.arange(plan.half) // rows % 2 == 0).astype(np.float32)
    tables = {
        "row": jnp.stack(const_halves(forward)),
        "rowinv": jnp.stack(const_halves(inverse)),
        "rowinv_t": const_halves(inverse.T)[0],
        "row_t": const_halves(forward.T)[0],
        "col": jnp.stack(const_halves(column)),
        "colinv": jnp.stack(const_halves(column.T)),
        "even": jnp.asarray(np.repeat(even[:, None], features, axis=1)),
    }

    def lines(flat):
        return flat.reshape(rows, merged // 128, 128)

    def flat(line_field):
        return line_field.reshape(1, rows, merged)

    one = launch_first(
        plan,
        {
            "lines_x": lines(current_atmosphere),
            "lines_t": lines(truth_one),
            "gain": pre_gain,
            "shift": pre_shift,
            "mix_in": mix_weight_in,
            "bias_in": mix_bias_in,
            "mix_out": mix_weight_out,
            "bias_out": mix_bias_out,
            "post_gain": post_gain,
            "post_shift": post_shift,
            "up": up_weight,
            "upb": up_bias,
            "down": down_weight,
            "downb": down_bias,
        },
        tables,
    )
    two = launch_second(
        plan,
        {"gain": pre_gain, "shift": pre_shift, "lines_t": lines(truth_two), "codes": storm_codes},
        one,
        tables,
    )
    three = launch_third(plan, {"gain": pre_gain}, one, two, tables)
    grads = unpack_gradients(plan, three)
    return (
        flat(two["lines"]),
        flat(three["lines_x"]),
        flat(three["lines_out"]),
        grads["pre_gain"].reshape(features),
        grads["pre_shift"].reshape(features),
        grads["mix_in"],
        grads["bias_in"],
        grads["mix_out"],
        grads["bias_out"],
        grads["post_gain"].reshape(features),
        grads["post_shift"].reshape(features),
        grads["up"],
        grads["upb"].reshape(plan.local),
        grads["down"],
        grads["downb"].reshape(features),
    )


def suits(mesh):
    spaces, chans = mesh.shape["space"], mesh.shape["chan"]
    return (spaces, chans) == (8, 4)


def solution(mesh):
    in_specs = (
        P(None, "space", "chan"),
        P(None, "space", "chan"),
        P(None, "space", "chan"),
        P(),
        P("chan"),
        P("chan"),
        P(None, "chan", None, None),
        P(None, "chan", None),
        P(None, "chan", None, None),
        P(None, "chan", None),
        P("chan"),
        P("chan"),
        P(None, "chan"),
        P("chan"),
        P("chan", None),
        P("chan"),
    )
    out_specs = (
        P(None, "space", "chan"),
        P(None, "space", "chan"),
        P(None, "space", "chan"),
        P("chan"),
        P("chan"),
        P(None, "chan", None, None),
        P(None, "chan", None),
        P(None, "chan", None, None),
        P(None, "chan", None),
        P("chan"),
        P("chan"),
        P(None, "chan"),
        P("chan"),
        P("chan", None),
        P("chan"),
    )
    return jax.shard_map(shards_fast if suits(mesh) else shards, mesh=mesh, in_specs=in_specs, out_specs=out_specs, check_vma=False)
```

```python
import functools
import math
import types

import jax
import jax.numpy as jnp
import ml_dtypes
import numpy as np
from jax import lax
from jax.experimental import pallas as pl
from jax.experimental.pallas import tpu as pltpu
from jax.sharding import PartitionSpec as P

W = 160
KW = 81


NORM_EPS = 1e-06
SHRINK_LEVEL = 0.01
FULL_PRECISION = lax.Precision.HIGHEST


def exact_gelu(values):
    return jax.nn.gelu(values, approximate=False)


def shrink(values):
    return values - jnp.clip(values, -SHRINK_LEVEL, SHRINK_LEVEL)


def block_mix(values, matrix):
    return jnp.einsum("bhkni,nio->bhkno", values, matrix, precision=FULL_PRECISION)


def row_tables(columns, kept_modes, padded_modes):
    places = jnp.arange(columns, dtype=jnp.int32)[:, None]
    orders = jnp.arange(padded_modes, dtype=jnp.int32)[None, :]
    angles = 2.0 * math.pi / columns * (places * orders % columns).astype(jnp.float32)
    factor = 1.0 / math.sqrt(columns)
    single = jnp.logical_or(orders == 0, 2 * orders == columns)
    doubled = jnp.where(single, 1.0, 2.0).astype(jnp.float32)
    used = jnp.where(orders < kept_modes, 1.0, 0.0).astype(jnp.float32)
    return (
        jnp.cos(angles) * factor * used,
        -jnp.sin(angles) * factor * used,
        jnp.transpose(jnp.cos(angles) * doubled * factor * used),
        jnp.transpose(jnp.sin(angles) * doubled * factor * used),
    )


def along_rows(values, tables):
    return jnp.stack(
        [
            jnp.einsum("bhwc,wk->bhkc", values, tables[0], precision=FULL_PRECISION),
            jnp.einsum("bhwc,wk->bhkc", values, tables[1], precision=FULL_PRECISION),
        ]
    )


def along_rows_back(paired, tables):
    return jnp.einsum("bhkc,wk->bhwc", paired[0], tables[0], precision=FULL_PRECISION) + jnp.einsum(
        "bhkc,wk->bhwc", paired[1], tables[1], precision=FULL_PRECISION
    )


def rows_inverse(paired, tables):
    return jnp.einsum("bhkc,kw->bhwc", paired[0], tables[2], precision=FULL_PRECISION) - jnp.einsum(
        "bhkc,kw->bhwc", paired[1], tables[3], precision=FULL_PRECISION
    )


def rows_inverse_back(values, tables):
    return jnp.stack(
        [
            jnp.einsum("bhwc,kw->bhkc", values, tables[2], precision=FULL_PRECISION),
            -jnp.einsum("bhwc,kw->bhkc", values, tables[3], precision=FULL_PRECISION),
        ]
    )


def column_tables(height):
    orders = jnp.arange(height, dtype=jnp.int32)[:, None]
    places = jnp.arange(height, dtype=jnp.int32)[None, :]
    angles = 2.0 * math.pi / height * (orders * places % height).astype(jnp.float32)
    factor = 1.0 / math.sqrt(height)
    return (jnp.cos(angles) * factor, jnp.sin(angles) * factor)


def to_freq(matrix, values):
    return jnp.einsum("kh,bhmc->bkmc", matrix, values, precision=FULL_PRECISION)


def from_freq(matrix, values):
    return jnp.einsum("kh,bkmc->bhmc", matrix, values, precision=FULL_PRECISION)


def spectral_core(paired, w_first, b_first, w_second, b_second):
    samples, height, kept_modes, channels = paired.shape[1:]
    blocks, block_size = (w_first.shape[1], w_first.shape[2])
    cosine, sine_table = column_tables(height)
    real_in, imag_in = (paired[0], paired[1])
    split_form = (samples, height, kept_modes, blocks, block_size)
    real_part = (to_freq(cosine, real_in) + to_freq(sine_table, imag_in)).reshape(split_form)
    imag_part = (to_freq(cosine, imag_in) - to_freq(sine_table, real_in)).reshape(split_form)
    first_real = jax.nn.relu(
        block_mix(real_part, w_first[0]) - block_mix(imag_part, w_first[1]) + b_first[0]
    )
    first_imag = jax.nn.relu(
        block_mix(imag_part, w_first[0]) + block_mix(real_part, w_first[1]) + b_first[1]
    )
    joined_form = (samples, height, kept_modes, channels)
    second_real = shrink(
        block_mix(first_real, w_second[0]) - block_mix(first_imag, w_second[1]) + b_second[0]
    ).reshape(joined_form)
    second_imag = shrink(
        block_mix(first_imag, w_second[0]) + block_mix(first_real, w_second[1]) + b_second[1]
    ).reshape(joined_form)
    out_real = from_freq(cosine, second_real) - from_freq(sine_table, second_imag)
    out_imag = from_freq(cosine, second_imag) + from_freq(sine_table, second_real)
    return jnp.stack([out_real, out_imag])


def column_layout(paired):
    return lax.all_to_all(paired, "space", split_axis=3, concat_axis=2, tiled=True)


def row_layout(paired):
    return lax.all_to_all(
        paired.astype(jnp.bfloat16), "space", split_axis=2, concat_axis=3, tiled=True
    ).astype(paired.dtype)


def norm_forward(values, gain, offset):
    width_all = values.shape[-1] * lax.axis_size("chan")
    totals = lax.psum((jnp.sum(values, axis=-1), jnp.sum(values * values, axis=-1)), "chan")
    average = totals[0] / width_all
    variance = totals[1] / width_all - average * average
    inverse_dev = lax.rsqrt(variance + NORM_EPS)[..., None]
    scaled = (values - average[..., None]) * inverse_dev
    return (scaled * gain + offset, (scaled, inverse_dev))


def norm_backward(gradient, gain, saved):
    scaled, inverse_dev = saved
    width_all = scaled.shape[-1] * lax.axis_size("chan")
    scaled_grad = gradient * gain
    totals = lax.psum(
        (jnp.sum(scaled_grad, axis=-1), jnp.sum(scaled_grad * scaled, axis=-1)), "chan"
    )
    values_grad = inverse_dev * (
        scaled_grad - totals[0][..., None] / width_all - scaled * (totals[1][..., None] / width_all)
    )
    return (
        values_grad,
        jnp.sum(gradient * scaled, axis=(0, 1, 2)),
        jnp.sum(gradient, axis=(0, 1, 2)),
    )


def shards(
    current_atmosphere,
    truth_one,
    truth_two,
    storm_codes,
    pre_gain,
    pre_shift,
    mix_weight_in,
    mix_bias_in,
    mix_weight_out,
    mix_bias_out,
    post_gain,
    post_shift,
    up_weight,
    up_bias,
    down_weight,
    down_bias,
):
    samples, rows_here, merged = current_atmosphere.shape
    columns = W
    channels = merged // columns
    total_rows = samples * rows_here * columns
    space_count = lax.axis_size("space")
    padded_modes = (KW + space_count - 1) // space_count * space_count
    tables = row_tables(columns, KW, padded_modes)

    def to_cells(flat_field):
        return jnp.transpose(
            flat_field.reshape(samples, rows_here, channels, columns), (0, 1, 3, 2)
        )

    def to_flat(cell_field):
        return jnp.transpose(cell_field, (0, 1, 3, 2)).reshape(samples, rows_here, merged)

    start_cells = to_cells(current_atmosphere)
    target_one = to_cells(truth_one)
    target_two = to_cells(truth_two)
    weight_of = (storm_codes.astype(jnp.float32) / 64.0).reshape(-1, 1, 1, 1)
    full_up, full_down, full_up_bias, full_down_bias = (up_weight, down_weight, up_bias, down_bias)

    def mlp_forward(inputs):
        gathered = lax.all_gather(inputs, "chan", axis=1, tiled=True)
        hidden = jnp.dot(
            gathered, full_up, preferred_element_type=jnp.float32
        ) + full_up_bias.astype(jnp.float32)
        active_full, gelu_pull = jax.vjp(exact_gelu, hidden)
        active = active_full.astype(jnp.bfloat16)
        product = jnp.dot(active, full_down, preferred_element_type=jnp.float32)
        output = lax.psum_scatter(
            product.astype(jnp.bfloat16), "chan", scatter_dimension=1, tiled=True
        ).astype(jnp.float32) + full_down_bias.astype(jnp.float32)
        return (output, (gathered, gelu_pull, active))

    def mlp_backward(gradient, saved):
        gathered, gelu_pull, active = saved
        grad_low = gradient.astype(jnp.bfloat16)
        grad_rows = lax.all_gather(grad_low, "chan", axis=1, tiled=True)
        down_bias_grad = jnp.sum(grad_low.astype(jnp.float32), axis=0)
        down_grad = jnp.dot(active.T, grad_rows, preferred_element_type=jnp.float32)
        active_grad = jnp.dot(grad_rows, full_down.T, preferred_element_type=jnp.float32)
        hidden_grad = gelu_pull(active_grad)[0].astype(jnp.bfloat16)
        up_grad = jnp.dot(gathered.T, hidden_grad, preferred_element_type=jnp.float32)
        up_bias_grad = jnp.sum(hidden_grad.astype(jnp.float32), axis=0)
        input_part = jnp.dot(hidden_grad, full_up.T, preferred_element_type=jnp.float32)
        input_grad = lax.psum_scatter(
            input_part.astype(jnp.bfloat16), "chan", scatter_dimension=1, tiled=True
        ).astype(jnp.float32)
        return (input_grad, (up_grad, up_bias_grad, down_grad, down_bias_grad))

    def forward_block(values):
        normed, first_saved = norm_forward(values, pre_gain, pre_shift)
        modal_in = column_layout(along_rows(normed, tables))
        filtered, core_pull = jax.vjp(
            spectral_core, modal_in, mix_weight_in, mix_bias_in, mix_weight_out, mix_bias_out
        )
        middle = rows_inverse(row_layout(filtered), tables) + normed + values
        entry, second_residuals = norm_forward(middle, post_gain, post_shift)
        output, mlp_saved = mlp_forward(entry.astype(jnp.bfloat16).reshape(total_rows, channels))
        return (
            output.reshape(values.shape) + middle,
            (first_saved, core_pull, second_residuals, mlp_saved),
        )

    def backward_block(gradient, saved):
        first_saved, core_pull, second_residuals, mlp_saved = saved
        mlp_grad, dense_grads = mlp_backward(gradient.reshape(total_rows, channels), mlp_saved)
        middle_part, post_gain_grad, post_shift_grad = norm_backward(
            mlp_grad.reshape(gradient.shape), post_gain, second_residuals
        )
        middle_grad = middle_part + gradient
        filter_grads = core_pull(column_layout(rows_inverse_back(middle_grad, tables)))
        normed_grad = along_rows_back(row_layout(filter_grads[0]), tables) + middle_grad
        input_part, pre_gain_grad, pre_shift_grad = norm_backward(
            normed_grad, pre_gain, first_saved
        )
        return (
            input_part + middle_grad,
            (pre_gain_grad, pre_shift_grad)
            + tuple(filter_grads[1:])
            + (post_gain_grad, post_shift_grad)
            + dense_grads,
        )

    first_out, first_saved_all = forward_block(start_cells)
    second_out, second_saved_all = forward_block(first_out)
    carried, grads_late = backward_block(weight_of * (second_out - target_two), second_saved_all)
    input_grad, grads_early = backward_block(
        weight_of * (first_out - target_one) + carried, first_saved_all
    )
    summed = jax.tree.map(jnp.add, grads_early, grads_late)
    (
        sum_pre_gain,
        sum_pre_shift,
        sum_mix_w_in,
        summed_mixing_bias_input,
        sum_mix_w_out,
        sum_mix_b_out,
        sum_post_gain,
        sum_post_shift,
        sum_up,
        sum_up_bias,
        sum_down,
        sum_down_bias,
    ) = summed
    totals = (
        lax.psum(sum_pre_gain.astype(jnp.bfloat16), "space").astype(jnp.float32),
        lax.psum(sum_pre_shift.astype(jnp.bfloat16), "space").astype(jnp.float32),
        lax.psum(sum_mix_w_in.astype(jnp.bfloat16), "space").astype(jnp.float32),
        lax.psum(summed_mixing_bias_input.astype(jnp.bfloat16), "space").astype(jnp.float32),
        lax.psum(sum_mix_w_out.astype(jnp.bfloat16), "space").astype(jnp.float32),
        lax.psum(sum_mix_b_out.astype(jnp.bfloat16), "space").astype(jnp.float32),
        lax.psum(sum_post_gain.astype(jnp.bfloat16), "space").astype(jnp.float32),
        lax.psum(sum_post_shift.astype(jnp.bfloat16), "space").astype(jnp.float32),
        lax.psum(sum_up.astype(jnp.bfloat16), "space").astype(jnp.float32),
        lax.psum(sum_up_bias.astype(jnp.bfloat16), "space").astype(jnp.float32),
        lax.psum(sum_down.astype(jnp.bfloat16), "space").astype(jnp.float32),
        lax.psum(sum_down_bias.astype(jnp.bfloat16), "space").astype(jnp.float32),
    )
    return (to_flat(first_out), to_flat(second_out), to_flat(input_grad)) + tuple(totals)


BF = jnp.bfloat16
F32 = jnp.float32
MESH_ID = pl.DeviceIdType.MESH
VMEM_BYTES = 66 * 1024 * 1024 - 1024 * 1024


def mm(a, b):
    return jnp.dot(a, b, preferred_element_type=F32)


def mm_nt(a, b):
    return lax.dot_general(a, b, (((1,), (1,)), ((), ())), preferred_element_type=F32)


def mm_tn(a, b):
    return lax.dot_general(a, b, (((0,), (0,)), ((), ())), preferred_element_type=F32)


def halves(v):
    high = v.astype(BF)
    return high, (v - high.astype(F32)).astype(BF)


def mm3(a, b):
    return mm(a[0], b[0]) + (mm(a[0], b[1]) + mm(a[1], b[0]))


def const_halves(table):
    table = np.asarray(table, np.float32)
    high = table.astype(ml_dtypes.bfloat16)
    low = (table - high.astype(np.float32)).astype(ml_dtypes.bfloat16)
    return jnp.asarray(high), jnp.asarray(low)


def row_constants(columns):
    half = columns // 2
    place = np.arange(columns)
    mode = np.arange(half)
    angle = 2.0 * np.pi * np.outer(mode, place) / columns
    real = np.cos(angle)
    imag = -np.sin(angle)
    imag[0] = np.cos(np.pi * place)
    forward = np.concatenate([real, imag]) / np.sqrt(columns)
    weight = np.where(mode == 0, 1.0, 2.0)
    inverse = (forward * np.concatenate([weight, weight])[:, None]).T
    return forward, inverse


def column_constants(height, rows, group):
    owners = height // rows
    angle = 2.0 * np.pi * np.outer(np.arange(height), np.arange(height)) / height
    cosine = np.cos(angle) / np.sqrt(height)
    sine = np.sin(angle) / np.sqrt(height)

    def spread(matrix):
        wide = np.zeros((group, height, owners, group, rows))
        for column in range(group):
            wide[column, :, :, column, :] = matrix.reshape(height, owners, rows)
        return wide.reshape(group * height, owners * group * rows)

    cosine, sine = spread(cosine), spread(sine)
    return np.block([[cosine, sine], [-sine, cosine]])


def signal_peers(axis, count, barrier):
    me = lax.axis_index(axis)
    for step in range(1, count):
        pl.semaphore_signal(
            barrier, inc=1, device_id={axis: lax.rem(me + step, count)}, device_id_type=MESH_ID
        )


def push(axis, count, step, source, target, send_sem, recv_sem):
    peer = lax.rem(lax.axis_index(axis) + step, count)
    return pltpu.make_async_remote_copy(
        src_ref=source,
        dst_ref=target,
        send_sem=send_sem.at[step],
        recv_sem=recv_sem.at[step],
        device_id={axis: peer},
        device_id_type=MESH_ID,
    )


def params(collective_id=None):
    return pltpu.CompilerParams(
        collective_id=collective_id,
        has_side_effects=collective_id is not None,
        vmem_limit_bytes=VMEM_BYTES,
    )


def launch(body, ins, outs, scratch, name, collective_id=None, in_specs=None, out_specs=None, grid=()):
    in_specs, out_specs = in_specs or {}, out_specs or {}
    names = list(ins) + list(outs) + list(scratch)
    whole = pl.BlockSpec(memory_space=pltpu.VMEM)
    results = pl.pallas_call(
        lambda *refs: body(types.SimpleNamespace(**dict(zip(names, refs)))),
        grid=grid,
        in_specs=[in_specs.get(key, whole) for key in ins],
        out_specs=[out_specs.get(key, whole) for key in outs],
        out_shape=[jax.ShapeDtypeStruct(*outs[key]) for key in outs],
        scratch_shapes=list(scratch.values()),
        compiler_params=params(collective_id),
        name=name,
    )(*ins.values())
    return dict(zip(outs, results))


IN_PLACE = pl.BlockSpec(memory_space=pl.ANY)


def sems(*counts):
    return pltpu.SemaphoreType.DMA(counts)


def run_copies(copies):
    for copy in copies:
        copy.start()
    for copy in copies:
        copy.wait()


def cells_from_lines(lines_ref, h, scratch_ref):
    features = scratch_ref.shape[1]
    per = 640 // W
    groups = features // per
    wide = jnp.concatenate(
        [lines_ref[h, pl.ds(part, groups, stride=5), :] for part in range(5)], axis=1
    )
    for part in range(per):
        piece = wide[:, part * W : (part + 1) * W]
        scratch_ref[0, pl.ds(part, groups, stride=per), :] = piece[:, :128]
        scratch_ref[1, pl.ds(part, groups, stride=per), :] = jnp.concatenate(
            [piece[:, 128:], jnp.zeros((groups, 256 - W), F32)], axis=1
        )
    return jnp.concatenate([scratch_ref[0], scratch_ref[1][:, : W - 128]], axis=1)


def enter(lines_ref, cells_ref, scratch_ref):
    def row(h, carry):
        cells_ref[h] = cells_from_lines(lines_ref, h, scratch_ref).T
        return carry

    lax.fori_loop(0, lines_ref.shape[0], row, 0)


def leave(cells_ref, lines_ref, scratch_ref):
    features = scratch_ref.shape[1]
    per = 640 // W
    groups = features // per

    def row(h, carry):
        block = cells_ref[h].T
        scratch_ref[0] = block[:, :128]
        scratch_ref[1] = jnp.concatenate([block[:, 128:], jnp.zeros((features, 256 - W), F32)], axis=1)
        wide = jnp.concatenate(
            [
                piece
                for part in range(per)
                for piece in (
                    scratch_ref[0, pl.ds(part, groups, stride=per), :],
                    scratch_ref[1, pl.ds(part, groups, stride=per), :][:, : W - 128],
                )
            ],
            axis=1,
        )
        for part in range(5):
            lines_ref[h, pl.ds(part, groups, stride=5), :] = wide[:, part * 128 : (part + 1) * 128]
        return carry

    lax.fori_loop(0, lines_ref.shape[0], row, 0)


def pack_lanes(flat_ref, place, real, imag):
    flat_ref[0, place, :] = real[:, :128]
    flat_ref[1, place, :] = imag[:, :128]
    flat_ref[2, place, :] = jnp.concatenate([real[:, 128:], imag[:, 128:]], axis=1)


def join_lanes(first, second, rest):
    real = jnp.concatenate([first, rest[:, :64]], axis=1)
    imag = jnp.concatenate([second, rest[:, 64:]], axis=1)
    return real, imag


def unpack_lanes(flat_ref, place):
    return join_lanes(flat_ref[0, place, :], flat_ref[1, place, :], flat_ref[2, place, :])


LEVEL = 32000.0


def encode_fixed(values):
    largest = jnp.max(jnp.abs(values), axis=1, keepdims=True)
    grade = jnp.ceil(jnp.log2(jnp.maximum(largest, 1e-30)) * 256.0 + 0.01)
    coded = jnp.round(values * (LEVEL * jnp.exp2(grade * (-1.0 / 256.0))))
    lines = [coded[k] for k in range(3)] + [grade[k] for k in range(3)] + [jnp.zeros((5, 128), F32)]
    return jnp.concatenate(lines, axis=0).astype(jnp.int32).astype(jnp.int16)


def decode_fixed(coded, thick):
    values = coded.astype(jnp.int32).astype(F32)
    scale = jnp.exp2(values[3 * thick : 3 * thick + 3] * (1.0 / 256.0)) * (1.0 / LEVEL)
    return [values[k * thick : (k + 1) * thick] * scale[k : k + 1] for k in range(3)]


def encode_plain(values):
    return jnp.concatenate([values[k] for k in range(3)], axis=0).astype(BF)


def decode_plain(coded, thick):
    values = coded.astype(F32)
    return [values[k * thick : (k + 1) * thick] for k in range(3)]


class Exchange:
    def __init__(self, fixed, spaces, thick, send_ref, recv_ref, send_sem, recv_sem):
        self.encode, self.decode = (encode_fixed, decode_fixed) if fixed else (encode_plain, decode_plain)
        self.spaces, self.thick = spaces, thick
        self.send_ref, self.recv_ref = send_ref, recv_ref
        self.send_sem, self.recv_sem = send_sem, recv_sem
        self.me = lax.axis_index("space")

    @staticmethod
    def shape(fixed, spaces, thick, pairs):
        return pltpu.VMEM((pairs, spaces, 3 * thick + (8 if fixed else 0), 128), jnp.int16 if fixed else BF)

    def copy(self, p, step):
        peer = lax.rem(self.me + step, self.spaces)
        return pltpu.make_async_remote_copy(
            src_ref=self.send_ref.at[p, peer],
            dst_ref=self.recv_ref.at[p, self.me],
            send_sem=self.send_sem.at[p, step],
            recv_sem=self.recv_sem.at[p, step],
            device_id={"space": peer},
            device_id_type=MESH_ID,
        )

    def send(self, p, flat_ref, start_of):
        for step in list(range(1, self.spaces)) + [0]:
            peer = lax.rem(self.me + step, self.spaces)
            rows = pl.ds(pl.multiple_of(start_of(peer), 8), self.thick)
            coded = self.encode(flat_ref[:, rows, :])
            if step:
                self.send_ref[p, peer] = coded
                self.copy(p, step).start()
            else:
                self.recv_ref[p, peer] = coded

    def arrive(self, p):
        for step in range(1, self.spaces):
            self.copy(p, step).wait_recv()

    def take(self, p, source):
        return self.decode(self.recv_ref[p, source], self.thick)

    def close(self, pairs):
        def pair(p, carry):
            for step in range(1, self.spaces):
                self.copy(p, step).wait_send()
            return carry

        lax.fori_loop(0, pairs, pair, 0)


def pair_inputs(q, exchange, even_ref):
    p = jnp.maximum(q - 1, 0)

    @pl.when(q != 1)
    def _():
        exchange.arrive(p)

    extra = (q == 0).astype(F32)
    zeroth = jnp.logical_and(exchange.me == 0, p == 0).astype(F32)
    parts = [join_lanes(*exchange.take(p, s)) for s in range(exchange.spaces)]
    real = jnp.concatenate([part[0] for part in parts], axis=0)
    imag = jnp.concatenate([part[1] for part in parts], axis=0)
    chosen = imag * (even_ref[...] * zeroth)
    real = real * (1.0 - extra) + chosen * extra
    imag = (imag - chosen) * (1.0 - extra)
    return p, zeroth, jnp.concatenate([real, imag], axis=0)


def pair_outputs(q, p, zeroth, result, exchange, even_ref, kept_ref, stage_ref):
    half = result.shape[0] // 2
    real, imag = result[:half], result[half:]

    @pl.when(q == 0)
    def _():
        kept_ref[...] = real

    @pl.when(q > 0)
    def _():
        chosen = even_ref[...] * zeroth
        pack_lanes(stage_ref, slice(None), real, imag * (1.0 - chosen) + kept_ref[...] * chosen)
        exchange.send(p, stage_ref, lambda peer: peer * exchange.thick)


def collect(exchange, pairs, chunk, flat_ref):
    def pair(p, carry):
        exchange.arrive(p)
        for s in range(exchange.spaces):
            rows = pl.ds(pl.multiple_of(s * chunk + p * exchange.thick, 8), exchange.thick)
            for k, part in enumerate(exchange.take(p, s)):
                flat_ref[k, rows, :] = part
        return carry

    lax.fori_loop(0, pairs, pair, 0)


def send_modes(exchange, pairs, chunk, flat_ref):
    def pair(p, carry):
        exchange.send(p, flat_ref, lambda peer: peer * chunk + p * exchange.thick)
        return carry

    lax.fori_loop(0, pairs, pair, 0)


class Plan:
    def __init__(self, rows, features, columns, spaces, chans, local):
        self.rows, self.features, self.columns = rows, features, columns
        self.spaces, self.chans, self.local = spaces, chans, local
        self.modes = columns // 2
        self.total = self.modes * rows
        self.chunk = self.total // spaces
        self.thick = 2 * rows
        self.half = self.thick * spaces
        self.pairs = self.chunk // self.thick
        self.cells = rows * columns // chans
        self.share = rows // chans
        self.width = features * chans
        self.tile = 256
        self.per = local // self.tile
        self.steps = chans * self.per
        self.size = features // 2
        self.small = 8 * self.size + 16
        self.field = ((rows, columns, features), F32)
        self.by_cells = ((chans, self.cells, features), BF)
        self.wide = ((self.cells, self.width), BF)
        self.tiles = ((self.steps, self.cells, self.tile), BF)
        self.lines = ((rows, features * columns // 128, 128), F32)
        self.dev = ((rows, columns, 8), F32)
        self.dev_wide = ((self.cells, 128), F32)
        self.kept = ((self.pairs + 1, 2 * self.half, features), BF)
        self.mix = ((2, 2, 2, features, features), BF)
        self.weights = ((2, chans, local, self.width), BF)
        self.rest = ((chans, 8, local), F32)
        self.sums = ((self.small, 128), F32)
        self.grads = ((2, self.steps, self.tile, self.width), BF)
        self.vectors = ((chans, 8, local), F32)

    def exchange_scratch(self, fixed_there, fixed_back):
        made = {}
        for name, fixed in (("1", fixed_there), ("2", fixed_back)):
            shape = Exchange.shape(fixed, self.spaces, self.thick, self.pairs)
            made["send" + name] = made["recv" + name] = shape
            made["s" + name] = made["r" + name] = sems(self.pairs, self.spaces)
        return made

    def spectral_scratch(self):
        return {
            "flat": pltpu.VMEM((3, self.total, 128), F32),
            "stage": pltpu.VMEM((3, self.half, 128), F32),
            "last": pltpu.VMEM((self.half, self.features), F32),
            "turn": pltpu.VMEM((2, self.features, 128), F32),
        }


def scratch_of(shaped):
    return pltpu.VMEM(*shaped)


def greet(plan):
    barrier = pltpu.get_barrier_semaphore()
    signal_peers("space", plan.spaces, barrier)
    signal_peers("chan", plan.chans, barrier)
    return lambda: pl.semaphore_wait(barrier, plan.spaces + plan.chans - 2)


def spread_chan(plan, source_ref, target_ref, send_sem, recv_sem):
    me = lax.axis_index("chan")
    copies = []
    for step in range(1, plan.chans):
        peer = lax.rem(me + step, plan.chans)
        copy = push("chan", plan.chans, step, source_ref.at[peer], target_ref.at[me], send_sem, recv_sem)
        copy.start()
        copies.append(copy)
    target_ref[me] = source_ref[me]
    return copies


def wait_all(copies):
    for copy in copies:
        copy.wait()


def rows_to_modes(plan, table, flat_ref, value_of, exact):
    def row(h, carry):
        value = value_of(h)
        out = mm3(table, halves(value)) if exact else mm(table, value.astype(BF))
        pack_lanes(flat_ref, pl.ds(h, plan.modes, stride=plan.rows), out[: plan.modes], out[plan.modes :])
        return carry

    lax.fori_loop(0, plan.rows, row, 0)


def filter_forward(plan, r, there, back, fine):
    half = plan.half

    def filter_pair(q, carry):
        p, zeroth, block = pair_inputs(q, there, r.even)
        spec = mm3((r.col[0], r.col[1]), halves(block))
        r.spec[q] = spec.astype(BF)
        parts = halves(spec)
        straight = mm3(parts, (r.mix[0, 0, 0], r.mix[0, 0, 1]))
        crossed = mm3(parts, (r.mix[0, 1, 0], r.mix[0, 1, 1]))
        first = jnp.concatenate(
            [
                jnp.maximum(straight[:half] - crossed[half:] + r.bias[0:1], 0.0),
                jnp.maximum(straight[half:] + crossed[:half] + r.bias[1:2], 0.0),
            ],
            axis=0,
        )
        r.first[q] = first.astype(BF)
        parts = halves(first)
        straight = mm3(parts, (r.mix[1, 0, 0], r.mix[1, 0, 1]))
        crossed = mm3(parts, (r.mix[1, 1, 0], r.mix[1, 1, 1]))
        second = jnp.concatenate(
            [
                straight[:half] - crossed[half:] + r.bias[2:3],
                straight[half:] + crossed[:half] + r.bias[3:4],
            ],
            axis=0,
        )
        second = second - jnp.clip(second, -SHRINK_LEVEL, SHRINK_LEVEL)
        r.second[q] = second.astype(BF)
        if fine:
            result = mm3((r.colinv[0], r.colinv[1]), halves(second))
        else:
            result = mm(r.colinv[0], second.astype(BF))
        pair_outputs(q, p, zeroth, result, back, r.even, r.last, r.stage)
        return carry

    lax.fori_loop(0, plan.pairs + 1, filter_pair, 0)


def modes_to_rows(plan, flat_ref, h):
    real, imag = unpack_lanes(flat_ref, pl.ds(h, plan.modes, stride=plan.rows))
    return jnp.concatenate([real, imag], axis=0)


def rows_of_chunks(plan, row, send_chunk):
    me = lax.axis_index("chan")
    for step in list(range(1, plan.chans)) + [0]:
        peer = lax.rem(me + step, plan.chans)

        def one(i, carry):
            row(peer * plan.share + i, peer, pl.ds(pl.multiple_of(i * plan.columns, 16), plan.columns))
            return carry

        lax.fori_loop(0, plan.share, one, 0)
        send_chunk(step, peer)


def rows_forward(plan, r, fine, unit_ref, x_ref, middle_ref):
    me = lax.axis_index("chan")
    gain, shift = r.gain[...].reshape(1, -1), r.shift[...].reshape(1, -1)
    copies = []

    def row(h, peer, place):
        block = modes_to_rows(plan, r.flat, h)
        if fine:
            out = mm3((r.rowinv[0], r.rowinv[1]), halves(block))
        else:
            out = mm(r.rowinv[0], block.astype(BF))
        middle = out + (unit_ref[h] * gain + shift) + x_ref[h]
        middle_ref[h] = middle
        r.own[peer, place, :] = middle.astype(BF)

    def send_chunk(step, peer):
        if step:
            copy = push("chan", plan.chans, step, r.own.at[peer], r.mid.at[me], r.s3, r.r3)
            copy.start()
            copies.append(copy)
        else:
            r.mid[me] = r.own[me]

    rows_of_chunks(plan, row, send_chunk)
    return copies


BLOCK = 80


def by_blocks(plan, step):
    def one(i, carry):
        step(pl.ds(pl.multiple_of(i * BLOCK, 16), BLOCK))
        return carry

    lax.fori_loop(0, plan.cells // BLOCK, one, 0)


def joined(chunks_ref, place):
    return jnp.concatenate([chunks_ref[j, place, :].astype(F32) for j in range(chunks_ref.shape[0])], axis=1)


def full_vector(gathered_ref, start, size):
    chans = gathered_ref.shape[0]
    return jnp.concatenate([gathered_ref[j, 1:2, start : start + size] for j in range(chans)], axis=1)


def moments(value):
    mean = jnp.mean(value, axis=1, keepdims=True)
    centred = value - mean
    return mean, centred, lax.rsqrt(jnp.mean(centred * centred, axis=1, keepdims=True) + NORM_EPS)


ERF = (0.254829592, -0.284496736, 1.421413741, -1.453152027, 1.061405429)


def gelu_and_slope(v):
    e = jnp.exp2(v * v * (-0.5 / math.log(2.0)))
    below = 1.0 + (0.3275911 * math.sqrt(0.5)) * jnp.abs(v)
    t = pl.reciprocal(below, approx=True)
    t = t * (2.0 - below * t)
    c = [0.5 * k for k in ERF]
    tail = (e * t) * (c[0] + t * (c[1] + t * (c[2] + t * (c[3] + t * c[4]))))
    below = jnp.where(v >= 0.0, 1.0 - tail, tail)
    active = v * below
    return active, below + (v * (1.0 / math.sqrt(2.0 * math.pi))) * e


def three_parts(v):
    a = v.astype(BF)
    rest = v - a.astype(F32)
    b = rest.astype(BF)
    return [a, b, (rest - b.astype(F32)).astype(BF)]


def tile_of(plan, t):
    return t // plan.per, pl.ds(pl.multiple_of((t % plan.per) * plan.tile, plan.tile), plan.tile)


def up_tile(plan, r, t):
    j, place = tile_of(plan, t)
    return r.w[0, j, :, place]


def down_tile(plan, r, t):
    j, place = tile_of(plan, t)
    return r.w[1, j, place, :]


def ffn_scratch(plan):
    shape = (plan.cells, plan.tile)
    made = {key: pltpu.VMEM(shape, F32) for key in ("wide_a", "wide_b")}
    made.update({key: pltpu.VMEM(shape, BF) for key in ("thin_a", "thin_b")})
    made.update(
        total=pltpu.VMEM((plan.cells, plan.width), F32),
        entry=scratch_of(plan.wide),
        unit_wide=scratch_of(plan.wide),
        dev_wide=scratch_of(plan.dev_wide),
        active=scratch_of(plan.tiles),
        slope=scratch_of(plan.tiles),
        gathered=scratch_of(plan.vectors),
    )
    return made


def staggered(plan, r, lead, turn, trail):
    last = plan.steps - 1
    r.thin_b[...] = jnp.zeros_like(r.thin_b)
    r.wide_a[...] = lead(0)

    def pair(u, carry):
        t = 2 * u
        r.wide_b[...] = lead(t + 1)
        trail(r.thin_b[...], jnp.maximum(t - 1, 0))
        r.thin_a[...] = turn(r.wide_a[...], t)
        r.wide_a[...] = lead(jnp.minimum(t + 2, last))
        trail(r.thin_a[...], t)
        r.thin_b[...] = turn(r.wide_b[...], t + 1)
        return carry

    lax.fori_loop(0, plan.steps // 2, pair, 0)
    trail(r.thin_b[...], last)


def ffn_forward(plan, r):
    gain = full_vector(r.gathered, 0, plan.features)
    shift = full_vector(r.gathered, plan.features, plan.features)
    bias = full_vector(r.gathered, 2 * plan.features, plan.features)

    def prepare(place):
        mean, centred, inverse = moments(joined(r.mid, place))
        unit = centred * inverse
        r.unit_wide[place, :] = unit.astype(BF)
        r.dev_wide[place, :] = jnp.broadcast_to(inverse, (BLOCK, 128))
        r.entry[place, :] = (unit * gain + shift).astype(BF)
        r.total[place, :] = jnp.broadcast_to(bias, (BLOCK, plan.width))

    by_blocks(plan, prepare)

    def lead(t):
        j, place = tile_of(plan, t)
        return mm(r.entry[...], up_tile(plan, r, t)) + r.gathered[j, 0:1, place]

    def turn(value, t):
        active, slope = gelu_and_slope(value)
        active = active.astype(BF)
        r.active[t] = active
        r.slope[t] = slope.astype(BF)
        return active

    def trail(active, t):
        r.total[...] += mm(active, down_tile(plan, r, t))

    staggered(plan, r, lead, turn, trail)


def ffn_backward(plan, r):
    r.small[...] = jnp.zeros_like(r.small)
    r.total[...] = jnp.zeros_like(r.total)

    def lead(t):
        return mm_nt(r.upper[...], down_tile(plan, r, t))

    def turn(value, t):
        lower = value * r.slope[t].astype(F32)
        r.upb[pl.ds(t, 1), :] = jnp.sum(lower, axis=0, keepdims=True)
        lower = lower.astype(BF)
        r.slope[t] = lower
        return lower

    def trail(lower, t):
        r.total[...] += mm_nt(lower, up_tile(plan, r, t))

    staggered(plan, r, lead, turn, trail)
    gain = full_vector(r.gathered, 0, plan.features)

    def finish(place):
        grad = r.total[place, :]
        unit = r.unit_wide[place, :].astype(F32)
        r.small[0:1, :] += jnp.sum(grad * unit, axis=0, keepdims=True)
        r.small[1:2, :] += jnp.sum(grad, axis=0, keepdims=True)
        r.small[2:3, :] += jnp.sum(r.upper[place, :].astype(F32), axis=0, keepdims=True)
        scaled = grad * gain
        one = jnp.mean(scaled, axis=1, keepdims=True)
        two = jnp.mean(scaled * unit, axis=1, keepdims=True)
        result = r.dev_wide[place, :][:, :1] * (scaled - one - unit * two)
        for j in range(plan.chans):
            r.leaving[j, place, :] = result[:, j * plan.features : (j + 1) * plan.features].astype(BF)

    by_blocks(plan, finish)


def vector_gradients(plan, r, rest_ref):
    rest_ref[...] = jnp.zeros_like(rest_ref)
    for j in range(plan.chans):
        for k in range(plan.per):
            line = j * plan.per + k
            rest_ref[j, 0:1, k * plan.tile : (k + 1) * plan.tile] = r.upb[line : line + 1, :]
        for k in range(3):
            rest_ref[j, 1 + k : 2 + k, 0 : plan.features] = r.small[
                k : k + 1, j * plan.features : (j + 1) * plan.features
            ]


def weight_gradients(r, t):
    return mm_tn(r.active[t], r.upper[...]), mm_tn(r.slope[t], r.entry[...])


def filter_backward(plan, r, there, back):
    half = plan.half
    r.mixgrad[...] = jnp.zeros_like(r.mixgrad)
    r.biasgrad[...] = jnp.zeros_like(r.biasgrad)

    def turned(v):
        return jnp.concatenate([v[half:], -v[:half]], axis=0)

    def note_bias(index, value):
        r.biasgrad[index : index + 1, :] += jnp.sum(value, axis=0, keepdims=True)

    def through(low, layer):
        straight = mm_nt(low, r.mix[layer, 0, 0])
        crossed = mm_nt(low, r.mix[layer, 1, 0])
        return jnp.concatenate([straight[:half] + crossed[half:], straight[half:] - crossed[:half]], axis=0)

    def filter_pair(q, carry):
        p, zeroth, block = pair_inputs(q, there, r.even)
        grad = mm(r.col[0], block.astype(BF))
        grad = jnp.where(r.second[q].astype(F32) == 0.0, 0.0, grad)
        note_bias(2, grad[:half])
        note_bias(3, grad[half:])
        low = grad.astype(BF)
        first = r.first[q]
        r.mixgrad[1, 0] += mm_tn(first, low)
        r.mixgrad[1, 1] += mm_tn(first, turned(grad).astype(BF))
        grad = jnp.where(first.astype(F32) > 0.0, through(low, 1), 0.0)
        note_bias(0, grad[:half])
        note_bias(1, grad[half:])
        low = grad.astype(BF)
        spec = r.spec[q]
        r.mixgrad[0, 0] += mm_tn(spec, low)
        r.mixgrad[0, 1] += mm_tn(spec, turned(grad).astype(BF))
        result = mm(r.colinv[0], through(low, 0).astype(BF))
        pair_outputs(q, p, zeroth, result, back, r.even, r.last, r.stage)
        return carry

    lax.fori_loop(0, plan.pairs + 1, filter_pair, 0)


def mix_gradients(plan, r, before_ref):
    size = plan.size
    for layer in range(2):
        for part in range(2):
            for block in range(2):
                own = slice(block * size, (block + 1) * size)
                piece = r.mixgrad[layer, part][own, own]
                piece = jnp.concatenate([piece, jnp.zeros((size, 128 - size), F32)], axis=1)
                start = ((layer * 2 + part) * 2 + block) * size
                place = slice(start, start + size)
                r.sums[place, :] = piece if before_ref is None else piece + before_ref[place, :]


def rows_backward(plan, r, unit_ref, before_ref):
    gain = r.gain[...].reshape(1, -1)
    me = lax.axis_index("chan")
    lane = lax.broadcasted_iota(jnp.int32, (plan.columns, 128), 1)

    def row(h, carry):
        table, one_sum, two_sum = carry
        block = modes_to_rows(plan, r.flat, h)
        grad = mm(r.row_t[...], block.astype(BF)) + r.out[h]
        unit = unit_ref[h]
        one_sum += jnp.sum(grad * unit, axis=0, keepdims=True)
        two_sum += jnp.sum(grad, axis=0, keepdims=True)
        scaled = grad * gain
        r.scaled[h] = scaled
        one = jnp.sum(scaled, axis=1, keepdims=True)
        two = jnp.sum(scaled * unit, axis=1, keepdims=True)
        table = jnp.where(lane == h, one, table)
        return jnp.where(lane == plan.rows + h, two, table), one_sum, two_sum

    none = jnp.zeros((1, plan.features), F32)
    table, one_sum, two_sum = lax.fori_loop(
        0, plan.rows, row, (jnp.zeros((plan.columns, 128), F32), none, none)
    )
    table = table.T[: 2 * plan.rows]
    r.mine[...] = table
    r.all[me] = table
    copies = [
        push("chan", plan.chans, step, r.mine, r.all.at[me], r.s4, r.r4) for step in range(1, plan.chans)
    ]
    for copy in copies:
        copy.start()
    vectors = jnp.concatenate([r.biasgrad[0:4], one_sum, two_sum, none, none], axis=0)
    wide = jnp.concatenate([vectors, jnp.zeros((8, 256 - plan.features), F32)], axis=1)
    wide = jnp.concatenate([wide[:, :128], wide[:, 128:]], axis=0)
    place = slice(8 * plan.size, plan.small)
    r.sums[place, :] = wide if before_ref is None else wide + before_ref[place, :]
    return copies


def input_gradient(plan, r, unit_ref, dev_ref):
    lane = lax.broadcasted_iota(jnp.int32, (plan.columns, 128), 1)
    means = sum(r.all[j] for j in range(plan.chans)) * (1.0 / plan.width)
    padding = jnp.zeros((128 - 2 * plan.rows, plan.columns), F32)
    means = jnp.concatenate([means, padding], axis=0).T

    def result(h):
        one = jnp.sum(jnp.where(lane == h, means, 0.0), axis=1, keepdims=True)
        two = jnp.sum(jnp.where(lane == plan.rows + h, means, 0.0), axis=1, keepdims=True)
        return r.out[h] + dev_ref[h][:, :1] * (r.scaled[h] - one - unit_ref[h] * two)

    return result


def norm_sums_scratch(plan):
    return {
        "scaled": scratch_of(plan.field),
        "mixgrad": pltpu.VMEM((2, 2, plan.features, plan.features), F32),
        "biasgrad": pltpu.VMEM((8, plan.features), F32),
        "mine": pltpu.VMEM((2 * plan.rows, plan.columns), F32),
        "all": pltpu.VMEM((plan.chans, 2 * plan.rows, plan.columns), F32),
        "s4": sems(plan.chans),
        "r4": sems(plan.chans),
    }


class Moves:
    def __init__(self, sem):
        self.sem, self.count, self.open = sem, 0, []

    def start(self, source, target):
        copy = pltpu.make_async_copy(source, target, self.sem.at[self.count])
        self.count += 1
        copy.start()
        self.open.append(copy)
        return copy

    def close(self):
        wait_all(self.open)


def launch_first(plan, args, tables):
    rows, features, chans = plan.rows, plan.features, plan.chans

    def body(r):
        me = lax.axis_index("chan")
        place = lax.axis_index("space")
        core = lax.rem(place, 2)
        sibling = place + 1 - 2 * core
        met = greet(plan)
        moves = Moves(r.dma)
        moves.start(r.up, r.w.at[0, me])
        moves.start(r.down, r.w.at[1, me])
        loaded = moves.start(r.lines_t, r.lines_in)
        own_weights = moves.open[:2]
        moves.open = []

        def spread(kind, source):
            return [
                push("chan", chans, step, source, r.w.at[kind, me], r.s5, r.r5) for step in range(1, chans)
            ]

        def row_of(ref):
            return ref[...].reshape(1, -1).astype(F32)

        r.vectors[...] = jnp.zeros_like(r.vectors)
        r.vectors[0:1, :] = row_of(r.upb)
        r.vectors[1:2, 0:features] = row_of(r.post_gain)
        r.vectors[1:2, features : 2 * features] = row_of(r.post_shift)
        r.vectors[1:2, 2 * features : 3 * features] = row_of(r.downb)
        r.gathered[me] = r.vectors[...]
        met()
        given = [push("chan", chans, step, r.vectors, r.gathered.at[me], r.s6, r.r6) for step in range(1, chans)]
        for copy in given:
            copy.start()
        for layer, (source, bias) in enumerate(((r.mix_in, r.bias_in), (r.mix_out, r.bias_out))):
            for part in range(2):
                zero = jnp.zeros((plan.size, plan.size), F32)
                value = jnp.concatenate(
                    [
                        jnp.concatenate([source[part, 0], zero], axis=1),
                        jnp.concatenate([zero, source[part, 1]], axis=1),
                    ],
                    axis=0,
                )
                high, low = halves(value)
                r.mix[layer, part, 0] = high
                r.mix[layer, part, 1] = low
                line = 2 * layer + part
                r.bias[line : line + 1, :] = jnp.concatenate([bias[part, 0:1, :], bias[part, 1:2, :]], axis=1)
        moves.start(r.mix, r.mix_kept)

        def first(h, carry):
            block = cells_from_lines(r.lines_x, h, r.turn)
            r.turned[h] = block
            total = jnp.sum(block, axis=0, keepdims=True)
            centred = block - total * (1.0 / features)
            r.mine[pl.ds(h, 1), :] = total
            r.mine[pl.ds(rows + h, 1), :] = jnp.sum(centred * centred, axis=0, keepdims=True)
            return carry

        lax.fori_loop(0, rows, first, 0)
        r.all[me] = r.mine[...]
        run_copies([push("chan", chans, step, r.mine, r.all.at[me], r.s4, r.r4) for step in range(1, chans)])
        for kind, source in enumerate((r.up, r.down)):

            @pl.when(core == kind)
            def _():
                for copy in spread(kind, source):
                    copy.start()

        totals = [r.all[j] for j in range(chans)]
        mean = sum(t[:rows] for t in totals) * (1.0 / plan.width)
        spread_sum = sum(
            t[rows:] + features * jnp.square(t[:rows] * (1.0 / features) - mean) for t in totals
        ) * (1.0 / plan.width)
        r.mine[pl.ds(0, rows), :] = mean
        r.mine[pl.ds(rows, rows), :] = lax.rsqrt(spread_sum + NORM_EPS)
        gain, shift = r.gain[...].reshape(1, -1), r.shift[...].reshape(1, -1)

        def normed(h):
            block = r.turned[h]
            inverse = r.mine[pl.ds(rows + h, 1), :]
            r.x[h] = block.T
            unit = ((block - r.mine[pl.ds(h, 1), :]) * inverse).T
            r.unit[h] = unit
            r.dev[h] = jnp.broadcast_to(inverse, (8, plan.columns)).T
            return unit * gain + shift

        there = Exchange(True, plan.spaces, plan.thick, r.send1, r.recv1, r.s1, r.r1)
        back = Exchange(True, plan.spaces, plan.thick, r.send2, r.recv2, r.s2, r.r2)
        rows_to_modes(plan, (r.row[0], r.row[1]), r.flat, normed, True)
        send_modes(there, plan.pairs, plan.chunk, r.flat)
        moves.start(r.unit, r.unit_kept)
        moves.start(r.dev, r.dev_kept)
        loaded.wait()
        enter(r.lines_in, r.cells_t, r.turn)
        moves.start(r.cells_t, r.cells_kept)
        filter_forward(plan, r, there, back, True)
        for source, target in ((r.spec, r.spec_kept), (r.first, r.first_kept), (r.second, r.second_kept)):
            moves.start(source, target)
        collect(back, plan.pairs, plan.chunk, r.flat)
        copies = rows_forward(plan, r, True, r.unit, r.x, r.middle)
        moves.start(r.middle, r.middle_kept)
        passed = []
        for step in range(1, chans):
            push("chan", chans, step, r.up, r.w.at[core, me], r.s5, r.r5).wait()
            sender = lax.rem(me - step + chans, chans)
            copy = pltpu.make_async_remote_copy(
                src_ref=r.w.at[core, sender],
                dst_ref=r.w.at[core, sender],
                send_sem=r.s7.at[step],
                recv_sem=r.r7.at[step],
                device_id={"space": sibling},
                device_id_type=MESH_ID,
            )
            copy.start()
            passed.append(copy)
        wait_all(copies + given + passed)
        wait_all(own_weights)
        moves.start(r.w, r.w_kept)
        ffn_forward(plan, r)
        saved = ("active", "slope", "entry", "unit_wide", "dev_wide", "gathered")
        for key in saved:
            moves.start(getattr(r, key), getattr(r, key + "_kept"))

        def last(block):
            outer = r.total[block, :]
            mean, _, inverse = moments(outer + joined(r.mid, block))
            stats = three_parts(mean) + three_parts(inverse)
            stats = jnp.concatenate(stats + [jnp.zeros((BLOCK, 256 - features - 6), BF)], axis=1)
            for j in range(chans):
                r.leaving[j, block, :] = jnp.concatenate(
                    [outer[:, j * features : (j + 1) * features].astype(BF), stats], axis=1
                )

        by_blocks(plan, last)
        wait_all(spread_chan(plan, r.leaving, r.home, r.s8, r.r8))
        there.close(plan.pairs)
        back.close(plan.pairs)
        moves.close()

    home = ((chans, plan.cells, 256), BF)
    outs = {
        "home": home,
        "middle_kept": plan.field,
        "unit_kept": plan.field,
        "dev_kept": plan.dev,
        "cells_kept": plan.field,
        "spec_kept": plan.kept,
        "first_kept": plan.kept,
        "second_kept": plan.kept,
        "mix_kept": plan.mix,
        "w_kept": plan.weights,
        "active_kept": plan.tiles,
        "slope_kept": plan.tiles,
        "entry_kept": plan.wide,
        "unit_wide_kept": plan.wide,
        "dev_wide_kept": plan.dev_wide,
        "gathered_kept": plan.vectors,
        "bias": ((8, features), F32),
    }
    ins = dict(args)
    ins.update({key: tables[key] for key in ("row", "rowinv", "col", "colinv", "even")})
    scratch = {
        "dma": sems(20),
        "x": scratch_of(plan.field),
        "unit": scratch_of(plan.field),
        "dev": scratch_of(plan.dev),
        "middle": scratch_of(plan.field),
        "cells_t": scratch_of(plan.field),
        "lines_in": scratch_of(plan.lines),
        "turned": pltpu.VMEM((rows, features, plan.columns), F32),
        "mine": pltpu.VMEM((2 * rows, plan.columns), F32),
        "all": pltpu.VMEM((chans, 2 * rows, plan.columns), F32),
        "spec": scratch_of(plan.kept),
        "first": scratch_of(plan.kept),
        "second": scratch_of(plan.kept),
        "mix": scratch_of(plan.mix),
        "w": scratch_of(plan.weights),
        "vectors": pltpu.VMEM((8, plan.local), F32),
        "own": scratch_of(plan.by_cells),
        "mid": scratch_of(plan.by_cells),
        "leaving": scratch_of(home),
        **plan.exchange_scratch(True, True),
        **plan.spectral_scratch(),
        **ffn_scratch(plan),
        **{key + str(k): sems(chans) for k in range(3, 9) for key in ("s", "r")},
    }
    in_place = ("up", "down", "lines_t")
    return launch(
        body,
        ins,
        outs,
        scratch,
        "first_forward",
        0,
        {key: IN_PLACE for key in in_place},
        {key: IN_PLACE for key in outs if key.endswith("_kept")},
    )


def launch_second(plan, args, one, tables):
    rows, features, chans = plan.rows, plan.features, plan.chans

    def body(r):
        me = lax.axis_index("chan")
        met = greet(plan)
        moves = Moves(r.dma)
        loaded = moves.start(r.lines_t, r.lines_in)
        weights = moves.start(r.w_kept, r.w)
        vectors = moves.start(r.gathered_kept, r.gathered)
        earlier = moves.start(r.cells_kept, r.cells_one)
        moves.open = []
        gain, shift = r.gain[...].reshape(1, -1), r.shift[...].reshape(1, -1)
        weight = r.codes[0].astype(F32) * (1.0 / 64.0)

        def normed(h):
            home = r.home[h].astype(F32)
            x = home[:, :features] + r.before[h]
            parts = [home[:, features + k : features + k + 1] for k in range(6)]
            mean = parts[0] + (parts[1] + parts[2])
            dev = parts[3] + (parts[4] + parts[5])
            unit = (x - mean) * dev
            r.x[h] = x
            r.unit[h] = unit
            r.dev[h] = jnp.broadcast_to(dev, (plan.columns, 8))
            return unit * gain + shift

        rows_to_modes(plan, (r.row[0], r.row[1]), r.flat, normed, True)
        met()
        there = Exchange(True, plan.spaces, plan.thick, r.send1, r.recv1, r.s1, r.r1)
        back = Exchange(False, plan.spaces, plan.thick, r.send2, r.recv2, r.s2, r.r2)
        send_modes(there, plan.pairs, plan.chunk, r.flat)
        loaded.wait()
        enter(r.lines_in, r.cells_t, r.turn)

        def low_target(h, peer, place):
            r.own[peer, place, :] = r.cells_t[h].astype(BF)

        targets = []

        def send_target(step, peer):
            if step:
                copy = push("chan", chans, step, r.own.at[peer], r.target.at[me], r.s5, r.r5)
                copy.start()
                targets.append(copy)
            else:
                r.target[me] = r.own[me]

        rows_of_chunks(plan, low_target, send_target)
        filter_forward(plan, r, there, back, False)
        collect(back, plan.pairs, plan.chunk, r.flat)
        there.close(plan.pairs)
        back.close(plan.pairs)
        wait_all(targets)
        copies = rows_forward(plan, r, False, r.unit, r.x, r.before)
        weights.wait()
        vectors.wait()
        wait_all(copies)
        ffn_forward(plan, r)

        def errors(block):
            outer = r.total[block, :]
            error = outer + joined(r.mid, block) - joined(r.target, block)
            r.upper[block, :] = (weight * error).astype(BF)
            for j in range(chans):
                r.leaving[j, block, :] = outer[:, j * features : (j + 1) * features].astype(BF)

        by_blocks(plan, errors)
        copies = spread_chan(plan, r.leaving, r.landed, r.s6, r.r6)
        for copy in copies:
            copy.wait_send()
        ffn_backward(plan, r)
        for copy in copies:
            copy.wait_recv()
        copies = spread_chan(plan, r.leaving, r.own, r.s7, r.r7)

        def grads(u, carry):
            for slot in range(2):
                t = 2 * u + slot
                stores = [
                    pltpu.make_async_copy(r.grad.at[slot, k], r.grads_kept.at[k, t], r.dma2.at[slot, k])
                    for k in range(2)
                ]

                @pl.when(u > 0)
                def _():
                    wait_all(stores)

                for k, value in enumerate(weight_gradients(r, t)):
                    r.grad[slot, k] = value.astype(BF)
                    stores[k].start()
            return carry

        lax.fori_loop(0, plan.steps // 2, grads, 0)
        vector_gradients(plan, r, r.rest)
        wait_all(copies)

        def middle_grad(h):
            quarter = h // plan.share
            place = pl.ds(pl.multiple_of((h % plan.share) * plan.columns, 16), plan.columns)
            x = r.landed[quarter, place, :].astype(F32) + r.before[h]
            r.before[h] = x
            grad = weight * (x - r.cells_t[h]) + r.own[quarter, place, :].astype(F32)
            r.out[h] = grad
            return grad

        rows_to_modes(plan, r.rowinv_t[...], r.flat, middle_grad, False)
        there = Exchange(False, plan.spaces, plan.thick, r.send3, r.recv3, r.s3_, r.r3_)
        back = Exchange(False, plan.spaces, plan.thick, r.send2, r.recv2, r.s2, r.r2)
        send_modes(there, plan.pairs, plan.chunk, r.flat)
        moves.start(r.before, r.second_x)
        leave(r.x, r.lines, r.turn)
        filter_backward(plan, r, there, back)
        mix_gradients(plan, r, None)
        collect(back, plan.pairs, plan.chunk, r.flat)
        copies = rows_backward(plan, r, r.unit, None)
        earlier.wait()
        wait_all(copies)
        result = input_gradient(plan, r, r.unit, r.dev)
        copies = []

        def row(h, peer, place):
            grad = weight * (r.x[h] - r.cells_one[h]) + result(h)
            r.out[h] = grad
            r.own[peer, place, :] = grad.astype(BF)

        def send_chunk(step, peer):
            if step:
                copy = push("chan", chans, step, r.own.at[peer], r.came.at[me], r.s8, r.r8)
                copy.start()
                copies.append(copy)
            else:
                r.came[me] = r.own[me]

        rows_of_chunks(plan, row, send_chunk)
        for slot in range(2):
            for k in range(2):
                pltpu.make_async_copy(
                    r.grad.at[slot, k], r.grads_kept.at[k, plan.steps - 2 + slot], r.dma2.at[slot, k]
                ).wait()
        wait_all(copies)
        there.close(plan.pairs)
        back.close(plan.pairs)
        moves.close()

    ins = {
        "home": one["home"].reshape(rows, plan.columns, 256),
        "before": one["middle_kept"],
        "w_kept": one["w_kept"],
        "gathered_kept": one["gathered_kept"],
        "cells_kept": one["cells_kept"],
        "mix": one["mix_kept"],
        "bias": one["bias"],
        **args,
    }
    ins.update({key: tables[key] for key in ("row", "rowinv", "rowinv_t", "row_t", "col", "colinv", "even")})
    outs = {
        "out": plan.field,
        "came": plan.by_cells,
        "lines": plan.lines,
        "second_x": plan.field,
        "sums": plan.sums,
        "rest": plan.rest,
        "grads_kept": plan.grads,
    }
    exchange = Exchange.shape(False, plan.spaces, plan.thick, plan.pairs)
    scratch = {
        "dma": sems(8),
        "dma2": sems(2, 2),
        "x": scratch_of(plan.field),
        "unit": scratch_of(plan.field),
        "dev": scratch_of(plan.dev),
        "cells_t": scratch_of(plan.field),
        "cells_one": scratch_of(plan.field),
        "lines_in": scratch_of(plan.lines),
        "spec": scratch_of(plan.kept),
        "first": scratch_of(plan.kept),
        "second": scratch_of(plan.kept),
        "w": scratch_of(plan.weights),
        "own": scratch_of(plan.by_cells),
        "mid": scratch_of(plan.by_cells),
        "target": scratch_of(plan.by_cells),
        "leaving": scratch_of(plan.by_cells),
        "landed": scratch_of(plan.by_cells),
        "upper": scratch_of(plan.wide),
        "small": pltpu.VMEM((8, plan.width), F32),
        "upb": pltpu.VMEM((16, plan.tile), F32),
        "grad": pltpu.VMEM((2, 2, plan.tile, plan.width), BF),
        "send3": exchange,
        "recv3": exchange,
        "s3_": sems(plan.pairs, plan.spaces),
        "r3_": sems(plan.pairs, plan.spaces),
        **plan.exchange_scratch(True, False),
        **plan.spectral_scratch(),
        **ffn_scratch(plan),
        **norm_sums_scratch(plan),
        **{key + str(k): sems(chans) for k in (3, 5, 6, 7, 8) for key in ("s", "r")},
    }
    in_specs = {key: IN_PLACE for key in ("w_kept", "gathered_kept", "cells_kept", "lines_t")}
    in_specs["codes"] = pl.BlockSpec(memory_space=pltpu.SMEM)
    return launch(
        body,
        ins,
        outs,
        scratch,
        "second_step",
        1,
        in_specs,
        {key: IN_PLACE for key in ("second_x", "grads_kept")},
    )


def launch_third(plan, args, one, two, tables):
    rows, features, chans, spaces = plan.rows, plan.features, plan.chans, plan.spaces
    local, width = plan.local, plan.width
    levels = spaces // 2
    piece = local // levels
    small = plan.small
    part = -(-(small + 32) // (16 * levels)) * 16

    def body(r):
        me = lax.axis_index("chan")
        place = lax.axis_index("space")
        core = lax.rem(place, 2)
        level = place // 2
        sibling = place + 1 - 2 * core
        others = [lax.rem(level + step, levels) for step in range(1, levels)]
        met = greet(plan)
        moves = Moves(r.dma)
        gradient = moves.start(r.g, r.out)
        early = [
            moves.start(source, target)
            for source, target in (
                (r.w_kept, r.w),
                (r.slope_kept, r.slope),
                (r.unit_wide_kept, r.unit_wide),
                (r.dev_wide_kept, r.dev_wide),
                (r.gathered_kept, r.gathered),
            )
        ]
        middle = [moves.start(r.active_kept, r.active), moves.start(r.entry_kept, r.entry)]
        late = [
            moves.start(source, target)
            for source, target in (
                (r.spec_kept, r.spec),
                (r.first_kept, r.first),
                (r.second_kept, r.second),
                (r.unit_kept, r.unit),
                (r.dev_kept, r.dev),
                (r.second_x, r.scaled),
            )
        ]
        moves.open = []

        def upper(block):
            r.upper[block, :] = joined(r.came, block).astype(BF)

        by_blocks(plan, upper)
        wait_all(early)
        ffn_backward(plan, r)
        met()
        copies = spread_chan(plan, r.leaving, r.own, r.s7, r.r7)
        vector_gradients(plan, r, r.rest)
        r.rest[...] += r.rest_before[...]
        vectors = [
            push("chan", chans, step, r.rest.at[lax.rem(me + step, chans)], r.rest_land.at[me], r.s6, r.r6)
            for step in range(1, chans)
        ]
        for copy in vectors:
            copy.start()
        r.rest_land[me] = r.rest[me]
        wait_all(middle)

        def order(i):
            return lax.rem((me + 1) * plan.per + i, plan.steps)

        def fetch(i, k):
            return pltpu.make_async_copy(r.grads_kept.at[k, order(i)], r.prev.at[i % 2, k], r.dma2.at[i % 2, k])

        def swap(i):
            return pltpu.make_async_remote_copy(
                src_ref=r.give.at[i % 2],
                dst_ref=r.take.at[i % 3],
                send_sem=r.s9.at[i],
                recv_sem=r.r9.at[i],
                device_id={"space": sibling},
                device_id_type=MESH_ID,
            )

        def ship(i):
            step = 1 + i // plan.per
            return pltpu.make_async_remote_copy(
                src_ref=r.keep.at[i],
                dst_ref=r.land.at[step - 1, i % plan.per],
                send_sem=r.s10.at[i],
                recv_sem=r.r10.at[i],
                device_id={"chan": lax.rem(me + step, chans)},
                device_id_type=MESH_ID,
            )

        for k in range(2):
            fetch(0, k).start()

        def settle(i):
            swap(i).wait()
            r.keep[i] = (r.keep[i].astype(F32) + r.take[i % 3].astype(F32)).astype(BF)

        def block(i, carry):
            for k in range(2):
                fetch(i, k).wait()

            @pl.when(i + 1 < plan.steps)
            def _():
                for k in range(2):
                    fetch(i + 1, k).start()

            values = [
                (value + r.prev[i % 2, k].astype(F32)).astype(BF)
                for k, value in enumerate(weight_gradients(r, order(i)))
            ]

            @pl.when(i > 0)
            def _():
                settle(i - 1)

                @pl.when(i - 1 < plan.steps - plan.per)
                def _():
                    ship(i - 1).start()

            for kind in range(2):

                @pl.when(core == kind)
                def _():
                    r.keep[i] = values[kind]
                    r.give[i % 2] = values[1 - kind]

            swap(i).start()
            return carry

        lax.fori_loop(0, plan.steps, block, 0)
        settle(plan.steps - 1)
        wait_all(copies)
        wait_all(late)
        gradient.wait()

        def middle_grad(h):
            quarter = h // plan.share
            rows_here = pl.ds(pl.multiple_of((h % plan.share) * plan.columns, 16), plan.columns)
            grad = r.out[h] + r.own[quarter, rows_here, :].astype(F32)
            r.out[h] = grad
            return grad

        rows_to_modes(plan, r.rowinv_t[...], r.flat, middle_grad, False)
        there = Exchange(False, spaces, plan.thick, r.send1, r.recv1, r.s1, r.r1)
        back = Exchange(False, spaces, plan.thick, r.send2, r.recv2, r.s2, r.r2)
        send_modes(there, plan.pairs, plan.chunk, r.flat)
        leave(r.scaled, r.lines, r.turn)
        moves.start(r.lines, r.lines_x)
        filter_backward(plan, r, there, back)
        mix_gradients(plan, r, r.sums_before)

        def arrived(i, carry):
            ship(i).wait()
            return carry

        lax.fori_loop(0, plan.steps - plan.per, arrived, 0)
        wait_all(vectors)
        def send(source, target, step, send_sem, recv_sem):
            return pltpu.make_async_remote_copy(
                src_ref=source,
                dst_ref=target,
                send_sem=send_sem.at[step],
                recv_sem=recv_sem.at[step],
                device_id={"space": 2 * others[step - 1] + core},
                device_id_type=MESH_ID,
            )

        def to_sibling(source, target, step, send_sem, recv_sem):
            return pltpu.make_async_remote_copy(
                src_ref=source,
                dst_ref=target,
                send_sem=send_sem.at[step],
                recv_sem=recv_sem.at[step],
                device_id={"space": sibling},
                device_id_type=MESH_ID,
            )

        def total(line, carry):
            tile, inside = line // (plan.tile // 64), line % (plan.tile // 64)
            own = pl.ds(pl.multiple_of(inside * 64, 64), 64)
            value = r.keep[plan.steps - plan.per + tile, own, :].astype(F32)
            value += sum(r.land[j, tile, own, :].astype(F32) for j in range(chans - 1))
            target = pl.ds(pl.multiple_of((line % (piece // 64)) * 64, 64), 64)
            r.a_send[line // (piece // 64), target, :] = value.astype(BF)
            return carry

        lax.fori_loop(0, local // 64, total, 0)
        collect(back, plan.pairs, plan.chunk, r.flat)
        wide = [
            send(r.a_send.at[others[step - 1]], r.a_land.at[level], step, r.s11, r.r11)
            for step in range(1, levels)
        ]
        for copy in wide:
            copy.start()
        copies = rows_backward(plan, r, r.unit, r.sums_before)
        r.table[...] = jnp.zeros_like(r.table)
        r.table[0:small, :] = r.sums[...]
        tail = sum(r.rest_land[j] for j in range(chans))
        for k in range(local // 128):
            lanes = slice(k * 128, (k + 1) * 128)
            r.table[small + k : small + k + 1, :] = tail[0:1, lanes]
        for k in range(3):
            line = jnp.concatenate([tail[1 + k : 2 + k, :features], jnp.zeros((1, 256 - features), F32)], axis=1)
            r.table[small + 8 + 2 * k : small + 9 + 2 * k, :] = line[:, :128]
            r.table[small + 9 + 2 * k : small + 10 + 2 * k, :] = line[:, 128:]
        for q in range(levels):
            r.b_send[q] = r.table[q * part : (q + 1) * part, :].astype(BF)
        thin = [
            send(r.b_send.at[others[step - 1]], r.b_land.at[level], step, r.s12, r.r12)
            for step in range(1, levels)
        ]
        for copy in thin:
            copy.start()
        wait_all(copies)
        result = input_gradient(plan, r, r.unit, r.dev)

        def finish(h, carry):
            r.out[h] = result(h)
            return carry

        lax.fori_loop(0, rows, finish, 0)
        a = r.a_send[level].astype(F32)
        b = r.b_send[level].astype(F32)
        for step in range(1, levels):
            wide[step - 1].wait()
            thin[step - 1].wait()
            source = lax.rem(level - step + levels, levels)
            a += r.a_land[source].astype(F32)
            b += r.b_land[source].astype(F32)
        r.a_own[...] = a.astype(BF)
        r.b_own[...] = b.astype(BF)
        last = [to_sibling(r.a_own, r.a_other.at[level], 0, r.s13, r.r13)]
        last += [to_sibling(r.b_own, r.b_other.at[level], 0, r.s14, r.r14)]
        again = []
        for step in range(1, levels):
            again.append(send(r.a_own, r.a_full.at[level], step, r.s15, r.r15))
            again.append(send(r.b_own, r.b_full.at[level], step, r.s16, r.r16))
        for copy in again + last:
            copy.start()
        r.a_full[level] = r.a_own[...]
        r.b_full[level] = r.b_own[...]
        moves.close()
        moves.open = []
        leave(r.out, r.lines, r.turn)
        moves.start(r.lines, r.lines_out)
        for step in range(1, levels):
            again[2 * step - 2].wait()
            again[2 * step - 1].wait()
            source = lax.rem(level - step + levels, levels)
            more = [to_sibling(r.a_full.at[source], r.a_other.at[source], step, r.s13, r.r13)]
            more += [to_sibling(r.b_full.at[source], r.b_other.at[source], step, r.s14, r.r14)]
            for copy in more:
                copy.start()
            last += more
        wait_all(last)
        moves.close()
        there.close(plan.pairs)
        back.close(plan.pairs)

    ins = {
        "g": two["out"],
        "came": two["came"],
        "second_x": two["second_x"],
        "sums_before": two["sums"],
        "rest_before": two["rest"],
        "grads_kept": two["grads_kept"],
        "mix": one["mix_kept"],
        **{
            key: one[key]
            for key in (
                "w_kept",
                "slope_kept",
                "active_kept",
                "entry_kept",
                "unit_wide_kept",
                "dev_wide_kept",
                "gathered_kept",
                "spec_kept",
                "first_kept",
                "second_kept",
                "unit_kept",
                "dev_kept",
            )
        },
        **args,
    }
    ins.update({key: tables[key] for key in ("rowinv_t", "row_t", "col", "colinv", "even")})
    outs = {
        "lines_x": plan.lines,
        "lines_out": plan.lines,
        "a_full": ((levels, piece, width), BF),
        "a_other": ((levels, piece, width), BF),
        "b_full": ((levels, part, 128), BF),
        "b_other": ((levels, part, 128), BF),
    }
    blocks = pltpu.VMEM((plan.steps, plan.tile, width), BF)
    scratch = {
        "dma": sems(16),
        "dma2": sems(2, 2),
        "lines": scratch_of(plan.lines),
        "unit": scratch_of(plan.field),
        "dev": scratch_of(plan.dev),
        "out": scratch_of(plan.field),
        "spec": scratch_of(plan.kept),
        "first": scratch_of(plan.kept),
        "second": scratch_of(plan.kept),
        "w": scratch_of(plan.weights),
        "own": scratch_of(plan.by_cells),
        "leaving": scratch_of(plan.by_cells),
        "upper": scratch_of(plan.wide),
        "small": pltpu.VMEM((8, width), F32),
        "upb": pltpu.VMEM((16, plan.tile), F32),
        "sums": scratch_of(plan.sums),
        "rest": scratch_of(plan.rest),
        "rest_land": scratch_of(plan.rest),
        "prev": pltpu.VMEM((2, 2, plan.tile, width), BF),
        "keep": blocks,
        "give": pltpu.VMEM((2, plan.tile, width), BF),
        "take": pltpu.VMEM((3, plan.tile, width), BF),
        "land": pltpu.VMEM((chans - 1, plan.per, plan.tile, width), BF),
        "table": pltpu.VMEM((part * levels, 128), F32),
        "a_send": pltpu.VMEM((levels, piece, width), BF),
        "a_land": pltpu.VMEM((levels, piece, width), BF),
        "a_own": pltpu.VMEM((piece, width), BF),
        "b_send": pltpu.VMEM((levels, part, 128), BF),
        "b_land": pltpu.VMEM((levels, part, 128), BF),
        "b_own": pltpu.VMEM((part, 128), BF),
        **plan.exchange_scratch(False, False),
        **plan.spectral_scratch(),
        **ffn_scratch(plan),
        **norm_sums_scratch(plan),
        **{key + str(k): sems(chans) for k in (6, 7) for key in ("s", "r")},
        **{key + str(k): sems(plan.steps) for k in (9, 10) for key in ("s", "r")},
        **{key + str(k): sems(levels) for k in range(11, 17) for key in ("s", "r")},
    }
    in_place = [key for key in ins if key.endswith("_kept") and key != "mix_kept"] + ["second_x", "g"]
    return launch(
        body,
        ins,
        outs,
        scratch,
        "first_backward",
        2,
        {key: IN_PLACE for key in in_place},
        {key: IN_PLACE for key in ("lines_x", "lines_out")},
    )


def unpack_gradients(plan, parts):
    features, small = plan.features, plan.small
    levels, piece, width = parts["a_full"].shape
    part = parts["b_full"].shape[1]
    local = levels * piece
    size = features // 2

    def body(r):
        swap = lax.rem(lax.axis_index("space"), 2) == 1
        for q in range(levels):
            own = slice(q * piece, (q + 1) * piece)
            mine, theirs = r.a_full[q].astype(F32), r.a_other[q].astype(F32)
            r.down[own, :] = jnp.where(swap, theirs, mine)
            r.up[:, own] = jnp.where(swap, mine, theirs).T
            r.table[q * part : (q + 1) * part, :] = r.b_full[q].astype(F32) + r.b_other[q].astype(F32)
        for layer, target in enumerate((r.mix_in, r.mix_out)):
            for half in range(2):
                for block in range(2):
                    start = ((layer * 2 + half) * 2 + block) * size
                    target[half, block] = r.table[start : start + size, :size]
        base = 8 * size

        def vector(k):
            return jnp.concatenate(
                [r.table[base + k : base + k + 1, :], r.table[base + 8 + k : base + 9 + k, : features - 128]], axis=1
            )

        for k, target in enumerate((r.bias_in, r.bias_in, r.bias_out, r.bias_out)):
            value = vector(k)
            target[k % 2, 0:1, :] = value[:, :size]
            target[k % 2, 1:2, :] = value[:, size:]
        r.pre_gain[...] = vector(4)
        r.pre_shift[...] = vector(5)
        for k in range(local // 128):
            r.upb[0:1, k * 128 : (k + 1) * 128] = r.table[small + k : small + k + 1, :]
        for k, target in enumerate((r.post_gain, r.post_shift, r.downb)):
            target[...] = jnp.concatenate(
                [
                    r.table[small + 8 + 2 * k : small + 9 + 2 * k, :],
                    r.table[small + 9 + 2 * k : small + 10 + 2 * k, : features - 128],
                ],
                axis=1,
            )


    return launch(
        body,
        {key: parts[key] for key in ("a_full", "a_other", "b_full", "b_other")},
        {
            "down": ((local, width), F32),
            "up": ((width, local), F32),
            "mix_in": ((2, 2, size, size), F32),
            "mix_out": ((2, 2, size, size), F32),
            "bias_in": ((2, 2, size), F32),
            "bias_out": ((2, 2, size), F32),
            "pre_gain": ((1, features), F32),
            "pre_shift": ((1, features), F32),
            "post_gain": ((1, features), F32),
            "post_shift": ((1, features), F32),
            "downb": ((1, features), F32),
            "upb": ((1, local), F32),
        },
        {"table": pltpu.VMEM((part * levels, 128), F32)},
        "unpack_gradients",
    )


def shards_fast(
    current_atmosphere,
    truth_one,
    truth_two,
    storm_codes,
    pre_gain,
    pre_shift,
    mix_weight_in,
    mix_bias_in,
    mix_weight_out,
    mix_bias_out,
    post_gain,
    post_shift,
    up_weight,
    up_bias,
    down_weight,
    down_bias,
):
    rows, merged = current_atmosphere.shape[1:]
    columns = W
    features = merged // columns
    plan = Plan(
        rows, features, columns, lax.axis_size("space"), lax.axis_size("chan"), up_weight.shape[1]
    )
    forward, inverse = row_constants(columns)
    column = column_constants(rows * plan.spaces, rows, 2)
    even = (np.arange(plan.half) // rows % 2 == 0).astype(np.float32)
    tables = {
        "row": jnp.stack(const_halves(forward)),
        "rowinv": jnp.stack(const_halves(inverse)),
        "rowinv_t": const_halves(inverse.T)[0],
        "row_t": const_halves(forward.T)[0],
        "col": jnp.stack(const_halves(column)),
        "colinv": jnp.stack(const_halves(column.T)),
        "even": jnp.asarray(np.repeat(even[:, None], features, axis=1)),
    }

    def lines(flat):
        return flat.reshape(rows, merged // 128, 128)

    def flat(line_field):
        return line_field.reshape(1, rows, merged)

    one = launch_first(
        plan,
        {
            "lines_x": lines(current_atmosphere),
            "lines_t": lines(truth_one),
            "gain": pre_gain,
            "shift": pre_shift,
            "mix_in": mix_weight_in,
            "bias_in": mix_bias_in,
            "mix_out": mix_weight_out,
            "bias_out": mix_bias_out,
            "post_gain": post_gain,
            "post_shift": post_shift,
            "up": up_weight,
            "upb": up_bias,
            "down": down_weight,
            "downb": down_bias,
        },
        tables,
    )
    two = launch_second(
        plan,
        {"gain": pre_gain, "shift": pre_shift, "lines_t": lines(truth_two), "codes": storm_codes},
        one,
        tables,
    )
    three = launch_third(plan, {"gain": pre_gain}, one, two, tables)
    grads = unpack_gradients(plan, three)
    return (
        flat(two["lines"]),
        flat(three["lines_x"]),
        flat(three["lines_out"]),
        grads["pre_gain"].reshape(features),
        grads["pre_shift"].reshape(features),
        grads["mix_in"],
        grads["bias_in"],
        grads["mix_out"],
        grads["bias_out"],
        grads["post_gain"].reshape(features),
        grads["post_shift"].reshape(features),
        grads["up"],
        grads["upb"].reshape(plan.local),
        grads["down"],
        grads["downb"].reshape(features),
    )


def suits(mesh):
    spaces, chans = mesh.shape["space"], mesh.shape["chan"]
    return (spaces, chans) == (8, 4)


def solution(mesh):
    in_specs = (
        P(None, "space", "chan"),
        P(None, "space", "chan"),
        P(None, "space", "chan"),
        P(),
        P("chan"),
        P("chan"),
        P(None, "chan", None, None),
        P(None, "chan", None),
        P(None, "chan", None, None),
        P(None, "chan", None),
        P("chan"),
        P("chan"),
        P(None, "chan"),
        P("chan"),
        P("chan", None),
        P("chan"),
    )
    out_specs = (
        P(None, "space", "chan"),
        P(None, "space", "chan"),
        P(None, "space", "chan"),
        P("chan"),
        P("chan"),
        P(None, "chan", None, None),
        P(None, "chan", None),
        P(None, "chan", None, None),
        P(None, "chan", None),
        P("chan"),
        P("chan"),
        P(None, "chan"),
        P("chan"),
        P("chan", None),
        P("chan"),
    )
    return jax.shard_map(shards_fast if suits(mesh) else shards, mesh=mesh, in_specs=in_specs, out_specs=out_specs, check_vma=False)
```

```python
import functools
import math
import types

import jax
import jax.numpy as jnp
import ml_dtypes
import numpy as np
from jax import lax
from jax.experimental import pallas as pl
from jax.experimental.pallas import tpu as pltpu
from jax.sharding import PartitionSpec as P

W = 160
KW = 81


NORM_EPS = 1e-06
SHRINK_LEVEL = 0.01
FULL_PRECISION = lax.Precision.HIGHEST


def exact_gelu(values):
    return jax.nn.gelu(values, approximate=False)


def shrink(values):
    return values - jnp.clip(values, -SHRINK_LEVEL, SHRINK_LEVEL)


def block_mix(values, matrix):
    return jnp.einsum("bhkni,nio->bhkno", values, matrix, precision=FULL_PRECISION)


def row_tables(columns, kept_modes, padded_modes):
    places = jnp.arange(columns, dtype=jnp.int32)[:, None]
    orders = jnp.arange(padded_modes, dtype=jnp.int32)[None, :]
    angles = 2.0 * math.pi / columns * (places * orders % columns).astype(jnp.float32)
    factor = 1.0 / math.sqrt(columns)
    single = jnp.logical_or(orders == 0, 2 * orders == columns)
    doubled = jnp.where(single, 1.0, 2.0).astype(jnp.float32)
    used = jnp.where(orders < kept_modes, 1.0, 0.0).astype(jnp.float32)
    return (
        jnp.cos(angles) * factor * used,
        -jnp.sin(angles) * factor * used,
        jnp.transpose(jnp.cos(angles) * doubled * factor * used),
        jnp.transpose(jnp.sin(angles) * doubled * factor * used),
    )


def along_rows(values, tables):
    return jnp.stack(
        [
            jnp.einsum("bhwc,wk->bhkc", values, tables[0], precision=FULL_PRECISION),
            jnp.einsum("bhwc,wk->bhkc", values, tables[1], precision=FULL_PRECISION),
        ]
    )


def along_rows_back(paired, tables):
    return jnp.einsum("bhkc,wk->bhwc", paired[0], tables[0], precision=FULL_PRECISION) + jnp.einsum(
        "bhkc,wk->bhwc", paired[1], tables[1], precision=FULL_PRECISION
    )


def rows_inverse(paired, tables):
    return jnp.einsum("bhkc,kw->bhwc", paired[0], tables[2], precision=FULL_PRECISION) - jnp.einsum(
        "bhkc,kw->bhwc", paired[1], tables[3], precision=FULL_PRECISION
    )


def rows_inverse_back(values, tables):
    return jnp.stack(
        [
            jnp.einsum("bhwc,kw->bhkc", values, tables[2], precision=FULL_PRECISION),
            -jnp.einsum("bhwc,kw->bhkc", values, tables[3], precision=FULL_PRECISION),
        ]
    )


def column_tables(height):
    orders = jnp.arange(height, dtype=jnp.int32)[:, None]
    places = jnp.arange(height, dtype=jnp.int32)[None, :]
    angles = 2.0 * math.pi / height * (orders * places % height).astype(jnp.float32)
    factor = 1.0 / math.sqrt(height)
    return (jnp.cos(angles) * factor, jnp.sin(angles) * factor)


def to_freq(matrix, values):
    return jnp.einsum("kh,bhmc->bkmc", matrix, values, precision=FULL_PRECISION)


def from_freq(matrix, values):
    return jnp.einsum("kh,bkmc->bhmc", matrix, values, precision=FULL_PRECISION)


def spectral_core(paired, w_first, b_first, w_second, b_second):
    samples, height, kept_modes, channels = paired.shape[1:]
    blocks, block_size = (w_first.shape[1], w_first.shape[2])
    cosine, sine_table = column_tables(height)
    real_in, imag_in = (paired[0], paired[1])
    split_form = (samples, height, kept_modes, blocks, block_size)
    real_part = (to_freq(cosine, real_in) + to_freq(sine_table, imag_in)).reshape(split_form)
    imag_part = (to_freq(cosine, imag_in) - to_freq(sine_table, real_in)).reshape(split_form)
    first_real = jax.nn.relu(
        block_mix(real_part, w_first[0]) - block_mix(imag_part, w_first[1]) + b_first[0]
    )
    first_imag = jax.nn.relu(
        block_mix(imag_part, w_first[0]) + block_mix(real_part, w_first[1]) + b_first[1]
    )
    joined_form = (samples, height, kept_modes, channels)
    second_real = shrink(
        block_mix(first_real, w_second[0]) - block_mix(first_imag, w_second[1]) + b_second[0]
    ).reshape(joined_form)
    second_imag = shrink(
        block_mix(first_imag, w_second[0]) + block_mix(first_real, w_second[1]) + b_second[1]
    ).reshape(joined_form)
    out_real = from_freq(cosine, second_real) - from_freq(sine_table, second_imag)
    out_imag = from_freq(cosine, second_imag) + from_freq(sine_table, second_real)
    return jnp.stack([out_real, out_imag])


def column_layout(paired):
    return lax.all_to_all(paired, "space", split_axis=3, concat_axis=2, tiled=True)


def row_layout(paired):
    return lax.all_to_all(
        paired.astype(jnp.bfloat16), "space", split_axis=2, concat_axis=3, tiled=True
    ).astype(paired.dtype)


def norm_forward(values, gain, offset):
    width_all = values.shape[-1] * lax.axis_size("chan")
    totals = lax.psum((jnp.sum(values, axis=-1), jnp.sum(values * values, axis=-1)), "chan")
    average = totals[0] / width_all
    variance = totals[1] / width_all - average * average
    inverse_dev = lax.rsqrt(variance + NORM_EPS)[..., None]
    scaled = (values - average[..., None]) * inverse_dev
    return (scaled * gain + offset, (scaled, inverse_dev))


def norm_backward(gradient, gain, saved):
    scaled, inverse_dev = saved
    width_all = scaled.shape[-1] * lax.axis_size("chan")
    scaled_grad = gradient * gain
    totals = lax.psum(
        (jnp.sum(scaled_grad, axis=-1), jnp.sum(scaled_grad * scaled, axis=-1)), "chan"
    )
    values_grad = inverse_dev * (
        scaled_grad - totals[0][..., None] / width_all - scaled * (totals[1][..., None] / width_all)
    )
    return (
        values_grad,
        jnp.sum(gradient * scaled, axis=(0, 1, 2)),
        jnp.sum(gradient, axis=(0, 1, 2)),
    )


def shards(
    current_atmosphere,
    truth_one,
    truth_two,
    storm_codes,
    pre_gain,
    pre_shift,
    mix_weight_in,
    mix_bias_in,
    mix_weight_out,
    mix_bias_out,
    post_gain,
    post_shift,
    up_weight,
    up_bias,
    down_weight,
    down_bias,
):
    samples, rows_here, merged = current_atmosphere.shape
    columns = W
    channels = merged // columns
    total_rows = samples * rows_here * columns
    space_count = lax.axis_size("space")
    padded_modes = (KW + space_count - 1) // space_count * space_count
    tables = row_tables(columns, KW, padded_modes)

    def to_cells(flat_field):
        return jnp.transpose(
            flat_field.reshape(samples, rows_here, channels, columns), (0, 1, 3, 2)
        )

    def to_flat(cell_field):
        return jnp.transpose(cell_field, (0, 1, 3, 2)).reshape(samples, rows_here, merged)

    start_cells = to_cells(current_atmosphere)
    target_one = to_cells(truth_one)
    target_two = to_cells(truth_two)
    weight_of = (storm_codes.astype(jnp.float32) / 64.0).reshape(-1, 1, 1, 1)
    full_up, full_down, full_up_bias, full_down_bias = (up_weight, down_weight, up_bias, down_bias)

    def mlp_forward(inputs):
        gathered = lax.all_gather(inputs, "chan", axis=1, tiled=True)
        hidden = jnp.dot(
            gathered, full_up, preferred_element_type=jnp.float32
        ) + full_up_bias.astype(jnp.float32)
        active_full, gelu_pull = jax.vjp(exact_gelu, hidden)
        active = active_full.astype(jnp.bfloat16)
        product = jnp.dot(active, full_down, preferred_element_type=jnp.float32)
        output = lax.psum_scatter(
            product.astype(jnp.bfloat16), "chan", scatter_dimension=1, tiled=True
        ).astype(jnp.float32) + full_down_bias.astype(jnp.float32)
        return (output, (gathered, gelu_pull, active))

    def mlp_backward(gradient, saved):
        gathered, gelu_pull, active = saved
        grad_low = gradient.astype(jnp.bfloat16)
        grad_rows = lax.all_gather(grad_low, "chan", axis=1, tiled=True)
        down_bias_grad = jnp.sum(grad_low.astype(jnp.float32), axis=0)
        down_grad = jnp.dot(active.T, grad_rows, preferred_element_type=jnp.float32)
        active_grad = jnp.dot(grad_rows, full_down.T, preferred_element_type=jnp.float32)
        hidden_grad = gelu_pull(active_grad)[0].astype(jnp.bfloat16)
        up_grad = jnp.dot(gathered.T, hidden_grad, preferred_element_type=jnp.float32)
        up_bias_grad = jnp.sum(hidden_grad.astype(jnp.float32), axis=0)
        input_part = jnp.dot(hidden_grad, full_up.T, preferred_element_type=jnp.float32)
        input_grad = lax.psum_scatter(
            input_part.astype(jnp.bfloat16), "chan", scatter_dimension=1, tiled=True
        ).astype(jnp.float32)
        return (input_grad, (up_grad, up_bias_grad, down_grad, down_bias_grad))

    def forward_block(values):
        normed, first_saved = norm_forward(values, pre_gain, pre_shift)
        modal_in = column_layout(along_rows(normed, tables))
        filtered, core_pull = jax.vjp(
            spectral_core, modal_in, mix_weight_in, mix_bias_in, mix_weight_out, mix_bias_out
        )
        middle = rows_inverse(row_layout(filtered), tables) + normed + values
        entry, second_residuals = norm_forward(middle, post_gain, post_shift)
        output, mlp_saved = mlp_forward(entry.astype(jnp.bfloat16).reshape(total_rows, channels))
        return (
            output.reshape(values.shape) + middle,
            (first_saved, core_pull, second_residuals, mlp_saved),
        )

    def backward_block(gradient, saved):
        first_saved, core_pull, second_residuals, mlp_saved = saved
        mlp_grad, dense_grads = mlp_backward(gradient.reshape(total_rows, channels), mlp_saved)
        middle_part, post_gain_grad, post_shift_grad = norm_backward(
            mlp_grad.reshape(gradient.shape), post_gain, second_residuals
        )
        middle_grad = middle_part + gradient
        filter_grads = core_pull(column_layout(rows_inverse_back(middle_grad, tables)))
        normed_grad = along_rows_back(row_layout(filter_grads[0]), tables) + middle_grad
        input_part, pre_gain_grad, pre_shift_grad = norm_backward(
            normed_grad, pre_gain, first_saved
        )
        return (
            input_part + middle_grad,
            (pre_gain_grad, pre_shift_grad)
            + tuple(filter_grads[1:])
            + (post_gain_grad, post_shift_grad)
            + dense_grads,
        )

    first_out, first_saved_all = forward_block(start_cells)
    second_out, second_saved_all = forward_block(first_out)
    carried, grads_late = backward_block(weight_of * (second_out - target_two), second_saved_all)
    input_grad, grads_early = backward_block(
        weight_of * (first_out - target_one) + carried, first_saved_all
    )
    summed = jax.tree.map(jnp.add, grads_early, grads_late)
    (
        sum_pre_gain,
        sum_pre_shift,
        sum_mix_w_in,
        summed_mixing_bias_input,
        sum_mix_w_out,
        sum_mix_b_out,
        sum_post_gain,
        sum_post_shift,
        sum_up,
        sum_up_bias,
        sum_down,
        sum_down_bias,
    ) = summed
    totals = (
        lax.psum(sum_pre_gain.astype(jnp.bfloat16), "space").astype(jnp.float32),
        lax.psum(sum_pre_shift.astype(jnp.bfloat16), "space").astype(jnp.float32),
        lax.psum(sum_mix_w_in.astype(jnp.bfloat16), "space").astype(jnp.float32),
        lax.psum(summed_mixing_bias_input.astype(jnp.bfloat16), "space").astype(jnp.float32),
        lax.psum(sum_mix_w_out.astype(jnp.bfloat16), "space").astype(jnp.float32),
        lax.psum(sum_mix_b_out.astype(jnp.bfloat16), "space").astype(jnp.float32),
        lax.psum(sum_post_gain.astype(jnp.bfloat16), "space").astype(jnp.float32),
        lax.psum(sum_post_shift.astype(jnp.bfloat16), "space").astype(jnp.float32),
        lax.psum(sum_up.astype(jnp.bfloat16), "space").astype(jnp.float32),
        lax.psum(sum_up_bias.astype(jnp.bfloat16), "space").astype(jnp.float32),
        lax.psum(sum_down.astype(jnp.bfloat16), "space").astype(jnp.float32),
        lax.psum(sum_down_bias.astype(jnp.bfloat16), "space").astype(jnp.float32),
    )
    return (to_flat(first_out), to_flat(second_out), to_flat(input_grad)) + tuple(totals)


BF = jnp.bfloat16
F32 = jnp.float32
MESH_ID = pl.DeviceIdType.MESH
VMEM_BYTES = 66 * 1024 * 1024 - 1024 * 1024


def mm(a, b):
    return jnp.dot(a, b, preferred_element_type=F32)


def mm_nt(a, b):
    return lax.dot_general(a, b, (((1,), (1,)), ((), ())), preferred_element_type=F32)


def mm_tn(a, b):
    return lax.dot_general(a, b, (((0,), (0,)), ((), ())), preferred_element_type=F32)


def halves(v):
    high = v.astype(BF)
    return high, (v - high.astype(F32)).astype(BF)


def mm3(a, b):
    return mm(a[0], b[0]) + (mm(a[0], b[1]) + mm(a[1], b[0]))


def const_halves(table):
    table = np.asarray(table, np.float32)
    high = table.astype(ml_dtypes.bfloat16)
    low = (table - high.astype(np.float32)).astype(ml_dtypes.bfloat16)
    return jnp.asarray(high), jnp.asarray(low)


def row_constants(columns):
    half = columns // 2
    place = np.arange(columns)
    mode = np.arange(half)
    angle = 2.0 * np.pi * np.outer(mode, place) / columns
    real = np.cos(angle)
    imag = -np.sin(angle)
    imag[0] = np.cos(np.pi * place)
    forward = np.concatenate([real, imag]) / np.sqrt(columns)
    weight = np.where(mode == 0, 1.0, 2.0)
    inverse = (forward * np.concatenate([weight, weight])[:, None]).T
    return forward, inverse


def column_constants(height, rows, group):
    owners = height // rows
    angle = 2.0 * np.pi * np.outer(np.arange(height), np.arange(height)) / height
    cosine = np.cos(angle) / np.sqrt(height)
    sine = np.sin(angle) / np.sqrt(height)

    def spread(matrix):
        wide = np.zeros((group, height, owners, group, rows))
        for column in range(group):
            wide[column, :, :, column, :] = matrix.reshape(height, owners, rows)
        return wide.reshape(group * height, owners * group * rows)

    cosine, sine = spread(cosine), spread(sine)
    return np.block([[cosine, sine], [-sine, cosine]])


def signal_peers(axis, count, barrier):
    me = lax.axis_index(axis)
    for step in range(1, count):
        pl.semaphore_signal(
            barrier, inc=1, device_id={axis: lax.rem(me + step, count)}, device_id_type=MESH_ID
        )


def push(axis, count, step, source, target, send_sem, recv_sem):
    peer = lax.rem(lax.axis_index(axis) + step, count)
    return pltpu.make_async_remote_copy(
        src_ref=source,
        dst_ref=target,
        send_sem=send_sem.at[step],
        recv_sem=recv_sem.at[step],
        device_id={axis: peer},
        device_id_type=MESH_ID,
    )


def params(collective_id=None):
    return pltpu.CompilerParams(
        collective_id=collective_id,
        has_side_effects=collective_id is not None,
        vmem_limit_bytes=VMEM_BYTES,
    )


def launch(body, ins, outs, scratch, name, collective_id=None, in_specs=None, out_specs=None, grid=()):
    in_specs, out_specs = in_specs or {}, out_specs or {}
    names = list(ins) + list(outs) + list(scratch)
    whole = pl.BlockSpec(memory_space=pltpu.VMEM)
    results = pl.pallas_call(
        lambda *refs: body(types.SimpleNamespace(**dict(zip(names, refs)))),
        grid=grid,
        in_specs=[in_specs.get(key, whole) for key in ins],
        out_specs=[out_specs.get(key, whole) for key in outs],
        out_shape=[jax.ShapeDtypeStruct(*outs[key]) for key in outs],
        scratch_shapes=list(scratch.values()),
        compiler_params=params(collective_id),
        name=name,
    )(*ins.values())
    return dict(zip(outs, results))


IN_PLACE = pl.BlockSpec(memory_space=pl.ANY)


def sems(*counts):
    return pltpu.SemaphoreType.DMA(counts)


def run_copies(copies):
    for copy in copies:
        copy.start()
    for copy in copies:
        copy.wait()


def cells_from_lines(lines_ref, h, scratch_ref):
    features = scratch_ref.shape[1]
    per = 640 // W
    groups = features // per
    wide = jnp.concatenate(
        [lines_ref[h, pl.ds(part, groups, stride=5), :] for part in range(5)], axis=1
    )
    for part in range(per):
        piece = wide[:, part * W : (part + 1) * W]
        scratch_ref[0, pl.ds(part, groups, stride=per), :] = piece[:, :128]
        scratch_ref[1, pl.ds(part, groups, stride=per), :] = jnp.concatenate(
            [piece[:, 128:], jnp.zeros((groups, 256 - W), F32)], axis=1
        )
    return jnp.concatenate([scratch_ref[0], scratch_ref[1][:, : W - 128]], axis=1)


def enter(lines_ref, cells_ref, scratch_ref):
    def row(h, carry):
        cells_ref[h] = cells_from_lines(lines_ref, h, scratch_ref).T
        return carry

    lax.fori_loop(0, lines_ref.shape[0], row, 0)


def leave(cells_ref, lines_ref, scratch_ref):
    features = scratch_ref.shape[1]
    per = 640 // W
    groups = features // per

    def row(h, carry):
        block = cells_ref[h].T
        scratch_ref[0] = block[:, :128]
        scratch_ref[1] = jnp.concatenate([block[:, 128:], jnp.zeros((features, 256 - W), F32)], axis=1)
        wide = jnp.concatenate(
            [
                piece
                for part in range(per)
                for piece in (
                    scratch_ref[0, pl.ds(part, groups, stride=per), :],
                    scratch_ref[1, pl.ds(part, groups, stride=per), :][:, : W - 128],
                )
            ],
            axis=1,
        )
        for part in range(5):
            lines_ref[h, pl.ds(part, groups, stride=5), :] = wide[:, part * 128 : (part + 1) * 128]
        return carry

    lax.fori_loop(0, lines_ref.shape[0], row, 0)


def pack_lanes(flat_ref, place, real, imag):
    flat_ref[0, place, :] = real[:, :128]
    flat_ref[1, place, :] = imag[:, :128]
    flat_ref[2, place, :] = jnp.concatenate([real[:, 128:], imag[:, 128:]], axis=1)


def join_lanes(first, second, rest):
    real = jnp.concatenate([first, rest[:, :64]], axis=1)
    imag = jnp.concatenate([second, rest[:, 64:]], axis=1)
    return real, imag


def unpack_lanes(flat_ref, place):
    return join_lanes(flat_ref[0, place, :], flat_ref[1, place, :], flat_ref[2, place, :])


LEVEL = 32000.0


class Exchange:
    def __init__(self, fixed, spaces, thick, send_ref, recv_ref, send_sem, recv_sem, scales=None):
        self.fixed, self.scales = fixed, scales
        self.spaces, self.thick = spaces, thick
        self.send_ref, self.recv_ref = send_ref, recv_ref
        self.send_sem, self.recv_sem = send_sem, recv_sem
        self.me = lax.axis_index("space")

    @staticmethod
    def shape(fixed, spaces, thick, pairs):
        return pltpu.VMEM((pairs, spaces, 3 * thick, 128), jnp.int16 if fixed else BF)

    def copy(self, p, step):
        peer = lax.rem(self.me + step, self.spaces)
        return pltpu.make_async_remote_copy(
            src_ref=self.send_ref.at[p, peer],
            dst_ref=self.recv_ref.at[p, self.me],
            send_sem=self.send_sem.at[p, step],
            recv_sem=self.recv_sem.at[p, step],
            device_id={"space": peer},
            device_id_type=MESH_ID,
        )

    def scale_copy(self, step):
        own_ref, all_ref, send_sem, recv_sem = self.scales
        return push("space", self.spaces, step, own_ref, all_ref.at[self.me], send_sem, recv_sem)

    def send_scales(self, flat_ref):
        own_ref, all_ref = self.scales[:2]
        largest = jnp.max(jnp.abs(flat_ref[...]), axis=1)
        own_ref[0:3, :] = jnp.maximum(largest, 1e-30) * (1.0 / LEVEL)
        own_ref[3:8, :] = jnp.ones((5, 128), F32)
        for step in range(1, self.spaces):
            self.scale_copy(step).start()
        all_ref[self.me] = own_ref[...]
        self.factor = 1.0 / own_ref[...]

    def encode(self, values):
        if not self.fixed:
            return jnp.concatenate([values[k] for k in range(3)], axis=0).astype(BF)
        lines = [jnp.round(values[k] * self.factor[k : k + 1]) for k in range(3)]
        return jnp.concatenate(lines, axis=0).astype(jnp.int32).astype(jnp.int16)

    def send(self, p, flat_ref, start_of):
        for step in list(range(1, self.spaces)) + [0]:
            peer = lax.rem(self.me + step, self.spaces)
            rows = pl.ds(pl.multiple_of(start_of(peer), 8), self.thick)
            coded = self.encode(flat_ref[:, rows, :])
            if step:
                self.send_ref[p, peer] = coded
                self.copy(p, step).start()
            else:
                self.recv_ref[p, peer] = coded

    def arrive(self, p):
        for step in range(1, self.spaces):
            self.copy(p, step).wait_recv()

    def arrive_scales(self):
        for step in range(1, self.spaces):
            self.scale_copy(step).wait_recv()

    def take(self, p, source):
        coded = self.recv_ref[p, source]
        values = (coded.astype(jnp.int32) if self.fixed else coded).astype(F32)
        parts = [values[k * self.thick : (k + 1) * self.thick] for k in range(3)]
        if self.fixed:
            scale = self.scales[1][source]
            parts = [part * scale[k : k + 1] for k, part in enumerate(parts)]
        return parts

    def close(self, pairs):
        def pair(p, carry):
            for step in range(1, self.spaces):
                self.copy(p, step).wait_send()
            return carry

        lax.fori_loop(0, pairs, pair, 0)
        if self.fixed:
            for step in range(1, self.spaces):
                self.scale_copy(step).wait_send()


def pair_inputs(q, exchange, even_ref):
    p = jnp.maximum(q - 1, 0)

    @pl.when(q != 1)
    def _():
        exchange.arrive(p)

    if exchange.fixed:

        @pl.when(q == 0)
        def _():
            exchange.arrive_scales()

    extra = (q == 0).astype(F32)
    zeroth = jnp.logical_and(exchange.me == 0, p == 0).astype(F32)
    parts = [join_lanes(*exchange.take(p, s)) for s in range(exchange.spaces)]
    real = jnp.concatenate([part[0] for part in parts], axis=0)
    imag = jnp.concatenate([part[1] for part in parts], axis=0)
    chosen = imag * (even_ref[...] * zeroth)
    real = real * (1.0 - extra) + chosen * extra
    imag = (imag - chosen) * (1.0 - extra)
    return p, zeroth, jnp.concatenate([real, imag], axis=0)


def pair_outputs(q, p, zeroth, result, exchange, even_ref, kept_ref, stage_ref):
    half = result.shape[0] // 2
    real, imag = result[:half], result[half:]

    @pl.when(q == 0)
    def _():
        kept_ref[...] = real

    @pl.when(q > 0)
    def _():
        chosen = even_ref[...] * zeroth
        pack_lanes(stage_ref, slice(None), real, imag * (1.0 - chosen) + kept_ref[...] * chosen)
        exchange.send(p, stage_ref, lambda peer: peer * exchange.thick)


def collect(exchange, pairs, chunk, flat_ref):
    def pair(p, carry):
        exchange.arrive(p)
        for s in range(exchange.spaces):
            rows = pl.ds(pl.multiple_of(s * chunk + p * exchange.thick, 8), exchange.thick)
            for k, part in enumerate(exchange.take(p, s)):
                flat_ref[k, rows, :] = part
        return carry

    lax.fori_loop(0, pairs, pair, 0)


def send_modes(exchange, pairs, chunk, flat_ref):
    if exchange.fixed:
        exchange.send_scales(flat_ref)

    def pair(p, carry):
        exchange.send(p, flat_ref, lambda peer: peer * chunk + p * exchange.thick)
        return carry

    lax.fori_loop(0, pairs, pair, 0)


class Plan:
    def __init__(self, rows, features, columns, spaces, chans, local):
        self.rows, self.features, self.columns = rows, features, columns
        self.spaces, self.chans, self.local = spaces, chans, local
        self.modes = columns // 2
        self.total = self.modes * rows
        self.chunk = self.total // spaces
        self.thick = 2 * rows
        self.half = self.thick * spaces
        self.pairs = self.chunk // self.thick
        self.cells = rows * columns // chans
        self.share = rows // chans
        self.width = features * chans
        self.tile = 256
        self.per = local // self.tile
        self.steps = chans * self.per
        self.size = features // 2
        self.small = 8 * self.size + 16
        self.field = ((rows, columns, features), F32)
        self.by_cells = ((chans, self.share, columns // 2 * 3, 128), BF)
        self.wide = ((self.cells, self.width), BF)
        self.tiles = ((self.steps, self.cells, self.tile), BF)
        self.lines = ((rows, features * columns // 128, 128), F32)
        self.dev = ((rows, columns, 8), F32)
        self.dev_wide = ((self.cells, 128), F32)
        self.kept = ((self.pairs + 1, 2 * self.half, features), BF)
        self.mix = ((2, 2, 2, features, features), BF)
        self.weights = ((2, chans, local, self.width), BF)
        self.rest = ((chans, 8, local), F32)
        self.sums = ((self.small, 128), F32)
        self.grads = ((2, self.steps, self.tile, self.width), BF)
        self.vectors = ((chans, 8, local), F32)

    def exchange_scratch(self, fixed_there, fixed_back):
        made = {}
        for name, fixed in (("1", fixed_there), ("2", fixed_back)):
            shape = Exchange.shape(fixed, self.spaces, self.thick, self.pairs)
            made["send" + name] = made["recv" + name] = shape
            made["s" + name] = made["r" + name] = sems(self.pairs, self.spaces)
        if fixed_there:
            made["scale"] = pltpu.VMEM((8, 128), F32)
            made["scale_all"] = pltpu.VMEM((self.spaces, 8, 128), F32)
            made["s20"] = made["r20"] = sems(self.spaces)
        return made

    def spectral_scratch(self):
        return {
            "flat": pltpu.VMEM((3, self.total, 128), F32),
            "stage": pltpu.VMEM((3, self.half, 128), F32),
            "last": pltpu.VMEM((self.half, self.features), F32),
            "turn": pltpu.VMEM((2, self.features, 128), F32),
            "even": pltpu.VMEM((self.half, self.features), F32),
        }


def pack_cells(value):
    side = value.shape[0] // 2
    rest = value[:, 128:]
    return jnp.concatenate([value[:, :128], jnp.concatenate([rest[:side], rest[side:]], axis=1)], axis=0)


def unpack_cells(packed):
    columns = packed.shape[0] // 3 * 2
    rest = packed[columns:]
    rest = jnp.concatenate([rest[:, :64], rest[:, 64:]], axis=0)
    return jnp.concatenate([packed[:columns], rest], axis=1)


def scratch_of(shaped):
    return pltpu.VMEM(*shaped)


def mark_even(plan, r):
    row = lax.broadcasted_iota(jnp.int32, (plan.half, plan.features), 0)
    r.even[...] = jnp.where(lax.rem(lax.div(row, plan.rows), 2) == 0, 1.0, 0.0)


def greet(plan):
    barrier = pltpu.get_barrier_semaphore()
    signal_peers("space", plan.spaces, barrier)
    signal_peers("chan", plan.chans, barrier)
    return lambda: pl.semaphore_wait(barrier, plan.spaces + plan.chans - 2)


def spread_chan(plan, source_ref, target_ref, send_sem, recv_sem):
    me = lax.axis_index("chan")
    copies = []
    for step in range(1, plan.chans):
        peer = lax.rem(me + step, plan.chans)
        copy = push("chan", plan.chans, step, source_ref.at[peer], target_ref.at[me], send_sem, recv_sem)
        copy.start()
        copies.append(copy)
    target_ref[me] = source_ref[me]
    return copies


def wait_all(copies):
    for copy in copies:
        copy.wait()


def rows_to_modes(plan, table, flat_ref, value_of, exact):
    def row(h, carry):
        value = value_of(h)
        out = mm3(table, halves(value)) if exact else mm(table, value.astype(BF))
        pack_lanes(flat_ref, pl.ds(h, plan.modes, stride=plan.rows), out[: plan.modes], out[plan.modes :])
        return carry

    lax.fori_loop(0, plan.rows, row, 0)


def filter_forward(plan, r, there, back, aside=None):
    half = plan.half

    def filter_pair(q, carry):
        if aside is not None:
            pl.when(q == plan.pairs)(aside)
        p, zeroth, block = pair_inputs(q, there, r.even)
        spec = mm3((r.col[0], r.col[1]), halves(block))
        r.spec[q] = spec.astype(BF)
        parts = halves(spec)
        straight = mm3(parts, (r.mix[0, 0, 0], r.mix[0, 0, 1]))
        crossed = mm3(parts, (r.mix[0, 1, 0], r.mix[0, 1, 1]))
        first = jnp.concatenate(
            [
                jnp.maximum(straight[:half] - crossed[half:] + r.bias[0:1], 0.0),
                jnp.maximum(straight[half:] + crossed[:half] + r.bias[1:2], 0.0),
            ],
            axis=0,
        )
        r.first[q] = first.astype(BF)
        parts = halves(first)
        straight = mm3(parts, (r.mix[1, 0, 0], r.mix[1, 0, 1]))
        crossed = mm3(parts, (r.mix[1, 1, 0], r.mix[1, 1, 1]))
        second = jnp.concatenate(
            [
                straight[:half] - crossed[half:] + r.bias[2:3],
                straight[half:] + crossed[:half] + r.bias[3:4],
            ],
            axis=0,
        )
        second = second - jnp.clip(second, -SHRINK_LEVEL, SHRINK_LEVEL)
        r.second[q] = second.astype(BF)
        result = mm(r.colinv[...], r.second[q])
        pair_outputs(q, p, zeroth, result, back, r.even, r.last, r.stage)
        return carry

    lax.fori_loop(0, plan.pairs + 1, filter_pair, 0)


def modes_to_rows(plan, flat_ref, h):
    real, imag = unpack_lanes(flat_ref, pl.ds(h, plan.modes, stride=plan.rows))
    return jnp.concatenate([real, imag], axis=0)


def rows_of_chunks(plan, row, send_chunk):
    me = lax.axis_index("chan")
    for step in list(range(1, plan.chans)) + [0]:
        peer = lax.rem(me + step, plan.chans)

        def one(i, carry):
            row(peer * plan.share + i, peer, i)
            return carry

        lax.fori_loop(0, plan.share, one, 0)
        send_chunk(step, peer)


def rows_forward(plan, r, unit_ref, x_ref, middle_ref):
    me = lax.axis_index("chan")
    gain, shift = r.gain[...].reshape(1, -1), r.shift[...].reshape(1, -1)
    copies = []

    def row(h, peer, place):
        block = modes_to_rows(plan, r.flat, h)
        out = mm(r.rowinv[...], block.astype(BF))
        middle = out + (unit_ref[h] * gain + shift) + x_ref[h]
        middle_ref[h] = middle
        r.own[peer, place] = pack_cells(middle).astype(BF)

    def send_chunk(step, peer):
        if step:
            copy = push("chan", plan.chans, step, r.own.at[peer], r.mid.at[me], r.s3, r.r3)
            copy.start()
            copies.append(copy)
        else:
            r.mid[me] = r.own[me]

    rows_of_chunks(plan, row, send_chunk)
    return copies


class Block:
    def __init__(self, plan, group, side):
        self.group, self.side, self.size = group, side, plan.columns // 2
        start = group * plan.columns + side * self.size
        self.cells = pl.ds(pl.multiple_of(start, 16), self.size)
        self.front = slice(side * self.size, (side + 1) * self.size)
        self.back = slice(plan.columns, plan.columns + self.size)
        self.lanes = slice(64 * side, 64 * side + 64)

    def get(self, chunks_ref):
        parts = []
        for j in range(chunks_ref.shape[0]):
            parts.append(chunks_ref[j, self.group, self.front, :].astype(F32))
            parts.append(chunks_ref[j, self.group, self.back, self.lanes].astype(F32))
        return jnp.concatenate(parts, axis=1)

    def put(self, chunks_ref, value):
        chans = chunks_ref.shape[0]
        features = value.shape[1] // chans
        for j in range(chans):
            part = value[:, j * features : (j + 1) * features].astype(BF)
            chunks_ref[j, self.group, self.front, :] = part[:, :128]
            chunks_ref[j, self.group, self.back, self.lanes] = part[:, 128:]


def by_blocks(plan, step):
    def one(group, carry):
        for side in range(2):
            step(Block(plan, group, side))
        return carry

    lax.fori_loop(0, plan.share, one, 0)


def full_vector(gathered_ref, start, size):
    chans = gathered_ref.shape[0]
    return jnp.concatenate([gathered_ref[j, 1:2, start : start + size] for j in range(chans)], axis=1)


def moments(value):
    mean = jnp.mean(value, axis=1, keepdims=True)
    centred = value - mean
    return mean, centred, lax.rsqrt(jnp.mean(centred * centred, axis=1, keepdims=True) + NORM_EPS)


ERF = (0.254829592, -0.284496736, 1.421413741, -1.453152027, 1.061405429)


def gelu_and_slope(v):
    e = jnp.exp2(v * v * (-0.5 / math.log(2.0)))
    below = 1.0 + (0.3275911 * math.sqrt(0.5)) * jnp.abs(v)
    t = pl.reciprocal(below, approx=True)
    t = t * (2.0 - below * t)
    c = [0.5 * k for k in ERF]
    tail = (e * t) * (c[0] + t * (c[1] + t * (c[2] + t * (c[3] + t * c[4]))))
    below = jnp.where(v >= 0.0, 1.0 - tail, tail)
    active = v * below
    return active, below + (v * (1.0 / math.sqrt(2.0 * math.pi))) * e


def three_parts(v):
    a = v.astype(BF)
    rest = v - a.astype(F32)
    b = rest.astype(BF)
    return [a, b, (rest - b.astype(F32)).astype(BF)]


def tile_of(plan, t):
    return t // plan.per, pl.ds(pl.multiple_of((t % plan.per) * plan.tile, plan.tile), plan.tile)


def up_tile(plan, r, t):
    j, place = tile_of(plan, t)
    return r.w[0, j, :, place]


def down_tile(plan, r, t):
    j, place = tile_of(plan, t)
    return r.w[1, j, place, :]


def ffn_scratch(plan):
    shape = (plan.cells, plan.tile)
    made = {key: pltpu.VMEM(shape, F32) for key in ("wide_a", "wide_b")}
    made.update({key: pltpu.VMEM(shape, BF) for key in ("thin_a", "thin_b")})
    made.update(
        total=pltpu.VMEM((plan.cells, plan.width), F32),
        entry=scratch_of(plan.wide),
        unit_wide=scratch_of(plan.wide),
        dev_wide=scratch_of(plan.dev_wide),
        active=scratch_of(plan.tiles),
        slope=scratch_of(plan.tiles),
        gathered=scratch_of(plan.vectors),
    )
    return made


def staggered(plan, r, lead, turn, trail):
    last = plan.steps - 1
    third = plan.cells // 3
    side = plan.cells // 2
    parts = plan.width // plan.tile
    r.thin_b[...] = jnp.zeros_like(r.thin_b)
    for k in range(2):
        r.wide_a[k * side : (k + 1) * side, :] = lead(0, slice(k * side, (k + 1) * side))

    def half_step(t, wide_now, wide_next, thin_past, thin_now):
        ahead, behind = jnp.minimum(t + 1, last), jnp.maximum(t - 1, 0)
        for k in range(3):
            place = slice(k * third, (k + 1) * third)
            thin_now[place, :] = turn(wide_now[place, :], t, place, k == 0)
            if k < 2:
                own = slice(k * side, (k + 1) * side)
                wide_next[own, :] = lead(ahead, own)
            trail(thin_past[...], behind, slice(k * parts // 3 * plan.tile, (k + 1) * parts // 3 * plan.tile))

    def pair(u, carry):
        half_step(2 * u, r.wide_a, r.wide_b, r.thin_b, r.thin_a)
        half_step(2 * u + 1, r.wide_b, r.wide_a, r.thin_a, r.thin_b)
        return carry

    lax.fori_loop(0, plan.steps // 2, pair, 0)
    trail(r.thin_b[...], last, slice(0, plan.width))


def ffn_forward(plan, r):
    gain = full_vector(r.gathered, 0, plan.features)
    shift = full_vector(r.gathered, plan.features, plan.features)
    bias = full_vector(r.gathered, 2 * plan.features, plan.features)

    def prepare(block):
        place = block.cells
        mean, centred, inverse = moments(block.get(r.mid))
        unit = centred * inverse
        r.unit_wide[place, :] = unit.astype(BF)
        r.dev_wide[place, :] = jnp.broadcast_to(inverse, (block.size, 128))
        r.entry[place, :] = (unit * gain + shift).astype(BF)
        r.total[place, :] = jnp.broadcast_to(bias, (block.size, plan.width))

    by_blocks(plan, prepare)

    def lead(t, rows):
        j, place = tile_of(plan, t)
        return mm(r.entry[rows, :], up_tile(plan, r, t)) + r.gathered[j, 0:1, place]

    def turn(value, t, rows, opening):
        active, slope = gelu_and_slope(value)
        active = active.astype(BF)
        r.active[t, rows, :] = active
        r.slope[t, rows, :] = slope.astype(BF)
        return active

    def trail(active, t, lanes):
        j, place = tile_of(plan, t)
        r.total[:, lanes] += mm(active, r.w[1, j, place, lanes])

    staggered(plan, r, lead, turn, trail)


def ffn_backward(plan, r):
    r.small[...] = jnp.zeros_like(r.small)
    r.total[...] = jnp.zeros_like(r.total)

    def lead(t, rows):
        return mm_nt(r.upper[rows, :], down_tile(plan, r, t))

    def turn(value, t, rows, opening):
        lower = value * r.slope[t, rows, :].astype(F32)
        bias = jnp.sum(lower, axis=0, keepdims=True)
        r.upb[pl.ds(t, 1), :] = bias if opening else r.upb[pl.ds(t, 1), :] + bias
        lower = lower.astype(BF)
        r.slope[t, rows, :] = lower
        return lower

    def trail(lower, t, lanes):
        j, place = tile_of(plan, t)
        r.total[:, lanes] += mm_nt(lower, r.w[0, j, lanes, place])

    staggered(plan, r, lead, turn, trail)
    gain = full_vector(r.gathered, 0, plan.features)

    def finish(block):
        place = block.cells
        grad = r.total[place, :]
        unit = r.unit_wide[place, :].astype(F32)
        r.small[0:1, :] += jnp.sum(grad * unit, axis=0, keepdims=True)
        r.small[1:2, :] += jnp.sum(grad, axis=0, keepdims=True)
        r.small[2:3, :] += jnp.sum(r.upper[place, :].astype(F32), axis=0, keepdims=True)
        scaled = grad * gain
        one = jnp.mean(scaled, axis=1, keepdims=True)
        two = jnp.mean(scaled * unit, axis=1, keepdims=True)
        result = r.dev_wide[place, :][:, :1] * (scaled - one - unit * two)
        block.put(r.leaving, result)

    by_blocks(plan, finish)


def vector_gradients(plan, r, rest_ref):
    rest_ref[...] = jnp.zeros_like(rest_ref)
    for j in range(plan.chans):
        for k in range(plan.per):
            line = j * plan.per + k
            rest_ref[j, 0:1, k * plan.tile : (k + 1) * plan.tile] = r.upb[line : line + 1, :]
        for k in range(3):
            rest_ref[j, 1 + k : 2 + k, 0 : plan.features] = r.small[
                k : k + 1, j * plan.features : (j + 1) * plan.features
            ]


def weight_gradients(r, t):
    return mm_tn(r.active[t], r.upper[...]), mm_tn(r.slope[t], r.entry[...])


def filter_backward(plan, r, there, back):
    half = plan.half
    r.mixgrad[...] = jnp.zeros_like(r.mixgrad)
    r.biasgrad[...] = jnp.zeros_like(r.biasgrad)

    def turned(v):
        return jnp.concatenate([v[half:], -v[:half]], axis=0)

    def note_bias(index, value):
        r.biasgrad[index : index + 1, :] += jnp.sum(value, axis=0, keepdims=True)

    def through(low, layer):
        straight = mm_nt(low, r.mix[layer, 0, 0])
        crossed = mm_nt(low, r.mix[layer, 1, 0])
        return jnp.concatenate([straight[:half] + crossed[half:], straight[half:] - crossed[:half]], axis=0)

    def filter_pair(q, carry):
        p, zeroth, block = pair_inputs(q, there, r.even)
        grad = mm(r.col[0], block.astype(BF))
        grad = jnp.where(r.second[q].astype(F32) == 0.0, 0.0, grad)
        note_bias(2, grad[:half])
        note_bias(3, grad[half:])
        low = grad.astype(BF)
        first = r.first[q]
        r.mixgrad[1, 0] += mm_tn(first, low)
        r.mixgrad[1, 1] += mm_tn(first, turned(grad).astype(BF))
        grad = jnp.where(first.astype(F32) > 0.0, through(low, 1), 0.0)
        note_bias(0, grad[:half])
        note_bias(1, grad[half:])
        low = grad.astype(BF)
        spec = r.spec[q]
        r.mixgrad[0, 0] += mm_tn(spec, low)
        r.mixgrad[0, 1] += mm_tn(spec, turned(grad).astype(BF))
        result = mm(r.colinv[...], through(low, 0).astype(BF))
        pair_outputs(q, p, zeroth, result, back, r.even, r.last, r.stage)
        return carry

    lax.fori_loop(0, plan.pairs + 1, filter_pair, 0)


def mix_gradients(plan, r, before_ref):
    size = plan.size
    for layer in range(2):
        for part in range(2):
            for block in range(2):
                own = slice(block * size, (block + 1) * size)
                piece = r.mixgrad[layer, part][own, own]
                piece = jnp.concatenate([piece, jnp.zeros((size, 128 - size), F32)], axis=1)
                start = ((layer * 2 + part) * 2 + block) * size
                place = slice(start, start + size)
                r.sums[place, :] = piece if before_ref is None else piece + before_ref[place, :]


def rows_backward(plan, r, unit_ref, before_ref):
    gain = r.gain[...].reshape(1, -1)
    me = lax.axis_index("chan")
    lane = lax.broadcasted_iota(jnp.int32, (plan.columns, 128), 1)

    def row(h, carry):
        table, one_sum, two_sum = carry
        block = modes_to_rows(plan, r.flat, h)
        grad = mm(r.row_t[...], block.astype(BF)) + r.out[h]
        unit = unit_ref[h]
        one_sum += jnp.sum(grad * unit, axis=0, keepdims=True)
        two_sum += jnp.sum(grad, axis=0, keepdims=True)
        scaled = grad * gain
        r.scaled[h] = scaled
        one = jnp.sum(scaled, axis=1, keepdims=True)
        two = jnp.sum(scaled * unit, axis=1, keepdims=True)
        table = jnp.where(lane == h, one, table)
        return jnp.where(lane == plan.rows + h, two, table), one_sum, two_sum

    none = jnp.zeros((1, plan.features), F32)
    table, one_sum, two_sum = lax.fori_loop(
        0, plan.rows, row, (jnp.zeros((plan.columns, 128), F32), none, none)
    )
    table = table.T[: 2 * plan.rows]
    r.mine[...] = table
    r.all[me] = table
    copies = [
        push("chan", plan.chans, step, r.mine, r.all.at[me], r.s4, r.r4) for step in range(1, plan.chans)
    ]
    for copy in copies:
        copy.start()
    vectors = jnp.concatenate([r.biasgrad[0:4], one_sum, two_sum, none, none], axis=0)
    wide = jnp.concatenate([vectors, jnp.zeros((8, 256 - plan.features), F32)], axis=1)
    wide = jnp.concatenate([wide[:, :128], wide[:, 128:]], axis=0)
    place = slice(8 * plan.size, plan.small)
    r.sums[place, :] = wide if before_ref is None else wide + before_ref[place, :]
    return copies


def input_gradient(plan, r, unit_ref, dev_ref):
    lane = lax.broadcasted_iota(jnp.int32, (plan.columns, 128), 1)
    means = sum(r.all[j] for j in range(plan.chans)) * (1.0 / plan.width)
    padding = jnp.zeros((128 - 2 * plan.rows, plan.columns), F32)
    means = jnp.concatenate([means, padding], axis=0).T

    def result(h):
        one = jnp.sum(jnp.where(lane == h, means, 0.0), axis=1, keepdims=True)
        two = jnp.sum(jnp.where(lane == plan.rows + h, means, 0.0), axis=1, keepdims=True)
        return r.out[h] + dev_ref[h][:, :1] * (r.scaled[h] - one - unit_ref[h] * two)

    return result


def norm_sums_scratch(plan):
    return {
        "scaled": scratch_of(plan.field),
        "mixgrad": pltpu.VMEM((2, 2, plan.features, plan.features), F32),
        "biasgrad": pltpu.VMEM((8, plan.features), F32),
        "mine": pltpu.VMEM((2 * plan.rows, plan.columns), F32),
        "all": pltpu.VMEM((plan.chans, 2 * plan.rows, plan.columns), F32),
        "s4": sems(plan.chans),
        "r4": sems(plan.chans),
    }


class Moves:
    def __init__(self, sem):
        self.sem, self.count, self.open = sem, 0, []

    def start(self, source, target):
        copy = pltpu.make_async_copy(source, target, self.sem.at[self.count])
        self.count += 1
        copy.start()
        self.open.append(copy)
        return copy

    def close(self):
        wait_all(self.open)


def launch_first(plan, args, tables):
    rows, features, chans = plan.rows, plan.features, plan.chans

    def body(r):
        me = lax.axis_index("chan")
        place = lax.axis_index("space")
        core = lax.rem(place, 2)
        sibling = place + 1 - 2 * core
        met = greet(plan)
        mark_even(plan, r)
        moves = Moves(r.dma)
        moves.start(r.up, r.w.at[0, me])
        moves.start(r.down, r.w.at[1, me])
        loaded = moves.start(r.lines_t, r.lines_in)
        own_weights = moves.open[:2]
        moves.open = []

        beside = me + 1 - 2 * lax.rem(me, 2)
        across = me + 2 - 4 * (me // 2)
        far = chans - 1 - me
        upper_half, lower_half = pl.ds(0, plan.local // 2), pl.ds(plan.local // 2, plan.local // 2)

        def hand(source, target, number, device):
            return pltpu.make_async_remote_copy(
                src_ref=source,
                dst_ref=target,
                send_sem=r.s5.at[number],
                recv_sem=r.r5.at[number],
                device_id=device,
                device_id_type=MESH_ID,
            )

        def own_to(number, source):
            peer = (beside, across)[number]
            return hand(source, r.w.at[core, me], number, {"chan": peer})

        def relay(number):
            slot = (beside, across)[number]
            part = r.w.at[core, slot, (upper_half, lower_half)[number]]
            return hand(part, part, 2 + number, {"chan": (across, beside)[number]})

        def to_core(number):
            if number < 2:
                part = r.w.at[core, (beside, across)[number]]
            else:
                part = r.w.at[core, far]
            return pltpu.make_async_remote_copy(
                src_ref=part,
                dst_ref=part,
                send_sem=r.s7.at[number],
                recv_sem=r.r7.at[number],
                device_id={"space": sibling},
                device_id_type=MESH_ID,
            )

        def pass_near():
            for number in range(2):
                own_to(number, r.up).wait_recv()
            for number in range(2):
                relay(number).start()
            for number in range(2):
                to_core(number).start()

        def pass_far():
            for number in range(2):
                relay(number).wait_recv()
            to_core(2).start()

        def close_weights():
            for number in range(2):
                own_to(number, r.up).wait_send()
                relay(number).wait_send()
            for number in range(3):
                to_core(number).wait()

        def row_of(ref):
            return ref[...].reshape(1, -1).astype(F32)

        r.vectors[...] = jnp.zeros_like(r.vectors)
        r.vectors[0:1, :] = row_of(r.upb)
        r.vectors[1:2, 0:features] = row_of(r.post_gain)
        r.vectors[1:2, features : 2 * features] = row_of(r.post_shift)
        r.vectors[1:2, 2 * features : 3 * features] = row_of(r.downb)
        r.gathered[me] = r.vectors[...]
        met()
        given = [push("chan", chans, step, r.vectors, r.gathered.at[me], r.s6, r.r6) for step in range(1, chans)]
        for copy in given:
            copy.start()
        for layer, (source, bias) in enumerate(((r.mix_in, r.bias_in), (r.mix_out, r.bias_out))):
            for part in range(2):
                zero = jnp.zeros((plan.size, plan.size), F32)
                value = jnp.concatenate(
                    [
                        jnp.concatenate([source[part, 0], zero], axis=1),
                        jnp.concatenate([zero, source[part, 1]], axis=1),
                    ],
                    axis=0,
                )
                high, low = halves(value)
                r.mix[layer, part, 0] = high
                r.mix[layer, part, 1] = low
                line = 2 * layer + part
                r.bias[line : line + 1, :] = jnp.concatenate([bias[part, 0:1, :], bias[part, 1:2, :]], axis=1)
        moves.start(r.mix, r.mix_kept)

        def first(h, carry):
            block = cells_from_lines(r.lines_x, h, r.turn)
            r.turned[h] = block
            total = jnp.sum(block, axis=0, keepdims=True)
            centred = block - total * (1.0 / features)
            r.mine[pl.ds(h, 1), :] = total
            r.mine[pl.ds(rows + h, 1), :] = jnp.sum(centred * centred, axis=0, keepdims=True)
            return carry

        lax.fori_loop(0, rows, first, 0)
        r.all[me] = r.mine[...]
        run_copies([push("chan", chans, step, r.mine, r.all.at[me], r.s4, r.r4) for step in range(1, chans)])
        for kind, source in enumerate((r.up, r.down)):

            @pl.when(core == kind)
            def _():
                for number in range(2):
                    own_to(number, source).start()

        totals = [r.all[j] for j in range(chans)]
        mean = sum(t[:rows] for t in totals) * (1.0 / plan.width)
        spread_sum = sum(
            t[rows:] + features * jnp.square(t[:rows] * (1.0 / features) - mean) for t in totals
        ) * (1.0 / plan.width)
        r.mine[pl.ds(0, rows), :] = mean
        r.mine[pl.ds(rows, rows), :] = lax.rsqrt(spread_sum + NORM_EPS)
        gain, shift = r.gain[...].reshape(1, -1), r.shift[...].reshape(1, -1)

        def normed(h):
            block = r.turned[h]
            inverse = r.mine[pl.ds(rows + h, 1), :]
            r.x[h] = block.T
            unit = ((block - r.mine[pl.ds(h, 1), :]) * inverse).T
            r.unit[h] = unit
            r.dev[h] = jnp.broadcast_to(inverse, (8, plan.columns)).T
            return unit * gain + shift

        scales = (r.scale, r.scale_all, r.s20, r.r20)
        there = Exchange(True, plan.spaces, plan.thick, r.send1, r.recv1, r.s1, r.r1, scales)
        back = Exchange(False, plan.spaces, plan.thick, r.send2, r.recv2, r.s2, r.r2)
        rows_to_modes(plan, (r.row[0], r.row[1]), r.flat, normed, True)
        send_modes(there, plan.pairs, plan.chunk, r.flat)
        moves.start(r.unit, r.unit_kept)
        moves.start(r.dev, r.dev_kept)
        loaded.wait()
        enter(r.lines_in, r.cells_t, r.turn)
        moves.start(r.cells_t, r.cells_kept)
        filter_forward(plan, r, there, back, pass_near)
        for source, target in ((r.spec, r.spec_kept), (r.first, r.first_kept), (r.second, r.second_kept)):
            moves.start(source, target)
        collect(back, plan.pairs, plan.chunk, r.flat)
        pass_far()
        copies = rows_forward(plan, r, r.unit, r.x, r.middle)
        moves.start(r.middle, r.middle_kept)
        wait_all(copies + given)
        close_weights()
        wait_all(own_weights)
        moves.start(r.w, r.w_kept)
        ffn_forward(plan, r)
        saved = ("active", "slope", "entry", "unit_wide", "dev_wide", "gathered")
        for key in saved:
            moves.start(getattr(r, key), getattr(r, key + "_kept"))

        def last(block):
            outer = r.total[block.cells, :]
            mean, _, inverse = moments(outer + block.get(r.mid))
            block.put(r.leaving, outer)
            r.stats[block.group, block.front, :] = jnp.concatenate(
                three_parts(mean) + three_parts(inverse) + [jnp.zeros((block.size, 122), BF)], axis=1
            )

        by_blocks(plan, last)
        copies = spread_chan(plan, r.leaving, r.home, r.s8, r.r8)
        for group in range(plan.share):
            r.stats_thin[group] = r.stats[group].astype(F32).T[:8].astype(BF)
        others = [
            push("chan", chans, step, r.stats_thin, r.stats_home.at[me], r.s9, r.r9) for step in range(1, chans)
        ]
        for copy in others:
            copy.start()
        r.stats_home[me] = r.stats_thin[...]
        wait_all(copies + others)
        there.close(plan.pairs)
        back.close(plan.pairs)
        moves.close()

    stats = ((chans, plan.share, 8, plan.columns), BF)
    outs = {
        "home": plan.by_cells,
        "stats_home": stats,
        "middle_kept": plan.field,
        "unit_kept": plan.field,
        "dev_kept": plan.dev,
        "cells_kept": plan.field,
        "spec_kept": plan.kept,
        "first_kept": plan.kept,
        "second_kept": plan.kept,
        "mix_kept": plan.mix,
        "w_kept": plan.weights,
        "active_kept": plan.tiles,
        "slope_kept": plan.tiles,
        "entry_kept": plan.wide,
        "unit_wide_kept": plan.wide,
        "dev_wide_kept": plan.dev_wide,
        "gathered_kept": plan.vectors,
        "bias": ((8, features), F32),
    }
    ins = dict(args)
    ins.update({key: tables[key] for key in ("row", "rowinv", "col", "colinv")})
    scratch = {
        "dma": sems(20),
        "x": scratch_of(plan.field),
        "unit": scratch_of(plan.field),
        "dev": scratch_of(plan.dev),
        "middle": scratch_of(plan.field),
        "cells_t": scratch_of(plan.field),
        "lines_in": scratch_of(plan.lines),
        "turned": pltpu.VMEM((rows, features, plan.columns), F32),
        "mine": pltpu.VMEM((2 * rows, plan.columns), F32),
        "all": pltpu.VMEM((chans, 2 * rows, plan.columns), F32),
        "spec": scratch_of(plan.kept),
        "first": scratch_of(plan.kept),
        "second": scratch_of(plan.kept),
        "mix": scratch_of(plan.mix),
        "w": scratch_of(plan.weights),
        "vectors": pltpu.VMEM((8, plan.local), F32),
        "own": scratch_of(plan.by_cells),
        "mid": scratch_of(plan.by_cells),
        "leaving": scratch_of(plan.by_cells),
        "stats": pltpu.VMEM((plan.share, plan.columns, 128), BF),
        "stats_thin": pltpu.VMEM(stats[0][1:], BF),
        **plan.exchange_scratch(True, False),
        **plan.spectral_scratch(),
        **ffn_scratch(plan),
        **{key + str(k): sems(chans) for k in range(3, 10) for key in ("s", "r")},
    }
    in_place = ("up", "down", "lines_t")
    return launch(
        body,
        ins,
        outs,
        scratch,
        "first_forward",
        0,
        {key: IN_PLACE for key in in_place},
        {key: IN_PLACE for key in outs if key.endswith("_kept")},
    )


def launch_second(plan, args, one, tables):
    rows, features, chans = plan.rows, plan.features, plan.chans

    def body(r):
        me = lax.axis_index("chan")
        met = greet(plan)
        mark_even(plan, r)
        moves = Moves(r.dma)
        loaded = moves.start(r.lines_t, r.lines_in)
        weights = moves.start(r.w_kept, r.w)
        vectors = moves.start(r.gathered_kept, r.gathered)
        earlier = moves.start(r.cells_kept, r.cells_one)
        moves.open = []
        gain, shift = r.gain[...].reshape(1, -1), r.shift[...].reshape(1, -1)
        weight = r.codes[0].astype(F32) * (1.0 / 64.0)

        def normed(h):
            quarter, inside = h // plan.share, h % plan.share
            x = unpack_cells(r.home[quarter, inside].astype(F32)) + r.before[h]
            stats = r.stats_home[quarter, inside].astype(F32).T
            parts = [stats[:, k : k + 1] for k in range(6)]
            mean = parts[0] + (parts[1] + parts[2])
            dev = parts[3] + (parts[4] + parts[5])
            unit = (x - mean) * dev
            r.x[h] = x
            r.unit[h] = unit
            r.dev[h] = jnp.broadcast_to(dev, (plan.columns, 8))
            return unit * gain + shift

        rows_to_modes(plan, (r.row[0], r.row[1]), r.flat, normed, True)
        met()
        scales = (r.scale, r.scale_all, r.s20, r.r20)
        there = Exchange(True, plan.spaces, plan.thick, r.send1, r.recv1, r.s1, r.r1, scales)
        back = Exchange(False, plan.spaces, plan.thick, r.send2, r.recv2, r.s2, r.r2)
        send_modes(there, plan.pairs, plan.chunk, r.flat)
        loaded.wait()
        enter(r.lines_in, r.cells_t, r.turn)

        def low_target(h, peer, place):
            r.own[peer, place] = pack_cells(r.cells_t[h]).astype(BF)

        targets = []

        def send_target(step, peer):
            if step:
                copy = push("chan", chans, step, r.own.at[peer], r.target.at[me], r.s5, r.r5)
                copy.start()
                targets.append(copy)
            else:
                r.target[me] = r.own[me]

        rows_of_chunks(plan, low_target, send_target)
        filter_forward(plan, r, there, back)
        collect(back, plan.pairs, plan.chunk, r.flat)
        there.close(plan.pairs)
        back.close(plan.pairs)
        wait_all(targets)
        copies = rows_forward(plan, r, r.unit, r.x, r.before)
        weights.wait()
        vectors.wait()
        wait_all(copies)
        ffn_forward(plan, r)

        def errors(block):
            outer = r.total[block.cells, :]
            error = outer + block.get(r.mid) - block.get(r.target)
            r.upper[block.cells, :] = (weight * error).astype(BF)
            block.put(r.leaving, outer)

        by_blocks(plan, errors)
        copies = spread_chan(plan, r.leaving, r.landed, r.s6, r.r6)
        for copy in copies:
            copy.wait_send()
        ffn_backward(plan, r)
        for copy in copies:
            copy.wait_recv()
        copies = spread_chan(plan, r.leaving, r.own, r.s7, r.r7)

        def grads(u, carry):
            for slot in range(2):
                t = 2 * u + slot
                stores = [
                    pltpu.make_async_copy(r.grad.at[slot, k], r.grads_kept.at[k, t], r.dma2.at[slot, k])
                    for k in range(2)
                ]

                @pl.when(u > 0)
                def _():
                    wait_all(stores)

                for k, value in enumerate(weight_gradients(r, t)):
                    r.grad[slot, k] = value.astype(BF)
                    stores[k].start()
            return carry

        lax.fori_loop(0, plan.steps // 2, grads, 0)
        vector_gradients(plan, r, r.rest)
        wait_all(copies)

        def middle_grad(h):
            quarter, inside = h // plan.share, h % plan.share
            x = unpack_cells(r.landed[quarter, inside].astype(F32)) + r.before[h]
            r.before[h] = x
            grad = weight * (x - r.cells_t[h]) + unpack_cells(r.own[quarter, inside].astype(F32))
            r.out[h] = grad
            return grad

        rows_to_modes(plan, r.rowinv_t[...], r.flat, middle_grad, False)
        there = Exchange(False, plan.spaces, plan.thick, r.send3, r.recv3, r.s3_, r.r3_)
        back = Exchange(False, plan.spaces, plan.thick, r.send2, r.recv2, r.s2, r.r2)
        send_modes(there, plan.pairs, plan.chunk, r.flat)
        moves.start(r.before, r.second_x)
        leave(r.x, r.lines, r.turn)
        filter_backward(plan, r, there, back)
        mix_gradients(plan, r, None)
        collect(back, plan.pairs, plan.chunk, r.flat)
        copies = rows_backward(plan, r, r.unit, None)
        earlier.wait()
        wait_all(copies)
        result = input_gradient(plan, r, r.unit, r.dev)
        copies = []

        def row(h, peer, place):
            grad = weight * (r.x[h] - r.cells_one[h]) + result(h)
            r.out[h] = grad
            r.own[peer, place] = pack_cells(grad).astype(BF)

        def send_chunk(step, peer):
            if step:
                copy = push("chan", chans, step, r.own.at[peer], r.came.at[me], r.s8, r.r8)
                copy.start()
                copies.append(copy)
            else:
                r.came[me] = r.own[me]

        rows_of_chunks(plan, row, send_chunk)
        for slot in range(2):
            for k in range(2):
                pltpu.make_async_copy(
                    r.grad.at[slot, k], r.grads_kept.at[k, plan.steps - 2 + slot], r.dma2.at[slot, k]
                ).wait()
        wait_all(copies)
        there.close(plan.pairs)
        back.close(plan.pairs)
        moves.close()

    ins = {
        "home": one["home"],
        "stats_home": one["stats_home"],
        "before": one["middle_kept"],
        "w_kept": one["w_kept"],
        "gathered_kept": one["gathered_kept"],
        "cells_kept": one["cells_kept"],
        "mix": one["mix_kept"],
        "bias": one["bias"],
        **args,
    }
    ins.update({key: tables[key] for key in ("row", "rowinv", "rowinv_t", "row_t", "col", "colinv")})
    outs = {
        "out": plan.field,
        "came": plan.by_cells,
        "lines": plan.lines,
        "second_x": plan.field,
        "sums": plan.sums,
        "rest": plan.rest,
        "grads_kept": plan.grads,
    }
    exchange = Exchange.shape(False, plan.spaces, plan.thick, plan.pairs)
    scratch = {
        "dma": sems(8),
        "dma2": sems(2, 2),
        "x": scratch_of(plan.field),
        "unit": scratch_of(plan.field),
        "dev": scratch_of(plan.dev),
        "cells_t": scratch_of(plan.field),
        "cells_one": scratch_of(plan.field),
        "lines_in": scratch_of(plan.lines),
        "spec": scratch_of(plan.kept),
        "first": scratch_of(plan.kept),
        "second": scratch_of(plan.kept),
        "w": scratch_of(plan.weights),
        "own": scratch_of(plan.by_cells),
        "mid": scratch_of(plan.by_cells),
        "target": scratch_of(plan.by_cells),
        "leaving": scratch_of(plan.by_cells),
        "landed": scratch_of(plan.by_cells),
        "upper": scratch_of(plan.wide),
        "small": pltpu.VMEM((8, plan.width), F32),
        "upb": pltpu.VMEM((16, plan.tile), F32),
        "grad": pltpu.VMEM((2, 2, plan.tile, plan.width), BF),
        "send3": exchange,
        "recv3": exchange,
        "s3_": sems(plan.pairs, plan.spaces),
        "r3_": sems(plan.pairs, plan.spaces),
        **plan.exchange_scratch(True, False),
        **plan.spectral_scratch(),
        **ffn_scratch(plan),
        **norm_sums_scratch(plan),
        **{key + str(k): sems(chans) for k in (3, 5, 6, 7, 8) for key in ("s", "r")},
    }
    in_specs = {key: IN_PLACE for key in ("w_kept", "gathered_kept", "cells_kept", "lines_t")}
    in_specs["codes"] = pl.BlockSpec(memory_space=pltpu.SMEM)
    return launch(
        body,
        ins,
        outs,
        scratch,
        "second_step",
        1,
        in_specs,
        {key: IN_PLACE for key in ("second_x", "grads_kept")},
    )


def launch_third(plan, args, one, two, tables):
    rows, features, chans, spaces = plan.rows, plan.features, plan.chans, plan.spaces
    local, width = plan.local, plan.width
    levels = spaces // 2
    piece = local // levels
    small = plan.small
    part = -(-(small + 32) // (16 * levels)) * 16

    def body(r):
        me = lax.axis_index("chan")
        place = lax.axis_index("space")
        core = lax.rem(place, 2)
        level = place // 2
        sibling = place + 1 - 2 * core
        others = [lax.rem(level + step, levels) for step in range(1, levels)]
        met = greet(plan)
        mark_even(plan, r)
        moves = Moves(r.dma)
        gradient = moves.start(r.g, r.out)
        early = [
            moves.start(source, target)
            for source, target in (
                (r.w_kept, r.w),
                (r.slope_kept, r.slope),
                (r.unit_wide_kept, r.unit_wide),
                (r.dev_wide_kept, r.dev_wide),
                (r.gathered_kept, r.gathered),
            )
        ]
        middle = [moves.start(r.active_kept, r.active), moves.start(r.entry_kept, r.entry)]
        late = [
            moves.start(source, target)
            for source, target in (
                (r.spec_kept, r.spec),
                (r.first_kept, r.first),
                (r.second_kept, r.second),
                (r.unit_kept, r.unit),
                (r.dev_kept, r.dev),
                (r.second_x, r.scaled),
            )
        ]
        moves.open = []

        def upper(block):
            r.upper[block.cells, :] = block.get(r.came).astype(BF)

        by_blocks(plan, upper)
        wait_all(early)
        ffn_backward(plan, r)
        met()
        copies = spread_chan(plan, r.leaving, r.own, r.s7, r.r7)
        vector_gradients(plan, r, r.rest)
        r.rest[...] += r.rest_before[...]
        vectors = [
            push("chan", chans, step, r.rest.at[lax.rem(me + step, chans)], r.rest_land.at[me], r.s6, r.r6)
            for step in range(1, chans)
        ]
        for copy in vectors:
            copy.start()
        r.rest_land[me] = r.rest[me]
        wait_all(middle)

        def order(i):
            return lax.rem((me + 1) * plan.per + i, plan.steps)

        def fetch(i, k):
            return pltpu.make_async_copy(r.grads_kept.at[k, order(i)], r.prev.at[i % 2, k], r.dma2.at[i % 2, k])

        def swap(i):
            return pltpu.make_async_remote_copy(
                src_ref=r.give.at[i % 2],
                dst_ref=r.take.at[i % 3],
                send_sem=r.s9.at[i],
                recv_sem=r.r9.at[i],
                device_id={"space": sibling},
                device_id_type=MESH_ID,
            )

        def ship(i):
            step = 1 + i // plan.per
            return pltpu.make_async_remote_copy(
                src_ref=r.keep.at[i],
                dst_ref=r.land.at[step - 1, i % plan.per],
                send_sem=r.s10.at[i],
                recv_sem=r.r10.at[i],
                device_id={"chan": lax.rem(me + step, chans)},
                device_id_type=MESH_ID,
            )

        for k in range(2):
            fetch(0, k).start()

        def settle(i):
            swap(i).wait()
            r.keep[i] = (r.keep[i].astype(F32) + r.take[i % 3].astype(F32)).astype(BF)

        def block(i, carry):
            for k in range(2):
                fetch(i, k).wait()

            @pl.when(i + 1 < plan.steps)
            def _():
                for k in range(2):
                    fetch(i + 1, k).start()

            values = [
                (value + r.prev[i % 2, k].astype(F32)).astype(BF)
                for k, value in enumerate(weight_gradients(r, order(i)))
            ]

            @pl.when(i > 0)
            def _():
                settle(i - 1)

                @pl.when(i - 1 < plan.steps - plan.per)
                def _():
                    ship(i - 1).start()

            for kind in range(2):

                @pl.when(core == kind)
                def _():
                    r.keep[i] = values[kind]
                    r.give[i % 2] = values[1 - kind]

            swap(i).start()
            return carry

        lax.fori_loop(0, plan.steps, block, 0)
        settle(plan.steps - 1)
        wait_all(copies)
        wait_all(late)
        gradient.wait()

        def middle_grad(h):
            quarter, inside = h // plan.share, h % plan.share
            grad = r.out[h] + unpack_cells(r.own[quarter, inside].astype(F32))
            r.out[h] = grad
            return grad

        rows_to_modes(plan, r.rowinv_t[...], r.flat, middle_grad, False)
        there = Exchange(False, spaces, plan.thick, r.send1, r.recv1, r.s1, r.r1)
        back = Exchange(False, spaces, plan.thick, r.send2, r.recv2, r.s2, r.r2)
        send_modes(there, plan.pairs, plan.chunk, r.flat)
        leave(r.scaled, r.lines, r.turn)
        moves.start(r.lines, r.lines_x)
        filter_backward(plan, r, there, back)
        mix_gradients(plan, r, r.sums_before)

        def arrived(i, carry):
            ship(i).wait()
            return carry

        lax.fori_loop(0, plan.steps - plan.per, arrived, 0)
        wait_all(vectors)
        def send(source, target, step, send_sem, recv_sem):
            return pltpu.make_async_remote_copy(
                src_ref=source,
                dst_ref=target,
                send_sem=send_sem.at[step],
                recv_sem=recv_sem.at[step],
                device_id={"space": 2 * others[step - 1] + core},
                device_id_type=MESH_ID,
            )

        def to_sibling(source, target, step, send_sem, recv_sem):
            return pltpu.make_async_remote_copy(
                src_ref=source,
                dst_ref=target,
                send_sem=send_sem.at[step],
                recv_sem=recv_sem.at[step],
                device_id={"space": sibling},
                device_id_type=MESH_ID,
            )

        def total(line, carry):
            tile, inside = line // (plan.tile // 64), line % (plan.tile // 64)
            own = pl.ds(pl.multiple_of(inside * 64, 64), 64)
            value = r.keep[plan.steps - plan.per + tile, own, :].astype(F32)
            value += sum(r.land[j, tile, own, :].astype(F32) for j in range(chans - 1))
            target = pl.ds(pl.multiple_of((line % (piece // 64)) * 64, 64), 64)
            r.a_send[line // (piece // 64), target, :] = value.astype(BF)
            return carry

        lax.fori_loop(0, local // 64, total, 0)
        collect(back, plan.pairs, plan.chunk, r.flat)
        wide = [
            send(r.a_send.at[others[step - 1]], r.a_land.at[level], step, r.s11, r.r11)
            for step in range(1, levels)
        ]
        for copy in wide:
            copy.start()
        copies = rows_backward(plan, r, r.unit, r.sums_before)
        r.table[...] = jnp.zeros_like(r.table)
        r.table[0:small, :] = r.sums[...]
        tail = sum(r.rest_land[j] for j in range(chans))
        for k in range(local // 128):
            lanes = slice(k * 128, (k + 1) * 128)
            r.table[small + k : small + k + 1, :] = tail[0:1, lanes]
        for k in range(3):
            line = jnp.concatenate([tail[1 + k : 2 + k, :features], jnp.zeros((1, 256 - features), F32)], axis=1)
            r.table[small + 8 + 2 * k : small + 9 + 2 * k, :] = line[:, :128]
            r.table[small + 9 + 2 * k : small + 10 + 2 * k, :] = line[:, 128:]
        for q in range(levels):
            r.b_send[q] = r.table[q * part : (q + 1) * part, :].astype(BF)
        thin = [
            send(r.b_send.at[others[step - 1]], r.b_land.at[level], step, r.s12, r.r12)
            for step in range(1, levels)
        ]
        for copy in thin:
            copy.start()
        wait_all(copies)
        result = input_gradient(plan, r, r.unit, r.dev)

        def finish(h, carry):
            r.out[h] = result(h)
            return carry

        lax.fori_loop(0, rows, finish, 0)
        a = r.a_send[level].astype(F32)
        b = r.b_send[level].astype(F32)
        for step in range(1, levels):
            wide[step - 1].wait()
            thin[step - 1].wait()
            source = lax.rem(level - step + levels, levels)
            a += r.a_land[source].astype(F32)
            b += r.b_land[source].astype(F32)
        r.a_own[...] = a.astype(BF)
        r.b_own[...] = b.astype(BF)
        last = [to_sibling(r.a_own, r.a_other.at[level], 0, r.s13, r.r13)]
        last += [to_sibling(r.b_own, r.b_other.at[level], 0, r.s14, r.r14)]
        again = []
        for step in range(1, levels):
            again.append(send(r.a_own, r.a_full.at[level], step, r.s15, r.r15))
            again.append(send(r.b_own, r.b_full.at[level], step, r.s16, r.r16))
        for copy in again + last:
            copy.start()
        r.a_full[level] = r.a_own[...]
        r.b_full[level] = r.b_own[...]
        moves.close()
        moves.open = []
        leave(r.out, r.lines, r.turn)
        moves.start(r.lines, r.lines_out)
        for step in range(1, levels):
            again[2 * step - 2].wait()
            again[2 * step - 1].wait()
            source = lax.rem(level - step + levels, levels)
            more = [to_sibling(r.a_full.at[source], r.a_other.at[source], step, r.s13, r.r13)]
            more += [to_sibling(r.b_full.at[source], r.b_other.at[source], step, r.s14, r.r14)]
            for copy in more:
                copy.start()
            last += more
        wait_all(last)
        moves.close()
        there.close(plan.pairs)
        back.close(plan.pairs)

    ins = {
        "g": two["out"],
        "came": two["came"],
        "second_x": two["second_x"],
        "sums_before": two["sums"],
        "rest_before": two["rest"],
        "grads_kept": two["grads_kept"],
        "mix": one["mix_kept"],
        **{
            key: one[key]
            for key in (
                "w_kept",
                "slope_kept",
                "active_kept",
                "entry_kept",
                "unit_wide_kept",
                "dev_wide_kept",
                "gathered_kept",
                "spec_kept",
                "first_kept",
                "second_kept",
                "unit_kept",
                "dev_kept",
            )
        },
        **args,
    }
    ins.update({key: tables[key] for key in ("rowinv_t", "row_t", "col", "colinv")})
    outs = {
        "lines_x": plan.lines,
        "lines_out": plan.lines,
        "a_full": ((levels, piece, width), BF),
        "a_other": ((levels, piece, width), BF),
        "b_full": ((levels, part, 128), BF),
        "b_other": ((levels, part, 128), BF),
    }
    blocks = pltpu.VMEM((plan.steps, plan.tile, width), BF)
    scratch = {
        "dma": sems(16),
        "dma2": sems(2, 2),
        "lines": scratch_of(plan.lines),
        "unit": scratch_of(plan.field),
        "dev": scratch_of(plan.dev),
        "out": scratch_of(plan.field),
        "spec": scratch_of(plan.kept),
        "first": scratch_of(plan.kept),
        "second": scratch_of(plan.kept),
        "w": scratch_of(plan.weights),
        "own": scratch_of(plan.by_cells),
        "leaving": scratch_of(plan.by_cells),
        "upper": scratch_of(plan.wide),
        "small": pltpu.VMEM((8, width), F32),
        "upb": pltpu.VMEM((16, plan.tile), F32),
        "sums": scratch_of(plan.sums),
        "rest": scratch_of(plan.rest),
        "rest_land": scratch_of(plan.rest),
        "prev": pltpu.VMEM((2, 2, plan.tile, width), BF),
        "keep": blocks,
        "give": pltpu.VMEM((2, plan.tile, width), BF),
        "take": pltpu.VMEM((3, plan.tile, width), BF),
        "land": pltpu.VMEM((chans - 1, plan.per, plan.tile, width), BF),
        "table": pltpu.VMEM((part * levels, 128), F32),
        "a_send": pltpu.VMEM((levels, piece, width), BF),
        "a_land": pltpu.VMEM((levels, piece, width), BF),
        "a_own": pltpu.VMEM((piece, width), BF),
        "b_send": pltpu.VMEM((levels, part, 128), BF),
        "b_land": pltpu.VMEM((levels, part, 128), BF),
        "b_own": pltpu.VMEM((part, 128), BF),
        **plan.exchange_scratch(False, False),
        **plan.spectral_scratch(),
        **ffn_scratch(plan),
        **norm_sums_scratch(plan),
        **{key + str(k): sems(chans) for k in (6, 7) for key in ("s", "r")},
        **{key + str(k): sems(plan.steps) for k in (9, 10) for key in ("s", "r")},
        **{key + str(k): sems(levels) for k in range(11, 17) for key in ("s", "r")},
    }
    in_place = [key for key in ins if key.endswith("_kept") and key != "mix_kept"] + ["second_x", "g"]
    return launch(
        body,
        ins,
        outs,
        scratch,
        "first_backward",
        2,
        {key: IN_PLACE for key in in_place},
        {key: IN_PLACE for key in ("lines_x", "lines_out")},
    )


def unpack_gradients(plan, parts, fields):
    features, small = plan.features, plan.small
    levels, piece, width = parts["a_full"].shape
    part = parts["b_full"].shape[1]
    local = levels * piece
    size = features // 2

    def body(r):
        swap = lax.rem(lax.axis_index("space"), 2) == 1
        for q in range(levels):
            own = slice(q * piece, (q + 1) * piece)
            mine, theirs = r.a_full[q].astype(F32), r.a_other[q].astype(F32)
            r.down[own, :] = jnp.where(swap, theirs, mine)
            r.up[:, own] = jnp.where(swap, mine, theirs).T
            r.table[q * part : (q + 1) * part, :] = r.b_full[q].astype(F32) + r.b_other[q].astype(F32)
        for layer, target in enumerate((r.mix_in, r.mix_out)):
            for half in range(2):
                for block in range(2):
                    start = ((layer * 2 + half) * 2 + block) * size
                    target[half, block] = r.table[start : start + size, :size]
        base = 8 * size

        def vector(k):
            return jnp.concatenate(
                [r.table[base + k : base + k + 1, :], r.table[base + 8 + k : base + 9 + k, : features - 128]], axis=1
            )

        for k, target in enumerate((r.bias_in, r.bias_in, r.bias_out, r.bias_out)):
            value = vector(k)
            target[k % 2, 0:1, :] = value[:, :size]
            target[k % 2, 1:2, :] = value[:, size:]
        r.pre_gain[...] = vector(4)
        r.pre_shift[...] = vector(5)
        r.upb[...] = jnp.concatenate(
            [r.table[small + k : small + k + 1, :] for k in range(local // 128)], axis=1
        ).reshape(local)

        def line(h, carry):
            for key in fields:
                getattr(r, key)[h] = getattr(r, key + "_in")[h]
            return carry

        lax.fori_loop(0, plan.rows, line, 0)
        for k, target in enumerate((r.post_gain, r.post_shift, r.downb)):
            target[...] = jnp.concatenate(
                [
                    r.table[small + 8 + 2 * k : small + 9 + 2 * k, :],
                    r.table[small + 9 + 2 * k : small + 10 + 2 * k, : features - 128],
                ],
                axis=1,
            )


    return launch(
        body,
        {
            **{key: parts[key] for key in ("a_full", "a_other", "b_full", "b_other")},
            **{key + "_in": value for key, value in fields.items()},
        },
        {
            "down": ((local, width), F32),
            "up": ((width, local), F32),
            "mix_in": ((2, 2, size, size), F32),
            "mix_out": ((2, 2, size, size), F32),
            "bias_in": ((2, 2, size), F32),
            "bias_out": ((2, 2, size), F32),
            "pre_gain": ((1, features), F32),
            "pre_shift": ((1, features), F32),
            "post_gain": ((1, features), F32),
            "post_shift": ((1, features), F32),
            "downb": ((1, features), F32),
            "upb": ((local,), F32),
            **{key: plan.lines for key in fields},
        },
        {"table": pltpu.VMEM((part * levels, 128), F32)},
        "unpack_gradients",
    )


def shards_fast(
    current_atmosphere,
    truth_one,
    truth_two,
    storm_codes,
    pre_gain,
    pre_shift,
    mix_weight_in,
    mix_bias_in,
    mix_weight_out,
    mix_bias_out,
    post_gain,
    post_shift,
    up_weight,
    up_bias,
    down_weight,
    down_bias,
):
    rows, merged = current_atmosphere.shape[1:]
    columns = W
    features = merged // columns
    plan = Plan(
        rows, features, columns, lax.axis_size("space"), lax.axis_size("chan"), up_weight.shape[1]
    )
    forward, inverse = row_constants(columns)
    column = column_constants(rows * plan.spaces, rows, 2)
    tables = {
        "row": jnp.stack(const_halves(forward)),
        "rowinv": const_halves(inverse)[0],
        "rowinv_t": const_halves(inverse.T)[0],
        "row_t": const_halves(forward.T)[0],
        "col": jnp.stack(const_halves(column)),
        "colinv": const_halves(column.T)[0],
    }

    def lines(flat):
        return flat.reshape(rows, merged // 128, 128)

    def flat(line_field):
        return line_field.reshape(1, rows, merged)

    one = launch_first(
        plan,
        {
            "lines_x": lines(current_atmosphere),
            "lines_t": lines(truth_one),
            "gain": pre_gain,
            "shift": pre_shift,
            "mix_in": mix_weight_in,
            "bias_in": mix_bias_in,
            "mix_out": mix_weight_out,
            "bias_out": mix_bias_out,
            "post_gain": post_gain,
            "post_shift": post_shift,
            "up": up_weight,
            "upb": up_bias,
            "down": down_weight,
            "downb": down_bias,
        },
        tables,
    )
    two = launch_second(
        plan,
        {"gain": pre_gain, "shift": pre_shift, "lines_t": lines(truth_two), "codes": storm_codes},
        one,
        tables,
    )
    three = launch_third(plan, {"gain": pre_gain}, one, two, tables)
    grads = unpack_gradients(
        plan, three, {"first": two["lines"], "second": three["lines_x"], "state": three["lines_out"]}
    )
    return (
        flat(grads["first"]),
        flat(grads["second"]),
        flat(grads["state"]),
        grads["pre_gain"].reshape(features),
        grads["pre_shift"].reshape(features),
        grads["mix_in"],
        grads["bias_in"],
        grads["mix_out"],
        grads["bias_out"],
        grads["post_gain"].reshape(features),
        grads["post_shift"].reshape(features),
        grads["up"],
        grads["upb"],
        grads["down"],
        grads["downb"].reshape(features),
    )


def suits(mesh):
    spaces, chans = mesh.shape["space"], mesh.shape["chan"]
    return (spaces, chans) == (8, 4)


def solution(mesh):
    in_specs = (
        P(None, "space", "chan"),
        P(None, "space", "chan"),
        P(None, "space", "chan"),
        P(),
        P("chan"),
        P("chan"),
        P(None, "chan", None, None),
        P(None, "chan", None),
        P(None, "chan", None, None),
        P(None, "chan", None),
        P("chan"),
        P("chan"),
        P(None, "chan"),
        P("chan"),
        P("chan", None),
        P("chan"),
    )
    out_specs = (
        P(None, "space", "chan"),
        P(None, "space", "chan"),
        P(None, "space", "chan"),
        P("chan"),
        P("chan"),
        P(None, "chan", None, None),
        P(None, "chan", None),
        P(None, "chan", None, None),
        P(None, "chan", None),
        P("chan"),
        P("chan"),
        P(None, "chan"),
        P("chan"),
        P("chan", None),
        P("chan"),
    )
    return jax.shard_map(shards_fast if suits(mesh) else shards, mesh=mesh, in_specs=in_specs, out_specs=out_specs, check_vma=False)
```

```python
import functools
import math
import types

import jax
import jax.numpy as jnp
import ml_dtypes
import numpy as np
from jax import lax
from jax.experimental import pallas as pl
from jax.experimental.pallas import tpu as pltpu
from jax.sharding import PartitionSpec as P

W = 160
KW = 81


NORM_EPS = 1e-06
SHRINK_LEVEL = 0.01
FULL_PRECISION = lax.Precision.HIGHEST


def exact_gelu(values):
    return jax.nn.gelu(values, approximate=False)


def shrink(values):
    return values - jnp.clip(values, -SHRINK_LEVEL, SHRINK_LEVEL)


def block_mix(values, matrix):
    return jnp.einsum("bhkni,nio->bhkno", values, matrix, precision=FULL_PRECISION)


def row_tables(columns, kept_modes, padded_modes):
    places = jnp.arange(columns, dtype=jnp.int32)[:, None]
    orders = jnp.arange(padded_modes, dtype=jnp.int32)[None, :]
    angles = 2.0 * math.pi / columns * (places * orders % columns).astype(jnp.float32)
    factor = 1.0 / math.sqrt(columns)
    single = jnp.logical_or(orders == 0, 2 * orders == columns)
    doubled = jnp.where(single, 1.0, 2.0).astype(jnp.float32)
    used = jnp.where(orders < kept_modes, 1.0, 0.0).astype(jnp.float32)
    return (
        jnp.cos(angles) * factor * used,
        -jnp.sin(angles) * factor * used,
        jnp.transpose(jnp.cos(angles) * doubled * factor * used),
        jnp.transpose(jnp.sin(angles) * doubled * factor * used),
    )


def along_rows(values, tables):
    return jnp.stack(
        [
            jnp.einsum("bhwc,wk->bhkc", values, tables[0], precision=FULL_PRECISION),
            jnp.einsum("bhwc,wk->bhkc", values, tables[1], precision=FULL_PRECISION),
        ]
    )


def along_rows_back(paired, tables):
    return jnp.einsum("bhkc,wk->bhwc", paired[0], tables[0], precision=FULL_PRECISION) + jnp.einsum(
        "bhkc,wk->bhwc", paired[1], tables[1], precision=FULL_PRECISION
    )


def rows_inverse(paired, tables):
    return jnp.einsum("bhkc,kw->bhwc", paired[0], tables[2], precision=FULL_PRECISION) - jnp.einsum(
        "bhkc,kw->bhwc", paired[1], tables[3], precision=FULL_PRECISION
    )


def rows_inverse_back(values, tables):
    return jnp.stack(
        [
            jnp.einsum("bhwc,kw->bhkc", values, tables[2], precision=FULL_PRECISION),
            -jnp.einsum("bhwc,kw->bhkc", values, tables[3], precision=FULL_PRECISION),
        ]
    )


def column_tables(height):
    orders = jnp.arange(height, dtype=jnp.int32)[:, None]
    places = jnp.arange(height, dtype=jnp.int32)[None, :]
    angles = 2.0 * math.pi / height * (orders * places % height).astype(jnp.float32)
    factor = 1.0 / math.sqrt(height)
    return (jnp.cos(angles) * factor, jnp.sin(angles) * factor)


def to_freq(matrix, values):
    return jnp.einsum("kh,bhmc->bkmc", matrix, values, precision=FULL_PRECISION)


def from_freq(matrix, values):
    return jnp.einsum("kh,bkmc->bhmc", matrix, values, precision=FULL_PRECISION)


def spectral_core(paired, w_first, b_first, w_second, b_second):
    samples, height, kept_modes, channels = paired.shape[1:]
    blocks, block_size = (w_first.shape[1], w_first.shape[2])
    cosine, sine_table = column_tables(height)
    real_in, imag_in = (paired[0], paired[1])
    split_form = (samples, height, kept_modes, blocks, block_size)
    real_part = (to_freq(cosine, real_in) + to_freq(sine_table, imag_in)).reshape(split_form)
    imag_part = (to_freq(cosine, imag_in) - to_freq(sine_table, real_in)).reshape(split_form)
    first_real = jax.nn.relu(
        block_mix(real_part, w_first[0]) - block_mix(imag_part, w_first[1]) + b_first[0]
    )
    first_imag = jax.nn.relu(
        block_mix(imag_part, w_first[0]) + block_mix(real_part, w_first[1]) + b_first[1]
    )
    joined_form = (samples, height, kept_modes, channels)
    second_real = shrink(
        block_mix(first_real, w_second[0]) - block_mix(first_imag, w_second[1]) + b_second[0]
    ).reshape(joined_form)
    second_imag = shrink(
        block_mix(first_imag, w_second[0]) + block_mix(first_real, w_second[1]) + b_second[1]
    ).reshape(joined_form)
    out_real = from_freq(cosine, second_real) - from_freq(sine_table, second_imag)
    out_imag = from_freq(cosine, second_imag) + from_freq(sine_table, second_real)
    return jnp.stack([out_real, out_imag])


def column_layout(paired):
    return lax.all_to_all(paired, "space", split_axis=3, concat_axis=2, tiled=True)


def row_layout(paired):
    return lax.all_to_all(
        paired.astype(jnp.bfloat16), "space", split_axis=2, concat_axis=3, tiled=True
    ).astype(paired.dtype)


def norm_forward(values, gain, offset):
    width_all = values.shape[-1] * lax.axis_size("chan")
    totals = lax.psum((jnp.sum(values, axis=-1), jnp.sum(values * values, axis=-1)), "chan")
    average = totals[0] / width_all
    variance = totals[1] / width_all - average * average
    inverse_dev = lax.rsqrt(variance + NORM_EPS)[..., None]
    scaled = (values - average[..., None]) * inverse_dev
    return (scaled * gain + offset, (scaled, inverse_dev))


def norm_backward(gradient, gain, saved):
    scaled, inverse_dev = saved
    width_all = scaled.shape[-1] * lax.axis_size("chan")
    scaled_grad = gradient * gain
    totals = lax.psum(
        (jnp.sum(scaled_grad, axis=-1), jnp.sum(scaled_grad * scaled, axis=-1)), "chan"
    )
    values_grad = inverse_dev * (
        scaled_grad - totals[0][..., None] / width_all - scaled * (totals[1][..., None] / width_all)
    )
    return (
        values_grad,
        jnp.sum(gradient * scaled, axis=(0, 1, 2)),
        jnp.sum(gradient, axis=(0, 1, 2)),
    )


def shards(
    current_atmosphere,
    truth_one,
    truth_two,
    storm_codes,
    pre_gain,
    pre_shift,
    mix_weight_in,
    mix_bias_in,
    mix_weight_out,
    mix_bias_out,
    post_gain,
    post_shift,
    up_weight,
    up_bias,
    down_weight,
    down_bias,
):
    samples, rows_here, merged = current_atmosphere.shape
    columns = W
    channels = merged // columns
    total_rows = samples * rows_here * columns
    space_count = lax.axis_size("space")
    padded_modes = (KW + space_count - 1) // space_count * space_count
    tables = row_tables(columns, KW, padded_modes)

    def to_cells(flat_field):
        return jnp.transpose(
            flat_field.reshape(samples, rows_here, channels, columns), (0, 1, 3, 2)
        )

    def to_flat(cell_field):
        return jnp.transpose(cell_field, (0, 1, 3, 2)).reshape(samples, rows_here, merged)

    start_cells = to_cells(current_atmosphere)
    target_one = to_cells(truth_one)
    target_two = to_cells(truth_two)
    weight_of = (storm_codes.astype(jnp.float32) / 64.0).reshape(-1, 1, 1, 1)
    full_up, full_down, full_up_bias, full_down_bias = (up_weight, down_weight, up_bias, down_bias)

    def mlp_forward(inputs):
        gathered = lax.all_gather(inputs, "chan", axis=1, tiled=True)
        hidden = jnp.dot(
            gathered, full_up, preferred_element_type=jnp.float32
        ) + full_up_bias.astype(jnp.float32)
        active_full, gelu_pull = jax.vjp(exact_gelu, hidden)
        active = active_full.astype(jnp.bfloat16)
        product = jnp.dot(active, full_down, preferred_element_type=jnp.float32)
        output = lax.psum_scatter(
            product.astype(jnp.bfloat16), "chan", scatter_dimension=1, tiled=True
        ).astype(jnp.float32) + full_down_bias.astype(jnp.float32)
        return (output, (gathered, gelu_pull, active))

    def mlp_backward(gradient, saved):
        gathered, gelu_pull, active = saved
        grad_low = gradient.astype(jnp.bfloat16)
        grad_rows = lax.all_gather(grad_low, "chan", axis=1, tiled=True)
        down_bias_grad = jnp.sum(grad_low.astype(jnp.float32), axis=0)
        down_grad = jnp.dot(active.T, grad_rows, preferred_element_type=jnp.float32)
        active_grad = jnp.dot(grad_rows, full_down.T, preferred_element_type=jnp.float32)
        hidden_grad = gelu_pull(active_grad)[0].astype(jnp.bfloat16)
        up_grad = jnp.dot(gathered.T, hidden_grad, preferred_element_type=jnp.float32)
        up_bias_grad = jnp.sum(hidden_grad.astype(jnp.float32), axis=0)
        input_part = jnp.dot(hidden_grad, full_up.T, preferred_element_type=jnp.float32)
        input_grad = lax.psum_scatter(
            input_part.astype(jnp.bfloat16), "chan", scatter_dimension=1, tiled=True
        ).astype(jnp.float32)
        return (input_grad, (up_grad, up_bias_grad, down_grad, down_bias_grad))

    def forward_block(values):
        normed, first_saved = norm_forward(values, pre_gain, pre_shift)
        modal_in = column_layout(along_rows(normed, tables))
        filtered, core_pull = jax.vjp(
            spectral_core, modal_in, mix_weight_in, mix_bias_in, mix_weight_out, mix_bias_out
        )
        middle = rows_inverse(row_layout(filtered), tables) + normed + values
        entry, second_residuals = norm_forward(middle, post_gain, post_shift)
        output, mlp_saved = mlp_forward(entry.astype(jnp.bfloat16).reshape(total_rows, channels))
        return (
            output.reshape(values.shape) + middle,
            (first_saved, core_pull, second_residuals, mlp_saved),
        )

    def backward_block(gradient, saved):
        first_saved, core_pull, second_residuals, mlp_saved = saved
        mlp_grad, dense_grads = mlp_backward(gradient.reshape(total_rows, channels), mlp_saved)
        middle_part, post_gain_grad, post_shift_grad = norm_backward(
            mlp_grad.reshape(gradient.shape), post_gain, second_residuals
        )
        middle_grad = middle_part + gradient
        filter_grads = core_pull(column_layout(rows_inverse_back(middle_grad, tables)))
        normed_grad = along_rows_back(row_layout(filter_grads[0]), tables) + middle_grad
        input_part, pre_gain_grad, pre_shift_grad = norm_backward(
            normed_grad, pre_gain, first_saved
        )
        return (
            input_part + middle_grad,
            (pre_gain_grad, pre_shift_grad)
            + tuple(filter_grads[1:])
            + (post_gain_grad, post_shift_grad)
            + dense_grads,
        )

    first_out, first_saved_all = forward_block(start_cells)
    second_out, second_saved_all = forward_block(first_out)
    carried, grads_late = backward_block(weight_of * (second_out - target_two), second_saved_all)
    input_grad, grads_early = backward_block(
        weight_of * (first_out - target_one) + carried, first_saved_all
    )
    summed = jax.tree.map(jnp.add, grads_early, grads_late)
    (
        sum_pre_gain,
        sum_pre_shift,
        sum_mix_w_in,
        summed_mixing_bias_input,
        sum_mix_w_out,
        sum_mix_b_out,
        sum_post_gain,
        sum_post_shift,
        sum_up,
        sum_up_bias,
        sum_down,
        sum_down_bias,
    ) = summed
    totals = (
        lax.psum(sum_pre_gain.astype(jnp.bfloat16), "space").astype(jnp.float32),
        lax.psum(sum_pre_shift.astype(jnp.bfloat16), "space").astype(jnp.float32),
        lax.psum(sum_mix_w_in.astype(jnp.bfloat16), "space").astype(jnp.float32),
        lax.psum(summed_mixing_bias_input.astype(jnp.bfloat16), "space").astype(jnp.float32),
        lax.psum(sum_mix_w_out.astype(jnp.bfloat16), "space").astype(jnp.float32),
        lax.psum(sum_mix_b_out.astype(jnp.bfloat16), "space").astype(jnp.float32),
        lax.psum(sum_post_gain.astype(jnp.bfloat16), "space").astype(jnp.float32),
        lax.psum(sum_post_shift.astype(jnp.bfloat16), "space").astype(jnp.float32),
        lax.psum(sum_up.astype(jnp.bfloat16), "space").astype(jnp.float32),
        lax.psum(sum_up_bias.astype(jnp.bfloat16), "space").astype(jnp.float32),
        lax.psum(sum_down.astype(jnp.bfloat16), "space").astype(jnp.float32),
        lax.psum(sum_down_bias.astype(jnp.bfloat16), "space").astype(jnp.float32),
    )
    return (to_flat(first_out), to_flat(second_out), to_flat(input_grad)) + tuple(totals)


BF = jnp.bfloat16
F32 = jnp.float32
MESH_ID = pl.DeviceIdType.MESH
VMEM_BYTES = 66 * 1024 * 1024 - 1024 * 1024


def mm(a, b):
    return jnp.dot(a, b, preferred_element_type=F32)


def mm_nt(a, b):
    return lax.dot_general(a, b, (((1,), (1,)), ((), ())), preferred_element_type=F32)


def mm_tn(a, b):
    return lax.dot_general(a, b, (((0,), (0,)), ((), ())), preferred_element_type=F32)


def halves(v):
    high = v.astype(BF)
    return high, (v - high.astype(F32)).astype(BF)


def mm3(a, b):
    return mm(a[0], b[0]) + (mm(a[0], b[1]) + mm(a[1], b[0]))


def const_halves(table):
    table = np.asarray(table, np.float32)
    high = table.astype(ml_dtypes.bfloat16)
    low = (table - high.astype(np.float32)).astype(ml_dtypes.bfloat16)
    return jnp.asarray(high), jnp.asarray(low)


def row_constants(columns):
    half = columns // 2
    place = np.arange(columns)
    mode = np.arange(half)
    angle = 2.0 * np.pi * np.outer(mode, place) / columns
    real = np.cos(angle)
    imag = -np.sin(angle)
    imag[0] = np.cos(np.pi * place)
    forward = np.concatenate([real, imag]) / np.sqrt(columns)
    weight = np.where(mode == 0, 1.0, 2.0)
    inverse = (forward * np.concatenate([weight, weight])[:, None]).T
    return forward, inverse


def column_constants(height, rows, group):
    owners = height // rows
    angle = 2.0 * np.pi * np.outer(np.arange(height), np.arange(height)) / height
    cosine = np.cos(angle) / np.sqrt(height)
    sine = np.sin(angle) / np.sqrt(height)

    def spread(matrix):
        wide = np.zeros((group, height, owners, group, rows))
        for column in range(group):
            wide[column, :, :, column, :] = matrix.reshape(height, owners, rows)
        return wide.reshape(group * height, owners * group * rows)

    cosine, sine = spread(cosine), spread(sine)
    return np.block([[cosine, sine], [-sine, cosine]])


def signal_peers(axis, count, barrier):
    me = lax.axis_index(axis)
    for step in range(1, count):
        pl.semaphore_signal(
            barrier, inc=1, device_id={axis: lax.rem(me + step, count)}, device_id_type=MESH_ID
        )


def push(axis, count, step, source, target, send_sem, recv_sem):
    peer = lax.rem(lax.axis_index(axis) + step, count)
    return pltpu.make_async_remote_copy(
        src_ref=source,
        dst_ref=target,
        send_sem=send_sem.at[step],
        recv_sem=recv_sem.at[step],
        device_id={axis: peer},
        device_id_type=MESH_ID,
    )


def params(collective_id=None):
    return pltpu.CompilerParams(
        collective_id=collective_id,
        has_side_effects=collective_id is not None,
        vmem_limit_bytes=VMEM_BYTES,
    )


def launch(body, ins, outs, scratch, name, collective_id=None, in_specs=None, out_specs=None, grid=()):
    in_specs, out_specs = in_specs or {}, out_specs or {}
    names = list(ins) + list(outs) + list(scratch)
    whole = pl.BlockSpec(memory_space=pltpu.VMEM)
    results = pl.pallas_call(
        lambda *refs: body(types.SimpleNamespace(**dict(zip(names, refs)))),
        grid=grid,
        in_specs=[in_specs.get(key, whole) for key in ins],
        out_specs=[out_specs.get(key, whole) for key in outs],
        out_shape=[jax.ShapeDtypeStruct(*outs[key]) for key in outs],
        scratch_shapes=list(scratch.values()),
        compiler_params=params(collective_id),
        name=name,
    )(*ins.values())
    return dict(zip(outs, results))


IN_PLACE = pl.BlockSpec(memory_space=pl.ANY)


def sems(*counts):
    return pltpu.SemaphoreType.DMA(counts)


def run_copies(copies):
    for copy in copies:
        copy.start()
    for copy in copies:
        copy.wait()


def cells_from_lines(lines_ref, h, scratch_ref):
    features = scratch_ref.shape[1]
    per = 640 // W
    groups = features // per
    wide = jnp.concatenate(
        [lines_ref[h, pl.ds(part, groups, stride=5), :] for part in range(5)], axis=1
    )
    for part in range(per):
        piece = wide[:, part * W : (part + 1) * W]
        scratch_ref[0, pl.ds(part, groups, stride=per), :] = piece[:, :128]
        scratch_ref[1, pl.ds(part, groups, stride=per), :] = jnp.concatenate(
            [piece[:, 128:], jnp.zeros((groups, 256 - W), F32)], axis=1
        )
    return jnp.concatenate([scratch_ref[0], scratch_ref[1][:, : W - 128]], axis=1)


def enter(lines_ref, cells_ref, scratch_ref):
    def row(h, carry):
        cells_ref[h] = cells_from_lines(lines_ref, h, scratch_ref).T
        return carry

    lax.fori_loop(0, lines_ref.shape[0], row, 0)


def leave(cells_ref, lines_ref, scratch_ref):
    features = scratch_ref.shape[1]
    per = 640 // W
    groups = features // per

    def row(h, carry):
        block = cells_ref[h].T
        scratch_ref[0] = block[:, :128]
        scratch_ref[1] = jnp.concatenate([block[:, 128:], jnp.zeros((features, 256 - W), F32)], axis=1)
        wide = jnp.concatenate(
            [
                piece
                for part in range(per)
                for piece in (
                    scratch_ref[0, pl.ds(part, groups, stride=per), :],
                    scratch_ref[1, pl.ds(part, groups, stride=per), :][:, : W - 128],
                )
            ],
            axis=1,
        )
        for part in range(5):
            lines_ref[h, pl.ds(part, groups, stride=5), :] = wide[:, part * 128 : (part + 1) * 128]
        return carry

    lax.fori_loop(0, lines_ref.shape[0], row, 0)


def pack_lanes(flat_ref, place, real, imag):
    flat_ref[0, place, :] = real[:, :128]
    flat_ref[1, place, :] = imag[:, :128]
    flat_ref[2, place, :] = jnp.concatenate([real[:, 128:], imag[:, 128:]], axis=1)


def join_lanes(first, second, rest):
    real = jnp.concatenate([first, rest[:, :64]], axis=1)
    imag = jnp.concatenate([second, rest[:, 64:]], axis=1)
    return real, imag


def unpack_lanes(flat_ref, place):
    return join_lanes(flat_ref[0, place, :], flat_ref[1, place, :], flat_ref[2, place, :])


LEVEL = 32000.0


class Exchange:
    def __init__(self, fixed, spaces, thick, send_ref, recv_ref, send_sem, recv_sem, scales=None):
        self.fixed, self.scales = fixed, scales
        self.spaces, self.thick = spaces, thick
        self.send_ref, self.recv_ref = send_ref, recv_ref
        self.send_sem, self.recv_sem = send_sem, recv_sem
        self.me = lax.axis_index("space")

    @staticmethod
    def shape(fixed, spaces, thick, pairs):
        return pltpu.VMEM((pairs, spaces, 3 * thick, 128), jnp.int16 if fixed else BF)

    def copy(self, p, step):
        peer = lax.rem(self.me + step, self.spaces)
        return pltpu.make_async_remote_copy(
            src_ref=self.send_ref.at[p, peer],
            dst_ref=self.recv_ref.at[p, self.me],
            send_sem=self.send_sem.at[p, step],
            recv_sem=self.recv_sem.at[p, step],
            device_id={"space": peer},
            device_id_type=MESH_ID,
        )

    def scale_copy(self, step):
        own_ref, all_ref, send_sem, recv_sem = self.scales
        return push("space", self.spaces, step, own_ref, all_ref.at[self.me], send_sem, recv_sem)

    def send_scales(self, flat_ref):
        own_ref, all_ref = self.scales[:2]
        largest = jnp.max(jnp.abs(flat_ref[...]), axis=1)
        own_ref[0:3, :] = jnp.maximum(largest, 1e-30) * (1.0 / LEVEL)
        own_ref[3:8, :] = jnp.ones((5, 128), F32)
        for step in range(1, self.spaces):
            self.scale_copy(step).start()
        all_ref[self.me] = own_ref[...]
        self.factor = 1.0 / own_ref[...]

    def encode(self, values):
        if not self.fixed:
            return jnp.concatenate([values[k] for k in range(3)], axis=0).astype(BF)
        lines = [jnp.round(values[k] * self.factor[k : k + 1]) for k in range(3)]
        return jnp.concatenate(lines, axis=0).astype(jnp.int32).astype(jnp.int16)

    def send(self, p, flat_ref, start_of):
        for step in list(range(1, self.spaces)) + [0]:
            peer = lax.rem(self.me + step, self.spaces)
            rows = pl.ds(pl.multiple_of(start_of(peer), 8), self.thick)
            coded = self.encode(flat_ref[:, rows, :])
            if step:
                self.send_ref[p, peer] = coded
                self.copy(p, step).start()
            else:
                self.recv_ref[p, peer] = coded

    def arrive(self, p):
        for step in range(1, self.spaces):
            self.copy(p, step).wait_recv()

    def arrive_scales(self):
        for step in range(1, self.spaces):
            self.scale_copy(step).wait_recv()

    def take(self, p, source):
        coded = self.recv_ref[p, source]
        values = (coded.astype(jnp.int32) if self.fixed else coded).astype(F32)
        parts = [values[k * self.thick : (k + 1) * self.thick] for k in range(3)]
        if self.fixed:
            scale = self.scales[1][source]
            parts = [part * scale[k : k + 1] for k, part in enumerate(parts)]
        return parts

    def close(self, pairs):
        def pair(p, carry):
            for step in range(1, self.spaces):
                self.copy(p, step).wait_send()
            return carry

        lax.fori_loop(0, pairs, pair, 0)
        if self.fixed:
            for step in range(1, self.spaces):
                self.scale_copy(step).wait_send()


def pair_inputs(q, exchange, even_ref):
    p = jnp.maximum(q - 1, 0)

    @pl.when(q != 1)
    def _():
        exchange.arrive(p)

    if exchange.fixed:

        @pl.when(q == 0)
        def _():
            exchange.arrive_scales()

    extra = (q == 0).astype(F32)
    zeroth = jnp.logical_and(exchange.me == 0, p == 0).astype(F32)
    parts = [join_lanes(*exchange.take(p, s)) for s in range(exchange.spaces)]
    real = jnp.concatenate([part[0] for part in parts], axis=0)
    imag = jnp.concatenate([part[1] for part in parts], axis=0)
    chosen = imag * (even_ref[...] * zeroth)
    real = real * (1.0 - extra) + chosen * extra
    imag = (imag - chosen) * (1.0 - extra)
    return p, zeroth, jnp.concatenate([real, imag], axis=0)


def pair_outputs(q, p, zeroth, result, exchange, even_ref, kept_ref, stage_ref):
    half = result.shape[0] // 2
    real, imag = result[:half], result[half:]

    @pl.when(q == 0)
    def _():
        kept_ref[...] = real

    @pl.when(q > 0)
    def _():
        chosen = even_ref[...] * zeroth
        pack_lanes(stage_ref, slice(None), real, imag * (1.0 - chosen) + kept_ref[...] * chosen)
        exchange.send(p, stage_ref, lambda peer: peer * exchange.thick)


def collect(exchange, pairs, chunk, flat_ref):
    def pair(p, carry):
        exchange.arrive(p)
        for s in range(exchange.spaces):
            rows = pl.ds(pl.multiple_of(s * chunk + p * exchange.thick, 8), exchange.thick)
            for k, part in enumerate(exchange.take(p, s)):
                flat_ref[k, rows, :] = part
        return carry

    lax.fori_loop(0, pairs, pair, 0)


def send_modes(exchange, pairs, chunk, flat_ref):
    if exchange.fixed:
        exchange.send_scales(flat_ref)

    def pair(p, carry):
        exchange.send(p, flat_ref, lambda peer: peer * chunk + p * exchange.thick)
        return carry

    lax.fori_loop(0, pairs, pair, 0)


class Plan:
    def __init__(self, rows, features, columns, spaces, chans, local):
        self.rows, self.features, self.columns = rows, features, columns
        self.spaces, self.chans, self.local = spaces, chans, local
        self.modes = columns // 2
        self.total = self.modes * rows
        self.chunk = self.total // spaces
        self.thick = 2 * rows
        self.half = self.thick * spaces
        self.pairs = self.chunk // self.thick
        self.cells = rows * columns // chans
        self.share = rows // chans
        self.width = features * chans
        self.tile = 256
        self.per = local // self.tile
        self.steps = chans * self.per
        self.size = features // 2
        self.small = 8 * self.size + 16
        self.field = ((rows, columns, features), F32)
        self.by_cells = ((chans, self.share, columns // 2 * 3, 128), BF)
        self.wide = ((self.cells, self.width), BF)
        self.tiles = ((self.steps, self.cells, self.tile), BF)
        self.lines = ((rows, features * columns // 128, 128), F32)
        self.dev = ((rows, columns, 8), F32)
        self.dev_wide = ((self.cells, 128), F32)
        self.kept = ((self.pairs + 1, 2 * self.half, features), BF)
        self.mix = ((2, 2, 2, features, features), BF)
        self.weights = ((2, chans, local, self.width), BF)
        self.rest = ((chans, 8, local), F32)
        self.sums = ((self.small, 128), F32)
        self.grads = ((2, self.steps, self.tile, self.width), BF)
        self.vectors = ((chans, 8, local), F32)

    def exchange_scratch(self, fixed_there, fixed_back):
        made = {}
        for name, fixed in (("1", fixed_there), ("2", fixed_back)):
            shape = Exchange.shape(fixed, self.spaces, self.thick, self.pairs)
            made["send" + name] = made["recv" + name] = shape
            made["s" + name] = made["r" + name] = sems(self.pairs, self.spaces)
        if fixed_there:
            made["scale"] = pltpu.VMEM((8, 128), F32)
            made["scale_all"] = pltpu.VMEM((self.spaces, 8, 128), F32)
            made["s20"] = made["r20"] = sems(self.spaces)
        return made

    def spectral_scratch(self):
        return {
            "flat": pltpu.VMEM((3, self.total, 128), F32),
            "stage": pltpu.VMEM((3, self.half, 128), F32),
            "last": pltpu.VMEM((self.half, self.features), F32),
            "turn": pltpu.VMEM((2, self.features, 128), F32),
            "even": pltpu.VMEM((self.half, self.features), F32),
        }


def pack_cells(value):
    side = value.shape[0] // 2
    rest = value[:, 128:]
    return jnp.concatenate([value[:, :128], jnp.concatenate([rest[:side], rest[side:]], axis=1)], axis=0)


def unpack_cells(packed):
    columns = packed.shape[0] // 3 * 2
    rest = packed[columns:]
    rest = jnp.concatenate([rest[:, :64], rest[:, 64:]], axis=0)
    return jnp.concatenate([packed[:columns], rest], axis=1)


def scratch_of(shaped):
    return pltpu.VMEM(*shaped)


def mark_even(plan, r):
    row = lax.broadcasted_iota(jnp.int32, (plan.half, plan.features), 0)
    r.even[...] = jnp.where(lax.rem(lax.div(row, plan.rows), 2) == 0, 1.0, 0.0)


def greet(plan):
    barrier = pltpu.get_barrier_semaphore()
    signal_peers("space", plan.spaces, barrier)
    signal_peers("chan", plan.chans, barrier)
    return lambda: pl.semaphore_wait(barrier, plan.spaces + plan.chans - 2)


def spread_chan(plan, source_ref, target_ref, send_sem, recv_sem):
    me = lax.axis_index("chan")
    copies = []
    for step in range(1, plan.chans):
        peer = lax.rem(me + step, plan.chans)
        copy = push("chan", plan.chans, step, source_ref.at[peer], target_ref.at[me], send_sem, recv_sem)
        copy.start()
        copies.append(copy)
    target_ref[me] = source_ref[me]
    return copies


def wait_all(copies):
    for copy in copies:
        copy.wait()


def rows_to_modes(plan, table, flat_ref, value_of, exact):
    def row(h, carry):
        value = value_of(h)
        out = mm3(table, halves(value)) if exact else mm(table, value.astype(BF))
        pack_lanes(flat_ref, pl.ds(h, plan.modes, stride=plan.rows), out[: plan.modes], out[plan.modes :])
        return carry

    lax.fori_loop(0, plan.rows, row, 0)


def filter_forward(plan, r, there, back, aside=None):
    half = plan.half

    def filter_pair(q, carry):
        if aside is not None:
            pl.when(q == plan.pairs)(aside)
        p, zeroth, block = pair_inputs(q, there, r.even)
        spec = mm3((r.col[0], r.col[1]), halves(block))
        r.spec[q] = spec.astype(BF)
        parts = halves(spec)
        straight = mm3(parts, (r.mix[0, 0, 0], r.mix[0, 0, 1]))
        crossed = mm3(parts, (r.mix[0, 1, 0], r.mix[0, 1, 1]))
        first = jnp.concatenate(
            [
                jnp.maximum(straight[:half] - crossed[half:] + r.bias[0:1], 0.0),
                jnp.maximum(straight[half:] + crossed[:half] + r.bias[1:2], 0.0),
            ],
            axis=0,
        )
        r.first[q] = first.astype(BF)
        parts = halves(first)
        straight = mm3(parts, (r.mix[1, 0, 0], r.mix[1, 0, 1]))
        crossed = mm3(parts, (r.mix[1, 1, 0], r.mix[1, 1, 1]))
        second = jnp.concatenate(
            [
                straight[:half] - crossed[half:] + r.bias[2:3],
                straight[half:] + crossed[:half] + r.bias[3:4],
            ],
            axis=0,
        )
        second = second - jnp.clip(second, -SHRINK_LEVEL, SHRINK_LEVEL)
        r.second[q] = second.astype(BF)
        result = mm(r.colinv[...], r.second[q])
        pair_outputs(q, p, zeroth, result, back, r.even, r.last, r.stage)
        return carry

    lax.fori_loop(0, plan.pairs + 1, filter_pair, 0)


def modes_to_rows(plan, flat_ref, h):
    real, imag = unpack_lanes(flat_ref, pl.ds(h, plan.modes, stride=plan.rows))
    return jnp.concatenate([real, imag], axis=0)


def rows_of_chunks(plan, row, send_chunk):
    me = lax.axis_index("chan")
    for step in list(range(1, plan.chans)) + [0]:
        peer = lax.rem(me + step, plan.chans)

        def one(i, carry):
            row(peer * plan.share + i, peer, i)
            return carry

        lax.fori_loop(0, plan.share, one, 0)
        send_chunk(step, peer)


def rows_forward(plan, r, unit_ref, x_ref, middle_ref):
    me = lax.axis_index("chan")
    gain, shift = r.gain[...].reshape(1, -1), r.shift[...].reshape(1, -1)
    copies = []

    def row(h, peer, place):
        block = modes_to_rows(plan, r.flat, h)
        out = mm(r.rowinv[...], block.astype(BF))
        middle = out + (unit_ref[h] * gain + shift) + x_ref[h]
        middle_ref[h] = middle
        r.own[peer, place] = pack_cells(middle).astype(BF)

    def send_chunk(step, peer):
        if step:
            copy = push("chan", plan.chans, step, r.own.at[peer], r.mid.at[me], r.s3, r.r3)
            copy.start()
            copies.append(copy)
        else:
            r.mid[me] = r.own[me]

    rows_of_chunks(plan, row, send_chunk)
    return copies


class Block:
    def __init__(self, plan, group, side):
        self.group, self.side, self.size = group, side, plan.columns // 2
        start = group * plan.columns + side * self.size
        self.cells = pl.ds(pl.multiple_of(start, 16), self.size)
        self.front = slice(side * self.size, (side + 1) * self.size)
        self.back = slice(plan.columns, plan.columns + self.size)
        self.lanes = slice(64 * side, 64 * side + 64)

    def get(self, chunks_ref):
        parts = []
        for j in range(chunks_ref.shape[0]):
            parts.append(chunks_ref[j, self.group, self.front, :].astype(F32))
            parts.append(chunks_ref[j, self.group, self.back, self.lanes].astype(F32))
        return jnp.concatenate(parts, axis=1)

    def put(self, chunks_ref, value):
        chans = chunks_ref.shape[0]
        features = value.shape[1] // chans
        for j in range(chans):
            part = value[:, j * features : (j + 1) * features].astype(BF)
            chunks_ref[j, self.group, self.front, :] = part[:, :128]
            chunks_ref[j, self.group, self.back, self.lanes] = part[:, 128:]


def by_blocks(plan, step):
    def one(group, carry):
        for side in range(2):
            step(Block(plan, group, side))
        return carry

    lax.fori_loop(0, plan.share, one, 0)


def full_vector(gathered_ref, start, size):
    chans = gathered_ref.shape[0]
    return jnp.concatenate([gathered_ref[j, 1:2, start : start + size] for j in range(chans)], axis=1)


def moments(value):
    mean = jnp.mean(value, axis=1, keepdims=True)
    centred = value - mean
    return mean, centred, lax.rsqrt(jnp.mean(centred * centred, axis=1, keepdims=True) + NORM_EPS)


ERF = (0.254829592, -0.284496736, 1.421413741, -1.453152027, 1.061405429)


def gelu_and_slope(v):
    e = jnp.exp2(v * v * (-0.5 / math.log(2.0)))
    below = 1.0 + (0.3275911 * math.sqrt(0.5)) * jnp.abs(v)
    t = pl.reciprocal(below, approx=True)
    t = t * (2.0 - below * t)
    c = [0.5 * k for k in ERF]
    tail = (e * t) * (c[0] + t * (c[1] + t * (c[2] + t * (c[3] + t * c[4]))))
    below = jnp.where(v >= 0.0, 1.0 - tail, tail)
    active = v * below
    return active, below + (v * (1.0 / math.sqrt(2.0 * math.pi))) * e


def three_parts(v):
    a = v.astype(BF)
    rest = v - a.astype(F32)
    b = rest.astype(BF)
    return [a, b, (rest - b.astype(F32)).astype(BF)]


def tile_of(plan, t):
    return t // plan.per, pl.ds(pl.multiple_of((t % plan.per) * plan.tile, plan.tile), plan.tile)


def up_tile(plan, r, t):
    j, place = tile_of(plan, t)
    return r.w[0, j, :, place]


def down_tile(plan, r, t):
    j, place = tile_of(plan, t)
    return r.w[1, j, place, :]


def ffn_scratch(plan):
    shape = (plan.cells, plan.tile)
    made = {key: pltpu.VMEM(shape, F32) for key in ("wide_a", "wide_b")}
    made.update({key: pltpu.VMEM(shape, BF) for key in ("thin_a", "thin_b")})
    made.update(
        total=pltpu.VMEM((plan.cells, plan.width), F32),
        entry=scratch_of(plan.wide),
        unit_wide=scratch_of(plan.wide),
        dev_wide=scratch_of(plan.dev_wide),
        active=scratch_of(plan.tiles),
        slope=scratch_of(plan.tiles),
        gathered=scratch_of(plan.vectors),
    )
    return made


def staggered(plan, r, lead, turn, trail, ready=None):
    last = plan.steps - 1
    third = plan.cells // 3
    side = plan.cells // 2
    parts = plan.width // plan.tile
    r.thin_b[...] = jnp.zeros_like(r.thin_b)
    for k in range(2):
        r.wide_a[k * side : (k + 1) * side, :] = lead(0, slice(k * side, (k + 1) * side))

    def half_step(t, wide_now, wide_next, thin_past, thin_now):
        ahead, behind = jnp.minimum(t + 1, last), jnp.maximum(t - 1, 0)
        for k in range(3):
            place = slice(k * third, (k + 1) * third)
            thin_now[place, :] = turn(wide_now[place, :], t, place, k == 0)
            if k < 2:
                own = slice(k * side, (k + 1) * side)
                wide_next[own, :] = lead(ahead, own)
            trail(thin_past[...], behind, slice(k * parts // 3 * plan.tile, (k + 1) * parts // 3 * plan.tile))

    def pair(u, carry):
        if ready is not None:
            for chunk in range(1, plan.chans):
                pl.when(u == (chunk * plan.per - 1) // 2)(functools.partial(ready, chunk))
        half_step(2 * u, r.wide_a, r.wide_b, r.thin_b, r.thin_a)
        half_step(2 * u + 1, r.wide_b, r.wide_a, r.thin_a, r.thin_b)
        return carry

    lax.fori_loop(0, plan.steps // 2, pair, 0)
    trail(r.thin_b[...], last, slice(0, plan.width))


def ffn_forward(plan, r):
    gain = full_vector(r.gathered, 0, plan.features)
    shift = full_vector(r.gathered, plan.features, plan.features)
    bias = full_vector(r.gathered, 2 * plan.features, plan.features)

    def prepare(block):
        place = block.cells
        mean, centred, inverse = moments(block.get(r.mid))
        unit = centred * inverse
        r.unit_wide[place, :] = unit.astype(BF)
        r.dev_wide[place, :] = jnp.broadcast_to(inverse, (block.size, 128))
        r.entry[place, :] = (unit * gain + shift).astype(BF)
        r.total[place, :] = jnp.broadcast_to(bias, (block.size, plan.width))

    by_blocks(plan, prepare)

    def lead(t, rows):
        j, place = tile_of(plan, t)
        return mm(r.entry[rows, :], up_tile(plan, r, t)) + r.gathered[j, 0:1, place]

    def turn(value, t, rows, opening):
        active, slope = gelu_and_slope(value)
        active = active.astype(BF)
        r.active[t, rows, :] = active
        r.slope[t, rows, :] = slope.astype(BF)
        return active

    def trail(active, t, lanes):
        j, place = tile_of(plan, t)
        r.total[:, lanes] += mm(active, r.w[1, j, place, lanes])

    staggered(plan, r, lead, turn, trail)


def ffn_backward(plan, r, ready=None):
    r.small[...] = jnp.zeros_like(r.small)
    r.total[...] = jnp.zeros_like(r.total)

    def lead(t, rows):
        return mm_nt(r.upper[rows, :], down_tile(plan, r, t))

    def turn(value, t, rows, opening):
        lower = value * r.slope[t, rows, :].astype(F32)
        bias = jnp.sum(lower, axis=0, keepdims=True)
        r.upb[pl.ds(t, 1), :] = bias if opening else r.upb[pl.ds(t, 1), :] + bias
        lower = lower.astype(BF)
        r.slope[t, rows, :] = lower
        return lower

    def trail(lower, t, lanes):
        j, place = tile_of(plan, t)
        r.total[:, lanes] += mm_nt(lower, r.w[0, j, lanes, place])

    staggered(plan, r, lead, turn, trail, ready)
    gain = full_vector(r.gathered, 0, plan.features)

    def finish(block):
        place = block.cells
        grad = r.total[place, :]
        unit = r.unit_wide[place, :].astype(F32)
        r.small[0:1, :] += jnp.sum(grad * unit, axis=0, keepdims=True)
        r.small[1:2, :] += jnp.sum(grad, axis=0, keepdims=True)
        r.small[2:3, :] += jnp.sum(r.upper[place, :].astype(F32), axis=0, keepdims=True)
        scaled = grad * gain
        one = jnp.mean(scaled, axis=1, keepdims=True)
        two = jnp.mean(scaled * unit, axis=1, keepdims=True)
        result = r.dev_wide[place, :][:, :1] * (scaled - one - unit * two)
        block.put(r.leaving, result)

    by_blocks(plan, finish)


def vector_gradients(plan, r, rest_ref):
    rest_ref[...] = jnp.zeros_like(rest_ref)
    for j in range(plan.chans):
        for k in range(plan.per):
            line = j * plan.per + k
            rest_ref[j, 0:1, k * plan.tile : (k + 1) * plan.tile] = r.upb[line : line + 1, :]
        for k in range(3):
            rest_ref[j, 1 + k : 2 + k, 0 : plan.features] = r.small[
                k : k + 1, j * plan.features : (j + 1) * plan.features
            ]


def weight_gradients(r, t):
    return mm_tn(r.active[t], r.upper[...]), mm_tn(r.slope[t], r.entry[...])


def filter_backward(plan, r, there, back, aside=None):
    half = plan.half
    r.mixgrad[...] = jnp.zeros_like(r.mixgrad)
    r.biasgrad[...] = jnp.zeros_like(r.biasgrad)

    def turned(v):
        return jnp.concatenate([v[half:], -v[:half]], axis=0)

    def note_bias(index, value):
        r.biasgrad[index : index + 1, :] += jnp.sum(value, axis=0, keepdims=True)

    def through(low, layer):
        straight = mm_nt(low, r.mix[layer, 0, 0])
        crossed = mm_nt(low, r.mix[layer, 1, 0])
        return jnp.concatenate([straight[:half] + crossed[half:], straight[half:] - crossed[:half]], axis=0)

    def filter_pair(q, carry):
        if aside is not None:
            pl.when(q == 3)(aside)
        p, zeroth, block = pair_inputs(q, there, r.even)
        grad = mm(r.col[0], block.astype(BF))
        grad = jnp.where(r.second[q].astype(F32) == 0.0, 0.0, grad)
        note_bias(2, grad[:half])
        note_bias(3, grad[half:])
        low = grad.astype(BF)
        first = r.first[q]
        r.mixgrad[1, 0] += mm_tn(first, low)
        r.mixgrad[1, 1] += mm_tn(first, turned(grad).astype(BF))
        grad = jnp.where(first.astype(F32) > 0.0, through(low, 1), 0.0)
        note_bias(0, grad[:half])
        note_bias(1, grad[half:])
        low = grad.astype(BF)
        spec = r.spec[q]
        r.mixgrad[0, 0] += mm_tn(spec, low)
        r.mixgrad[0, 1] += mm_tn(spec, turned(grad).astype(BF))
        result = mm(r.colinv[...], through(low, 0).astype(BF))
        pair_outputs(q, p, zeroth, result, back, r.even, r.last, r.stage)
        return carry

    lax.fori_loop(0, plan.pairs + 1, filter_pair, 0)


def mix_gradients(plan, r, before_ref):
    size = plan.size
    for layer in range(2):
        for part in range(2):
            for block in range(2):
                own = slice(block * size, (block + 1) * size)
                piece = r.mixgrad[layer, part][own, own]
                piece = jnp.concatenate([piece, jnp.zeros((size, 128 - size), F32)], axis=1)
                start = ((layer * 2 + part) * 2 + block) * size
                place = slice(start, start + size)
                r.sums[place, :] = piece if before_ref is None else piece + before_ref[place, :]


def rows_backward(plan, r, unit_ref, before_ref):
    gain = r.gain[...].reshape(1, -1)
    me = lax.axis_index("chan")
    lane = lax.broadcasted_iota(jnp.int32, (plan.columns, 128), 1)

    def row(h, carry):
        table, one_sum, two_sum = carry
        block = modes_to_rows(plan, r.flat, h)
        grad = mm(r.row_t[...], block.astype(BF)) + r.out[h]
        unit = unit_ref[h]
        one_sum += jnp.sum(grad * unit, axis=0, keepdims=True)
        two_sum += jnp.sum(grad, axis=0, keepdims=True)
        scaled = grad * gain
        r.scaled[h] = scaled
        one = jnp.sum(scaled, axis=1, keepdims=True)
        two = jnp.sum(scaled * unit, axis=1, keepdims=True)
        table = jnp.where(lane == h, one, table)
        return jnp.where(lane == plan.rows + h, two, table), one_sum, two_sum

    none = jnp.zeros((1, plan.features), F32)
    table, one_sum, two_sum = lax.fori_loop(
        0, plan.rows, row, (jnp.zeros((plan.columns, 128), F32), none, none)
    )
    table = table.T[: 2 * plan.rows]
    r.mine[...] = table
    r.all[me] = table
    copies = [
        push("chan", plan.chans, step, r.mine, r.all.at[me], r.s4, r.r4) for step in range(1, plan.chans)
    ]
    for copy in copies:
        copy.start()
    vectors = jnp.concatenate([r.biasgrad[0:4], one_sum, two_sum, none, none], axis=0)
    wide = jnp.concatenate([vectors, jnp.zeros((8, 256 - plan.features), F32)], axis=1)
    wide = jnp.concatenate([wide[:, :128], wide[:, 128:]], axis=0)
    place = slice(8 * plan.size, plan.small)
    r.sums[place, :] = wide if before_ref is None else wide + before_ref[place, :]
    return copies


def input_gradient(plan, r, unit_ref, dev_ref):
    lane = lax.broadcasted_iota(jnp.int32, (plan.columns, 128), 1)
    means = sum(r.all[j] for j in range(plan.chans)) * (1.0 / plan.width)
    padding = jnp.zeros((128 - 2 * plan.rows, plan.columns), F32)
    means = jnp.concatenate([means, padding], axis=0).T

    def result(h):
        one = jnp.sum(jnp.where(lane == h, means, 0.0), axis=1, keepdims=True)
        two = jnp.sum(jnp.where(lane == plan.rows + h, means, 0.0), axis=1, keepdims=True)
        return r.out[h] + dev_ref[h][:, :1] * (r.scaled[h] - one - unit_ref[h] * two)

    return result


def norm_sums_scratch(plan):
    return {
        "scaled": scratch_of(plan.field),
        "mixgrad": pltpu.VMEM((2, 2, plan.features, plan.features), F32),
        "biasgrad": pltpu.VMEM((8, plan.features), F32),
        "mine": pltpu.VMEM((2 * plan.rows, plan.columns), F32),
        "all": pltpu.VMEM((plan.chans, 2 * plan.rows, plan.columns), F32),
        "s4": sems(plan.chans),
        "r4": sems(plan.chans),
    }


class Moves:
    def __init__(self, sem):
        self.sem, self.count, self.open = sem, 0, []

    def start(self, source, target):
        copy = pltpu.make_async_copy(source, target, self.sem.at[self.count])
        self.count += 1
        copy.start()
        self.open.append(copy)
        return copy

    def close(self):
        wait_all(self.open)


def launch_first(plan, args, tables):
    rows, features, chans = plan.rows, plan.features, plan.chans

    def body(r):
        me = lax.axis_index("chan")
        place = lax.axis_index("space")
        core = lax.rem(place, 2)
        sibling = place + 1 - 2 * core
        met = greet(plan)
        mark_even(plan, r)
        moves = Moves(r.dma)
        moves.start(r.up, r.w.at[0, me])
        moves.start(r.down, r.w.at[1, me])
        loaded = moves.start(r.lines_t, r.lines_in)
        own_weights = moves.open[:2]
        moves.open = []

        beside = me + 1 - 2 * lax.rem(me, 2)
        across = me + 2 - 4 * (me // 2)
        far = chans - 1 - me
        upper_half, lower_half = pl.ds(0, plan.local // 2), pl.ds(plan.local // 2, plan.local // 2)

        def hand(source, target, number, device):
            return pltpu.make_async_remote_copy(
                src_ref=source,
                dst_ref=target,
                send_sem=r.s5.at[number],
                recv_sem=r.r5.at[number],
                device_id=device,
                device_id_type=MESH_ID,
            )

        def own_to(number, source):
            peer = (beside, across)[number]
            return hand(source, r.w.at[core, me], number, {"chan": peer})

        def relay(number):
            slot = (beside, across)[number]
            part = r.w.at[core, slot, (upper_half, lower_half)[number]]
            return hand(part, part, 2 + number, {"chan": (across, beside)[number]})

        def to_core(number):
            if number < 2:
                part = r.w.at[core, (beside, across)[number]]
            else:
                part = r.w.at[core, far]
            return pltpu.make_async_remote_copy(
                src_ref=part,
                dst_ref=part,
                send_sem=r.s7.at[number],
                recv_sem=r.r7.at[number],
                device_id={"space": sibling},
                device_id_type=MESH_ID,
            )

        def pass_near():
            for number in range(2):
                own_to(number, r.up).wait_recv()
            for number in range(2):
                relay(number).start()
            for number in range(2):
                to_core(number).start()

        def pass_far():
            for number in range(2):
                relay(number).wait_recv()
            to_core(2).start()

        def close_weights():
            for number in range(2):
                own_to(number, r.up).wait_send()
                relay(number).wait_send()
            for number in range(3):
                to_core(number).wait()

        def row_of(ref):
            return ref[...].reshape(1, -1).astype(F32)

        r.vectors[...] = jnp.zeros_like(r.vectors)
        r.vectors[0:1, :] = row_of(r.upb)
        r.vectors[1:2, 0:features] = row_of(r.post_gain)
        r.vectors[1:2, features : 2 * features] = row_of(r.post_shift)
        r.vectors[1:2, 2 * features : 3 * features] = row_of(r.downb)
        r.gathered[me] = r.vectors[...]
        met()
        given = [push("chan", chans, step, r.vectors, r.gathered.at[me], r.s6, r.r6) for step in range(1, chans)]
        for copy in given:
            copy.start()
        for layer, (source, bias) in enumerate(((r.mix_in, r.bias_in), (r.mix_out, r.bias_out))):
            for part in range(2):
                zero = jnp.zeros((plan.size, plan.size), F32)
                value = jnp.concatenate(
                    [
                        jnp.concatenate([source[part, 0], zero], axis=1),
                        jnp.concatenate([zero, source[part, 1]], axis=1),
                    ],
                    axis=0,
                )
                high, low = halves(value)
                r.mix[layer, part, 0] = high
                r.mix[layer, part, 1] = low
                line = 2 * layer + part
                r.bias[line : line + 1, :] = jnp.concatenate([bias[part, 0:1, :], bias[part, 1:2, :]], axis=1)
        moves.start(r.mix, r.mix_kept)

        def first(h, carry):
            block = cells_from_lines(r.lines_x, h, r.turn)
            r.turned[h] = block
            total = jnp.sum(block, axis=0, keepdims=True)
            centred = block - total * (1.0 / features)
            r.mine[pl.ds(h, 1), :] = total
            r.mine[pl.ds(rows + h, 1), :] = jnp.sum(centred * centred, axis=0, keepdims=True)
            return carry

        lax.fori_loop(0, rows, first, 0)
        r.all[me] = r.mine[...]
        run_copies([push("chan", chans, step, r.mine, r.all.at[me], r.s4, r.r4) for step in range(1, chans)])
        for kind, source in enumerate((r.up, r.down)):

            @pl.when(core == kind)
            def _():
                for number in range(2):
                    own_to(number, source).start()

        totals = [r.all[j] for j in range(chans)]
        mean = sum(t[:rows] for t in totals) * (1.0 / plan.width)
        spread_sum = sum(
            t[rows:] + features * jnp.square(t[:rows] * (1.0 / features) - mean) for t in totals
        ) * (1.0 / plan.width)
        r.mine[pl.ds(0, rows), :] = mean
        r.mine[pl.ds(rows, rows), :] = lax.rsqrt(spread_sum + NORM_EPS)
        gain, shift = r.gain[...].reshape(1, -1), r.shift[...].reshape(1, -1)

        def normed(h):
            block = r.turned[h]
            inverse = r.mine[pl.ds(rows + h, 1), :]
            r.x[h] = block.T
            unit = ((block - r.mine[pl.ds(h, 1), :]) * inverse).T
            r.unit[h] = unit
            r.dev[h] = jnp.broadcast_to(inverse, (8, plan.columns)).T
            return unit * gain + shift

        scales = (r.scale, r.scale_all, r.s20, r.r20)
        there = Exchange(True, plan.spaces, plan.thick, r.send1, r.recv1, r.s1, r.r1, scales)
        back = Exchange(False, plan.spaces, plan.thick, r.send2, r.recv2, r.s2, r.r2)
        rows_to_modes(plan, (r.row[0], r.row[1]), r.flat, normed, True)
        send_modes(there, plan.pairs, plan.chunk, r.flat)
        moves.start(r.unit, r.unit_kept)
        moves.start(r.dev, r.dev_kept)
        loaded.wait()
        enter(r.lines_in, r.cells_t, r.turn)
        moves.start(r.cells_t, r.cells_kept)
        filter_forward(plan, r, there, back, pass_near)
        for source, target in ((r.spec, r.spec_kept), (r.first, r.first_kept), (r.second, r.second_kept)):
            moves.start(source, target)
        collect(back, plan.pairs, plan.chunk, r.flat)
        pass_far()
        copies = rows_forward(plan, r, r.unit, r.x, r.middle)
        moves.start(r.middle, r.middle_kept)
        wait_all(copies + given)
        close_weights()
        wait_all(own_weights)
        moves.start(r.w, r.w_kept)
        ffn_forward(plan, r)
        saved = ("active", "slope", "entry", "unit_wide", "dev_wide", "gathered")
        for key in saved:
            moves.start(getattr(r, key), getattr(r, key + "_kept"))

        def last(block):
            outer = r.total[block.cells, :]
            mean, _, inverse = moments(outer + block.get(r.mid))
            block.put(r.leaving, outer)
            r.stats[block.group, block.front, :] = jnp.concatenate(
                three_parts(mean) + three_parts(inverse) + [jnp.zeros((block.size, 122), BF)], axis=1
            )

        by_blocks(plan, last)
        copies = spread_chan(plan, r.leaving, r.home, r.s8, r.r8)
        for group in range(plan.share):
            r.stats_thin[group] = r.stats[group].astype(F32).T[:8].astype(BF)
        others = [
            push("chan", chans, step, r.stats_thin, r.stats_home.at[me], r.s9, r.r9) for step in range(1, chans)
        ]
        for copy in others:
            copy.start()
        r.stats_home[me] = r.stats_thin[...]
        wait_all(copies + others)
        there.close(plan.pairs)
        back.close(plan.pairs)
        moves.close()

    stats = ((chans, plan.share, 8, plan.columns), BF)
    outs = {
        "home": plan.by_cells,
        "stats_home": stats,
        "middle_kept": plan.field,
        "unit_kept": plan.field,
        "dev_kept": plan.dev,
        "cells_kept": plan.field,
        "spec_kept": plan.kept,
        "first_kept": plan.kept,
        "second_kept": plan.kept,
        "mix_kept": plan.mix,
        "w_kept": plan.weights,
        "active_kept": plan.tiles,
        "slope_kept": plan.tiles,
        "entry_kept": plan.wide,
        "unit_wide_kept": plan.wide,
        "dev_wide_kept": plan.dev_wide,
        "gathered_kept": plan.vectors,
        "bias": ((8, features), F32),
    }
    ins = dict(args)
    ins.update({key: tables[key] for key in ("row", "rowinv", "col", "colinv")})
    scratch = {
        "dma": sems(20),
        "x": scratch_of(plan.field),
        "unit": scratch_of(plan.field),
        "dev": scratch_of(plan.dev),
        "middle": scratch_of(plan.field),
        "cells_t": scratch_of(plan.field),
        "lines_in": scratch_of(plan.lines),
        "turned": pltpu.VMEM((rows, features, plan.columns), F32),
        "mine": pltpu.VMEM((2 * rows, plan.columns), F32),
        "all": pltpu.VMEM((chans, 2 * rows, plan.columns), F32),
        "spec": scratch_of(plan.kept),
        "first": scratch_of(plan.kept),
        "second": scratch_of(plan.kept),
        "mix": scratch_of(plan.mix),
        "w": scratch_of(plan.weights),
        "vectors": pltpu.VMEM((8, plan.local), F32),
        "own": scratch_of(plan.by_cells),
        "mid": scratch_of(plan.by_cells),
        "leaving": scratch_of(plan.by_cells),
        "stats": pltpu.VMEM((plan.share, plan.columns, 128), BF),
        "stats_thin": pltpu.VMEM(stats[0][1:], BF),
        **plan.exchange_scratch(True, False),
        **plan.spectral_scratch(),
        **ffn_scratch(plan),
        **{key + str(k): sems(chans) for k in range(3, 10) for key in ("s", "r")},
    }
    in_place = ("up", "down", "lines_t")
    return launch(
        body,
        ins,
        outs,
        scratch,
        "first_forward",
        0,
        {key: IN_PLACE for key in in_place},
        {key: IN_PLACE for key in outs if key.endswith("_kept")},
    )


def launch_second(plan, args, one, tables):
    rows, features, chans = plan.rows, plan.features, plan.chans

    def body(r):
        me = lax.axis_index("chan")
        met = greet(plan)
        mark_even(plan, r)
        moves = Moves(r.dma)
        loaded = moves.start(r.lines_t, r.lines_in)
        weights = moves.start(r.w_kept, r.w)
        vectors = moves.start(r.gathered_kept, r.gathered)
        earlier = moves.start(r.cells_kept, r.cells_one)
        moves.open = []
        gain, shift = r.gain[...].reshape(1, -1), r.shift[...].reshape(1, -1)
        weight = r.codes[0].astype(F32) * (1.0 / 64.0)

        def normed(h):
            quarter, inside = h // plan.share, h % plan.share
            x = unpack_cells(r.home[quarter, inside].astype(F32)) + r.before[h]
            stats = r.stats_home[quarter, inside].astype(F32).T
            parts = [stats[:, k : k + 1] for k in range(6)]
            mean = parts[0] + (parts[1] + parts[2])
            dev = parts[3] + (parts[4] + parts[5])
            unit = (x - mean) * dev
            r.x[h] = x
            r.unit[h] = unit
            r.dev[h] = jnp.broadcast_to(dev, (plan.columns, 8))
            return unit * gain + shift

        rows_to_modes(plan, (r.row[0], r.row[1]), r.flat, normed, True)
        met()
        scales = (r.scale, r.scale_all, r.s20, r.r20)
        there = Exchange(True, plan.spaces, plan.thick, r.send1, r.recv1, r.s1, r.r1, scales)
        back = Exchange(False, plan.spaces, plan.thick, r.send2, r.recv2, r.s2, r.r2)
        send_modes(there, plan.pairs, plan.chunk, r.flat)
        loaded.wait()
        enter(r.lines_in, r.cells_t, r.turn)

        def low_target(h, peer, place):
            r.own[peer, place] = pack_cells(r.cells_t[h]).astype(BF)

        targets = []

        def send_target(step, peer):
            if step:
                copy = push("chan", chans, step, r.own.at[peer], r.target.at[me], r.s5, r.r5)
                copy.start()
                targets.append(copy)
            else:
                r.target[me] = r.own[me]

        rows_of_chunks(plan, low_target, send_target)
        filter_forward(plan, r, there, back)
        collect(back, plan.pairs, plan.chunk, r.flat)
        there.close(plan.pairs)
        back.close(plan.pairs)
        wait_all(targets)
        copies = rows_forward(plan, r, r.unit, r.x, r.before)
        weights.wait()
        vectors.wait()
        wait_all(copies)
        ffn_forward(plan, r)

        def errors(block):
            outer = r.total[block.cells, :]
            error = outer + block.get(r.mid) - block.get(r.target)
            r.upper[block.cells, :] = (weight * error).astype(BF)
            block.put(r.leaving, outer)

        by_blocks(plan, errors)
        copies = spread_chan(plan, r.leaving, r.landed, r.s6, r.r6)
        for copy in copies:
            copy.wait_send()
        ffn_backward(plan, r)
        for copy in copies:
            copy.wait_recv()
        copies = spread_chan(plan, r.leaving, r.own, r.s7, r.r7)

        def grads(u, carry):
            for slot in range(2):
                t = 2 * u + slot
                stores = [
                    pltpu.make_async_copy(r.grad.at[slot, k], r.grads_kept.at[k, t], r.dma2.at[slot, k])
                    for k in range(2)
                ]

                @pl.when(u > 0)
                def _():
                    wait_all(stores)

                for k, value in enumerate(weight_gradients(r, t)):
                    r.grad[slot, k] = value.astype(BF)
                    stores[k].start()
            return carry

        lax.fori_loop(0, plan.steps // 2, grads, 0)
        vector_gradients(plan, r, r.rest)
        wait_all(copies)

        def middle_grad(h):
            quarter, inside = h // plan.share, h % plan.share
            x = unpack_cells(r.landed[quarter, inside].astype(F32)) + r.before[h]
            r.before[h] = x
            grad = weight * (x - r.cells_t[h]) + unpack_cells(r.own[quarter, inside].astype(F32))
            r.out[h] = grad
            return grad

        rows_to_modes(plan, r.rowinv_t[...], r.flat, middle_grad, False)
        there = Exchange(False, plan.spaces, plan.thick, r.send3, r.recv3, r.s3_, r.r3_)
        back = Exchange(False, plan.spaces, plan.thick, r.send2, r.recv2, r.s2, r.r2)
        send_modes(there, plan.pairs, plan.chunk, r.flat)
        moves.start(r.before, r.second_x)
        leave(r.x, r.lines_in, r.turn)
        moves.start(r.lines_in, r.lines)
        filter_backward(plan, r, there, back)
        mix_gradients(plan, r, None)
        collect(back, plan.pairs, plan.chunk, r.flat)
        copies = rows_backward(plan, r, r.unit, None)
        earlier.wait()
        wait_all(copies)
        result = input_gradient(plan, r, r.unit, r.dev)
        copies = []

        def row(h, peer, place):
            grad = weight * (r.x[h] - r.cells_one[h]) + result(h)
            r.out[h] = grad
            r.own[peer, place] = pack_cells(grad).astype(BF)

        def send_chunk(step, peer):
            if step:
                copy = push("chan", chans, step, r.own.at[peer], r.came.at[me], r.s8, r.r8)
                copy.start()
                copies.append(copy)
            else:
                r.came[me] = r.own[me]

        rows_of_chunks(plan, row, send_chunk)
        for slot in range(2):
            for k in range(2):
                pltpu.make_async_copy(
                    r.grad.at[slot, k], r.grads_kept.at[k, plan.steps - 2 + slot], r.dma2.at[slot, k]
                ).wait()
        wait_all(copies)
        there.close(plan.pairs)
        back.close(plan.pairs)
        moves.close()

    ins = {
        "home": one["home"],
        "stats_home": one["stats_home"],
        "before": one["middle_kept"],
        "w_kept": one["w_kept"],
        "gathered_kept": one["gathered_kept"],
        "cells_kept": one["cells_kept"],
        "mix": one["mix_kept"],
        "bias": one["bias"],
        **args,
    }
    ins.update({key: tables[key] for key in ("row", "rowinv", "rowinv_t", "row_t", "col", "colinv")})
    outs = {
        "out": plan.field,
        "came": plan.by_cells,
        "lines": plan.lines,
        "second_x": plan.field,
        "sums": plan.sums,
        "rest": plan.rest,
        "grads_kept": plan.grads,
    }
    exchange = Exchange.shape(False, plan.spaces, plan.thick, plan.pairs)
    scratch = {
        "dma": sems(8),
        "dma2": sems(2, 2),
        "x": scratch_of(plan.field),
        "unit": scratch_of(plan.field),
        "dev": scratch_of(plan.dev),
        "cells_t": scratch_of(plan.field),
        "cells_one": scratch_of(plan.field),
        "lines_in": scratch_of(plan.lines),
        "spec": scratch_of(plan.kept),
        "first": scratch_of(plan.kept),
        "second": scratch_of(plan.kept),
        "w": scratch_of(plan.weights),
        "own": scratch_of(plan.by_cells),
        "mid": scratch_of(plan.by_cells),
        "target": scratch_of(plan.by_cells),
        "leaving": scratch_of(plan.by_cells),
        "landed": scratch_of(plan.by_cells),
        "upper": scratch_of(plan.wide),
        "small": pltpu.VMEM((8, plan.width), F32),
        "upb": pltpu.VMEM((16, plan.tile), F32),
        "grad": pltpu.VMEM((2, 2, plan.tile, plan.width), BF),
        "send3": exchange,
        "recv3": exchange,
        "s3_": sems(plan.pairs, plan.spaces),
        "r3_": sems(plan.pairs, plan.spaces),
        **plan.exchange_scratch(True, False),
        **plan.spectral_scratch(),
        **ffn_scratch(plan),
        **norm_sums_scratch(plan),
        **{key + str(k): sems(chans) for k in (3, 5, 6, 7, 8) for key in ("s", "r")},
    }
    in_specs = {key: IN_PLACE for key in ("w_kept", "gathered_kept", "cells_kept", "lines_t")}
    in_specs["codes"] = pl.BlockSpec(memory_space=pltpu.SMEM)
    return launch(
        body,
        ins,
        outs,
        scratch,
        "second_step",
        1,
        in_specs,
        {key: IN_PLACE for key in ("second_x", "grads_kept", "lines")},
    )


def launch_third(plan, args, one, two, tables):
    rows, features, chans, spaces = plan.rows, plan.features, plan.chans, plan.spaces
    local, width = plan.local, plan.width
    levels = spaces // 2
    piece = local // levels
    small = plan.small
    part = -(-(small + 32) // (16 * levels)) * 16

    def body(r):
        me = lax.axis_index("chan")
        place = lax.axis_index("space")
        core = lax.rem(place, 2)
        level = place // 2
        sibling = place + 1 - 2 * core
        others = [lax.rem(level + step, levels) for step in range(1, levels)]
        met = greet(plan)
        mark_even(plan, r)
        moves = Moves(r.dma)
        early = [
            moves.start(source, target)
            for source, target in (
                (r.gathered_kept, r.gathered),
                (r.unit_wide_kept, r.unit_wide),
                (r.dev_wide_kept, r.dev_wide),
            )
        ]
        chunks = []
        for j in range(chans):
            tiles = pl.ds(j * plan.per, plan.per)
            chunks.append(
                [
                    moves.start(r.w_kept.at[1, j], r.w.at[1, j]),
                    moves.start(r.slope_kept.at[tiles], r.slope.at[tiles]),
                    moves.start(r.w_kept.at[0, j], r.w.at[0, j]),
                ]
            )
        middle = [moves.start(r.active_kept, r.active), moves.start(r.entry_kept, r.entry)]
        moves.open = []

        def upper(block):
            r.upper[block.cells, :] = block.get(r.came).astype(BF)

        by_blocks(plan, upper)
        wait_all(early)
        wait_all(chunks[0])
        ffn_backward(plan, r, lambda chunk: wait_all(chunks[chunk]))
        late = [
            moves.start(source, target)
            for source, target in (
                (r.g, r.out),
                (r.unit_kept, r.unit),
                (r.spec_kept, r.spec),
                (r.first_kept, r.first),
                (r.second_kept, r.second),
                (r.dev_kept, r.dev),
            )
        ]
        moves.open = []
        met()
        copies = spread_chan(plan, r.leaving, r.own, r.s7, r.r7)
        vector_gradients(plan, r, r.rest)
        r.rest[...] += r.rest_before[...]
        vectors = [
            push("chan", chans, step, r.rest.at[lax.rem(me + step, chans)], r.rest_land.at[me], r.s6, r.r6)
            for step in range(1, chans)
        ]
        for copy in vectors:
            copy.start()
        r.rest_land[me] = r.rest[me]
        wait_all(middle)

        column, line = lax.rem(me, 2), me // 2
        beside = me + 1 - 2 * column
        across = me + 2 - 4 * line
        near, under = pl.ds(0, plan.tile // 2), pl.ds(plan.tile // 2, plan.tile // 2)

        def order(i):
            k = i // plan.per
            owner_column = column + (1 - k // 2) * (1 - 2 * column)
            owner_line = line + (1 - k % 2) * (1 - 2 * line)
            return (2 * owner_line + owner_column) * plan.per + i % plan.per

        def fetch(i, k):
            return pltpu.make_async_copy(r.grads_kept.at[k, order(i)], r.prev.at[i % 2, k], r.dma2.at[i % 2, k])

        def swap(i):
            return pltpu.make_async_remote_copy(
                src_ref=r.give.at[i % 2],
                dst_ref=r.take.at[i % 3],
                send_sem=r.s9.at[i],
                recv_sem=r.r9.at[i],
                device_id={"space": sibling},
                device_id_type=MESH_ID,
            )

        def to_chan(source, target, sem, number, device):
            return pltpu.make_async_remote_copy(
                src_ref=source,
                dst_ref=target,
                send_sem=sem[0].at[number],
                recv_sem=sem[1].at[number],
                device_id={"chan": device},
                device_id_type=MESH_ID,
            )

        def ship_near(i):
            target = r.land_near.at[i // plan.per, i % plan.per]
            return to_chan(r.keep.at[i, near], target, (r.s10, r.r10), i, beside)

        def ship_under(j):
            i = j + (j // plan.per) * plan.per
            target = r.land_under.at[j // plan.per, j % plan.per]
            return to_chan(r.keep.at[i, under], target, (r.s17, r.r17), j, across)

        def on_across(k):
            return to_chan(
                r.keep.at[2 * plan.per + k, near], r.land_on.at[0, k], (r.s18, r.r18), k, across
            )

        def on_beside(k):
            return to_chan(
                r.keep.at[plan.per + k, under], r.land_on.at[1, k], (r.s18, r.r18), plan.per + k, beside
            )

        def pass_on():
            def tile(k, carry):
                for arrived, land, start, part, onward in (
                    (ship_near, r.land_near, 2 * plan.per, near, on_across),
                    (ship_under, r.land_under, plan.per, under, on_beside),
                ):
                    arrived(k).wait_recv()
                    value = r.keep[start + k, part, :].astype(F32) + land[0, k].astype(F32)
                    r.keep[start + k, part, :] = value.astype(BF)
                    onward(k).start()
                return carry

            lax.fori_loop(0, plan.per, tile, 0)

        for k in range(2):
            fetch(0, k).start()

        def settle(i):
            swap(i).wait()
            r.keep[i] = (r.keep[i].astype(F32) + r.take[i % 3].astype(F32)).astype(BF)

        shipped = plan.steps - plan.per

        def leave_block(i):
            settle(i)

            @pl.when(i < 2 * plan.per)
            def _():
                ship_near(i).start()

            @pl.when(i < plan.per)
            def _():
                ship_under(i).start()

            @pl.when(i >= 2 * plan.per)
            def _():
                ship_under(i - plan.per).start()

        def make_block(i, before):
            for k in range(2):
                fetch(i, k).wait()

            @pl.when(i + 1 < plan.steps)
            def _():
                for k in range(2):
                    fetch(i + 1, k).start()

            values = [
                (value + r.prev[i % 2, k].astype(F32)).astype(BF)
                for k, value in enumerate(weight_gradients(r, order(i)))
            ]
            before(i)
            for kind in range(2):

                @pl.when(core == kind)
                def _():
                    r.keep[i] = values[kind]
                    r.give[i % 2] = values[1 - kind]

            swap(i).start()

        def others_block(i, carry):
            make_block(i, lambda i: pl.when(i > 0)(lambda: leave_block(i - 1)))
            return carry

        def own_block(i, carry):
            make_block(i, lambda i: pl.when(i > shipped)(lambda: settle(i - 1)))
            return carry

        lax.fori_loop(0, shipped, others_block, 0)
        leave_block(shipped - 1)
        wait_all(copies)
        wait_all(late)

        def middle_grad(h):
            quarter, inside = h // plan.share, h % plan.share
            grad = r.out[h] + unpack_cells(r.own[quarter, inside].astype(F32))
            r.out[h] = grad
            return grad

        rows_to_modes(plan, r.rowinv_t[...], r.flat, middle_grad, False)
        there = Exchange(False, spaces, plan.thick, r.send1, r.recv1, r.s1, r.r1)
        back = Exchange(False, spaces, plan.thick, r.send2, r.recv2, r.s2, r.r2)
        send_modes(there, plan.pairs, plan.chunk, r.flat)
        lax.fori_loop(shipped, plan.steps, own_block, 0)
        settle(plan.steps - 1)
        filter_backward(plan, r, there, back, pass_on)
        mix_gradients(plan, r, r.sums_before)

        def arrived(k, carry):
            ship_near(k).wait_send()
            ship_near(plan.per + k).wait()
            ship_under(k).wait_send()
            ship_under(plan.per + k).wait()
            on_across(k).wait()
            on_beside(k).wait()
            return carry

        lax.fori_loop(0, plan.per, arrived, 0)
        wait_all(vectors)
        def send(source, target, step, send_sem, recv_sem):
            return pltpu.make_async_remote_copy(
                src_ref=source,
                dst_ref=target,
                send_sem=send_sem.at[step],
                recv_sem=recv_sem.at[step],
                device_id={"space": 2 * others[step - 1] + core},
                device_id_type=MESH_ID,
            )

        def to_sibling(source, target, step, send_sem, recv_sem):
            return pltpu.make_async_remote_copy(
                src_ref=source,
                dst_ref=target,
                send_sem=send_sem.at[step],
                recv_sem=recv_sem.at[step],
                device_id={"space": sibling},
                device_id_type=MESH_ID,
            )

        def total(tile, carry):
            for half, land in enumerate((r.land_near, r.land_under)):
                for sub in range(2):
                    inside = pl.ds(64 * sub, 64)
                    value = r.keep[3 * plan.per + tile, pl.ds(128 * half + 64 * sub, 64), :].astype(F32)
                    value += land[1, tile, inside, :].astype(F32) + r.land_on[half, tile, inside, :].astype(F32)
                    number = 4 * tile + 2 * half + sub
                    target = pl.ds(pl.multiple_of((number % (piece // 64)) * 64, 64), 64)
                    r.a_send[number // (piece // 64), target, :] = value.astype(BF)
            return carry

        lax.fori_loop(0, plan.per, total, 0)
        wide = [
            send(r.a_send.at[others[step - 1]], r.a_land.at[level], step, r.s11, r.r11)
            for step in range(1, levels)
        ]
        for copy in wide:
            copy.start()
        collect(back, plan.pairs, plan.chunk, r.flat)
        copies = rows_backward(plan, r, r.unit, r.sums_before)
        r.table[...] = jnp.zeros_like(r.table)
        r.table[0:small, :] = r.sums[...]
        tail = sum(r.rest_land[j] for j in range(chans))
        for k in range(local // 128):
            lanes = slice(k * 128, (k + 1) * 128)
            r.table[small + k : small + k + 1, :] = tail[0:1, lanes]
        for k in range(3):
            line = jnp.concatenate([tail[1 + k : 2 + k, :features], jnp.zeros((1, 256 - features), F32)], axis=1)
            r.table[small + 8 + 2 * k : small + 9 + 2 * k, :] = line[:, :128]
            r.table[small + 9 + 2 * k : small + 10 + 2 * k, :] = line[:, 128:]
        for q in range(levels):
            r.b_send[q] = r.table[q * part : (q + 1) * part, :].astype(BF)
        thin = [
            send(r.b_send.at[others[step - 1]], r.b_land.at[level], step, r.s12, r.r12)
            for step in range(1, levels)
        ]
        for copy in thin:
            copy.start()
        wait_all(copies)
        result = input_gradient(plan, r, r.unit, r.dev)

        def finish(h, carry):
            r.out[h] = result(h)
            return carry

        lax.fori_loop(0, rows, finish, 0)
        moves.start(r.second_x, r.scaled).wait()
        moves.open = []
        leave(r.scaled, r.lines, r.turn)
        moves.start(r.lines, r.lines_x)
        a = r.a_send[level].astype(F32)
        b = r.b_send[level].astype(F32)
        for step in range(1, levels):
            wide[step - 1].wait()
            thin[step - 1].wait()
            source = lax.rem(level - step + levels, levels)
            a += r.a_land[source].astype(F32)
            b += r.b_land[source].astype(F32)
        r.a_own[...] = a.astype(BF)
        r.b_own[...] = b.astype(BF)
        last = [to_sibling(r.a_own, r.a_other.at[level], 0, r.s13, r.r13)]
        last += [to_sibling(r.b_own, r.b_other.at[level], 0, r.s14, r.r14)]
        again = []
        for step in range(1, levels):
            again.append(send(r.a_own, r.a_full.at[level], step, r.s15, r.r15))
            again.append(send(r.b_own, r.b_full.at[level], step, r.s16, r.r16))
        for copy in again + last:
            copy.start()
        r.a_full[level] = r.a_own[...]
        r.b_full[level] = r.b_own[...]
        moves.close()
        moves.open = []
        leave(r.out, r.lines, r.turn)
        moves.start(r.lines, r.lines_out)
        for step in range(1, levels):
            again[2 * step - 2].wait()
            again[2 * step - 1].wait()
            source = lax.rem(level - step + levels, levels)
            more = [to_sibling(r.a_full.at[source], r.a_other.at[source], step, r.s13, r.r13)]
            more += [to_sibling(r.b_full.at[source], r.b_other.at[source], step, r.s14, r.r14)]
            for copy in more:
                copy.start()
            last += more
        wait_all(last)
        moves.close()
        there.close(plan.pairs)
        back.close(plan.pairs)

    ins = {
        "g": two["out"],
        "came": two["came"],
        "second_x": two["second_x"],
        "sums_before": two["sums"],
        "rest_before": two["rest"],
        "grads_kept": two["grads_kept"],
        "mix": one["mix_kept"],
        **{
            key: one[key]
            for key in (
                "w_kept",
                "slope_kept",
                "active_kept",
                "entry_kept",
                "unit_wide_kept",
                "dev_wide_kept",
                "gathered_kept",
                "spec_kept",
                "first_kept",
                "second_kept",
                "unit_kept",
                "dev_kept",
            )
        },
        **args,
    }
    ins.update({key: tables[key] for key in ("rowinv_t", "row_t", "col", "colinv")})
    outs = {
        "lines_x": plan.lines,
        "lines_out": plan.lines,
        "a_full": ((levels, piece, width), BF),
        "a_other": ((levels, piece, width), BF),
        "b_full": ((levels, part, 128), BF),
        "b_other": ((levels, part, 128), BF),
    }
    blocks = pltpu.VMEM((plan.steps, plan.tile, width), BF)
    scratch = {
        "dma": sems(28),
        "dma2": sems(2, 2),
        "lines": scratch_of(plan.lines),
        "unit": scratch_of(plan.field),
        "dev": scratch_of(plan.dev),
        "out": scratch_of(plan.field),
        "spec": scratch_of(plan.kept),
        "first": scratch_of(plan.kept),
        "second": scratch_of(plan.kept),
        "w": scratch_of(plan.weights),
        "own": scratch_of(plan.by_cells),
        "leaving": scratch_of(plan.by_cells),
        "upper": scratch_of(plan.wide),
        "small": pltpu.VMEM((8, width), F32),
        "upb": pltpu.VMEM((16, plan.tile), F32),
        "sums": scratch_of(plan.sums),
        "rest": scratch_of(plan.rest),
        "rest_land": scratch_of(plan.rest),
        "prev": pltpu.VMEM((2, 2, plan.tile, width), BF),
        "keep": blocks,
        "give": pltpu.VMEM((2, plan.tile, width), BF),
        "take": pltpu.VMEM((3, plan.tile, width), BF),
        "land_near": pltpu.VMEM((2, plan.per, plan.tile // 2, width), BF),
        "land_under": pltpu.VMEM((2, plan.per, plan.tile // 2, width), BF),
        "land_on": pltpu.VMEM((2, plan.per, plan.tile // 2, width), BF),
        "table": pltpu.VMEM((part * levels, 128), F32),
        "a_send": pltpu.VMEM((levels, piece, width), BF),
        "a_land": pltpu.VMEM((levels, piece, width), BF),
        "a_own": pltpu.VMEM((piece, width), BF),
        "b_send": pltpu.VMEM((levels, part, 128), BF),
        "b_land": pltpu.VMEM((levels, part, 128), BF),
        "b_own": pltpu.VMEM((part, 128), BF),
        **plan.exchange_scratch(False, False),
        **plan.spectral_scratch(),
        **ffn_scratch(plan),
        **norm_sums_scratch(plan),
        **{key + str(k): sems(chans) for k in (6, 7) for key in ("s", "r")},
        **{key + str(k): sems(plan.steps) for k in (9, 10, 17, 18) for key in ("s", "r")},
        **{key + str(k): sems(levels) for k in range(11, 17) for key in ("s", "r")},
    }
    in_place = [key for key in ins if key.endswith("_kept") and key != "mix_kept"] + ["second_x", "g"]
    return launch(
        body,
        ins,
        outs,
        scratch,
        "first_backward",
        2,
        {key: IN_PLACE for key in in_place},
        {key: IN_PLACE for key in ("lines_x", "lines_out")},
    )


def unpack_gradients(plan, parts, fields):
    features, small = plan.features, plan.small
    levels, piece, width = parts["a_full"].shape
    part = parts["b_full"].shape[1]
    local = levels * piece
    size = features // 2

    def body(r):
        swap = lax.rem(lax.axis_index("space"), 2) == 1
        for q in range(levels):
            own = slice(q * piece, (q + 1) * piece)
            mine, theirs = r.a_full[q].astype(F32), r.a_other[q].astype(F32)
            r.down[own, :] = jnp.where(swap, theirs, mine)
            r.up[:, own] = jnp.where(swap, mine, theirs).T
            r.table[q * part : (q + 1) * part, :] = r.b_full[q].astype(F32) + r.b_other[q].astype(F32)
        for layer, target in enumerate((r.mix_in, r.mix_out)):
            for half in range(2):
                for block in range(2):
                    start = ((layer * 2 + half) * 2 + block) * size
                    target[half, block] = r.table[start : start + size, :size]
        base = 8 * size

        def vector(k):
            return jnp.concatenate(
                [r.table[base + k : base + k + 1, :], r.table[base + 8 + k : base + 9 + k, : features - 128]], axis=1
            )

        for k, target in enumerate((r.bias_in, r.bias_in, r.bias_out, r.bias_out)):
            value = vector(k)
            target[k % 2, 0:1, :] = value[:, :size]
            target[k % 2, 1:2, :] = value[:, size:]
        r.pre_gain[...] = vector(4)
        r.pre_shift[...] = vector(5)
        r.upb[...] = jnp.concatenate(
            [r.table[small + k : small + k + 1, :] for k in range(local // 128)], axis=1
        ).reshape(local)

        def line(h, carry):
            for key in fields:
                getattr(r, key)[h] = getattr(r, key + "_in")[h]
            return carry

        lax.fori_loop(0, plan.rows, line, 0)
        for k, target in enumerate((r.post_gain, r.post_shift, r.downb)):
            target[...] = jnp.concatenate(
                [
                    r.table[small + 8 + 2 * k : small + 9 + 2 * k, :],
                    r.table[small + 9 + 2 * k : small + 10 + 2 * k, : features - 128],
                ],
                axis=1,
            )


    return launch(
        body,
        {
            **{key: parts[key] for key in ("a_full", "a_other", "b_full", "b_other")},
            **{key + "_in": value for key, value in fields.items()},
        },
        {
            "down": ((local, width), F32),
            "up": ((width, local), F32),
            "mix_in": ((2, 2, size, size), F32),
            "mix_out": ((2, 2, size, size), F32),
            "bias_in": ((2, 2, size), F32),
            "bias_out": ((2, 2, size), F32),
            "pre_gain": ((1, features), F32),
            "pre_shift": ((1, features), F32),
            "post_gain": ((1, features), F32),
            "post_shift": ((1, features), F32),
            "downb": ((1, features), F32),
            "upb": ((local,), F32),
            **{key: plan.lines for key in fields},
        },
        {"table": pltpu.VMEM((part * levels, 128), F32)},
        "unpack_gradients",
    )


def shards_fast(
    current_atmosphere,
    truth_one,
    truth_two,
    storm_codes,
    pre_gain,
    pre_shift,
    mix_weight_in,
    mix_bias_in,
    mix_weight_out,
    mix_bias_out,
    post_gain,
    post_shift,
    up_weight,
    up_bias,
    down_weight,
    down_bias,
):
    rows, merged = current_atmosphere.shape[1:]
    columns = W
    features = merged // columns
    plan = Plan(
        rows, features, columns, lax.axis_size("space"), lax.axis_size("chan"), up_weight.shape[1]
    )
    forward, inverse = row_constants(columns)
    column = column_constants(rows * plan.spaces, rows, 2)
    tables = {
        "row": jnp.stack(const_halves(forward)),
        "rowinv": const_halves(inverse)[0],
        "rowinv_t": const_halves(inverse.T)[0],
        "row_t": const_halves(forward.T)[0],
        "col": jnp.stack(const_halves(column)),
        "colinv": const_halves(column.T)[0],
    }

    def lines(flat):
        return flat.reshape(rows, merged // 128, 128)

    def flat(line_field):
        return line_field.reshape(1, rows, merged)

    one = launch_first(
        plan,
        {
            "lines_x": lines(current_atmosphere),
            "lines_t": lines(truth_one),
            "gain": pre_gain,
            "shift": pre_shift,
            "mix_in": mix_weight_in,
            "bias_in": mix_bias_in,
            "mix_out": mix_weight_out,
            "bias_out": mix_bias_out,
            "post_gain": post_gain,
            "post_shift": post_shift,
            "up": up_weight,
            "upb": up_bias,
            "down": down_weight,
            "downb": down_bias,
        },
        tables,
    )
    two = launch_second(
        plan,
        {"gain": pre_gain, "shift": pre_shift, "lines_t": lines(truth_two), "codes": storm_codes},
        one,
        tables,
    )
    three = launch_third(plan, {"gain": pre_gain}, one, two, tables)
    grads = unpack_gradients(
        plan, three, {"first": two["lines"], "second": three["lines_x"], "state": three["lines_out"]}
    )
    return (
        flat(grads["first"]),
        flat(grads["second"]),
        flat(grads["state"]),
        grads["pre_gain"].reshape(features),
        grads["pre_shift"].reshape(features),
        grads["mix_in"],
        grads["bias_in"],
        grads["mix_out"],
        grads["bias_out"],
        grads["post_gain"].reshape(features),
        grads["post_shift"].reshape(features),
        grads["up"],
        grads["upb"],
        grads["down"],
        grads["downb"].reshape(features),
    )


def suits(mesh):
    spaces, chans = mesh.shape["space"], mesh.shape["chan"]
    return (spaces, chans) == (8, 4)


def solution(mesh):
    in_specs = (
        P(None, "space", "chan"),
        P(None, "space", "chan"),
        P(None, "space", "chan"),
        P(),
        P("chan"),
        P("chan"),
        P(None, "chan", None, None),
        P(None, "chan", None),
        P(None, "chan", None, None),
        P(None, "chan", None),
        P("chan"),
        P("chan"),
        P(None, "chan"),
        P("chan"),
        P("chan", None),
        P("chan"),
    )
    out_specs = (
        P(None, "space", "chan"),
        P(None, "space", "chan"),
        P(None, "space", "chan"),
        P("chan"),
        P("chan"),
        P(None, "chan", None, None),
        P(None, "chan", None),
        P(None, "chan", None, None),
        P(None, "chan", None),
        P("chan"),
        P("chan"),
        P(None, "chan"),
        P("chan"),
        P("chan", None),
        P("chan"),
    )
    return jax.shard_map(shards_fast if suits(mesh) else shards, mesh=mesh, in_specs=in_specs, out_specs=out_specs, check_vma=False)
```

```python
import functools
import math
import types

import jax
import jax.numpy as jnp
import ml_dtypes
import numpy as np
from jax import lax
from jax.experimental import pallas as pl
from jax.experimental.pallas import tpu as pltpu
from jax.sharding import PartitionSpec as P

W = 160
KW = 81


NORM_EPS = 1e-06
SHRINK_LEVEL = 0.01
FULL_PRECISION = lax.Precision.HIGHEST


def exact_gelu(values):
    return jax.nn.gelu(values, approximate=False)


def shrink(values):
    return values - jnp.clip(values, -SHRINK_LEVEL, SHRINK_LEVEL)


def block_mix(values, matrix):
    return jnp.einsum("bhkni,nio->bhkno", values, matrix, precision=FULL_PRECISION)


def row_tables(columns, kept_modes, padded_modes):
    places = jnp.arange(columns, dtype=jnp.int32)[:, None]
    orders = jnp.arange(padded_modes, dtype=jnp.int32)[None, :]
    angles = 2.0 * math.pi / columns * (places * orders % columns).astype(jnp.float32)
    factor = 1.0 / math.sqrt(columns)
    single = jnp.logical_or(orders == 0, 2 * orders == columns)
    doubled = jnp.where(single, 1.0, 2.0).astype(jnp.float32)
    used = jnp.where(orders < kept_modes, 1.0, 0.0).astype(jnp.float32)
    return (
        jnp.cos(angles) * factor * used,
        -jnp.sin(angles) * factor * used,
        jnp.transpose(jnp.cos(angles) * doubled * factor * used),
        jnp.transpose(jnp.sin(angles) * doubled * factor * used),
    )


def along_rows(values, tables):
    return jnp.stack(
        [
            jnp.einsum("bhwc,wk->bhkc", values, tables[0], precision=FULL_PRECISION),
            jnp.einsum("bhwc,wk->bhkc", values, tables[1], precision=FULL_PRECISION),
        ]
    )


def along_rows_back(paired, tables):
    return jnp.einsum("bhkc,wk->bhwc", paired[0], tables[0], precision=FULL_PRECISION) + jnp.einsum(
        "bhkc,wk->bhwc", paired[1], tables[1], precision=FULL_PRECISION
    )


def rows_inverse(paired, tables):
    return jnp.einsum("bhkc,kw->bhwc", paired[0], tables[2], precision=FULL_PRECISION) - jnp.einsum(
        "bhkc,kw->bhwc", paired[1], tables[3], precision=FULL_PRECISION
    )


def rows_inverse_back(values, tables):
    return jnp.stack(
        [
            jnp.einsum("bhwc,kw->bhkc", values, tables[2], precision=FULL_PRECISION),
            -jnp.einsum("bhwc,kw->bhkc", values, tables[3], precision=FULL_PRECISION),
        ]
    )


def column_tables(height):
    orders = jnp.arange(height, dtype=jnp.int32)[:, None]
    places = jnp.arange(height, dtype=jnp.int32)[None, :]
    angles = 2.0 * math.pi / height * (orders * places % height).astype(jnp.float32)
    factor = 1.0 / math.sqrt(height)
    return (jnp.cos(angles) * factor, jnp.sin(angles) * factor)


def to_freq(matrix, values):
    return jnp.einsum("kh,bhmc->bkmc", matrix, values, precision=FULL_PRECISION)


def from_freq(matrix, values):
    return jnp.einsum("kh,bkmc->bhmc", matrix, values, precision=FULL_PRECISION)


def spectral_core(paired, w_first, b_first, w_second, b_second):
    samples, height, kept_modes, channels = paired.shape[1:]
    blocks, block_size = (w_first.shape[1], w_first.shape[2])
    cosine, sine_table = column_tables(height)
    real_in, imag_in = (paired[0], paired[1])
    split_form = (samples, height, kept_modes, blocks, block_size)
    real_part = (to_freq(cosine, real_in) + to_freq(sine_table, imag_in)).reshape(split_form)
    imag_part = (to_freq(cosine, imag_in) - to_freq(sine_table, real_in)).reshape(split_form)
    first_real = jax.nn.relu(
        block_mix(real_part, w_first[0]) - block_mix(imag_part, w_first[1]) + b_first[0]
    )
    first_imag = jax.nn.relu(
        block_mix(imag_part, w_first[0]) + block_mix(real_part, w_first[1]) + b_first[1]
    )
    joined_form = (samples, height, kept_modes, channels)
    second_real = shrink(
        block_mix(first_real, w_second[0]) - block_mix(first_imag, w_second[1]) + b_second[0]
    ).reshape(joined_form)
    second_imag = shrink(
        block_mix(first_imag, w_second[0]) + block_mix(first_real, w_second[1]) + b_second[1]
    ).reshape(joined_form)
    out_real = from_freq(cosine, second_real) - from_freq(sine_table, second_imag)
    out_imag = from_freq(cosine, second_imag) + from_freq(sine_table, second_real)
    return jnp.stack([out_real, out_imag])


def column_layout(paired):
    return lax.all_to_all(paired, "space", split_axis=3, concat_axis=2, tiled=True)


def row_layout(paired):
    return lax.all_to_all(
        paired.astype(jnp.bfloat16), "space", split_axis=2, concat_axis=3, tiled=True
    ).astype(paired.dtype)


def norm_forward(values, gain, offset):
    width_all = values.shape[-1] * lax.axis_size("chan")
    totals = lax.psum((jnp.sum(values, axis=-1), jnp.sum(values * values, axis=-1)), "chan")
    average = totals[0] / width_all
    variance = totals[1] / width_all - average * average
    inverse_dev = lax.rsqrt(variance + NORM_EPS)[..., None]
    scaled = (values - average[..., None]) * inverse_dev
    return (scaled * gain + offset, (scaled, inverse_dev))


def norm_backward(gradient, gain, saved):
    scaled, inverse_dev = saved
    width_all = scaled.shape[-1] * lax.axis_size("chan")
    scaled_grad = gradient * gain
    totals = lax.psum(
        (jnp.sum(scaled_grad, axis=-1), jnp.sum(scaled_grad * scaled, axis=-1)), "chan"
    )
    values_grad = inverse_dev * (
        scaled_grad - totals[0][..., None] / width_all - scaled * (totals[1][..., None] / width_all)
    )
    return (
        values_grad,
        jnp.sum(gradient * scaled, axis=(0, 1, 2)),
        jnp.sum(gradient, axis=(0, 1, 2)),
    )


def shards(
    current_atmosphere,
    truth_one,
    truth_two,
    storm_codes,
    pre_gain,
    pre_shift,
    mix_weight_in,
    mix_bias_in,
    mix_weight_out,
    mix_bias_out,
    post_gain,
    post_shift,
    up_weight,
    up_bias,
    down_weight,
    down_bias,
):
    samples, rows_here, merged = current_atmosphere.shape
    columns = W
    channels = merged // columns
    total_rows = samples * rows_here * columns
    space_count = lax.axis_size("space")
    padded_modes = (KW + space_count - 1) // space_count * space_count
    tables = row_tables(columns, KW, padded_modes)

    def to_cells(flat_field):
        return jnp.transpose(
            flat_field.reshape(samples, rows_here, channels, columns), (0, 1, 3, 2)
        )

    def to_flat(cell_field):
        return jnp.transpose(cell_field, (0, 1, 3, 2)).reshape(samples, rows_here, merged)

    start_cells = to_cells(current_atmosphere)
    target_one = to_cells(truth_one)
    target_two = to_cells(truth_two)
    weight_of = (storm_codes.astype(jnp.float32) / 64.0).reshape(-1, 1, 1, 1)
    full_up, full_down, full_up_bias, full_down_bias = (up_weight, down_weight, up_bias, down_bias)

    def mlp_forward(inputs):
        gathered = lax.all_gather(inputs, "chan", axis=1, tiled=True)
        hidden = jnp.dot(
            gathered, full_up, preferred_element_type=jnp.float32
        ) + full_up_bias.astype(jnp.float32)
        active_full, gelu_pull = jax.vjp(exact_gelu, hidden)
        active = active_full.astype(jnp.bfloat16)
        product = jnp.dot(active, full_down, preferred_element_type=jnp.float32)
        output = lax.psum_scatter(
            product.astype(jnp.bfloat16), "chan", scatter_dimension=1, tiled=True
        ).astype(jnp.float32) + full_down_bias.astype(jnp.float32)
        return (output, (gathered, gelu_pull, active))

    def mlp_backward(gradient, saved):
        gathered, gelu_pull, active = saved
        grad_low = gradient.astype(jnp.bfloat16)
        grad_rows = lax.all_gather(grad_low, "chan", axis=1, tiled=True)
        down_bias_grad = jnp.sum(grad_low.astype(jnp.float32), axis=0)
        down_grad = jnp.dot(active.T, grad_rows, preferred_element_type=jnp.float32)
        active_grad = jnp.dot(grad_rows, full_down.T, preferred_element_type=jnp.float32)
        hidden_grad = gelu_pull(active_grad)[0].astype(jnp.bfloat16)
        up_grad = jnp.dot(gathered.T, hidden_grad, preferred_element_type=jnp.float32)
        up_bias_grad = jnp.sum(hidden_grad.astype(jnp.float32), axis=0)
        input_part = jnp.dot(hidden_grad, full_up.T, preferred_element_type=jnp.float32)
        input_grad = lax.psum_scatter(
            input_part.astype(jnp.bfloat16), "chan", scatter_dimension=1, tiled=True
        ).astype(jnp.float32)
        return (input_grad, (up_grad, up_bias_grad, down_grad, down_bias_grad))

    def forward_block(values):
        normed, first_saved = norm_forward(values, pre_gain, pre_shift)
        modal_in = column_layout(along_rows(normed, tables))
        filtered, core_pull = jax.vjp(
            spectral_core, modal_in, mix_weight_in, mix_bias_in, mix_weight_out, mix_bias_out
        )
        middle = rows_inverse(row_layout(filtered), tables) + normed + values
        entry, second_residuals = norm_forward(middle, post_gain, post_shift)
        output, mlp_saved = mlp_forward(entry.astype(jnp.bfloat16).reshape(total_rows, channels))
        return (
            output.reshape(values.shape) + middle,
            (first_saved, core_pull, second_residuals, mlp_saved),
        )

    def backward_block(gradient, saved):
        first_saved, core_pull, second_residuals, mlp_saved = saved
        mlp_grad, dense_grads = mlp_backward(gradient.reshape(total_rows, channels), mlp_saved)
        middle_part, post_gain_grad, post_shift_grad = norm_backward(
            mlp_grad.reshape(gradient.shape), post_gain, second_residuals
        )
        middle_grad = middle_part + gradient
        filter_grads = core_pull(column_layout(rows_inverse_back(middle_grad, tables)))
        normed_grad = along_rows_back(row_layout(filter_grads[0]), tables) + middle_grad
        input_part, pre_gain_grad, pre_shift_grad = norm_backward(
            normed_grad, pre_gain, first_saved
        )
        return (
            input_part + middle_grad,
            (pre_gain_grad, pre_shift_grad)
            + tuple(filter_grads[1:])
            + (post_gain_grad, post_shift_grad)
            + dense_grads,
        )

    first_out, first_saved_all = forward_block(start_cells)
    second_out, second_saved_all = forward_block(first_out)
    carried, grads_late = backward_block(weight_of * (second_out - target_two), second_saved_all)
    input_grad, grads_early = backward_block(
        weight_of * (first_out - target_one) + carried, first_saved_all
    )
    summed = jax.tree.map(jnp.add, grads_early, grads_late)
    (
        sum_pre_gain,
        sum_pre_shift,
        sum_mix_w_in,
        summed_mixing_bias_input,
        sum_mix_w_out,
        sum_mix_b_out,
        sum_post_gain,
        sum_post_shift,
        sum_up,
        sum_up_bias,
        sum_down,
        sum_down_bias,
    ) = summed
    totals = (
        lax.psum(sum_pre_gain.astype(jnp.bfloat16), "space").astype(jnp.float32),
        lax.psum(sum_pre_shift.astype(jnp.bfloat16), "space").astype(jnp.float32),
        lax.psum(sum_mix_w_in.astype(jnp.bfloat16), "space").astype(jnp.float32),
        lax.psum(summed_mixing_bias_input.astype(jnp.bfloat16), "space").astype(jnp.float32),
        lax.psum(sum_mix_w_out.astype(jnp.bfloat16), "space").astype(jnp.float32),
        lax.psum(sum_mix_b_out.astype(jnp.bfloat16), "space").astype(jnp.float32),
        lax.psum(sum_post_gain.astype(jnp.bfloat16), "space").astype(jnp.float32),
        lax.psum(sum_post_shift.astype(jnp.bfloat16), "space").astype(jnp.float32),
        lax.psum(sum_up.astype(jnp.bfloat16), "space").astype(jnp.float32),
        lax.psum(sum_up_bias.astype(jnp.bfloat16), "space").astype(jnp.float32),
        lax.psum(sum_down.astype(jnp.bfloat16), "space").astype(jnp.float32),
        lax.psum(sum_down_bias.astype(jnp.bfloat16), "space").astype(jnp.float32),
    )
    return (to_flat(first_out), to_flat(second_out), to_flat(input_grad)) + tuple(totals)


BF = jnp.bfloat16
F32 = jnp.float32
MESH_ID = pl.DeviceIdType.MESH
VMEM_BYTES = 66 * 1024 * 1024 - 1024 * 1024


def mm(a, b):
    return jnp.dot(a, b, preferred_element_type=F32)


def mm_nt(a, b):
    return lax.dot_general(a, b, (((1,), (1,)), ((), ())), preferred_element_type=F32)


def mm_tn(a, b):
    return lax.dot_general(a, b, (((0,), (0,)), ((), ())), preferred_element_type=F32)


def halves(v):
    high = v.astype(BF)
    return high, (v - high.astype(F32)).astype(BF)


def mm3(a, b):
    return mm(a[0], b[0]) + (mm(a[0], b[1]) + mm(a[1], b[0]))


def const_halves(table):
    table = np.asarray(table, np.float32)
    high = table.astype(ml_dtypes.bfloat16)
    low = (table - high.astype(np.float32)).astype(ml_dtypes.bfloat16)
    return jnp.asarray(high), jnp.asarray(low)


def row_constants(columns):
    half = columns // 2
    place = np.arange(columns)
    mode = np.arange(half)
    angle = 2.0 * np.pi * np.outer(mode, place) / columns
    real = np.cos(angle)
    imag = -np.sin(angle)
    imag[0] = np.cos(np.pi * place)
    forward = np.concatenate([real, imag]) / np.sqrt(columns)
    weight = np.where(mode == 0, 1.0, 2.0)
    inverse = (forward * np.concatenate([weight, weight])[:, None]).T
    return forward, inverse


def column_constants(height, rows, group):
    owners = height // rows
    angle = 2.0 * np.pi * np.outer(np.arange(height), np.arange(height)) / height
    cosine = np.cos(angle) / np.sqrt(height)
    sine = np.sin(angle) / np.sqrt(height)

    def spread(matrix):
        wide = np.zeros((group, height, owners, group, rows))
        for column in range(group):
            wide[column, :, :, column, :] = matrix.reshape(height, owners, rows)
        return wide.reshape(group * height, owners * group * rows)

    cosine, sine = spread(cosine), spread(sine)
    return np.block([[cosine, sine], [-sine, cosine]])


def signal_peers(axis, count, barrier):
    me = lax.axis_index(axis)
    for step in range(1, count):
        pl.semaphore_signal(
            barrier, inc=1, device_id={axis: lax.rem(me + step, count)}, device_id_type=MESH_ID
        )


def push(axis, count, step, source, target, send_sem, recv_sem):
    peer = lax.rem(lax.axis_index(axis) + step, count)
    return pltpu.make_async_remote_copy(
        src_ref=source,
        dst_ref=target,
        send_sem=send_sem.at[step],
        recv_sem=recv_sem.at[step],
        device_id={axis: peer},
        device_id_type=MESH_ID,
    )


def params(collective_id=None):
    return pltpu.CompilerParams(
        collective_id=collective_id,
        has_side_effects=collective_id is not None,
        vmem_limit_bytes=VMEM_BYTES,
    )


def launch(body, ins, outs, scratch, name, collective_id=None, in_specs=None, out_specs=None, grid=()):
    in_specs, out_specs = in_specs or {}, out_specs or {}
    names = list(ins) + list(outs) + list(scratch)
    whole = pl.BlockSpec(memory_space=pltpu.VMEM)
    results = pl.pallas_call(
        lambda *refs: body(types.SimpleNamespace(**dict(zip(names, refs)))),
        grid=grid,
        in_specs=[in_specs.get(key, whole) for key in ins],
        out_specs=[out_specs.get(key, whole) for key in outs],
        out_shape=[jax.ShapeDtypeStruct(*outs[key]) for key in outs],
        scratch_shapes=list(scratch.values()),
        compiler_params=params(collective_id),
        name=name,
    )(*ins.values())
    return dict(zip(outs, results))


IN_PLACE = pl.BlockSpec(memory_space=pl.ANY)


def sems(*counts):
    return pltpu.SemaphoreType.DMA(counts)


def run_copies(copies):
    for copy in copies:
        copy.start()
    for copy in copies:
        copy.wait()


def cells_from_lines(lines_ref, h, scratch_ref):
    features = scratch_ref.shape[1]
    per = 640 // W
    groups = features // per
    wide = jnp.concatenate(
        [lines_ref[h, pl.ds(part, groups, stride=5), :] for part in range(5)], axis=1
    )
    for part in range(per):
        piece = wide[:, part * W : (part + 1) * W]
        scratch_ref[0, pl.ds(part, groups, stride=per), :] = piece[:, :128]
        scratch_ref[1, pl.ds(part, groups, stride=per), :] = jnp.concatenate(
            [piece[:, 128:], jnp.zeros((groups, 256 - W), F32)], axis=1
        )
    return jnp.concatenate([scratch_ref[0], scratch_ref[1][:, : W - 128]], axis=1)


def enter(lines_ref, cells_ref, scratch_ref):
    def row(h, carry):
        cells_ref[h] = cells_from_lines(lines_ref, h, scratch_ref).T
        return carry

    lax.fori_loop(0, lines_ref.shape[0], row, 0)


def leave(cells_ref, lines_ref, scratch_ref):
    features = scratch_ref.shape[1]
    per = 640 // W
    groups = features // per

    def row(h, carry):
        block = cells_ref[h].T
        scratch_ref[0] = block[:, :128]
        scratch_ref[1] = jnp.concatenate([block[:, 128:], jnp.zeros((features, 256 - W), F32)], axis=1)
        wide = jnp.concatenate(
            [
                piece
                for part in range(per)
                for piece in (
                    scratch_ref[0, pl.ds(part, groups, stride=per), :],
                    scratch_ref[1, pl.ds(part, groups, stride=per), :][:, : W - 128],
                )
            ],
            axis=1,
        )
        for part in range(5):
            lines_ref[h, pl.ds(part, groups, stride=5), :] = wide[:, part * 128 : (part + 1) * 128]
        return carry

    lax.fori_loop(0, lines_ref.shape[0], row, 0)


def pack_lanes(flat_ref, place, real, imag):
    flat_ref[0, place, :] = real[:, :128]
    flat_ref[1, place, :] = imag[:, :128]
    flat_ref[2, place, :] = jnp.concatenate([real[:, 128:], imag[:, 128:]], axis=1)


def join_lanes(first, second, rest):
    real = jnp.concatenate([first, rest[:, :64]], axis=1)
    imag = jnp.concatenate([second, rest[:, 64:]], axis=1)
    return real, imag


def unpack_lanes(flat_ref, place):
    return join_lanes(flat_ref[0, place, :], flat_ref[1, place, :], flat_ref[2, place, :])


LEVEL = 32000.0


class Exchange:
    def __init__(self, fixed, spaces, thick, send_ref, recv_ref, send_sem, recv_sem, scales=None):
        self.fixed, self.scales = fixed, scales
        self.spaces, self.thick = spaces, thick
        self.send_ref, self.recv_ref = send_ref, recv_ref
        self.send_sem, self.recv_sem = send_sem, recv_sem
        self.me = lax.axis_index("space")

    @staticmethod
    def shape(fixed, spaces, thick, pairs):
        return pltpu.VMEM((pairs, spaces, 3 * thick, 128), jnp.int16 if fixed else BF)

    def copy(self, p, step):
        peer = lax.rem(self.me + step, self.spaces)
        return pltpu.make_async_remote_copy(
            src_ref=self.send_ref.at[p, peer],
            dst_ref=self.recv_ref.at[p, self.me],
            send_sem=self.send_sem.at[p, step],
            recv_sem=self.recv_sem.at[p, step],
            device_id={"space": peer},
            device_id_type=MESH_ID,
        )

    def scale_copy(self, step):
        own_ref, all_ref, send_sem, recv_sem = self.scales
        return push("space", self.spaces, step, own_ref, all_ref.at[self.me], send_sem, recv_sem)

    def send_scales(self, flat_ref):
        own_ref, all_ref = self.scales[:2]
        largest = jnp.max(jnp.abs(flat_ref[...]), axis=1)
        own_ref[0:3, :] = jnp.maximum(largest, 1e-30) * (1.0 / LEVEL)
        own_ref[3:8, :] = jnp.ones((5, 128), F32)
        for step in range(1, self.spaces):
            self.scale_copy(step).start()
        all_ref[self.me] = own_ref[...]
        self.factor = 1.0 / own_ref[...]

    def encode(self, values):
        if not self.fixed:
            return jnp.concatenate([values[k] for k in range(3)], axis=0).astype(BF)
        lines = [jnp.round(values[k] * self.factor[k : k + 1]) for k in range(3)]
        return jnp.concatenate(lines, axis=0).astype(jnp.int32).astype(jnp.int16)

    def send(self, p, flat_ref, start_of):
        for step in list(range(1, self.spaces)) + [0]:
            peer = lax.rem(self.me + step, self.spaces)
            rows = pl.ds(pl.multiple_of(start_of(peer), 8), self.thick)
            coded = self.encode(flat_ref[:, rows, :])
            if step:
                self.send_ref[p, peer] = coded
                self.copy(p, step).start()
            else:
                self.recv_ref[p, peer] = coded

    def arrive(self, p):
        for step in range(1, self.spaces):
            self.copy(p, step).wait_recv()

    def arrive_scales(self):
        for step in range(1, self.spaces):
            self.scale_copy(step).wait_recv()

    def take(self, p, source):
        coded = self.recv_ref[p, source]
        values = (coded.astype(jnp.int32) if self.fixed else coded).astype(F32)
        parts = [values[k * self.thick : (k + 1) * self.thick] for k in range(3)]
        if self.fixed:
            scale = self.scales[1][source]
            parts = [part * scale[k : k + 1] for k, part in enumerate(parts)]
        return parts

    def close(self, pairs):
        def pair(p, carry):
            for step in range(1, self.spaces):
                self.copy(p, step).wait_send()
            return carry

        lax.fori_loop(0, pairs, pair, 0)
        if self.fixed:
            for step in range(1, self.spaces):
                self.scale_copy(step).wait_send()


def pair_inputs(q, exchange, even_ref):
    p = jnp.maximum(q - 1, 0)

    @pl.when(q != 1)
    def _():
        exchange.arrive(p)

    if exchange.fixed:

        @pl.when(q == 0)
        def _():
            exchange.arrive_scales()

    extra = (q == 0).astype(F32)
    zeroth = jnp.logical_and(exchange.me == 0, p == 0).astype(F32)
    parts = [join_lanes(*exchange.take(p, s)) for s in range(exchange.spaces)]
    real = jnp.concatenate([part[0] for part in parts], axis=0)
    imag = jnp.concatenate([part[1] for part in parts], axis=0)
    chosen = imag * (even_ref[...] * zeroth)
    real = real * (1.0 - extra) + chosen * extra
    imag = (imag - chosen) * (1.0 - extra)
    return p, zeroth, jnp.concatenate([real, imag], axis=0)


def pair_outputs(q, p, zeroth, result, exchange, even_ref, kept_ref, stage_ref):
    half = result.shape[0] // 2
    real, imag = result[:half], result[half:]

    @pl.when(q == 0)
    def _():
        kept_ref[...] = real

    @pl.when(q > 0)
    def _():
        chosen = even_ref[...] * zeroth
        pack_lanes(stage_ref, slice(None), real, imag * (1.0 - chosen) + kept_ref[...] * chosen)
        exchange.send(p, stage_ref, lambda peer: peer * exchange.thick)


def collect(exchange, pairs, chunk, flat_ref):
    def pair(p, carry):
        exchange.arrive(p)
        for s in range(exchange.spaces):
            rows = pl.ds(pl.multiple_of(s * chunk + p * exchange.thick, 8), exchange.thick)
            for k, part in enumerate(exchange.take(p, s)):
                flat_ref[k, rows, :] = part
        return carry

    lax.fori_loop(0, pairs, pair, 0)


def send_modes(exchange, pairs, chunk, flat_ref):
    if exchange.fixed:
        exchange.send_scales(flat_ref)

    def pair(p, carry):
        exchange.send(p, flat_ref, lambda peer: peer * chunk + p * exchange.thick)
        return carry

    lax.fori_loop(0, pairs, pair, 0)


class Plan:
    def __init__(self, rows, features, columns, spaces, chans, local):
        self.rows, self.features, self.columns = rows, features, columns
        self.spaces, self.chans, self.local = spaces, chans, local
        self.modes = columns // 2
        self.total = self.modes * rows
        self.chunk = self.total // spaces
        self.thick = 2 * rows
        self.half = self.thick * spaces
        self.pairs = self.chunk // self.thick
        self.cells = rows * columns // chans
        self.share = rows // chans
        self.width = features * chans
        self.tile = 256
        self.per = local // self.tile
        self.steps = chans * self.per
        self.size = features // 2
        self.small = 8 * self.size + 16
        self.field = ((rows, columns, features), F32)
        self.by_cells = ((chans, self.share, columns // 2 * 3, 128), BF)
        self.wide = ((self.cells, self.width), BF)
        self.tiles = ((self.steps, self.cells, self.tile), BF)
        self.lines = ((rows, features * columns // 128, 128), F32)
        self.dev = ((-(-rows // 8) * 8, columns), F32)
        self.dev_wide = ((self.cells, 128), F32)
        self.kept = ((self.pairs + 1, 2 * self.half, features), BF)
        self.mix = ((2, 2, 2, features, features), BF)
        self.weights = ((2, chans, local, self.width), BF)
        self.rest = ((chans, 8, local), F32)
        self.sums = ((self.small, 128), F32)
        self.grads = ((2, self.steps, self.tile, self.width), BF)
        self.vectors = ((chans, 8, local), F32)

    def exchange_scratch(self, fixed_there, fixed_back):
        made = {}
        for name, fixed in (("1", fixed_there), ("2", fixed_back)):
            shape = Exchange.shape(fixed, self.spaces, self.thick, self.pairs)
            made["send" + name] = made["recv" + name] = shape
            made["s" + name] = made["r" + name] = sems(self.pairs, self.spaces)
        if fixed_there:
            made["scale"] = pltpu.VMEM((8, 128), F32)
            made["scale_all"] = pltpu.VMEM((self.spaces, 8, 128), F32)
            made["s20"] = made["r20"] = sems(self.spaces)
        return made

    def spectral_scratch(self):
        return {
            "flat": pltpu.VMEM((3, self.total, 128), F32),
            "stage": pltpu.VMEM((3, self.half, 128), F32),
            "last": pltpu.VMEM((self.half, self.features), F32),
            "turn": pltpu.VMEM((2, self.features, 128), F32),
            "even": pltpu.VMEM((self.half, self.features), F32),
        }


def pack_cells(value):
    side = value.shape[0] // 2
    rest = value[:, 128:]
    return jnp.concatenate([value[:, :128], jnp.concatenate([rest[:side], rest[side:]], axis=1)], axis=0)


def unpack_cells(packed):
    columns = packed.shape[0] // 3 * 2
    rest = packed[columns:]
    rest = jnp.concatenate([rest[:, :64], rest[:, 64:]], axis=0)
    return jnp.concatenate([packed[:columns], rest], axis=1)


def three_parts(v):
    a = v.astype(BF)
    rest = v - a.astype(F32)
    b = rest.astype(BF)
    return [a, b, (rest - b.astype(F32)).astype(BF)]


def stack_rows(rows):
    lines = [part.astype(F32) for row in rows for part in three_parts(row)]
    lines.append(jnp.zeros((16 - len(lines), rows[0].shape[1]), F32))
    return jnp.concatenate(lines, axis=0).astype(BF)


def over_lanes(table, features, number):
    line = lax.broadcasted_iota(jnp.int32, (16, features), 0)
    chosen = jnp.logical_and(line >= 3 * number, line < 3 * number + 3)
    return mm_tn(table, jnp.where(chosen, 1.0, 0.0).astype(BF))


def lane_sums(value):
    return mm_nt(jnp.ones((16, value.shape[1]), BF), value.astype(BF))[0:1]


def scratch_of(shaped):
    return pltpu.VMEM(*shaped)


def mark_even(plan, r):
    row = lax.broadcasted_iota(jnp.int32, (plan.half, plan.features), 0)
    r.even[...] = jnp.where(lax.rem(lax.div(row, plan.rows), 2) == 0, 1.0, 0.0)


def greet(plan):
    barrier = pltpu.get_barrier_semaphore()
    signal_peers("space", plan.spaces, barrier)
    signal_peers("chan", plan.chans, barrier)
    return lambda: pl.semaphore_wait(barrier, plan.spaces + plan.chans - 2)


def spread_chan(plan, source_ref, target_ref, send_sem, recv_sem):
    me = lax.axis_index("chan")
    copies = []
    for step in range(1, plan.chans):
        peer = lax.rem(me + step, plan.chans)
        copy = push("chan", plan.chans, step, source_ref.at[peer], target_ref.at[me], send_sem, recv_sem)
        copy.start()
        copies.append(copy)
    target_ref[me] = source_ref[me]
    return copies


def wait_all(copies):
    for copy in copies:
        copy.wait()


def rows_to_modes(plan, table, flat_ref, value_of, exact):
    def row(h, carry):
        value = value_of(h)
        out = mm3(table, halves(value)) if exact else mm(table, value.astype(BF))
        pack_lanes(flat_ref, pl.ds(h, plan.modes, stride=plan.rows), out[: plan.modes], out[plan.modes :])
        return carry

    lax.fori_loop(0, plan.rows, row, 0, unroll=4)


def filter_forward(plan, r, there, back, aside=None):
    half = plan.half

    def filter_pair(q, carry):
        if aside is not None:
            pl.when(q == plan.pairs)(aside)
        p, zeroth, block = pair_inputs(q, there, r.even)
        spec = mm3((r.col[0], r.col[1]), halves(block))
        r.spec[q] = spec.astype(BF)
        parts = halves(spec)
        straight = mm3(parts, (r.mix[0, 0, 0], r.mix[0, 0, 1]))
        crossed = mm3(parts, (r.mix[0, 1, 0], r.mix[0, 1, 1]))
        first = jnp.concatenate(
            [
                jnp.maximum(straight[:half] - crossed[half:] + r.bias[0:1], 0.0),
                jnp.maximum(straight[half:] + crossed[:half] + r.bias[1:2], 0.0),
            ],
            axis=0,
        )
        r.first[q] = first.astype(BF)
        parts = halves(first)
        straight = mm3(parts, (r.mix[1, 0, 0], r.mix[1, 0, 1]))
        crossed = mm3(parts, (r.mix[1, 1, 0], r.mix[1, 1, 1]))
        second = jnp.concatenate(
            [
                straight[:half] - crossed[half:] + r.bias[2:3],
                straight[half:] + crossed[:half] + r.bias[3:4],
            ],
            axis=0,
        )
        second = second - jnp.clip(second, -SHRINK_LEVEL, SHRINK_LEVEL)
        r.second[q] = second.astype(BF)
        result = mm(r.colinv[...], r.second[q])
        pair_outputs(q, p, zeroth, result, back, r.even, r.last, r.stage)
        return carry

    lax.fori_loop(0, plan.pairs + 1, filter_pair, 0)


def modes_to_rows(plan, flat_ref, h):
    real, imag = unpack_lanes(flat_ref, pl.ds(h, plan.modes, stride=plan.rows))
    return jnp.concatenate([real, imag], axis=0)


def rows_of_chunks(plan, row, send_chunk):
    me = lax.axis_index("chan")
    for step in list(range(1, plan.chans)) + [0]:
        peer = lax.rem(me + step, plan.chans)

        def one(i, carry):
            row(peer * plan.share + i, peer, i)
            return carry

        lax.fori_loop(0, plan.share, one, 0, unroll=True)
        send_chunk(step, peer)


def rows_forward(plan, r, unit_ref, x_ref, middle_ref):
    me = lax.axis_index("chan")
    gain, shift = r.gain[...].reshape(1, -1), r.shift[...].reshape(1, -1)
    copies = []

    def row(h, peer, place):
        block = modes_to_rows(plan, r.flat, h)
        out = mm(r.rowinv[...], block.astype(BF))
        middle = out + (unit_ref[h] * gain + shift) + x_ref[h]
        middle_ref[h] = middle
        r.own[peer, place] = pack_cells(middle).astype(BF)

    def send_chunk(step, peer):
        if step:
            copy = push("chan", plan.chans, step, r.own.at[peer], r.mid.at[me], r.s3, r.r3)
            copy.start()
            copies.append(copy)
        else:
            r.mid[me] = r.own[me]

    rows_of_chunks(plan, row, send_chunk)
    return copies


class Block:
    def __init__(self, plan, group, side):
        self.group, self.side, self.size = group, side, plan.columns // 2
        start = group * plan.columns + side * self.size
        self.cells = pl.ds(pl.multiple_of(start, 16), self.size)
        self.front = slice(side * self.size, (side + 1) * self.size)
        self.back = slice(plan.columns, plan.columns + self.size)
        self.lanes = slice(64 * side, 64 * side + 64)

    def get(self, chunks_ref):
        parts = []
        for j in range(chunks_ref.shape[0]):
            parts.append(chunks_ref[j, self.group, self.front, :].astype(F32))
            parts.append(chunks_ref[j, self.group, self.back, self.lanes].astype(F32))
        return jnp.concatenate(parts, axis=1)

    def put(self, chunks_ref, value):
        chans = chunks_ref.shape[0]
        features = value.shape[1] // chans
        for j in range(chans):
            part = value[:, j * features : (j + 1) * features].astype(BF)
            chunks_ref[j, self.group, self.front, :] = part[:, :128]
            chunks_ref[j, self.group, self.back, self.lanes] = part[:, 128:]


def by_blocks(plan, step):
    def one(group, carry):
        for side in range(2):
            step(Block(plan, group, side))
        return carry

    lax.fori_loop(0, plan.share, one, 0, unroll=True)


def full_vector(gathered_ref, start, size):
    chans = gathered_ref.shape[0]
    return jnp.concatenate([gathered_ref[j, 1:2, start : start + size] for j in range(chans)], axis=1)


def moments(value):
    mean = jnp.mean(value, axis=1, keepdims=True)
    centred = value - mean
    return mean, centred, lax.rsqrt(jnp.mean(centred * centred, axis=1, keepdims=True) + NORM_EPS)


ERF = (0.254829592, -0.284496736, 1.421413741, -1.453152027, 1.061405429)


def gelu_and_slope(v):
    e = jnp.exp2(v * v * (-0.5 / math.log(2.0)))
    below = 1.0 + (0.3275911 * math.sqrt(0.5)) * jnp.abs(v)
    t = pl.reciprocal(below, approx=True)
    t = t * (2.0 - below * t)
    c = [0.5 * k for k in ERF]
    tail = (e * t) * (c[0] + t * (c[1] + t * (c[2] + t * (c[3] + t * c[4]))))
    below = jnp.where(v >= 0.0, 1.0 - tail, tail)
    active = v * below
    return active, below + (v * (1.0 / math.sqrt(2.0 * math.pi))) * e


def tile_of(plan, t):
    return t // plan.per, pl.ds(pl.multiple_of((t % plan.per) * plan.tile, plan.tile), plan.tile)


def up_tile(plan, r, t):
    j, place = tile_of(plan, t)
    return r.w[0, j, :, place]


def down_tile(plan, r, t):
    j, place = tile_of(plan, t)
    return r.w[1, j, place, :]


def ffn_scratch(plan):
    shape = (plan.cells, plan.tile)
    made = {key: pltpu.VMEM(shape, F32) for key in ("wide_a", "wide_b")}
    made.update({key: pltpu.VMEM(shape, BF) for key in ("thin_a", "thin_b")})
    made.update(
        total=pltpu.VMEM((plan.cells, plan.width), F32),
        entry=scratch_of(plan.wide),
        unit_wide=scratch_of(plan.wide),
        dev_wide=scratch_of(plan.dev_wide),
        active=scratch_of(plan.tiles),
        slope=scratch_of(plan.tiles),
        gathered=scratch_of(plan.vectors),
    )
    return made


def staggered(plan, r, lead, turn, trail, ready=None):
    last = plan.steps - 1
    third = plan.cells // 3
    side = plan.cells // 2
    parts = plan.width // plan.tile
    r.thin_b[...] = jnp.zeros_like(r.thin_b)
    for k in range(2):
        r.wide_a[k * side : (k + 1) * side, :] = lead(0, slice(k * side, (k + 1) * side))

    def half_step(t, wide_now, wide_next, thin_past, thin_now):
        ahead, behind = jnp.minimum(t + 1, last), jnp.maximum(t - 1, 0)
        for k in range(3):
            place = slice(k * third, (k + 1) * third)
            thin_now[place, :] = turn(wide_now[place, :], t, place, k == 0)
            if k < 2:
                own = slice(k * side, (k + 1) * side)
                wide_next[own, :] = lead(ahead, own)
            trail(thin_past[...], behind, slice(k * parts // 3 * plan.tile, (k + 1) * parts // 3 * plan.tile))

    def pair(u, carry):
        if ready is not None:
            for chunk in range(1, plan.chans):
                pl.when(u == (chunk * plan.per - 1) // 2)(functools.partial(ready, chunk))
        half_step(2 * u, r.wide_a, r.wide_b, r.thin_b, r.thin_a)
        half_step(2 * u + 1, r.wide_b, r.wide_a, r.thin_a, r.thin_b)
        return carry

    lax.fori_loop(0, plan.steps // 2, pair, 0)
    trail(r.thin_b[...], last, slice(0, plan.width))


def ffn_forward(plan, r):
    gain = full_vector(r.gathered, 0, plan.features)
    shift = full_vector(r.gathered, plan.features, plan.features)
    bias = full_vector(r.gathered, 2 * plan.features, plan.features)

    def prepare(block):
        place = block.cells
        mean, centred, inverse = moments(block.get(r.mid))
        unit = centred * inverse
        r.unit_wide[place, :] = unit.astype(BF)
        r.dev_wide[place, :] = jnp.broadcast_to(inverse, (block.size, 128))
        r.entry[place, :] = (unit * gain + shift).astype(BF)
        r.total[place, :] = jnp.broadcast_to(bias, (block.size, plan.width))

    by_blocks(plan, prepare)

    def lead(t, rows):
        j, place = tile_of(plan, t)
        return mm(r.entry[rows, :], up_tile(plan, r, t)) + r.gathered[j, 0:1, place]

    def turn(value, t, rows, opening):
        active, slope = gelu_and_slope(value)
        active = active.astype(BF)
        r.active[t, rows, :] = active
        r.slope[t, rows, :] = slope.astype(BF)
        return active

    def trail(active, t, lanes):
        j, place = tile_of(plan, t)
        r.total[:, lanes] += mm(active, r.w[1, j, place, lanes])

    staggered(plan, r, lead, turn, trail)


def ffn_backward(plan, r, ready=None):
    r.small[...] = jnp.zeros_like(r.small)
    r.total[...] = jnp.zeros_like(r.total)

    def lead(t, rows):
        return mm_nt(r.upper[rows, :], down_tile(plan, r, t))

    def turn(value, t, rows, opening):
        lower = value * r.slope[t, rows, :].astype(F32)
        bias = jnp.sum(lower, axis=0, keepdims=True)
        r.upb[pl.ds(t, 1), :] = bias if opening else r.upb[pl.ds(t, 1), :] + bias
        lower = lower.astype(BF)
        r.slope[t, rows, :] = lower
        return lower

    def trail(lower, t, lanes):
        j, place = tile_of(plan, t)
        r.total[:, lanes] += mm_nt(lower, r.w[0, j, lanes, place])

    staggered(plan, r, lead, turn, trail, ready)
    gain = full_vector(r.gathered, 0, plan.features)

    def finish(block):
        place = block.cells
        grad = r.total[place, :]
        unit = r.unit_wide[place, :].astype(F32)
        r.small[0:1, :] += jnp.sum(grad * unit, axis=0, keepdims=True)
        r.small[1:2, :] += jnp.sum(grad, axis=0, keepdims=True)
        r.small[2:3, :] += jnp.sum(r.upper[place, :].astype(F32), axis=0, keepdims=True)
        scaled = grad * gain
        one = jnp.mean(scaled, axis=1, keepdims=True)
        two = jnp.mean(scaled * unit, axis=1, keepdims=True)
        result = r.dev_wide[place, :][:, :1] * (scaled - one - unit * two)
        block.put(r.leaving, result)

    by_blocks(plan, finish)


def vector_gradients(plan, r, rest_ref):
    rest_ref[...] = jnp.zeros_like(rest_ref)
    for j in range(plan.chans):
        for k in range(plan.per):
            line = j * plan.per + k
            rest_ref[j, 0:1, k * plan.tile : (k + 1) * plan.tile] = r.upb[line : line + 1, :]
        for k in range(3):
            rest_ref[j, 1 + k : 2 + k, 0 : plan.features] = r.small[
                k : k + 1, j * plan.features : (j + 1) * plan.features
            ]


def weight_gradients(r, t):
    return mm_tn(r.active[t], r.upper[...]), mm_tn(r.slope[t], r.entry[...])


def filter_backward(plan, r, there, back, aside=None):
    half = plan.half
    r.mixgrad[...] = jnp.zeros_like(r.mixgrad)
    r.biasgrad[...] = jnp.zeros_like(r.biasgrad)

    def turned(v):
        return jnp.concatenate([v[half:], -v[:half]], axis=0)

    def note_bias(index, value):
        r.biasgrad[index : index + 1, :] += jnp.sum(value, axis=0, keepdims=True)

    def through(low, layer):
        straight = mm_nt(low, r.mix[layer, 0, 0])
        crossed = mm_nt(low, r.mix[layer, 1, 0])
        return jnp.concatenate([straight[:half] + crossed[half:], straight[half:] - crossed[:half]], axis=0)

    def filter_pair(q, carry):
        if aside is not None:
            pl.when(q == 3)(aside)
        p, zeroth, block = pair_inputs(q, there, r.even)
        grad = mm(r.col[0], block.astype(BF))
        grad = jnp.where(r.second[q].astype(F32) == 0.0, 0.0, grad)
        note_bias(2, grad[:half])
        note_bias(3, grad[half:])
        low = grad.astype(BF)
        first = r.first[q]
        r.mixgrad[1, 0] += mm_tn(first, low)
        r.mixgrad[1, 1] += mm_tn(first, turned(grad).astype(BF))
        grad = jnp.where(first.astype(F32) > 0.0, through(low, 1), 0.0)
        note_bias(0, grad[:half])
        note_bias(1, grad[half:])
        low = grad.astype(BF)
        spec = r.spec[q]
        r.mixgrad[0, 0] += mm_tn(spec, low)
        r.mixgrad[0, 1] += mm_tn(spec, turned(grad).astype(BF))
        result = mm(r.colinv[...], through(low, 0).astype(BF))
        pair_outputs(q, p, zeroth, result, back, r.even, r.last, r.stage)
        return carry

    lax.fori_loop(0, plan.pairs + 1, filter_pair, 0)


def mix_gradients(plan, r, before_ref):
    size = plan.size
    for layer in range(2):
        for part in range(2):
            for block in range(2):
                own = slice(block * size, (block + 1) * size)
                piece = r.mixgrad[layer, part][own, own]
                piece = jnp.concatenate([piece, jnp.zeros((size, 128 - size), F32)], axis=1)
                start = ((layer * 2 + part) * 2 + block) * size
                place = slice(start, start + size)
                r.sums[place, :] = piece if before_ref is None else piece + before_ref[place, :]


def rows_backward(plan, r, unit_ref, before_ref):
    gain = r.gain[...].reshape(1, -1)
    me = lax.axis_index("chan")

    def row(h, carry):
        one_sum, two_sum = carry
        block = modes_to_rows(plan, r.flat, h)
        grad = mm(r.row_t[...], block.astype(BF)) + r.out[h]
        unit = unit_ref[h]
        one_sum += jnp.sum(grad * unit, axis=0, keepdims=True)
        two_sum += jnp.sum(grad, axis=0, keepdims=True)
        scaled = grad * gain
        r.scaled[h] = scaled
        r.mine[pl.ds(h, 1), :] = lane_sums(scaled)
        r.mine[pl.ds(plan.rows + h, 1), :] = lane_sums(scaled * unit)
        return one_sum, two_sum

    none = jnp.zeros((1, plan.features), F32)
    one_sum, two_sum = lax.fori_loop(0, plan.rows, row, (none, none), unroll=4)
    r.all[me] = r.mine[...]
    copies = [
        push("chan", plan.chans, step, r.mine, r.all.at[me], r.s4, r.r4) for step in range(1, plan.chans)
    ]
    for copy in copies:
        copy.start()
    vectors = jnp.concatenate([r.biasgrad[0:4], one_sum, two_sum, none, none], axis=0)
    wide = jnp.concatenate([vectors, jnp.zeros((8, 256 - plan.features), F32)], axis=1)
    wide = jnp.concatenate([wide[:, :128], wide[:, 128:]], axis=0)
    place = slice(8 * plan.size, plan.small)
    r.sums[place, :] = wide if before_ref is None else wide + before_ref[place, :]
    return copies


def input_gradient(plan, r, unit_ref, dev_ref):
    r.mine[...] = sum(r.all[j] for j in range(plan.chans)) * (1.0 / plan.width)

    def result(h):
        table = stack_rows(
            [r.mine[pl.ds(h, 1), :], r.mine[pl.ds(plan.rows + h, 1), :], dev_ref[pl.ds(h, 1), :]]
        )
        one, two, dev = [over_lanes(table, plan.features, k) for k in range(3)]
        return r.out[h] + dev * (r.scaled[h] - one - unit_ref[h] * two)

    return result


def norm_sums_scratch(plan):
    return {
        "scaled": scratch_of(plan.field),
        "mixgrad": pltpu.VMEM((2, 2, plan.features, plan.features), F32),
        "biasgrad": pltpu.VMEM((8, plan.features), F32),
        "mine": pltpu.VMEM((2 * plan.rows, plan.columns), F32),
        "all": pltpu.VMEM((plan.chans, 2 * plan.rows, plan.columns), F32),
        "s4": sems(plan.chans),
        "r4": sems(plan.chans),
    }


class Moves:
    def __init__(self, sem):
        self.sem, self.count, self.open = sem, 0, []

    def start(self, source, target):
        copy = pltpu.make_async_copy(source, target, self.sem.at[self.count])
        self.count += 1
        copy.start()
        self.open.append(copy)
        return copy

    def close(self):
        wait_all(self.open)


def launch_first(plan, args, tables):
    rows, features, chans = plan.rows, plan.features, plan.chans

    def body(r):
        me = lax.axis_index("chan")
        place = lax.axis_index("space")
        core = lax.rem(place, 2)
        sibling = place + 1 - 2 * core
        met = greet(plan)
        moves = Moves(r.dma)
        moves.start(r.up, r.w.at[0, me])
        moves.start(r.down, r.w.at[1, me])
        loaded = moves.start(r.lines_t, r.lines_in)
        own_weights = moves.open[:2]
        moves.open = []

        beside = me + 1 - 2 * lax.rem(me, 2)
        across = me + 2 - 4 * (me // 2)
        far = chans - 1 - me
        upper_half, lower_half = pl.ds(0, plan.local // 2), pl.ds(plan.local // 2, plan.local // 2)

        def hand(source, target, number, device):
            return pltpu.make_async_remote_copy(
                src_ref=source,
                dst_ref=target,
                send_sem=r.s5.at[number],
                recv_sem=r.r5.at[number],
                device_id=device,
                device_id_type=MESH_ID,
            )

        def own_to(number, source):
            peer = (beside, across)[number]
            return hand(source, r.w.at[core, me], number, {"chan": peer})

        def relay(number):
            slot = (beside, across)[number]
            part = r.w.at[core, slot, (upper_half, lower_half)[number]]
            return hand(part, part, 2 + number, {"chan": (across, beside)[number]})

        def to_core(number):
            if number < 2:
                part = r.w.at[core, (beside, across)[number]]
            else:
                part = r.w.at[core, far]
            return pltpu.make_async_remote_copy(
                src_ref=part,
                dst_ref=part,
                send_sem=r.s7.at[number],
                recv_sem=r.r7.at[number],
                device_id={"space": sibling},
                device_id_type=MESH_ID,
            )

        def pass_near():
            for number in range(2):
                own_to(number, r.up).wait_recv()
            for number in range(2):
                relay(number).start()
            for number in range(2):
                to_core(number).start()

        def pass_far():
            for number in range(2):
                relay(number).wait_recv()
            to_core(2).start()

        def close_weights():
            for number in range(2):
                own_to(number, r.up).wait_send()
                relay(number).wait_send()
            for number in range(3):
                to_core(number).wait()

        def first(h, carry):
            block = cells_from_lines(r.lines_x, h, r.turn)
            r.turned[h] = block
            total = jnp.sum(block, axis=0, keepdims=True)
            centred = block - total * (1.0 / features)
            r.mine[pl.ds(h, 1), :] = total
            r.mine[pl.ds(rows + h, 1), :] = jnp.sum(centred * centred, axis=0, keepdims=True)
            return carry

        lax.fori_loop(0, rows, first, 0)
        r.all[me] = r.mine[...]
        met()
        sums = [push("chan", chans, step, r.mine, r.all.at[me], r.s4, r.r4) for step in range(1, chans)]
        for copy in sums:
            copy.start()
        mark_even(plan, r)

        def row_of(ref):
            return ref[...].reshape(1, -1).astype(F32)

        r.vectors[...] = jnp.zeros_like(r.vectors)
        r.vectors[0:1, :] = row_of(r.upb)
        r.vectors[1:2, 0:features] = row_of(r.post_gain)
        r.vectors[1:2, features : 2 * features] = row_of(r.post_shift)
        r.vectors[1:2, 2 * features : 3 * features] = row_of(r.downb)
        r.gathered[me] = r.vectors[...]
        for layer, (source, bias) in enumerate(((r.mix_in, r.bias_in), (r.mix_out, r.bias_out))):
            for part in range(2):
                zero = jnp.zeros((plan.size, plan.size), F32)
                value = jnp.concatenate(
                    [
                        jnp.concatenate([source[part, 0], zero], axis=1),
                        jnp.concatenate([zero, source[part, 1]], axis=1),
                    ],
                    axis=0,
                )
                high, low = halves(value)
                r.mix[layer, part, 0] = high
                r.mix[layer, part, 1] = low
                line = 2 * layer + part
                r.bias[line : line + 1, :] = jnp.concatenate([bias[part, 0:1, :], bias[part, 1:2, :]], axis=1)
        moves.start(r.mix, r.mix_kept)

        wait_all(sums)
        given = [push("chan", chans, step, r.vectors, r.gathered.at[me], r.s6, r.r6) for step in range(1, chans)]
        for copy in given:
            copy.start()
        for kind, source in enumerate((r.up, r.down)):

            @pl.when(core == kind)
            def _():
                for number in range(2):
                    own_to(number, source).start()

        totals = [r.all[j] for j in range(chans)]
        mean = sum(t[:rows] for t in totals) * (1.0 / plan.width)
        spread_sum = sum(
            t[rows:] + features * jnp.square(t[:rows] * (1.0 / features) - mean) for t in totals
        ) * (1.0 / plan.width)
        r.mine[pl.ds(0, rows), :] = mean
        r.mine[pl.ds(rows, rows), :] = lax.rsqrt(spread_sum + NORM_EPS)
        gain, shift = r.gain[...].reshape(1, -1), r.shift[...].reshape(1, -1)

        def normed(h):
            block = r.turned[h]
            inverse = r.mine[pl.ds(rows + h, 1), :]
            r.x[h] = block.T
            unit = ((block - r.mine[pl.ds(h, 1), :]) * inverse).T
            r.unit[h] = unit
            r.dev[pl.ds(h, 1), :] = inverse
            return unit * gain + shift

        scales = (r.scale, r.scale_all, r.s20, r.r20)
        there = Exchange(True, plan.spaces, plan.thick, r.send1, r.recv1, r.s1, r.r1, scales)
        back = Exchange(False, plan.spaces, plan.thick, r.send2, r.recv2, r.s2, r.r2)
        rows_to_modes(plan, (r.row[0], r.row[1]), r.flat, normed, True)
        send_modes(there, plan.pairs, plan.chunk, r.flat)
        moves.start(r.unit, r.unit_kept)
        moves.start(r.dev, r.dev_kept)
        loaded.wait()
        enter(r.lines_in, r.cells_t, r.turn)
        moves.start(r.cells_t, r.cells_kept)
        filter_forward(plan, r, there, back, pass_near)
        for source, target in ((r.spec, r.spec_kept), (r.first, r.first_kept), (r.second, r.second_kept)):
            moves.start(source, target)
        collect(back, plan.pairs, plan.chunk, r.flat)
        pass_far()
        copies = rows_forward(plan, r, r.unit, r.x, r.middle)
        moves.start(r.middle, r.middle_kept)
        wait_all(copies + given)
        close_weights()
        wait_all(own_weights)
        moves.start(r.w, r.w_kept)
        ffn_forward(plan, r)
        saved = ("active", "slope", "entry", "unit_wide", "dev_wide", "gathered")
        for key in saved:
            moves.start(getattr(r, key), getattr(r, key + "_kept"))

        def last(block):
            outer = r.total[block.cells, :]
            mean, _, inverse = moments(outer + block.get(r.mid))
            block.put(r.leaving, outer)
            r.stats[block.group, block.front, :] = jnp.concatenate(
                three_parts(mean) + three_parts(inverse) + [jnp.zeros((block.size, 122), BF)], axis=1
            )

        by_blocks(plan, last)
        copies = spread_chan(plan, r.leaving, r.home, r.s8, r.r8)
        for group in range(plan.share):
            r.stats_thin[group] = r.stats[group].astype(F32).T[:16].astype(BF)
        others = [
            push("chan", chans, step, r.stats_thin, r.stats_home.at[me], r.s9, r.r9) for step in range(1, chans)
        ]
        for copy in others:
            copy.start()
        r.stats_home[me] = r.stats_thin[...]
        wait_all(copies + others)
        there.close(plan.pairs)
        back.close(plan.pairs)
        moves.close()

    stats = ((chans, plan.share, 16, plan.columns), BF)
    outs = {
        "home": plan.by_cells,
        "stats_home": stats,
        "middle_kept": plan.field,
        "unit_kept": plan.field,
        "dev_kept": plan.dev,
        "cells_kept": plan.field,
        "spec_kept": plan.kept,
        "first_kept": plan.kept,
        "second_kept": plan.kept,
        "mix_kept": plan.mix,
        "w_kept": plan.weights,
        "active_kept": plan.tiles,
        "slope_kept": plan.tiles,
        "entry_kept": plan.wide,
        "unit_wide_kept": plan.wide,
        "dev_wide_kept": plan.dev_wide,
        "gathered_kept": plan.vectors,
        "bias": ((8, features), F32),
    }
    ins = dict(args)
    ins.update({key: tables[key] for key in ("row", "rowinv", "col", "colinv")})
    scratch = {
        "dma": sems(20),
        "x": scratch_of(plan.field),
        "unit": scratch_of(plan.field),
        "dev": scratch_of(plan.dev),
        "middle": scratch_of(plan.field),
        "cells_t": scratch_of(plan.field),
        "lines_in": scratch_of(plan.lines),
        "turned": pltpu.VMEM((rows, features, plan.columns), F32),
        "mine": pltpu.VMEM((2 * rows, plan.columns), F32),
        "all": pltpu.VMEM((chans, 2 * rows, plan.columns), F32),
        "spec": scratch_of(plan.kept),
        "first": scratch_of(plan.kept),
        "second": scratch_of(plan.kept),
        "mix": scratch_of(plan.mix),
        "w": scratch_of(plan.weights),
        "vectors": pltpu.VMEM((8, plan.local), F32),
        "own": scratch_of(plan.by_cells),
        "mid": scratch_of(plan.by_cells),
        "leaving": scratch_of(plan.by_cells),
        "stats": pltpu.VMEM((plan.share, plan.columns, 128), BF),
        "stats_thin": pltpu.VMEM(stats[0][1:], BF),
        **plan.exchange_scratch(True, False),
        **plan.spectral_scratch(),
        **ffn_scratch(plan),
        **{key + str(k): sems(chans) for k in range(3, 10) for key in ("s", "r")},
    }
    in_place = ("up", "down", "lines_t")
    return launch(
        body,
        ins,
        outs,
        scratch,
        "first_forward",
        0,
        {key: IN_PLACE for key in in_place},
        {key: IN_PLACE for key in outs if key.endswith("_kept")},
    )


def launch_second(plan, args, one, tables):
    rows, features, chans = plan.rows, plan.features, plan.chans

    def body(r):
        me = lax.axis_index("chan")
        met = greet(plan)
        mark_even(plan, r)
        moves = Moves(r.dma)
        loaded = moves.start(r.lines_t, r.lines_in)
        weights = moves.start(r.w_kept, r.w)
        vectors = moves.start(r.gathered_kept, r.gathered)
        earlier = moves.start(r.cells_kept, r.cells_one)
        moves.open = []
        gain, shift = r.gain[...].reshape(1, -1), r.shift[...].reshape(1, -1)
        weight = r.codes[0].astype(F32) * (1.0 / 64.0)

        def normed(h):
            quarter, inside = h // plan.share, h % plan.share
            x = unpack_cells(r.home[quarter, inside].astype(F32)) + r.before[h]
            table = r.stats_home[quarter, inside]
            unit = (x - over_lanes(table, features, 0)) * over_lanes(table, features, 1)
            r.x[h] = x
            r.unit[h] = unit
            r.dev[pl.ds(h, 1), :] = jnp.sum(table[3:6].astype(F32), axis=0, keepdims=True)
            return unit * gain + shift

        rows_to_modes(plan, (r.row[0], r.row[1]), r.flat, normed, True)
        met()
        scales = (r.scale, r.scale_all, r.s20, r.r20)
        there = Exchange(True, plan.spaces, plan.thick, r.send1, r.recv1, r.s1, r.r1, scales)
        back = Exchange(False, plan.spaces, plan.thick, r.send2, r.recv2, r.s2, r.r2)
        send_modes(there, plan.pairs, plan.chunk, r.flat)
        loaded.wait()
        enter(r.lines_in, r.cells_t, r.turn)

        def low_target(h, peer, place):
            r.own[peer, place] = pack_cells(r.cells_t[h]).astype(BF)

        targets = []

        def send_target(step, peer):
            if step:
                copy = push("chan", chans, step, r.own.at[peer], r.target.at[me], r.s5, r.r5)
                copy.start()
                targets.append(copy)
            else:
                r.target[me] = r.own[me]

        rows_of_chunks(plan, low_target, send_target)
        filter_forward(plan, r, there, back)
        collect(back, plan.pairs, plan.chunk, r.flat)
        there.close(plan.pairs)
        back.close(plan.pairs)
        wait_all(targets)
        copies = rows_forward(plan, r, r.unit, r.x, r.before)
        weights.wait()
        vectors.wait()
        wait_all(copies)
        ffn_forward(plan, r)

        def errors(block):
            outer = r.total[block.cells, :]
            error = outer + block.get(r.mid) - block.get(r.target)
            r.upper[block.cells, :] = (weight * error).astype(BF)
            block.put(r.leaving, outer)

        by_blocks(plan, errors)
        copies = spread_chan(plan, r.leaving, r.landed, r.s6, r.r6)
        for copy in copies:
            copy.wait_send()
        ffn_backward(plan, r)
        for copy in copies:
            copy.wait_recv()
        copies = spread_chan(plan, r.leaving, r.own, r.s7, r.r7)

        def grads(u, carry):
            for slot in range(2):
                t = 2 * u + slot
                stores = [
                    pltpu.make_async_copy(r.grad.at[slot, k], r.grads_kept.at[k, t], r.dma2.at[slot, k])
                    for k in range(2)
                ]

                @pl.when(u > 0)
                def _():
                    wait_all(stores)

                for k, value in enumerate(weight_gradients(r, t)):
                    r.grad[slot, k] = value.astype(BF)
                    stores[k].start()
            return carry

        lax.fori_loop(0, plan.steps // 2, grads, 0)
        vector_gradients(plan, r, r.rest)
        wait_all(copies)

        def middle_grad(h):
            quarter, inside = h // plan.share, h % plan.share
            x = unpack_cells(r.landed[quarter, inside].astype(F32)) + r.before[h]
            r.before[h] = x
            grad = weight * (x - r.cells_t[h]) + unpack_cells(r.own[quarter, inside].astype(F32))
            r.out[h] = grad
            return grad

        rows_to_modes(plan, r.rowinv_t[...], r.flat, middle_grad, False)
        there = Exchange(False, plan.spaces, plan.thick, r.send3, r.recv3, r.s3_, r.r3_)
        back = Exchange(False, plan.spaces, plan.thick, r.send2, r.recv2, r.s2, r.r2)
        send_modes(there, plan.pairs, plan.chunk, r.flat)
        moves.start(r.before, r.second_x)
        leave(r.x, r.lines_in, r.turn)
        moves.start(r.lines_in, r.lines)
        filter_backward(plan, r, there, back)
        mix_gradients(plan, r, None)
        collect(back, plan.pairs, plan.chunk, r.flat)
        copies = rows_backward(plan, r, r.unit, None)
        earlier.wait()
        wait_all(copies)
        result = input_gradient(plan, r, r.unit, r.dev)
        copies = []

        def row(h, peer, place):
            grad = weight * (r.x[h] - r.cells_one[h]) + result(h)
            r.out[h] = grad
            r.own[peer, place] = pack_cells(grad).astype(BF)

        def send_chunk(step, peer):
            if step:
                copy = push("chan", chans, step, r.own.at[peer], r.came.at[me], r.s8, r.r8)
                copy.start()
                copies.append(copy)
            else:
                r.came[me] = r.own[me]

        rows_of_chunks(plan, row, send_chunk)
        for slot in range(2):
            for k in range(2):
                pltpu.make_async_copy(
                    r.grad.at[slot, k], r.grads_kept.at[k, plan.steps - 2 + slot], r.dma2.at[slot, k]
                ).wait()
        wait_all(copies)
        there.close(plan.pairs)
        back.close(plan.pairs)
        moves.close()

    ins = {
        "home": one["home"],
        "stats_home": one["stats_home"],
        "before": one["middle_kept"],
        "w_kept": one["w_kept"],
        "gathered_kept": one["gathered_kept"],
        "cells_kept": one["cells_kept"],
        "mix": one["mix_kept"],
        "bias": one["bias"],
        **args,
    }
    ins.update({key: tables[key] for key in ("row", "rowinv", "rowinv_t", "row_t", "col", "colinv")})
    outs = {
        "out": plan.field,
        "came": plan.by_cells,
        "lines": plan.lines,
        "second_x": plan.field,
        "sums": plan.sums,
        "rest": plan.rest,
        "grads_kept": plan.grads,
    }
    exchange = Exchange.shape(False, plan.spaces, plan.thick, plan.pairs)
    scratch = {
        "dma": sems(8),
        "dma2": sems(2, 2),
        "x": scratch_of(plan.field),
        "unit": scratch_of(plan.field),
        "dev": scratch_of(plan.dev),
        "cells_t": scratch_of(plan.field),
        "cells_one": scratch_of(plan.field),
        "lines_in": scratch_of(plan.lines),
        "spec": scratch_of(plan.kept),
        "first": scratch_of(plan.kept),
        "second": scratch_of(plan.kept),
        "w": scratch_of(plan.weights),
        "own": scratch_of(plan.by_cells),
        "mid": scratch_of(plan.by_cells),
        "target": scratch_of(plan.by_cells),
        "leaving": scratch_of(plan.by_cells),
        "landed": scratch_of(plan.by_cells),
        "upper": scratch_of(plan.wide),
        "small": pltpu.VMEM((8, plan.width), F32),
        "upb": pltpu.VMEM((16, plan.tile), F32),
        "grad": pltpu.VMEM((2, 2, plan.tile, plan.width), BF),
        "send3": exchange,
        "recv3": exchange,
        "s3_": sems(plan.pairs, plan.spaces),
        "r3_": sems(plan.pairs, plan.spaces),
        **plan.exchange_scratch(True, False),
        **plan.spectral_scratch(),
        **ffn_scratch(plan),
        **norm_sums_scratch(plan),
        **{key + str(k): sems(chans) for k in (3, 5, 6, 7, 8) for key in ("s", "r")},
    }
    in_specs = {key: IN_PLACE for key in ("w_kept", "gathered_kept", "cells_kept", "lines_t")}
    in_specs["codes"] = pl.BlockSpec(memory_space=pltpu.SMEM)
    return launch(
        body,
        ins,
        outs,
        scratch,
        "second_step",
        1,
        in_specs,
        {key: IN_PLACE for key in ("second_x", "grads_kept", "lines")},
    )


def launch_third(plan, args, one, two, tables):
    rows, features, chans, spaces = plan.rows, plan.features, plan.chans, plan.spaces
    local, width = plan.local, plan.width
    levels = spaces // 2
    piece = local // levels
    small = plan.small
    part = -(-(small + 32) // (16 * levels)) * 16

    def body(r):
        me = lax.axis_index("chan")
        place = lax.axis_index("space")
        core = lax.rem(place, 2)
        level = place // 2
        sibling = place + 1 - 2 * core
        others = [lax.rem(level + step, levels) for step in range(1, levels)]
        met = greet(plan)
        mark_even(plan, r)
        moves = Moves(r.dma)
        early = [
            moves.start(source, target)
            for source, target in (
                (r.gathered_kept, r.gathered),
                (r.unit_wide_kept, r.unit_wide),
                (r.dev_wide_kept, r.dev_wide),
            )
        ]
        chunks = []
        for j in range(chans):
            tiles = pl.ds(j * plan.per, plan.per)
            chunks.append(
                [
                    moves.start(r.w_kept.at[1, j], r.w.at[1, j]),
                    moves.start(r.slope_kept.at[tiles], r.slope.at[tiles]),
                    moves.start(r.w_kept.at[0, j], r.w.at[0, j]),
                ]
            )
        middle = [moves.start(r.active_kept, r.active), moves.start(r.entry_kept, r.entry)]
        moves.open = []

        def upper(block):
            r.upper[block.cells, :] = block.get(r.came).astype(BF)

        by_blocks(plan, upper)
        wait_all(early)
        wait_all(chunks[0])
        ffn_backward(plan, r, lambda chunk: wait_all(chunks[chunk]))
        late = [
            moves.start(source, target)
            for source, target in (
                (r.g, r.out),
                (r.unit_kept, r.unit),
                (r.spec_kept, r.spec),
                (r.first_kept, r.first),
                (r.second_kept, r.second),
                (r.dev_kept, r.dev),
            )
        ]
        moves.open = []
        met()
        copies = spread_chan(plan, r.leaving, r.own, r.s7, r.r7)
        vector_gradients(plan, r, r.rest)
        r.rest[...] += r.rest_before[...]
        vectors = [
            push("chan", chans, step, r.rest.at[lax.rem(me + step, chans)], r.rest_land.at[me], r.s6, r.r6)
            for step in range(1, chans)
        ]
        for copy in vectors:
            copy.start()
        r.rest_land[me] = r.rest[me]
        wait_all(middle)

        column, line = lax.rem(me, 2), me // 2
        beside = me + 1 - 2 * column
        across = me + 2 - 4 * line
        near, under = pl.ds(0, plan.tile // 2), pl.ds(plan.tile // 2, plan.tile // 2)

        def order(i):
            k = i // plan.per
            owner_column = column + (1 - k // 2) * (1 - 2 * column)
            owner_line = line + (1 - k % 2) * (1 - 2 * line)
            return (2 * owner_line + owner_column) * plan.per + i % plan.per

        def fetch(i, k):
            return pltpu.make_async_copy(r.grads_kept.at[k, order(i)], r.prev.at[i % 2, k], r.dma2.at[i % 2, k])

        def swap(i):
            return pltpu.make_async_remote_copy(
                src_ref=r.give.at[i % 2],
                dst_ref=r.take.at[i % 3],
                send_sem=r.s9.at[i],
                recv_sem=r.r9.at[i],
                device_id={"space": sibling},
                device_id_type=MESH_ID,
            )

        def to_chan(source, target, sem, number, device):
            return pltpu.make_async_remote_copy(
                src_ref=source,
                dst_ref=target,
                send_sem=sem[0].at[number],
                recv_sem=sem[1].at[number],
                device_id={"chan": device},
                device_id_type=MESH_ID,
            )

        def ship_near(i):
            target = r.land_near.at[i // plan.per, i % plan.per]
            return to_chan(r.keep.at[i, near], target, (r.s10, r.r10), i, beside)

        def ship_under(j):
            i = j + (j // plan.per) * plan.per
            target = r.land_under.at[j // plan.per, j % plan.per]
            return to_chan(r.keep.at[i, under], target, (r.s17, r.r17), j, across)

        def on_across(k):
            return to_chan(
                r.keep.at[2 * plan.per + k, near], r.land_on.at[0, k], (r.s18, r.r18), k, across
            )

        def on_beside(k):
            return to_chan(
                r.keep.at[plan.per + k, under], r.land_on.at[1, k], (r.s18, r.r18), plan.per + k, beside
            )

        def pass_on():
            def tile(k, carry):
                for arrived, land, start, part, onward in (
                    (ship_near, r.land_near, 2 * plan.per, near, on_across),
                    (ship_under, r.land_under, plan.per, under, on_beside),
                ):
                    arrived(k).wait_recv()
                    value = r.keep[start + k, part, :].astype(F32) + land[0, k].astype(F32)
                    r.keep[start + k, part, :] = value.astype(BF)
                    onward(k).start()
                return carry

            lax.fori_loop(0, plan.per, tile, 0)

        for k in range(2):
            fetch(0, k).start()

        def settle(i):
            swap(i).wait()
            r.keep[i] = (r.keep[i].astype(F32) + r.take[i % 3].astype(F32)).astype(BF)

        shipped = plan.steps - plan.per

        def leave_block(i):
            settle(i)

            @pl.when(i < 2 * plan.per)
            def _():
                ship_near(i).start()

            @pl.when(i < plan.per)
            def _():
                ship_under(i).start()

            @pl.when(i >= 2 * plan.per)
            def _():
                ship_under(i - plan.per).start()

        def make_block(i, before):
            for k in range(2):
                fetch(i, k).wait()

            @pl.when(i + 1 < plan.steps)
            def _():
                for k in range(2):
                    fetch(i + 1, k).start()

            values = [
                (value + r.prev[i % 2, k].astype(F32)).astype(BF)
                for k, value in enumerate(weight_gradients(r, order(i)))
            ]
            before(i)
            for kind in range(2):

                @pl.when(core == kind)
                def _():
                    r.keep[i] = values[kind]
                    r.give[i % 2] = values[1 - kind]

            swap(i).start()

        def others_block(i, carry):
            make_block(i, lambda i: pl.when(i > 0)(lambda: leave_block(i - 1)))
            return carry

        def own_block(i, carry):
            make_block(i, lambda i: pl.when(i > shipped)(lambda: settle(i - 1)))
            return carry

        lax.fori_loop(0, shipped, others_block, 0)
        leave_block(shipped - 1)
        wait_all(copies)
        wait_all(late)

        def middle_grad(h):
            quarter, inside = h // plan.share, h % plan.share
            grad = r.out[h] + unpack_cells(r.own[quarter, inside].astype(F32))
            r.out[h] = grad
            return grad

        rows_to_modes(plan, r.rowinv_t[...], r.flat, middle_grad, False)
        there = Exchange(False, spaces, plan.thick, r.send1, r.recv1, r.s1, r.r1)
        back = Exchange(False, spaces, plan.thick, r.send2, r.recv2, r.s2, r.r2)
        send_modes(there, plan.pairs, plan.chunk, r.flat)
        lax.fori_loop(shipped, plan.steps, own_block, 0)
        settle(plan.steps - 1)
        filter_backward(plan, r, there, back, pass_on)
        mix_gradients(plan, r, r.sums_before)

        def arrived(k, carry):
            ship_near(k).wait_send()
            ship_near(plan.per + k).wait()
            ship_under(k).wait_send()
            ship_under(plan.per + k).wait()
            on_across(k).wait()
            on_beside(k).wait()
            return carry

        lax.fori_loop(0, plan.per, arrived, 0)
        wait_all(vectors)
        def send(source, target, step, send_sem, recv_sem):
            return pltpu.make_async_remote_copy(
                src_ref=source,
                dst_ref=target,
                send_sem=send_sem.at[step],
                recv_sem=recv_sem.at[step],
                device_id={"space": 2 * others[step - 1] + core},
                device_id_type=MESH_ID,
            )

        def to_sibling(source, target, step, send_sem, recv_sem):
            return pltpu.make_async_remote_copy(
                src_ref=source,
                dst_ref=target,
                send_sem=send_sem.at[step],
                recv_sem=recv_sem.at[step],
                device_id={"space": sibling},
                device_id_type=MESH_ID,
            )

        def total(tile, carry):
            for half, land in enumerate((r.land_near, r.land_under)):
                for sub in range(2):
                    inside = pl.ds(64 * sub, 64)
                    value = r.keep[3 * plan.per + tile, pl.ds(128 * half + 64 * sub, 64), :].astype(F32)
                    value += land[1, tile, inside, :].astype(F32) + r.land_on[half, tile, inside, :].astype(F32)
                    number = 4 * tile + 2 * half + sub
                    target = pl.ds(pl.multiple_of((number % (piece // 64)) * 64, 64), 64)
                    r.a_send[number // (piece // 64), target, :] = value.astype(BF)
            return carry

        lax.fori_loop(0, plan.per, total, 0)
        wide = [
            send(r.a_send.at[others[step - 1]], r.a_land.at[level], step, r.s11, r.r11)
            for step in range(1, levels)
        ]
        for copy in wide:
            copy.start()
        collect(back, plan.pairs, plan.chunk, r.flat)
        copies = rows_backward(plan, r, r.unit, r.sums_before)
        r.table[...] = jnp.zeros_like(r.table)
        r.table[0:small, :] = r.sums[...]
        tail = sum(r.rest_land[j] for j in range(chans))
        for k in range(local // 128):
            lanes = slice(k * 128, (k + 1) * 128)
            r.table[small + k : small + k + 1, :] = tail[0:1, lanes]
        for k in range(3):
            line = jnp.concatenate([tail[1 + k : 2 + k, :features], jnp.zeros((1, 256 - features), F32)], axis=1)
            r.table[small + 8 + 2 * k : small + 9 + 2 * k, :] = line[:, :128]
            r.table[small + 9 + 2 * k : small + 10 + 2 * k, :] = line[:, 128:]
        for q in range(levels):
            r.b_send[q] = r.table[q * part : (q + 1) * part, :].astype(BF)
        thin = [
            send(r.b_send.at[others[step - 1]], r.b_land.at[level], step, r.s12, r.r12)
            for step in range(1, levels)
        ]
        for copy in thin:
            copy.start()
        wait_all(copies)
        result = input_gradient(plan, r, r.unit, r.dev)

        def finish(h, carry):
            r.out[h] = result(h)
            return carry

        lax.fori_loop(0, rows, finish, 0, unroll=3)
        moves.start(r.second_x, r.scaled).wait()
        moves.open = []
        leave(r.scaled, r.lines, r.turn)
        moves.start(r.lines, r.lines_x)
        a = r.a_send[level].astype(F32)
        b = r.b_send[level].astype(F32)
        for step in range(1, levels):
            wide[step - 1].wait()
            thin[step - 1].wait()
            source = lax.rem(level - step + levels, levels)
            a += r.a_land[source].astype(F32)
            b += r.b_land[source].astype(F32)
        r.a_own[...] = a.astype(BF)
        r.b_own[...] = b.astype(BF)
        last = [to_sibling(r.a_own, r.a_other.at[level], 0, r.s13, r.r13)]
        last += [to_sibling(r.b_own, r.b_other.at[level], 0, r.s14, r.r14)]
        again = []
        for step in range(1, levels):
            again.append(send(r.a_own, r.a_full.at[level], step, r.s15, r.r15))
            again.append(send(r.b_own, r.b_full.at[level], step, r.s16, r.r16))
        for copy in again + last:
            copy.start()
        r.a_full[level] = r.a_own[...]
        r.b_full[level] = r.b_own[...]
        moves.close()
        moves.open = []
        leave(r.out, r.lines, r.turn)
        moves.start(r.lines, r.lines_out)
        for step in range(1, levels):
            again[2 * step - 2].wait()
            again[2 * step - 1].wait()
            source = lax.rem(level - step + levels, levels)
            more = [to_sibling(r.a_full.at[source], r.a_other.at[source], step, r.s13, r.r13)]
            more += [to_sibling(r.b_full.at[source], r.b_other.at[source], step, r.s14, r.r14)]
            for copy in more:
                copy.start()
            last += more
        wait_all(last)
        moves.close()
        there.close(plan.pairs)
        back.close(plan.pairs)

    ins = {
        "g": two["out"],
        "came": two["came"],
        "second_x": two["second_x"],
        "sums_before": two["sums"],
        "rest_before": two["rest"],
        "grads_kept": two["grads_kept"],
        "mix": one["mix_kept"],
        **{
            key: one[key]
            for key in (
                "w_kept",
                "slope_kept",
                "active_kept",
                "entry_kept",
                "unit_wide_kept",
                "dev_wide_kept",
                "gathered_kept",
                "spec_kept",
                "first_kept",
                "second_kept",
                "unit_kept",
                "dev_kept",
            )
        },
        **args,
    }
    ins.update({key: tables[key] for key in ("rowinv_t", "row_t", "col", "colinv")})
    outs = {
        "lines_x": plan.lines,
        "lines_out": plan.lines,
        "a_full": ((levels, piece, width), BF),
        "a_other": ((levels, piece, width), BF),
        "b_full": ((levels, part, 128), BF),
        "b_other": ((levels, part, 128), BF),
    }
    blocks = pltpu.VMEM((plan.steps, plan.tile, width), BF)
    scratch = {
        "dma": sems(28),
        "dma2": sems(2, 2),
        "lines": scratch_of(plan.lines),
        "unit": scratch_of(plan.field),
        "dev": scratch_of(plan.dev),
        "out": scratch_of(plan.field),
        "spec": scratch_of(plan.kept),
        "first": scratch_of(plan.kept),
        "second": scratch_of(plan.kept),
        "w": scratch_of(plan.weights),
        "own": scratch_of(plan.by_cells),
        "leaving": scratch_of(plan.by_cells),
        "upper": scratch_of(plan.wide),
        "small": pltpu.VMEM((8, width), F32),
        "upb": pltpu.VMEM((16, plan.tile), F32),
        "sums": scratch_of(plan.sums),
        "rest": scratch_of(plan.rest),
        "rest_land": scratch_of(plan.rest),
        "prev": pltpu.VMEM((2, 2, plan.tile, width), BF),
        "keep": blocks,
        "give": pltpu.VMEM((2, plan.tile, width), BF),
        "take": pltpu.VMEM((3, plan.tile, width), BF),
        "land_near": pltpu.VMEM((2, plan.per, plan.tile // 2, width), BF),
        "land_under": pltpu.VMEM((2, plan.per, plan.tile // 2, width), BF),
        "land_on": pltpu.VMEM((2, plan.per, plan.tile // 2, width), BF),
        "table": pltpu.VMEM((part * levels, 128), F32),
        "a_send": pltpu.VMEM((levels, piece, width), BF),
        "a_land": pltpu.VMEM((levels, piece, width), BF),
        "a_own": pltpu.VMEM((piece, width), BF),
        "b_send": pltpu.VMEM((levels, part, 128), BF),
        "b_land": pltpu.VMEM((levels, part, 128), BF),
        "b_own": pltpu.VMEM((part, 128), BF),
        **plan.exchange_scratch(False, False),
        **plan.spectral_scratch(),
        **ffn_scratch(plan),
        **norm_sums_scratch(plan),
        **{key + str(k): sems(chans) for k in (6, 7) for key in ("s", "r")},
        **{key + str(k): sems(plan.steps) for k in (9, 10, 17, 18) for key in ("s", "r")},
        **{key + str(k): sems(levels) for k in range(11, 17) for key in ("s", "r")},
    }
    in_place = [key for key in ins if key.endswith("_kept") and key != "mix_kept"] + ["second_x", "g"]
    return launch(
        body,
        ins,
        outs,
        scratch,
        "first_backward",
        2,
        {key: IN_PLACE for key in in_place},
        {key: IN_PLACE for key in ("lines_x", "lines_out")},
    )


def unpack_gradients(plan, parts, fields):
    features, small = plan.features, plan.small
    levels, piece, width = parts["a_full"].shape
    part = parts["b_full"].shape[1]
    local = levels * piece
    size = features // 2

    def body(r):
        swap = lax.rem(lax.axis_index("space"), 2) == 1
        for q in range(levels):
            own = slice(q * piece, (q + 1) * piece)
            mine, theirs = r.a_full[q].astype(F32), r.a_other[q].astype(F32)
            r.down[own, :] = jnp.where(swap, theirs, mine)
            r.up[:, own] = jnp.where(swap, mine, theirs).T
            r.table[q * part : (q + 1) * part, :] = r.b_full[q].astype(F32) + r.b_other[q].astype(F32)
        for layer, target in enumerate((r.mix_in, r.mix_out)):
            for half in range(2):
                for block in range(2):
                    start = ((layer * 2 + half) * 2 + block) * size
                    target[half, block] = r.table[start : start + size, :size]
        base = 8 * size

        def vector(k):
            return jnp.concatenate(
                [r.table[base + k : base + k + 1, :], r.table[base + 8 + k : base + 9 + k, : features - 128]], axis=1
            )

        for k, target in enumerate((r.bias_in, r.bias_in, r.bias_out, r.bias_out)):
            value = vector(k)
            target[k % 2, 0:1, :] = value[:, :size]
            target[k % 2, 1:2, :] = value[:, size:]
        r.pre_gain[...] = vector(4)
        r.pre_shift[...] = vector(5)
        r.upb[...] = jnp.concatenate(
            [r.table[small + k : small + k + 1, :] for k in range(local // 128)], axis=1
        ).reshape(local)

        def line(h, carry):
            for key in fields:
                getattr(r, key)[h] = getattr(r, key + "_in")[h]
            return carry

        lax.fori_loop(0, plan.rows, line, 0)
        for k, target in enumerate((r.post_gain, r.post_shift, r.downb)):
            target[...] = jnp.concatenate(
                [
                    r.table[small + 8 + 2 * k : small + 9 + 2 * k, :],
                    r.table[small + 9 + 2 * k : small + 10 + 2 * k, : features - 128],
                ],
                axis=1,
            )


    return launch(
        body,
        {
            **{key: parts[key] for key in ("a_full", "a_other", "b_full", "b_other")},
            **{key + "_in": value for key, value in fields.items()},
        },
        {
            "down": ((local, width), F32),
            "up": ((width, local), F32),
            "mix_in": ((2, 2, size, size), F32),
            "mix_out": ((2, 2, size, size), F32),
            "bias_in": ((2, 2, size), F32),
            "bias_out": ((2, 2, size), F32),
            "pre_gain": ((1, features), F32),
            "pre_shift": ((1, features), F32),
            "post_gain": ((1, features), F32),
            "post_shift": ((1, features), F32),
            "downb": ((1, features), F32),
            "upb": ((local,), F32),
            **{key: plan.lines for key in fields},
        },
        {"table": pltpu.VMEM((part * levels, 128), F32)},
        "unpack_gradients",
    )


def shards_fast(
    current_atmosphere,
    truth_one,
    truth_two,
    storm_codes,
    pre_gain,
    pre_shift,
    mix_weight_in,
    mix_bias_in,
    mix_weight_out,
    mix_bias_out,
    post_gain,
    post_shift,
    up_weight,
    up_bias,
    down_weight,
    down_bias,
):
    rows, merged = current_atmosphere.shape[1:]
    columns = W
    features = merged // columns
    plan = Plan(
        rows, features, columns, lax.axis_size("space"), lax.axis_size("chan"), up_weight.shape[1]
    )
    forward, inverse = row_constants(columns)
    column = column_constants(rows * plan.spaces, rows, 2)
    tables = {
        "row": jnp.stack(const_halves(forward)),
        "rowinv": const_halves(inverse)[0],
        "rowinv_t": const_halves(inverse.T)[0],
        "row_t": const_halves(forward.T)[0],
        "col": jnp.stack(const_halves(column)),
        "colinv": const_halves(column.T)[0],
    }

    def lines(flat):
        return flat.reshape(rows, merged // 128, 128)

    def flat(line_field):
        return line_field.reshape(1, rows, merged)

    one = launch_first(
        plan,
        {
            "lines_x": lines(current_atmosphere),
            "lines_t": lines(truth_one),
            "gain": pre_gain,
            "shift": pre_shift,
            "mix_in": mix_weight_in,
            "bias_in": mix_bias_in,
            "mix_out": mix_weight_out,
            "bias_out": mix_bias_out,
            "post_gain": post_gain,
            "post_shift": post_shift,
            "up": up_weight,
            "upb": up_bias,
            "down": down_weight,
            "downb": down_bias,
        },
        tables,
    )
    two = launch_second(
        plan,
        {"gain": pre_gain, "shift": pre_shift, "lines_t": lines(truth_two), "codes": storm_codes},
        one,
        tables,
    )
    three = launch_third(plan, {"gain": pre_gain}, one, two, tables)
    grads = unpack_gradients(
        plan, three, {"first": two["lines"], "second": three["lines_x"], "state": three["lines_out"]}
    )
    return (
        flat(grads["first"]),
        flat(grads["second"]),
        flat(grads["state"]),
        grads["pre_gain"].reshape(features),
        grads["pre_shift"].reshape(features),
        grads["mix_in"],
        grads["bias_in"],
        grads["mix_out"],
        grads["bias_out"],
        grads["post_gain"].reshape(features),
        grads["post_shift"].reshape(features),
        grads["up"],
        grads["upb"],
        grads["down"],
        grads["downb"].reshape(features),
    )


def suits(mesh):
    spaces, chans = mesh.shape["space"], mesh.shape["chan"]
    return (spaces, chans) == (8, 4)


def solution(mesh):
    in_specs = (
        P(None, "space", "chan"),
        P(None, "space", "chan"),
        P(None, "space", "chan"),
        P(),
        P("chan"),
        P("chan"),
        P(None, "chan", None, None),
        P(None, "chan", None),
        P(None, "chan", None, None),
        P(None, "chan", None),
        P("chan"),
        P("chan"),
        P(None, "chan"),
        P("chan"),
        P("chan", None),
        P("chan"),
    )
    out_specs = (
        P(None, "space", "chan"),
        P(None, "space", "chan"),
        P(None, "space", "chan"),
        P("chan"),
        P("chan"),
        P(None, "chan", None, None),
        P(None, "chan", None),
        P(None, "chan", None, None),
        P(None, "chan", None),
        P("chan"),
        P("chan"),
        P(None, "chan"),
        P("chan"),
        P("chan", None),
        P("chan"),
    )
    return jax.shard_map(shards_fast if suits(mesh) else shards, mesh=mesh, in_specs=in_specs, out_specs=out_specs, check_vma=False)
```

```python
import functools
import math
import types

import jax
import jax.numpy as jnp
import ml_dtypes
import numpy as np
from jax import lax
from jax.experimental import pallas as pl
from jax.experimental.pallas import tpu as pltpu
from jax.sharding import PartitionSpec as P

W = 160
KW = 81


NORM_EPS = 1e-06
SHRINK_LEVEL = 0.01
FULL_PRECISION = lax.Precision.HIGHEST


def exact_gelu(values):
    return jax.nn.gelu(values, approximate=False)


def shrink(values):
    return values - jnp.clip(values, -SHRINK_LEVEL, SHRINK_LEVEL)


def block_mix(values, matrix):
    return jnp.einsum("bhkni,nio->bhkno", values, matrix, precision=FULL_PRECISION)


def row_tables(columns, kept_modes, padded_modes):
    places = jnp.arange(columns, dtype=jnp.int32)[:, None]
    orders = jnp.arange(padded_modes, dtype=jnp.int32)[None, :]
    angles = 2.0 * math.pi / columns * (places * orders % columns).astype(jnp.float32)
    factor = 1.0 / math.sqrt(columns)
    single = jnp.logical_or(orders == 0, 2 * orders == columns)
    doubled = jnp.where(single, 1.0, 2.0).astype(jnp.float32)
    used = jnp.where(orders < kept_modes, 1.0, 0.0).astype(jnp.float32)
    return (
        jnp.cos(angles) * factor * used,
        -jnp.sin(angles) * factor * used,
        jnp.transpose(jnp.cos(angles) * doubled * factor * used),
        jnp.transpose(jnp.sin(angles) * doubled * factor * used),
    )


def along_rows(values, tables):
    return jnp.stack(
        [
            jnp.einsum("bhwc,wk->bhkc", values, tables[0], precision=FULL_PRECISION),
            jnp.einsum("bhwc,wk->bhkc", values, tables[1], precision=FULL_PRECISION),
        ]
    )


def along_rows_back(paired, tables):
    return jnp.einsum("bhkc,wk->bhwc", paired[0], tables[0], precision=FULL_PRECISION) + jnp.einsum(
        "bhkc,wk->bhwc", paired[1], tables[1], precision=FULL_PRECISION
    )


def rows_inverse(paired, tables):
    return jnp.einsum("bhkc,kw->bhwc", paired[0], tables[2], precision=FULL_PRECISION) - jnp.einsum(
        "bhkc,kw->bhwc", paired[1], tables[3], precision=FULL_PRECISION
    )


def rows_inverse_back(values, tables):
    return jnp.stack(
        [
            jnp.einsum("bhwc,kw->bhkc", values, tables[2], precision=FULL_PRECISION),
            -jnp.einsum("bhwc,kw->bhkc", values, tables[3], precision=FULL_PRECISION),
        ]
    )


def column_tables(height):
    orders = jnp.arange(height, dtype=jnp.int32)[:, None]
    places = jnp.arange(height, dtype=jnp.int32)[None, :]
    angles = 2.0 * math.pi / height * (orders * places % height).astype(jnp.float32)
    factor = 1.0 / math.sqrt(height)
    return (jnp.cos(angles) * factor, jnp.sin(angles) * factor)


def to_freq(matrix, values):
    return jnp.einsum("kh,bhmc->bkmc", matrix, values, precision=FULL_PRECISION)


def from_freq(matrix, values):
    return jnp.einsum("kh,bkmc->bhmc", matrix, values, precision=FULL_PRECISION)


def spectral_core(paired, w_first, b_first, w_second, b_second):
    samples, height, kept_modes, channels = paired.shape[1:]
    blocks, block_size = (w_first.shape[1], w_first.shape[2])
    cosine, sine_table = column_tables(height)
    real_in, imag_in = (paired[0], paired[1])
    split_form = (samples, height, kept_modes, blocks, block_size)
    real_part = (to_freq(cosine, real_in) + to_freq(sine_table, imag_in)).reshape(split_form)
    imag_part = (to_freq(cosine, imag_in) - to_freq(sine_table, real_in)).reshape(split_form)
    first_real = jax.nn.relu(
        block_mix(real_part, w_first[0]) - block_mix(imag_part, w_first[1]) + b_first[0]
    )
    first_imag = jax.nn.relu(
        block_mix(imag_part, w_first[0]) + block_mix(real_part, w_first[1]) + b_first[1]
    )
    joined_form = (samples, height, kept_modes, channels)
    second_real = shrink(
        block_mix(first_real, w_second[0]) - block_mix(first_imag, w_second[1]) + b_second[0]
    ).reshape(joined_form)
    second_imag = shrink(
        block_mix(first_imag, w_second[0]) + block_mix(first_real, w_second[1]) + b_second[1]
    ).reshape(joined_form)
    out_real = from_freq(cosine, second_real) - from_freq(sine_table, second_imag)
    out_imag = from_freq(cosine, second_imag) + from_freq(sine_table, second_real)
    return jnp.stack([out_real, out_imag])


def column_layout(paired):
    return lax.all_to_all(paired, "space", split_axis=3, concat_axis=2, tiled=True)


def row_layout(paired):
    return lax.all_to_all(
        paired.astype(jnp.bfloat16), "space", split_axis=2, concat_axis=3, tiled=True
    ).astype(paired.dtype)


def norm_forward(values, gain, offset):
    width_all = values.shape[-1] * lax.axis_size("chan")
    totals = lax.psum((jnp.sum(values, axis=-1), jnp.sum(values * values, axis=-1)), "chan")
    average = totals[0] / width_all
    variance = totals[1] / width_all - average * average
    inverse_dev = lax.rsqrt(variance + NORM_EPS)[..., None]
    scaled = (values - average[..., None]) * inverse_dev
    return (scaled * gain + offset, (scaled, inverse_dev))


def norm_backward(gradient, gain, saved):
    scaled, inverse_dev = saved
    width_all = scaled.shape[-1] * lax.axis_size("chan")
    scaled_grad = gradient * gain
    totals = lax.psum(
        (jnp.sum(scaled_grad, axis=-1), jnp.sum(scaled_grad * scaled, axis=-1)), "chan"
    )
    values_grad = inverse_dev * (
        scaled_grad - totals[0][..., None] / width_all - scaled * (totals[1][..., None] / width_all)
    )
    return (
        values_grad,
        jnp.sum(gradient * scaled, axis=(0, 1, 2)),
        jnp.sum(gradient, axis=(0, 1, 2)),
    )


def shards(
    current_atmosphere,
    truth_one,
    truth_two,
    storm_codes,
    pre_gain,
    pre_shift,
    mix_weight_in,
    mix_bias_in,
    mix_weight_out,
    mix_bias_out,
    post_gain,
    post_shift,
    up_weight,
    up_bias,
    down_weight,
    down_bias,
):
    samples, rows_here, merged = current_atmosphere.shape
    columns = W
    channels = merged // columns
    total_rows = samples * rows_here * columns
    space_count = lax.axis_size("space")
    padded_modes = (KW + space_count - 1) // space_count * space_count
    tables = row_tables(columns, KW, padded_modes)

    def to_cells(flat_field):
        return jnp.transpose(
            flat_field.reshape(samples, rows_here, channels, columns), (0, 1, 3, 2)
        )

    def to_flat(cell_field):
        return jnp.transpose(cell_field, (0, 1, 3, 2)).reshape(samples, rows_here, merged)

    start_cells = to_cells(current_atmosphere)
    target_one = to_cells(truth_one)
    target_two = to_cells(truth_two)
    weight_of = (storm_codes.astype(jnp.float32) / 64.0).reshape(-1, 1, 1, 1)
    full_up, full_down, full_up_bias, full_down_bias = (up_weight, down_weight, up_bias, down_bias)

    def mlp_forward(inputs):
        gathered = lax.all_gather(inputs, "chan", axis=1, tiled=True)
        hidden = jnp.dot(
            gathered, full_up, preferred_element_type=jnp.float32
        ) + full_up_bias.astype(jnp.float32)
        active_full, gelu_pull = jax.vjp(exact_gelu, hidden)
        active = active_full.astype(jnp.bfloat16)
        product = jnp.dot(active, full_down, preferred_element_type=jnp.float32)
        output = lax.psum_scatter(
            product.astype(jnp.bfloat16), "chan", scatter_dimension=1, tiled=True
        ).astype(jnp.float32) + full_down_bias.astype(jnp.float32)
        return (output, (gathered, gelu_pull, active))

    def mlp_backward(gradient, saved):
        gathered, gelu_pull, active = saved
        grad_low = gradient.astype(jnp.bfloat16)
        grad_rows = lax.all_gather(grad_low, "chan", axis=1, tiled=True)
        down_bias_grad = jnp.sum(grad_low.astype(jnp.float32), axis=0)
        down_grad = jnp.dot(active.T, grad_rows, preferred_element_type=jnp.float32)
        active_grad = jnp.dot(grad_rows, full_down.T, preferred_element_type=jnp.float32)
        hidden_grad = gelu_pull(active_grad)[0].astype(jnp.bfloat16)
        up_grad = jnp.dot(gathered.T, hidden_grad, preferred_element_type=jnp.float32)
        up_bias_grad = jnp.sum(hidden_grad.astype(jnp.float32), axis=0)
        input_part = jnp.dot(hidden_grad, full_up.T, preferred_element_type=jnp.float32)
        input_grad = lax.psum_scatter(
            input_part.astype(jnp.bfloat16), "chan", scatter_dimension=1, tiled=True
        ).astype(jnp.float32)
        return (input_grad, (up_grad, up_bias_grad, down_grad, down_bias_grad))

    def forward_block(values):
        normed, first_saved = norm_forward(values, pre_gain, pre_shift)
        modal_in = column_layout(along_rows(normed, tables))
        filtered, core_pull = jax.vjp(
            spectral_core, modal_in, mix_weight_in, mix_bias_in, mix_weight_out, mix_bias_out
        )
        middle = rows_inverse(row_layout(filtered), tables) + normed + values
        entry, second_residuals = norm_forward(middle, post_gain, post_shift)
        output, mlp_saved = mlp_forward(entry.astype(jnp.bfloat16).reshape(total_rows, channels))
        return (
            output.reshape(values.shape) + middle,
            (first_saved, core_pull, second_residuals, mlp_saved),
        )

    def backward_block(gradient, saved):
        first_saved, core_pull, second_residuals, mlp_saved = saved
        mlp_grad, dense_grads = mlp_backward(gradient.reshape(total_rows, channels), mlp_saved)
        middle_part, post_gain_grad, post_shift_grad = norm_backward(
            mlp_grad.reshape(gradient.shape), post_gain, second_residuals
        )
        middle_grad = middle_part + gradient
        filter_grads = core_pull(column_layout(rows_inverse_back(middle_grad, tables)))
        normed_grad = along_rows_back(row_layout(filter_grads[0]), tables) + middle_grad
        input_part, pre_gain_grad, pre_shift_grad = norm_backward(
            normed_grad, pre_gain, first_saved
        )
        return (
            input_part + middle_grad,
            (pre_gain_grad, pre_shift_grad)
            + tuple(filter_grads[1:])
            + (post_gain_grad, post_shift_grad)
            + dense_grads,
        )

    first_out, first_saved_all = forward_block(start_cells)
    second_out, second_saved_all = forward_block(first_out)
    carried, grads_late = backward_block(weight_of * (second_out - target_two), second_saved_all)
    input_grad, grads_early = backward_block(
        weight_of * (first_out - target_one) + carried, first_saved_all
    )
    summed = jax.tree.map(jnp.add, grads_early, grads_late)
    (
        sum_pre_gain,
        sum_pre_shift,
        sum_mix_w_in,
        summed_mixing_bias_input,
        sum_mix_w_out,
        sum_mix_b_out,
        sum_post_gain,
        sum_post_shift,
        sum_up,
        sum_up_bias,
        sum_down,
        sum_down_bias,
    ) = summed
    totals = (
        lax.psum(sum_pre_gain.astype(jnp.bfloat16), "space").astype(jnp.float32),
        lax.psum(sum_pre_shift.astype(jnp.bfloat16), "space").astype(jnp.float32),
        lax.psum(sum_mix_w_in.astype(jnp.bfloat16), "space").astype(jnp.float32),
        lax.psum(summed_mixing_bias_input.astype(jnp.bfloat16), "space").astype(jnp.float32),
        lax.psum(sum_mix_w_out.astype(jnp.bfloat16), "space").astype(jnp.float32),
        lax.psum(sum_mix_b_out.astype(jnp.bfloat16), "space").astype(jnp.float32),
        lax.psum(sum_post_gain.astype(jnp.bfloat16), "space").astype(jnp.float32),
        lax.psum(sum_post_shift.astype(jnp.bfloat16), "space").astype(jnp.float32),
        lax.psum(sum_up.astype(jnp.bfloat16), "space").astype(jnp.float32),
        lax.psum(sum_up_bias.astype(jnp.bfloat16), "space").astype(jnp.float32),
        lax.psum(sum_down.astype(jnp.bfloat16), "space").astype(jnp.float32),
        lax.psum(sum_down_bias.astype(jnp.bfloat16), "space").astype(jnp.float32),
    )
    return (to_flat(first_out), to_flat(second_out), to_flat(input_grad)) + tuple(totals)


BF = jnp.bfloat16
F32 = jnp.float32
MESH_ID = pl.DeviceIdType.MESH
VMEM_BYTES = 66 * 1024 * 1024 - 1024 * 1024


def mm(a, b):
    return jnp.dot(a, b, preferred_element_type=F32)


def mm_nt(a, b):
    return lax.dot_general(a, b, (((1,), (1,)), ((), ())), preferred_element_type=F32)


def mm_tn(a, b):
    return lax.dot_general(a, b, (((0,), (0,)), ((), ())), preferred_element_type=F32)


def halves(v):
    high = v.astype(BF)
    return high, (v - high.astype(F32)).astype(BF)


def mm3(a, b):
    return mm(a[0], b[0]) + (mm(a[0], b[1]) + mm(a[1], b[0]))


def const_halves(table):
    table = np.asarray(table, np.float32)
    high = table.astype(ml_dtypes.bfloat16)
    low = (table - high.astype(np.float32)).astype(ml_dtypes.bfloat16)
    return jnp.asarray(high), jnp.asarray(low)


def row_constants(columns):
    half = columns // 2
    place = np.arange(columns)
    mode = np.arange(half)
    angle = 2.0 * np.pi * np.outer(mode, place) / columns
    real = np.cos(angle)
    imag = -np.sin(angle)
    imag[0] = np.cos(np.pi * place)
    forward = np.concatenate([real, imag]) / np.sqrt(columns)
    weight = np.where(mode == 0, 1.0, 2.0)
    inverse = (forward * np.concatenate([weight, weight])[:, None]).T
    return forward, inverse


def column_constants(height, rows, group):
    owners = height // rows
    angle = 2.0 * np.pi * np.outer(np.arange(height), np.arange(height)) / height
    cosine = np.cos(angle) / np.sqrt(height)
    sine = np.sin(angle) / np.sqrt(height)

    def spread(matrix):
        wide = np.zeros((group, height, owners, group, rows))
        for column in range(group):
            wide[column, :, :, column, :] = matrix.reshape(height, owners, rows)
        return wide.reshape(group * height, owners * group * rows)

    cosine, sine = spread(cosine), spread(sine)
    return np.block([[cosine, sine], [-sine, cosine]])


def partner(me, count, step):
    flip = (count - step) % count
    result, bit = 0, 1
    while bit < count:
        digit = lax.rem(me // bit, 2)
        result += bit * (1 - digit if flip // bit % 2 else digit)
        bit *= 2
    return result


def signal_peers(axis, count, barrier):
    me = lax.axis_index(axis)
    for step in range(1, count):
        pl.semaphore_signal(
            barrier, inc=1, device_id={axis: lax.rem(me + step, count)}, device_id_type=MESH_ID
        )


def push(axis, count, step, source, target, send_sem, recv_sem):
    peer = lax.rem(lax.axis_index(axis) + step, count)
    return pltpu.make_async_remote_copy(
        src_ref=source,
        dst_ref=target,
        send_sem=send_sem.at[step],
        recv_sem=recv_sem.at[step],
        device_id={axis: peer},
        device_id_type=MESH_ID,
    )


def params(collective_id=None):
    return pltpu.CompilerParams(
        collective_id=collective_id,
        has_side_effects=collective_id is not None,
        vmem_limit_bytes=VMEM_BYTES,
    )


def launch(body, ins, outs, scratch, name, collective_id=None, in_specs=None, out_specs=None, grid=()):
    in_specs, out_specs = in_specs or {}, out_specs or {}
    names = list(ins) + list(outs) + list(scratch)
    whole = pl.BlockSpec(memory_space=pltpu.VMEM)
    results = pl.pallas_call(
        lambda *refs: body(types.SimpleNamespace(**dict(zip(names, refs)))),
        grid=grid,
        in_specs=[in_specs.get(key, whole) for key in ins],
        out_specs=[out_specs.get(key, whole) for key in outs],
        out_shape=[jax.ShapeDtypeStruct(*outs[key]) for key in outs],
        scratch_shapes=list(scratch.values()),
        compiler_params=params(collective_id),
        name=name,
    )(*ins.values())
    return dict(zip(outs, results))


IN_PLACE = pl.BlockSpec(memory_space=pl.ANY)


def sems(*counts):
    return pltpu.SemaphoreType.DMA(counts)


def run_copies(copies):
    for copy in copies:
        copy.start()
    for copy in copies:
        copy.wait()


def cells_from_lines(lines_ref, h, scratch_ref):
    features = scratch_ref.shape[1]
    per = 640 // W
    groups = features // per
    wide = jnp.concatenate(
        [lines_ref[h, pl.ds(part, groups, stride=5), :] for part in range(5)], axis=1
    )
    for part in range(per):
        piece = wide[:, part * W : (part + 1) * W]
        scratch_ref[0, pl.ds(part, groups, stride=per), :] = piece[:, :128]
        scratch_ref[1, pl.ds(part, groups, stride=per), :] = jnp.concatenate(
            [piece[:, 128:], jnp.zeros((groups, 256 - W), F32)], axis=1
        )
    return jnp.concatenate([scratch_ref[0], scratch_ref[1][:, : W - 128]], axis=1)


def enter(lines_ref, cells_ref, scratch_ref):
    def row(h, carry):
        cells_ref[h] = cells_from_lines(lines_ref, h, scratch_ref).T
        return carry

    lax.fori_loop(0, lines_ref.shape[0], row, 0)


def leave(cells_ref, lines_ref, scratch_ref):
    features = scratch_ref.shape[1]
    per = 640 // W
    groups = features // per

    def row(h, carry):
        block = cells_ref[h].T
        scratch_ref[0] = block[:, :128]
        scratch_ref[1] = jnp.concatenate([block[:, 128:], jnp.zeros((features, 256 - W), F32)], axis=1)
        wide = jnp.concatenate(
            [
                piece
                for part in range(per)
                for piece in (
                    scratch_ref[0, pl.ds(part, groups, stride=per), :],
                    scratch_ref[1, pl.ds(part, groups, stride=per), :][:, : W - 128],
                )
            ],
            axis=1,
        )
        for part in range(5):
            lines_ref[h, pl.ds(part, groups, stride=5), :] = wide[:, part * 128 : (part + 1) * 128]
        return carry

    lax.fori_loop(0, lines_ref.shape[0], row, 0)


def pack_lanes(flat_ref, place, real, imag):
    flat_ref[0, place, :] = real[:, :128]
    flat_ref[1, place, :] = imag[:, :128]
    flat_ref[2, place, :] = jnp.concatenate([real[:, 128:], imag[:, 128:]], axis=1)


def join_lanes(first, second, rest):
    real = jnp.concatenate([first, rest[:, :64]], axis=1)
    imag = jnp.concatenate([second, rest[:, 64:]], axis=1)
    return real, imag


def unpack_lanes(flat_ref, place):
    return join_lanes(flat_ref[0, place, :], flat_ref[1, place, :], flat_ref[2, place, :])


LEVEL = 32000.0


class Exchange:
    def __init__(self, fixed, spaces, thick, send_ref, recv_ref, send_sem, recv_sem, scales=None):
        self.fixed, self.scales = fixed, scales
        self.spaces, self.thick = spaces, thick
        self.send_ref, self.recv_ref = send_ref, recv_ref
        self.send_sem, self.recv_sem = send_sem, recv_sem
        self.me = lax.axis_index("space")

    @staticmethod
    def shape(fixed, spaces, thick, pairs):
        return pltpu.VMEM((pairs, spaces, 3 * thick, 128), jnp.int16 if fixed else BF)

    def copy(self, p, step):
        peer = partner(self.me, self.spaces, step)
        return pltpu.make_async_remote_copy(
            src_ref=self.send_ref.at[p, peer],
            dst_ref=self.recv_ref.at[p, self.me],
            send_sem=self.send_sem.at[p, step],
            recv_sem=self.recv_sem.at[p, step],
            device_id={"space": peer},
            device_id_type=MESH_ID,
        )

    def scale_copy(self, step):
        own_ref, all_ref, send_sem, recv_sem = self.scales
        return push("space", self.spaces, step, own_ref, all_ref.at[self.me], send_sem, recv_sem)

    def send_scales(self, flat_ref):
        own_ref, all_ref = self.scales[:2]
        largest = jnp.max(jnp.abs(flat_ref[...]), axis=1)
        own_ref[0:3, :] = jnp.maximum(largest, 1e-30) * (1.0 / LEVEL)
        own_ref[3:8, :] = jnp.ones((5, 128), F32)
        for step in range(1, self.spaces):
            self.scale_copy(step).start()
        all_ref[self.me] = own_ref[...]
        self.factor = 1.0 / own_ref[...]

    def encode(self, values):
        if not self.fixed:
            return jnp.concatenate([values[k] for k in range(3)], axis=0).astype(BF)
        lines = [jnp.round(values[k] * self.factor[k : k + 1]) for k in range(3)]
        return jnp.concatenate(lines, axis=0).astype(jnp.int32).astype(jnp.int16)

    def send(self, p, flat_ref, start_of):
        for step in list(range(1, self.spaces)) + [0]:
            peer = partner(self.me, self.spaces, step)
            rows = pl.ds(pl.multiple_of(start_of(peer), 8), self.thick)
            coded = self.encode(flat_ref[:, rows, :])
            if step:
                self.send_ref[p, peer] = coded
                self.copy(p, step).start()
            else:
                self.recv_ref[p, peer] = coded

    def arrive(self, p):
        for step in range(1, self.spaces):
            self.copy(p, step).wait_recv()

    def arrive_scales(self):
        for step in range(1, self.spaces):
            self.scale_copy(step).wait_recv()

    def take(self, p, source):
        coded = self.recv_ref[p, source]
        values = (coded.astype(jnp.int32) if self.fixed else coded).astype(F32)
        parts = [values[k * self.thick : (k + 1) * self.thick] for k in range(3)]
        if self.fixed:
            scale = self.scales[1][source]
            parts = [part * scale[k : k + 1] for k, part in enumerate(parts)]
        return parts

    def close(self, pairs):
        def pair(p, carry):
            for step in range(1, self.spaces):
                self.copy(p, step).wait_send()
            return carry

        lax.fori_loop(0, pairs, pair, 0)
        if self.fixed:
            for step in range(1, self.spaces):
                self.scale_copy(step).wait_send()


def pair_inputs(q, exchange, even_ref):
    p = jnp.maximum(q - 1, 0)

    @pl.when(q != 1)
    def _():
        exchange.arrive(p)

    if exchange.fixed:

        @pl.when(q == 0)
        def _():
            exchange.arrive_scales()

    extra = (q == 0).astype(F32)
    zeroth = jnp.logical_and(exchange.me == 0, p == 0).astype(F32)
    parts = [join_lanes(*exchange.take(p, s)) for s in range(exchange.spaces)]
    real = jnp.concatenate([part[0] for part in parts], axis=0)
    imag = jnp.concatenate([part[1] for part in parts], axis=0)
    chosen = imag * (even_ref[...] * zeroth)
    real = real * (1.0 - extra) + chosen * extra
    imag = (imag - chosen) * (1.0 - extra)
    return p, zeroth, jnp.concatenate([real, imag], axis=0)


def pair_outputs(q, p, zeroth, result, exchange, even_ref, kept_ref, stage_ref):
    half = result.shape[0] // 2
    real, imag = result[:half], result[half:]

    @pl.when(q == 0)
    def _():
        kept_ref[...] = real

    @pl.when(q > 0)
    def _():
        chosen = even_ref[...] * zeroth
        pack_lanes(stage_ref, slice(None), real, imag * (1.0 - chosen) + kept_ref[...] * chosen)
        exchange.send(p, stage_ref, lambda peer: peer * exchange.thick)


def collect(exchange, pairs, chunk, flat_ref):
    def pair(p, carry):
        exchange.arrive(p)
        for s in range(exchange.spaces):
            rows = pl.ds(pl.multiple_of(s * chunk + p * exchange.thick, 8), exchange.thick)
            for k, part in enumerate(exchange.take(p, s)):
                flat_ref[k, rows, :] = part
        return carry

    lax.fori_loop(0, pairs, pair, 0)


def send_modes(exchange, pairs, chunk, flat_ref):
    if exchange.fixed:
        exchange.send_scales(flat_ref)

    def pair(p, carry):
        exchange.send(p, flat_ref, lambda peer: peer * chunk + p * exchange.thick)
        return carry

    lax.fori_loop(0, pairs, pair, 0)


class Plan:
    def __init__(self, rows, features, columns, spaces, chans, local):
        self.rows, self.features, self.columns = rows, features, columns
        self.spaces, self.chans, self.local = spaces, chans, local
        self.modes = columns // 2
        self.total = self.modes * rows
        self.chunk = self.total // spaces
        self.thick = 2 * rows
        self.half = self.thick * spaces
        self.pairs = self.chunk // self.thick
        self.cells = rows * columns // chans
        self.share = rows // chans
        self.width = features * chans
        self.tile = 256
        self.per = local // self.tile
        self.steps = chans * self.per
        self.size = features // 2
        self.small = 8 * self.size + 16
        self.field = ((rows, columns, features), F32)
        self.by_cells = ((chans, self.share, columns // 2 * 3, 128), BF)
        self.wide = ((self.cells, self.width), BF)
        self.tiles = ((self.steps, self.cells, self.tile), BF)
        self.lines = ((rows, features * columns // 128, 128), F32)
        self.dev = ((-(-rows // 8) * 8, columns), F32)
        self.dev_wide = ((self.cells, 128), F32)
        self.kept = ((self.pairs + 1, 2 * self.half, features), BF)
        self.mix = ((2, 2, 2, features, features), BF)
        self.weights = ((2, chans, local, self.width), BF)
        self.rest = ((chans, 8, local), F32)
        self.sums = ((self.small, 128), F32)
        self.grads = ((2, self.steps, self.tile, self.width), BF)
        self.vectors = ((chans, 8, local), F32)

    def exchange_scratch(self, fixed_there, fixed_back):
        made = {}
        for name, fixed in (("1", fixed_there), ("2", fixed_back)):
            shape = Exchange.shape(fixed, self.spaces, self.thick, self.pairs)
            made["send" + name] = made["recv" + name] = shape
            made["s" + name] = made["r" + name] = sems(self.pairs, self.spaces)
        if fixed_there:
            made["scale"] = pltpu.VMEM((8, 128), F32)
            made["scale_all"] = pltpu.VMEM((self.spaces, 8, 128), F32)
            made["s20"] = made["r20"] = sems(self.spaces)
        return made

    def spectral_scratch(self):
        return {
            "flat": pltpu.VMEM((3, self.total, 128), F32),
            "stage": pltpu.VMEM((3, self.half, 128), F32),
            "last": pltpu.VMEM((self.half, self.features), F32),
            "turn": pltpu.VMEM((2, self.features, 128), F32),
            "even": pltpu.VMEM((self.half, self.features), F32),
        }


def pack_cells(value):
    side = value.shape[0] // 2
    rest = value[:, 128:]
    return jnp.concatenate([value[:, :128], jnp.concatenate([rest[:side], rest[side:]], axis=1)], axis=0)


def unpack_cells(packed):
    columns = packed.shape[0] // 3 * 2
    rest = packed[columns:]
    rest = jnp.concatenate([rest[:, :64], rest[:, 64:]], axis=0)
    return jnp.concatenate([packed[:columns], rest], axis=1)


def three_parts(v):
    a = v.astype(BF)
    rest = v - a.astype(F32)
    b = rest.astype(BF)
    return [a, b, (rest - b.astype(F32)).astype(BF)]


def stack_rows(rows):
    lines = [part.astype(F32) for row in rows for part in three_parts(row)]
    lines.append(jnp.zeros((16 - len(lines), rows[0].shape[1]), F32))
    return jnp.concatenate(lines, axis=0).astype(BF)


def over_lanes(table, features, number):
    line = lax.broadcasted_iota(jnp.int32, (16, features), 0)
    chosen = jnp.logical_and(line >= 3 * number, line < 3 * number + 3)
    return mm_tn(table, jnp.where(chosen, 1.0, 0.0).astype(BF))


def lane_sums(value):
    return mm_nt(jnp.ones((16, value.shape[1]), BF), value.astype(BF))[0:1]


def scratch_of(shaped):
    return pltpu.VMEM(*shaped)


def mark_even(plan, r):
    row = lax.broadcasted_iota(jnp.int32, (plan.half, plan.features), 0)
    r.even[...] = jnp.where(lax.rem(lax.div(row, plan.rows), 2) == 0, 1.0, 0.0)


def greet(plan):
    barrier = pltpu.get_barrier_semaphore()
    signal_peers("space", plan.spaces, barrier)
    signal_peers("chan", plan.chans, barrier)
    return lambda: pl.semaphore_wait(barrier, plan.spaces + plan.chans - 2)


def spread_chan(plan, source_ref, target_ref, send_sem, recv_sem):
    me = lax.axis_index("chan")
    copies = []
    for step in range(1, plan.chans):
        peer = lax.rem(me + step, plan.chans)
        copy = push("chan", plan.chans, step, source_ref.at[peer], target_ref.at[me], send_sem, recv_sem)
        copy.start()
        copies.append(copy)
    target_ref[me] = source_ref[me]
    return copies


def wait_all(copies):
    for copy in copies:
        copy.wait()


def rows_to_modes(plan, table, flat_ref, value_of, exact):
    def row(h, carry):
        value = value_of(h)
        out = mm3(table, halves(value)) if exact else mm(table, value.astype(BF))
        pack_lanes(flat_ref, pl.ds(h, plan.modes, stride=plan.rows), out[: plan.modes], out[plan.modes :])
        return carry

    lax.fori_loop(0, plan.rows, row, 0, unroll=4)


def filter_forward(plan, r, there, back, aside=None):
    half = plan.half

    def filter_pair(q, carry):
        if aside is not None:
            pl.when(q == plan.pairs)(aside)
        p, zeroth, block = pair_inputs(q, there, r.even)
        spec = mm3((r.col[0], r.col[1]), halves(block))
        r.spec[q] = spec.astype(BF)
        parts = halves(spec)
        straight = mm3(parts, (r.mix[0, 0, 0], r.mix[0, 0, 1]))
        crossed = mm3(parts, (r.mix[0, 1, 0], r.mix[0, 1, 1]))
        first = jnp.concatenate(
            [
                jnp.maximum(straight[:half] - crossed[half:] + r.bias[0:1], 0.0),
                jnp.maximum(straight[half:] + crossed[:half] + r.bias[1:2], 0.0),
            ],
            axis=0,
        )
        r.first[q] = first.astype(BF)
        parts = halves(first)
        straight = mm3(parts, (r.mix[1, 0, 0], r.mix[1, 0, 1]))
        crossed = mm3(parts, (r.mix[1, 1, 0], r.mix[1, 1, 1]))
        second = jnp.concatenate(
            [
                straight[:half] - crossed[half:] + r.bias[2:3],
                straight[half:] + crossed[:half] + r.bias[3:4],
            ],
            axis=0,
        )
        second = second - jnp.clip(second, -SHRINK_LEVEL, SHRINK_LEVEL)
        r.second[q] = second.astype(BF)
        result = mm(r.colinv[...], r.second[q])
        pair_outputs(q, p, zeroth, result, back, r.even, r.last, r.stage)
        return carry

    lax.fori_loop(0, plan.pairs + 1, filter_pair, 0)


def modes_to_rows(plan, flat_ref, h):
    real, imag = unpack_lanes(flat_ref, pl.ds(h, plan.modes, stride=plan.rows))
    return jnp.concatenate([real, imag], axis=0)


def rows_of_chunks(plan, row, send_chunk):
    me = lax.axis_index("chan")
    for step in list(range(1, plan.chans)) + [0]:
        peer = lax.rem(me + step, plan.chans)

        def one(i, carry):
            row(peer * plan.share + i, peer, i)
            return carry

        lax.fori_loop(0, plan.share, one, 0, unroll=True)
        send_chunk(step, peer)


def rows_forward(plan, r, unit_ref, x_ref, middle_ref):
    me = lax.axis_index("chan")
    gain, shift = r.gain[...].reshape(1, -1), r.shift[...].reshape(1, -1)
    copies = []

    def row(h, peer, place):
        block = modes_to_rows(plan, r.flat, h)
        out = mm(r.rowinv[...], block.astype(BF))
        middle = out + (unit_ref[h] * gain + shift) + x_ref[h]
        middle_ref[h] = middle
        r.own[peer, place] = pack_cells(middle).astype(BF)

    def send_chunk(step, peer):
        if step:
            copy = push("chan", plan.chans, step, r.own.at[peer], r.mid.at[me], r.s3, r.r3)
            copy.start()
            copies.append(copy)
        else:
            r.mid[me] = r.own[me]

    rows_of_chunks(plan, row, send_chunk)
    return copies


class Block:
    def __init__(self, plan, group, side):
        self.group, self.side, self.size = group, side, plan.columns // 2
        start = group * plan.columns + side * self.size
        self.cells = pl.ds(pl.multiple_of(start, 16), self.size)
        self.front = slice(side * self.size, (side + 1) * self.size)
        self.back = slice(plan.columns, plan.columns + self.size)
        self.lanes = slice(64 * side, 64 * side + 64)

    def get(self, chunks_ref):
        parts = []
        for j in range(chunks_ref.shape[0]):
            parts.append(chunks_ref[j, self.group, self.front, :].astype(F32))
            parts.append(chunks_ref[j, self.group, self.back, self.lanes].astype(F32))
        return jnp.concatenate(parts, axis=1)

    def put(self, chunks_ref, value):
        chans = chunks_ref.shape[0]
        features = value.shape[1] // chans
        for j in range(chans):
            part = value[:, j * features : (j + 1) * features].astype(BF)
            chunks_ref[j, self.group, self.front, :] = part[:, :128]
            chunks_ref[j, self.group, self.back, self.lanes] = part[:, 128:]


def by_blocks(plan, step):
    def one(group, carry):
        for side in range(2):
            step(Block(plan, group, side))
        return carry

    lax.fori_loop(0, plan.share, one, 0, unroll=True)


def full_vector(gathered_ref, start, size):
    chans = gathered_ref.shape[0]
    return jnp.concatenate([gathered_ref[j, 1:2, start : start + size] for j in range(chans)], axis=1)


def moments(value):
    mean = jnp.mean(value, axis=1, keepdims=True)
    centred = value - mean
    return mean, centred, lax.rsqrt(jnp.mean(centred * centred, axis=1, keepdims=True) + NORM_EPS)


ERF = (0.254829592, -0.284496736, 1.421413741, -1.453152027, 1.061405429)


def gelu_and_slope(v):
    e = jnp.exp2(v * v * (-0.5 / math.log(2.0)))
    below = 1.0 + (0.3275911 * math.sqrt(0.5)) * jnp.abs(v)
    t = pl.reciprocal(below, approx=True)
    t = t * (2.0 - below * t)
    c = [0.5 * k for k in ERF]
    tail = (e * t) * (c[0] + t * (c[1] + t * (c[2] + t * (c[3] + t * c[4]))))
    below = jnp.where(v >= 0.0, 1.0 - tail, tail)
    active = v * below
    return active, below + (v * (1.0 / math.sqrt(2.0 * math.pi))) * e


def tile_of(plan, t):
    return t // plan.per, pl.ds(pl.multiple_of((t % plan.per) * plan.tile, plan.tile), plan.tile)


def up_tile(plan, r, t):
    j, place = tile_of(plan, t)
    return r.w[0, j, :, place]


def down_tile(plan, r, t):
    j, place = tile_of(plan, t)
    return r.w[1, j, place, :]


def ffn_scratch(plan):
    shape = (plan.cells, plan.tile)
    made = {key: pltpu.VMEM(shape, F32) for key in ("wide_a", "wide_b")}
    made.update({key: pltpu.VMEM(shape, BF) for key in ("thin_a", "thin_b")})
    made.update(
        total=pltpu.VMEM((plan.cells, plan.width), F32),
        entry=scratch_of(plan.wide),
        unit_wide=scratch_of(plan.wide),
        dev_wide=scratch_of(plan.dev_wide),
        active=scratch_of(plan.tiles),
        slope=scratch_of(plan.tiles),
        gathered=scratch_of(plan.vectors),
    )
    return made


def staggered(plan, r, lead, turn, trail, ready=None):
    last = plan.steps - 1
    third = plan.cells // 3
    side = plan.cells // 2
    parts = plan.width // plan.tile
    r.thin_b[...] = jnp.zeros_like(r.thin_b)
    for k in range(2):
        r.wide_a[k * side : (k + 1) * side, :] = lead(0, slice(k * side, (k + 1) * side))

    def half_step(t, wide_now, wide_next, thin_past, thin_now):
        ahead, behind = jnp.minimum(t + 1, last), jnp.maximum(t - 1, 0)
        for k in range(3):
            place = slice(k * third, (k + 1) * third)
            thin_now[place, :] = turn(wide_now[place, :], t, place, k == 0)
            if k < 2:
                own = slice(k * side, (k + 1) * side)
                wide_next[own, :] = lead(ahead, own)
            trail(thin_past[...], behind, slice(k * parts // 3 * plan.tile, (k + 1) * parts // 3 * plan.tile))

    def pair(u, carry):
        if ready is not None:
            for chunk in range(1, plan.chans):
                pl.when(u == (chunk * plan.per - 1) // 2)(functools.partial(ready, chunk))
        half_step(2 * u, r.wide_a, r.wide_b, r.thin_b, r.thin_a)
        half_step(2 * u + 1, r.wide_b, r.wide_a, r.thin_a, r.thin_b)
        return carry

    lax.fori_loop(0, plan.steps // 2, pair, 0)
    trail(r.thin_b[...], last, slice(0, plan.width))


def ffn_forward(plan, r):
    gain = full_vector(r.gathered, 0, plan.features)
    shift = full_vector(r.gathered, plan.features, plan.features)
    bias = full_vector(r.gathered, 2 * plan.features, plan.features)

    def prepare(block):
        place = block.cells
        mean, centred, inverse = moments(block.get(r.mid))
        unit = centred * inverse
        r.unit_wide[place, :] = unit.astype(BF)
        r.dev_wide[place, :] = jnp.broadcast_to(inverse, (block.size, 128))
        r.entry[place, :] = (unit * gain + shift).astype(BF)
        r.total[place, :] = jnp.broadcast_to(bias, (block.size, plan.width))

    by_blocks(plan, prepare)

    def lead(t, rows):
        j, place = tile_of(plan, t)
        return mm(r.entry[rows, :], up_tile(plan, r, t)) + r.gathered[j, 0:1, place]

    def turn(value, t, rows, opening):
        active, slope = gelu_and_slope(value)
        active = active.astype(BF)
        r.active[t, rows, :] = active
        r.slope[t, rows, :] = slope.astype(BF)
        return active

    def trail(active, t, lanes):
        j, place = tile_of(plan, t)
        r.total[:, lanes] += mm(active, r.w[1, j, place, lanes])

    staggered(plan, r, lead, turn, trail)


def ffn_backward(plan, r, ready=None):
    r.small[...] = jnp.zeros_like(r.small)
    r.total[...] = jnp.zeros_like(r.total)

    def lead(t, rows):
        return mm_nt(r.upper[rows, :], down_tile(plan, r, t))

    def turn(value, t, rows, opening):
        lower = value * r.slope[t, rows, :].astype(F32)
        bias = jnp.sum(lower, axis=0, keepdims=True)
        r.upb[pl.ds(t, 1), :] = bias if opening else r.upb[pl.ds(t, 1), :] + bias
        lower = lower.astype(BF)
        r.slope[t, rows, :] = lower
        return lower

    def trail(lower, t, lanes):
        j, place = tile_of(plan, t)
        r.total[:, lanes] += mm_nt(lower, r.w[0, j, lanes, place])

    staggered(plan, r, lead, turn, trail, ready)
    gain = full_vector(r.gathered, 0, plan.features)

    def finish(block):
        place = block.cells
        grad = r.total[place, :]
        unit = r.unit_wide[place, :].astype(F32)
        r.small[0:1, :] += jnp.sum(grad * unit, axis=0, keepdims=True)
        r.small[1:2, :] += jnp.sum(grad, axis=0, keepdims=True)
        r.small[2:3, :] += jnp.sum(r.upper[place, :].astype(F32), axis=0, keepdims=True)
        scaled = grad * gain
        one = jnp.mean(scaled, axis=1, keepdims=True)
        two = jnp.mean(scaled * unit, axis=1, keepdims=True)
        result = r.dev_wide[place, :][:, :1] * (scaled - one - unit * two)
        block.put(r.leaving, result)

    by_blocks(plan, finish)


def vector_gradients(plan, r, rest_ref):
    rest_ref[...] = jnp.zeros_like(rest_ref)
    for j in range(plan.chans):
        for k in range(plan.per):
            line = j * plan.per + k
            rest_ref[j, 0:1, k * plan.tile : (k + 1) * plan.tile] = r.upb[line : line + 1, :]
        for k in range(3):
            rest_ref[j, 1 + k : 2 + k, 0 : plan.features] = r.small[
                k : k + 1, j * plan.features : (j + 1) * plan.features
            ]


def weight_gradients(r, t):
    return mm_tn(r.active[t], r.upper[...]), mm_tn(r.slope[t], r.entry[...])


def filter_backward(plan, r, there, back, aside=None):
    half = plan.half
    r.mixgrad[...] = jnp.zeros_like(r.mixgrad)
    r.biasgrad[...] = jnp.zeros_like(r.biasgrad)

    def turned(v):
        return jnp.concatenate([v[half:], -v[:half]], axis=0)

    def note_bias(index, value):
        r.biasgrad[index : index + 1, :] += jnp.sum(value, axis=0, keepdims=True)

    def through(low, layer):
        straight = mm_nt(low, r.mix[layer, 0, 0])
        crossed = mm_nt(low, r.mix[layer, 1, 0])
        return jnp.concatenate([straight[:half] + crossed[half:], straight[half:] - crossed[:half]], axis=0)

    def filter_pair(q, carry):
        if aside is not None:
            pl.when(q == 3)(aside)
        p, zeroth, block = pair_inputs(q, there, r.even)
        grad = mm(r.col[0], block.astype(BF))
        grad = jnp.where(r.second[q].astype(F32) == 0.0, 0.0, grad)
        note_bias(2, grad[:half])
        note_bias(3, grad[half:])
        low = grad.astype(BF)
        first = r.first[q]
        r.mixgrad[1, 0] += mm_tn(first, low)
        r.mixgrad[1, 1] += mm_tn(first, turned(grad).astype(BF))
        grad = jnp.where(first.astype(F32) > 0.0, through(low, 1), 0.0)
        note_bias(0, grad[:half])
        note_bias(1, grad[half:])
        low = grad.astype(BF)
        spec = r.spec[q]
        r.mixgrad[0, 0] += mm_tn(spec, low)
        r.mixgrad[0, 1] += mm_tn(spec, turned(grad).astype(BF))
        result = mm(r.colinv[...], through(low, 0).astype(BF))
        pair_outputs(q, p, zeroth, result, back, r.even, r.last, r.stage)
        return carry

    lax.fori_loop(0, plan.pairs + 1, filter_pair, 0)


def mix_gradients(plan, r, before_ref):
    size = plan.size
    for layer in range(2):
        for part in range(2):
            for block in range(2):
                own = slice(block * size, (block + 1) * size)
                piece = r.mixgrad[layer, part][own, own]
                piece = jnp.concatenate([piece, jnp.zeros((size, 128 - size), F32)], axis=1)
                start = ((layer * 2 + part) * 2 + block) * size
                place = slice(start, start + size)
                r.sums[place, :] = piece if before_ref is None else piece + before_ref[place, :]


def rows_backward(plan, r, unit_ref, before_ref):
    gain = r.gain[...].reshape(1, -1)
    me = lax.axis_index("chan")

    def row(h, carry):
        one_sum, two_sum = carry
        block = modes_to_rows(plan, r.flat, h)
        grad = mm(r.row_t[...], block.astype(BF)) + r.out[h]
        unit = unit_ref[h]
        one_sum += jnp.sum(grad * unit, axis=0, keepdims=True)
        two_sum += jnp.sum(grad, axis=0, keepdims=True)
        scaled = grad * gain
        r.scaled[h] = scaled
        r.mine[pl.ds(h, 1), :] = lane_sums(scaled)
        r.mine[pl.ds(plan.rows + h, 1), :] = lane_sums(scaled * unit)
        return one_sum, two_sum

    none = jnp.zeros((1, plan.features), F32)
    one_sum, two_sum = lax.fori_loop(0, plan.rows, row, (none, none), unroll=4)
    r.all[me] = r.mine[...]
    copies = [
        push("chan", plan.chans, step, r.mine, r.all.at[me], r.s4, r.r4) for step in range(1, plan.chans)
    ]
    for copy in copies:
        copy.start()
    vectors = jnp.concatenate([r.biasgrad[0:4], one_sum, two_sum, none, none], axis=0)
    wide = jnp.concatenate([vectors, jnp.zeros((8, 256 - plan.features), F32)], axis=1)
    wide = jnp.concatenate([wide[:, :128], wide[:, 128:]], axis=0)
    place = slice(8 * plan.size, plan.small)
    r.sums[place, :] = wide if before_ref is None else wide + before_ref[place, :]
    return copies


def input_gradient(plan, r, unit_ref, dev_ref):
    r.mine[...] = sum(r.all[j] for j in range(plan.chans)) * (1.0 / plan.width)

    def result(h):
        table = stack_rows(
            [r.mine[pl.ds(h, 1), :], r.mine[pl.ds(plan.rows + h, 1), :], dev_ref[pl.ds(h, 1), :]]
        )
        one, two, dev = [over_lanes(table, plan.features, k) for k in range(3)]
        return r.out[h] + dev * (r.scaled[h] - one - unit_ref[h] * two)

    return result


def norm_sums_scratch(plan):
    return {
        "scaled": scratch_of(plan.field),
        "mixgrad": pltpu.VMEM((2, 2, plan.features, plan.features), F32),
        "biasgrad": pltpu.VMEM((8, plan.features), F32),
        "mine": pltpu.VMEM((2 * plan.rows, plan.columns), F32),
        "all": pltpu.VMEM((plan.chans, 2 * plan.rows, plan.columns), F32),
        "s4": sems(plan.chans),
        "r4": sems(plan.chans),
    }


class Moves:
    def __init__(self, sem):
        self.sem, self.count, self.open = sem, 0, []

    def start(self, source, target):
        copy = pltpu.make_async_copy(source, target, self.sem.at[self.count])
        self.count += 1
        copy.start()
        self.open.append(copy)
        return copy

    def close(self):
        wait_all(self.open)


def launch_first(plan, args, tables):
    rows, features, chans = plan.rows, plan.features, plan.chans

    def body(r):
        me = lax.axis_index("chan")
        place = lax.axis_index("space")
        core = lax.rem(place, 2)
        sibling = place + 1 - 2 * core
        met = greet(plan)
        moves = Moves(r.dma)
        moves.start(r.up, r.w.at[0, me])
        moves.start(r.down, r.w.at[1, me])
        loaded = moves.start(r.lines_t, r.lines_in)
        own_weights = moves.open[:2]
        moves.open = []

        beside = me + 1 - 2 * lax.rem(me, 2)
        across = me + 2 - 4 * (me // 2)
        far = chans - 1 - me
        upper_half, lower_half = pl.ds(0, plan.local // 2), pl.ds(plan.local // 2, plan.local // 2)

        def hand(source, target, number, device):
            return pltpu.make_async_remote_copy(
                src_ref=source,
                dst_ref=target,
                send_sem=r.s5.at[number],
                recv_sem=r.r5.at[number],
                device_id=device,
                device_id_type=MESH_ID,
            )

        def own_to(number, source):
            peer = (beside, across)[number]
            return hand(source, r.w.at[core, me], number, {"chan": peer})

        def relay(number):
            slot = (beside, across)[number]
            part = r.w.at[core, slot, (upper_half, lower_half)[number]]
            return hand(part, part, 2 + number, {"chan": (across, beside)[number]})

        def to_core(number):
            if number < 2:
                part = r.w.at[core, (beside, across)[number]]
            else:
                part = r.w.at[core, far]
            return pltpu.make_async_remote_copy(
                src_ref=part,
                dst_ref=part,
                send_sem=r.s7.at[number],
                recv_sem=r.r7.at[number],
                device_id={"space": sibling},
                device_id_type=MESH_ID,
            )

        def pass_near():
            for number in range(2):
                own_to(number, r.up).wait_recv()
            for number in range(2):
                relay(number).start()
            for number in range(2):
                to_core(number).start()

        def pass_far():
            for number in range(2):
                relay(number).wait_recv()
            to_core(2).start()

        def close_weights():
            for number in range(2):
                own_to(number, r.up).wait_send()
                relay(number).wait_send()
            for number in range(3):
                to_core(number).wait()

        def first(h, carry):
            block = cells_from_lines(r.lines_x, h, r.turn)
            r.turned[h] = block
            total = jnp.sum(block, axis=0, keepdims=True)
            centred = block - total * (1.0 / features)
            r.mine[pl.ds(h, 1), :] = total
            r.mine[pl.ds(rows + h, 1), :] = jnp.sum(centred * centred, axis=0, keepdims=True)
            return carry

        lax.fori_loop(0, rows, first, 0)
        r.all[me] = r.mine[...]
        met()
        sums = [push("chan", chans, step, r.mine, r.all.at[me], r.s4, r.r4) for step in range(1, chans)]
        for copy in sums:
            copy.start()
        mark_even(plan, r)

        def row_of(ref):
            return ref[...].reshape(1, -1).astype(F32)

        r.vectors[...] = jnp.zeros_like(r.vectors)
        r.vectors[0:1, :] = row_of(r.upb)
        r.vectors[1:2, 0:features] = row_of(r.post_gain)
        r.vectors[1:2, features : 2 * features] = row_of(r.post_shift)
        r.vectors[1:2, 2 * features : 3 * features] = row_of(r.downb)
        r.gathered[me] = r.vectors[...]
        for layer, (source, bias) in enumerate(((r.mix_in, r.bias_in), (r.mix_out, r.bias_out))):
            for part in range(2):
                zero = jnp.zeros((plan.size, plan.size), F32)
                value = jnp.concatenate(
                    [
                        jnp.concatenate([source[part, 0], zero], axis=1),
                        jnp.concatenate([zero, source[part, 1]], axis=1),
                    ],
                    axis=0,
                )
                high, low = halves(value)
                r.mix[layer, part, 0] = high
                r.mix[layer, part, 1] = low
                line = 2 * layer + part
                r.bias[line : line + 1, :] = jnp.concatenate([bias[part, 0:1, :], bias[part, 1:2, :]], axis=1)
        moves.start(r.mix, r.mix_kept)


        def turn_row(h, carry):
            r.x[h] = r.turned[h].T
            return carry

        lax.fori_loop(0, rows, turn_row, 0, unroll=2)
        wait_all(sums)
        given = [push("chan", chans, step, r.vectors, r.gathered.at[me], r.s6, r.r6) for step in range(1, chans)]
        for copy in given:
            copy.start()
        for kind, source in enumerate((r.up, r.down)):

            @pl.when(core == kind)
            def _():
                for number in range(2):
                    own_to(number, source).start()

        totals = [r.all[j] for j in range(chans)]
        mean = sum(t[:rows] for t in totals) * (1.0 / plan.width)
        spread_sum = sum(
            t[rows:] + features * jnp.square(t[:rows] * (1.0 / features) - mean) for t in totals
        ) * (1.0 / plan.width)
        r.mine[pl.ds(0, rows), :] = mean
        r.mine[pl.ds(rows, rows), :] = lax.rsqrt(spread_sum + NORM_EPS)
        gain, shift = r.gain[...].reshape(1, -1), r.shift[...].reshape(1, -1)

        def normed(h):
            inverse = r.mine[pl.ds(rows + h, 1), :]
            table = stack_rows([r.mine[pl.ds(h, 1), :], inverse])
            unit = (r.x[h] - over_lanes(table, features, 0)) * over_lanes(table, features, 1)
            r.unit[h] = unit
            r.dev[pl.ds(h, 1), :] = inverse
            return unit * gain + shift

        scales = (r.scale, r.scale_all, r.s20, r.r20)
        there = Exchange(True, plan.spaces, plan.thick, r.send1, r.recv1, r.s1, r.r1, scales)
        back = Exchange(False, plan.spaces, plan.thick, r.send2, r.recv2, r.s2, r.r2)
        rows_to_modes(plan, (r.row[0], r.row[1]), r.flat, normed, True)
        send_modes(there, plan.pairs, plan.chunk, r.flat)
        moves.start(r.unit, r.unit_kept)
        moves.start(r.dev, r.dev_kept)
        loaded.wait()
        enter(r.lines_in, r.cells_t, r.turn)
        moves.start(r.cells_t, r.cells_kept)
        filter_forward(plan, r, there, back, pass_near)
        for source, target in ((r.spec, r.spec_kept), (r.first, r.first_kept), (r.second, r.second_kept)):
            moves.start(source, target)
        collect(back, plan.pairs, plan.chunk, r.flat)
        pass_far()
        copies = rows_forward(plan, r, r.unit, r.x, r.middle)
        moves.start(r.middle, r.middle_kept)
        wait_all(copies + given)
        close_weights()
        wait_all(own_weights)
        moves.start(r.w, r.w_kept)
        ffn_forward(plan, r)
        saved = ("active", "slope", "entry", "unit_wide", "dev_wide", "gathered")
        for key in saved:
            moves.start(getattr(r, key), getattr(r, key + "_kept"))

        def last(block):
            outer = r.total[block.cells, :]
            mean, _, inverse = moments(outer + block.get(r.mid))
            block.put(r.leaving, outer)
            r.stats[block.group, block.front, :] = jnp.concatenate(
                three_parts(mean) + three_parts(inverse) + [jnp.zeros((block.size, 122), BF)], axis=1
            )

        by_blocks(plan, last)
        copies = spread_chan(plan, r.leaving, r.home, r.s8, r.r8)
        for group in range(plan.share):
            r.stats_thin[group] = r.stats[group].astype(F32).T[:16].astype(BF)
        others = [
            push("chan", chans, step, r.stats_thin, r.stats_home.at[me], r.s9, r.r9) for step in range(1, chans)
        ]
        for copy in others:
            copy.start()
        r.stats_home[me] = r.stats_thin[...]
        wait_all(copies + others)
        there.close(plan.pairs)
        back.close(plan.pairs)
        moves.close()

    stats = ((chans, plan.share, 16, plan.columns), BF)
    outs = {
        "home": plan.by_cells,
        "stats_home": stats,
        "middle_kept": plan.field,
        "unit_kept": plan.field,
        "dev_kept": plan.dev,
        "cells_kept": plan.field,
        "spec_kept": plan.kept,
        "first_kept": plan.kept,
        "second_kept": plan.kept,
        "mix_kept": plan.mix,
        "w_kept": plan.weights,
        "active_kept": plan.tiles,
        "slope_kept": plan.tiles,
        "entry_kept": plan.wide,
        "unit_wide_kept": plan.wide,
        "dev_wide_kept": plan.dev_wide,
        "gathered_kept": plan.vectors,
        "bias": ((8, features), F32),
    }
    ins = dict(args)
    ins.update({key: tables[key] for key in ("row", "rowinv", "col", "colinv")})
    scratch = {
        "dma": sems(20),
        "x": scratch_of(plan.field),
        "unit": scratch_of(plan.field),
        "dev": scratch_of(plan.dev),
        "middle": scratch_of(plan.field),
        "cells_t": scratch_of(plan.field),
        "lines_in": scratch_of(plan.lines),
        "turned": pltpu.VMEM((rows, features, plan.columns), F32),
        "mine": pltpu.VMEM((2 * rows, plan.columns), F32),
        "all": pltpu.VMEM((chans, 2 * rows, plan.columns), F32),
        "spec": scratch_of(plan.kept),
        "first": scratch_of(plan.kept),
        "second": scratch_of(plan.kept),
        "mix": scratch_of(plan.mix),
        "w": scratch_of(plan.weights),
        "vectors": pltpu.VMEM((8, plan.local), F32),
        "own": scratch_of(plan.by_cells),
        "mid": scratch_of(plan.by_cells),
        "leaving": scratch_of(plan.by_cells),
        "stats": pltpu.VMEM((plan.share, plan.columns, 128), BF),
        "stats_thin": pltpu.VMEM(stats[0][1:], BF),
        **plan.exchange_scratch(True, False),
        **plan.spectral_scratch(),
        **ffn_scratch(plan),
        **{key + str(k): sems(chans) for k in range(3, 10) for key in ("s", "r")},
    }
    in_place = ("up", "down", "lines_t")
    return launch(
        body,
        ins,
        outs,
        scratch,
        "first_forward",
        0,
        {key: IN_PLACE for key in in_place},
        {key: IN_PLACE for key in outs if key.endswith("_kept")},
    )


def launch_second(plan, args, one, tables):
    rows, features, chans = plan.rows, plan.features, plan.chans

    def body(r):
        me = lax.axis_index("chan")
        met = greet(plan)
        mark_even(plan, r)
        moves = Moves(r.dma)
        loaded = moves.start(r.lines_t, r.lines_in)
        weights = moves.start(r.w_kept, r.w)
        vectors = moves.start(r.gathered_kept, r.gathered)
        earlier = moves.start(r.cells_kept, r.cells_one)
        moves.open = []
        gain, shift = r.gain[...].reshape(1, -1), r.shift[...].reshape(1, -1)
        weight = r.codes[0].astype(F32) * (1.0 / 64.0)

        def normed(h):
            quarter, inside = h // plan.share, h % plan.share
            x = unpack_cells(r.home[quarter, inside].astype(F32)) + r.before[h]
            table = r.stats_home[quarter, inside]
            unit = (x - over_lanes(table, features, 0)) * over_lanes(table, features, 1)
            r.x[h] = x
            r.unit[h] = unit
            r.dev[pl.ds(h, 1), :] = jnp.sum(table[3:6].astype(F32), axis=0, keepdims=True)
            return unit * gain + shift

        rows_to_modes(plan, (r.row[0], r.row[1]), r.flat, normed, True)
        met()
        scales = (r.scale, r.scale_all, r.s20, r.r20)
        there = Exchange(True, plan.spaces, plan.thick, r.send1, r.recv1, r.s1, r.r1, scales)
        back = Exchange(False, plan.spaces, plan.thick, r.send2, r.recv2, r.s2, r.r2)
        send_modes(there, plan.pairs, plan.chunk, r.flat)
        loaded.wait()
        enter(r.lines_in, r.cells_t, r.turn)

        def low_target(h, peer, place):
            r.own[peer, place] = pack_cells(r.cells_t[h]).astype(BF)

        targets = []

        def send_target(step, peer):
            if step:
                copy = push("chan", chans, step, r.own.at[peer], r.target.at[me], r.s5, r.r5)
                copy.start()
                targets.append(copy)
            else:
                r.target[me] = r.own[me]

        rows_of_chunks(plan, low_target, send_target)
        filter_forward(plan, r, there, back)
        collect(back, plan.pairs, plan.chunk, r.flat)
        there.close(plan.pairs)
        back.close(plan.pairs)
        wait_all(targets)
        copies = rows_forward(plan, r, r.unit, r.x, r.before)
        weights.wait()
        vectors.wait()
        wait_all(copies)
        ffn_forward(plan, r)

        def errors(block):
            outer = r.total[block.cells, :]
            error = outer + block.get(r.mid) - block.get(r.target)
            r.upper[block.cells, :] = (weight * error).astype(BF)
            block.put(r.leaving, outer)

        by_blocks(plan, errors)
        copies = spread_chan(plan, r.leaving, r.landed, r.s6, r.r6)
        for copy in copies:
            copy.wait_send()
        ffn_backward(plan, r)
        for copy in copies:
            copy.wait_recv()
        copies = spread_chan(plan, r.leaving, r.own, r.s7, r.r7)

        def grads(u, carry):
            for slot in range(2):
                t = 2 * u + slot
                stores = [
                    pltpu.make_async_copy(r.grad.at[slot, k], r.grads_kept.at[k, t], r.dma2.at[slot, k])
                    for k in range(2)
                ]

                @pl.when(u > 0)
                def _():
                    wait_all(stores)

                for k, value in enumerate(weight_gradients(r, t)):
                    r.grad[slot, k] = value.astype(BF)
                    stores[k].start()
            return carry

        lax.fori_loop(0, plan.steps // 2, grads, 0)
        vector_gradients(plan, r, r.rest)
        wait_all(copies)

        def middle_grad(h):
            quarter, inside = h // plan.share, h % plan.share
            x = unpack_cells(r.landed[quarter, inside].astype(F32)) + r.before[h]
            r.before[h] = x
            grad = weight * (x - r.cells_t[h]) + unpack_cells(r.own[quarter, inside].astype(F32))
            r.out[h] = grad
            return grad

        rows_to_modes(plan, r.rowinv_t[...], r.flat, middle_grad, False)
        there = Exchange(False, plan.spaces, plan.thick, r.send3, r.recv3, r.s3_, r.r3_)
        back = Exchange(False, plan.spaces, plan.thick, r.send2, r.recv2, r.s2, r.r2)
        send_modes(there, plan.pairs, plan.chunk, r.flat)
        moves.start(r.before, r.second_x)
        leave(r.x, r.lines_in, r.turn)
        moves.start(r.lines_in, r.lines)
        filter_backward(plan, r, there, back)
        mix_gradients(plan, r, None)
        collect(back, plan.pairs, plan.chunk, r.flat)
        copies = rows_backward(plan, r, r.unit, None)
        earlier.wait()
        wait_all(copies)
        result = input_gradient(plan, r, r.unit, r.dev)
        copies = []

        def row(h, peer, place):
            grad = weight * (r.x[h] - r.cells_one[h]) + result(h)
            r.out[h] = grad
            r.own[peer, place] = pack_cells(grad).astype(BF)

        def send_chunk(step, peer):
            if step:
                copy = push("chan", chans, step, r.own.at[peer], r.came.at[me], r.s8, r.r8)
                copy.start()
                copies.append(copy)
            else:
                r.came[me] = r.own[me]

        rows_of_chunks(plan, row, send_chunk)
        for slot in range(2):
            for k in range(2):
                pltpu.make_async_copy(
                    r.grad.at[slot, k], r.grads_kept.at[k, plan.steps - 2 + slot], r.dma2.at[slot, k]
                ).wait()
        wait_all(copies)
        there.close(plan.pairs)
        back.close(plan.pairs)
        moves.close()

    ins = {
        "home": one["home"],
        "stats_home": one["stats_home"],
        "before": one["middle_kept"],
        "w_kept": one["w_kept"],
        "gathered_kept": one["gathered_kept"],
        "cells_kept": one["cells_kept"],
        "mix": one["mix_kept"],
        "bias": one["bias"],
        **args,
    }
    ins.update({key: tables[key] for key in ("row", "rowinv", "rowinv_t", "row_t", "col", "colinv")})
    outs = {
        "out": plan.field,
        "came": plan.by_cells,
        "lines": plan.lines,
        "second_x": plan.field,
        "sums": plan.sums,
        "rest": plan.rest,
        "grads_kept": plan.grads,
    }
    exchange = Exchange.shape(False, plan.spaces, plan.thick, plan.pairs)
    scratch = {
        "dma": sems(8),
        "dma2": sems(2, 2),
        "x": scratch_of(plan.field),
        "unit": scratch_of(plan.field),
        "dev": scratch_of(plan.dev),
        "cells_t": scratch_of(plan.field),
        "cells_one": scratch_of(plan.field),
        "lines_in": scratch_of(plan.lines),
        "spec": scratch_of(plan.kept),
        "first": scratch_of(plan.kept),
        "second": scratch_of(plan.kept),
        "w": scratch_of(plan.weights),
        "own": scratch_of(plan.by_cells),
        "mid": scratch_of(plan.by_cells),
        "target": scratch_of(plan.by_cells),
        "leaving": scratch_of(plan.by_cells),
        "landed": scratch_of(plan.by_cells),
        "upper": scratch_of(plan.wide),
        "small": pltpu.VMEM((8, plan.width), F32),
        "upb": pltpu.VMEM((16, plan.tile), F32),
        "grad": pltpu.VMEM((2, 2, plan.tile, plan.width), BF),
        "send3": exchange,
        "recv3": exchange,
        "s3_": sems(plan.pairs, plan.spaces),
        "r3_": sems(plan.pairs, plan.spaces),
        **plan.exchange_scratch(True, False),
        **plan.spectral_scratch(),
        **ffn_scratch(plan),
        **norm_sums_scratch(plan),
        **{key + str(k): sems(chans) for k in (3, 5, 6, 7, 8) for key in ("s", "r")},
    }
    in_specs = {key: IN_PLACE for key in ("w_kept", "gathered_kept", "cells_kept", "lines_t")}
    in_specs["codes"] = pl.BlockSpec(memory_space=pltpu.SMEM)
    return launch(
        body,
        ins,
        outs,
        scratch,
        "second_step",
        1,
        in_specs,
        {key: IN_PLACE for key in ("second_x", "grads_kept", "lines")},
    )


def launch_third(plan, args, one, two, tables):
    rows, features, chans, spaces = plan.rows, plan.features, plan.chans, plan.spaces
    local, width = plan.local, plan.width
    levels = spaces // 2
    piece = local // levels
    small = plan.small
    part = -(-(small + 32) // (16 * levels)) * 16

    def body(r):
        me = lax.axis_index("chan")
        place = lax.axis_index("space")
        core = lax.rem(place, 2)
        level = place // 2
        sibling = place + 1 - 2 * core
        others = [lax.rem(level + step, levels) for step in range(1, levels)]
        met = greet(plan)
        mark_even(plan, r)
        moves = Moves(r.dma)
        early = [
            moves.start(source, target)
            for source, target in (
                (r.gathered_kept, r.gathered),
                (r.unit_wide_kept, r.unit_wide),
                (r.dev_wide_kept, r.dev_wide),
            )
        ]
        chunks = []
        for j in range(chans):
            tiles = pl.ds(j * plan.per, plan.per)
            chunks.append(
                [
                    moves.start(r.w_kept.at[1, j], r.w.at[1, j]),
                    moves.start(r.slope_kept.at[tiles], r.slope.at[tiles]),
                    moves.start(r.w_kept.at[0, j], r.w.at[0, j]),
                ]
            )
        middle = [moves.start(r.active_kept, r.active), moves.start(r.entry_kept, r.entry)]
        moves.open = []

        def upper(block):
            r.upper[block.cells, :] = block.get(r.came).astype(BF)

        by_blocks(plan, upper)
        wait_all(early)
        wait_all(chunks[0])
        ffn_backward(plan, r, lambda chunk: wait_all(chunks[chunk]))
        late = [
            moves.start(source, target)
            for source, target in (
                (r.g, r.out),
                (r.unit_kept, r.unit),
                (r.spec_kept, r.spec),
                (r.first_kept, r.first),
                (r.second_kept, r.second),
                (r.dev_kept, r.dev),
            )
        ]
        moves.open = []
        met()
        copies = spread_chan(plan, r.leaving, r.own, r.s7, r.r7)
        vector_gradients(plan, r, r.rest)
        r.rest[...] += r.rest_before[...]
        vectors = [
            push("chan", chans, step, r.rest.at[lax.rem(me + step, chans)], r.rest_land.at[me], r.s6, r.r6)
            for step in range(1, chans)
        ]
        for copy in vectors:
            copy.start()
        r.rest_land[me] = r.rest[me]
        wait_all(middle)

        column, line = lax.rem(me, 2), me // 2
        beside = me + 1 - 2 * column
        across = me + 2 - 4 * line
        near, under = pl.ds(0, plan.tile // 2), pl.ds(plan.tile // 2, plan.tile // 2)

        def order(i):
            k = i // plan.per
            owner_column = column + (1 - k // 2) * (1 - 2 * column)
            owner_line = line + (1 - k % 2) * (1 - 2 * line)
            return (2 * owner_line + owner_column) * plan.per + i % plan.per

        def fetch(i, k):
            return pltpu.make_async_copy(r.grads_kept.at[k, order(i)], r.prev.at[i % 2, k], r.dma2.at[i % 2, k])

        def swap(i):
            return pltpu.make_async_remote_copy(
                src_ref=r.give.at[i % 2],
                dst_ref=r.take.at[i % 3],
                send_sem=r.s9.at[i],
                recv_sem=r.r9.at[i],
                device_id={"space": sibling},
                device_id_type=MESH_ID,
            )

        def to_chan(source, target, sem, number, device):
            return pltpu.make_async_remote_copy(
                src_ref=source,
                dst_ref=target,
                send_sem=sem[0].at[number],
                recv_sem=sem[1].at[number],
                device_id={"chan": device},
                device_id_type=MESH_ID,
            )

        def ship_near(i):
            target = r.land_near.at[i // plan.per, i % plan.per]
            return to_chan(r.keep.at[i, near], target, (r.s10, r.r10), i, beside)

        def ship_under(j):
            i = j + (j // plan.per) * plan.per
            target = r.land_under.at[j // plan.per, j % plan.per]
            return to_chan(r.keep.at[i, under], target, (r.s17, r.r17), j, across)

        def on_across(k):
            return to_chan(
                r.keep.at[2 * plan.per + k, near], r.land_on.at[0, k], (r.s18, r.r18), k, across
            )

        def on_beside(k):
            return to_chan(
                r.keep.at[plan.per + k, under], r.land_on.at[1, k], (r.s18, r.r18), plan.per + k, beside
            )

        def pass_on():
            def tile(k, carry):
                for arrived, land, start, part, onward in (
                    (ship_near, r.land_near, 2 * plan.per, near, on_across),
                    (ship_under, r.land_under, plan.per, under, on_beside),
                ):
                    arrived(k).wait_recv()
                    value = r.keep[start + k, part, :].astype(F32) + land[0, k].astype(F32)
                    r.keep[start + k, part, :] = value.astype(BF)
                    onward(k).start()
                return carry

            lax.fori_loop(0, plan.per, tile, 0)

        for k in range(2):
            fetch(0, k).start()

        def settle(i):
            swap(i).wait()
            r.keep[i] = (r.keep[i].astype(F32) + r.take[i % 3].astype(F32)).astype(BF)

        shipped = plan.steps - plan.per

        def leave_block(i):
            settle(i)

            @pl.when(i < 2 * plan.per)
            def _():
                ship_near(i).start()

            @pl.when(i < plan.per)
            def _():
                ship_under(i).start()

            @pl.when(i >= 2 * plan.per)
            def _():
                ship_under(i - plan.per).start()

        def make_block(i, before):
            for k in range(2):
                fetch(i, k).wait()

            @pl.when(i + 1 < plan.steps)
            def _():
                for k in range(2):
                    fetch(i + 1, k).start()

            values = [
                (value + r.prev[i % 2, k].astype(F32)).astype(BF)
                for k, value in enumerate(weight_gradients(r, order(i)))
            ]
            before(i)
            for kind in range(2):

                @pl.when(core == kind)
                def _():
                    r.keep[i] = values[kind]
                    r.give[i % 2] = values[1 - kind]

            swap(i).start()

        def others_block(i, carry):
            make_block(i, lambda i: pl.when(i > 0)(lambda: leave_block(i - 1)))
            return carry

        def own_block(i, carry):
            make_block(i, lambda i: pl.when(i > shipped)(lambda: settle(i - 1)))
            return carry

        lax.fori_loop(0, shipped, others_block, 0)
        leave_block(shipped - 1)
        wait_all(copies)
        wait_all(late)

        def middle_grad(h):
            quarter, inside = h // plan.share, h % plan.share
            grad = r.out[h] + unpack_cells(r.own[quarter, inside].astype(F32))
            r.out[h] = grad
            return grad

        rows_to_modes(plan, r.rowinv_t[...], r.flat, middle_grad, False)
        there = Exchange(False, spaces, plan.thick, r.send1, r.recv1, r.s1, r.r1)
        back = Exchange(False, spaces, plan.thick, r.send2, r.recv2, r.s2, r.r2)
        send_modes(there, plan.pairs, plan.chunk, r.flat)
        lax.fori_loop(shipped, plan.steps, own_block, 0)
        settle(plan.steps - 1)
        filter_backward(plan, r, there, back, pass_on)
        mix_gradients(plan, r, r.sums_before)

        def arrived(k, carry):
            ship_near(k).wait_send()
            ship_near(plan.per + k).wait()
            ship_under(k).wait_send()
            ship_under(plan.per + k).wait()
            on_across(k).wait()
            on_beside(k).wait()
            return carry

        lax.fori_loop(0, plan.per, arrived, 0)
        wait_all(vectors)
        def send(source, target, step, send_sem, recv_sem):
            return pltpu.make_async_remote_copy(
                src_ref=source,
                dst_ref=target,
                send_sem=send_sem.at[step],
                recv_sem=recv_sem.at[step],
                device_id={"space": 2 * others[step - 1] + core},
                device_id_type=MESH_ID,
            )

        def to_sibling(source, target, step, send_sem, recv_sem):
            return pltpu.make_async_remote_copy(
                src_ref=source,
                dst_ref=target,
                send_sem=send_sem.at[step],
                recv_sem=recv_sem.at[step],
                device_id={"space": sibling},
                device_id_type=MESH_ID,
            )

        def total(tile, carry):
            for half, land in enumerate((r.land_near, r.land_under)):
                for sub in range(2):
                    inside = pl.ds(64 * sub, 64)
                    value = r.keep[3 * plan.per + tile, pl.ds(128 * half + 64 * sub, 64), :].astype(F32)
                    value += land[1, tile, inside, :].astype(F32) + r.land_on[half, tile, inside, :].astype(F32)
                    number = 4 * tile + 2 * half + sub
                    target = pl.ds(pl.multiple_of((number % (piece // 64)) * 64, 64), 64)
                    r.a_send[number // (piece // 64), target, :] = value.astype(BF)
            return carry

        lax.fori_loop(0, plan.per, total, 0)
        wide = [
            send(r.a_send.at[others[step - 1]], r.a_land.at[level], step, r.s11, r.r11)
            for step in range(1, levels)
        ]
        for copy in wide:
            copy.start()
        collect(back, plan.pairs, plan.chunk, r.flat)
        copies = rows_backward(plan, r, r.unit, r.sums_before)
        r.table[...] = jnp.zeros_like(r.table)
        r.table[0:small, :] = r.sums[...]
        tail = sum(r.rest_land[j] for j in range(chans))
        for k in range(local // 128):
            lanes = slice(k * 128, (k + 1) * 128)
            r.table[small + k : small + k + 1, :] = tail[0:1, lanes]
        for k in range(3):
            line = jnp.concatenate([tail[1 + k : 2 + k, :features], jnp.zeros((1, 256 - features), F32)], axis=1)
            r.table[small + 8 + 2 * k : small + 9 + 2 * k, :] = line[:, :128]
            r.table[small + 9 + 2 * k : small + 10 + 2 * k, :] = line[:, 128:]
        for q in range(levels):
            r.b_send[q] = r.table[q * part : (q + 1) * part, :].astype(BF)
        thin = [
            send(r.b_send.at[others[step - 1]], r.b_land.at[level], step, r.s12, r.r12)
            for step in range(1, levels)
        ]
        for copy in thin:
            copy.start()
        wait_all(copies)
        result = input_gradient(plan, r, r.unit, r.dev)

        def finish(h, carry):
            r.out[h] = result(h)
            return carry

        lax.fori_loop(0, rows, finish, 0, unroll=3)
        moves.start(r.second_x, r.scaled).wait()
        moves.open = []
        leave(r.scaled, r.lines, r.turn)
        moves.start(r.lines, r.lines_x)
        a = r.a_send[level].astype(F32)
        b = r.b_send[level].astype(F32)
        for step in range(1, levels):
            wide[step - 1].wait()
            thin[step - 1].wait()
            source = lax.rem(level - step + levels, levels)
            a += r.a_land[source].astype(F32)
            b += r.b_land[source].astype(F32)
        r.a_own[...] = a.astype(BF)
        r.b_own[...] = b.astype(BF)
        last = [to_sibling(r.a_own, r.a_other.at[level], 0, r.s13, r.r13)]
        last += [to_sibling(r.b_own, r.b_other.at[level], 0, r.s14, r.r14)]
        again = []
        for step in range(1, levels):
            again.append(send(r.a_own, r.a_full.at[level], step, r.s15, r.r15))
            again.append(send(r.b_own, r.b_full.at[level], step, r.s16, r.r16))
        for copy in again + last:
            copy.start()
        r.a_full[level] = r.a_own[...]
        r.b_full[level] = r.b_own[...]
        moves.close()
        moves.open = []
        leave(r.out, r.lines, r.turn)
        moves.start(r.lines, r.lines_out)
        for step in range(1, levels):
            again[2 * step - 2].wait()
            again[2 * step - 1].wait()
            source = lax.rem(level - step + levels, levels)
            more = [to_sibling(r.a_full.at[source], r.a_other.at[source], step, r.s13, r.r13)]
            more += [to_sibling(r.b_full.at[source], r.b_other.at[source], step, r.s14, r.r14)]
            for copy in more:
                copy.start()
            last += more
        wait_all(last)
        moves.close()
        there.close(plan.pairs)
        back.close(plan.pairs)

    ins = {
        "g": two["out"],
        "came": two["came"],
        "second_x": two["second_x"],
        "sums_before": two["sums"],
        "rest_before": two["rest"],
        "grads_kept": two["grads_kept"],
        "mix": one["mix_kept"],
        **{
            key: one[key]
            for key in (
                "w_kept",
                "slope_kept",
                "active_kept",
                "entry_kept",
                "unit_wide_kept",
                "dev_wide_kept",
                "gathered_kept",
                "spec_kept",
                "first_kept",
                "second_kept",
                "unit_kept",
                "dev_kept",
            )
        },
        **args,
    }
    ins.update({key: tables[key] for key in ("rowinv_t", "row_t", "col", "colinv")})
    outs = {
        "lines_x": plan.lines,
        "lines_out": plan.lines,
        "a_full": ((levels, piece, width), BF),
        "a_other": ((levels, piece, width), BF),
        "b_full": ((levels, part, 128), BF),
        "b_other": ((levels, part, 128), BF),
    }
    blocks = pltpu.VMEM((plan.steps, plan.tile, width), BF)
    scratch = {
        "dma": sems(28),
        "dma2": sems(2, 2),
        "lines": scratch_of(plan.lines),
        "unit": scratch_of(plan.field),
        "dev": scratch_of(plan.dev),
        "out": scratch_of(plan.field),
        "spec": scratch_of(plan.kept),
        "first": scratch_of(plan.kept),
        "second": scratch_of(plan.kept),
        "w": scratch_of(plan.weights),
        "own": scratch_of(plan.by_cells),
        "leaving": scratch_of(plan.by_cells),
        "upper": scratch_of(plan.wide),
        "small": pltpu.VMEM((8, width), F32),
        "upb": pltpu.VMEM((16, plan.tile), F32),
        "sums": scratch_of(plan.sums),
        "rest": scratch_of(plan.rest),
        "rest_land": scratch_of(plan.rest),
        "prev": pltpu.VMEM((2, 2, plan.tile, width), BF),
        "keep": blocks,
        "give": pltpu.VMEM((2, plan.tile, width), BF),
        "take": pltpu.VMEM((3, plan.tile, width), BF),
        "land_near": pltpu.VMEM((2, plan.per, plan.tile // 2, width), BF),
        "land_under": pltpu.VMEM((2, plan.per, plan.tile // 2, width), BF),
        "land_on": pltpu.VMEM((2, plan.per, plan.tile // 2, width), BF),
        "table": pltpu.VMEM((part * levels, 128), F32),
        "a_send": pltpu.VMEM((levels, piece, width), BF),
        "a_land": pltpu.VMEM((levels, piece, width), BF),
        "a_own": pltpu.VMEM((piece, width), BF),
        "b_send": pltpu.VMEM((levels, part, 128), BF),
        "b_land": pltpu.VMEM((levels, part, 128), BF),
        "b_own": pltpu.VMEM((part, 128), BF),
        **plan.exchange_scratch(False, False),
        **plan.spectral_scratch(),
        **ffn_scratch(plan),
        **norm_sums_scratch(plan),
        **{key + str(k): sems(chans) for k in (6, 7) for key in ("s", "r")},
        **{key + str(k): sems(plan.steps) for k in (9, 10, 17, 18) for key in ("s", "r")},
        **{key + str(k): sems(levels) for k in range(11, 17) for key in ("s", "r")},
    }
    in_place = [key for key in ins if key.endswith("_kept") and key != "mix_kept"] + ["second_x", "g"]
    return launch(
        body,
        ins,
        outs,
        scratch,
        "first_backward",
        2,
        {key: IN_PLACE for key in in_place},
        {key: IN_PLACE for key in ("lines_x", "lines_out")},
    )


def unpack_gradients(plan, parts, fields):
    features, small = plan.features, plan.small
    levels, piece, width = parts["a_full"].shape
    part = parts["b_full"].shape[1]
    local = levels * piece
    size = features // 2

    def body(r):
        swap = lax.rem(lax.axis_index("space"), 2) == 1
        moves = Moves(r.dma)
        waiting = [(moves.start(getattr(r, key + "_in"), getattr(r, key + "_held")), key) for key in fields]
        for q in range(levels):
            own = slice(q * piece, (q + 1) * piece)
            mine, theirs = r.a_full[q], r.a_other[q]
            r.down_made[own, :] = jnp.where(swap, theirs, mine).astype(F32)
            r.up_made[:, own] = jnp.where(swap, mine, theirs).T.astype(F32)
            moves.start(r.down_made.at[pl.ds(q * piece, piece)], r.down.at[pl.ds(q * piece, piece)])
            if q % 2:
                lanes = pl.ds((q - 1) * piece, 2 * piece)
                moves.start(r.up_made.at[:, lanes], r.up.at[:, lanes])
            if q < len(waiting):
                loaded, key = waiting[q]
                loaded.wait()
                moves.start(getattr(r, key + "_held"), getattr(r, key))
            r.table[q * part : (q + 1) * part, :] = r.b_full[q].astype(F32) + r.b_other[q].astype(F32)
        for layer, target in enumerate((r.mix_in, r.mix_out)):
            for half in range(2):
                for block in range(2):
                    start = ((layer * 2 + half) * 2 + block) * size
                    target[half, block] = r.table[start : start + size, :size]
        base = 8 * size

        def vector(k):
            return jnp.concatenate(
                [r.table[base + k : base + k + 1, :], r.table[base + 8 + k : base + 9 + k, : features - 128]], axis=1
            )

        for k, target in enumerate((r.bias_in, r.bias_in, r.bias_out, r.bias_out)):
            value = vector(k)
            target[k % 2, 0:1, :] = value[:, :size]
            target[k % 2, 1:2, :] = value[:, size:]
        r.pre_gain[...] = vector(4)
        r.pre_shift[...] = vector(5)
        r.upb[...] = jnp.concatenate(
            [r.table[small + k : small + k + 1, :] for k in range(local // 128)], axis=1
        ).reshape(local)
        for k, target in enumerate((r.post_gain, r.post_shift, r.downb)):
            target[...] = jnp.concatenate(
                [
                    r.table[small + 8 + 2 * k : small + 9 + 2 * k, :],
                    r.table[small + 9 + 2 * k : small + 10 + 2 * k, : features - 128],
                ],
                axis=1,
            )
        moves.open = moves.open[len(waiting) :]
        moves.close()

    return launch(
        body,
        {
            **{key: parts[key] for key in ("a_full", "a_other", "b_full", "b_other")},
            **{key + "_in": value for key, value in fields.items()},
        },
        {
            "down": ((local, width), F32),
            "up": ((width, local), F32),
            "mix_in": ((2, 2, size, size), F32),
            "mix_out": ((2, 2, size, size), F32),
            "bias_in": ((2, 2, size), F32),
            "bias_out": ((2, 2, size), F32),
            "pre_gain": ((1, features), F32),
            "pre_shift": ((1, features), F32),
            "post_gain": ((1, features), F32),
            "post_shift": ((1, features), F32),
            "downb": ((1, features), F32),
            "upb": ((local,), F32),
            **{key: plan.lines for key in fields},
        },
        {
            "table": pltpu.VMEM((part * levels, 128), F32),
            "down_made": pltpu.VMEM((local, width), F32),
            "up_made": pltpu.VMEM((width, local), F32),
            "dma": sems(16),
            **{key + "_held": scratch_of(plan.lines) for key in fields},
        },
        "unpack_gradients",
        None,
        {key + "_in": IN_PLACE for key in fields},
        {key: IN_PLACE for key in ("down", "up", *fields)},
    )


def shards_fast(
    current_atmosphere,
    truth_one,
    truth_two,
    storm_codes,
    pre_gain,
    pre_shift,
    mix_weight_in,
    mix_bias_in,
    mix_weight_out,
    mix_bias_out,
    post_gain,
    post_shift,
    up_weight,
    up_bias,
    down_weight,
    down_bias,
):
    rows, merged = current_atmosphere.shape[1:]
    columns = W
    features = merged // columns
    plan = Plan(
        rows, features, columns, lax.axis_size("space"), lax.axis_size("chan"), up_weight.shape[1]
    )
    forward, inverse = row_constants(columns)
    column = column_constants(rows * plan.spaces, rows, 2)
    tables = {
        "row": jnp.stack(const_halves(forward)),
        "rowinv": const_halves(inverse)[0],
        "rowinv_t": const_halves(inverse.T)[0],
        "row_t": const_halves(forward.T)[0],
        "col": jnp.stack(const_halves(column)),
        "colinv": const_halves(column.T)[0],
    }

    def lines(flat):
        return flat.reshape(rows, merged // 128, 128)

    def flat(line_field):
        return line_field.reshape(1, rows, merged)

    one = launch_first(
        plan,
        {
            "lines_x": lines(current_atmosphere),
            "lines_t": lines(truth_one),
            "gain": pre_gain,
            "shift": pre_shift,
            "mix_in": mix_weight_in,
            "bias_in": mix_bias_in,
            "mix_out": mix_weight_out,
            "bias_out": mix_bias_out,
            "post_gain": post_gain,
            "post_shift": post_shift,
            "up": up_weight,
            "upb": up_bias,
            "down": down_weight,
            "downb": down_bias,
        },
        tables,
    )
    two = launch_second(
        plan,
        {"gain": pre_gain, "shift": pre_shift, "lines_t": lines(truth_two), "codes": storm_codes},
        one,
        tables,
    )
    three = launch_third(plan, {"gain": pre_gain}, one, two, tables)
    grads = unpack_gradients(
        plan, three, {"first": two["lines"], "second": three["lines_x"], "state": three["lines_out"]}
    )
    return (
        flat(grads["first"]),
        flat(grads["second"]),
        flat(grads["state"]),
        grads["pre_gain"].reshape(features),
        grads["pre_shift"].reshape(features),
        grads["mix_in"],
        grads["bias_in"],
        grads["mix_out"],
        grads["bias_out"],
        grads["post_gain"].reshape(features),
        grads["post_shift"].reshape(features),
        grads["up"],
        grads["upb"],
        grads["down"],
        grads["downb"].reshape(features),
    )


def suits(mesh):
    spaces, chans = mesh.shape["space"], mesh.shape["chan"]
    return (spaces, chans) == (8, 4)


def solution(mesh):
    in_specs = (
        P(None, "space", "chan"),
        P(None, "space", "chan"),
        P(None, "space", "chan"),
        P(),
        P("chan"),
        P("chan"),
        P(None, "chan", None, None),
        P(None, "chan", None),
        P(None, "chan", None, None),
        P(None, "chan", None),
        P("chan"),
        P("chan"),
        P(None, "chan"),
        P("chan"),
        P("chan", None),
        P("chan"),
    )
    out_specs = (
        P(None, "space", "chan"),
        P(None, "space", "chan"),
        P(None, "space", "chan"),
        P("chan"),
        P("chan"),
        P(None, "chan", None, None),
        P(None, "chan", None),
        P(None, "chan", None, None),
        P(None, "chan", None),
        P("chan"),
        P("chan"),
        P(None, "chan"),
        P("chan"),
        P("chan", None),
        P("chan"),
    )
    return jax.shard_map(shards_fast if suits(mesh) else shards, mesh=mesh, in_specs=in_specs, out_specs=out_specs, check_vma=False)
```

```python
import functools
import math
import types

import jax
import jax.numpy as jnp
import ml_dtypes
import numpy as np
from jax import lax
from jax.experimental import pallas as pl
from jax.experimental.pallas import tpu as pltpu
from jax.sharding import PartitionSpec as P

W = 160
KW = 81


NORM_EPS = 1e-06
SHRINK_LEVEL = 0.01
FULL_PRECISION = lax.Precision.HIGHEST


def exact_gelu(values):
    return jax.nn.gelu(values, approximate=False)


def shrink(values):
    return values - jnp.clip(values, -SHRINK_LEVEL, SHRINK_LEVEL)


def block_mix(values, matrix):
    return jnp.einsum("bhkni,nio->bhkno", values, matrix, precision=FULL_PRECISION)


def row_tables(columns, kept_modes, padded_modes):
    places = jnp.arange(columns, dtype=jnp.int32)[:, None]
    orders = jnp.arange(padded_modes, dtype=jnp.int32)[None, :]
    angles = 2.0 * math.pi / columns * (places * orders % columns).astype(jnp.float32)
    factor = 1.0 / math.sqrt(columns)
    single = jnp.logical_or(orders == 0, 2 * orders == columns)
    doubled = jnp.where(single, 1.0, 2.0).astype(jnp.float32)
    used = jnp.where(orders < kept_modes, 1.0, 0.0).astype(jnp.float32)
    return (
        jnp.cos(angles) * factor * used,
        -jnp.sin(angles) * factor * used,
        jnp.transpose(jnp.cos(angles) * doubled * factor * used),
        jnp.transpose(jnp.sin(angles) * doubled * factor * used),
    )


def along_rows(values, tables):
    return jnp.stack(
        [
            jnp.einsum("bhwc,wk->bhkc", values, tables[0], precision=FULL_PRECISION),
            jnp.einsum("bhwc,wk->bhkc", values, tables[1], precision=FULL_PRECISION),
        ]
    )


def along_rows_back(paired, tables):
    return jnp.einsum("bhkc,wk->bhwc", paired[0], tables[0], precision=FULL_PRECISION) + jnp.einsum(
        "bhkc,wk->bhwc", paired[1], tables[1], precision=FULL_PRECISION
    )


def rows_inverse(paired, tables):
    return jnp.einsum("bhkc,kw->bhwc", paired[0], tables[2], precision=FULL_PRECISION) - jnp.einsum(
        "bhkc,kw->bhwc", paired[1], tables[3], precision=FULL_PRECISION
    )


def rows_inverse_back(values, tables):
    return jnp.stack(
        [
            jnp.einsum("bhwc,kw->bhkc", values, tables[2], precision=FULL_PRECISION),
            -jnp.einsum("bhwc,kw->bhkc", values, tables[3], precision=FULL_PRECISION),
        ]
    )


def column_tables(height):
    orders = jnp.arange(height, dtype=jnp.int32)[:, None]
    places = jnp.arange(height, dtype=jnp.int32)[None, :]
    angles = 2.0 * math.pi / height * (orders * places % height).astype(jnp.float32)
    factor = 1.0 / math.sqrt(height)
    return (jnp.cos(angles) * factor, jnp.sin(angles) * factor)


def to_freq(matrix, values):
    return jnp.einsum("kh,bhmc->bkmc", matrix, values, precision=FULL_PRECISION)


def from_freq(matrix, values):
    return jnp.einsum("kh,bkmc->bhmc", matrix, values, precision=FULL_PRECISION)


def spectral_core(paired, w_first, b_first, w_second, b_second):
    samples, height, kept_modes, channels = paired.shape[1:]
    blocks, block_size = (w_first.shape[1], w_first.shape[2])
    cosine, sine_table = column_tables(height)
    real_in, imag_in = (paired[0], paired[1])
    split_form = (samples, height, kept_modes, blocks, block_size)
    real_part = (to_freq(cosine, real_in) + to_freq(sine_table, imag_in)).reshape(split_form)
    imag_part = (to_freq(cosine, imag_in) - to_freq(sine_table, real_in)).reshape(split_form)
    first_real = jax.nn.relu(
        block_mix(real_part, w_first[0]) - block_mix(imag_part, w_first[1]) + b_first[0]
    )
    first_imag = jax.nn.relu(
        block_mix(imag_part, w_first[0]) + block_mix(real_part, w_first[1]) + b_first[1]
    )
    joined_form = (samples, height, kept_modes, channels)
    second_real = shrink(
        block_mix(first_real, w_second[0]) - block_mix(first_imag, w_second[1]) + b_second[0]
    ).reshape(joined_form)
    second_imag = shrink(
        block_mix(first_imag, w_second[0]) + block_mix(first_real, w_second[1]) + b_second[1]
    ).reshape(joined_form)
    out_real = from_freq(cosine, second_real) - from_freq(sine_table, second_imag)
    out_imag = from_freq(cosine, second_imag) + from_freq(sine_table, second_real)
    return jnp.stack([out_real, out_imag])


def column_layout(paired):
    return lax.all_to_all(paired, "space", split_axis=3, concat_axis=2, tiled=True)


def row_layout(paired):
    return lax.all_to_all(
        paired.astype(jnp.bfloat16), "space", split_axis=2, concat_axis=3, tiled=True
    ).astype(paired.dtype)


def norm_forward(values, gain, offset):
    width_all = values.shape[-1] * lax.axis_size("chan")
    totals = lax.psum((jnp.sum(values, axis=-1), jnp.sum(values * values, axis=-1)), "chan")
    average = totals[0] / width_all
    variance = totals[1] / width_all - average * average
    inverse_dev = lax.rsqrt(variance + NORM_EPS)[..., None]
    scaled = (values - average[..., None]) * inverse_dev
    return (scaled * gain + offset, (scaled, inverse_dev))


def norm_backward(gradient, gain, saved):
    scaled, inverse_dev = saved
    width_all = scaled.shape[-1] * lax.axis_size("chan")
    scaled_grad = gradient * gain
    totals = lax.psum(
        (jnp.sum(scaled_grad, axis=-1), jnp.sum(scaled_grad * scaled, axis=-1)), "chan"
    )
    values_grad = inverse_dev * (
        scaled_grad - totals[0][..., None] / width_all - scaled * (totals[1][..., None] / width_all)
    )
    return (
        values_grad,
        jnp.sum(gradient * scaled, axis=(0, 1, 2)),
        jnp.sum(gradient, axis=(0, 1, 2)),
    )


def shards(
    current_atmosphere,
    truth_one,
    truth_two,
    storm_codes,
    pre_gain,
    pre_shift,
    mix_weight_in,
    mix_bias_in,
    mix_weight_out,
    mix_bias_out,
    post_gain,
    post_shift,
    up_weight,
    up_bias,
    down_weight,
    down_bias,
):
    samples, rows_here, merged = current_atmosphere.shape
    columns = W
    channels = merged // columns
    total_rows = samples * rows_here * columns
    space_count = lax.axis_size("space")
    padded_modes = (KW + space_count - 1) // space_count * space_count
    tables = row_tables(columns, KW, padded_modes)

    def to_cells(flat_field):
        return jnp.transpose(
            flat_field.reshape(samples, rows_here, channels, columns), (0, 1, 3, 2)
        )

    def to_flat(cell_field):
        return jnp.transpose(cell_field, (0, 1, 3, 2)).reshape(samples, rows_here, merged)

    start_cells = to_cells(current_atmosphere)
    target_one = to_cells(truth_one)
    target_two = to_cells(truth_two)
    weight_of = (storm_codes.astype(jnp.float32) / 64.0).reshape(-1, 1, 1, 1)
    full_up, full_down, full_up_bias, full_down_bias = (up_weight, down_weight, up_bias, down_bias)

    def mlp_forward(inputs):
        gathered = lax.all_gather(inputs, "chan", axis=1, tiled=True)
        hidden = jnp.dot(
            gathered, full_up, preferred_element_type=jnp.float32
        ) + full_up_bias.astype(jnp.float32)
        active_full, gelu_pull = jax.vjp(exact_gelu, hidden)
        active = active_full.astype(jnp.bfloat16)
        product = jnp.dot(active, full_down, preferred_element_type=jnp.float32)
        output = lax.psum_scatter(
            product.astype(jnp.bfloat16), "chan", scatter_dimension=1, tiled=True
        ).astype(jnp.float32) + full_down_bias.astype(jnp.float32)
        return (output, (gathered, gelu_pull, active))

    def mlp_backward(gradient, saved):
        gathered, gelu_pull, active = saved
        grad_low = gradient.astype(jnp.bfloat16)
        grad_rows = lax.all_gather(grad_low, "chan", axis=1, tiled=True)
        down_bias_grad = jnp.sum(grad_low.astype(jnp.float32), axis=0)
        down_grad = jnp.dot(active.T, grad_rows, preferred_element_type=jnp.float32)
        active_grad = jnp.dot(grad_rows, full_down.T, preferred_element_type=jnp.float32)
        hidden_grad = gelu_pull(active_grad)[0].astype(jnp.bfloat16)
        up_grad = jnp.dot(gathered.T, hidden_grad, preferred_element_type=jnp.float32)
        up_bias_grad = jnp.sum(hidden_grad.astype(jnp.float32), axis=0)
        input_part = jnp.dot(hidden_grad, full_up.T, preferred_element_type=jnp.float32)
        input_grad = lax.psum_scatter(
            input_part.astype(jnp.bfloat16), "chan", scatter_dimension=1, tiled=True
        ).astype(jnp.float32)
        return (input_grad, (up_grad, up_bias_grad, down_grad, down_bias_grad))

    def forward_block(values):
        normed, first_saved = norm_forward(values, pre_gain, pre_shift)
        modal_in = column_layout(along_rows(normed, tables))
        filtered, core_pull = jax.vjp(
            spectral_core, modal_in, mix_weight_in, mix_bias_in, mix_weight_out, mix_bias_out
        )
        middle = rows_inverse(row_layout(filtered), tables) + normed + values
        entry, second_residuals = norm_forward(middle, post_gain, post_shift)
        output, mlp_saved = mlp_forward(entry.astype(jnp.bfloat16).reshape(total_rows, channels))
        return (
            output.reshape(values.shape) + middle,
            (first_saved, core_pull, second_residuals, mlp_saved),
        )

    def backward_block(gradient, saved):
        first_saved, core_pull, second_residuals, mlp_saved = saved
        mlp_grad, dense_grads = mlp_backward(gradient.reshape(total_rows, channels), mlp_saved)
        middle_part, post_gain_grad, post_shift_grad = norm_backward(
            mlp_grad.reshape(gradient.shape), post_gain, second_residuals
        )
        middle_grad = middle_part + gradient
        filter_grads = core_pull(column_layout(rows_inverse_back(middle_grad, tables)))
        normed_grad = along_rows_back(row_layout(filter_grads[0]), tables) + middle_grad
        input_part, pre_gain_grad, pre_shift_grad = norm_backward(
            normed_grad, pre_gain, first_saved
        )
        return (
            input_part + middle_grad,
            (pre_gain_grad, pre_shift_grad)
            + tuple(filter_grads[1:])
            + (post_gain_grad, post_shift_grad)
            + dense_grads,
        )

    first_out, first_saved_all = forward_block(start_cells)
    second_out, second_saved_all = forward_block(first_out)
    carried, grads_late = backward_block(weight_of * (second_out - target_two), second_saved_all)
    input_grad, grads_early = backward_block(
        weight_of * (first_out - target_one) + carried, first_saved_all
    )
    summed = jax.tree.map(jnp.add, grads_early, grads_late)
    (
        sum_pre_gain,
        sum_pre_shift,
        sum_mix_w_in,
        summed_mixing_bias_input,
        sum_mix_w_out,
        sum_mix_b_out,
        sum_post_gain,
        sum_post_shift,
        sum_up,
        sum_up_bias,
        sum_down,
        sum_down_bias,
    ) = summed
    totals = (
        lax.psum(sum_pre_gain.astype(jnp.bfloat16), "space").astype(jnp.float32),
        lax.psum(sum_pre_shift.astype(jnp.bfloat16), "space").astype(jnp.float32),
        lax.psum(sum_mix_w_in.astype(jnp.bfloat16), "space").astype(jnp.float32),
        lax.psum(summed_mixing_bias_input.astype(jnp.bfloat16), "space").astype(jnp.float32),
        lax.psum(sum_mix_w_out.astype(jnp.bfloat16), "space").astype(jnp.float32),
        lax.psum(sum_mix_b_out.astype(jnp.bfloat16), "space").astype(jnp.float32),
        lax.psum(sum_post_gain.astype(jnp.bfloat16), "space").astype(jnp.float32),
        lax.psum(sum_post_shift.astype(jnp.bfloat16), "space").astype(jnp.float32),
        lax.psum(sum_up.astype(jnp.bfloat16), "space").astype(jnp.float32),
        lax.psum(sum_up_bias.astype(jnp.bfloat16), "space").astype(jnp.float32),
        lax.psum(sum_down.astype(jnp.bfloat16), "space").astype(jnp.float32),
        lax.psum(sum_down_bias.astype(jnp.bfloat16), "space").astype(jnp.float32),
    )
    return (to_flat(first_out), to_flat(second_out), to_flat(input_grad)) + tuple(totals)


BF = jnp.bfloat16
F32 = jnp.float32
MESH_ID = pl.DeviceIdType.MESH
VMEM_BYTES = 66 * 1024 * 1024 - 1024 * 1024


def mm(a, b):
    return jnp.dot(a, b, preferred_element_type=F32)


def mm_nt(a, b):
    return lax.dot_general(a, b, (((1,), (1,)), ((), ())), preferred_element_type=F32)


def mm_tn(a, b):
    return lax.dot_general(a, b, (((0,), (0,)), ((), ())), preferred_element_type=F32)


def halves(v):
    high = v.astype(BF)
    return high, (v - high.astype(F32)).astype(BF)


def mm3(a, b):
    return mm(a[0], b[0]) + (mm(a[0], b[1]) + mm(a[1], b[0]))


def const_halves(table):
    table = np.asarray(table, np.float32)
    high = table.astype(ml_dtypes.bfloat16)
    low = (table - high.astype(np.float32)).astype(ml_dtypes.bfloat16)
    return jnp.asarray(high), jnp.asarray(low)


def row_constants(columns):
    half = columns // 2
    place = np.arange(columns)
    mode = np.arange(half)
    angle = 2.0 * np.pi * np.outer(mode, place) / columns
    real = np.cos(angle)
    imag = -np.sin(angle)
    imag[0] = np.cos(np.pi * place)
    forward = np.concatenate([real, imag]) / np.sqrt(columns)
    weight = np.where(mode == 0, 1.0, 2.0)
    inverse = (forward * np.concatenate([weight, weight])[:, None]).T
    return forward, inverse


def column_constants(height, rows, group):
    owners = height // rows
    angle = 2.0 * np.pi * np.outer(np.arange(height), np.arange(height)) / height
    cosine = np.cos(angle) / np.sqrt(height)
    sine = np.sin(angle) / np.sqrt(height)

    def spread(matrix):
        wide = np.zeros((group, height, owners, group, rows))
        for column in range(group):
            wide[column, :, :, column, :] = matrix.reshape(height, owners, rows)
        return wide.reshape(group * height, owners * group * rows)

    cosine, sine = spread(cosine), spread(sine)
    return np.block([[cosine, sine], [-sine, cosine]])


def partner(me, count, step):
    flip = (count - step) % count
    result, bit = 0, 1
    while bit < count:
        digit = lax.rem(me // bit, 2)
        result += bit * (1 - digit if flip // bit % 2 else digit)
        bit *= 2
    return result


def signal_peers(axis, count, barrier):
    me = lax.axis_index(axis)
    for step in range(1, count):
        pl.semaphore_signal(
            barrier, inc=1, device_id={axis: lax.rem(me + step, count)}, device_id_type=MESH_ID
        )


def push(axis, count, step, source, target, send_sem, recv_sem):
    peer = lax.rem(lax.axis_index(axis) + step, count)
    return pltpu.make_async_remote_copy(
        src_ref=source,
        dst_ref=target,
        send_sem=send_sem.at[step],
        recv_sem=recv_sem.at[step],
        device_id={axis: peer},
        device_id_type=MESH_ID,
    )


def params(collective_id=None):
    return pltpu.CompilerParams(
        collective_id=collective_id,
        has_side_effects=collective_id is not None,
        vmem_limit_bytes=VMEM_BYTES,
    )


def launch(body, ins, outs, scratch, name, collective_id=None, in_specs=None, out_specs=None, grid=()):
    in_specs, out_specs = in_specs or {}, out_specs or {}
    names = list(ins) + list(outs) + list(scratch)
    whole = pl.BlockSpec(memory_space=pltpu.VMEM)
    results = pl.pallas_call(
        lambda *refs: body(types.SimpleNamespace(**dict(zip(names, refs)))),
        grid=grid,
        in_specs=[in_specs.get(key, whole) for key in ins],
        out_specs=[out_specs.get(key, whole) for key in outs],
        out_shape=[jax.ShapeDtypeStruct(*outs[key]) for key in outs],
        scratch_shapes=list(scratch.values()),
        compiler_params=params(collective_id),
        name=name,
    )(*ins.values())
    return dict(zip(outs, results))


IN_PLACE = pl.BlockSpec(memory_space=pl.ANY)


def sems(*counts):
    return pltpu.SemaphoreType.DMA(counts)


def run_copies(copies):
    for copy in copies:
        copy.start()
    for copy in copies:
        copy.wait()


def cells_from_lines(lines_ref, h, scratch_ref):
    features = scratch_ref.shape[1]
    per = 640 // W
    groups = features // per
    wide = jnp.concatenate(
        [lines_ref[h, pl.ds(part, groups, stride=5), :] for part in range(5)], axis=1
    )
    for part in range(per):
        piece = wide[:, part * W : (part + 1) * W]
        scratch_ref[0, pl.ds(part, groups, stride=per), :] = piece[:, :128]
        scratch_ref[1, pl.ds(part, groups, stride=per), :] = jnp.concatenate(
            [piece[:, 128:], jnp.zeros((groups, 256 - W), F32)], axis=1
        )
    return jnp.concatenate([scratch_ref[0], scratch_ref[1][:, : W - 128]], axis=1)


def enter(lines_ref, cells_ref, scratch_ref):
    def row(h, carry):
        cells_ref[h] = cells_from_lines(lines_ref, h, scratch_ref).T
        return carry

    lax.fori_loop(0, lines_ref.shape[0], row, 0)


def leave(cells_ref, lines_ref, scratch_ref):
    features = scratch_ref.shape[1]
    per = 640 // W
    groups = features // per

    def row(h, carry):
        block = cells_ref[h].T
        scratch_ref[0] = block[:, :128]
        scratch_ref[1] = jnp.concatenate([block[:, 128:], jnp.zeros((features, 256 - W), F32)], axis=1)
        wide = jnp.concatenate(
            [
                piece
                for part in range(per)
                for piece in (
                    scratch_ref[0, pl.ds(part, groups, stride=per), :],
                    scratch_ref[1, pl.ds(part, groups, stride=per), :][:, : W - 128],
                )
            ],
            axis=1,
        )
        for part in range(5):
            lines_ref[h, pl.ds(part, groups, stride=5), :] = wide[:, part * 128 : (part + 1) * 128]
        return carry

    lax.fori_loop(0, lines_ref.shape[0], row, 0)


def pack_lanes(flat_ref, place, real, imag):
    flat_ref[0, place, :] = real[:, :128]
    flat_ref[1, place, :] = imag[:, :128]
    flat_ref[2, place, :] = jnp.concatenate([real[:, 128:], imag[:, 128:]], axis=1)


def join_lanes(first, second, rest):
    real = jnp.concatenate([first, rest[:, :64]], axis=1)
    imag = jnp.concatenate([second, rest[:, 64:]], axis=1)
    return real, imag


def unpack_lanes(flat_ref, place):
    return join_lanes(flat_ref[0, place, :], flat_ref[1, place, :], flat_ref[2, place, :])


LEVEL = 32000.0


class Exchange:
    def __init__(self, fixed, spaces, thick, send_ref, recv_ref, send_sem, recv_sem, scales=None):
        self.fixed, self.scales = fixed, scales
        self.spaces, self.thick = spaces, thick
        self.send_ref, self.recv_ref = send_ref, recv_ref
        self.send_sem, self.recv_sem = send_sem, recv_sem
        self.me = lax.axis_index("space")

    @staticmethod
    def shape(fixed, spaces, thick, pairs):
        return pltpu.VMEM((pairs, spaces, 3 * thick, 128), jnp.int16 if fixed else BF)

    def copy(self, p, step):
        peer = partner(self.me, self.spaces, step)
        return pltpu.make_async_remote_copy(
            src_ref=self.send_ref.at[p, peer],
            dst_ref=self.recv_ref.at[p, self.me],
            send_sem=self.send_sem.at[p, step],
            recv_sem=self.recv_sem.at[p, step],
            device_id={"space": peer},
            device_id_type=MESH_ID,
        )

    def scale_copy(self, step):
        own_ref, all_ref, send_sem, recv_sem = self.scales
        return push("space", self.spaces, step, own_ref, all_ref.at[self.me], send_sem, recv_sem)

    def send_scales(self, flat_ref):
        own_ref, all_ref = self.scales[:2]
        largest = jnp.max(jnp.abs(flat_ref[...]), axis=1)
        own_ref[0:3, :] = jnp.maximum(largest, 1e-30) * (1.0 / LEVEL)
        own_ref[3:8, :] = jnp.ones((5, 128), F32)
        for step in range(1, self.spaces):
            self.scale_copy(step).start()
        all_ref[self.me] = own_ref[...]
        self.factor = 1.0 / own_ref[...]

    def encode(self, values):
        if not self.fixed:
            return jnp.concatenate([values[k] for k in range(3)], axis=0).astype(BF)
        lines = [jnp.round(values[k] * self.factor[k : k + 1]) for k in range(3)]
        return jnp.concatenate(lines, axis=0).astype(jnp.int32).astype(jnp.int16)

    def send(self, p, flat_ref, start_of):
        for step in list(range(1, self.spaces)) + [0]:
            peer = partner(self.me, self.spaces, step)
            rows = pl.ds(pl.multiple_of(start_of(peer), 8), self.thick)
            coded = self.encode(flat_ref[:, rows, :])
            if step:
                self.send_ref[p, peer] = coded
                self.copy(p, step).start()
            else:
                self.recv_ref[p, peer] = coded

    def arrive(self, p):
        for step in range(1, self.spaces):
            self.copy(p, step).wait_recv()

    def arrive_scales(self):
        for step in range(1, self.spaces):
            self.scale_copy(step).wait_recv()

    def take(self, p, source):
        coded = self.recv_ref[p, source]
        values = (coded.astype(jnp.int32) if self.fixed else coded).astype(F32)
        parts = [values[k * self.thick : (k + 1) * self.thick] for k in range(3)]
        if self.fixed:
            scale = self.scales[1][source]
            parts = [part * scale[k : k + 1] for k, part in enumerate(parts)]
        return parts

    def close(self, pairs):
        def pair(p, carry):
            for step in range(1, self.spaces):
                self.copy(p, step).wait_send()
            return carry

        lax.fori_loop(0, pairs, pair, 0)
        if self.fixed:
            for step in range(1, self.spaces):
                self.scale_copy(step).wait_send()


def pair_inputs(q, exchange, even_ref):
    p = jnp.maximum(q - 1, 0)

    @pl.when(q != 1)
    def _():
        exchange.arrive(p)

    if exchange.fixed:

        @pl.when(q == 0)
        def _():
            exchange.arrive_scales()

    extra = (q == 0).astype(F32)
    zeroth = jnp.logical_and(exchange.me == 0, p == 0).astype(F32)
    parts = [join_lanes(*exchange.take(p, s)) for s in range(exchange.spaces)]
    real = jnp.concatenate([part[0] for part in parts], axis=0)
    imag = jnp.concatenate([part[1] for part in parts], axis=0)
    chosen = imag * (even_ref[...] * zeroth)
    real = real * (1.0 - extra) + chosen * extra
    imag = (imag - chosen) * (1.0 - extra)
    return p, zeroth, jnp.concatenate([real, imag], axis=0)


def pair_outputs(q, p, zeroth, result, exchange, even_ref, kept_ref, stage_ref):
    half = result.shape[0] // 2
    real, imag = result[:half], result[half:]

    @pl.when(q == 0)
    def _():
        kept_ref[...] = real

    @pl.when(q > 0)
    def _():
        chosen = even_ref[...] * zeroth
        pack_lanes(stage_ref, slice(None), real, imag * (1.0 - chosen) + kept_ref[...] * chosen)
        exchange.send(p, stage_ref, lambda peer: peer * exchange.thick)


def collect(exchange, pairs, chunk, flat_ref):
    def pair(p, carry):
        exchange.arrive(p)
        for s in range(exchange.spaces):
            rows = pl.ds(pl.multiple_of(s * chunk + p * exchange.thick, 8), exchange.thick)
            for k, part in enumerate(exchange.take(p, s)):
                flat_ref[k, rows, :] = part
        return carry

    lax.fori_loop(0, pairs, pair, 0)


def send_modes(exchange, pairs, chunk, flat_ref):
    if exchange.fixed:
        exchange.send_scales(flat_ref)

    def pair(p, carry):
        exchange.send(p, flat_ref, lambda peer: peer * chunk + p * exchange.thick)
        return carry

    lax.fori_loop(0, pairs, pair, 0)


class Plan:
    def __init__(self, rows, features, columns, spaces, chans, local):
        self.rows, self.features, self.columns = rows, features, columns
        self.spaces, self.chans, self.local = spaces, chans, local
        self.modes = columns // 2
        self.total = self.modes * rows
        self.chunk = self.total // spaces
        self.thick = 2 * rows
        self.half = self.thick * spaces
        self.pairs = self.chunk // self.thick
        self.cells = rows * columns // chans
        self.share = rows // chans
        self.width = features * chans
        self.tile = 256
        self.per = local // self.tile
        self.steps = chans * self.per
        self.size = features // 2
        self.small = 8 * self.size + 16
        self.field = ((rows, columns, features), F32)
        self.by_cells = ((chans, self.share, columns // 2 * 3, 128), BF)
        self.wide = ((self.cells, self.width), BF)
        self.tiles = ((self.steps, self.cells, self.tile), BF)
        self.lines = ((rows, features * columns // 128, 128), F32)
        self.dev = ((-(-rows // 8) * 8, columns), F32)
        self.dev_wide = ((self.cells, 128), F32)
        self.kept = ((self.pairs + 1, 2 * self.half, features), BF)
        self.mix = ((2, 2, 2, features, features), BF)
        self.weights = ((2, chans, local, self.width), BF)
        self.rest = ((chans, 8, local), F32)
        self.sums = ((self.small, 128), F32)
        self.grads = ((2, self.steps, self.tile, self.width), BF)
        self.vectors = ((chans, 8, local), F32)

    def exchange_scratch(self, fixed_there, fixed_back):
        made = {}
        for name, fixed in (("1", fixed_there), ("2", fixed_back)):
            shape = Exchange.shape(fixed, self.spaces, self.thick, self.pairs)
            made["send" + name] = made["recv" + name] = shape
            made["s" + name] = made["r" + name] = sems(self.pairs, self.spaces)
        if fixed_there:
            made["scale"] = pltpu.VMEM((8, 128), F32)
            made["scale_all"] = pltpu.VMEM((self.spaces, 8, 128), F32)
            made["s20"] = made["r20"] = sems(self.spaces)
        return made

    def spectral_scratch(self):
        return {
            "flat": pltpu.VMEM((3, self.total, 128), F32),
            "stage": pltpu.VMEM((3, self.half, 128), F32),
            "last": pltpu.VMEM((self.half, self.features), F32),
            "turn": pltpu.VMEM((2, self.features, 128), F32),
            "even": pltpu.VMEM((self.half, self.features), F32),
        }


def pack_cells(value):
    side = value.shape[0] // 2
    rest = value[:, 128:]
    return jnp.concatenate([value[:, :128], jnp.concatenate([rest[:side], rest[side:]], axis=1)], axis=0)


def unpack_cells(packed):
    columns = packed.shape[0] // 3 * 2
    rest = packed[columns:]
    rest = jnp.concatenate([rest[:, :64], rest[:, 64:]], axis=0)
    return jnp.concatenate([packed[:columns], rest], axis=1)


def three_parts(v):
    a = v.astype(BF)
    rest = v - a.astype(F32)
    b = rest.astype(BF)
    return [a, b, (rest - b.astype(F32)).astype(BF)]


def stack_rows(rows):
    lines = [part.astype(F32) for row in rows for part in three_parts(row)]
    lines.append(jnp.zeros((16 - len(lines), rows[0].shape[1]), F32))
    return jnp.concatenate(lines, axis=0).astype(BF)


def over_lanes(table, features, number):
    line = lax.broadcasted_iota(jnp.int32, (16, features), 0)
    chosen = jnp.logical_and(line >= 3 * number, line < 3 * number + 3)
    return mm_tn(table, jnp.where(chosen, 1.0, 0.0).astype(BF))


def lane_sums(value):
    return mm_nt(jnp.ones((16, value.shape[1]), BF), value.astype(BF))[0:1]


def scratch_of(shaped):
    return pltpu.VMEM(*shaped)


def mark_even(plan, r):
    row = lax.broadcasted_iota(jnp.int32, (plan.half, plan.features), 0)
    r.even[...] = jnp.where(lax.rem(lax.div(row, plan.rows), 2) == 0, 1.0, 0.0)


def greet(plan):
    barrier = pltpu.get_barrier_semaphore()
    signal_peers("space", plan.spaces, barrier)
    signal_peers("chan", plan.chans, barrier)
    return lambda: pl.semaphore_wait(barrier, plan.spaces + plan.chans - 2)


def spread_chan(plan, source_ref, target_ref, send_sem, recv_sem):
    me = lax.axis_index("chan")
    copies = []
    for step in range(1, plan.chans):
        peer = lax.rem(me + step, plan.chans)
        copy = push("chan", plan.chans, step, source_ref.at[peer], target_ref.at[me], send_sem, recv_sem)
        copy.start()
        copies.append(copy)
    target_ref[me] = source_ref[me]
    return copies


def wait_all(copies):
    for copy in copies:
        copy.wait()


def rows_to_modes(plan, table, flat_ref, value_of, exact):
    def row(h, carry):
        value = value_of(h)
        out = mm3(table, halves(value)) if exact else mm(table, value.astype(BF))
        pack_lanes(flat_ref, pl.ds(h, plan.modes, stride=plan.rows), out[: plan.modes], out[plan.modes :])
        return carry

    lax.fori_loop(0, plan.rows, row, 0, unroll=4)


def filter_forward(plan, r, there, back, aside=None):
    half = plan.half

    def filter_pair(q, carry):
        if aside is not None:
            pl.when(q == plan.pairs)(aside)
        p, zeroth, block = pair_inputs(q, there, r.even)
        spec = mm3((r.col[0], r.col[1]), halves(block))
        r.spec[q] = spec.astype(BF)
        parts = halves(spec)
        straight = mm3(parts, (r.mix[0, 0, 0], r.mix[0, 0, 1]))
        crossed = mm3(parts, (r.mix[0, 1, 0], r.mix[0, 1, 1]))
        first = jnp.concatenate(
            [
                jnp.maximum(straight[:half] - crossed[half:] + r.bias[0:1], 0.0),
                jnp.maximum(straight[half:] + crossed[:half] + r.bias[1:2], 0.0),
            ],
            axis=0,
        )
        r.first[q] = first.astype(BF)
        parts = halves(first)
        straight = mm3(parts, (r.mix[1, 0, 0], r.mix[1, 0, 1]))
        crossed = mm3(parts, (r.mix[1, 1, 0], r.mix[1, 1, 1]))
        second = jnp.concatenate(
            [
                straight[:half] - crossed[half:] + r.bias[2:3],
                straight[half:] + crossed[:half] + r.bias[3:4],
            ],
            axis=0,
        )
        second = second - jnp.clip(second, -SHRINK_LEVEL, SHRINK_LEVEL)
        r.second[q] = second.astype(BF)
        result = mm(r.colinv[...], r.second[q])
        pair_outputs(q, p, zeroth, result, back, r.even, r.last, r.stage)
        return carry

    lax.fori_loop(0, plan.pairs + 1, filter_pair, 0)


def modes_to_rows(plan, flat_ref, h):
    real, imag = unpack_lanes(flat_ref, pl.ds(h, plan.modes, stride=plan.rows))
    return jnp.concatenate([real, imag], axis=0)


def rows_of_chunks(plan, row, send_chunk):
    me = lax.axis_index("chan")
    for step in list(range(1, plan.chans)) + [0]:
        peer = lax.rem(me + step, plan.chans)

        def one(i, carry):
            row(peer * plan.share + i, peer, i)
            return carry

        lax.fori_loop(0, plan.share, one, 0, unroll=True)
        send_chunk(step, peer)


def rows_forward(plan, r, unit_ref, x_ref, middle_ref):
    me = lax.axis_index("chan")
    gain, shift = r.gain[...].reshape(1, -1), r.shift[...].reshape(1, -1)
    copies = []

    def row(h, peer, place):
        block = modes_to_rows(plan, r.flat, h)
        out = mm(r.rowinv[...], block.astype(BF))
        middle = out + (unit_ref[h] * gain + shift) + x_ref[h]
        middle_ref[h] = middle
        r.own[peer, place] = pack_cells(middle).astype(BF)

    def send_chunk(step, peer):
        if step:
            copy = push("chan", plan.chans, step, r.own.at[peer], r.mid.at[me], r.s3, r.r3)
            copy.start()
            copies.append(copy)
        else:
            r.mid[me] = r.own[me]

    rows_of_chunks(plan, row, send_chunk)
    return copies


class Block:
    def __init__(self, plan, group, side):
        self.group, self.side, self.size = group, side, plan.columns // 2
        start = group * plan.columns + side * self.size
        self.cells = pl.ds(pl.multiple_of(start, 16), self.size)
        self.front = slice(side * self.size, (side + 1) * self.size)
        self.back = slice(plan.columns, plan.columns + self.size)
        self.lanes = slice(64 * side, 64 * side + 64)

    def get(self, chunks_ref):
        parts = []
        for j in range(chunks_ref.shape[0]):
            parts.append(chunks_ref[j, self.group, self.front, :].astype(F32))
            parts.append(chunks_ref[j, self.group, self.back, self.lanes].astype(F32))
        return jnp.concatenate(parts, axis=1)

    def put(self, chunks_ref, value):
        chans = chunks_ref.shape[0]
        features = value.shape[1] // chans
        for j in range(chans):
            part = value[:, j * features : (j + 1) * features].astype(BF)
            chunks_ref[j, self.group, self.front, :] = part[:, :128]
            chunks_ref[j, self.group, self.back, self.lanes] = part[:, 128:]


def by_blocks(plan, step):
    def one(group, carry):
        for side in range(2):
            step(Block(plan, group, side))
        return carry

    lax.fori_loop(0, plan.share, one, 0, unroll=True)


def full_vector(gathered_ref, start, size):
    chans = gathered_ref.shape[0]
    return jnp.concatenate([gathered_ref[j, 1:2, start : start + size] for j in range(chans)], axis=1)


def moments(value):
    mean = jnp.mean(value, axis=1, keepdims=True)
    centred = value - mean
    return mean, centred, lax.rsqrt(jnp.mean(centred * centred, axis=1, keepdims=True) + NORM_EPS)


ERF = (0.254829592, -0.284496736, 1.421413741, -1.453152027, 1.061405429)


def gelu_and_slope(v):
    e = jnp.exp2(v * v * (-0.5 / math.log(2.0)))
    below = 1.0 + (0.3275911 * math.sqrt(0.5)) * jnp.abs(v)
    t = pl.reciprocal(below, approx=True)
    t = t * (2.0 - below * t)
    c = [0.5 * k for k in ERF]
    tail = (e * t) * (c[0] + t * (c[1] + t * (c[2] + t * (c[3] + t * c[4]))))
    below = jnp.where(v >= 0.0, 1.0 - tail, tail)
    active = v * below
    return active, below + (v * (1.0 / math.sqrt(2.0 * math.pi))) * e


def tile_of(plan, t):
    return t // plan.per, pl.ds(pl.multiple_of((t % plan.per) * plan.tile, plan.tile), plan.tile)


def up_tile(plan, r, t):
    j, place = tile_of(plan, t)
    return r.w[0, j, :, place]


def down_tile(plan, r, t):
    j, place = tile_of(plan, t)
    return r.w[1, j, place, :]


def ffn_scratch(plan):
    shape = (plan.cells, plan.tile)
    made = {key: pltpu.VMEM(shape, F32) for key in ("wide_a", "wide_b")}
    made.update({key: pltpu.VMEM(shape, BF) for key in ("thin_a", "thin_b")})
    made.update(
        total=pltpu.VMEM((plan.cells, plan.width), F32),
        entry=scratch_of(plan.wide),
        unit_wide=scratch_of(plan.wide),
        dev_wide=scratch_of(plan.dev_wide),
        active=scratch_of(plan.tiles),
        slope=scratch_of(plan.tiles),
        gathered=scratch_of(plan.vectors),
    )
    return made


def staggered(plan, r, lead, turn, trail, ready=None):
    last = plan.steps - 1
    third = plan.cells // 3
    side = plan.cells // 2
    parts = plan.width // plan.tile
    r.thin_b[...] = jnp.zeros_like(r.thin_b)
    for k in range(2):
        r.wide_a[k * side : (k + 1) * side, :] = lead(0, slice(k * side, (k + 1) * side))

    def half_step(t, wide_now, wide_next, thin_past, thin_now):
        ahead, behind = jnp.minimum(t + 1, last), jnp.maximum(t - 1, 0)
        for k in range(3):
            place = slice(k * third, (k + 1) * third)
            thin_now[place, :] = turn(wide_now[place, :], t, place, k == 0)
            if k < 2:
                own = slice(k * side, (k + 1) * side)
                wide_next[own, :] = lead(ahead, own)
            trail(thin_past[...], behind, slice(k * parts // 3 * plan.tile, (k + 1) * parts // 3 * plan.tile))

    def pair(u, carry):
        if ready is not None:
            for chunk in range(1, plan.chans):
                pl.when(u == (chunk * plan.per - 1) // 2)(functools.partial(ready, chunk))
        half_step(2 * u, r.wide_a, r.wide_b, r.thin_b, r.thin_a)
        half_step(2 * u + 1, r.wide_b, r.wide_a, r.thin_a, r.thin_b)
        return carry

    lax.fori_loop(0, plan.steps // 2, pair, 0)
    trail(r.thin_b[...], last, slice(0, plan.width))


def ffn_forward(plan, r):
    gain = full_vector(r.gathered, 0, plan.features)
    shift = full_vector(r.gathered, plan.features, plan.features)
    bias = full_vector(r.gathered, 2 * plan.features, plan.features)

    def prepare(block):
        place = block.cells
        mean, centred, inverse = moments(block.get(r.mid))
        unit = centred * inverse
        r.unit_wide[place, :] = unit.astype(BF)
        r.dev_wide[place, :] = jnp.broadcast_to(inverse, (block.size, 128))
        r.entry[place, :] = (unit * gain + shift).astype(BF)
        r.total[place, :] = jnp.broadcast_to(bias, (block.size, plan.width))

    by_blocks(plan, prepare)

    def lead(t, rows):
        j, place = tile_of(plan, t)
        return mm(r.entry[rows, :], up_tile(plan, r, t)) + r.gathered[j, 0:1, place]

    def turn(value, t, rows, opening):
        active, slope = gelu_and_slope(value)
        active = active.astype(BF)
        r.active[t, rows, :] = active
        r.slope[t, rows, :] = slope.astype(BF)
        return active

    def trail(active, t, lanes):
        j, place = tile_of(plan, t)
        r.total[:, lanes] += mm(active, r.w[1, j, place, lanes])

    staggered(plan, r, lead, turn, trail)


def ffn_backward(plan, r, ready=None):
    r.small[...] = jnp.zeros_like(r.small)
    r.total[...] = jnp.zeros_like(r.total)

    def lead(t, rows):
        return mm_nt(r.upper[rows, :], down_tile(plan, r, t))

    def turn(value, t, rows, opening):
        lower = value * r.slope[t, rows, :].astype(F32)
        bias = jnp.sum(lower, axis=0, keepdims=True)
        r.upb[pl.ds(t, 1), :] = bias if opening else r.upb[pl.ds(t, 1), :] + bias
        lower = lower.astype(BF)
        r.slope[t, rows, :] = lower
        return lower

    def trail(lower, t, lanes):
        j, place = tile_of(plan, t)
        r.total[:, lanes] += mm_nt(lower, r.w[0, j, lanes, place])

    staggered(plan, r, lead, turn, trail, ready)
    gain = full_vector(r.gathered, 0, plan.features)

    def finish(block):
        place = block.cells
        grad = r.total[place, :]
        unit = r.unit_wide[place, :].astype(F32)
        r.small[0:1, :] += jnp.sum(grad * unit, axis=0, keepdims=True)
        r.small[1:2, :] += jnp.sum(grad, axis=0, keepdims=True)
        r.small[2:3, :] += jnp.sum(r.upper[place, :].astype(F32), axis=0, keepdims=True)
        scaled = grad * gain
        one = jnp.mean(scaled, axis=1, keepdims=True)
        two = jnp.mean(scaled * unit, axis=1, keepdims=True)
        result = r.dev_wide[place, :][:, :1] * (scaled - one - unit * two)
        block.put(r.leaving, result)

    by_blocks(plan, finish)


def vector_gradients(plan, r, rest_ref):
    rest_ref[...] = jnp.zeros_like(rest_ref)
    for j in range(plan.chans):
        for k in range(plan.per):
            line = j * plan.per + k
            rest_ref[j, 0:1, k * plan.tile : (k + 1) * plan.tile] = r.upb[line : line + 1, :]
        for k in range(3):
            rest_ref[j, 1 + k : 2 + k, 0 : plan.features] = r.small[
                k : k + 1, j * plan.features : (j + 1) * plan.features
            ]


def weight_gradients(r, t):
    return mm_tn(r.active[t], r.upper[...]), mm_tn(r.slope[t], r.entry[...])


def filter_backward(plan, r, there, back, aside=None):
    half = plan.half
    r.mixgrad[...] = jnp.zeros_like(r.mixgrad)
    r.biasgrad[...] = jnp.zeros_like(r.biasgrad)

    def turned(v):
        return jnp.concatenate([v[half:], -v[:half]], axis=0)

    def note_bias(index, value):
        r.biasgrad[index : index + 1, :] += jnp.sum(value, axis=0, keepdims=True)

    def through(low, layer):
        straight = mm_nt(low, r.mix[layer, 0, 0])
        crossed = mm_nt(low, r.mix[layer, 1, 0])
        return jnp.concatenate([straight[:half] + crossed[half:], straight[half:] - crossed[:half]], axis=0)

    def filter_pair(q, carry):
        if aside is not None:
            pl.when(q == 3)(aside)
        p, zeroth, block = pair_inputs(q, there, r.even)
        grad = mm(r.col[0], block.astype(BF))
        grad = jnp.where(r.second[q].astype(F32) == 0.0, 0.0, grad)
        note_bias(2, grad[:half])
        note_bias(3, grad[half:])
        low = grad.astype(BF)
        first = r.first[q]
        r.mixgrad[1, 0] += mm_tn(first, low)
        r.mixgrad[1, 1] += mm_tn(first, turned(grad).astype(BF))
        grad = jnp.where(first.astype(F32) > 0.0, through(low, 1), 0.0)
        note_bias(0, grad[:half])
        note_bias(1, grad[half:])
        low = grad.astype(BF)
        spec = r.spec[q]
        r.mixgrad[0, 0] += mm_tn(spec, low)
        r.mixgrad[0, 1] += mm_tn(spec, turned(grad).astype(BF))
        result = mm(r.colinv[...], through(low, 0).astype(BF))
        pair_outputs(q, p, zeroth, result, back, r.even, r.last, r.stage)
        return carry

    lax.fori_loop(0, plan.pairs + 1, filter_pair, 0)


def mix_gradients(plan, r, before_ref):
    size = plan.size
    for layer in range(2):
        for part in range(2):
            for block in range(2):
                own = slice(block * size, (block + 1) * size)
                piece = r.mixgrad[layer, part][own, own]
                piece = jnp.concatenate([piece, jnp.zeros((size, 128 - size), F32)], axis=1)
                start = ((layer * 2 + part) * 2 + block) * size
                place = slice(start, start + size)
                r.sums[place, :] = piece if before_ref is None else piece + before_ref[place, :]


def rows_backward(plan, r, unit_ref, before_ref):
    gain = r.gain[...].reshape(1, -1)
    me = lax.axis_index("chan")

    def row(h, carry):
        one_sum, two_sum = carry
        block = modes_to_rows(plan, r.flat, h)
        grad = mm(r.row_t[...], block.astype(BF)) + r.out[h]
        unit = unit_ref[h]
        one_sum += jnp.sum(grad * unit, axis=0, keepdims=True)
        two_sum += jnp.sum(grad, axis=0, keepdims=True)
        scaled = grad * gain
        r.scaled[h] = scaled
        r.mine[pl.ds(h, 1), :] = lane_sums(scaled)
        r.mine[pl.ds(plan.rows + h, 1), :] = lane_sums(scaled * unit)
        return one_sum, two_sum

    none = jnp.zeros((1, plan.features), F32)
    one_sum, two_sum = lax.fori_loop(0, plan.rows, row, (none, none), unroll=4)
    r.all[me] = r.mine[...]
    copies = [
        push("chan", plan.chans, step, r.mine, r.all.at[me], r.s4, r.r4) for step in range(1, plan.chans)
    ]
    for copy in copies:
        copy.start()
    vectors = jnp.concatenate([r.biasgrad[0:4], one_sum, two_sum, none, none], axis=0)
    wide = jnp.concatenate([vectors, jnp.zeros((8, 256 - plan.features), F32)], axis=1)
    wide = jnp.concatenate([wide[:, :128], wide[:, 128:]], axis=0)
    place = slice(8 * plan.size, plan.small)
    r.sums[place, :] = wide if before_ref is None else wide + before_ref[place, :]
    return copies


def input_gradient(plan, r, unit_ref, dev_ref):
    r.mine[...] = sum(r.all[j] for j in range(plan.chans)) * (1.0 / plan.width)

    def result(h):
        table = stack_rows(
            [r.mine[pl.ds(h, 1), :], r.mine[pl.ds(plan.rows + h, 1), :], dev_ref[pl.ds(h, 1), :]]
        )
        one, two, dev = [over_lanes(table, plan.features, k) for k in range(3)]
        return r.out[h] + dev * (r.scaled[h] - one - unit_ref[h] * two)

    return result


def norm_sums_scratch(plan):
    return {
        "scaled": scratch_of(plan.field),
        "mixgrad": pltpu.VMEM((2, 2, plan.features, plan.features), F32),
        "biasgrad": pltpu.VMEM((8, plan.features), F32),
        "mine": pltpu.VMEM((2 * plan.rows, plan.columns), F32),
        "all": pltpu.VMEM((plan.chans, 2 * plan.rows, plan.columns), F32),
        "s4": sems(plan.chans),
        "r4": sems(plan.chans),
    }


class Moves:
    def __init__(self, sem):
        self.sem, self.count, self.open = sem, 0, []

    def start(self, source, target):
        copy = pltpu.make_async_copy(source, target, self.sem.at[self.count])
        self.count += 1
        copy.start()
        self.open.append(copy)
        return copy

    def close(self):
        wait_all(self.open)


def launch_first(plan, args, tables):
    rows, features, chans = plan.rows, plan.features, plan.chans

    def body(r):
        me = lax.axis_index("chan")
        place = lax.axis_index("space")
        core = lax.rem(place, 2)
        sibling = place + 1 - 2 * core
        met = greet(plan)
        moves = Moves(r.dma)
        moves.start(r.up, r.w.at[0, me])
        moves.start(r.down, r.w.at[1, me])
        loaded = moves.start(r.lines_t, r.lines_in)
        own_weights = moves.open[:2]
        moves.open = []

        beside = me + 1 - 2 * lax.rem(me, 2)
        across = me + 2 - 4 * (me // 2)
        far = chans - 1 - me
        upper_half, lower_half = pl.ds(0, plan.local // 2), pl.ds(plan.local // 2, plan.local // 2)

        def hand(source, target, number, device):
            return pltpu.make_async_remote_copy(
                src_ref=source,
                dst_ref=target,
                send_sem=r.s5.at[number],
                recv_sem=r.r5.at[number],
                device_id=device,
                device_id_type=MESH_ID,
            )

        def own_to(number, source):
            peer = (beside, across)[number]
            return hand(source, r.w.at[core, me], number, {"chan": peer})

        def relay(number):
            slot = (beside, across)[number]
            part = r.w.at[core, slot, (upper_half, lower_half)[number]]
            return hand(part, part, 2 + number, {"chan": (across, beside)[number]})

        def to_core(number):
            if number < 2:
                part = r.w.at[core, (beside, across)[number]]
            else:
                part = r.w.at[core, far]
            return pltpu.make_async_remote_copy(
                src_ref=part,
                dst_ref=part,
                send_sem=r.s7.at[number],
                recv_sem=r.r7.at[number],
                device_id={"space": sibling},
                device_id_type=MESH_ID,
            )

        def pass_near():
            for number in range(2):
                own_to(number, r.up).wait_recv()
            for number in range(2):
                relay(number).start()
            for number in range(2):
                to_core(number).start()

        def pass_far():
            for number in range(2):
                relay(number).wait_recv()
            to_core(2).start()

        def close_weights():
            for number in range(2):
                own_to(number, r.up).wait_send()
                relay(number).wait_send()
            for number in range(3):
                to_core(number).wait()

        def first(h, carry):
            block = cells_from_lines(r.lines_x, h, r.turn)
            r.turned[h] = block
            total = jnp.sum(block, axis=0, keepdims=True)
            centred = block - total * (1.0 / features)
            r.mine[pl.ds(h, 1), :] = total
            r.mine[pl.ds(rows + h, 1), :] = jnp.sum(centred * centred, axis=0, keepdims=True)
            return carry

        lax.fori_loop(0, rows, first, 0)
        r.all[me] = r.mine[...]
        met()
        sums = [push("chan", chans, step, r.mine, r.all.at[me], r.s4, r.r4) for step in range(1, chans)]
        for copy in sums:
            copy.start()
        mark_even(plan, r)

        def row_of(ref):
            return ref[...].reshape(1, -1).astype(F32)

        r.vectors[...] = jnp.zeros_like(r.vectors)
        r.vectors[0:1, :] = row_of(r.upb)
        r.vectors[1:2, 0:features] = row_of(r.post_gain)
        r.vectors[1:2, features : 2 * features] = row_of(r.post_shift)
        r.vectors[1:2, 2 * features : 3 * features] = row_of(r.downb)
        r.gathered[me] = r.vectors[...]
        for layer, (source, bias) in enumerate(((r.mix_in, r.bias_in), (r.mix_out, r.bias_out))):
            for part in range(2):
                zero = jnp.zeros((plan.size, plan.size), F32)
                value = jnp.concatenate(
                    [
                        jnp.concatenate([source[part, 0], zero], axis=1),
                        jnp.concatenate([zero, source[part, 1]], axis=1),
                    ],
                    axis=0,
                )
                high, low = halves(value)
                r.mix[layer, part, 0] = high
                r.mix[layer, part, 1] = low
                line = 2 * layer + part
                r.bias[line : line + 1, :] = jnp.concatenate([bias[part, 0:1, :], bias[part, 1:2, :]], axis=1)
        moves.start(r.mix, r.mix_kept)


        def turn_row(h, carry):
            r.x[h] = r.turned[h].T
            return carry

        lax.fori_loop(0, rows, turn_row, 0, unroll=2)
        wait_all(sums)
        given = [push("chan", chans, step, r.vectors, r.gathered.at[me], r.s6, r.r6) for step in range(1, chans)]
        for copy in given:
            copy.start()
        for kind, source in enumerate((r.up, r.down)):

            @pl.when(core == kind)
            def _():
                for number in range(2):
                    own_to(number, source).start()

        totals = [r.all[j] for j in range(chans)]
        mean = sum(t[:rows] for t in totals) * (1.0 / plan.width)
        spread_sum = sum(
            t[rows:] + features * jnp.square(t[:rows] * (1.0 / features) - mean) for t in totals
        ) * (1.0 / plan.width)
        r.mine[pl.ds(0, rows), :] = mean
        r.mine[pl.ds(rows, rows), :] = lax.rsqrt(spread_sum + NORM_EPS)
        gain, shift = r.gain[...].reshape(1, -1), r.shift[...].reshape(1, -1)

        def normed(h):
            inverse = r.mine[pl.ds(rows + h, 1), :]
            table = stack_rows([r.mine[pl.ds(h, 1), :], inverse])
            unit = (r.x[h] - over_lanes(table, features, 0)) * over_lanes(table, features, 1)
            r.unit[h] = unit
            r.dev[pl.ds(h, 1), :] = inverse
            return unit * gain + shift

        scales = (r.scale, r.scale_all, r.s20, r.r20)
        there = Exchange(True, plan.spaces, plan.thick, r.send1, r.recv1, r.s1, r.r1, scales)
        back = Exchange(False, plan.spaces, plan.thick, r.send2, r.recv2, r.s2, r.r2)
        rows_to_modes(plan, (r.row[0], r.row[1]), r.flat, normed, True)
        send_modes(there, plan.pairs, plan.chunk, r.flat)
        moves.start(r.unit, r.unit_kept)
        moves.start(r.dev, r.dev_kept)
        loaded.wait()
        enter(r.lines_in, r.cells_t, r.turn)
        moves.start(r.cells_t, r.cells_kept)
        filter_forward(plan, r, there, back, pass_near)
        for source, target in ((r.spec, r.spec_kept), (r.first, r.first_kept), (r.second, r.second_kept)):
            moves.start(source, target)
        collect(back, plan.pairs, plan.chunk, r.flat)
        pass_far()
        copies = rows_forward(plan, r, r.unit, r.x, r.middle)
        moves.start(r.middle, r.middle_kept)
        wait_all(copies + given)
        close_weights()
        wait_all(own_weights)
        moves.start(r.w, r.w_kept)
        ffn_forward(plan, r)
        saved = ("active", "slope", "entry", "unit_wide", "dev_wide", "gathered")
        for key in saved:
            moves.start(getattr(r, key), getattr(r, key + "_kept"))

        def last(block):
            outer = r.total[block.cells, :]
            mean, _, inverse = moments(outer + block.get(r.mid))
            block.put(r.leaving, outer)
            r.stats[block.group, block.front, :] = jnp.concatenate(
                three_parts(mean) + three_parts(inverse) + [jnp.zeros((block.size, 122), BF)], axis=1
            )

        by_blocks(plan, last)
        copies = spread_chan(plan, r.leaving, r.home, r.s8, r.r8)
        for group in range(plan.share):
            r.stats_thin[group] = r.stats[group].astype(F32).T[:16].astype(BF)
        others = [
            push("chan", chans, step, r.stats_thin, r.stats_home.at[me], r.s9, r.r9) for step in range(1, chans)
        ]
        for copy in others:
            copy.start()
        r.stats_home[me] = r.stats_thin[...]
        wait_all(copies + others)
        there.close(plan.pairs)
        back.close(plan.pairs)
        moves.close()

    stats = ((chans, plan.share, 16, plan.columns), BF)
    outs = {
        "home": plan.by_cells,
        "stats_home": stats,
        "middle_kept": plan.field,
        "unit_kept": plan.field,
        "dev_kept": plan.dev,
        "cells_kept": plan.field,
        "spec_kept": plan.kept,
        "first_kept": plan.kept,
        "second_kept": plan.kept,
        "mix_kept": plan.mix,
        "w_kept": plan.weights,
        "active_kept": plan.tiles,
        "slope_kept": plan.tiles,
        "entry_kept": plan.wide,
        "unit_wide_kept": plan.wide,
        "dev_wide_kept": plan.dev_wide,
        "gathered_kept": plan.vectors,
        "bias": ((8, features), F32),
    }
    ins = dict(args)
    ins.update({key: tables[key] for key in ("row", "rowinv", "col", "colinv")})
    scratch = {
        "dma": sems(20),
        "x": scratch_of(plan.field),
        "unit": scratch_of(plan.field),
        "dev": scratch_of(plan.dev),
        "middle": scratch_of(plan.field),
        "cells_t": scratch_of(plan.field),
        "lines_in": scratch_of(plan.lines),
        "turned": pltpu.VMEM((rows, features, plan.columns), F32),
        "mine": pltpu.VMEM((2 * rows, plan.columns), F32),
        "all": pltpu.VMEM((chans, 2 * rows, plan.columns), F32),
        "spec": scratch_of(plan.kept),
        "first": scratch_of(plan.kept),
        "second": scratch_of(plan.kept),
        "mix": scratch_of(plan.mix),
        "w": scratch_of(plan.weights),
        "vectors": pltpu.VMEM((8, plan.local), F32),
        "own": scratch_of(plan.by_cells),
        "mid": scratch_of(plan.by_cells),
        "leaving": scratch_of(plan.by_cells),
        "stats": pltpu.VMEM((plan.share, plan.columns, 128), BF),
        "stats_thin": pltpu.VMEM(stats[0][1:], BF),
        **plan.exchange_scratch(True, False),
        **plan.spectral_scratch(),
        **ffn_scratch(plan),
        **{key + str(k): sems(chans) for k in range(3, 10) for key in ("s", "r")},
    }
    in_place = ("up", "down", "lines_t")
    return launch(
        body,
        ins,
        outs,
        scratch,
        "first_forward",
        0,
        {key: IN_PLACE for key in in_place},
        {key: IN_PLACE for key in outs if key.endswith("_kept")},
    )


def launch_second(plan, args, one, tables):
    rows, features, chans = plan.rows, plan.features, plan.chans

    def body(r):
        me = lax.axis_index("chan")
        met = greet(plan)
        mark_even(plan, r)
        moves = Moves(r.dma)
        loaded = moves.start(r.lines_t, r.lines_in)
        weights = moves.start(r.w_kept, r.w)
        vectors = moves.start(r.gathered_kept, r.gathered)
        earlier = moves.start(r.cells_kept, r.cells_one)
        held = [
            moves.start(r.col_kept, r.col),
            moves.start(r.mix_kept, r.mix),
            moves.start(r.colinv_kept, r.colinv),
        ]
        moves.open = []
        gain, shift = r.gain[...].reshape(1, -1), r.shift[...].reshape(1, -1)
        weight = r.codes[0].astype(F32) * (1.0 / 64.0)

        def normed(h):
            quarter, inside = h // plan.share, h % plan.share
            x = unpack_cells(r.home[quarter, inside].astype(F32)) + r.before[h]
            table = r.stats_home[quarter, inside]
            unit = (x - over_lanes(table, features, 0)) * over_lanes(table, features, 1)
            r.x[h] = x
            r.unit[h] = unit
            r.dev[pl.ds(h, 1), :] = jnp.sum(table[3:6].astype(F32), axis=0, keepdims=True)
            return unit * gain + shift

        rows_to_modes(plan, (r.row[0], r.row[1]), r.flat, normed, True)
        met()
        scales = (r.scale, r.scale_all, r.s20, r.r20)
        there = Exchange(True, plan.spaces, plan.thick, r.send1, r.recv1, r.s1, r.r1, scales)
        back = Exchange(False, plan.spaces, plan.thick, r.send2, r.recv2, r.s2, r.r2)
        send_modes(there, plan.pairs, plan.chunk, r.flat)
        loaded.wait()
        enter(r.lines_in, r.cells_t, r.turn)

        def low_target(h, peer, place):
            r.own[peer, place] = pack_cells(r.cells_t[h]).astype(BF)

        targets = []

        def send_target(step, peer):
            if step:
                copy = push("chan", chans, step, r.own.at[peer], r.target.at[me], r.s5, r.r5)
                copy.start()
                targets.append(copy)
            else:
                r.target[me] = r.own[me]

        rows_of_chunks(plan, low_target, send_target)
        wait_all(held)
        filter_forward(plan, r, there, back)
        collect(back, plan.pairs, plan.chunk, r.flat)
        there.close(plan.pairs)
        back.close(plan.pairs)
        wait_all(targets)
        copies = rows_forward(plan, r, r.unit, r.x, r.before)
        weights.wait()
        vectors.wait()
        wait_all(copies)
        ffn_forward(plan, r)

        def errors(block):
            outer = r.total[block.cells, :]
            error = outer + block.get(r.mid) - block.get(r.target)
            r.upper[block.cells, :] = (weight * error).astype(BF)
            block.put(r.leaving, outer)

        by_blocks(plan, errors)
        copies = spread_chan(plan, r.leaving, r.landed, r.s6, r.r6)
        for copy in copies:
            copy.wait_send()
        ffn_backward(plan, r)
        for copy in copies:
            copy.wait_recv()
        copies = spread_chan(plan, r.leaving, r.own, r.s7, r.r7)

        def grads(u, carry):
            for slot in range(2):
                t = 2 * u + slot
                stores = [
                    pltpu.make_async_copy(r.grad.at[slot, k], r.grads_kept.at[k, t], r.dma2.at[slot, k])
                    for k in range(2)
                ]

                @pl.when(u > 0)
                def _():
                    wait_all(stores)

                for k, value in enumerate(weight_gradients(r, t)):
                    r.grad[slot, k] = value.astype(BF)
                    stores[k].start()
            return carry

        lax.fori_loop(0, plan.steps // 2, grads, 0)
        vector_gradients(plan, r, r.rest)
        wait_all(copies)

        def middle_grad(h):
            quarter, inside = h // plan.share, h % plan.share
            x = unpack_cells(r.landed[quarter, inside].astype(F32)) + r.before[h]
            r.before[h] = x
            grad = weight * (x - r.cells_t[h]) + unpack_cells(r.own[quarter, inside].astype(F32))
            r.out[h] = grad
            return grad

        rows_to_modes(plan, r.rowinv_t[...], r.flat, middle_grad, False)
        there = Exchange(False, plan.spaces, plan.thick, r.send3, r.recv3, r.s3_, r.r3_)
        back = Exchange(False, plan.spaces, plan.thick, r.send2, r.recv2, r.s2, r.r2)
        send_modes(there, plan.pairs, plan.chunk, r.flat)
        moves.start(r.before, r.second_x)
        leave(r.x, r.lines_in, r.turn)
        moves.start(r.lines_in, r.lines)
        filter_backward(plan, r, there, back)
        mix_gradients(plan, r, None)
        collect(back, plan.pairs, plan.chunk, r.flat)
        copies = rows_backward(plan, r, r.unit, None)
        earlier.wait()
        wait_all(copies)
        result = input_gradient(plan, r, r.unit, r.dev)
        copies = []

        def row(h, peer, place):
            grad = weight * (r.x[h] - r.cells_one[h]) + result(h)
            r.out[h] = grad
            r.own[peer, place] = pack_cells(grad).astype(BF)

        def send_chunk(step, peer):
            some = pl.ds(peer * plan.share, plan.share)
            moves.start(r.out.at[some], r.out_kept.at[some])
            if step:
                copy = push("chan", chans, step, r.own.at[peer], r.came.at[me], r.s8, r.r8)
                copy.start()
                copies.append(copy)
            else:
                r.came[me] = r.own[me]

        rows_of_chunks(plan, row, send_chunk)
        for slot in range(2):
            for k in range(2):
                pltpu.make_async_copy(
                    r.grad.at[slot, k], r.grads_kept.at[k, plan.steps - 2 + slot], r.dma2.at[slot, k]
                ).wait()
        wait_all(copies)
        there.close(plan.pairs)
        back.close(plan.pairs)
        moves.close()

    ins = {
        "home": one["home"],
        "stats_home": one["stats_home"],
        "before": one["middle_kept"],
        "w_kept": one["w_kept"],
        "gathered_kept": one["gathered_kept"],
        "cells_kept": one["cells_kept"],
        "mix_kept": one["mix_kept"],
        "bias": one["bias"],
        **args,
    }
    ins.update({key: tables[key] for key in ("row", "rowinv", "rowinv_t", "row_t")})
    ins.update(col_kept=tables["col"], colinv_kept=tables["colinv"])
    outs = {
        "out_kept": plan.field,
        "came": plan.by_cells,
        "lines": plan.lines,
        "second_x": plan.field,
        "sums": plan.sums,
        "rest": plan.rest,
        "grads_kept": plan.grads,
    }
    exchange = Exchange.shape(False, plan.spaces, plan.thick, plan.pairs)
    scratch = {
        "dma": sems(16),
        "out": scratch_of(plan.field),
        "mix": scratch_of(plan.mix),
        "col": pltpu.VMEM(tables["col"].shape, BF),
        "colinv": pltpu.VMEM(tables["colinv"].shape, BF),
        "dma2": sems(2, 2),
        "x": scratch_of(plan.field),
        "unit": scratch_of(plan.field),
        "dev": scratch_of(plan.dev),
        "cells_t": scratch_of(plan.field),
        "cells_one": scratch_of(plan.field),
        "lines_in": scratch_of(plan.lines),
        "spec": scratch_of(plan.kept),
        "first": scratch_of(plan.kept),
        "second": scratch_of(plan.kept),
        "w": scratch_of(plan.weights),
        "own": scratch_of(plan.by_cells),
        "mid": scratch_of(plan.by_cells),
        "target": scratch_of(plan.by_cells),
        "leaving": scratch_of(plan.by_cells),
        "landed": scratch_of(plan.by_cells),
        "upper": scratch_of(plan.wide),
        "small": pltpu.VMEM((8, plan.width), F32),
        "upb": pltpu.VMEM((16, plan.tile), F32),
        "grad": pltpu.VMEM((2, 2, plan.tile, plan.width), BF),
        "send3": exchange,
        "recv3": exchange,
        "s3_": sems(plan.pairs, plan.spaces),
        "r3_": sems(plan.pairs, plan.spaces),
        **plan.exchange_scratch(True, False),
        **plan.spectral_scratch(),
        **ffn_scratch(plan),
        **norm_sums_scratch(plan),
        **{key + str(k): sems(chans) for k in (3, 5, 6, 7, 8) for key in ("s", "r")},
    }
    in_specs = {key: IN_PLACE for key in ins if key.endswith("_kept") or key == "lines_t"}
    in_specs["codes"] = pl.BlockSpec(memory_space=pltpu.SMEM)
    return launch(
        body,
        ins,
        outs,
        scratch,
        "second_step",
        1,
        in_specs,
        {key: IN_PLACE for key in ("second_x", "grads_kept", "lines", "out_kept")},
    )


def launch_third(plan, args, one, two, tables):
    rows, features, chans, spaces = plan.rows, plan.features, plan.chans, plan.spaces
    local, width = plan.local, plan.width
    levels = spaces // 2
    piece = local // levels
    small = plan.small
    part = -(-(small + 32) // (16 * levels)) * 16

    def body(r):
        me = lax.axis_index("chan")
        place = lax.axis_index("space")
        core = lax.rem(place, 2)
        level = place // 2
        sibling = place + 1 - 2 * core
        others = [lax.rem(level + step, levels) for step in range(1, levels)]
        met = greet(plan)
        mark_even(plan, r)
        moves = Moves(r.dma)
        early = [
            moves.start(source, target)
            for source, target in (
                (r.gathered_kept, r.gathered),
                (r.unit_wide_kept, r.unit_wide),
                (r.dev_wide_kept, r.dev_wide),
            )
        ]
        chunks = []
        for j in range(chans):
            tiles = pl.ds(j * plan.per, plan.per)
            chunks.append(
                [
                    moves.start(r.w_kept.at[1, j], r.w.at[1, j]),
                    moves.start(r.slope_kept.at[tiles], r.slope.at[tiles]),
                    moves.start(r.w_kept.at[0, j], r.w.at[0, j]),
                ]
            )
        middle = [moves.start(r.active_kept, r.active), moves.start(r.entry_kept, r.entry)]
        moves.open = []

        def upper(block):
            r.upper[block.cells, :] = block.get(r.came).astype(BF)

        by_blocks(plan, upper)
        wait_all(early)
        wait_all(chunks[0])
        ffn_backward(plan, r, lambda chunk: wait_all(chunks[chunk]))
        late = [
            moves.start(source, target)
            for source, target in (
                (r.g, r.out),
                (r.unit_kept, r.unit),
                (r.spec_kept, r.spec),
                (r.first_kept, r.first),
                (r.second_kept, r.second),
                (r.dev_kept, r.dev),
                (r.mix_kept, r.mix),
                (r.col_kept, r.col),
                (r.colinv_kept, r.colinv),
            )
        ]
        moves.open = []
        met()
        copies = spread_chan(plan, r.leaving, r.own, r.s7, r.r7)
        vector_gradients(plan, r, r.rest)
        r.rest[...] += r.rest_before[...]
        vectors = [
            push("chan", chans, step, r.rest.at[lax.rem(me + step, chans)], r.rest_land.at[me], r.s6, r.r6)
            for step in range(1, chans)
        ]
        for copy in vectors:
            copy.start()
        r.rest_land[me] = r.rest[me]
        wait_all(middle)

        column, line = lax.rem(me, 2), me // 2
        beside = me + 1 - 2 * column
        across = me + 2 - 4 * line
        near, under = pl.ds(0, plan.tile // 2), pl.ds(plan.tile // 2, plan.tile // 2)

        def order(i):
            k = i // plan.per
            owner_column = column + (1 - k // 2) * (1 - 2 * column)
            owner_line = line + (1 - k % 2) * (1 - 2 * line)
            return (2 * owner_line + owner_column) * plan.per + i % plan.per

        def fetch(i, k):
            return pltpu.make_async_copy(r.grads_kept.at[k, order(i)], r.prev.at[i % 2, k], r.dma2.at[i % 2, k])

        def swap(i):
            return pltpu.make_async_remote_copy(
                src_ref=r.give.at[i % 2],
                dst_ref=r.take.at[i % 3],
                send_sem=r.s9.at[i],
                recv_sem=r.r9.at[i],
                device_id={"space": sibling},
                device_id_type=MESH_ID,
            )

        def to_chan(source, target, sem, number, device):
            return pltpu.make_async_remote_copy(
                src_ref=source,
                dst_ref=target,
                send_sem=sem[0].at[number],
                recv_sem=sem[1].at[number],
                device_id={"chan": device},
                device_id_type=MESH_ID,
            )

        def ship_near(i):
            target = r.land_near.at[i // plan.per, i % plan.per]
            return to_chan(r.keep.at[i, near], target, (r.s10, r.r10), i, beside)

        def ship_under(j):
            i = j + (j // plan.per) * plan.per
            target = r.land_under.at[j // plan.per, j % plan.per]
            return to_chan(r.keep.at[i, under], target, (r.s17, r.r17), j, across)

        def on_across(k):
            return to_chan(
                r.keep.at[2 * plan.per + k, near], r.land_on.at[0, k], (r.s18, r.r18), k, across
            )

        def on_beside(k):
            return to_chan(
                r.keep.at[plan.per + k, under], r.land_on.at[1, k], (r.s18, r.r18), plan.per + k, beside
            )

        def pass_on():
            def tile(k, carry):
                for arrived, land, start, part, onward in (
                    (ship_near, r.land_near, 2 * plan.per, near, on_across),
                    (ship_under, r.land_under, plan.per, under, on_beside),
                ):
                    arrived(k).wait_recv()
                    value = r.keep[start + k, part, :].astype(F32) + land[0, k].astype(F32)
                    r.keep[start + k, part, :] = value.astype(BF)
                    onward(k).start()
                return carry

            lax.fori_loop(0, plan.per, tile, 0)

        for k in range(2):
            fetch(0, k).start()

        def settle(i):
            swap(i).wait()
            r.keep[i] = (r.keep[i].astype(F32) + r.take[i % 3].astype(F32)).astype(BF)

        shipped = plan.steps - plan.per

        def leave_block(i):
            settle(i)

            @pl.when(i < 2 * plan.per)
            def _():
                ship_near(i).start()

            @pl.when(i < plan.per)
            def _():
                ship_under(i).start()

            @pl.when(i >= 2 * plan.per)
            def _():
                ship_under(i - plan.per).start()

        def make_block(i, before):
            for k in range(2):
                fetch(i, k).wait()

            @pl.when(i + 1 < plan.steps)
            def _():
                for k in range(2):
                    fetch(i + 1, k).start()

            values = [
                (value + r.prev[i % 2, k].astype(F32)).astype(BF)
                for k, value in enumerate(weight_gradients(r, order(i)))
            ]
            before(i)
            for kind in range(2):

                @pl.when(core == kind)
                def _():
                    r.keep[i] = values[kind]
                    r.give[i % 2] = values[1 - kind]

            swap(i).start()

        def others_block(i, carry):
            make_block(i, lambda i: pl.when(i > 0)(lambda: leave_block(i - 1)))
            return carry

        def own_block(i, carry):
            make_block(i, lambda i: pl.when(i > shipped)(lambda: settle(i - 1)))
            return carry

        lax.fori_loop(0, shipped, others_block, 0)
        leave_block(shipped - 1)
        wait_all(copies)
        wait_all(late)

        def middle_grad(h):
            quarter, inside = h // plan.share, h % plan.share
            grad = r.out[h] + unpack_cells(r.own[quarter, inside].astype(F32))
            r.out[h] = grad
            return grad

        rows_to_modes(plan, r.rowinv_t[...], r.flat, middle_grad, False)
        there = Exchange(False, spaces, plan.thick, r.send1, r.recv1, r.s1, r.r1)
        back = Exchange(False, spaces, plan.thick, r.send2, r.recv2, r.s2, r.r2)
        send_modes(there, plan.pairs, plan.chunk, r.flat)
        lax.fori_loop(shipped, plan.steps, own_block, 0)
        settle(plan.steps - 1)
        filter_backward(plan, r, there, back, pass_on)
        mix_gradients(plan, r, r.sums_before)

        def arrived(k, carry):
            ship_near(k).wait_send()
            ship_near(plan.per + k).wait()
            ship_under(k).wait_send()
            ship_under(plan.per + k).wait()
            on_across(k).wait()
            on_beside(k).wait()
            return carry

        lax.fori_loop(0, plan.per, arrived, 0)
        wait_all(vectors)
        def send(source, target, step, send_sem, recv_sem):
            return pltpu.make_async_remote_copy(
                src_ref=source,
                dst_ref=target,
                send_sem=send_sem.at[step],
                recv_sem=recv_sem.at[step],
                device_id={"space": 2 * others[step - 1] + core},
                device_id_type=MESH_ID,
            )

        def to_sibling(source, target, step, send_sem, recv_sem):
            return pltpu.make_async_remote_copy(
                src_ref=source,
                dst_ref=target,
                send_sem=send_sem.at[step],
                recv_sem=recv_sem.at[step],
                device_id={"space": sibling},
                device_id_type=MESH_ID,
            )

        def total(tile, carry):
            for half, land in enumerate((r.land_near, r.land_under)):
                for sub in range(2):
                    inside = pl.ds(64 * sub, 64)
                    value = r.keep[3 * plan.per + tile, pl.ds(128 * half + 64 * sub, 64), :].astype(F32)
                    value += land[1, tile, inside, :].astype(F32) + r.land_on[half, tile, inside, :].astype(F32)
                    number = 4 * tile + 2 * half + sub
                    target = pl.ds(pl.multiple_of((number % (piece // 64)) * 64, 64), 64)
                    r.a_send[number // (piece // 64), target, :] = value.astype(BF)
            return carry

        lax.fori_loop(0, plan.per, total, 0)
        wide = [
            send(r.a_send.at[others[step - 1]], r.a_land.at[level], step, r.s11, r.r11)
            for step in range(1, levels)
        ]
        for copy in wide:
            copy.start()
        collect(back, plan.pairs, plan.chunk, r.flat)
        copies = rows_backward(plan, r, r.unit, r.sums_before)
        r.table[...] = jnp.zeros_like(r.table)
        r.table[0:small, :] = r.sums[...]
        tail = sum(r.rest_land[j] for j in range(chans))
        for k in range(local // 128):
            lanes = slice(k * 128, (k + 1) * 128)
            r.table[small + k : small + k + 1, :] = tail[0:1, lanes]
        for k in range(3):
            line = jnp.concatenate([tail[1 + k : 2 + k, :features], jnp.zeros((1, 256 - features), F32)], axis=1)
            r.table[small + 8 + 2 * k : small + 9 + 2 * k, :] = line[:, :128]
            r.table[small + 9 + 2 * k : small + 10 + 2 * k, :] = line[:, 128:]
        for q in range(levels):
            r.b_send[q] = r.table[q * part : (q + 1) * part, :].astype(BF)
        thin = [
            send(r.b_send.at[others[step - 1]], r.b_land.at[level], step, r.s12, r.r12)
            for step in range(1, levels)
        ]
        for copy in thin:
            copy.start()
        wait_all(copies)
        result = input_gradient(plan, r, r.unit, r.dev)

        def finish(h, carry):
            r.out[h] = result(h)
            return carry

        lax.fori_loop(0, rows, finish, 0, unroll=3)
        moves.start(r.second_x, r.scaled).wait()
        moves.open = []
        leave(r.scaled, r.lines, r.turn)
        moves.start(r.lines, r.lines_x)
        a = r.a_send[level].astype(F32)
        b = r.b_send[level].astype(F32)
        for step in range(1, levels):
            wide[step - 1].wait()
            thin[step - 1].wait()
            source = lax.rem(level - step + levels, levels)
            a += r.a_land[source].astype(F32)
            b += r.b_land[source].astype(F32)
        r.a_own[...] = a.astype(BF)
        r.b_own[...] = b.astype(BF)
        last = [to_sibling(r.a_own, r.a_other.at[level], 0, r.s13, r.r13)]
        last += [to_sibling(r.b_own, r.b_other.at[level], 0, r.s14, r.r14)]
        again = []
        for step in range(1, levels):
            again.append(send(r.a_own, r.a_full.at[level], step, r.s15, r.r15))
            again.append(send(r.b_own, r.b_full.at[level], step, r.s16, r.r16))
        for copy in again + last:
            copy.start()
        r.a_full[level] = r.a_own[...]
        r.b_full[level] = r.b_own[...]
        moves.close()
        moves.open = []
        leave(r.out, r.lines, r.turn)
        moves.start(r.lines, r.lines_out)
        for step in range(1, levels):
            again[2 * step - 2].wait()
            again[2 * step - 1].wait()
            source = lax.rem(level - step + levels, levels)
            more = [to_sibling(r.a_full.at[source], r.a_other.at[source], step, r.s13, r.r13)]
            more += [to_sibling(r.b_full.at[source], r.b_other.at[source], step, r.s14, r.r14)]
            for copy in more:
                copy.start()
            last += more
        wait_all(last)
        moves.close()
        there.close(plan.pairs)
        back.close(plan.pairs)

    ins = {
        "g": two["out_kept"],
        "came": two["came"],
        "second_x": two["second_x"],
        "sums_before": two["sums"],
        "rest_before": two["rest"],
        "grads_kept": two["grads_kept"],
        "mix_kept": one["mix_kept"],
        **{
            key: one[key]
            for key in (
                "w_kept",
                "slope_kept",
                "active_kept",
                "entry_kept",
                "unit_wide_kept",
                "dev_wide_kept",
                "gathered_kept",
                "spec_kept",
                "first_kept",
                "second_kept",
                "unit_kept",
                "dev_kept",
            )
        },
        **args,
    }
    ins.update({key: tables[key] for key in ("rowinv_t", "row_t")})
    ins.update(col_kept=tables["col"], colinv_kept=tables["colinv"])
    outs = {
        "lines_x": plan.lines,
        "lines_out": plan.lines,
        "a_full": ((levels, piece, width), BF),
        "a_other": ((levels, piece, width), BF),
        "b_full": ((levels, part, 128), BF),
        "b_other": ((levels, part, 128), BF),
    }
    blocks = pltpu.VMEM((plan.steps, plan.tile, width), BF)
    scratch = {
        "dma": sems(32),
        "mix": scratch_of(plan.mix),
        "col": pltpu.VMEM(tables["col"].shape, BF),
        "colinv": pltpu.VMEM(tables["colinv"].shape, BF),
        "dma2": sems(2, 2),
        "lines": scratch_of(plan.lines),
        "unit": scratch_of(plan.field),
        "dev": scratch_of(plan.dev),
        "out": scratch_of(plan.field),
        "spec": scratch_of(plan.kept),
        "first": scratch_of(plan.kept),
        "second": scratch_of(plan.kept),
        "w": scratch_of(plan.weights),
        "own": scratch_of(plan.by_cells),
        "leaving": scratch_of(plan.by_cells),
        "upper": scratch_of(plan.wide),
        "small": pltpu.VMEM((8, width), F32),
        "upb": pltpu.VMEM((16, plan.tile), F32),
        "sums": scratch_of(plan.sums),
        "rest": scratch_of(plan.rest),
        "rest_land": scratch_of(plan.rest),
        "prev": pltpu.VMEM((2, 2, plan.tile, width), BF),
        "keep": blocks,
        "give": pltpu.VMEM((2, plan.tile, width), BF),
        "take": pltpu.VMEM((3, plan.tile, width), BF),
        "land_near": pltpu.VMEM((2, plan.per, plan.tile // 2, width), BF),
        "land_under": pltpu.VMEM((2, plan.per, plan.tile // 2, width), BF),
        "land_on": pltpu.VMEM((2, plan.per, plan.tile // 2, width), BF),
        "table": pltpu.VMEM((part * levels, 128), F32),
        "a_send": pltpu.VMEM((levels, piece, width), BF),
        "a_land": pltpu.VMEM((levels, piece, width), BF),
        "a_own": pltpu.VMEM((piece, width), BF),
        "b_send": pltpu.VMEM((levels, part, 128), BF),
        "b_land": pltpu.VMEM((levels, part, 128), BF),
        "b_own": pltpu.VMEM((part, 128), BF),
        **plan.exchange_scratch(False, False),
        **plan.spectral_scratch(),
        **ffn_scratch(plan),
        **norm_sums_scratch(plan),
        **{key + str(k): sems(chans) for k in (6, 7) for key in ("s", "r")},
        **{key + str(k): sems(plan.steps) for k in (9, 10, 17, 18) for key in ("s", "r")},
        **{key + str(k): sems(levels) for k in range(11, 17) for key in ("s", "r")},
    }
    in_place = [key for key in ins if key.endswith("_kept")] + ["second_x", "g"]
    return launch(
        body,
        ins,
        outs,
        scratch,
        "first_backward",
        2,
        {key: IN_PLACE for key in in_place},
        {key: IN_PLACE for key in ("lines_x", "lines_out")},
    )


def unpack_gradients(plan, parts, fields):
    features, small = plan.features, plan.small
    levels, piece, width = parts["a_full"].shape
    part = parts["b_full"].shape[1]
    local = levels * piece
    size = features // 2

    def body(r):
        swap = lax.rem(lax.axis_index("space"), 2) == 1
        moves = Moves(r.dma)
        waiting = [(moves.start(getattr(r, key + "_in"), getattr(r, key + "_held")), key) for key in fields]
        for q in range(levels):
            own = slice(q * piece, (q + 1) * piece)
            mine, theirs = r.a_full[q], r.a_other[q]
            r.down_made[own, :] = jnp.where(swap, theirs, mine).astype(F32)
            r.up_made[:, own] = jnp.where(swap, mine, theirs).T.astype(F32)
            moves.start(r.down_made.at[pl.ds(q * piece, piece)], r.down.at[pl.ds(q * piece, piece)])
            if q % 2:
                lanes = pl.ds((q - 1) * piece, 2 * piece)
                moves.start(r.up_made.at[:, lanes], r.up.at[:, lanes])
            if q < len(waiting):
                loaded, key = waiting[q]
                loaded.wait()
                moves.start(getattr(r, key + "_held"), getattr(r, key))
            r.table[q * part : (q + 1) * part, :] = r.b_full[q].astype(F32) + r.b_other[q].astype(F32)
        for layer, target in enumerate((r.mix_in, r.mix_out)):
            for half in range(2):
                for block in range(2):
                    start = ((layer * 2 + half) * 2 + block) * size
                    target[half, block] = r.table[start : start + size, :size]
        base = 8 * size

        def vector(k):
            return jnp.concatenate(
                [r.table[base + k : base + k + 1, :], r.table[base + 8 + k : base + 9 + k, : features - 128]], axis=1
            )

        for k, target in enumerate((r.bias_in, r.bias_in, r.bias_out, r.bias_out)):
            value = vector(k)
            target[k % 2, 0:1, :] = value[:, :size]
            target[k % 2, 1:2, :] = value[:, size:]
        r.pre_gain[...] = vector(4)
        r.pre_shift[...] = vector(5)
        r.upb[...] = jnp.concatenate(
            [r.table[small + k : small + k + 1, :] for k in range(local // 128)], axis=1
        ).reshape(local)
        for k, target in enumerate((r.post_gain, r.post_shift, r.downb)):
            target[...] = jnp.concatenate(
                [
                    r.table[small + 8 + 2 * k : small + 9 + 2 * k, :],
                    r.table[small + 9 + 2 * k : small + 10 + 2 * k, : features - 128],
                ],
                axis=1,
            )
        moves.open = moves.open[len(waiting) :]
        moves.close()

    return launch(
        body,
        {
            **{key: parts[key] for key in ("a_full", "a_other", "b_full", "b_other")},
            **{key + "_in": value for key, value in fields.items()},
        },
        {
            "down": ((local, width), F32),
            "up": ((width, local), F32),
            "mix_in": ((2, 2, size, size), F32),
            "mix_out": ((2, 2, size, size), F32),
            "bias_in": ((2, 2, size), F32),
            "bias_out": ((2, 2, size), F32),
            "pre_gain": ((1, features), F32),
            "pre_shift": ((1, features), F32),
            "post_gain": ((1, features), F32),
            "post_shift": ((1, features), F32),
            "downb": ((1, features), F32),
            "upb": ((local,), F32),
            **{key: plan.lines for key in fields},
        },
        {
            "table": pltpu.VMEM((part * levels, 128), F32),
            "down_made": pltpu.VMEM((local, width), F32),
            "up_made": pltpu.VMEM((width, local), F32),
            "dma": sems(16),
            **{key + "_held": scratch_of(plan.lines) for key in fields},
        },
        "unpack_gradients",
        None,
        {key + "_in": IN_PLACE for key in fields},
        {key: IN_PLACE for key in ("down", "up", *fields)},
    )


def shards_fast(
    current_atmosphere,
    truth_one,
    truth_two,
    storm_codes,
    pre_gain,
    pre_shift,
    mix_weight_in,
    mix_bias_in,
    mix_weight_out,
    mix_bias_out,
    post_gain,
    post_shift,
    up_weight,
    up_bias,
    down_weight,
    down_bias,
):
    rows, merged = current_atmosphere.shape[1:]
    columns = W
    features = merged // columns
    plan = Plan(
        rows, features, columns, lax.axis_size("space"), lax.axis_size("chan"), up_weight.shape[1]
    )
    forward, inverse = row_constants(columns)
    column = column_constants(rows * plan.spaces, rows, 2)
    tables = {
        "row": jnp.stack(const_halves(forward)),
        "rowinv": const_halves(inverse)[0],
        "rowinv_t": const_halves(inverse.T)[0],
        "row_t": const_halves(forward.T)[0],
        "col": jnp.stack(const_halves(column)),
        "colinv": const_halves(column.T)[0],
    }

    def lines(flat):
        return flat.reshape(rows, merged // 128, 128)

    def flat(line_field):
        return line_field.reshape(1, rows, merged)

    one = launch_first(
        plan,
        {
            "lines_x": lines(current_atmosphere),
            "lines_t": lines(truth_one),
            "gain": pre_gain,
            "shift": pre_shift,
            "mix_in": mix_weight_in,
            "bias_in": mix_bias_in,
            "mix_out": mix_weight_out,
            "bias_out": mix_bias_out,
            "post_gain": post_gain,
            "post_shift": post_shift,
            "up": up_weight,
            "upb": up_bias,
            "down": down_weight,
            "downb": down_bias,
        },
        tables,
    )
    two = launch_second(
        plan,
        {"gain": pre_gain, "shift": pre_shift, "lines_t": lines(truth_two), "codes": storm_codes},
        one,
        tables,
    )
    three = launch_third(plan, {"gain": pre_gain}, one, two, tables)
    grads = unpack_gradients(
        plan, three, {"first": two["lines"], "second": three["lines_x"], "state": three["lines_out"]}
    )
    return (
        flat(grads["first"]),
        flat(grads["second"]),
        flat(grads["state"]),
        grads["pre_gain"].reshape(features),
        grads["pre_shift"].reshape(features),
        grads["mix_in"],
        grads["bias_in"],
        grads["mix_out"],
        grads["bias_out"],
        grads["post_gain"].reshape(features),
        grads["post_shift"].reshape(features),
        grads["up"],
        grads["upb"],
        grads["down"],
        grads["downb"].reshape(features),
    )


def suits(mesh):
    spaces, chans = mesh.shape["space"], mesh.shape["chan"]
    return (spaces, chans) == (8, 4)


def solution(mesh):
    in_specs = (
        P(None, "space", "chan"),
        P(None, "space", "chan"),
        P(None, "space", "chan"),
        P(),
        P("chan"),
        P("chan"),
        P(None, "chan", None, None),
        P(None, "chan", None),
        P(None, "chan", None, None),
        P(None, "chan", None),
        P("chan"),
        P("chan"),
        P(None, "chan"),
        P("chan"),
        P("chan", None),
        P("chan"),
    )
    out_specs = (
        P(None, "space", "chan"),
        P(None, "space", "chan"),
        P(None, "space", "chan"),
        P("chan"),
        P("chan"),
        P(None, "chan", None, None),
        P(None, "chan", None),
        P(None, "chan", None, None),
        P(None, "chan", None),
        P("chan"),
        P("chan"),
        P(None, "chan"),
        P("chan"),
        P("chan", None),
        P("chan"),
    )
    return jax.shard_map(shards_fast if suits(mesh) else shards, mesh=mesh, in_specs=in_specs, out_specs=out_specs, check_vma=False)
```

```python
import functools
import math
import types

import jax
import jax.numpy as jnp
import ml_dtypes
import numpy as np
from jax import lax
from jax.experimental import pallas as pl
from jax.experimental.pallas import tpu as pltpu
from jax.sharding import PartitionSpec as P

W = 160
KW = 81


NORM_EPS = 1e-06
SHRINK_LEVEL = 0.01
FULL_PRECISION = lax.Precision.HIGHEST


def exact_gelu(values):
    return jax.nn.gelu(values, approximate=False)


def shrink(values):
    return values - jnp.clip(values, -SHRINK_LEVEL, SHRINK_LEVEL)


def block_mix(values, matrix):
    return jnp.einsum("bhkni,nio->bhkno", values, matrix, precision=FULL_PRECISION)


def row_tables(columns, kept_modes, padded_modes):
    places = jnp.arange(columns, dtype=jnp.int32)[:, None]
    orders = jnp.arange(padded_modes, dtype=jnp.int32)[None, :]
    angles = 2.0 * math.pi / columns * (places * orders % columns).astype(jnp.float32)
    factor = 1.0 / math.sqrt(columns)
    single = jnp.logical_or(orders == 0, 2 * orders == columns)
    doubled = jnp.where(single, 1.0, 2.0).astype(jnp.float32)
    used = jnp.where(orders < kept_modes, 1.0, 0.0).astype(jnp.float32)
    return (
        jnp.cos(angles) * factor * used,
        -jnp.sin(angles) * factor * used,
        jnp.transpose(jnp.cos(angles) * doubled * factor * used),
        jnp.transpose(jnp.sin(angles) * doubled * factor * used),
    )


def along_rows(values, tables):
    return jnp.stack(
        [
            jnp.einsum("bhwc,wk->bhkc", values, tables[0], precision=FULL_PRECISION),
            jnp.einsum("bhwc,wk->bhkc", values, tables[1], precision=FULL_PRECISION),
        ]
    )


def along_rows_back(paired, tables):
    return jnp.einsum("bhkc,wk->bhwc", paired[0], tables[0], precision=FULL_PRECISION) + jnp.einsum(
        "bhkc,wk->bhwc", paired[1], tables[1], precision=FULL_PRECISION
    )


def rows_inverse(paired, tables):
    return jnp.einsum("bhkc,kw->bhwc", paired[0], tables[2], precision=FULL_PRECISION) - jnp.einsum(
        "bhkc,kw->bhwc", paired[1], tables[3], precision=FULL_PRECISION
    )


def rows_inverse_back(values, tables):
    return jnp.stack(
        [
            jnp.einsum("bhwc,kw->bhkc", values, tables[2], precision=FULL_PRECISION),
            -jnp.einsum("bhwc,kw->bhkc", values, tables[3], precision=FULL_PRECISION),
        ]
    )


def column_tables(height):
    orders = jnp.arange(height, dtype=jnp.int32)[:, None]
    places = jnp.arange(height, dtype=jnp.int32)[None, :]
    angles = 2.0 * math.pi / height * (orders * places % height).astype(jnp.float32)
    factor = 1.0 / math.sqrt(height)
    return (jnp.cos(angles) * factor, jnp.sin(angles) * factor)


def to_freq(matrix, values):
    return jnp.einsum("kh,bhmc->bkmc", matrix, values, precision=FULL_PRECISION)


def from_freq(matrix, values):
    return jnp.einsum("kh,bkmc->bhmc", matrix, values, precision=FULL_PRECISION)


def spectral_core(paired, w_first, b_first, w_second, b_second):
    samples, height, kept_modes, channels = paired.shape[1:]
    blocks, block_size = (w_first.shape[1], w_first.shape[2])
    cosine, sine_table = column_tables(height)
    real_in, imag_in = (paired[0], paired[1])
    split_form = (samples, height, kept_modes, blocks, block_size)
    real_part = (to_freq(cosine, real_in) + to_freq(sine_table, imag_in)).reshape(split_form)
    imag_part = (to_freq(cosine, imag_in) - to_freq(sine_table, real_in)).reshape(split_form)
    first_real = jax.nn.relu(
        block_mix(real_part, w_first[0]) - block_mix(imag_part, w_first[1]) + b_first[0]
    )
    first_imag = jax.nn.relu(
        block_mix(imag_part, w_first[0]) + block_mix(real_part, w_first[1]) + b_first[1]
    )
    joined_form = (samples, height, kept_modes, channels)
    second_real = shrink(
        block_mix(first_real, w_second[0]) - block_mix(first_imag, w_second[1]) + b_second[0]
    ).reshape(joined_form)
    second_imag = shrink(
        block_mix(first_imag, w_second[0]) + block_mix(first_real, w_second[1]) + b_second[1]
    ).reshape(joined_form)
    out_real = from_freq(cosine, second_real) - from_freq(sine_table, second_imag)
    out_imag = from_freq(cosine, second_imag) + from_freq(sine_table, second_real)
    return jnp.stack([out_real, out_imag])


def column_layout(paired):
    return lax.all_to_all(paired, "space", split_axis=3, concat_axis=2, tiled=True)


def row_layout(paired):
    return lax.all_to_all(
        paired.astype(jnp.bfloat16), "space", split_axis=2, concat_axis=3, tiled=True
    ).astype(paired.dtype)


def norm_forward(values, gain, offset):
    width_all = values.shape[-1] * lax.axis_size("chan")
    totals = lax.psum((jnp.sum(values, axis=-1), jnp.sum(values * values, axis=-1)), "chan")
    average = totals[0] / width_all
    variance = totals[1] / width_all - average * average
    inverse_dev = lax.rsqrt(variance + NORM_EPS)[..., None]
    scaled = (values - average[..., None]) * inverse_dev
    return (scaled * gain + offset, (scaled, inverse_dev))


def norm_backward(gradient, gain, saved):
    scaled, inverse_dev = saved
    width_all = scaled.shape[-1] * lax.axis_size("chan")
    scaled_grad = gradient * gain
    totals = lax.psum(
        (jnp.sum(scaled_grad, axis=-1), jnp.sum(scaled_grad * scaled, axis=-1)), "chan"
    )
    values_grad = inverse_dev * (
        scaled_grad - totals[0][..., None] / width_all - scaled * (totals[1][..., None] / width_all)
    )
    return (
        values_grad,
        jnp.sum(gradient * scaled, axis=(0, 1, 2)),
        jnp.sum(gradient, axis=(0, 1, 2)),
    )


def shards(
    current_atmosphere,
    truth_one,
    truth_two,
    storm_codes,
    pre_gain,
    pre_shift,
    mix_weight_in,
    mix_bias_in,
    mix_weight_out,
    mix_bias_out,
    post_gain,
    post_shift,
    up_weight,
    up_bias,
    down_weight,
    down_bias,
):
    samples, rows_here, merged = current_atmosphere.shape
    columns = W
    channels = merged // columns
    total_rows = samples * rows_here * columns
    space_count = lax.axis_size("space")
    padded_modes = (KW + space_count - 1) // space_count * space_count
    tables = row_tables(columns, KW, padded_modes)

    def to_cells(flat_field):
        return jnp.transpose(
            flat_field.reshape(samples, rows_here, channels, columns), (0, 1, 3, 2)
        )

    def to_flat(cell_field):
        return jnp.transpose(cell_field, (0, 1, 3, 2)).reshape(samples, rows_here, merged)

    start_cells = to_cells(current_atmosphere)
    target_one = to_cells(truth_one)
    target_two = to_cells(truth_two)
    weight_of = (storm_codes.astype(jnp.float32) / 64.0).reshape(-1, 1, 1, 1)
    full_up, full_down, full_up_bias, full_down_bias = (up_weight, down_weight, up_bias, down_bias)

    def mlp_forward(inputs):
        gathered = lax.all_gather(inputs, "chan", axis=1, tiled=True)
        hidden = jnp.dot(
            gathered, full_up, preferred_element_type=jnp.float32
        ) + full_up_bias.astype(jnp.float32)
        active_full, gelu_pull = jax.vjp(exact_gelu, hidden)
        active = active_full.astype(jnp.bfloat16)
        product = jnp.dot(active, full_down, preferred_element_type=jnp.float32)
        output = lax.psum_scatter(
            product.astype(jnp.bfloat16), "chan", scatter_dimension=1, tiled=True
        ).astype(jnp.float32) + full_down_bias.astype(jnp.float32)
        return (output, (gathered, gelu_pull, active))

    def mlp_backward(gradient, saved):
        gathered, gelu_pull, active = saved
        grad_low = gradient.astype(jnp.bfloat16)
        grad_rows = lax.all_gather(grad_low, "chan", axis=1, tiled=True)
        down_bias_grad = jnp.sum(grad_low.astype(jnp.float32), axis=0)
        down_grad = jnp.dot(active.T, grad_rows, preferred_element_type=jnp.float32)
        active_grad = jnp.dot(grad_rows, full_down.T, preferred_element_type=jnp.float32)
        hidden_grad = gelu_pull(active_grad)[0].astype(jnp.bfloat16)
        up_grad = jnp.dot(gathered.T, hidden_grad, preferred_element_type=jnp.float32)
        up_bias_grad = jnp.sum(hidden_grad.astype(jnp.float32), axis=0)
        input_part = jnp.dot(hidden_grad, full_up.T, preferred_element_type=jnp.float32)
        input_grad = lax.psum_scatter(
            input_part.astype(jnp.bfloat16), "chan", scatter_dimension=1, tiled=True
        ).astype(jnp.float32)
        return (input_grad, (up_grad, up_bias_grad, down_grad, down_bias_grad))

    def forward_block(values):
        normed, first_saved = norm_forward(values, pre_gain, pre_shift)
        modal_in = column_layout(along_rows(normed, tables))
        filtered, core_pull = jax.vjp(
            spectral_core, modal_in, mix_weight_in, mix_bias_in, mix_weight_out, mix_bias_out
        )
        middle = rows_inverse(row_layout(filtered), tables) + normed + values
        entry, second_residuals = norm_forward(middle, post_gain, post_shift)
        output, mlp_saved = mlp_forward(entry.astype(jnp.bfloat16).reshape(total_rows, channels))
        return (
            output.reshape(values.shape) + middle,
            (first_saved, core_pull, second_residuals, mlp_saved),
        )

    def backward_block(gradient, saved):
        first_saved, core_pull, second_residuals, mlp_saved = saved
        mlp_grad, dense_grads = mlp_backward(gradient.reshape(total_rows, channels), mlp_saved)
        middle_part, post_gain_grad, post_shift_grad = norm_backward(
            mlp_grad.reshape(gradient.shape), post_gain, second_residuals
        )
        middle_grad = middle_part + gradient
        filter_grads = core_pull(column_layout(rows_inverse_back(middle_grad, tables)))
        normed_grad = along_rows_back(row_layout(filter_grads[0]), tables) + middle_grad
        input_part, pre_gain_grad, pre_shift_grad = norm_backward(
            normed_grad, pre_gain, first_saved
        )
        return (
            input_part + middle_grad,
            (pre_gain_grad, pre_shift_grad)
            + tuple(filter_grads[1:])
            + (post_gain_grad, post_shift_grad)
            + dense_grads,
        )

    first_out, first_saved_all = forward_block(start_cells)
    second_out, second_saved_all = forward_block(first_out)
    carried, grads_late = backward_block(weight_of * (second_out - target_two), second_saved_all)
    input_grad, grads_early = backward_block(
        weight_of * (first_out - target_one) + carried, first_saved_all
    )
    summed = jax.tree.map(jnp.add, grads_early, grads_late)
    (
        sum_pre_gain,
        sum_pre_shift,
        sum_mix_w_in,
        summed_mixing_bias_input,
        sum_mix_w_out,
        sum_mix_b_out,
        sum_post_gain,
        sum_post_shift,
        sum_up,
        sum_up_bias,
        sum_down,
        sum_down_bias,
    ) = summed
    totals = (
        lax.psum(sum_pre_gain.astype(jnp.bfloat16), "space").astype(jnp.float32),
        lax.psum(sum_pre_shift.astype(jnp.bfloat16), "space").astype(jnp.float32),
        lax.psum(sum_mix_w_in.astype(jnp.bfloat16), "space").astype(jnp.float32),
        lax.psum(summed_mixing_bias_input.astype(jnp.bfloat16), "space").astype(jnp.float32),
        lax.psum(sum_mix_w_out.astype(jnp.bfloat16), "space").astype(jnp.float32),
        lax.psum(sum_mix_b_out.astype(jnp.bfloat16), "space").astype(jnp.float32),
        lax.psum(sum_post_gain.astype(jnp.bfloat16), "space").astype(jnp.float32),
        lax.psum(sum_post_shift.astype(jnp.bfloat16), "space").astype(jnp.float32),
        lax.psum(sum_up.astype(jnp.bfloat16), "space").astype(jnp.float32),
        lax.psum(sum_up_bias.astype(jnp.bfloat16), "space").astype(jnp.float32),
        lax.psum(sum_down.astype(jnp.bfloat16), "space").astype(jnp.float32),
        lax.psum(sum_down_bias.astype(jnp.bfloat16), "space").astype(jnp.float32),
    )
    return (to_flat(first_out), to_flat(second_out), to_flat(input_grad)) + tuple(totals)


BF = jnp.bfloat16
F32 = jnp.float32
MESH_ID = pl.DeviceIdType.MESH
VMEM_BYTES = 66 * 1024 * 1024 - 1024 * 1024


def mm(a, b):
    return jnp.dot(a, b, preferred_element_type=F32)


def mm_nt(a, b):
    return lax.dot_general(a, b, (((1,), (1,)), ((), ())), preferred_element_type=F32)


def mm_tn(a, b):
    return lax.dot_general(a, b, (((0,), (0,)), ((), ())), preferred_element_type=F32)


def halves(v):
    high = v.astype(BF)
    return high, (v - high.astype(F32)).astype(BF)


def mm3(a, b):
    return mm(a[0], b[0]) + (mm(a[0], b[1]) + mm(a[1], b[0]))


def const_halves(table):
    table = np.asarray(table, np.float32)
    high = table.astype(ml_dtypes.bfloat16)
    low = (table - high.astype(np.float32)).astype(ml_dtypes.bfloat16)
    return jnp.asarray(high), jnp.asarray(low)


def row_constants(columns):
    half = columns // 2
    place = np.arange(columns)
    mode = np.arange(half)
    angle = 2.0 * np.pi * np.outer(mode, place) / columns
    real = np.cos(angle)
    imag = -np.sin(angle)
    imag[0] = np.cos(np.pi * place)
    forward = np.concatenate([real, imag]) / np.sqrt(columns)
    weight = np.where(mode == 0, 1.0, 2.0)
    inverse = (forward * np.concatenate([weight, weight])[:, None]).T
    return forward, inverse


def column_constants(height, rows, group):
    owners = height // rows
    angle = 2.0 * np.pi * np.outer(np.arange(height), np.arange(height)) / height
    cosine = np.cos(angle) / np.sqrt(height)
    sine = np.sin(angle) / np.sqrt(height)

    def spread(matrix):
        wide = np.zeros((group, height, owners, group, rows))
        for column in range(group):
            wide[column, :, :, column, :] = matrix.reshape(height, owners, rows)
        return wide.reshape(group * height, owners * group * rows)

    cosine, sine = spread(cosine), spread(sine)
    return np.block([[cosine, sine], [-sine, cosine]])


def partner(me, count, step):
    flip = (count - step) % count
    result, bit = 0, 1
    while bit < count:
        digit = lax.rem(me // bit, 2)
        result += bit * (1 - digit if flip // bit % 2 else digit)
        bit *= 2
    return result


class Order:
    far = False


def chan_peer(me, count, step):
    return partner(me, count, step) if Order.far else lax.rem(me + step, count)


def signal_peers(axis, count, barrier):
    me = lax.axis_index(axis)
    for step in range(1, count):
        pl.semaphore_signal(
            barrier, inc=1, device_id={axis: lax.rem(me + step, count)}, device_id_type=MESH_ID
        )


def push(axis, count, step, source, target, send_sem, recv_sem):
    me = lax.axis_index(axis)
    peer = chan_peer(me, count, step) if axis == "chan" else lax.rem(me + step, count)
    return pltpu.make_async_remote_copy(
        src_ref=source,
        dst_ref=target,
        send_sem=send_sem.at[step],
        recv_sem=recv_sem.at[step],
        device_id={axis: peer},
        device_id_type=MESH_ID,
    )


def params(collective_id=None):
    return pltpu.CompilerParams(
        collective_id=collective_id,
        has_side_effects=collective_id is not None,
        vmem_limit_bytes=VMEM_BYTES,
    )


def launch(body, ins, outs, scratch, name, collective_id=None, in_specs=None, out_specs=None, grid=()):
    in_specs, out_specs = in_specs or {}, out_specs or {}
    names = list(ins) + list(outs) + list(scratch)
    whole = pl.BlockSpec(memory_space=pltpu.VMEM)
    results = pl.pallas_call(
        lambda *refs: body(types.SimpleNamespace(**dict(zip(names, refs)))),
        grid=grid,
        in_specs=[in_specs.get(key, whole) for key in ins],
        out_specs=[out_specs.get(key, whole) for key in outs],
        out_shape=[jax.ShapeDtypeStruct(*outs[key]) for key in outs],
        scratch_shapes=list(scratch.values()),
        compiler_params=params(collective_id),
        name=name,
    )(*ins.values())
    return dict(zip(outs, results))


IN_PLACE = pl.BlockSpec(memory_space=pl.ANY)


def sems(*counts):
    return pltpu.SemaphoreType.DMA(counts)


def run_copies(copies):
    for copy in copies:
        copy.start()
    for copy in copies:
        copy.wait()


def cells_from_lines(lines_ref, h, scratch_ref):
    features = scratch_ref.shape[1]
    per = 640 // W
    groups = features // per
    wide = jnp.concatenate(
        [lines_ref[h, pl.ds(part, groups, stride=5), :] for part in range(5)], axis=1
    )
    for part in range(per):
        piece = wide[:, part * W : (part + 1) * W]
        scratch_ref[0, pl.ds(part, groups, stride=per), :] = piece[:, :128]
        scratch_ref[1, pl.ds(part, groups, stride=per), :] = jnp.concatenate(
            [piece[:, 128:], jnp.zeros((groups, 256 - W), F32)], axis=1
        )
    return jnp.concatenate([scratch_ref[0], scratch_ref[1][:, : W - 128]], axis=1)


def enter(lines_ref, cells_ref, scratch_ref):
    def row(h, carry):
        cells_ref[h] = cells_from_lines(lines_ref, h, scratch_ref).T
        return carry

    lax.fori_loop(0, lines_ref.shape[0], row, 0)


def leave(cells_ref, lines_ref, scratch_ref):
    features = scratch_ref.shape[1]
    per = 640 // W
    groups = features // per

    def row(h, carry):
        block = cells_ref[h].T
        scratch_ref[0] = block[:, :128]
        scratch_ref[1] = jnp.concatenate([block[:, 128:], jnp.zeros((features, 256 - W), F32)], axis=1)
        wide = jnp.concatenate(
            [
                piece
                for part in range(per)
                for piece in (
                    scratch_ref[0, pl.ds(part, groups, stride=per), :],
                    scratch_ref[1, pl.ds(part, groups, stride=per), :][:, : W - 128],
                )
            ],
            axis=1,
        )
        for part in range(5):
            lines_ref[h, pl.ds(part, groups, stride=5), :] = wide[:, part * 128 : (part + 1) * 128]
        return carry

    lax.fori_loop(0, lines_ref.shape[0], row, 0)


def pack_lanes(flat_ref, place, real, imag):
    flat_ref[0, place, :] = real[:, :128]
    flat_ref[1, place, :] = imag[:, :128]
    flat_ref[2, place, :] = jnp.concatenate([real[:, 128:], imag[:, 128:]], axis=1)


def join_lanes(first, second, rest):
    real = jnp.concatenate([first, rest[:, :64]], axis=1)
    imag = jnp.concatenate([second, rest[:, 64:]], axis=1)
    return real, imag


def unpack_lanes(flat_ref, place):
    return join_lanes(flat_ref[0, place, :], flat_ref[1, place, :], flat_ref[2, place, :])


LEVEL = 32000.0


class Exchange:
    def __init__(self, fixed, spaces, thick, send_ref, recv_ref, send_sem, recv_sem, scales=None):
        self.fixed, self.scales = fixed, scales
        self.spaces, self.thick = spaces, thick
        self.send_ref, self.recv_ref = send_ref, recv_ref
        self.send_sem, self.recv_sem = send_sem, recv_sem
        self.me = lax.axis_index("space")

    @staticmethod
    def shape(fixed, spaces, thick, pairs):
        return pltpu.VMEM((pairs, spaces, 3 * thick, 128), jnp.int16 if fixed else BF)

    def copy(self, p, step):
        peer = partner(self.me, self.spaces, step)
        return pltpu.make_async_remote_copy(
            src_ref=self.send_ref.at[p, peer],
            dst_ref=self.recv_ref.at[p, self.me],
            send_sem=self.send_sem.at[p, step],
            recv_sem=self.recv_sem.at[p, step],
            device_id={"space": peer},
            device_id_type=MESH_ID,
        )

    def scale_copy(self, step):
        own_ref, all_ref, send_sem, recv_sem = self.scales
        return push("space", self.spaces, step, own_ref, all_ref.at[self.me], send_sem, recv_sem)

    def send_scales(self, flat_ref):
        own_ref, all_ref = self.scales[:2]
        largest = jnp.max(jnp.abs(flat_ref[...]), axis=1)
        own_ref[0:3, :] = jnp.maximum(largest, 1e-30) * (1.0 / LEVEL)
        own_ref[3:8, :] = jnp.ones((5, 128), F32)
        for step in range(1, self.spaces):
            self.scale_copy(step).start()
        all_ref[self.me] = own_ref[...]
        self.factor = 1.0 / own_ref[...]

    def encode(self, values):
        if not self.fixed:
            return jnp.concatenate([values[k] for k in range(3)], axis=0).astype(BF)
        lines = [jnp.round(values[k] * self.factor[k : k + 1]) for k in range(3)]
        return jnp.concatenate(lines, axis=0).astype(jnp.int32).astype(jnp.int16)

    def send(self, p, flat_ref, start_of):
        for step in list(range(1, self.spaces)) + [0]:
            peer = partner(self.me, self.spaces, step)
            rows = pl.ds(pl.multiple_of(start_of(peer), 8), self.thick)
            coded = self.encode(flat_ref[:, rows, :])
            if step:
                self.send_ref[p, peer] = coded
                self.copy(p, step).start()
            else:
                self.recv_ref[p, peer] = coded

    def arrive(self, p):
        for step in range(1, self.spaces):
            self.copy(p, step).wait_recv()

    def arrive_scales(self):
        for step in range(1, self.spaces):
            self.scale_copy(step).wait_recv()

    def take(self, p, source):
        coded = self.recv_ref[p, source]
        values = (coded.astype(jnp.int32) if self.fixed else coded).astype(F32)
        parts = [values[k * self.thick : (k + 1) * self.thick] for k in range(3)]
        if self.fixed:
            scale = self.scales[1][source]
            parts = [part * scale[k : k + 1] for k, part in enumerate(parts)]
        return parts

    def close(self, pairs):
        def pair(p, carry):
            for step in range(1, self.spaces):
                self.copy(p, step).wait_send()
            return carry

        lax.fori_loop(0, pairs, pair, 0)
        if self.fixed:
            for step in range(1, self.spaces):
                self.scale_copy(step).wait_send()


def pair_inputs(q, exchange, even_ref):
    p = jnp.maximum(q - 1, 0)

    @pl.when(q != 1)
    def _():
        exchange.arrive(p)

    if exchange.fixed:

        @pl.when(q == 0)
        def _():
            exchange.arrive_scales()

    extra = (q == 0).astype(F32)
    zeroth = jnp.logical_and(exchange.me == 0, p == 0).astype(F32)
    parts = [join_lanes(*exchange.take(p, s)) for s in range(exchange.spaces)]
    real = jnp.concatenate([part[0] for part in parts], axis=0)
    imag = jnp.concatenate([part[1] for part in parts], axis=0)
    chosen = imag * (even_ref[...] * zeroth)
    real = real * (1.0 - extra) + chosen * extra
    imag = (imag - chosen) * (1.0 - extra)
    return p, zeroth, jnp.concatenate([real, imag], axis=0)


def pair_outputs(q, p, zeroth, result, exchange, even_ref, kept_ref, stage_ref):
    half = result.shape[0] // 2
    real, imag = result[:half], result[half:]

    @pl.when(q == 0)
    def _():
        kept_ref[...] = real

    @pl.when(q > 0)
    def _():
        chosen = even_ref[...] * zeroth
        pack_lanes(stage_ref, slice(None), real, imag * (1.0 - chosen) + kept_ref[...] * chosen)
        exchange.send(p, stage_ref, lambda peer: peer * exchange.thick)


def collect(exchange, pairs, chunk, flat_ref):
    def pair(p, carry):
        exchange.arrive(p)
        for s in range(exchange.spaces):
            rows = pl.ds(pl.multiple_of(s * chunk + p * exchange.thick, 8), exchange.thick)
            for k, part in enumerate(exchange.take(p, s)):
                flat_ref[k, rows, :] = part
        return carry

    lax.fori_loop(0, pairs, pair, 0)


def send_modes(exchange, pairs, chunk, flat_ref):
    if exchange.fixed:
        exchange.send_scales(flat_ref)

    def pair(p, carry):
        exchange.send(p, flat_ref, lambda peer: peer * chunk + p * exchange.thick)
        return carry

    lax.fori_loop(0, pairs, pair, 0)


class Plan:
    def __init__(self, rows, features, columns, spaces, chans, local):
        self.rows, self.features, self.columns = rows, features, columns
        self.spaces, self.chans, self.local = spaces, chans, local
        self.modes = columns // 2
        self.total = self.modes * rows
        self.chunk = self.total // spaces
        self.thick = 2 * rows
        self.half = self.thick * spaces
        self.pairs = self.chunk // self.thick
        self.cells = rows * columns // chans
        self.share = rows // chans
        self.width = features * chans
        self.tile = 256
        self.per = local // self.tile
        self.steps = chans * self.per
        self.size = features // 2
        self.small = 8 * self.size + 16
        self.field = ((rows, columns, features), F32)
        self.by_cells = ((chans, self.share, columns // 2 * 3, 128), BF)
        self.wide = ((self.cells, self.width), BF)
        self.tiles = ((self.steps, self.cells, self.tile), BF)
        self.lines = ((rows, features * columns // 128, 128), F32)
        self.dev = ((-(-rows // 8) * 8, columns), F32)
        self.dev_wide = ((self.cells, 128), F32)
        self.kept = ((self.pairs + 1, 2 * self.half, features), BF)
        self.mix = ((2, 2, 2, features, features), BF)
        self.weights = ((2, chans, local, self.width), BF)
        self.rest = ((chans, 8, local), F32)
        self.sums = ((self.small, 128), F32)
        self.grads = ((2, self.steps, self.tile, self.width), BF)
        self.vectors = ((chans, 8, local), F32)

    def exchange_scratch(self, fixed_there, fixed_back):
        made = {}
        for name, fixed in (("1", fixed_there), ("2", fixed_back)):
            shape = Exchange.shape(fixed, self.spaces, self.thick, self.pairs)
            made["send" + name] = made["recv" + name] = shape
            made["s" + name] = made["r" + name] = sems(self.pairs, self.spaces)
        if fixed_there:
            made["scale"] = pltpu.VMEM((8, 128), F32)
            made["scale_all"] = pltpu.VMEM((self.spaces, 8, 128), F32)
            made["s20"] = made["r20"] = sems(self.spaces)
        return made

    def spectral_scratch(self):
        return {
            "flat": pltpu.VMEM((3, self.total, 128), F32),
            "stage": pltpu.VMEM((3, self.half, 128), F32),
            "last": pltpu.VMEM((self.half, self.features), F32),
            "turn": pltpu.VMEM((2, self.features, 128), F32),
            "even": pltpu.VMEM((self.half, self.features), F32),
        }


def pack_cells(value):
    side = value.shape[0] // 2
    rest = value[:, 128:]
    return jnp.concatenate([value[:, :128], jnp.concatenate([rest[:side], rest[side:]], axis=1)], axis=0)


def unpack_cells(packed):
    columns = packed.shape[0] // 3 * 2
    rest = packed[columns:]
    rest = jnp.concatenate([rest[:, :64], rest[:, 64:]], axis=0)
    return jnp.concatenate([packed[:columns], rest], axis=1)


def three_parts(v):
    a = v.astype(BF)
    rest = v - a.astype(F32)
    b = rest.astype(BF)
    return [a, b, (rest - b.astype(F32)).astype(BF)]


def stack_rows(rows):
    lines = [part.astype(F32) for row in rows for part in three_parts(row)]
    lines.append(jnp.zeros((16 - len(lines), rows[0].shape[1]), F32))
    return jnp.concatenate(lines, axis=0).astype(BF)


def over_lanes(table, features, number):
    line = lax.broadcasted_iota(jnp.int32, (16, features), 0)
    chosen = jnp.logical_and(line >= 3 * number, line < 3 * number + 3)
    return mm_tn(table, jnp.where(chosen, 1.0, 0.0).astype(BF))


def lane_sums(value):
    return mm_nt(jnp.ones((16, value.shape[1]), BF), value.astype(BF))[0:1]


def scratch_of(shaped):
    return pltpu.VMEM(*shaped)


def mark_even(plan, r):
    row = lax.broadcasted_iota(jnp.int32, (plan.half, plan.features), 0)
    r.even[...] = jnp.where(lax.rem(lax.div(row, plan.rows), 2) == 0, 1.0, 0.0)


def greet(plan):
    barrier = pltpu.get_barrier_semaphore()
    signal_peers("space", plan.spaces, barrier)
    signal_peers("chan", plan.chans, barrier)
    return lambda: pl.semaphore_wait(barrier, plan.spaces + plan.chans - 2)


def spread_chan(plan, source_ref, target_ref, send_sem, recv_sem):
    me = lax.axis_index("chan")
    copies = []
    for step in range(1, plan.chans):
        peer = chan_peer(me, plan.chans, step)
        copy = push("chan", plan.chans, step, source_ref.at[peer], target_ref.at[me], send_sem, recv_sem)
        copy.start()
        copies.append(copy)
    target_ref[me] = source_ref[me]
    return copies


def wait_all(copies):
    for copy in copies:
        copy.wait()


def rows_to_modes(plan, table, flat_ref, value_of, exact):
    def row(h, carry):
        value = value_of(h)
        out = mm3(table, halves(value)) if exact else mm(table, value.astype(BF))
        pack_lanes(flat_ref, pl.ds(h, plan.modes, stride=plan.rows), out[: plan.modes], out[plan.modes :])
        return carry

    lax.fori_loop(0, plan.rows, row, 0, unroll=4)


def filter_forward(plan, r, there, back, aside=None):
    half = plan.half

    def filter_pair(q, carry):
        if aside is not None:
            pl.when(q == plan.pairs)(aside)
        p, zeroth, block = pair_inputs(q, there, r.even)
        spec = mm3((r.col[0], r.col[1]), halves(block))
        r.spec[q] = spec.astype(BF)
        parts = halves(spec)
        straight = mm3(parts, (r.mix[0, 0, 0], r.mix[0, 0, 1]))
        crossed = mm3(parts, (r.mix[0, 1, 0], r.mix[0, 1, 1]))
        first = jnp.concatenate(
            [
                jnp.maximum(straight[:half] - crossed[half:] + r.bias[0:1], 0.0),
                jnp.maximum(straight[half:] + crossed[:half] + r.bias[1:2], 0.0),
            ],
            axis=0,
        )
        r.first[q] = first.astype(BF)
        parts = halves(first)
        straight = mm3(parts, (r.mix[1, 0, 0], r.mix[1, 0, 1]))
        crossed = mm3(parts, (r.mix[1, 1, 0], r.mix[1, 1, 1]))
        second = jnp.concatenate(
            [
                straight[:half] - crossed[half:] + r.bias[2:3],
                straight[half:] + crossed[:half] + r.bias[3:4],
            ],
            axis=0,
        )
        second = second - jnp.clip(second, -SHRINK_LEVEL, SHRINK_LEVEL)
        r.second[q] = second.astype(BF)
        result = mm(r.colinv[...], r.second[q])
        pair_outputs(q, p, zeroth, result, back, r.even, r.last, r.stage)
        return carry

    lax.fori_loop(0, plan.pairs + 1, filter_pair, 0)


def modes_to_rows(plan, flat_ref, h):
    real, imag = unpack_lanes(flat_ref, pl.ds(h, plan.modes, stride=plan.rows))
    return jnp.concatenate([real, imag], axis=0)


def rows_of_chunks(plan, row, send_chunk):
    me = lax.axis_index("chan")
    for step in list(range(1, plan.chans)) + [0]:
        peer = chan_peer(me, plan.chans, step)

        def one(i, carry):
            row(peer * plan.share + i, peer, i)
            return carry

        lax.fori_loop(0, plan.share, one, 0, unroll=True)
        send_chunk(step, peer)


def rows_forward(plan, r, unit_ref, x_ref, middle_ref):
    me = lax.axis_index("chan")
    gain, shift = r.gain[...].reshape(1, -1), r.shift[...].reshape(1, -1)
    copies = []

    def row(h, peer, place):
        block = modes_to_rows(plan, r.flat, h)
        out = mm(r.rowinv[...], block.astype(BF))
        middle = out + (unit_ref[h] * gain + shift) + x_ref[h]
        middle_ref[h] = middle
        r.own[peer, place] = pack_cells(middle).astype(BF)

    def send_chunk(step, peer):
        if step:
            copy = push("chan", plan.chans, step, r.own.at[peer], r.mid.at[me], r.s3, r.r3)
            copy.start()
            copies.append(copy)
        else:
            r.mid[me] = r.own[me]

    rows_of_chunks(plan, row, send_chunk)
    return copies


class Block:
    def __init__(self, plan, group, side):
        self.group, self.side, self.size = group, side, plan.columns // 2
        start = group * plan.columns + side * self.size
        self.cells = pl.ds(pl.multiple_of(start, 16), self.size)
        self.front = slice(side * self.size, (side + 1) * self.size)
        self.back = slice(plan.columns, plan.columns + self.size)
        self.lanes = slice(64 * side, 64 * side + 64)

    def get(self, chunks_ref):
        parts = []
        for j in range(chunks_ref.shape[0]):
            parts.append(chunks_ref[j, self.group, self.front, :].astype(F32))
            parts.append(chunks_ref[j, self.group, self.back, self.lanes].astype(F32))
        return jnp.concatenate(parts, axis=1)

    def put(self, chunks_ref, value):
        chans = chunks_ref.shape[0]
        features = value.shape[1] // chans
        for j in range(chans):
            part = value[:, j * features : (j + 1) * features].astype(BF)
            chunks_ref[j, self.group, self.front, :] = part[:, :128]
            chunks_ref[j, self.group, self.back, self.lanes] = part[:, 128:]


def by_blocks(plan, step):
    def one(group, carry):
        for side in range(2):
            step(Block(plan, group, side))
        return carry

    lax.fori_loop(0, plan.share, one, 0, unroll=True)


def full_vector(gathered_ref, start, size):
    chans = gathered_ref.shape[0]
    return jnp.concatenate([gathered_ref[j, 1:2, start : start + size] for j in range(chans)], axis=1)


def moments(value):
    mean = jnp.mean(value, axis=1, keepdims=True)
    centred = value - mean
    return mean, centred, lax.rsqrt(jnp.mean(centred * centred, axis=1, keepdims=True) + NORM_EPS)


ERF = (0.254829592, -0.284496736, 1.421413741, -1.453152027, 1.061405429)


def gelu_and_slope(v):
    e = jnp.exp2(v * v * (-0.5 / math.log(2.0)))
    below = 1.0 + (0.3275911 * math.sqrt(0.5)) * jnp.abs(v)
    t = pl.reciprocal(below, approx=True)
    t = t * (2.0 - below * t)
    c = [0.5 * k for k in ERF]
    tail = (e * t) * (c[0] + t * (c[1] + t * (c[2] + t * (c[3] + t * c[4]))))
    below = jnp.where(v >= 0.0, 1.0 - tail, tail)
    active = v * below
    return active, below + (v * (1.0 / math.sqrt(2.0 * math.pi))) * e


def tile_of(plan, t):
    return t // plan.per, pl.ds(pl.multiple_of((t % plan.per) * plan.tile, plan.tile), plan.tile)


def up_tile(plan, r, t):
    j, place = tile_of(plan, t)
    return r.w[0, j, :, place]


def down_tile(plan, r, t):
    j, place = tile_of(plan, t)
    return r.w[1, j, place, :]


def ffn_scratch(plan):
    shape = (plan.cells, plan.tile)
    made = {key: pltpu.VMEM(shape, F32) for key in ("wide_a", "wide_b")}
    made.update({key: pltpu.VMEM(shape, BF) for key in ("thin_a", "thin_b")})
    made.update(
        total=pltpu.VMEM((plan.cells, plan.width), F32),
        entry=scratch_of(plan.wide),
        unit_wide=scratch_of(plan.wide),
        dev_wide=scratch_of(plan.dev_wide),
        active=scratch_of(plan.tiles),
        slope=scratch_of(plan.tiles),
        gathered=scratch_of(plan.vectors),
    )
    return made


def staggered(plan, r, lead, turn, trail, ready=None):
    last = plan.steps - 1
    third = plan.cells // 3
    side = plan.cells // 2
    parts = plan.width // plan.tile
    r.thin_b[...] = jnp.zeros_like(r.thin_b)
    for k in range(2):
        r.wide_a[k * side : (k + 1) * side, :] = lead(0, slice(k * side, (k + 1) * side))

    def half_step(t, wide_now, wide_next, thin_past, thin_now):
        ahead, behind = jnp.minimum(t + 1, last), jnp.maximum(t - 1, 0)
        for k in range(3):
            place = slice(k * third, (k + 1) * third)
            thin_now[place, :] = turn(wide_now[place, :], t, place, k == 0)
            if k < 2:
                own = slice(k * side, (k + 1) * side)
                wide_next[own, :] = lead(ahead, own)
            trail(thin_past[...], behind, slice(k * parts // 3 * plan.tile, (k + 1) * parts // 3 * plan.tile))

    def pair(u, carry):
        if ready is not None:
            for chunk in range(1, plan.chans):
                pl.when(u == (chunk * plan.per - 1) // 2)(functools.partial(ready, chunk))
        half_step(2 * u, r.wide_a, r.wide_b, r.thin_b, r.thin_a)
        half_step(2 * u + 1, r.wide_b, r.wide_a, r.thin_a, r.thin_b)
        return carry

    lax.fori_loop(0, plan.steps // 2, pair, 0)
    trail(r.thin_b[...], last, slice(0, plan.width))


def ffn_forward(plan, r):
    gain = full_vector(r.gathered, 0, plan.features)
    shift = full_vector(r.gathered, plan.features, plan.features)
    bias = full_vector(r.gathered, 2 * plan.features, plan.features)

    def prepare(block):
        place = block.cells
        mean, centred, inverse = moments(block.get(r.mid))
        unit = centred * inverse
        r.unit_wide[place, :] = unit.astype(BF)
        r.dev_wide[place, :] = jnp.broadcast_to(inverse, (block.size, 128))
        r.entry[place, :] = (unit * gain + shift).astype(BF)
        r.total[place, :] = jnp.broadcast_to(bias, (block.size, plan.width))

    by_blocks(plan, prepare)

    def lead(t, rows):
        j, place = tile_of(plan, t)
        return mm(r.entry[rows, :], up_tile(plan, r, t)) + r.gathered[j, 0:1, place]

    def turn(value, t, rows, opening):
        active, slope = gelu_and_slope(value)
        active = active.astype(BF)
        r.active[t, rows, :] = active
        r.slope[t, rows, :] = slope.astype(BF)
        return active

    def trail(active, t, lanes):
        j, place = tile_of(plan, t)
        r.total[:, lanes] += mm(active, r.w[1, j, place, lanes])

    staggered(plan, r, lead, turn, trail)


def ffn_backward(plan, r, ready=None):
    r.small[...] = jnp.zeros_like(r.small)
    r.total[...] = jnp.zeros_like(r.total)

    def lead(t, rows):
        return mm_nt(r.upper[rows, :], down_tile(plan, r, t))

    def turn(value, t, rows, opening):
        lower = value * r.slope[t, rows, :].astype(F32)
        bias = jnp.sum(lower, axis=0, keepdims=True)
        r.upb[pl.ds(t, 1), :] = bias if opening else r.upb[pl.ds(t, 1), :] + bias
        lower = lower.astype(BF)
        r.slope[t, rows, :] = lower
        return lower

    def trail(lower, t, lanes):
        j, place = tile_of(plan, t)
        r.total[:, lanes] += mm_nt(lower, r.w[0, j, lanes, place])

    staggered(plan, r, lead, turn, trail, ready)
    gain = full_vector(r.gathered, 0, plan.features)

    def finish(block):
        place = block.cells
        grad = r.total[place, :]
        unit = r.unit_wide[place, :].astype(F32)
        r.small[0:1, :] += jnp.sum(grad * unit, axis=0, keepdims=True)
        r.small[1:2, :] += jnp.sum(grad, axis=0, keepdims=True)
        r.small[2:3, :] += jnp.sum(r.upper[place, :].astype(F32), axis=0, keepdims=True)
        scaled = grad * gain
        one = jnp.mean(scaled, axis=1, keepdims=True)
        two = jnp.mean(scaled * unit, axis=1, keepdims=True)
        result = r.dev_wide[place, :][:, :1] * (scaled - one - unit * two)
        block.put(r.leaving, result)

    by_blocks(plan, finish)


def vector_gradients(plan, r, rest_ref):
    rest_ref[...] = jnp.zeros_like(rest_ref)
    for j in range(plan.chans):
        for k in range(plan.per):
            line = j * plan.per + k
            rest_ref[j, 0:1, k * plan.tile : (k + 1) * plan.tile] = r.upb[line : line + 1, :]
        for k in range(3):
            rest_ref[j, 1 + k : 2 + k, 0 : plan.features] = r.small[
                k : k + 1, j * plan.features : (j + 1) * plan.features
            ]


def weight_gradients(r, t):
    return mm_tn(r.active[t], r.upper[...]), mm_tn(r.slope[t], r.entry[...])


def filter_backward(plan, r, there, back, aside=None):
    half = plan.half
    r.mixgrad[...] = jnp.zeros_like(r.mixgrad)
    r.biasgrad[...] = jnp.zeros_like(r.biasgrad)

    def turned(v):
        return jnp.concatenate([v[half:], -v[:half]], axis=0)

    def note_bias(index, value):
        r.biasgrad[index : index + 1, :] += jnp.sum(value, axis=0, keepdims=True)

    def through(low, layer):
        straight = mm_nt(low, r.mix[layer, 0, 0])
        crossed = mm_nt(low, r.mix[layer, 1, 0])
        return jnp.concatenate([straight[:half] + crossed[half:], straight[half:] - crossed[:half]], axis=0)

    def filter_pair(q, carry):
        if aside is not None:
            pl.when(q == 3)(aside)
        p, zeroth, block = pair_inputs(q, there, r.even)
        grad = mm(r.col[0], block.astype(BF))
        grad = jnp.where(r.second[q].astype(F32) == 0.0, 0.0, grad)
        note_bias(2, grad[:half])
        note_bias(3, grad[half:])
        low = grad.astype(BF)
        first = r.first[q]
        r.mixgrad[1, 0] += mm_tn(first, low)
        r.mixgrad[1, 1] += mm_tn(first, turned(grad).astype(BF))
        grad = jnp.where(first.astype(F32) > 0.0, through(low, 1), 0.0)
        note_bias(0, grad[:half])
        note_bias(1, grad[half:])
        low = grad.astype(BF)
        spec = r.spec[q]
        r.mixgrad[0, 0] += mm_tn(spec, low)
        r.mixgrad[0, 1] += mm_tn(spec, turned(grad).astype(BF))
        result = mm(r.colinv[...], through(low, 0).astype(BF))
        pair_outputs(q, p, zeroth, result, back, r.even, r.last, r.stage)
        return carry

    lax.fori_loop(0, plan.pairs + 1, filter_pair, 0)


def mix_gradients(plan, r, before_ref):
    size = plan.size
    for layer in range(2):
        for part in range(2):
            for block in range(2):
                own = slice(block * size, (block + 1) * size)
                piece = r.mixgrad[layer, part][own, own]
                piece = jnp.concatenate([piece, jnp.zeros((size, 128 - size), F32)], axis=1)
                start = ((layer * 2 + part) * 2 + block) * size
                place = slice(start, start + size)
                r.sums[place, :] = piece if before_ref is None else piece + before_ref[place, :]


def rows_backward(plan, r, unit_ref, before_ref):
    gain = r.gain[...].reshape(1, -1)
    me = lax.axis_index("chan")

    def row(h, carry):
        one_sum, two_sum = carry
        block = modes_to_rows(plan, r.flat, h)
        grad = mm(r.row_t[...], block.astype(BF)) + r.out[h]
        unit = unit_ref[h]
        one_sum += jnp.sum(grad * unit, axis=0, keepdims=True)
        two_sum += jnp.sum(grad, axis=0, keepdims=True)
        scaled = grad * gain
        r.scaled[h] = scaled
        r.mine[pl.ds(h, 1), :] = lane_sums(scaled)
        r.mine[pl.ds(plan.rows + h, 1), :] = lane_sums(scaled * unit)
        return one_sum, two_sum

    none = jnp.zeros((1, plan.features), F32)
    one_sum, two_sum = lax.fori_loop(0, plan.rows, row, (none, none), unroll=4)
    r.all[me] = r.mine[...]
    copies = [
        push("chan", plan.chans, step, r.mine, r.all.at[me], r.s4, r.r4) for step in range(1, plan.chans)
    ]
    for copy in copies:
        copy.start()
    vectors = jnp.concatenate([r.biasgrad[0:4], one_sum, two_sum, none, none], axis=0)
    wide = jnp.concatenate([vectors, jnp.zeros((8, 256 - plan.features), F32)], axis=1)
    wide = jnp.concatenate([wide[:, :128], wide[:, 128:]], axis=0)
    place = slice(8 * plan.size, plan.small)
    r.sums[place, :] = wide if before_ref is None else wide + before_ref[place, :]
    return copies


def input_gradient(plan, r, unit_ref, dev_ref):
    r.mine[...] = sum(r.all[j] for j in range(plan.chans)) * (1.0 / plan.width)

    def result(h):
        table = stack_rows(
            [r.mine[pl.ds(h, 1), :], r.mine[pl.ds(plan.rows + h, 1), :], dev_ref[pl.ds(h, 1), :]]
        )
        one, two, dev = [over_lanes(table, plan.features, k) for k in range(3)]
        return r.out[h] + dev * (r.scaled[h] - one - unit_ref[h] * two)

    return result


def norm_sums_scratch(plan):
    return {
        "scaled": scratch_of(plan.field),
        "mixgrad": pltpu.VMEM((2, 2, plan.features, plan.features), F32),
        "biasgrad": pltpu.VMEM((8, plan.features), F32),
        "mine": pltpu.VMEM((2 * plan.rows, plan.columns), F32),
        "all": pltpu.VMEM((plan.chans, 2 * plan.rows, plan.columns), F32),
        "s4": sems(plan.chans),
        "r4": sems(plan.chans),
    }


class Moves:
    def __init__(self, sem):
        self.sem, self.count, self.open = sem, 0, []

    def start(self, source, target):
        copy = pltpu.make_async_copy(source, target, self.sem.at[self.count])
        self.count += 1
        copy.start()
        self.open.append(copy)
        return copy

    def close(self):
        wait_all(self.open)


def launch_first(plan, args, tables):
    rows, features, chans = plan.rows, plan.features, plan.chans

    def body(r):
        me = lax.axis_index("chan")
        place = lax.axis_index("space")
        core = lax.rem(place, 2)
        sibling = place + 1 - 2 * core
        met = greet(plan)
        moves = Moves(r.dma)
        moves.start(r.up, r.w.at[0, me])
        moves.start(r.down, r.w.at[1, me])
        loaded = moves.start(r.lines_t, r.lines_in)
        own_weights = moves.open[:2]
        moves.open = []

        beside = me + 1 - 2 * lax.rem(me, 2)
        across = me + 2 - 4 * (me // 2)
        far = chans - 1 - me
        upper_half, lower_half = pl.ds(0, plan.local // 2), pl.ds(plan.local // 2, plan.local // 2)

        def hand(source, target, number, device):
            return pltpu.make_async_remote_copy(
                src_ref=source,
                dst_ref=target,
                send_sem=r.s5.at[number],
                recv_sem=r.r5.at[number],
                device_id=device,
                device_id_type=MESH_ID,
            )

        def own_to(number, source):
            peer = (beside, across)[number]
            return hand(source, r.w.at[core, me], number, {"chan": peer})

        def relay(number):
            slot = (beside, across)[number]
            part = r.w.at[core, slot, (upper_half, lower_half)[number]]
            return hand(part, part, 2 + number, {"chan": (across, beside)[number]})

        def to_core(number):
            if number < 2:
                part = r.w.at[core, (beside, across)[number]]
            else:
                part = r.w.at[core, far]
            return pltpu.make_async_remote_copy(
                src_ref=part,
                dst_ref=part,
                send_sem=r.s7.at[number],
                recv_sem=r.r7.at[number],
                device_id={"space": sibling},
                device_id_type=MESH_ID,
            )

        def pass_near():
            for number in range(2):
                own_to(number, r.up).wait_recv()
            for number in range(2):
                relay(number).start()
            for number in range(2):
                to_core(number).start()

        def pass_far():
            for number in range(2):
                relay(number).wait_recv()
            to_core(2).start()

        def close_weights():
            for number in range(2):
                own_to(number, r.up).wait_send()
                relay(number).wait_send()
            for number in range(3):
                to_core(number).wait()

        def first(h, carry):
            block = cells_from_lines(r.lines_x, h, r.turn)
            r.turned[h] = block
            total = jnp.sum(block, axis=0, keepdims=True)
            centred = block - total * (1.0 / features)
            r.mine[pl.ds(h, 1), :] = total
            r.mine[pl.ds(rows + h, 1), :] = jnp.sum(centred * centred, axis=0, keepdims=True)
            return carry

        lax.fori_loop(0, rows, first, 0)
        r.all[me] = r.mine[...]
        met()
        sums = [push("chan", chans, step, r.mine, r.all.at[me], r.s4, r.r4) for step in range(1, chans)]
        for copy in sums:
            copy.start()
        mark_even(plan, r)

        def row_of(ref):
            return ref[...].reshape(1, -1).astype(F32)

        r.vectors[...] = jnp.zeros_like(r.vectors)
        r.vectors[0:1, :] = row_of(r.upb)
        r.vectors[1:2, 0:features] = row_of(r.post_gain)
        r.vectors[1:2, features : 2 * features] = row_of(r.post_shift)
        r.vectors[1:2, 2 * features : 3 * features] = row_of(r.downb)
        r.gathered[me] = r.vectors[...]
        for layer, (source, bias) in enumerate(((r.mix_in, r.bias_in), (r.mix_out, r.bias_out))):
            for part in range(2):
                zero = jnp.zeros((plan.size, plan.size), F32)
                value = jnp.concatenate(
                    [
                        jnp.concatenate([source[part, 0], zero], axis=1),
                        jnp.concatenate([zero, source[part, 1]], axis=1),
                    ],
                    axis=0,
                )
                high, low = halves(value)
                r.mix[layer, part, 0] = high
                r.mix[layer, part, 1] = low
                line = 2 * layer + part
                r.bias[line : line + 1, :] = jnp.concatenate([bias[part, 0:1, :], bias[part, 1:2, :]], axis=1)
        moves.start(r.mix, r.mix_kept)


        def turn_row(h, carry):
            r.x[h] = r.turned[h].T
            return carry

        lax.fori_loop(0, rows, turn_row, 0, unroll=2)
        wait_all(sums)
        given = [push("chan", chans, step, r.vectors, r.gathered.at[me], r.s6, r.r6) for step in range(1, chans)]
        for copy in given:
            copy.start()
        for kind, source in enumerate((r.up, r.down)):

            @pl.when(core == kind)
            def _():
                for number in range(2):
                    own_to(number, source).start()

        totals = [r.all[j] for j in range(chans)]
        mean = sum(t[:rows] for t in totals) * (1.0 / plan.width)
        spread_sum = sum(
            t[rows:] + features * jnp.square(t[:rows] * (1.0 / features) - mean) for t in totals
        ) * (1.0 / plan.width)
        r.mine[pl.ds(0, rows), :] = mean
        r.mine[pl.ds(rows, rows), :] = lax.rsqrt(spread_sum + NORM_EPS)
        gain, shift = r.gain[...].reshape(1, -1), r.shift[...].reshape(1, -1)

        def normed(h):
            inverse = r.mine[pl.ds(rows + h, 1), :]
            table = stack_rows([r.mine[pl.ds(h, 1), :], inverse])
            unit = (r.x[h] - over_lanes(table, features, 0)) * over_lanes(table, features, 1)
            r.unit[h] = unit
            r.dev[pl.ds(h, 1), :] = inverse
            return unit * gain + shift

        scales = (r.scale, r.scale_all, r.s20, r.r20)
        there = Exchange(True, plan.spaces, plan.thick, r.send1, r.recv1, r.s1, r.r1, scales)
        back = Exchange(False, plan.spaces, plan.thick, r.send2, r.recv2, r.s2, r.r2)
        rows_to_modes(plan, (r.row[0], r.row[1]), r.flat, normed, True)
        send_modes(there, plan.pairs, plan.chunk, r.flat)
        moves.start(r.unit, r.unit_kept)
        moves.start(r.dev, r.dev_kept)
        loaded.wait()
        enter(r.lines_in, r.cells_t, r.turn)
        moves.start(r.cells_t, r.cells_kept)
        filter_forward(plan, r, there, back, pass_near)
        for source, target in ((r.spec, r.spec_kept), (r.first, r.first_kept), (r.second, r.second_kept)):
            moves.start(source, target)
        collect(back, plan.pairs, plan.chunk, r.flat)
        pass_far()
        copies = rows_forward(plan, r, r.unit, r.x, r.middle)
        moves.start(r.middle, r.middle_kept)
        wait_all(copies + given)
        close_weights()
        wait_all(own_weights)
        moves.start(r.w, r.w_kept)
        ffn_forward(plan, r)
        saved = ("active", "slope", "entry", "unit_wide", "dev_wide", "gathered")
        for key in saved:
            moves.start(getattr(r, key), getattr(r, key + "_kept"))

        def last(block):
            outer = r.total[block.cells, :]
            mean, _, inverse = moments(outer + block.get(r.mid))
            block.put(r.leaving, outer)
            r.stats[block.group, block.front, :] = jnp.concatenate(
                three_parts(mean) + three_parts(inverse) + [jnp.zeros((block.size, 122), BF)], axis=1
            )

        by_blocks(plan, last)
        copies = spread_chan(plan, r.leaving, r.home, r.s8, r.r8)
        for group in range(plan.share):
            r.stats_thin[group] = r.stats[group].astype(F32).T[:16].astype(BF)
        others = [
            push("chan", chans, step, r.stats_thin, r.stats_home.at[me], r.s9, r.r9) for step in range(1, chans)
        ]
        for copy in others:
            copy.start()
        r.stats_home[me] = r.stats_thin[...]
        wait_all(copies + others)
        there.close(plan.pairs)
        back.close(plan.pairs)
        moves.close()

    stats = ((chans, plan.share, 16, plan.columns), BF)
    outs = {
        "home": plan.by_cells,
        "stats_home": stats,
        "middle_kept": plan.field,
        "unit_kept": plan.field,
        "dev_kept": plan.dev,
        "cells_kept": plan.field,
        "spec_kept": plan.kept,
        "first_kept": plan.kept,
        "second_kept": plan.kept,
        "mix_kept": plan.mix,
        "w_kept": plan.weights,
        "active_kept": plan.tiles,
        "slope_kept": plan.tiles,
        "entry_kept": plan.wide,
        "unit_wide_kept": plan.wide,
        "dev_wide_kept": plan.dev_wide,
        "gathered_kept": plan.vectors,
        "bias": ((8, features), F32),
    }
    ins = dict(args)
    ins.update({key: tables[key] for key in ("row", "rowinv", "col", "colinv")})
    scratch = {
        "dma": sems(20),
        "x": scratch_of(plan.field),
        "unit": scratch_of(plan.field),
        "dev": scratch_of(plan.dev),
        "middle": scratch_of(plan.field),
        "cells_t": scratch_of(plan.field),
        "lines_in": scratch_of(plan.lines),
        "turned": pltpu.VMEM((rows, features, plan.columns), F32),
        "mine": pltpu.VMEM((2 * rows, plan.columns), F32),
        "all": pltpu.VMEM((chans, 2 * rows, plan.columns), F32),
        "spec": scratch_of(plan.kept),
        "first": scratch_of(plan.kept),
        "second": scratch_of(plan.kept),
        "mix": scratch_of(plan.mix),
        "w": scratch_of(plan.weights),
        "vectors": pltpu.VMEM((8, plan.local), F32),
        "own": scratch_of(plan.by_cells),
        "mid": scratch_of(plan.by_cells),
        "leaving": scratch_of(plan.by_cells),
        "stats": pltpu.VMEM((plan.share, plan.columns, 128), BF),
        "stats_thin": pltpu.VMEM(stats[0][1:], BF),
        **plan.exchange_scratch(True, False),
        **plan.spectral_scratch(),
        **ffn_scratch(plan),
        **{key + str(k): sems(chans) for k in range(3, 10) for key in ("s", "r")},
    }
    in_place = ("up", "down", "lines_t")
    return launch(
        body,
        ins,
        outs,
        scratch,
        "first_forward",
        0,
        {key: IN_PLACE for key in in_place},
        {key: IN_PLACE for key in outs if key.endswith("_kept")},
    )


def launch_second(plan, args, one, tables):
    rows, features, chans = plan.rows, plan.features, plan.chans

    def body(r):
        me = lax.axis_index("chan")
        met = greet(plan)
        mark_even(plan, r)
        moves = Moves(r.dma)
        loaded = moves.start(r.lines_t, r.lines_in)
        weights = moves.start(r.w_kept, r.w)
        vectors = moves.start(r.gathered_kept, r.gathered)
        earlier = moves.start(r.cells_kept, r.cells_one)
        held = [
            moves.start(r.col_kept, r.col),
            moves.start(r.mix_kept, r.mix),
            moves.start(r.colinv_kept, r.colinv),
        ]
        moves.open = []
        gain, shift = r.gain[...].reshape(1, -1), r.shift[...].reshape(1, -1)
        weight = r.codes[0].astype(F32) * (1.0 / 64.0)

        def normed(h):
            quarter, inside = h // plan.share, h % plan.share
            x = unpack_cells(r.home[quarter, inside].astype(F32)) + r.before[h]
            table = r.stats_home[quarter, inside]
            unit = (x - over_lanes(table, features, 0)) * over_lanes(table, features, 1)
            r.x[h] = x
            r.unit[h] = unit
            r.dev[pl.ds(h, 1), :] = jnp.sum(table[3:6].astype(F32), axis=0, keepdims=True)
            return unit * gain + shift

        rows_to_modes(plan, (r.row[0], r.row[1]), r.flat, normed, True)
        met()
        scales = (r.scale, r.scale_all, r.s20, r.r20)
        there = Exchange(True, plan.spaces, plan.thick, r.send1, r.recv1, r.s1, r.r1, scales)
        back = Exchange(False, plan.spaces, plan.thick, r.send2, r.recv2, r.s2, r.r2)
        send_modes(there, plan.pairs, plan.chunk, r.flat)
        loaded.wait()
        enter(r.lines_in, r.cells_t, r.turn)

        def low_target(h, peer, place):
            r.own[peer, place] = pack_cells(r.cells_t[h]).astype(BF)

        targets = []

        def send_target(step, peer):
            if step:
                copy = push("chan", chans, step, r.own.at[peer], r.target.at[me], r.s5, r.r5)
                copy.start()
                targets.append(copy)
            else:
                r.target[me] = r.own[me]

        rows_of_chunks(plan, low_target, send_target)
        wait_all(held)
        filter_forward(plan, r, there, back)
        collect(back, plan.pairs, plan.chunk, r.flat)
        there.close(plan.pairs)
        back.close(plan.pairs)
        wait_all(targets)
        copies = rows_forward(plan, r, r.unit, r.x, r.before)
        weights.wait()
        vectors.wait()
        wait_all(copies)
        ffn_forward(plan, r)

        def errors(block):
            outer = r.total[block.cells, :]
            error = outer + block.get(r.mid) - block.get(r.target)
            r.upper[block.cells, :] = (weight * error).astype(BF)
            block.put(r.leaving, outer)

        by_blocks(plan, errors)
        copies = spread_chan(plan, r.leaving, r.landed, r.s6, r.r6)
        for copy in copies:
            copy.wait_send()
        ffn_backward(plan, r)
        for copy in copies:
            copy.wait_recv()
        copies = spread_chan(plan, r.leaving, r.own, r.s7, r.r7)

        def grads(u, carry):
            for slot in range(2):
                t = 2 * u + slot
                stores = [
                    pltpu.make_async_copy(r.grad.at[slot, k], r.grads_kept.at[k, t], r.dma2.at[slot, k])
                    for k in range(2)
                ]

                @pl.when(u > 0)
                def _():
                    wait_all(stores)

                for k, value in enumerate(weight_gradients(r, t)):
                    r.grad[slot, k] = value.astype(BF)
                    stores[k].start()
            return carry

        lax.fori_loop(0, plan.steps // 2, grads, 0)
        vector_gradients(plan, r, r.rest)
        wait_all(copies)

        def middle_grad(h):
            quarter, inside = h // plan.share, h % plan.share
            x = unpack_cells(r.landed[quarter, inside].astype(F32)) + r.before[h]
            r.before[h] = x
            grad = weight * (x - r.cells_t[h]) + unpack_cells(r.own[quarter, inside].astype(F32))
            r.out[h] = grad
            return grad

        rows_to_modes(plan, r.rowinv_t[...], r.flat, middle_grad, False)
        there = Exchange(False, plan.spaces, plan.thick, r.send3, r.recv3, r.s3_, r.r3_)
        back = Exchange(False, plan.spaces, plan.thick, r.send2, r.recv2, r.s2, r.r2)
        send_modes(there, plan.pairs, plan.chunk, r.flat)
        moves.start(r.before, r.second_x)
        leave(r.x, r.lines_in, r.turn)
        moves.start(r.lines_in, r.lines)
        filter_backward(plan, r, there, back)
        mix_gradients(plan, r, None)
        collect(back, plan.pairs, plan.chunk, r.flat)
        copies = rows_backward(plan, r, r.unit, None)
        earlier.wait()
        wait_all(copies)
        result = input_gradient(plan, r, r.unit, r.dev)
        copies = []

        def row(h, peer, place):
            grad = weight * (r.x[h] - r.cells_one[h]) + result(h)
            r.out[h] = grad
            r.own[peer, place] = pack_cells(grad).astype(BF)

        def send_chunk(step, peer):
            some = pl.ds(peer * plan.share, plan.share)
            moves.start(r.out.at[some], r.out_kept.at[some])
            if step:
                copy = push("chan", chans, step, r.own.at[peer], r.came.at[me], r.s8, r.r8)
                copy.start()
                copies.append(copy)
            else:
                r.came[me] = r.own[me]

        rows_of_chunks(plan, row, send_chunk)
        for slot in range(2):
            for k in range(2):
                pltpu.make_async_copy(
                    r.grad.at[slot, k], r.grads_kept.at[k, plan.steps - 2 + slot], r.dma2.at[slot, k]
                ).wait()
        wait_all(copies)
        there.close(plan.pairs)
        back.close(plan.pairs)
        moves.close()

    ins = {
        "home": one["home"],
        "stats_home": one["stats_home"],
        "before": one["middle_kept"],
        "w_kept": one["w_kept"],
        "gathered_kept": one["gathered_kept"],
        "cells_kept": one["cells_kept"],
        "mix_kept": one["mix_kept"],
        "bias": one["bias"],
        **args,
    }
    ins.update({key: tables[key] for key in ("row", "rowinv", "rowinv_t", "row_t")})
    ins.update(col_kept=tables["col"], colinv_kept=tables["colinv"])
    outs = {
        "out_kept": plan.field,
        "came": plan.by_cells,
        "lines": plan.lines,
        "second_x": plan.field,
        "sums": plan.sums,
        "rest": plan.rest,
        "grads_kept": plan.grads,
    }
    exchange = Exchange.shape(False, plan.spaces, plan.thick, plan.pairs)
    scratch = {
        "dma": sems(16),
        "out": scratch_of(plan.field),
        "mix": scratch_of(plan.mix),
        "col": pltpu.VMEM(tables["col"].shape, BF),
        "colinv": pltpu.VMEM(tables["colinv"].shape, BF),
        "dma2": sems(2, 2),
        "x": scratch_of(plan.field),
        "unit": scratch_of(plan.field),
        "dev": scratch_of(plan.dev),
        "cells_t": scratch_of(plan.field),
        "cells_one": scratch_of(plan.field),
        "lines_in": scratch_of(plan.lines),
        "spec": scratch_of(plan.kept),
        "first": scratch_of(plan.kept),
        "second": scratch_of(plan.kept),
        "w": scratch_of(plan.weights),
        "own": scratch_of(plan.by_cells),
        "mid": scratch_of(plan.by_cells),
        "target": scratch_of(plan.by_cells),
        "leaving": scratch_of(plan.by_cells),
        "landed": scratch_of(plan.by_cells),
        "upper": scratch_of(plan.wide),
        "small": pltpu.VMEM((8, plan.width), F32),
        "upb": pltpu.VMEM((16, plan.tile), F32),
        "grad": pltpu.VMEM((2, 2, plan.tile, plan.width), BF),
        "send3": exchange,
        "recv3": exchange,
        "s3_": sems(plan.pairs, plan.spaces),
        "r3_": sems(plan.pairs, plan.spaces),
        **plan.exchange_scratch(True, False),
        **plan.spectral_scratch(),
        **ffn_scratch(plan),
        **norm_sums_scratch(plan),
        **{key + str(k): sems(chans) for k in (3, 5, 6, 7, 8) for key in ("s", "r")},
    }
    in_specs = {key: IN_PLACE for key in ins if key.endswith("_kept") or key == "lines_t"}
    in_specs["codes"] = pl.BlockSpec(memory_space=pltpu.SMEM)
    Order.far = True
    made = launch(
        body,
        ins,
        outs,
        scratch,
        "second_step",
        1,
        in_specs,
        {key: IN_PLACE for key in ("second_x", "grads_kept", "lines", "out_kept")},
    )
    Order.far = False
    return made


def launch_third(plan, args, one, two, tables):
    rows, features, chans, spaces = plan.rows, plan.features, plan.chans, plan.spaces
    local, width = plan.local, plan.width
    levels = spaces // 2
    piece = local // levels
    small = plan.small
    part = -(-(small + 32) // (16 * levels)) * 16

    def body(r):
        me = lax.axis_index("chan")
        place = lax.axis_index("space")
        core = lax.rem(place, 2)
        level = place // 2
        sibling = place + 1 - 2 * core
        others = [lax.rem(level + step, levels) for step in range(1, levels)]
        met = greet(plan)
        mark_even(plan, r)
        moves = Moves(r.dma)
        early = [
            moves.start(source, target)
            for source, target in (
                (r.gathered_kept, r.gathered),
                (r.unit_wide_kept, r.unit_wide),
                (r.dev_wide_kept, r.dev_wide),
            )
        ]
        chunks = []
        for j in range(chans):
            tiles = pl.ds(j * plan.per, plan.per)
            chunks.append(
                [
                    moves.start(r.w_kept.at[1, j], r.w.at[1, j]),
                    moves.start(r.slope_kept.at[tiles], r.slope.at[tiles]),
                    moves.start(r.w_kept.at[0, j], r.w.at[0, j]),
                ]
            )
        middle = [moves.start(r.active_kept, r.active), moves.start(r.entry_kept, r.entry)]
        moves.open = []

        def upper(block):
            r.upper[block.cells, :] = block.get(r.came).astype(BF)

        by_blocks(plan, upper)
        wait_all(early)
        wait_all(chunks[0])
        ffn_backward(plan, r, lambda chunk: wait_all(chunks[chunk]))
        late = [
            moves.start(source, target)
            for source, target in (
                (r.g, r.out),
                (r.unit_kept, r.unit),
                (r.spec_kept, r.spec),
                (r.first_kept, r.first),
                (r.second_kept, r.second),
                (r.dev_kept, r.dev),
                (r.mix_kept, r.mix),
                (r.col_kept, r.col),
                (r.colinv_kept, r.colinv),
            )
        ]
        moves.open = []
        met()
        copies = spread_chan(plan, r.leaving, r.own, r.s7, r.r7)
        vector_gradients(plan, r, r.rest)
        r.rest[...] += r.rest_before[...]
        vectors = [
            push("chan", chans, step, r.rest.at[lax.rem(me + step, chans)], r.rest_land.at[me], r.s6, r.r6)
            for step in range(1, chans)
        ]
        for copy in vectors:
            copy.start()
        r.rest_land[me] = r.rest[me]
        wait_all(middle)

        column, line = lax.rem(me, 2), me // 2
        beside = me + 1 - 2 * column
        across = me + 2 - 4 * line
        near, under = pl.ds(0, plan.tile // 2), pl.ds(plan.tile // 2, plan.tile // 2)

        def order(i):
            k = i // plan.per
            owner_column = column + (1 - k // 2) * (1 - 2 * column)
            owner_line = line + (1 - k % 2) * (1 - 2 * line)
            return (2 * owner_line + owner_column) * plan.per + i % plan.per

        def fetch(i, k):
            return pltpu.make_async_copy(r.grads_kept.at[k, order(i)], r.prev.at[i % 2, k], r.dma2.at[i % 2, k])

        def swap(i):
            return pltpu.make_async_remote_copy(
                src_ref=r.give.at[i % 2],
                dst_ref=r.take.at[i % 3],
                send_sem=r.s9.at[i],
                recv_sem=r.r9.at[i],
                device_id={"space": sibling},
                device_id_type=MESH_ID,
            )

        def to_chan(source, target, sem, number, device):
            return pltpu.make_async_remote_copy(
                src_ref=source,
                dst_ref=target,
                send_sem=sem[0].at[number],
                recv_sem=sem[1].at[number],
                device_id={"chan": device},
                device_id_type=MESH_ID,
            )

        def ship_near(i):
            target = r.land_near.at[i // plan.per, i % plan.per]
            return to_chan(r.keep.at[i, near], target, (r.s10, r.r10), i, beside)

        def ship_under(j):
            i = j + (j // plan.per) * plan.per
            target = r.land_under.at[j // plan.per, j % plan.per]
            return to_chan(r.keep.at[i, under], target, (r.s17, r.r17), j, across)

        def on_across(k):
            return to_chan(
                r.keep.at[2 * plan.per + k, near], r.land_on.at[0, k], (r.s18, r.r18), k, across
            )

        def on_beside(k):
            return to_chan(
                r.keep.at[plan.per + k, under], r.land_on.at[1, k], (r.s18, r.r18), plan.per + k, beside
            )

        def pass_on():
            def tile(k, carry):
                for arrived, land, start, part, onward in (
                    (ship_near, r.land_near, 2 * plan.per, near, on_across),
                    (ship_under, r.land_under, plan.per, under, on_beside),
                ):
                    arrived(k).wait_recv()
                    value = r.keep[start + k, part, :].astype(F32) + land[0, k].astype(F32)
                    r.keep[start + k, part, :] = value.astype(BF)
                    onward(k).start()
                return carry

            lax.fori_loop(0, plan.per, tile, 0)

        for k in range(2):
            fetch(0, k).start()

        def settle(i):
            swap(i).wait()
            r.keep[i] = (r.keep[i].astype(F32) + r.take[i % 3].astype(F32)).astype(BF)

        shipped = plan.steps - plan.per

        def leave_block(i):
            settle(i)

            @pl.when(i < 2 * plan.per)
            def _():
                ship_near(i).start()

            @pl.when(i < plan.per)
            def _():
                ship_under(i).start()

            @pl.when(i >= 2 * plan.per)
            def _():
                ship_under(i - plan.per).start()

        def make_block(i, before):
            for k in range(2):
                fetch(i, k).wait()

            @pl.when(i + 1 < plan.steps)
            def _():
                for k in range(2):
                    fetch(i + 1, k).start()

            values = [
                (value + r.prev[i % 2, k].astype(F32)).astype(BF)
                for k, value in enumerate(weight_gradients(r, order(i)))
            ]
            before(i)
            for kind in range(2):

                @pl.when(core == kind)
                def _():
                    r.keep[i] = values[kind]
                    r.give[i % 2] = values[1 - kind]

            swap(i).start()

        def others_block(i, carry):
            make_block(i, lambda i: pl.when(i > 0)(lambda: leave_block(i - 1)))
            return carry

        def own_block(i, carry):
            make_block(i, lambda i: pl.when(i > shipped)(lambda: settle(i - 1)))
            return carry

        lax.fori_loop(0, shipped, others_block, 0)
        leave_block(shipped - 1)
        wait_all(copies)
        wait_all(late)

        def middle_grad(h):
            quarter, inside = h // plan.share, h % plan.share
            grad = r.out[h] + unpack_cells(r.own[quarter, inside].astype(F32))
            r.out[h] = grad
            return grad

        rows_to_modes(plan, r.rowinv_t[...], r.flat, middle_grad, False)
        there = Exchange(False, spaces, plan.thick, r.send1, r.recv1, r.s1, r.r1)
        back = Exchange(False, spaces, plan.thick, r.send2, r.recv2, r.s2, r.r2)
        send_modes(there, plan.pairs, plan.chunk, r.flat)
        lax.fori_loop(shipped, plan.steps, own_block, 0)
        settle(plan.steps - 1)
        filter_backward(plan, r, there, back, pass_on)
        mix_gradients(plan, r, r.sums_before)

        def arrived(k, carry):
            ship_near(k).wait_send()
            ship_near(plan.per + k).wait()
            ship_under(k).wait_send()
            ship_under(plan.per + k).wait()
            on_across(k).wait()
            on_beside(k).wait()
            return carry

        lax.fori_loop(0, plan.per, arrived, 0)
        wait_all(vectors)
        def send(source, target, step, send_sem, recv_sem):
            return pltpu.make_async_remote_copy(
                src_ref=source,
                dst_ref=target,
                send_sem=send_sem.at[step],
                recv_sem=recv_sem.at[step],
                device_id={"space": 2 * others[step - 1] + core},
                device_id_type=MESH_ID,
            )

        def to_sibling(source, target, step, send_sem, recv_sem):
            return pltpu.make_async_remote_copy(
                src_ref=source,
                dst_ref=target,
                send_sem=send_sem.at[step],
                recv_sem=recv_sem.at[step],
                device_id={"space": sibling},
                device_id_type=MESH_ID,
            )

        def total(tile, carry):
            for half, land in enumerate((r.land_near, r.land_under)):
                for sub in range(2):
                    inside = pl.ds(64 * sub, 64)
                    value = r.keep[3 * plan.per + tile, pl.ds(128 * half + 64 * sub, 64), :].astype(F32)
                    value += land[1, tile, inside, :].astype(F32) + r.land_on[half, tile, inside, :].astype(F32)
                    number = 4 * tile + 2 * half + sub
                    target = pl.ds(pl.multiple_of((number % (piece // 64)) * 64, 64), 64)
                    r.a_send[number // (piece // 64), target, :] = value.astype(BF)
            return carry

        lax.fori_loop(0, plan.per, total, 0)
        wide = [
            send(r.a_send.at[others[step - 1]], r.a_land.at[level], step, r.s11, r.r11)
            for step in range(1, levels)
        ]
        for copy in wide:
            copy.start()
        collect(back, plan.pairs, plan.chunk, r.flat)
        copies = rows_backward(plan, r, r.unit, r.sums_before)
        r.table[...] = jnp.zeros_like(r.table)
        r.table[0:small, :] = r.sums[...]
        tail = sum(r.rest_land[j] for j in range(chans))
        for k in range(local // 128):
            lanes = slice(k * 128, (k + 1) * 128)
            r.table[small + k : small + k + 1, :] = tail[0:1, lanes]
        for k in range(3):
            line = jnp.concatenate([tail[1 + k : 2 + k, :features], jnp.zeros((1, 256 - features), F32)], axis=1)
            r.table[small + 8 + 2 * k : small + 9 + 2 * k, :] = line[:, :128]
            r.table[small + 9 + 2 * k : small + 10 + 2 * k, :] = line[:, 128:]
        for q in range(levels):
            r.b_send[q] = r.table[q * part : (q + 1) * part, :].astype(BF)
        thin = [
            send(r.b_send.at[others[step - 1]], r.b_land.at[level], step, r.s12, r.r12)
            for step in range(1, levels)
        ]
        for copy in thin:
            copy.start()
        wait_all(copies)
        result = input_gradient(plan, r, r.unit, r.dev)

        def finish(h, carry):
            r.out[h] = result(h)
            return carry

        lax.fori_loop(0, rows, finish, 0, unroll=3)
        moves.start(r.second_x, r.scaled).wait()
        moves.open = []
        leave(r.scaled, r.lines, r.turn)
        moves.start(r.lines, r.lines_x)
        a = r.a_send[level].astype(F32)
        b = r.b_send[level].astype(F32)
        for step in range(1, levels):
            wide[step - 1].wait()
            thin[step - 1].wait()
            source = lax.rem(level - step + levels, levels)
            a += r.a_land[source].astype(F32)
            b += r.b_land[source].astype(F32)
        r.a_own[...] = a.astype(BF)
        r.b_own[...] = b.astype(BF)
        last = [to_sibling(r.a_own, r.a_other.at[level], 0, r.s13, r.r13)]
        last += [to_sibling(r.b_own, r.b_other.at[level], 0, r.s14, r.r14)]
        again = []
        for step in range(1, levels):
            again.append(send(r.a_own, r.a_full.at[level], step, r.s15, r.r15))
            again.append(send(r.b_own, r.b_full.at[level], step, r.s16, r.r16))
        for copy in again + last:
            copy.start()
        r.a_full[level] = r.a_own[...]
        r.b_full[level] = r.b_own[...]
        moves.close()
        moves.open = []
        leave(r.out, r.lines, r.turn)
        moves.start(r.lines, r.lines_out)
        for step in range(1, levels):
            again[2 * step - 2].wait()
            again[2 * step - 1].wait()
            source = lax.rem(level - step + levels, levels)
            more = [to_sibling(r.a_full.at[source], r.a_other.at[source], step, r.s13, r.r13)]
            more += [to_sibling(r.b_full.at[source], r.b_other.at[source], step, r.s14, r.r14)]
            for copy in more:
                copy.start()
            last += more
        wait_all(last)
        moves.close()
        there.close(plan.pairs)
        back.close(plan.pairs)

    ins = {
        "g": two["out_kept"],
        "came": two["came"],
        "second_x": two["second_x"],
        "sums_before": two["sums"],
        "rest_before": two["rest"],
        "grads_kept": two["grads_kept"],
        "mix_kept": one["mix_kept"],
        **{
            key: one[key]
            for key in (
                "w_kept",
                "slope_kept",
                "active_kept",
                "entry_kept",
                "unit_wide_kept",
                "dev_wide_kept",
                "gathered_kept",
                "spec_kept",
                "first_kept",
                "second_kept",
                "unit_kept",
                "dev_kept",
            )
        },
        **args,
    }
    ins.update({key: tables[key] for key in ("rowinv_t", "row_t")})
    ins.update(col_kept=tables["col"], colinv_kept=tables["colinv"])
    outs = {
        "lines_x": plan.lines,
        "lines_out": plan.lines,
        "a_full": ((levels, piece, width), BF),
        "a_other": ((levels, piece, width), BF),
        "b_full": ((levels, part, 128), BF),
        "b_other": ((levels, part, 128), BF),
    }
    blocks = pltpu.VMEM((plan.steps, plan.tile, width), BF)
    scratch = {
        "dma": sems(32),
        "mix": scratch_of(plan.mix),
        "col": pltpu.VMEM(tables["col"].shape, BF),
        "colinv": pltpu.VMEM(tables["colinv"].shape, BF),
        "dma2": sems(2, 2),
        "lines": scratch_of(plan.lines),
        "unit": scratch_of(plan.field),
        "dev": scratch_of(plan.dev),
        "out": scratch_of(plan.field),
        "spec": scratch_of(plan.kept),
        "first": scratch_of(plan.kept),
        "second": scratch_of(plan.kept),
        "w": scratch_of(plan.weights),
        "own": scratch_of(plan.by_cells),
        "leaving": scratch_of(plan.by_cells),
        "upper": scratch_of(plan.wide),
        "small": pltpu.VMEM((8, width), F32),
        "upb": pltpu.VMEM((16, plan.tile), F32),
        "sums": scratch_of(plan.sums),
        "rest": scratch_of(plan.rest),
        "rest_land": scratch_of(plan.rest),
        "prev": pltpu.VMEM((2, 2, plan.tile, width), BF),
        "keep": blocks,
        "give": pltpu.VMEM((2, plan.tile, width), BF),
        "take": pltpu.VMEM((3, plan.tile, width), BF),
        "land_near": pltpu.VMEM((2, plan.per, plan.tile // 2, width), BF),
        "land_under": pltpu.VMEM((2, plan.per, plan.tile // 2, width), BF),
        "land_on": pltpu.VMEM((2, plan.per, plan.tile // 2, width), BF),
        "table": pltpu.VMEM((part * levels, 128), F32),
        "a_send": pltpu.VMEM((levels, piece, width), BF),
        "a_land": pltpu.VMEM((levels, piece, width), BF),
        "a_own": pltpu.VMEM((piece, width), BF),
        "b_send": pltpu.VMEM((levels, part, 128), BF),
        "b_land": pltpu.VMEM((levels, part, 128), BF),
        "b_own": pltpu.VMEM((part, 128), BF),
        **plan.exchange_scratch(False, False),
        **plan.spectral_scratch(),
        **ffn_scratch(plan),
        **norm_sums_scratch(plan),
        **{key + str(k): sems(chans) for k in (6, 7) for key in ("s", "r")},
        **{key + str(k): sems(plan.steps) for k in (9, 10, 17, 18) for key in ("s", "r")},
        **{key + str(k): sems(levels) for k in range(11, 17) for key in ("s", "r")},
    }
    in_place = [key for key in ins if key.endswith("_kept")] + ["second_x", "g"]
    return launch(
        body,
        ins,
        outs,
        scratch,
        "first_backward",
        2,
        {key: IN_PLACE for key in in_place},
        {key: IN_PLACE for key in ("lines_x", "lines_out")},
    )


def unpack_gradients(plan, parts, fields):
    features, small = plan.features, plan.small
    levels, piece, width = parts["a_full"].shape
    part = parts["b_full"].shape[1]
    local = levels * piece
    size = features // 2

    def body(r):
        swap = lax.rem(lax.axis_index("space"), 2) == 1
        moves = Moves(r.dma)
        waiting = [(moves.start(getattr(r, key + "_in"), getattr(r, key + "_held")), key) for key in fields]
        for q in range(levels):
            own = slice(q * piece, (q + 1) * piece)
            mine, theirs = r.a_full[q], r.a_other[q]
            r.down_made[own, :] = jnp.where(swap, theirs, mine).astype(F32)
            r.up_made[:, own] = jnp.where(swap, mine, theirs).T.astype(F32)
            moves.start(r.down_made.at[pl.ds(q * piece, piece)], r.down.at[pl.ds(q * piece, piece)])
            if q % 2:
                lanes = pl.ds((q - 1) * piece, 2 * piece)
                moves.start(r.up_made.at[:, lanes], r.up.at[:, lanes])
            if q < len(waiting):
                loaded, key = waiting[q]
                loaded.wait()
                moves.start(getattr(r, key + "_held"), getattr(r, key))
            r.table[q * part : (q + 1) * part, :] = r.b_full[q].astype(F32) + r.b_other[q].astype(F32)
        for layer, target in enumerate((r.mix_in, r.mix_out)):
            for half in range(2):
                for block in range(2):
                    start = ((layer * 2 + half) * 2 + block) * size
                    target[half, block] = r.table[start : start + size, :size]
        base = 8 * size

        def vector(k):
            return jnp.concatenate(
                [r.table[base + k : base + k + 1, :], r.table[base + 8 + k : base + 9 + k, : features - 128]], axis=1
            )

        for k, target in enumerate((r.bias_in, r.bias_in, r.bias_out, r.bias_out)):
            value = vector(k)
            target[k % 2, 0:1, :] = value[:, :size]
            target[k % 2, 1:2, :] = value[:, size:]
        r.pre_gain[...] = vector(4)
        r.pre_shift[...] = vector(5)
        r.upb[...] = jnp.concatenate(
            [r.table[small + k : small + k + 1, :] for k in range(local // 128)], axis=1
        ).reshape(local)
        for k, target in enumerate((r.post_gain, r.post_shift, r.downb)):
            target[...] = jnp.concatenate(
                [
                    r.table[small + 8 + 2 * k : small + 9 + 2 * k, :],
                    r.table[small + 9 + 2 * k : small + 10 + 2 * k, : features - 128],
                ],
                axis=1,
            )
        moves.open = moves.open[len(waiting) :]
        moves.close()

    return launch(
        body,
        {
            **{key: parts[key] for key in ("a_full", "a_other", "b_full", "b_other")},
            **{key + "_in": value for key, value in fields.items()},
        },
        {
            "down": ((local, width), F32),
            "up": ((width, local), F32),
            "mix_in": ((2, 2, size, size), F32),
            "mix_out": ((2, 2, size, size), F32),
            "bias_in": ((2, 2, size), F32),
            "bias_out": ((2, 2, size), F32),
            "pre_gain": ((1, features), F32),
            "pre_shift": ((1, features), F32),
            "post_gain": ((1, features), F32),
            "post_shift": ((1, features), F32),
            "downb": ((1, features), F32),
            "upb": ((local,), F32),
            **{key: plan.lines for key in fields},
        },
        {
            "table": pltpu.VMEM((part * levels, 128), F32),
            "down_made": pltpu.VMEM((local, width), F32),
            "up_made": pltpu.VMEM((width, local), F32),
            "dma": sems(16),
            **{key + "_held": scratch_of(plan.lines) for key in fields},
        },
        "unpack_gradients",
        None,
        {key + "_in": IN_PLACE for key in fields},
        {key: IN_PLACE for key in ("down", "up", *fields)},
    )


def shards_fast(
    current_atmosphere,
    truth_one,
    truth_two,
    storm_codes,
    pre_gain,
    pre_shift,
    mix_weight_in,
    mix_bias_in,
    mix_weight_out,
    mix_bias_out,
    post_gain,
    post_shift,
    up_weight,
    up_bias,
    down_weight,
    down_bias,
):
    rows, merged = current_atmosphere.shape[1:]
    columns = W
    features = merged // columns
    plan = Plan(
        rows, features, columns, lax.axis_size("space"), lax.axis_size("chan"), up_weight.shape[1]
    )
    forward, inverse = row_constants(columns)
    column = column_constants(rows * plan.spaces, rows, 2)
    tables = {
        "row": jnp.stack(const_halves(forward)),
        "rowinv": const_halves(inverse)[0],
        "rowinv_t": const_halves(inverse.T)[0],
        "row_t": const_halves(forward.T)[0],
        "col": jnp.stack(const_halves(column)),
        "colinv": const_halves(column.T)[0],
    }

    def lines(flat):
        return flat.reshape(rows, merged // 128, 128)

    def flat(line_field):
        return line_field.reshape(1, rows, merged)

    one = launch_first(
        plan,
        {
            "lines_x": lines(current_atmosphere),
            "lines_t": lines(truth_one),
            "gain": pre_gain,
            "shift": pre_shift,
            "mix_in": mix_weight_in,
            "bias_in": mix_bias_in,
            "mix_out": mix_weight_out,
            "bias_out": mix_bias_out,
            "post_gain": post_gain,
            "post_shift": post_shift,
            "up": up_weight,
            "upb": up_bias,
            "down": down_weight,
            "downb": down_bias,
        },
        tables,
    )
    two = launch_second(
        plan,
        {"gain": pre_gain, "shift": pre_shift, "lines_t": lines(truth_two), "codes": storm_codes},
        one,
        tables,
    )
    three = launch_third(plan, {"gain": pre_gain}, one, two, tables)
    grads = unpack_gradients(
        plan, three, {"first": two["lines"], "second": three["lines_x"], "state": three["lines_out"]}
    )
    return (
        flat(grads["first"]),
        flat(grads["second"]),
        flat(grads["state"]),
        grads["pre_gain"].reshape(features),
        grads["pre_shift"].reshape(features),
        grads["mix_in"],
        grads["bias_in"],
        grads["mix_out"],
        grads["bias_out"],
        grads["post_gain"].reshape(features),
        grads["post_shift"].reshape(features),
        grads["up"],
        grads["upb"],
        grads["down"],
        grads["downb"].reshape(features),
    )


def suits(mesh):
    spaces, chans = mesh.shape["space"], mesh.shape["chan"]
    return (spaces, chans) == (8, 4)


def solution(mesh):
    in_specs = (
        P(None, "space", "chan"),
        P(None, "space", "chan"),
        P(None, "space", "chan"),
        P(),
        P("chan"),
        P("chan"),
        P(None, "chan", None, None),
        P(None, "chan", None),
        P(None, "chan", None, None),
        P(None, "chan", None),
        P("chan"),
        P("chan"),
        P(None, "chan"),
        P("chan"),
        P("chan", None),
        P("chan"),
    )
    out_specs = (
        P(None, "space", "chan"),
        P(None, "space", "chan"),
        P(None, "space", "chan"),
        P("chan"),
        P("chan"),
        P(None, "chan", None, None),
        P(None, "chan", None),
        P(None, "chan", None, None),
        P(None, "chan", None),
        P("chan"),
        P("chan"),
        P(None, "chan"),
        P("chan"),
        P("chan", None),
        P("chan"),
    )
    return jax.shard_map(shards_fast if suits(mesh) else shards, mesh=mesh, in_specs=in_specs, out_specs=out_specs, check_vma=False)
```
